32 devices in a mesh: expert: 8 (over z, y), wshard: 4 (over x, core).
Axes of the slice: x: 2, y: 2, z: 4, core: 2. Of those that a mesh axis runs over, the one named last changes fastest.
Arguments:
- tokens: bfloat16 [16384, 1024], P(('expert', 'wshard')), may hold values from -6 to 6
- norm1_gain: bfloat16 [1024], P('wshard'), may hold values from 0.5 to 1.5
- norm1_shift: bfloat16 [1024], P('wshard'), may hold values from -1 to 1
- w_qkv: bfloat16 [1024, 3072], P('wshard'), may hold values from -0.1875 to 0.1875
- w_out: bfloat16 [1024, 1024], P('wshard'), may hold values from -3 to 3
- norm2_gain: bfloat16 [1024], P('wshard'), may hold values from 0.5 to 1.5
- norm2_shift: bfloat16 [1024], P('wshard'), may hold values from -1 to 1
- w_router: bfloat16 [1024, 16], P('wshard'), may hold values from -0.09375 to 0.09375
- w_up: bfloat16 [16, 1024, 4096], P('expert', None, 'wshard'), may hold values from -0.1875 to 0.1875
- w_down: bfloat16 [16, 4096, 1024], P('expert', 'wshard'), may hold values from -3 to 3
- routes: int32 [16384, 1], P(('expert', 'wshard')), may hold values from 0 to 15
- priority: int32 [32, 512], P(('expert', 'wshard')), may hold values from 0 to 511, each once within a row
- prefix: int32 [32], P(('expert', 'wshard')), may hold values from 51 to 256
- cotangent: bfloat16 [16384, 1024], P(('expert', 'wshard')), may hold values from -6 to 6
Outputs:
- output: bfloat16 [16384, 1024], P(('expert', 'wshard'))
- grad_tokens: float32 [16384, 1024], P(('expert', 'wshard'))
- grad_norm1_gain: float32 [1024], P('wshard')
- grad_norm1_shift: float32 [1024], P('wshard')
- grad_w_qkv: float32 [1024, 3072], P('wshard')
- grad_w_out: float32 [1024, 1024], P('wshard')
- grad_norm2_gain: float32 [1024], P('wshard')
- grad_norm2_shift: float32 [1024], P('wshard')
- grad_router: float32 [1024, 16], P('wshard')
- grad_up: float32 [16, 1024, 4096], P('expert', None, 'wshard')
- grad_down: float32 [16, 4096, 1024], P('expert', 'wshard')
The draws below stay inside these ranges and needn't reach their ends.
Inputs may be any that keep to these rules, and one draw needn't show every extreme that they name: `routes`: each token names one expert; every expert is named by some token. `priority`: each row orders the 512 tokens of one sequence, each number once.
All inputs are finite; a program needn't handle non-finite values.
Results may differ from the reference program's by a relative error of at most 0.02.
Values may be sent and summed in bfloat16 or wider, within the bound.
A program may use at most 256 MiB of HBM per device.

```python
import math
import jax
import jax.numpy as jnp
from jax import lax

D = 1024
HEADS = 16
HEAD_DIM = 64
FF = 4096
TOK_DEV = 512
EXPERTS = 16
SEQS = 32
TOKENS = 16384


def set_ends(array, own_key, least, top_value):
    shape = array.shape
    index_at = [jax.random.randint(jax.random.fold_in(own_key, axis), (), 0, shape[axis]) for axis in range(len(shape))]
    array = array.at[tuple(index_at)].set(least)
    longest = shape.index(max(shape))
    index_at[longest] = (index_at[longest] + 1) % shape[longest]
    return array.at[tuple(index_at)].set(top_value)


def steps_of(rng, shape, pieces, low, top_value):
    level = 1.0
    for position, shards_of in pieces:
        steps = jax.random.uniform(jax.random.fold_in(jax.random.fold_in(rng, 6), position), (shards_of,), jnp.float32, low / len(pieces), top_value / len(pieces))
        level = level * jnp.repeat(jnp.exp(steps), shape[position] // shards_of).reshape((-1,) + (1,) * (len(shape) - 1 - position))
    return level


def choose_distinct(stream_key, rows, amount, top, lift):
    ranking = jax.random.permutation(jax.random.fold_in(stream_key, 1), amount)
    pull = ranking
    for power in range(3):
        pull = pull * pull // amount
    pull = pull * lift // amount
    lots = jax.random.randint(jax.random.fold_in(stream_key, 2), (rows, amount), 0, 4096) + pull
    holders = jax.random.permutation(jax.random.fold_in(stream_key, 3), rows)[jnp.arange(amount) % rows]
    lots = jnp.where(jnp.arange(rows)[:, None] == holders[None, :], 1 << 14, lots)
    merit = lots * amount + jnp.arange(amount)
    return lax.top_k(merit.astype(jnp.int32), top)[1].astype(jnp.int32)


def gaussian(own_key, dims, deviation, most, pieces=(), held_as=jnp.bfloat16):
    values = deviation * jax.random.normal(own_key, dims, jnp.float32)
    if pieces:
        values = values * steps_of(own_key, dims, pieces, -0.22, 0.18)
    return jnp.clip(values, -most, most).astype(held_as)


def setup_inputs(seed: int = 0) -> dict:
    keys = jax.random.split(jax.random.key(seed), 15)
    tokens = gaussian(keys[0], (TOKENS, D), 1.0, 6.0, ((0, 32),))
    norm1_gain = jnp.clip(1.0 + 0.1 * jax.random.normal(keys[1], (D,), jnp.float32), 0.5, 1.5).astype(jnp.bfloat16)
    norm1_shift = gaussian(keys[2], (D,), 0.2, 1.0, ((0, 4),))
    w_qkv = gaussian(keys[3], (D, 3 * D), D ** -0.5, 0.1875, ((0, 4),))
    w_out = gaussian(keys[4], (D, D), (max(1, 2 * D // TOK_DEV)) ** -0.5, 3.0, ((0, 4),))
    norm2_gain = jnp.clip(1.0 + 0.1 * jax.random.normal(keys[5], (D,), jnp.float32), 0.5, 1.5).astype(jnp.bfloat16)
    norm2_shift = gaussian(keys[6], (D,), 0.2, 1.0, ((0, 4),))
    w_router = gaussian(keys[7], (D, EXPERTS), (4 * D) ** -0.5, 0.09375, ((0, 4),))
    w_up = gaussian(keys[8], (EXPERTS, D, FF), D ** -0.5, 0.1875, ((0, 8), (2, 4)))
    w_down = gaussian(keys[9], (EXPERTS, FF, D), (max(1, FF // (4 * EXPERTS * EXPERTS))) ** -0.5, 3.0, ((0, 8), (1, 4)))
    routes = choose_distinct(keys[10], TOKENS, EXPERTS, 1, 512)
    priority = jax.vmap(lambda own: jax.random.permutation(own, TOK_DEV))(jax.random.split(keys[11], SEQS)).reshape((SEQS, TOK_DEV)).astype(jnp.int32)
    prefix = set_ends(jax.random.randint(keys[12], (SEQS,), TOK_DEV // 10, TOK_DEV // 2 + 1), jax.random.fold_in(keys[12], 1), TOK_DEV // 10, (TOK_DEV // 2 + 1) - 1).astype(jnp.int32)
    cotangent = gaussian(keys[13], (TOKENS, D), 1.0, 6.0, ((0, 32),))
    return dict(tokens=tokens, norm1_gain=norm1_gain, norm1_shift=norm1_shift, w_qkv=w_qkv, w_out=w_out, norm2_gain=norm2_gain, norm2_shift=norm2_shift, w_router=w_router, w_up=w_up, w_down=w_down, routes=routes, priority=priority, prefix=prefix, cotangent=cotangent)


@jax.custom_vjp
def low(v):
    return lax.optimization_barrier(v.astype(jnp.bfloat16)).astype(jnp.float32)

@jax.custom_vjp
def low_back(v):
    return v

def low_keep(v):
    return (low(v), None)

def low_pass(kept, grad):
    return (grad,)

def back_keep(v):
    return (v, None)

def back_low(kept, grad):
    return (low(grad),)
low.defvjp(low_keep, low_pass)
low_back.defvjp(back_keep, back_low)
epsilon = 1e-05

def multiply(left, right):
    return jnp.dot(left, right, precision=lax.Precision.HIGHEST, preferred_element_type=jnp.float32)

def norm_rows(values, gain_vec, shift_vec):
    row_mean = lax.optimization_barrier(jnp.mean(values, axis=-1, keepdims=True))
    centered = values - row_mean
    return centered * lax.rsqrt(lax.optimization_barrier(jnp.mean(centered * centered, axis=-1, keepdims=True)) + epsilon) * gain_vec + shift_vec

def softmax_rows(scores):
    row_max = lax.optimization_barrier(jnp.max(scores, axis=-1, keepdims=True))
    exponent = jnp.exp(scores - row_max)
    return exponent / lax.optimization_barrier(jnp.sum(exponent, axis=-1, keepdims=True))

def assign_slots(route_ids, order_ids, expert_count, capacity):
    token_count = route_ids.shape[0]
    same_expert = route_ids[:, None] == route_ids[None, :]
    earlier = order_ids[None, :] < order_ids[:, None]
    rank_ids = lax.optimization_barrier(jnp.sum((same_expert & earlier).astype(jnp.int32), axis=1)).astype(jnp.int32)
    is_kept = rank_ids < capacity
    slot_index = jnp.where(is_kept, route_ids * capacity + rank_ids, expert_count * capacity).astype(jnp.int32)
    slot_ids = jnp.arange(expert_count * capacity, dtype=jnp.int32)
    match_table = slot_index[None, :] == slot_ids[:, None]
    token_ids = jnp.arange(token_count, dtype=jnp.int32)
    filled = jnp.any(match_table, axis=1)
    picked = lax.optimization_barrier(jnp.sum(jnp.where(match_table, token_ids[None, :], 0), axis=1)).astype(jnp.int32)
    slot_source = jnp.where(filled, picked, token_count).astype(jnp.int32)
    return (is_kept, slot_index, slot_source)

def attend_sequence(rows_in, prefix_len, gain_one, shift_one, qkv_weight, out_weight):
    token_count = rows_in.shape[0]
    model_width = rows_in.shape[1]
    act_one = low(norm_rows(rows_in, gain_one, shift_one))
    qkv = low(low_back(multiply(act_one, qkv_weight)))
    query_heads = qkv[:, :model_width].reshape(token_count, HEADS, HEAD_DIM)
    key_heads = qkv[:, model_width:2 * model_width].reshape(token_count, HEADS, HEAD_DIM)
    value_heads = qkv[:, 2 * model_width:].reshape(token_count, HEADS, HEAD_DIM)
    scores = jnp.einsum('qhd,khd->hqk', query_heads, key_heads, precision=lax.Precision.HIGHEST) * (1.0 / math.sqrt(HEAD_DIM))
    positions = jnp.arange(token_count, dtype=jnp.int32)
    allowed = (positions[None, :] <= positions[:, None]) | (positions[None, :] < prefix_len)
    scores = low_back(jnp.where(allowed[None], scores, -1e+30))
    attn_probs = low(softmax_rows(scores))
    merged = jnp.einsum('hqk,khd->qhd', attn_probs, value_heads, precision=lax.Precision.HIGHEST).reshape(token_count, model_width)
    merged = low(low_back(merged))
    return low_back(multiply(merged, out_weight))

def expert_rows(expert_item):
    rows_in, up_weight, down_weight = expert_item
    pre_act = low_back(multiply(rows_in, up_weight))
    act_hidden = low(jax.nn.gelu(pre_act, approximate=True))
    return low(low_back(multiply(act_hidden, down_weight)))

def reference(tokens, norm1_gain, norm1_shift, w_qkv, w_out, norm2_gain, norm2_shift, w_router, w_up, w_down, routes, priority, prefix, cotangent):
    seq_count = prefix.shape[0]
    row_count = tokens.shape[0] // seq_count
    model_width = tokens.shape[1]
    expert_count = w_router.shape[1]
    capacity = row_count // expert_count
    route_ids = routes[:, 0]

    def slots_of(seq_item):
        return assign_slots(seq_item[0], seq_item[1], expert_count, capacity)
    is_kept, slot_index, slot_source = lax.map(slots_of, (route_ids.reshape(seq_count, row_count), priority))
    token_base = jnp.arange(seq_count, dtype=jnp.int32)[:, None] * row_count
    source_index = jnp.where(slot_source < row_count, slot_source + token_base, seq_count * row_count).reshape(-1)
    slot_base = jnp.arange(seq_count, dtype=jnp.int32)[:, None] * (expert_count * capacity)
    back_index = jnp.where(is_kept, slot_index + slot_base, seq_count * expert_count * capacity).reshape(-1)
    chosen = route_ids[:, None] == jnp.arange(expert_count, dtype=jnp.int32)[None, :]

    def layer(tokens_float, gain_one, shift_one, qkv_weight, out_weight, gain_two, shift_two, router_weight, up_weight, down_weight):

        def attend_one(seq_item):
            return attend_sequence(seq_item[0], seq_item[1], gain_one, shift_one, qkv_weight, out_weight)
        attn_out = lax.map(jax.checkpoint(attend_one), (tokens_float.reshape(seq_count, row_count, model_width), prefix)).reshape(-1, model_width)
        hidden = tokens_float + attn_out
        act_two = low(norm_rows(hidden, gain_two, shift_two))
        logits = low_back(multiply(act_two, router_weight))
        gate_prob = softmax_rows(logits)
        gate_value = lax.optimization_barrier(jnp.sum(jnp.where(chosen, gate_prob, 0.0), axis=1))
        padded = jnp.concatenate([act_two, jnp.zeros((1, model_width), jnp.float32)], axis=0)
        sent_rows = low_back(padded[source_index]).reshape(seq_count, expert_count, capacity, model_width)
        by_expert = jnp.transpose(sent_rows, (1, 0, 2, 3)).reshape(expert_count, seq_count * capacity, model_width)
        produced = lax.map(jax.checkpoint(expert_rows), (by_expert, up_weight, down_weight))
        back_rows = jnp.transpose(produced.reshape(expert_count, seq_count, capacity, model_width), (1, 0, 2, 3)).reshape(-1, model_width)
        back_rows = jnp.concatenate([back_rows, jnp.zeros((1, model_width), jnp.float32)], axis=0)
        combined = back_rows[back_index]
        return hidden + gate_value[:, None] * combined
    floats = (tokens.astype(jnp.float32), norm1_gain.astype(jnp.float32), norm1_shift.astype(jnp.float32), w_qkv.astype(jnp.float32), w_out.astype(jnp.float32), norm2_gain.astype(jnp.float32), norm2_shift.astype(jnp.float32), w_router.astype(jnp.float32), w_up.astype(jnp.float32), w_down.astype(jnp.float32))
    output, pullback = jax.vjp(layer, *floats)
    grads = pullback(cotangent.astype(jnp.float32))
    return (output.astype(jnp.bfloat16), grads[0], grads[1], grads[2], grads[3], grads[4], grads[5], grads[6], grads[7], grads[8], grads[9])
```

```python
import functools
import math

import jax
import jax.numpy as jnp
from jax import lax
from jax.experimental import pallas as pl
from jax.experimental.pallas import tpu as pltpu
from jax.sharding import PartitionSpec as P

HEADS = 16
HEAD_DIM = 64


epsilon = 1e-05
VMEM_LIMIT = 66_000_000


def normalize(values, gain_vec, shift_vec):
    row_mean = jnp.mean(values, axis=-1, keepdims=True)
    centered = values - row_mean
    inverse = lax.rsqrt(jnp.mean(centered * centered, axis=-1, keepdims=True) + epsilon)
    scaled = centered * inverse
    return (scaled * gain_vec + shift_vec, scaled, inverse)


def norm_back(grad_rows, scaled, inverse, gain_vec):
    weighted = grad_rows * gain_vec
    mean_one = jnp.mean(weighted, axis=-1, keepdims=True)
    mean_two = jnp.mean(weighted * scaled, axis=-1, keepdims=True)
    grad_inputs = inverse * (weighted - mean_one - scaled * mean_two)
    return (grad_inputs, jnp.sum(grad_rows * scaled, axis=0), jnp.sum(grad_rows, axis=0))


def contract_rows(left, right):
    return lax.dot_general(
        left, right, (((0,), (0,)), ((), ())), preferred_element_type=jnp.float32
    )


def times_transpose(left, right):
    return lax.dot_general(
        left, right, (((1,), (1,)), ((), ())), preferred_element_type=jnp.float32
    )


def gelu_tanh(values):
    return jax.nn.gelu(values, approximate=True)


def assign_slots(route_ids, order_ids, expert_count, capacity):
    token_count = route_ids.shape[0]
    same_expert = route_ids[:, None] == route_ids[None, :]
    earlier = order_ids[None, :] < order_ids[:, None]
    rank_ids = jnp.sum((same_expert & earlier).astype(jnp.int32), axis=1)
    is_kept = rank_ids < capacity
    slot_index = jnp.where(is_kept, route_ids * capacity + rank_ids, expert_count * capacity)
    slot_ids = jnp.arange(expert_count * capacity, dtype=jnp.int32)
    match_table = slot_index[None, :] == slot_ids[:, None]
    token_ids = jnp.arange(token_count, dtype=jnp.int32)
    filled = jnp.any(match_table, axis=1)
    picked = jnp.sum(jnp.where(match_table, token_ids[None, :], 0), axis=1)
    slot_source = jnp.where(filled, picked, token_count)
    return (slot_index, slot_source)


def group_heads(values, groups):
    token_count = values.shape[0]
    return jnp.transpose(values.reshape(token_count, groups, -1, HEAD_DIM), (1, 0, 2, 3))


def block_scores(query_block, key_group, block_start, prefix_len):
    block_rows = query_block.shape[0]
    key_count = key_group.shape[0]
    scores = jnp.einsum(
        "qgd,kgd->gqk", query_block, key_group, preferred_element_type=jnp.float32
    ) * (1.0 / math.sqrt(HEAD_DIM))
    query_pos = block_start + jnp.arange(block_rows, dtype=jnp.int32)
    key_pos = jnp.arange(key_count, dtype=jnp.int32)
    allowed = (key_pos[None, :] <= query_pos[:, None]) | (key_pos[None, :] < prefix_len)
    return jnp.where(allowed[None], scores, -1e30)


def attend_forward(query_heads, key_heads, value_heads, prefix_len):
    token_count = query_heads.shape[0]
    group_size = min(4, HEADS)
    groups = HEADS // group_size
    block_rows = min(512, token_count)
    blocks = token_count // block_rows
    starts = jnp.arange(blocks, dtype=jnp.int32) * block_rows

    def one_group(group_item):
        query_group, key_group, value_group = group_item
        query_blocks = query_group.reshape(blocks, block_rows, group_size, HEAD_DIM)

        def one_block(block_item):
            query_block, block_start = block_item
            scores = block_scores(query_block, key_group, block_start, prefix_len)
            row_max = jnp.max(scores, axis=-1, keepdims=True)
            exponent = jnp.exp(scores - row_max)
            row_total = jnp.sum(exponent, axis=-1, keepdims=True)
            attn_probs = (exponent / row_total).astype(jnp.bfloat16)
            result = jnp.einsum(
                "gqk,kgd->qgd", attn_probs, value_group, preferred_element_type=jnp.float32
            )
            return (result, (row_max + jnp.log(row_total))[..., 0])

        return lax.map(one_block, (query_blocks, starts))

    attended, log_totals = lax.map(
        one_group,
        (
            group_heads(query_heads, groups),
            group_heads(key_heads, groups),
            group_heads(value_heads, groups),
        ),
    )
    merged = (
        jnp.transpose(attended, (1, 2, 0, 3, 4))
        .reshape(token_count, HEADS * HEAD_DIM)
        .astype(jnp.bfloat16)
    )
    return (merged, log_totals)


def attend_backward(query_heads, key_heads, value_heads, grad_merged, log_totals, prefix_len):
    token_count = query_heads.shape[0]
    group_size = min(4, HEADS)
    groups = HEADS // group_size
    block_rows = min(512, token_count)
    blocks = token_count // block_rows
    starts = jnp.arange(blocks, dtype=jnp.int32) * block_rows
    score_scale = 1.0 / math.sqrt(HEAD_DIM)

    def one_group(group_item):
        query_group, key_group, value_group, grad_group, total_group = group_item
        query_blocks = query_group.reshape(blocks, block_rows, group_size, HEAD_DIM)
        grad_blocks = grad_group.reshape(blocks, block_rows, group_size, HEAD_DIM)

        def one_block(carry, block_item):
            grad_keys, grad_vals = carry
            query_block, grad_block, total_block, block_start = block_item
            scores = block_scores(query_block, key_group, block_start, prefix_len)
            attn_probs = jnp.exp(scores - total_block[..., None])
            grad_probs = jnp.einsum(
                "qgd,kgd->gqk", grad_block, value_group, preferred_element_type=jnp.float32
            )
            row_delta = jnp.sum(attn_probs * grad_probs, axis=-1, keepdims=True)
            grad_scores = (attn_probs * (grad_probs - row_delta)).astype(jnp.bfloat16)
            grad_vals = grad_vals + jnp.einsum(
                "gqk,qgd->kgd",
                attn_probs.astype(jnp.bfloat16),
                grad_block,
                preferred_element_type=jnp.float32,
            )
            grad_keys = (
                grad_keys
                + jnp.einsum(
                    "gqk,qgd->kgd", grad_scores, query_block, preferred_element_type=jnp.float32
                )
                * score_scale
            )
            grad_query = (
                jnp.einsum(
                    "gqk,kgd->qgd", grad_scores, key_group, preferred_element_type=jnp.float32
                )
                * score_scale
            )
            return ((grad_keys, grad_vals), grad_query)

        zero_keys = jnp.zeros(key_group.shape, jnp.float32)
        carried, grad_queries = lax.scan(
            one_block, (zero_keys, zero_keys), (query_blocks, grad_blocks, total_group, starts)
        )
        return (grad_queries, carried[0], carried[1])

    grad_queries, grad_keys, grad_vals = lax.map(
        one_group,
        (
            group_heads(query_heads, groups),
            group_heads(key_heads, groups),
            group_heads(value_heads, groups),
            group_heads(grad_merged, groups),
            log_totals,
        ),
    )
    query_part = jnp.transpose(grad_queries, (1, 2, 0, 3, 4)).reshape(token_count, HEADS * HEAD_DIM)
    key_part = jnp.transpose(grad_keys, (1, 0, 2, 3)).reshape(token_count, HEADS * HEAD_DIM)
    value_part = jnp.transpose(grad_vals, (1, 0, 2, 3)).reshape(token_count, HEADS * HEAD_DIM)
    return jnp.concatenate([query_part, key_part, value_part], axis=1).astype(jnp.bfloat16)


MESH = pl.DeviceIdType.MESH
LANES = 128


def dot_nn(left, right):
    return lax.dot_general(
        left, right, (((1,), (0,)), ((), ())), preferred_element_type=jnp.float32
    )


def dot_nt(left, right):
    return lax.dot_general(
        left, right, (((1,), (1,)), ((), ())), preferred_element_type=jnp.float32
    )


def dot_tn(left, right):
    return lax.dot_general(
        left, right, (((0,), (0,)), ((), ())), preferred_element_type=jnp.float32
    )


class Place:
    def __init__(self, owners):
        self.owners = owners
        self.e = lax.axis_index("expert")
        self.w = lax.axis_index("wshard")
        self.c = lax.rem(self.w, 2)
        self.x = lax.div(self.w, 2)
        self.sib = self.w + 1 - 2 * self.c
        self.far = lax.rem(self.w + 2, 4)
        self.diag = 3 - self.w
        self.pair = self.e + 1 - 2 * lax.rem(self.e, 2)

    def ahead(self, k):
        return lax.rem(self.e + k, self.owners)

    def behind(self, k):
        return lax.rem(self.e + self.owners - k, self.owners)


def remote(src, dst, send, recv, device):
    return pltpu.make_async_remote_copy(
        src_ref=src,
        dst_ref=dst,
        send_sem=send,
        recv_sem=recv,
        device_id=device,
        device_id_type=MESH,
    )


def greet(peers):
    barrier = pltpu.get_barrier_semaphore()
    for peer in peers:
        pl.semaphore_signal(barrier, inc=1, device_id=peer, device_id_type=MESH)
    pl.semaphore_wait(barrier, len(peers))


class Dispatch:
    def __init__(self, place, capacity, send_ref, rows_ref, sems):
        self.p, self.cap, self.src, self.rows = place, capacity, send_ref, rows_ref
        self.own_sem, self.send, self.recv = sems
        self.own = pltpu.make_async_copy(
            self.src.at[place.e], self.slice(0, place.c, place.x), self.own_sem
        )
        self.direct = {
            k: remote(
                self.src.at[place.ahead(k)],
                self.slice(k, place.c, place.x),
                self.send.at[0, k],
                self.recv.at[0, k],
                (place.ahead(k), place.w),
            )
            for k in range(1, place.owners)
        }
        self.to_sib, self.to_far, self.relayed = {}, {}, {}

    def slice(self, k, core, side):
        start = ((((k // 2) * 2 + core) * 2 + side) * 2 + k % 2) * self.cap
        return self.rows.at[:, pl.ds(pl.multiple_of(start, self.cap), self.cap)]

    def hop(self, k, core, side, which, peer):
        part = self.slice(k, core, side)
        return remote(
            part, part, self.send.at[which, k], self.recv.at[which, k], (self.p.e, peer)
        )

    def start(self):
        self.own.start()
        for copy in self.direct.values():
            copy.start()

    def forward(self, k):
        if k == 0:
            self.own.wait()
        else:
            self.direct[k].wait_recv()
        self.to_far[k] = self.hop(k, self.p.c, self.p.x, 2, self.p.far)
        self.to_far[k].start()
        self.to_sib[k] = self.hop(k, self.p.c, self.p.x, 1, self.p.sib)
        self.to_sib[k].start()

    def relay(self, k):
        self.to_far[k].wait_recv()
        self.relayed[k] = self.hop(k, self.p.c, 1 - self.p.x, 3, self.p.sib)
        self.relayed[k].start()

    def ready(self, k):
        self.to_sib[k].wait_recv()
        self.relayed[k].wait_recv()

    def drain(self):
        for group in (self.direct, self.to_sib, self.to_far, self.relayed):
            for copy in group.values():
                copy.wait_send()


class Return:
    def __init__(self, place, capacity, experts, part, got, mid, far, done, home, sems):
        self.p, self.cap, self.experts = place, capacity, experts
        self.part, self.got, self.mid, self.far, self.done, self.home = (
            part, got, mid, far, done, home,
        )
        self.own_sem, self.send, self.recv, self.home_send, self.home_recv = sems
        self.swapped, self.crossed, self.homed = {}, {}, {}

    def span(self, start, size):
        return pl.ds(pl.multiple_of(start, size), size)

    def swap(self, j):
        size = 4 * self.cap
        self.swapped[j] = remote(
            self.part.at[:, self.span((j * 2 + 1 - self.p.c) * size, size)],
            self.got.at[:, self.span(j * size, size)],
            self.send.at[0, j],
            self.recv.at[0, j],
            (self.p.e, self.p.sib),
        )
        self.swapped[j].start()

    def pair_sum(self, expert, j, side):
        size = 2 * self.cap
        mine = self.part[expert, self.span(((j * 2 + self.p.c) * 2 + side) * size, size), :]
        theirs = self.got[expert, self.span((j * 2 + side) * size, size), :]
        return mine.astype(jnp.float32) + theirs.astype(jnp.float32)

    def cross(self, j):
        self.swapped[j].wait_recv()
        size = 2 * self.cap
        for expert in range(self.experts):
            self.mid[expert, pl.ds(j * size, size), :] = self.pair_sum(
                expert, j, 1 - self.p.x
            ).astype(jnp.bfloat16)
        part = pl.ds(j * size, size)
        self.crossed[j] = remote(
            self.mid.at[:, part],
            self.far.at[:, part],
            self.send.at[1, j],
            self.recv.at[1, j],
            (self.p.e, self.p.far),
        )
        self.crossed[j].start()

    def finish(self, j):
        self.crossed[j].wait_recv()
        size = 2 * self.cap
        for expert in range(self.experts):
            total = self.pair_sum(expert, j, self.p.x) + self.far[
                expert, pl.ds(j * size, size), :
            ].astype(jnp.float32)
            total = total.astype(jnp.bfloat16)
            self.done[2 * j, expert] = total[: self.cap]
            self.done[2 * j + 1, expert] = total[self.cap :]
        for k in (2 * j, 2 * j + 1):
            if k == 0:
                copy = pltpu.make_async_copy(
                    self.done.at[0], self.home.at[self.p.e], self.own_sem
                )
            else:
                copy = remote(
                    self.done.at[k],
                    self.home.at[self.p.e],
                    self.home_send.at[k],
                    self.home_recv.at[k],
                    (self.p.behind(k), self.p.w),
                )
            copy.start()
            self.homed[k] = copy

    def drain(self):
        for group in (self.swapped, self.crossed):
            for copy in group.values():
                copy.wait_send()
        for k, copy in self.homed.items():
            copy.wait()


def gelu_pair(v):
    root = math.sqrt(2.0 / math.pi)
    square = v * v
    t = jnp.tanh(v * (root + (root * 0.044715) * square))
    half = 0.5 + 0.5 * t
    slope = half + (half * (1.0 - t)) * (v * (root + (3.0 * root * 0.044715) * square))
    return v * half, slope


def expert_kernel(
    dims,
    send_ref, grads_hbm, up_hbm, down_hbm, router_ref,
    home_out, home_grad, rows_out, scaled_out, hidden_out, pre_out, router_grad,
    rows, grads, scaled, hidden, pre, up, down,
    part_out, part_grad, got_out, got_grad, mid_out, mid_grad,
    far_out, far_grad, done_out, done_grad,
    load_sem, own_sem, disp_send, disp_recv, red_send, red_recv, home_send, home_recv,
):
    owners, experts, capacity, width, units, expert_count = dims
    place = Place(owners)
    loads = [
        pltpu.make_async_copy(src, dst, load_sem.at[i])
        for i, (src, dst) in enumerate(
            [(up_hbm, up), (grads_hbm, grads), (down_hbm, down)]
        )
    ]
    for load in loads:
        load.start()
    greet(
        [(place.ahead(k), place.w) for k in range(1, owners)]
        + [(place.e, place.sib), (place.e, place.far)]
    )
    dispatch = Dispatch(
        place, capacity, send_ref, rows, (own_sem.at[0], disp_send, disp_recv)
    )
    ret = [
        Return(
            place, capacity, experts, part, got, mid, far, done, home,
            (own_sem.at[1 + i], red_send.at[i], red_recv.at[i], home_send.at[i], home_recv.at[i]),
        )
        for i, (part, got, mid, far, done, home) in enumerate(
            [
                (part_grad, got_grad, mid_grad, far_grad, done_grad, home_grad),
                (part_out, got_out, mid_out, far_out, done_out, home_out),
            ]
        )
    ]
    dispatch.start()
    router_grad[...] = jnp.zeros_like(router_grad)
    tile = min(256, units)
    wide = min(256, width)
    chunks = owners // 2
    size = 8 * capacity
    lane = lax.broadcasted_iota(jnp.int32, (size, LANES), 1)

    def compute(j):
        span = pl.ds(j * size, size)

        def one_expert(expert, carry):
            logits = dot_nn(rows[expert, span, :], router_ref[...])
            logits = jnp.where(lane < expert_count, logits, -1e30)
            exponent = jnp.exp(logits - jnp.max(logits, axis=1, keepdims=True))
            prob = exponent / jnp.sum(exponent, axis=1, keepdims=True)
            mine = lane == place.e * experts + expert
            gate = jnp.sum(jnp.where(mine, prob, 0.0), axis=1, keepdims=True)
            scaled[expert, span, :] = (
                gate * grads[expert, span, :].astype(jnp.float32)
            ).astype(jnp.bfloat16)

            def one_tile(n, carry):
                cols = pl.ds(pl.multiple_of(n * tile, tile), tile)
                value, slope = gelu_pair(dot_nn(rows[expert, span, :], up[expert, :, cols]))
                hidden[expert, span, cols] = value.astype(jnp.bfloat16)
                back = dot_nt(scaled[expert, span, :], down[expert, cols, :])
                pre[expert, span, cols] = (back * slope).astype(jnp.bfloat16)
                return carry

            lax.fori_loop(0, units // tile, one_tile, 0)

            def one_out(n, total):
                cols = pl.ds(pl.multiple_of(n * wide, wide), wide)
                value = dot_nn(hidden[expert, span, :], down[expert, :, cols])
                part_out[expert, span, cols] = value.astype(jnp.bfloat16)
                weighted = value * grads[expert, span, cols].astype(jnp.float32)
                for start in range(0, wide, LANES):
                    total = total + weighted[:, start : start + LANES]
                return total

            total = lax.fori_loop(
                0, width // wide, one_out, jnp.zeros((size, LANES), jnp.float32)
            )
            grad_gate = jnp.sum(total, axis=1, keepdims=True)
            grad_logits = (
                prob * ((jnp.where(mine, 1.0, 0.0) - gate) * grad_gate)
            ).astype(jnp.bfloat16)

            def one_in(n, carry):
                cols = pl.ds(pl.multiple_of(n * wide, wide), wide)
                value = dot_nt(pre[expert, span, :], up[expert, cols, :]) + dot_nt(
                    grad_logits, router_ref[cols, :]
                )
                part_grad[expert, span, cols] = value.astype(jnp.bfloat16)
                router_grad[:, cols] += dot_tn(grad_logits, rows[expert, span, cols])
                return carry

            lax.fori_loop(0, width // wide, one_in, 0)
            return carry

        lax.fori_loop(0, experts, one_expert, 0)

    for k in (0, 1):
        dispatch.forward(k)
    for j in range(chunks):
        if j + 1 < chunks:
            for k in (2 * j + 2, 2 * j + 3):
                dispatch.forward(k)
        for k in (2 * j, 2 * j + 1):
            dispatch.relay(k)
        for k in (2 * j, 2 * j + 1):
            dispatch.ready(k)
        if j == 0:
            for load in loads:
                load.wait()
        compute(j)
        ret[0].swap(j)
        ret[1].swap(j)
        if j >= 1:
            ret[0].cross(j - 1)
        if j >= 2:
            ret[0].finish(j - 2)
    ret[0].cross(chunks - 1)
    stores = [
        pltpu.make_async_copy(src, dst, load_sem.at[i])
        for i, (src, dst) in enumerate(
            [(rows, rows_out), (scaled, scaled_out), (hidden, hidden_out), (pre, pre_out)]
        )
    ]
    for store in stores:
        store.start()
    if chunks >= 2:
        ret[0].finish(chunks - 2)
    for j in range(chunks):
        ret[1].cross(j)
    ret[0].finish(chunks - 1)
    for j in range(chunks):
        ret[1].finish(j)
    for store in stores:
        store.wait()
    dispatch.drain()
    for each in ret:
        each.drain()


def run_experts(owners, capacity, expert_count, send_rows, grads, w_up, w_down, router):
    experts, width, units = w_up.shape
    slots = owners * 4 * capacity
    chunks = owners // 2
    dims = (owners, experts, capacity, width, units, expert_count)
    any_spec = pl.BlockSpec(memory_space=pl.ANY)
    vmem_spec = pl.BlockSpec(memory_space=pltpu.VMEM)
    bf16 = jnp.bfloat16
    home = jax.ShapeDtypeStruct((owners, experts, capacity, width), bf16)
    slab = jax.ShapeDtypeStruct((experts, slots, width), bf16)
    thin = jax.ShapeDtypeStruct((experts, slots, units), bf16)
    dma = pltpu.SemaphoreType.DMA

    def vm(*shape):
        return pltpu.VMEM(shape, bf16)

    return pl.pallas_call(
        functools.partial(expert_kernel, dims),
        out_shape=(
            home, home, slab, slab, thin, thin,
            jax.ShapeDtypeStruct((LANES, width), jnp.float32),
        ),
        in_specs=[any_spec] * 4 + [vmem_spec],
        out_specs=(any_spec,) * 6 + (vmem_spec,),
        scratch_shapes=[
            vm(experts, slots, width),
            vm(experts, slots, width),
            vm(experts, slots, width),
            vm(experts, slots, units),
            vm(experts, slots, units),
            vm(experts, width, units),
            vm(experts, units, width),
            vm(experts, slots, width),
            vm(experts, slots, width),
            vm(experts, slots // 2, width),
            vm(experts, slots // 2, width),
            vm(experts, slots // 4, width),
            vm(experts, slots // 4, width),
            vm(experts, slots // 4, width),
            vm(experts, slots // 4, width),
            vm(owners, experts, capacity, width),
            vm(owners, experts, capacity, width),
            dma((4,)),
            dma((3,)),
            dma((4, owners)),
            dma((4, owners)),
            dma((2, 2, chunks)),
            dma((2, 2, chunks)),
            dma((2, owners)),
            dma((2, owners)),
        ],
        compiler_params=pltpu.CompilerParams(
            collective_id=1, has_side_effects=True, vmem_limit_bytes=VMEM_LIMIT
        ),
        name="experts",
    )(send_rows, grads, w_up, w_down, router)


def front_kernel(
    dims,
    tokens_ref, small_hbm, qkv_hbm, out_hbm, grads_hbm,
    qkv_ref, act_ref, small_out, out_full, grads_rows, weight_out,
    small, weight, total,
    own_sem, disp_send, disp_recv, small_send, small_recv, near_send, near_recv,
    hop_send, hop_recv, pair_send, pair_recv, rel_send, rel_recv, prel_send, prel_recv,
):
    owners, capacity, pieces = dims
    place = Place(owners)
    shard = qkv_hbm.shape[0]
    half = shard // 2
    step = half // pieces
    here = (place.e, place.w)
    jobs = ((qkv_hbm, weight), (out_hbm, out_full))

    def block(ref, owner, start, size):
        return ref.at[pl.ds(pl.multiple_of(owner * shard + start, step), size)]

    own = [
        pltpu.make_async_copy(src, block(dst, place.w, 0, shard), own_sem.at[1 + i])
        for i, (src, dst) in enumerate(jobs)
    ]
    for copy in own:
        copy.start()
    own_small = pltpu.make_async_copy(small_hbm, small.at[place.w], own_sem.at[3])
    own_small.start()
    greet(
        [(place.ahead(k), place.w) for k in range(1, owners)]
        + [(place.e, place.sib), (place.e, place.far), (place.e, place.diag)]
    )
    smalls = [
        remote(small_hbm, small.at[place.w], small_send.at[i], small_recv.at[i], (place.e, peer))
        for i, peer in enumerate((place.sib, place.far, place.diag))
    ]
    for copy in smalls:
        copy.start()
    parity = lax.rem(place.e, 2)
    first = parity * half
    second = half - first
    hops, nears, pairs, relays, pair_relays = {}, {}, {}, {}, {}

    def start_job(i):
        src, dst = jobs[i]
        for n in range(pieces):
            hops[i, n] = remote(
                src.at[pl.ds(pl.multiple_of(first + n * step, step), step)],
                block(dst, place.w, first + n * step, step),
                hop_send.at[i, n], hop_recv.at[i, n], (place.e, place.far),
            )
            hops[i, n].start()
        nears[i] = remote(
            src, block(dst, place.w, 0, shard), near_send.at[i], near_recv.at[i],
            (place.e, place.sib),
        )
        nears[i].start()

    def pass_on(i, n):
        dst = jobs[i][1]
        hops[i, n].wait_recv()
        part = block(dst, place.far, first + n * step, step)
        pairs[i, n] = remote(
            part, part, pair_send.at[i, n], pair_recv.at[i, n], (place.pair, place.w)
        )
        pairs[i, n].start()
        relays[i, n] = remote(
            part, part, rel_send.at[i, n], rel_recv.at[i, n], (place.e, place.sib)
        )
        relays[i, n].start()

    def pass_pair(i, n):
        dst = jobs[i][1]
        pairs[i, n].wait_recv()
        part = block(dst, place.far, second + n * step, step)
        pair_relays[i, n] = remote(
            part, part, prel_send.at[i, n], prel_recv.at[i, n], (place.e, place.sib)
        )
        pair_relays[i, n].start()

    start_job(0)
    dispatch = Dispatch(place, capacity, grads_hbm, grads_rows, (own_sem.at[0], disp_send, disp_recv))
    dispatch.start()
    start_job(1)
    own_small.wait()
    for copy in smalls:
        copy.wait_recv()
    small_out[...] = small[...]
    gain = jnp.concatenate([small[i, 0:1, :] for i in range(4)], axis=1).astype(jnp.float32)
    shift = jnp.concatenate([small[i, 1:2, :] for i in range(4)], axis=1).astype(jnp.float32)
    rows, width = tokens_ref.shape
    band = min(64, rows)

    def norm_band(i, carry):
        span = pl.ds(pl.multiple_of(i * band, band), band)
        value = tokens_ref[span, :].astype(jnp.float32)
        centered = value - jnp.mean(value, axis=1, keepdims=True)
        inverse = lax.rsqrt(jnp.mean(centered * centered, axis=1, keepdims=True) + epsilon)
        act_ref[span, :] = (centered * inverse * gain + shift).astype(jnp.bfloat16)
        return carry

    lax.fori_loop(0, rows // band, norm_band, 0)
    columns = weight.shape[1]
    tile = min(512, columns)

    def multiply(owner, cols):
        depth = pl.ds(pl.multiple_of(owner * shard, shard), shard)
        return dot_nn(act_ref[:, depth], weight[depth, cols])

    def first_tile(n, carry):
        cols = pl.ds(pl.multiple_of(n * tile, tile), tile)
        total[:, cols] = multiply(place.w, cols) + multiply(place.sib, cols)
        return carry

    def last_tile(n, carry):
        cols = pl.ds(pl.multiple_of(n * tile, tile), tile)
        value = total[:, cols] + multiply(place.far, cols) + multiply(place.diag, cols)
        qkv_ref[:, cols] = value.astype(jnp.bfloat16)
        return carry

    own[0].wait()
    nears[0].wait_recv()
    lax.fori_loop(0, columns // tile, first_tile, 0)
    for n in range(pieces):
        pass_on(0, n)
        if n >= 1:
            pass_pair(0, n - 1)
    pass_pair(0, pieces - 1)
    for n in range(pieces):
        relays[0, n].wait_recv()
        pair_relays[0, n].wait_recv()
    keep = pltpu.make_async_copy(weight, weight_out, own_sem.at[4])
    keep.start()
    lax.fori_loop(0, columns // tile, last_tile, 0)
    for k in range(owners):
        dispatch.forward(k)
        if k >= 2:
            dispatch.relay(k - 2)
    for n in range(pieces):
        pass_on(1, n)
        if n >= 1:
            pass_pair(1, n - 1)
    pass_pair(1, pieces - 1)
    for k in range(owners - 2, owners):
        dispatch.relay(k)
    for k in range(owners):
        dispatch.ready(k)
    for n in range(pieces):
        relays[1, n].wait_recv()
        pair_relays[1, n].wait_recv()
    nears[1].wait_recv()
    own[1].wait()
    keep.wait()
    for copy in smalls:
        copy.wait_send()
    for group in (hops, nears, pairs, relays, pair_relays):
        for copy in group.values():
            copy.wait_send()
    dispatch.drain()


def run_front(owners, capacity, tokens, small, w_qkv, w_out, grads):
    rows, width = tokens.shape
    shard, columns = w_qkv.shape
    experts = grads.shape[1]
    pieces = 4
    any_spec = pl.BlockSpec(memory_space=pl.ANY)
    vmem_spec = pl.BlockSpec(memory_space=pltpu.VMEM)
    bf16 = jnp.bfloat16
    dma = pltpu.SemaphoreType.DMA
    return pl.pallas_call(
        functools.partial(front_kernel, (owners, capacity, pieces)),
        out_shape=(
            jax.ShapeDtypeStruct((rows, columns), bf16),
            jax.ShapeDtypeStruct((rows, width), bf16),
            jax.ShapeDtypeStruct((4,) + small.shape, bf16),
            jax.ShapeDtypeStruct((4 * shard, width), bf16),
            jax.ShapeDtypeStruct((experts, owners * 4 * capacity, width), bf16),
            jax.ShapeDtypeStruct((4 * shard, columns), bf16),
        ),
        in_specs=[vmem_spec] + [any_spec] * 4,
        out_specs=(vmem_spec, vmem_spec, vmem_spec, any_spec, any_spec, any_spec),
        scratch_shapes=[
            pltpu.VMEM((4,) + small.shape, bf16),
            pltpu.VMEM((4 * shard, columns), bf16),
            pltpu.VMEM((rows, columns), jnp.float32),
            dma((5,)),
            dma((4, owners)),
            dma((4, owners)),
            dma((3,)),
            dma((3,)),
            dma((2,)),
            dma((2,)),
        ]
        + [dma((2, pieces)) for _ in range(8)],
        compiler_params=pltpu.CompilerParams(
            collective_id=0, has_side_effects=True, vmem_limit_bytes=VMEM_LIMIT
        ),
        name="front",
    )(tokens, small, w_qkv, w_out, grads)


def masked_softmax(scores):
    exponent = jnp.exp(scores - jnp.max(scores, axis=1, keepdims=True))
    return exponent * (1.0 / jnp.sum(exponent, axis=1, keepdims=True))


def attend_head(query, key, value, prefix_len):
    half = query.shape[0] // 2
    query = query * (1.0 / math.sqrt(HEAD_DIM))
    row = lax.broadcasted_iota(jnp.int32, (half, half), 0)
    col = lax.broadcasted_iota(jnp.int32, (half, half), 1)
    low = dot_nt(query[:half], key[:half])
    low = jnp.where((col <= row) | (col < prefix_len), low, -1e30)
    low = masked_softmax(low).astype(jnp.bfloat16)
    high = dot_nt(query[half:], key)
    high = jnp.concatenate(
        [high[:, :half], jnp.where(col <= row, high[:, half:], -1e30)], axis=1
    )
    high = masked_softmax(high).astype(jnp.bfloat16)
    return low, high, dot_nn(low, value[:half]), dot_nn(high, value)


def attend_kernel(prefix_ref, query_ref, key_ref, value_ref, merged_ref, low_ref, high_ref):
    half = query_ref.shape[0] // 2
    for head in range(2):
        part = slice(head * HEAD_DIM, (head + 1) * HEAD_DIM)
        low, high, top, bottom = attend_head(
            query_ref[:, part], key_ref[:, part], value_ref[:, part], prefix_ref[0]
        )
        low_ref[head] = low
        high_ref[head] = high
        merged_ref[:half, part] = top.astype(jnp.bfloat16)
        merged_ref[half:, part] = bottom.astype(jnp.bfloat16)


def attend(qkv, prefix):
    rows, columns = qkv.shape
    width = columns // 3
    pairs = width // LANES
    half = rows // 2

    def column(part):
        return pl.BlockSpec((rows, LANES), lambda i, _: (0, part * pairs + i))

    return pl.pallas_call(
        attend_kernel,
        grid_spec=pltpu.PrefetchScalarGridSpec(
            num_scalar_prefetch=1,
            grid=(pairs,),
            in_specs=[column(0), column(1), column(2)],
            out_specs=[
                pl.BlockSpec((rows, LANES), lambda i, _: (0, i)),
                pl.BlockSpec((2, half, half), lambda i, _: (i, 0, 0)),
                pl.BlockSpec((2, half, rows), lambda i, _: (i, 0, 0)),
            ],
        ),
        out_shape=(
            jax.ShapeDtypeStruct((rows, width), jnp.bfloat16),
            jax.ShapeDtypeStruct((2 * pairs, half, half), jnp.bfloat16),
            jax.ShapeDtypeStruct((2 * pairs, half, rows), jnp.bfloat16),
        ),
        name="attend",
    )(prefix, qkv, qkv, qkv)


def score_grads(probs, grad_probs):
    probs = probs.astype(jnp.float32)
    weighted = probs * grad_probs
    total = jnp.sum(weighted, axis=1, keepdims=True)
    return (weighted - probs * total).astype(jnp.bfloat16)


def attend_back_head(query, key, value, low, high, grad):
    half = query.shape[0] // 2
    scale = 1.0 / math.sqrt(HEAD_DIM)
    query = query * scale
    grad_low = score_grads(low, dot_nt(grad[:half], value[:half]))
    grad_high = score_grads(high, dot_nt(grad[half:], value))
    grad_query = jnp.concatenate(
        [dot_nn(grad_low, key[:half]), dot_nn(grad_high, key)], axis=0
    )
    value_all = dot_tn(high, grad[half:])
    key_all = dot_tn(grad_high, query[half:])
    grad_value = jnp.concatenate(
        [value_all[:half] + dot_tn(low, grad[:half]), value_all[half:]], axis=0
    )
    grad_key = jnp.concatenate(
        [key_all[:half] + dot_tn(grad_low, query[:half]), key_all[half:]], axis=0
    )
    return (
        (grad_query * scale).astype(jnp.bfloat16),
        grad_key.astype(jnp.bfloat16),
        grad_value.astype(jnp.bfloat16),
    )


def attend_back_kernel(query_ref, key_ref, value_ref, low_ref, high_ref, grad_ref, out_ref):
    for head in range(2):
        part = slice(head * HEAD_DIM, (head + 1) * HEAD_DIM)
        results = attend_back_head(
            query_ref[:, part], key_ref[:, part], value_ref[:, part],
            low_ref[head], high_ref[head], grad_ref[:, part],
        )
        for i in range(3):
            out_ref[i, :, part] = results[i]


def attend_back(qkv, low, high, grad_merged):
    rows, columns = qkv.shape
    width = columns // 3
    pairs = width // LANES
    half = rows // 2

    def column(part):
        return pl.BlockSpec((rows, LANES), lambda i: (0, part * pairs + i))

    return pl.pallas_call(
        attend_back_kernel,
        grid=(pairs,),
        in_specs=[
            column(0), column(1), column(2),
            pl.BlockSpec((2, half, half), lambda i: (i, 0, 0)),
            pl.BlockSpec((2, half, rows), lambda i: (i, 0, 0)),
            column(0),
        ],
        out_specs=pl.BlockSpec((3, rows, LANES), lambda i: (0, 0, i)),
        out_shape=jax.ShapeDtypeStruct((3, rows, width), jnp.bfloat16),
        name="attend_back",
    )(qkv, qkv, qkv, low, high, grad_merged)


class Reduce:
    def __init__(self, place, part, got, mid, far, half, pair, slim, lines, done, sems):
        self.p = place
        self.part, self.got, self.mid, self.far = part, got, mid, far
        self.half, self.pair, self.slim, self.lines, self.done = half, pair, slim, lines, done
        (self.send, self.recv, self.line_send, self.line_recv) = sems
        self.copies = {}
        self.shard = done.shape[1]
        self.halves = self.shard // 2
        self.count = place.owners // 2
        self.slice = self.halves // self.count
        self.bit = lax.rem(place.e, 2)
        self.level = lax.div(place.e, 2)

    def go(self, name, n, step, src, dst, device):
        copy = remote(src, dst, self.send.at[step, n], self.recv.at[step, n], device)
        copy.start()
        self.copies[name, n] = copy

    def swap(self, n):
        self.go(
            "swap", n, 0, self.part.at[n, :, 1 - self.p.c], self.got.at[n], (self.p.e, self.p.sib)
        )

    def pair_sum(self, n, side):
        return self.part[n, side, self.p.c].astype(jnp.float32) + self.got[n, side].astype(
            jnp.float32
        )

    def cross(self, n):
        self.copies["swap", n].wait_recv()
        self.mid[n] = self.pair_sum(n, 1 - self.p.x).astype(jnp.bfloat16)
        self.go("cross", n, 1, self.mid.at[n], self.far.at[n], (self.p.e, self.p.far))

    def fold(self, n):
        self.copies["cross", n].wait_recv()
        total = self.pair_sum(n, self.p.x) + self.far[n].astype(jnp.float32)
        self.half[n] = total.astype(jnp.bfloat16)
        other = pl.multiple_of((1 - self.bit) * self.halves, self.halves)
        self.go(
            "fold", n, 2, self.half.at[n, pl.ds(other, self.halves)], self.pair.at[n],
            (self.p.pair, self.p.w),
        )

    def spread(self, n):
        self.copies["fold", n].wait_recv()
        own = pl.multiple_of(self.bit * self.halves, self.halves)
        total = self.half[n, pl.ds(own, self.halves), :].astype(jnp.float32) + self.pair[
            n
        ].astype(jnp.float32)
        self.slim[n] = total.astype(jnp.bfloat16)
        for k in range(1, self.count):
            target = lax.rem(self.level + k, self.count)
            start = pl.multiple_of(target * self.slice, self.slice)
            copy = remote(
                self.slim.at[n, pl.ds(start, self.slice)], self.lines.at[n, k],
                self.line_send.at[0, n, k], self.line_recv.at[0, n, k],
                (self.p.ahead(2 * k), self.p.w),
            )
            copy.start()
            self.copies["spread", n, k] = copy

    def collect(self, n):
        start = pl.multiple_of(self.level * self.slice, self.slice)
        total = self.slim[n, pl.ds(start, self.slice), :].astype(jnp.float32)
        for k in range(1, self.count):
            self.copies["spread", n, k].wait_recv()
            total = total + self.lines[n, k].astype(jnp.float32)
        row = pl.multiple_of(self.bit * self.halves + self.level * self.slice, self.slice)
        self.done[n, pl.ds(row, self.slice), :] = total.astype(jnp.bfloat16)
        part = self.done.at[n, pl.ds(row, self.slice)]
        for k in range(1, self.count):
            copy = remote(
                part, part, self.line_send.at[1, n, k], self.line_recv.at[1, n, k],
                (self.p.ahead(2 * k), self.p.w),
            )
            copy.start()
            self.copies["collect", n, k] = copy

    def share(self, n):
        for k in range(1, self.count):
            self.copies["collect", n, k].wait_recv()
        own = pl.multiple_of(self.bit * self.halves, self.halves)
        part = self.done.at[n, pl.ds(own, self.halves)]
        self.go("share", n, 3, part, part, (self.p.pair, self.p.w))

    def finish(self, n):
        self.copies["share", n].wait_recv()

    def drain(self):
        for copy in self.copies.values():
            copy.wait_send()


def tail_kernel(
    dims,
    act_ref, grads_ref, weight_ref, tokens_ref, hidden_ref, merged_ref, attn_ref, gain_ref, small_ref,
    tokens_out, qkv_out, out_out, small_out,
    act_t, merged_t, part, got, mid, far, half, pair, slim, lines, done,
    small, small_part, small_got, small_mid, small_far, small_sum, small_all,
    send, recv, line_send, line_recv, small_send, small_recv, all_send, all_recv, out_sem,
):
    owners, out_chunks, chunks = dims
    place = Place(owners)
    greet(
        [(place.ahead(k), place.w) for k in range(1, owners)]
        + [(place.e, place.sib), (place.e, place.far)]
    )
    reduce = Reduce(
        place, part, got, mid, far, half, pair, slim, lines, done,
        (send, recv, line_send, line_recv),
    )
    rows, width = tokens_ref.shape
    shard = width // 4
    tile = part.shape[-1]
    merged_t[...] = merged_ref[...].T
    act_t[...] = act_ref[...].T

    def weight_grad(n):
        if n < out_chunks:
            left, right = merged_t, attn_ref[:, n * tile : (n + 1) * tile]
        else:
            start = (n - out_chunks) * tile
            right = grads_ref[start // width, :, start % width : start % width + tile]
            left = act_t
        for owner in range(4):
            value = dot_nn(left[owner * shard : (owner + 1) * shard, :], right)
            part[n, owner // 2, owner % 2] = value.astype(jnp.bfloat16)

    band = min(128, rows)
    bands = rows // band
    small[...] = small_ref[...]

    def norm_band(i):
        span = slice(i * band, (i + 1) * band)
        grad = sum(
            dot_nt(grads_ref[part_of, span, :], weight_ref[:, part_of * width : (part_of + 1) * width])
            for part_of in range(3)
        )
        value = tokens_ref[span, :].astype(jnp.float32)
        centered = value - jnp.mean(value, axis=1, keepdims=True)
        inverse = lax.rsqrt(jnp.mean(centered * centered, axis=1, keepdims=True) + epsilon)
        scaled = centered * inverse
        weighted = grad * gain_ref[...]
        mean_one = jnp.mean(weighted, axis=1, keepdims=True)
        mean_two = jnp.mean(weighted * scaled, axis=1, keepdims=True)
        tokens_out[span, :] = hidden_ref[span, :] + inverse * (
            weighted - mean_one - scaled * mean_two
        )
        small[0:1, :] += jnp.sum(grad * scaled, axis=0, keepdims=True)
        small[1:2, :] += jnp.sum(grad, axis=0, keepdims=True)

    stages = [
        reduce.cross, reduce.fold, reduce.spread, reduce.collect, reduce.share, reduce.finish,
    ]
    small_copies = []

    def small_swap():
        for owner in range(4):
            small_part[owner // 2, owner % 2] = small[:, owner * shard : (owner + 1) * shard]
        copy = remote(
            small_part.at[:, 1 - place.c], small_got, small_send.at[0], small_recv.at[0],
            (place.e, place.sib),
        )
        copy.start()
        small_copies.append(copy)

    def small_cross():
        small_copies[0].wait_recv()
        small_mid[...] = small_part[1 - place.x, place.c] + small_got[1 - place.x]
        copy = remote(
            small_mid, small_far, small_send.at[1], small_recv.at[1], (place.e, place.far)
        )
        copy.start()
        small_copies.append(copy)

    def small_spread():
        small_copies[1].wait_recv()
        small_sum[...] = small_part[place.x, place.c] + small_got[place.x] + small_far[...]
        for k in range(1, owners):
            copy = remote(
                small_sum, small_all.at[k], all_send.at[k], all_recv.at[k],
                (place.ahead(k), place.w),
            )
            copy.start()
            small_copies.append(copy)

    def small_finish():
        total = small_sum[...]
        for k in range(1, owners):
            small_copies[1 + k].wait_recv()
            total = total + small_all[k]
        small_out[...] = total

    def store(n):
        if n < out_chunks:
            target = out_out.at[:, pl.ds(n * tile, tile)]
        else:
            target = qkv_out.at[:, pl.ds((n - out_chunks) * tile, tile)]
        return pltpu.make_async_copy(done.at[n], target, out_sem.at[n])

    stores = {}
    smalls = [small_swap, small_cross, small_spread, small_finish]
    for slot in range(chunks + len(stages)):
        if slot < chunks:
            weight_grad(slot)
            reduce.swap(slot)
        for s in range(len(stages) - 1, -1, -1):
            n = slot - 1 - s
            if 0 <= n < chunks:
                stages[s](n)
                if s == len(stages) - 1:
                    stores[n] = store(n)
                    stores[n].start()
        if slot >= chunks - bands and slot < chunks:
            norm_band(slot - (chunks - bands))
        if slot >= chunks and smalls:
            smalls.pop(0)()
    for copy in stores.values():
        copy.wait()
    reduce.drain()
    for copy in small_copies:
        copy.wait_send()


def run_tail(owners, act_one, grad_qkv, weight, tokens, grad_hidden, merged, grad_attn, gain, small):
    rows, width = tokens.shape
    shard = width // 4
    tile = min(512, width)
    out_chunks = width // tile
    chunks = 4 * out_chunks
    count = owners // 2
    half = shard // 2
    any_spec = pl.BlockSpec(memory_space=pl.ANY)
    vmem_spec = pl.BlockSpec(memory_space=pltpu.VMEM)
    bf16, f32 = jnp.bfloat16, jnp.float32
    dma = pltpu.SemaphoreType.DMA
    lead = small.shape[0]

    def vm(*shape):
        return pltpu.VMEM(shape, bf16)

    return pl.pallas_call(
        functools.partial(tail_kernel, (owners, out_chunks, chunks)),
        out_shape=(
            jax.ShapeDtypeStruct((rows, width), f32),
            jax.ShapeDtypeStruct((shard, 3 * width), bf16),
            jax.ShapeDtypeStruct((shard, width), bf16),
            jax.ShapeDtypeStruct((lead, shard), f32),
        ),
        in_specs=[vmem_spec] * 9,
        out_specs=(vmem_spec, any_spec, any_spec, vmem_spec),
        scratch_shapes=[
            vm(width, rows),
            vm(width, rows),
            vm(chunks, 2, 2, shard, tile),
            vm(chunks, 2, shard, tile),
            vm(chunks, shard, tile),
            vm(chunks, shard, tile),
            vm(chunks, shard, tile),
            vm(chunks, half, tile),
            vm(chunks, half, tile),
            vm(chunks, count, half // count, tile),
            vm(chunks, shard, tile),
            pltpu.VMEM((lead, width), f32),
            pltpu.VMEM((2, 2, lead, shard), f32),
            pltpu.VMEM((2, lead, shard), f32),
            pltpu.VMEM((lead, shard), f32),
            pltpu.VMEM((lead, shard), f32),
            pltpu.VMEM((lead, shard), f32),
            pltpu.VMEM((owners, lead, shard), f32),
            dma((4, chunks)),
            dma((4, chunks)),
            dma((2, chunks, count)),
            dma((2, chunks, count)),
            dma((2,)),
            dma((2,)),
            dma((owners,)),
            dma((owners,)),
            dma((chunks,)),
        ],
        compiler_params=pltpu.CompilerParams(
            collective_id=2, has_side_effects=True, vmem_limit_bytes=VMEM_LIMIT
        ),
        name="tail",
    )(act_one, grad_qkv, weight, tokens, grad_hidden, merged, grad_attn, gain, small)


def on_device_plain(
    tokens,
    norm1_gain,
    norm1_shift,
    w_qkv,
    w_out,
    norm2_gain,
    norm2_shift,
    w_router,
    w_up,
    w_down,
    routes,
    priority,
    prefix,
    cotangent,
):
    row_count, model_width = tokens.shape
    expert_count = w_router.shape[1]
    capacity = row_count // expert_count
    owners = lax.axis_size("expert")
    local_experts = w_up.shape[0]
    slot_count = expert_count * capacity
    prefix_len = prefix[0]
    small = jnp.concatenate(
        [
            norm1_gain[None],
            norm1_shift[None],
            norm2_gain[None],
            norm2_shift[None],
            w_router.T,
        ],
        axis=0,
    )
    qkv_full = lax.all_gather(w_qkv, "wshard", axis=0, tiled=True)
    small_full = lax.all_gather(small, "wshard", axis=1, tiled=True)
    out_full = lax.all_gather(w_out, "wshard", axis=0, tiled=True)
    gain_one, shift_one, gain_two, shift_two = (small_full[i] for i in range(4))
    router_full = small_full[4:].T
    gain_one = gain_one.astype(jnp.float32)
    gain_two = gain_two.astype(jnp.float32)
    inputs = tokens.astype(jnp.float32)
    normed_one, scaled_one, inverse_one = normalize(inputs, gain_one, shift_one.astype(jnp.float32))
    act_one = normed_one.astype(jnp.bfloat16)
    qkv = jnp.dot(act_one, qkv_full, preferred_element_type=jnp.float32).astype(jnp.bfloat16)
    query_heads = qkv[:, :model_width]
    key_heads = qkv[:, model_width : 2 * model_width]
    value_heads = qkv[:, 2 * model_width :]
    merged, log_totals = attend_forward(query_heads, key_heads, value_heads, prefix_len)
    attn_out = jnp.dot(merged, out_full, preferred_element_type=jnp.float32)
    hidden = inputs + attn_out
    normed_two, scaled_two, inverse_two = normalize(hidden, gain_two, shift_two.astype(jnp.float32))
    act_two = normed_two.astype(jnp.bfloat16)
    logits = jnp.dot(act_two, router_full, preferred_element_type=jnp.float32)
    row_max = jnp.max(logits, axis=-1, keepdims=True)
    exponent = jnp.exp(logits - row_max)
    gate_prob = exponent / jnp.sum(exponent, axis=-1, keepdims=True)
    route_ids = routes[:, 0]
    chosen = route_ids[:, None] == jnp.arange(expert_count, dtype=jnp.int32)[None, :]
    gate_value = jnp.sum(jnp.where(chosen, gate_prob, 0.0), axis=1)
    slot_index, slot_source = assign_slots(route_ids, priority[0], expert_count, capacity)
    zero_row = jnp.zeros((1, model_width), jnp.bfloat16)
    padded = jnp.concatenate([act_two, zero_row], axis=0)
    send_rows = padded[slot_source].reshape(owners, local_experts * capacity, model_width)
    arrived = lax.all_to_all(send_rows, "expert", split_axis=0, concat_axis=0, tiled=True).reshape(
        owners, local_experts, capacity, model_width
    )
    group = lax.axis_size("wshard")
    local_rows = owners * capacity

    def by_expert(chunk):
        rows = jnp.transpose(chunk, (1, 0, 2, 3)).reshape(local_experts, local_rows, model_width)
        return lax.all_gather(rows, "wshard", axis=1, tiled=True)

    def home_rows(rows):
        own = lax.psum_scatter(rows.astype(jnp.bfloat16), "wshard", scatter_dimension=1, tiled=True)
        own = own.reshape(local_experts, owners, capacity, model_width)
        return jnp.transpose(own, (1, 0, 2, 3)).reshape(
            owners, local_experts * capacity, model_width
        )

    grad_output = cotangent.astype(jnp.float32)
    grad_combined = (gate_value[:, None] * grad_output).astype(jnp.bfloat16)
    grad_padded = jnp.concatenate([grad_combined, zero_row], axis=0)
    grad_send = grad_padded[slot_source].reshape(owners, local_experts * capacity, model_width)
    grad_arrived = lax.all_to_all(
        grad_send, "expert", split_axis=0, concat_axis=0, tiled=True
    ).reshape(owners, local_experts, capacity, model_width)
    rows_in = by_expert(arrived)
    grad_rows = by_expert(grad_arrived)
    pre_act = jnp.einsum("erd,edf->erf", rows_in, w_up, preferred_element_type=jnp.float32)
    activated, gelu_pull = jax.vjp(gelu_tanh, pre_act)
    act_hidden = activated.astype(jnp.bfloat16)
    produced = jnp.einsum(
        "erf,efd->erd", act_hidden, w_down, preferred_element_type=jnp.float32
    )
    expert_out = home_rows(produced)
    returned = lax.all_to_all(expert_out, "expert", split_axis=0, concat_axis=0, tiled=True)
    slots_back = jnp.concatenate([returned.reshape(slot_count, model_width), zero_row], axis=0)
    combined = slots_back[slot_index].astype(jnp.float32)
    output = (hidden + gate_value[:, None] * combined).astype(jnp.bfloat16)
    grad_gate = jnp.sum(grad_output * combined, axis=1)
    grad_down = jnp.einsum(
        "erf,erd->efd", act_hidden, grad_rows, preferred_element_type=jnp.float32
    )
    grad_hidden_units = jnp.einsum(
        "erd,efd->erf", grad_rows, w_down, preferred_element_type=jnp.float32
    )
    grad_pre = gelu_pull(grad_hidden_units)[0].astype(jnp.bfloat16)
    grad_up = jnp.einsum("erd,erf->edf", rows_in, grad_pre, preferred_element_type=jnp.float32)
    grad_expert_in = jnp.einsum(
        "erf,edf->erd", grad_pre, w_up, preferred_element_type=jnp.float32
    )
    grad_send_back = home_rows(grad_expert_in)
    grad_back = lax.all_to_all(grad_send_back, "expert", split_axis=0, concat_axis=0, tiled=True)
    grad_slots = jnp.concatenate([grad_back.reshape(slot_count, model_width), zero_row], axis=0)
    grad_act_two = grad_slots[slot_index].astype(jnp.float32)
    grad_logits = (
        gate_prob * (jnp.where(chosen, grad_gate[:, None], 0.0) - (gate_value * grad_gate)[:, None])
    ).astype(jnp.bfloat16)
    grad_router = contract_rows(act_two, grad_logits)
    grad_act_two = grad_act_two + times_transpose(grad_logits, router_full)
    grad_from_two, grad_gain_two, grad_shift_two = norm_back(
        grad_act_two, scaled_two, inverse_two, gain_two
    )
    grad_hidden = grad_output + grad_from_two
    grad_attn = grad_hidden.astype(jnp.bfloat16)
    grad_out_w = contract_rows(merged, grad_attn)
    grad_merged = times_transpose(grad_attn, out_full).astype(jnp.bfloat16)
    grad_qkv = attend_backward(
        query_heads, key_heads, value_heads, grad_merged, log_totals, prefix_len
    )
    grad_qkv_w = contract_rows(act_one, grad_qkv)
    grad_act_one = times_transpose(grad_qkv, qkv_full)
    grad_from_one, grad_gain_one, grad_shift_one = norm_back(
        grad_act_one, scaled_one, inverse_one, gain_one
    )
    grad_tokens = grad_hidden + grad_from_one
    small_grad = jnp.concatenate(
        [
            grad_gain_one[None],
            grad_shift_one[None],
            grad_gain_two[None],
            grad_shift_two[None],
            grad_router.T,
        ],
        axis=0,
    )
    out_share = lax.psum_scatter(
        grad_out_w.astype(jnp.bfloat16), "wshard", scatter_dimension=0, tiled=True
    )
    qkv_share = lax.psum_scatter(
        grad_qkv_w.astype(jnp.bfloat16), "wshard", scatter_dimension=0, tiled=True
    )
    small_share = lax.psum_scatter(small_grad, "wshard", scatter_dimension=1, tiled=True)
    out_total = lax.psum(out_share, "expert").astype(jnp.float32)
    qkv_total = lax.psum(qkv_share, "expert").astype(jnp.float32)
    small_total = lax.psum(small_share, "expert")
    totals = (
        small_total[0],
        small_total[1],
        qkv_total,
        out_total,
        small_total[2],
        small_total[3],
        small_total[4:].T,
    )
    return (
        output,
        grad_tokens,
        totals[0],
        totals[1],
        totals[2],
        totals[3],
        totals[4],
        totals[5],
        totals[6],
        grad_up,
        grad_down,
    )


def on_device(
    tokens,
    norm1_gain,
    norm1_shift,
    w_qkv,
    w_out,
    norm2_gain,
    norm2_shift,
    w_router,
    w_up,
    w_down,
    routes,
    priority,
    prefix,
    cotangent,
):
    row_count, model_width = tokens.shape
    expert_count = w_router.shape[1]
    capacity = row_count // expert_count
    owners = lax.axis_size("expert")
    local_experts = w_up.shape[0]
    slot_count = expert_count * capacity
    prefix_len = prefix[0]
    route_ids = routes[:, 0]
    slot_index, slot_source = assign_slots(route_ids, priority[0], expert_count, capacity)
    zero_row = jnp.zeros((1, model_width), jnp.bfloat16)

    def to_slots(values):
        padded = jnp.concatenate([values, zero_row], axis=0)
        return padded[slot_source].reshape(owners, local_experts, capacity, model_width)

    def from_slots(values):
        padded = jnp.concatenate([values.reshape(slot_count, model_width), zero_row], axis=0)
        return padded[slot_index].astype(jnp.float32)

    small = jnp.concatenate(
        [norm1_gain[None], norm1_shift[None], norm2_gain[None], norm2_shift[None], w_router.T],
        axis=0,
    )
    small_rows = small.shape[0]
    small = jnp.pad(small, ((0, -small_rows % 16), (0, 0)))
    qkv, act_one, small_full, out_full, grad_rows, w_qkv_full = run_front(
        owners, capacity, tokens, small, w_qkv, w_out, to_slots(cotangent)
    )
    small_full = jnp.transpose(small_full, (1, 0, 2)).reshape(-1, model_width)
    gain_one, shift_one, gain_two, shift_two = (
        small_full[i].astype(jnp.float32) for i in range(4)
    )
    router_full = small_full[4:small_rows].T
    router_wide = jnp.pad(router_full, ((0, 0), (0, LANES - expert_count)))
    inputs = tokens.astype(jnp.float32)
    merged, low, high = attend(qkv, prefix)
    attn_out = jnp.dot(merged, out_full, preferred_element_type=jnp.float32)
    hidden = inputs + attn_out
    normed_two, scaled_two, inverse_two = normalize(hidden, gain_two, shift_two)
    act_two = normed_two.astype(jnp.bfloat16)
    logits = jnp.dot(act_two, router_full, preferred_element_type=jnp.float32)
    gate_prob = jax.nn.softmax(logits, axis=-1)
    chosen = route_ids[:, None] == jnp.arange(expert_count, dtype=jnp.int32)[None, :]
    gate_value = jnp.sum(jnp.where(chosen, gate_prob, 0.0), axis=1)
    home_out, home_grad, rows, scaled, act_hidden, grad_pre, grad_router = run_experts(
        owners, capacity, expert_count, to_slots(act_two), grad_rows, w_up, w_down, router_wide
    )
    grad_down = jnp.einsum("erf,erd->efd", act_hidden, scaled, preferred_element_type=jnp.float32)
    grad_up = jnp.einsum("erd,erf->edf", rows, grad_pre, preferred_element_type=jnp.float32)
    combined = from_slots(home_out)
    output = (hidden + gate_value[:, None] * combined).astype(jnp.bfloat16)
    grad_output = cotangent.astype(jnp.float32)
    grad_act_two = from_slots(home_grad)
    grad_from_two, grad_gain_two, grad_shift_two = norm_back(
        grad_act_two, scaled_two, inverse_two, gain_two
    )
    grad_hidden = grad_output + grad_from_two
    grad_attn = grad_hidden.astype(jnp.bfloat16)
    grad_merged = times_transpose(grad_attn, out_full).astype(jnp.bfloat16)
    grad_qkv = attend_back(qkv, low, high, grad_merged)
    small_grad = jnp.concatenate(
        [
            jnp.zeros((2, model_width), jnp.float32),
            grad_gain_two[None],
            grad_shift_two[None],
            grad_router[:expert_count],
        ],
        axis=0,
    )
    small_grad = jnp.pad(small_grad, ((0, -small_rows % 8), (0, 0)))
    grad_tokens, qkv_total, out_total, small_total = run_tail(
        owners, act_one, grad_qkv, w_qkv_full, tokens, grad_hidden, merged, grad_attn,
        gain_one[None], small_grad,
    )
    return (
        output,
        grad_tokens,
        small_total[0],
        small_total[1],
        qkv_total.astype(jnp.float32),
        out_total.astype(jnp.float32),
        small_total[2],
        small_total[3],
        small_total[4:small_rows].T,
        grad_up,
        grad_down,
    )


def solution(mesh):
    placed = (
        P(("expert", "wshard"), None),
        P("wshard"),
        P("wshard"),
        P("wshard", None),
        P("wshard", None),
        P("wshard"),
        P("wshard"),
        P("wshard", None),
        P("expert", None, "wshard"),
        P("expert", "wshard", None),
        P(("expert", "wshard"), None),
        P(("expert", "wshard"), None),
        P(("expert", "wshard")),
        P(("expert", "wshard"), None),
    )
    owners, group = mesh.shape["expert"], mesh.shape["wshard"]

    def body(*args):
        capacity = args[0].shape[0] // args[7].shape[1]
        fits = group == 4 and owners % 2 == 0 and capacity % 16 == 0
        return (on_device if fits else on_device_plain)(*args)

    return jax.shard_map(
        body,
        mesh=mesh,
        in_specs=placed,
        out_specs=(
            P(("expert", "wshard"), None),
            P(("expert", "wshard"), None),
            P("wshard"),
            P("wshard"),
            P("wshard", None),
            P("wshard", None),
            P("wshard"),
            P("wshard"),
            P("wshard", None),
            P("expert", None, "wshard"),
            P("expert", "wshard", None),
        ),
        check_vma=False,
    )
```

```python
import functools
import math

import jax
import jax.numpy as jnp
from jax import lax
from jax.experimental import pallas as pl
from jax.experimental.pallas import tpu as pltpu
from jax.sharding import PartitionSpec as P

HEADS = 16
HEAD_DIM = 64


epsilon = 1e-05
VMEM_LIMIT = 66_000_000


def normalize(values, gain_vec, shift_vec):
    row_mean = jnp.mean(values, axis=-1, keepdims=True)
    centered = values - row_mean
    inverse = lax.rsqrt(jnp.mean(centered * centered, axis=-1, keepdims=True) + epsilon)
    scaled = centered * inverse
    return (scaled * gain_vec + shift_vec, scaled, inverse)


def norm_back(grad_rows, scaled, inverse, gain_vec):
    weighted = grad_rows * gain_vec
    mean_one = jnp.mean(weighted, axis=-1, keepdims=True)
    mean_two = jnp.mean(weighted * scaled, axis=-1, keepdims=True)
    grad_inputs = inverse * (weighted - mean_one - scaled * mean_two)
    return (grad_inputs, jnp.sum(grad_rows * scaled, axis=0), jnp.sum(grad_rows, axis=0))


def contract_rows(left, right):
    return lax.dot_general(
        left, right, (((0,), (0,)), ((), ())), preferred_element_type=jnp.float32
    )


def times_transpose(left, right):
    return lax.dot_general(
        left, right, (((1,), (1,)), ((), ())), preferred_element_type=jnp.float32
    )


def gelu_tanh(values):
    return jax.nn.gelu(values, approximate=True)


def assign_slots(route_ids, order_ids, expert_count, capacity):
    token_count = route_ids.shape[0]
    same_expert = route_ids[:, None] == route_ids[None, :]
    earlier = order_ids[None, :] < order_ids[:, None]
    rank_ids = jnp.sum((same_expert & earlier).astype(jnp.int32), axis=1)
    is_kept = rank_ids < capacity
    slot_index = jnp.where(is_kept, route_ids * capacity + rank_ids, expert_count * capacity)
    slot_ids = jnp.arange(expert_count * capacity, dtype=jnp.int32)
    match_table = slot_index[None, :] == slot_ids[:, None]
    token_ids = jnp.arange(token_count, dtype=jnp.int32)
    filled = jnp.any(match_table, axis=1)
    picked = jnp.sum(jnp.where(match_table, token_ids[None, :], 0), axis=1)
    slot_source = jnp.where(filled, picked, token_count)
    return (slot_index, slot_source)


def group_heads(values, groups):
    token_count = values.shape[0]
    return jnp.transpose(values.reshape(token_count, groups, -1, HEAD_DIM), (1, 0, 2, 3))


def block_scores(query_block, key_group, block_start, prefix_len):
    block_rows = query_block.shape[0]
    key_count = key_group.shape[0]
    scores = jnp.einsum(
        "qgd,kgd->gqk", query_block, key_group, preferred_element_type=jnp.float32
    ) * (1.0 / math.sqrt(HEAD_DIM))
    query_pos = block_start + jnp.arange(block_rows, dtype=jnp.int32)
    key_pos = jnp.arange(key_count, dtype=jnp.int32)
    allowed = (key_pos[None, :] <= query_pos[:, None]) | (key_pos[None, :] < prefix_len)
    return jnp.where(allowed[None], scores, -1e30)


def attend_forward(query_heads, key_heads, value_heads, prefix_len):
    token_count = query_heads.shape[0]
    group_size = min(4, HEADS)
    groups = HEADS // group_size
    block_rows = min(512, token_count)
    blocks = token_count // block_rows
    starts = jnp.arange(blocks, dtype=jnp.int32) * block_rows

    def one_group(group_item):
        query_group, key_group, value_group = group_item
        query_blocks = query_group.reshape(blocks, block_rows, group_size, HEAD_DIM)

        def one_block(block_item):
            query_block, block_start = block_item
            scores = block_scores(query_block, key_group, block_start, prefix_len)
            row_max = jnp.max(scores, axis=-1, keepdims=True)
            exponent = jnp.exp(scores - row_max)
            row_total = jnp.sum(exponent, axis=-1, keepdims=True)
            attn_probs = (exponent / row_total).astype(jnp.bfloat16)
            result = jnp.einsum(
                "gqk,kgd->qgd", attn_probs, value_group, preferred_element_type=jnp.float32
            )
            return (result, (row_max + jnp.log(row_total))[..., 0])

        return lax.map(one_block, (query_blocks, starts))

    attended, log_totals = lax.map(
        one_group,
        (
            group_heads(query_heads, groups),
            group_heads(key_heads, groups),
            group_heads(value_heads, groups),
        ),
    )
    merged = (
        jnp.transpose(attended, (1, 2, 0, 3, 4))
        .reshape(token_count, HEADS * HEAD_DIM)
        .astype(jnp.bfloat16)
    )
    return (merged, log_totals)


def attend_backward(query_heads, key_heads, value_heads, grad_merged, log_totals, prefix_len):
    token_count = query_heads.shape[0]
    group_size = min(4, HEADS)
    groups = HEADS // group_size
    block_rows = min(512, token_count)
    blocks = token_count // block_rows
    starts = jnp.arange(blocks, dtype=jnp.int32) * block_rows
    score_scale = 1.0 / math.sqrt(HEAD_DIM)

    def one_group(group_item):
        query_group, key_group, value_group, grad_group, total_group = group_item
        query_blocks = query_group.reshape(blocks, block_rows, group_size, HEAD_DIM)
        grad_blocks = grad_group.reshape(blocks, block_rows, group_size, HEAD_DIM)

        def one_block(carry, block_item):
            grad_keys, grad_vals = carry
            query_block, grad_block, total_block, block_start = block_item
            scores = block_scores(query_block, key_group, block_start, prefix_len)
            attn_probs = jnp.exp(scores - total_block[..., None])
            grad_probs = jnp.einsum(
                "qgd,kgd->gqk", grad_block, value_group, preferred_element_type=jnp.float32
            )
            row_delta = jnp.sum(attn_probs * grad_probs, axis=-1, keepdims=True)
            grad_scores = (attn_probs * (grad_probs - row_delta)).astype(jnp.bfloat16)
            grad_vals = grad_vals + jnp.einsum(
                "gqk,qgd->kgd",
                attn_probs.astype(jnp.bfloat16),
                grad_block,
                preferred_element_type=jnp.float32,
            )
            grad_keys = (
                grad_keys
                + jnp.einsum(
                    "gqk,qgd->kgd", grad_scores, query_block, preferred_element_type=jnp.float32
                )
                * score_scale
            )
            grad_query = (
                jnp.einsum(
                    "gqk,kgd->qgd", grad_scores, key_group, preferred_element_type=jnp.float32
                )
                * score_scale
            )
            return ((grad_keys, grad_vals), grad_query)

        zero_keys = jnp.zeros(key_group.shape, jnp.float32)
        carried, grad_queries = lax.scan(
            one_block, (zero_keys, zero_keys), (query_blocks, grad_blocks, total_group, starts)
        )
        return (grad_queries, carried[0], carried[1])

    grad_queries, grad_keys, grad_vals = lax.map(
        one_group,
        (
            group_heads(query_heads, groups),
            group_heads(key_heads, groups),
            group_heads(value_heads, groups),
            group_heads(grad_merged, groups),
            log_totals,
        ),
    )
    query_part = jnp.transpose(grad_queries, (1, 2, 0, 3, 4)).reshape(token_count, HEADS * HEAD_DIM)
    key_part = jnp.transpose(grad_keys, (1, 0, 2, 3)).reshape(token_count, HEADS * HEAD_DIM)
    value_part = jnp.transpose(grad_vals, (1, 0, 2, 3)).reshape(token_count, HEADS * HEAD_DIM)
    return jnp.concatenate([query_part, key_part, value_part], axis=1).astype(jnp.bfloat16)


MESH = pl.DeviceIdType.MESH
LANES = 128


def dot_nn(left, right):
    return lax.dot_general(
        left, right, (((1,), (0,)), ((), ())), preferred_element_type=jnp.float32
    )


def dot_nt(left, right):
    return lax.dot_general(
        left, right, (((1,), (1,)), ((), ())), preferred_element_type=jnp.float32
    )


def dot_tn(left, right):
    return lax.dot_general(
        left, right, (((0,), (0,)), ((), ())), preferred_element_type=jnp.float32
    )


def span(start, size):
    return pl.ds(pl.multiple_of(start, size), size)


def every(start, stop, step):
    def body(i, carry):
        step(i)
        return carry

    lax.fori_loop(start, stop, body, 0)


class Place:
    def __init__(self, owners):
        self.owners = owners
        self.e = lax.axis_index("expert")
        self.w = lax.axis_index("wshard")
        self.c = lax.rem(self.w, 2)
        self.x = lax.div(self.w, 2)
        self.sib = self.w + 1 - 2 * self.c
        self.far = lax.rem(self.w + 2, 4)
        self.diag = 3 - self.w
        self.pair = self.e + 1 - 2 * lax.rem(self.e, 2)

    def ahead(self, k):
        return lax.rem(self.e + k, self.owners)

    def behind(self, k):
        return lax.rem(self.e + self.owners - k, self.owners)


def remote(src, dst, send, recv, device):
    return pltpu.make_async_remote_copy(
        src_ref=src,
        dst_ref=dst,
        send_sem=send,
        recv_sem=recv,
        device_id=device,
        device_id_type=MESH,
    )


def greet(peers):
    barrier = pltpu.get_barrier_semaphore()
    for peer in peers:
        pl.semaphore_signal(barrier, inc=1, device_id=peer, device_id_type=MESH)
    pl.semaphore_wait(barrier, len(peers))


class Dispatch:
    def __init__(self, place, capacity, send_ref, rows_ref, sems):
        self.p, self.cap, self.src, self.rows = place, capacity, send_ref, rows_ref
        self.own_sem, self.send, self.recv = sems

    def slice(self, k, core, side):
        start = (((lax.div(k, 2) * 2 + core) * 2 + side) * 2 + lax.rem(k, 2)) * self.cap
        return self.rows.at[:, span(start, self.cap)]

    def own(self):
        return pltpu.make_async_copy(
            self.src.at[self.p.e], self.slice(0, self.p.c, self.p.x), self.own_sem
        )

    def direct(self, k):
        return remote(
            self.src.at[self.p.ahead(k)],
            self.slice(k, self.p.c, self.p.x),
            self.send.at[0, k],
            self.recv.at[0, k],
            (self.p.ahead(k), self.p.w),
        )

    def hop(self, k, side, which, peer):
        part = self.slice(k, self.p.c, side)
        return remote(
            part, part, self.send.at[which, k], self.recv.at[which, k], (self.p.e, peer)
        )

    def to_sib(self, k):
        return self.hop(k, self.p.x, 1, self.p.sib)

    def to_far(self, k):
        return self.hop(k, self.p.x, 2, self.p.far)

    def relayed(self, k):
        return self.hop(k, 1 - self.p.x, 3, self.p.sib)

    def start(self):
        self.own().start()
        every(1, self.p.owners, lambda k: self.direct(k).start())

    def forward(self, k):
        k = jnp.int32(k)

        @pl.when(k == 0)
        def _():
            self.own().wait()

        @pl.when(k > 0)
        def _():
            self.direct(k).wait_recv()

        self.to_far(k).start()
        self.to_sib(k).start()

    def relay(self, k):
        self.to_far(k).wait_recv()
        self.relayed(k).start()

    def ready(self, k):
        self.to_sib(k).wait_recv()
        self.relayed(k).wait_recv()

    def drain(self):
        every(1, self.p.owners, lambda k: self.direct(k).wait_send())

        def rest(k):
            self.to_sib(k).wait_send()
            self.to_far(k).wait_send()
            self.relayed(k).wait_send()

        every(0, self.p.owners, rest)


class Return:
    def __init__(self, place, capacity, experts, part, got, mid, far, done, home, sems):
        self.p, self.cap, self.experts = place, capacity, experts
        self.part, self.got, self.mid, self.far, self.done, self.home = (
            part, got, mid, far, done, home,
        )
        self.own_sem, self.send, self.recv, self.home_send, self.home_recv = sems
        self.swapped, self.crossed, self.homed = {}, {}, {}

    def swap(self, j):
        size = 4 * self.cap
        self.swapped[j] = remote(
            self.part.at[:, span((j * 2 + 1 - self.p.c) * size, size)],
            self.got.at[:, span(j * size, size)],
            self.send.at[0, j],
            self.recv.at[0, j],
            (self.p.e, self.p.sib),
        )
        self.swapped[j].start()

    def pair_sum(self, expert, j, side):
        size = 2 * self.cap
        mine = self.part[expert, span(((j * 2 + self.p.c) * 2 + side) * size, size), :]
        theirs = self.got[expert, span((j * 2 + side) * size, size), :]
        return mine.astype(jnp.float32) + theirs.astype(jnp.float32)

    def cross(self, j):
        self.swapped[j].wait_recv()
        size = 2 * self.cap
        for expert in range(self.experts):
            self.mid[expert, pl.ds(j * size, size), :] = self.pair_sum(
                expert, j, 1 - self.p.x
            ).astype(jnp.bfloat16)
        part = pl.ds(j * size, size)
        self.crossed[j] = remote(
            self.mid.at[:, part],
            self.far.at[:, part],
            self.send.at[1, j],
            self.recv.at[1, j],
            (self.p.e, self.p.far),
        )
        self.crossed[j].start()

    def finish(self, j):
        self.crossed[j].wait_recv()
        size = 2 * self.cap
        for expert in range(self.experts):
            total = self.pair_sum(expert, j, self.p.x) + self.far[
                expert, pl.ds(j * size, size), :
            ].astype(jnp.float32)
            total = total.astype(jnp.bfloat16)
            self.done[2 * j, expert] = total[: self.cap]
            self.done[2 * j + 1, expert] = total[self.cap :]
        for k in (2 * j, 2 * j + 1):
            if k == 0:
                copy = pltpu.make_async_copy(
                    self.done.at[0], self.home.at[self.p.e], self.own_sem
                )
            else:
                copy = remote(
                    self.done.at[k],
                    self.home.at[self.p.e],
                    self.home_send.at[k],
                    self.home_recv.at[k],
                    (self.p.behind(k), self.p.w),
                )
            copy.start()
            self.homed[k] = copy

    def drain(self):
        for group in (self.swapped, self.crossed):
            for copy in group.values():
                copy.wait_send()
        for k, copy in self.homed.items():
            copy.wait()


def gelu_pair(v):
    root = math.sqrt(2.0 / math.pi)
    square = v * v
    t = jnp.tanh(v * (root + (root * 0.044715) * square))
    half = 0.5 + 0.5 * t
    slope = half + (half * (1.0 - t)) * (v * (root + (3.0 * root * 0.044715) * square))
    return v * half, slope


def expert_kernel(
    dims,
    send_ref, grads_hbm, up_hbm, down_hbm, router_ref,
    home_out, home_grad, rows_out, scaled_out, hidden_out, pre_out, router_grad,
    rows, grads, scaled, hidden, pre, up, down,
    part_out, part_grad, got_out, got_grad, mid_out, mid_grad,
    far_out, far_grad, done_out, done_grad,
    load_sem, own_sem, disp_send, disp_recv, red_send, red_recv, home_send, home_recv,
):
    owners, experts, capacity, width, units, expert_count = dims
    place = Place(owners)
    loads = [
        pltpu.make_async_copy(src, dst, load_sem.at[i])
        for i, (src, dst) in enumerate(
            [(up_hbm, up), (grads_hbm, grads), (down_hbm, down)]
        )
    ]
    for load in loads:
        load.start()
    greet(
        [(place.ahead(k), place.w) for k in range(1, owners)]
        + [(place.e, place.sib), (place.e, place.far)]
    )
    dispatch = Dispatch(
        place, capacity, send_ref, rows, (own_sem.at[0], disp_send, disp_recv)
    )
    ret = [
        Return(
            place, capacity, experts, part, got, mid, far, done, home,
            (own_sem.at[1 + i], red_send.at[i], red_recv.at[i], home_send.at[i], home_recv.at[i]),
        )
        for i, (part, got, mid, far, done, home) in enumerate(
            [
                (part_grad, got_grad, mid_grad, far_grad, done_grad, home_grad),
                (part_out, got_out, mid_out, far_out, done_out, home_out),
            ]
        )
    ]
    dispatch.start()
    router_grad[...] = jnp.zeros_like(router_grad)
    tile = min(256, units)
    wide = min(256, width)
    chunks = owners // 2
    size = 8 * capacity
    lane = lax.broadcasted_iota(jnp.int32, (size, LANES), 1)

    def compute(j):
        here = pl.ds(j * size, size)

        def one_expert(expert, carry):
            logits = dot_nn(rows[expert, here, :], router_ref[...])
            logits = jnp.where(lane < expert_count, logits, -1e30)
            exponent = jnp.exp(logits - jnp.max(logits, axis=1, keepdims=True))
            prob = exponent / jnp.sum(exponent, axis=1, keepdims=True)
            mine = lane == place.e * experts + expert
            gate = jnp.sum(jnp.where(mine, prob, 0.0), axis=1, keepdims=True)
            scaled[expert, here, :] = (
                gate * grads[expert, here, :].astype(jnp.float32)
            ).astype(jnp.bfloat16)

            def one_tile(n, carry):
                cols = pl.ds(pl.multiple_of(n * tile, tile), tile)
                value, slope = gelu_pair(dot_nn(rows[expert, here, :], up[expert, :, cols]))
                hidden[expert, here, cols] = value.astype(jnp.bfloat16)
                back = dot_nt(scaled[expert, here, :], down[expert, cols, :])
                pre[expert, here, cols] = (back * slope).astype(jnp.bfloat16)
                return carry

            lax.fori_loop(0, units // tile, one_tile, 0)

            def one_out(n, total):
                cols = pl.ds(pl.multiple_of(n * wide, wide), wide)
                value = dot_nn(hidden[expert, here, :], down[expert, :, cols])
                part_out[expert, here, cols] = (gate * value).astype(jnp.bfloat16)
                weighted = value * grads[expert, here, cols].astype(jnp.float32)
                for start in range(0, wide, LANES):
                    total = total + weighted[:, start : start + LANES]
                return total

            total = lax.fori_loop(
                0, width // wide, one_out, jnp.zeros((size, LANES), jnp.float32)
            )
            grad_gate = jnp.sum(total, axis=1, keepdims=True)
            grad_logits = (
                prob * ((jnp.where(mine, 1.0, 0.0) - gate) * grad_gate)
            ).astype(jnp.bfloat16)

            def one_in(n, carry):
                cols = pl.ds(pl.multiple_of(n * wide, wide), wide)
                value = dot_nt(pre[expert, here, :], up[expert, cols, :]) + dot_nt(
                    grad_logits, router_ref[cols, :]
                )
                part_grad[expert, here, cols] = value.astype(jnp.bfloat16)
                router_grad[:, cols] += dot_tn(grad_logits, rows[expert, here, cols])
                return carry

            lax.fori_loop(0, width // wide, one_in, 0)
            return carry

        lax.fori_loop(0, experts, one_expert, 0)

    for k in (0, 1):
        dispatch.forward(k)
    for j in range(chunks):
        if j + 1 < chunks:
            for k in (2 * j + 2, 2 * j + 3):
                dispatch.forward(k)
        for k in (2 * j, 2 * j + 1):
            dispatch.relay(k)
        for k in (2 * j, 2 * j + 1):
            dispatch.ready(k)
        if j == 0:
            for load in loads:
                load.wait()
        compute(j)
        ret[0].swap(j)
        ret[1].swap(j)
        if j >= 1:
            ret[0].cross(j - 1)
        if j >= 2:
            ret[0].finish(j - 2)
    ret[0].cross(chunks - 1)
    stores = [
        pltpu.make_async_copy(src, dst, load_sem.at[i])
        for i, (src, dst) in enumerate(
            [(rows, rows_out), (scaled, scaled_out), (hidden, hidden_out), (pre, pre_out)]
        )
    ]
    for store in stores:
        store.start()
    if chunks >= 2:
        ret[0].finish(chunks - 2)
    for j in range(chunks):
        ret[1].cross(j)
    ret[0].finish(chunks - 1)
    for j in range(chunks):
        ret[1].finish(j)
    for store in stores:
        store.wait()
    dispatch.drain()
    for each in ret:
        each.drain()


def run_experts(owners, capacity, expert_count, send_rows, grads, w_up, w_down, router):
    experts, width, units = w_up.shape
    slots = owners * 4 * capacity
    chunks = owners // 2
    dims = (owners, experts, capacity, width, units, expert_count)
    any_spec = pl.BlockSpec(memory_space=pl.ANY)
    vmem_spec = pl.BlockSpec(memory_space=pltpu.VMEM)
    bf16 = jnp.bfloat16
    home = jax.ShapeDtypeStruct((owners, experts, capacity, width), bf16)
    slab = jax.ShapeDtypeStruct((experts, slots, width), bf16)
    thin = jax.ShapeDtypeStruct((experts, slots, units), bf16)
    dma = pltpu.SemaphoreType.DMA

    def vm(*shape):
        return pltpu.VMEM(shape, bf16)

    return pl.pallas_call(
        functools.partial(expert_kernel, dims),
        out_shape=(
            home, home, slab, slab, thin, thin,
            jax.ShapeDtypeStruct((LANES, width), jnp.float32),
        ),
        in_specs=[any_spec] * 4 + [vmem_spec],
        out_specs=(any_spec,) * 6 + (vmem_spec,),
        scratch_shapes=[
            vm(experts, slots, width),
            vm(experts, slots, width),
            vm(experts, slots, width),
            vm(experts, slots, units),
            vm(experts, slots, units),
            vm(experts, width, units),
            vm(experts, units, width),
            vm(experts, slots, width),
            vm(experts, slots, width),
            vm(experts, slots // 2, width),
            vm(experts, slots // 2, width),
            vm(experts, slots // 4, width),
            vm(experts, slots // 4, width),
            vm(experts, slots // 4, width),
            vm(experts, slots // 4, width),
            vm(owners, experts, capacity, width),
            vm(owners, experts, capacity, width),
            dma((4,)),
            dma((3,)),
            dma((4, owners)),
            dma((4, owners)),
            dma((2, 2, chunks)),
            dma((2, 2, chunks)),
            dma((2, owners)),
            dma((2, owners)),
        ],
        compiler_params=pltpu.CompilerParams(
            collective_id=1, has_side_effects=True, vmem_limit_bytes=VMEM_LIMIT
        ),
        name="experts",
    )(send_rows, grads, w_up, w_down, router)


def masked_softmax(scores):
    exponent = jnp.exp(scores - jnp.max(scores, axis=1, keepdims=True))
    return exponent * (1.0 / jnp.sum(exponent, axis=1, keepdims=True))


def attend_head(query, key, value, prefix_len):
    half = query.shape[0] // 2
    query = query * (1.0 / math.sqrt(HEAD_DIM))
    row = lax.broadcasted_iota(jnp.int32, (half, half), 0)
    col = lax.broadcasted_iota(jnp.int32, (half, half), 1)
    low = dot_nt(query[:half], key[:half])
    low = jnp.where((col <= row) | (col < prefix_len), low, -1e30)
    low = masked_softmax(low).astype(jnp.bfloat16)
    high = dot_nt(query[half:], key)
    high = jnp.concatenate(
        [high[:, :half], jnp.where(col <= row, high[:, half:], -1e30)], axis=1
    )
    high = masked_softmax(high).astype(jnp.bfloat16)
    return low, high, dot_nn(low, value[:half]), dot_nn(high, value)


def score_grads(probs, grad_probs):
    probs = probs.astype(jnp.float32)
    weighted = probs * grad_probs
    total = jnp.sum(weighted, axis=1, keepdims=True)
    return (weighted - probs * total).astype(jnp.bfloat16)


def attend_back_head(query, key, value, low, high, grad):
    half = query.shape[0] // 2
    scale = 1.0 / math.sqrt(HEAD_DIM)
    query = query * scale
    grad_low = score_grads(low, dot_nt(grad[:half], value[:half]))
    grad_high = score_grads(high, dot_nt(grad[half:], value))
    grad_query = jnp.concatenate(
        [dot_nn(grad_low, key[:half]), dot_nn(grad_high, key)], axis=0
    )
    value_all = dot_tn(high, grad[half:])
    key_all = dot_tn(grad_high, query[half:])
    grad_value = jnp.concatenate(
        [value_all[:half] + dot_tn(low, grad[:half]), value_all[half:]], axis=0
    )
    grad_key = jnp.concatenate(
        [key_all[:half] + dot_tn(grad_low, query[:half]), key_all[half:]], axis=0
    )
    return (
        (grad_query * scale).astype(jnp.bfloat16),
        grad_key.astype(jnp.bfloat16),
        grad_value.astype(jnp.bfloat16),
    )


class Gather:
    def __init__(self, place, pieces, src, dst, sems):
        self.p, self.src, self.dst = place, src, dst
        self.send, self.recv, self.near_send, self.near_recv, self.own_sem = sems
        self.shard = src.shape[0]
        self.half = self.shard // 2
        self.step = self.half // pieces
        self.pieces = pieces
        self.first = lax.rem(place.e, 2) * self.half
        self.second = self.half - self.first

    def block(self, owner, start, size):
        return self.dst.at[pl.ds(pl.multiple_of(owner * self.shard + start, self.step), size)]

    def own(self):
        return pltpu.make_async_copy(self.src, self.block(self.p.w, 0, self.shard), self.own_sem)

    def near(self):
        return remote(
            self.src, self.block(self.p.w, 0, self.shard), self.near_send, self.near_recv,
            (self.p.e, self.p.sib),
        )

    def hop(self, n):
        return remote(
            self.src.at[span(self.first + n * self.step, self.step)],
            self.block(self.p.w, self.first + n * self.step, self.step),
            self.send.at[0, n], self.recv.at[0, n], (self.p.e, self.p.far),
        )

    def pass_from(self, start, n, which, device):
        part = self.block(self.p.far, start + n * self.step, self.step)
        return remote(part, part, self.send.at[which, n], self.recv.at[which, n], device)

    def pairs(self, n):
        return self.pass_from(self.first, n, 1, (self.p.pair, self.p.w))

    def relay(self, n):
        return self.pass_from(self.first, n, 2, (self.p.e, self.p.sib))

    def pair_relay(self, n):
        return self.pass_from(self.second, n, 3, (self.p.e, self.p.sib))

    def start(self):
        every(0, self.pieces, lambda n: self.hop(n).start())
        self.near().start()

    def pass_on(self, n):
        self.hop(n).wait_recv()
        self.pairs(n).start()
        self.relay(n).start()

    def pass_pair(self, n):
        self.pairs(n).wait_recv()
        self.pair_relay(n).start()

    def near_ready(self):
        self.own().wait()
        self.near().wait_recv()

    def far_ready(self):
        def one(n):
            self.relay(n).wait_recv()
            self.pair_relay(n).wait_recv()

        every(0, self.pieces, one)

    def drain(self):
        self.near().wait_send()

        def one(n):
            for copy in (self.hop(n), self.pairs(n), self.relay(n), self.pair_relay(n)):
                copy.wait_send()

        every(0, self.pieces, one)


def slot_tables(routes_ref, priority_ref, capacity, pick_ref, back_ref):
    count = routes_ref.shape[0]
    row = lax.broadcasted_iota(jnp.int32, (count, count), 0).astype(jnp.float32)
    col = lax.broadcasted_iota(jnp.int32, (count, count), 1).astype(jnp.float32)
    eye = row == col
    route_col = routes_ref[...].astype(jnp.float32)
    order_row = priority_ref[...].astype(jnp.float32)
    route_row = jnp.sum(jnp.where(eye, route_col, 0.0), axis=0, keepdims=True)
    order_col = jnp.sum(jnp.where(eye, order_row, 0.0), axis=1, keepdims=True)
    same = route_col == route_row
    rank_row = jnp.sum(
        jnp.where(same & (order_col < order_row), 1.0, 0.0), axis=0, keepdims=True
    )
    rank_col = jnp.sum(
        jnp.where(same & (order_row < order_col), 1.0, 0.0), axis=1, keepdims=True
    )
    slots = float(count)
    slot_row = jnp.where(rank_row < capacity, route_row * capacity + rank_row, slots)
    slot_col = jnp.where(rank_col < capacity, route_col * capacity + rank_col, slots)
    pick_ref[...] = jnp.where(slot_row == row, 1.0, 0.0).astype(jnp.bfloat16)
    back_ref[...] = jnp.where(slot_col == col, 1.0, 0.0).astype(jnp.bfloat16)


def norm_stats(value):
    centered = value - jnp.mean(value, axis=1, keepdims=True)
    inverse = lax.rsqrt(jnp.mean(centered * centered, axis=1, keepdims=True) + epsilon)
    return centered * inverse, inverse


def front_kernel(
    dims,
    prefix_ref, routes_ref, priority_ref, tokens_ref, cot_ref, small_hbm, qkv_hbm, out_hbm,
    qkv_out, act_out, merged_out, back_out, weight_out, out_full, low_out, high_out, grads_rows,
    hidden_ref, send_ref, small_out,
    small, weight, out_w, total, qkv, act, merged, act_two, turned, pick, back, grads_send, low_buf, high_buf,
    own_sem, disp_send, disp_recv, small_send, small_recv, near_send, near_recv,
    gat_send, gat_recv, store_sem, prob_sem,
):
    owners, capacity, pieces = dims
    place = Place(owners)
    rows, width = tokens_ref.shape
    shard = qkv_hbm.shape[0]
    gathers = [
        Gather(
            place, pieces, src, dst,
            (gat_send.at[i], gat_recv.at[i], near_send.at[i], near_recv.at[i], own_sem.at[1 + i]),
        )
        for i, (src, dst) in enumerate(((qkv_hbm, weight), (out_hbm, out_w)))
    ]
    for gather in gathers:
        gather.own().start()
    own_small = pltpu.make_async_copy(small_hbm, small.at[place.w], own_sem.at[3])
    own_small.start()
    greet(
        [(place.ahead(k), place.w) for k in range(1, owners)]
        + [(place.e, place.sib), (place.e, place.far), (place.e, place.diag)]
    )
    smalls = [
        remote(small_hbm, small.at[place.w], small_send.at[i], small_recv.at[i], (place.e, peer))
        for i, peer in enumerate((place.sib, place.far, place.diag))
    ]
    for copy in smalls:
        copy.start()
    for gather in gathers:
        gather.start()
    slot_tables(routes_ref, priority_ref, capacity, pick, back)
    tile = min(256, width)
    shape = grads_send.shape[:3]

    def to_slots(values_ref, slots_ref):
        def one(n):
            cols = span(n * tile, tile)
            value = dot_nn(pick[...], values_ref[:, cols]).astype(jnp.bfloat16)
            slots_ref[:, :, :, cols] = value.reshape(shape + (tile,))

        every(0, width // tile, one)

    to_slots(cot_ref, grads_send)
    dispatch = Dispatch(
        place, capacity, grads_send, grads_rows, (own_sem.at[0], disp_send, disp_recv)
    )
    dispatch.start()
    own_small.wait()
    for copy in smalls:
        copy.wait_recv()
    small_out[...] = small[...]

    def vector(which):
        parts = [small[i, which : which + 1, :] for i in range(4)]
        return jnp.concatenate(parts, axis=1).astype(jnp.float32)

    band = min(64, rows)
    gain, shift = vector(0), vector(1)

    def norm_band(i):
        part = span(i * band, band)
        scaled, _ = norm_stats(tokens_ref[part, :].astype(jnp.float32))
        act[part, :] = (scaled * gain + shift).astype(jnp.bfloat16)

    every(0, rows // band, norm_band)
    turned[0] = act[...].T
    columns = weight.shape[1]
    wide = min(512, columns)

    def multiply(owner, cols):
        depth = span(owner * shard, shard)
        return dot_nn(act[:, depth], weight[depth, cols])

    def first_tile(n):
        cols = span(n * wide, wide)
        total[:, cols] = multiply(place.w, cols) + multiply(place.sib, cols)

    def last_tile(n):
        cols = span(n * wide, wide)
        value = total[:, cols] + multiply(place.far, cols) + multiply(place.diag, cols)
        qkv[:, cols] = value.astype(jnp.bfloat16)

    gathers[0].near_ready()
    every(0, columns // wide, first_tile)

    def pass_piece(gather, n):
        @pl.when(n < pieces)
        def _():
            gather.pass_on(n)

        @pl.when(n >= 1)
        def _():
            gather.pass_pair(n - 1)

    every(0, pieces + 1, lambda n: pass_piece(gathers[0], n))
    gathers[0].far_ready()
    every(0, columns // wide, last_tile)
    stores = [
        pltpu.make_async_copy(src, dst, store_sem.at[i])
        for i, (src, dst) in enumerate(
            [(qkv, qkv_out), (turned.at[0], act_out), (back, back_out), (weight, weight_out),
             (turned.at[1], merged_out), (out_w, out_full)]
        )
    ]
    for store in stores[:4]:
        store.start()
    half = rows // 2
    pairs = width // LANES

    def keep_probs(i):
        slot = lax.rem(i, 2)
        return (
            pltpu.make_async_copy(
                low_buf.at[slot], low_out.at[pl.ds(2 * i, 2)], prob_sem.at[0, slot]
            ),
            pltpu.make_async_copy(
                high_buf.at[slot], high_out.at[pl.ds(2 * i, 2)], prob_sem.at[1, slot]
            ),
        )

    def attend_pair(i):
        slot = lax.rem(i, 2)

        @pl.when(i >= 2)
        def _():
            for copy in keep_probs(i - 2):
                copy.wait()

        query, key, value = (
            qkv[:, span(part * width + i * LANES, LANES)] for part in range(3)
        )
        tops, bottoms = [], []
        for head in range(2):
            part = slice(head * HEAD_DIM, (head + 1) * HEAD_DIM)
            low, high, top, bottom = attend_head(
                query[:, part], key[:, part], value[:, part], prefix_ref[0]
            )
            low_buf[slot, head] = low
            high_buf[slot, head] = high
            tops.append(top)
            bottoms.append(bottom)
        cols = span(i * LANES, LANES)
        merged[:half, cols] = jnp.concatenate(tops, axis=1).astype(jnp.bfloat16)
        merged[half:, cols] = jnp.concatenate(bottoms, axis=1).astype(jnp.bfloat16)
        for copy in keep_probs(i):
            copy.start()

    def attend_step(i):
        @pl.when(i < pairs)
        def _():
            attend_pair(i)

        @pl.when(i < owners)
        def _():
            dispatch.forward(i)

        @pl.when((i >= 1) & (i < pieces + 2))
        def _():
            pass_piece(gathers[1], i - 1)

        @pl.when((i >= 2) & (i < owners + 2))
        def _():
            dispatch.relay(i - 2)

    every(0, max(pairs, owners + 2), attend_step)
    turned[1] = merged[...].T
    stores[4].start()
    gathers[1].near_ready()
    gathers[1].far_ready()
    stores[5].start()
    gain_two, shift_two = vector(2), vector(3)
    band_two = min(128, rows)

    def middle(i):
        part = span(i * band_two, band_two)
        value = tokens_ref[part, :].astype(jnp.float32) + dot_nn(merged[part, :], out_w[...])
        hidden_ref[part, :] = value
        scaled, _ = norm_stats(value)
        act_two[part, :] = (scaled * gain_two + shift_two).astype(jnp.bfloat16)

    every(0, rows // band_two, middle)
    to_slots(act_two, send_ref)
    for i in (pairs - 2, pairs - 1):
        for copy in keep_probs(i):
            copy.wait()
    every(0, owners, dispatch.ready)
    for store in stores:
        store.wait()
    for copy in smalls:
        copy.wait_send()
    for gather in gathers:
        gather.drain()
    dispatch.drain()


def run_front(owners, experts, capacity, prefix, routes, priority, tokens, cotangent, small, w_qkv, w_out):
    rows, width = tokens.shape
    shard, columns = w_qkv.shape
    half = rows // 2
    heads = width // HEAD_DIM
    pieces = 4
    any_spec = pl.BlockSpec(memory_space=pl.ANY)
    vmem_spec = pl.BlockSpec(memory_space=pltpu.VMEM)
    bf16, f32 = jnp.bfloat16, jnp.float32
    dma = pltpu.SemaphoreType.DMA

    def out(*shape):
        return jax.ShapeDtypeStruct(shape, bf16)

    def vm(*shape):
        return pltpu.VMEM(shape, bf16)

    return pl.pallas_call(
        functools.partial(front_kernel, (owners, capacity, pieces)),
        out_shape=(
            out(rows, columns),
            out(width, rows),
            out(width, rows),
            out(rows, rows),
            out(4 * shard, columns),
            out(4 * shard, width),
            out(heads, half, half),
            out(heads, half, rows),
            out(experts, owners * 4 * capacity, width),
            jax.ShapeDtypeStruct((rows, width), f32),
            out(owners, experts, capacity, width),
            out(4, *small.shape),
        ),
        in_specs=[pl.BlockSpec(memory_space=pltpu.SMEM)] + [vmem_spec] * 4 + [any_spec] * 3,
        out_specs=(any_spec,) * 9 + (vmem_spec,) * 3,
        scratch_shapes=[
            vm(4, *small.shape),
            vm(4 * shard, columns),
            vm(4 * shard, width),
            pltpu.VMEM((rows, columns), f32),
            vm(rows, columns),
            vm(rows, width),
            vm(rows, width),
            vm(rows, width),
            vm(2, width, rows),
            vm(rows, rows),
            vm(rows, rows),
            vm(owners, experts, capacity, width),
            vm(2, 2, half, half),
            vm(2, 2, half, rows),
            dma((4,)),
            dma((4, owners)),
            dma((4, owners)),
            dma((3,)),
            dma((3,)),
            dma((2,)),
            dma((2,)),
            dma((2, 4, pieces)),
            dma((2, 4, pieces)),
            dma((6,)),
            dma((2, 2)),
        ],
        compiler_params=pltpu.CompilerParams(
            collective_id=0, has_side_effects=True, vmem_limit_bytes=VMEM_LIMIT
        ),
        name="front",
    )(prefix, routes, priority, tokens, cotangent, small, w_qkv, w_out)


class Reduce:
    def __init__(self, place, part, got, far, pair, lines, done, sems):
        self.p = place
        self.part, self.got, self.far = part, got, far
        self.pair, self.lines, self.done = pair, lines, done
        self.send, self.recv, self.line_send, self.line_recv = sems
        self.chunks = part.shape[0]
        self.halves = done.shape[1] // 2
        self.count = place.owners // 2
        self.slice = self.halves // self.count
        self.bit = lax.rem(place.e, 2)
        self.level = lax.div(place.e, 2)

    def step(self, which, n, src, dst, device):
        return remote(src, dst, self.send.at[which, n], self.recv.at[which, n], device)

    def swapped(self, n):
        return self.step(
            0, n, self.part.at[n, :, 1 - self.p.c], self.got.at[n], (self.p.e, self.p.sib)
        )

    def crossed(self, n):
        return self.step(
            1, n, self.part.at[n, 1 - self.p.x, self.p.c], self.far.at[n], (self.p.e, self.p.far)
        )

    def folded(self, n):
        other = span((1 - self.bit) * self.halves, self.halves)
        return self.step(
            2, n, self.part.at[n, self.p.x, self.p.c, other], self.pair.at[n],
            (self.p.pair, self.p.w),
        )

    def shared(self, n):
        part = self.done.at[n, span(self.bit * self.halves, self.halves)]
        return self.step(3, n, part, part, (self.p.pair, self.p.w))

    def line(self, which, n, k, src, dst):
        return remote(
            src, dst, self.line_send.at[which, n, k], self.line_recv.at[which, n, k],
            (self.p.ahead(2 * k), self.p.w),
        )

    def row(self, level):
        return span(self.bit * self.halves + level * self.slice, self.slice)

    def spreads(self, n, k):
        target = lax.rem(self.level + k, self.count)
        return self.line(
            0, n, k, self.part.at[n, self.p.x, self.p.c, self.row(target)], self.lines.at[n, k]
        )

    def collects(self, n, k):
        part = self.done.at[n, self.row(self.level)]
        return self.line(1, n, k, part, part)

    def pair_sum(self, n, side):
        return self.part[n, side, self.p.c].astype(jnp.float32) + self.got[n, side].astype(
            jnp.float32
        )

    def swap(self, n):
        self.swapped(n).start()

    def cross(self, n):
        self.swapped(n).wait_recv()
        side = 1 - self.p.x
        self.part[n, side, self.p.c] = self.pair_sum(n, side).astype(jnp.bfloat16)
        self.crossed(n).start()

    def fold(self, n):
        self.crossed(n).wait_recv()
        total = self.pair_sum(n, self.p.x) + self.far[n].astype(jnp.float32)
        self.part[n, self.p.x, self.p.c] = total.astype(jnp.bfloat16)
        self.folded(n).start()

    def spread(self, n):
        self.folded(n).wait_recv()
        own = span(self.bit * self.halves, self.halves)
        total = self.part[n, self.p.x, self.p.c, own, :].astype(jnp.float32) + self.pair[
            n
        ].astype(jnp.float32)
        self.part[n, self.p.x, self.p.c, own, :] = total.astype(jnp.bfloat16)
        for k in range(1, self.count):
            self.spreads(n, k).start()

    def collect(self, n):
        total = self.part[n, self.p.x, self.p.c, self.row(self.level), :].astype(jnp.float32)
        for k in range(1, self.count):
            self.spreads(n, k).wait_recv()
            total = total + self.lines[n, k].astype(jnp.float32)
        self.done[n, self.row(self.level), :] = total.astype(jnp.bfloat16)
        for k in range(1, self.count):
            self.collects(n, k).start()

    def share(self, n):
        for k in range(1, self.count):
            self.collects(n, k).wait_recv()
        self.shared(n).start()

    def finish(self, n):
        self.shared(n).wait_recv()

    def stages(self):
        return (self.cross, self.fold, self.spread, self.collect, self.share, self.finish)

    def drain(self):
        def one(n):
            for copy in (self.swapped(n), self.crossed(n), self.folded(n), self.shared(n)):
                copy.wait_send()
            for k in range(1, self.count):
                self.spreads(n, k).wait_send()
                self.collects(n, k).wait_send()

        every(0, self.chunks, one)


class Small:
    def __init__(self, place, value, part, got, mid, far, total, others, out, sems):
        self.p, self.value, self.part, self.got, self.mid = place, value, part, got, mid
        self.far, self.total, self.others, self.out = far, total, others, out
        self.send, self.recv, self.all_send, self.all_recv = sems

    def swapped(self):
        return remote(
            self.part.at[:, 1 - self.p.c], self.got, self.send.at[0], self.recv.at[0],
            (self.p.e, self.p.sib),
        )

    def crossed(self):
        return remote(
            self.mid, self.far, self.send.at[1], self.recv.at[1], (self.p.e, self.p.far)
        )

    def spreads(self, k):
        return remote(
            self.total, self.others.at[k], self.all_send.at[k], self.all_recv.at[k],
            (self.p.ahead(k), self.p.w),
        )

    def swap(self):
        size = self.part.shape[-1]
        for owner in range(4):
            self.part[owner // 2, owner % 2] = self.value[:, owner * size : (owner + 1) * size]
        self.swapped().start()

    def cross(self):
        self.swapped().wait_recv()
        self.mid[...] = self.part[1 - self.p.x, self.p.c] + self.got[1 - self.p.x]
        self.crossed().start()

    def spread(self):
        self.crossed().wait_recv()
        self.total[...] = self.part[self.p.x, self.p.c] + self.got[self.p.x] + self.far[...]
        for k in range(1, self.p.owners):
            self.spreads(k).start()

    def finish(self):
        total = self.total[...]
        for k in range(1, self.p.owners):
            self.spreads(k).wait_recv()
            total = total + self.others[k]
        self.out[...] = total

    def drain(self):
        self.swapped().wait_send()
        self.crossed().wait_send()
        for k in range(1, self.p.owners):
            self.spreads(k).wait_send()


def norm_back_rows(grad, scaled, inverse, gain):
    weighted = grad * gain
    mean_one = jnp.mean(weighted, axis=1, keepdims=True)
    mean_two = jnp.mean(weighted * scaled, axis=1, keepdims=True)
    return inverse * (weighted - mean_one - scaled * mean_two)


def back_kernel(
    dims,
    home_grad_ref, home_out_ref, back_ref, hidden_ref, cot_ref, tokens_ref, vectors_ref, router_ref,
    act_hbm, merged_hbm, qkv_hbm, weight_hbm, out_hbm, low_hbm, high_hbm,
    output_ref, tokens_out, small_out, qkv_out, out_out,
    act_t, merged_t, qkv, weight, out_w, low_buf, high_buf, attn, grad_merged, grad_qkv,
    part_q, got_q, far_q, pair_q, lines_q, done_q,
    part_o, got_o, far_o, pair_o, lines_o, done_o,
    small, small_part, small_got, small_mid, small_far, small_sum, small_all,
    load_sem, prob_sem, send_q, recv_q, lsend_q, lrecv_q, send_o, recv_o, lsend_o, lrecv_o,
    small_send, small_recv, all_send, all_recv, out_sem,
):
    (owners,) = dims
    place = Place(owners)
    loads = [
        pltpu.make_async_copy(src, dst, load_sem.at[i])
        for i, (src, dst) in enumerate(
            [(merged_hbm, merged_t), (out_hbm, out_w), (qkv_hbm, qkv), (act_hbm, act_t),
             (weight_hbm, weight)]
        )
    ]

    def load_probs(i):
        slot = lax.rem(i, 2)
        return (
            pltpu.make_async_copy(
                low_hbm.at[pl.ds(2 * i, 2)], low_buf.at[slot], prob_sem.at[0, slot]
            ),
            pltpu.make_async_copy(
                high_hbm.at[pl.ds(2 * i, 2)], high_buf.at[slot], prob_sem.at[1, slot]
            ),
        )

    for load in loads:
        load.start()
    for load in load_probs(0):
        load.start()
    greet(
        [(place.ahead(k), place.w) for k in range(1, owners)]
        + [(place.e, place.sib), (place.e, place.far)]
    )
    reduce_o = Reduce(
        place, part_o, got_o, far_o, pair_o, lines_o, done_o, (send_o, recv_o, lsend_o, lrecv_o)
    )
    reduce_q = Reduce(
        place, part_q, got_q, far_q, pair_q, lines_q, done_q, (send_q, recv_q, lsend_q, lrecv_q)
    )
    smalls = Small(
        place, small, small_part, small_got, small_mid, small_far, small_sum, small_all, small_out,
        (small_send, small_recv, all_send, all_recv),
    )
    rows, width = tokens_ref.shape
    shard = width // 4
    band = min(128, rows)
    lead = small.shape[0]

    def vector(which):
        parts = [vectors_ref[i, which : which + 1, :] for i in range(4)]
        return jnp.concatenate(parts, axis=1).astype(jnp.float32)

    gain_one, gain_two = vector(0), vector(2)
    small[0:4, :] = jnp.zeros((4, width), jnp.float32)
    small[4:lead, :] = router_ref[0 : lead - 4, :]

    def post(i):
        part = span(i * band, band)
        grad = dot_nn(back_ref[part, :], home_grad_ref[...])
        scaled, inverse = norm_stats(hidden_ref[part, :])
        value = cot_ref[part, :].astype(jnp.float32) + norm_back_rows(
            grad, scaled, inverse, gain_two
        )
        tokens_out[part, :] = value
        attn[part, :] = value.astype(jnp.bfloat16)
        small[2:3, :] += jnp.sum(grad * scaled, axis=0, keepdims=True)
        small[3:4, :] += jnp.sum(grad, axis=0, keepdims=True)

    every(0, rows // band, post)
    loads[0].wait()

    def weight_grad(part, n, left, right):
        def one(owner):
            value = dot_nn(left[span(owner * shard, shard), :], right)
            part[n, lax.div(owner, 2), lax.rem(owner, 2)] = value.astype(jnp.bfloat16)

        every(0, 4, one)

    tile_o = part_o.shape[-1]
    out_chunks = part_o.shape[0]
    for n in range(out_chunks):
        weight_grad(part_o, n, merged_t, attn[:, n * tile_o : (n + 1) * tile_o])
        reduce_o.swap(n)
    loads[1].wait()

    def merged_band(i):
        part = span(i * band, band)
        grad_merged[part, :] = dot_nt(attn[part, :], out_w[...]).astype(jnp.bfloat16)

    every(0, rows // band, merged_band)
    for load in loads[2:4]:
        load.wait()
    pairs = part_q.shape[0]

    def attend_pair(i):
        slot = lax.rem(i, 2)
        for load in load_probs(i):
            load.wait()

        @pl.when(i + 1 < pairs)
        def _():
            for load in load_probs(i + 1):
                load.start()

        cols = span(i * LANES, LANES)
        query, key, value = (
            qkv[:, span(part * width + i * LANES, LANES)] for part in range(3)
        )
        grad = grad_merged[:, cols]
        results = []
        for head in range(2):
            part = slice(head * HEAD_DIM, (head + 1) * HEAD_DIM)
            results.append(
                attend_back_head(
                    query[:, part], key[:, part], value[:, part],
                    low_buf[slot, head], high_buf[slot, head], grad[:, part],
                )
            )
        for which in range(3):
            grad_qkv[:, span(which * width + i * LANES, LANES)] = jnp.concatenate(
                [results[0][which], results[1][which]], axis=1
            )
        right = jnp.concatenate(
            [grad_qkv[:, span(which * width + i * LANES, LANES)] for which in range(3)], axis=1
        )
        weight_grad(part_q, i, act_t, right)
        reduce_q.swap(i)

    def input_band(i):
        part = span(i * band, band)
        grad = dot_nt(grad_qkv[part, :], weight[...])
        scaled, inverse = norm_stats(tokens_ref[part, :].astype(jnp.float32))
        tokens_out[part, :] += norm_back_rows(grad, scaled, inverse, gain_one)
        small[0:1, :] += jnp.sum(grad * scaled, axis=0, keepdims=True)
        small[1:2, :] += jnp.sum(grad, axis=0, keepdims=True)

    def output_band(i):
        part = span(i * band, band)
        value = hidden_ref[part, :] + dot_nn(back_ref[part, :], home_out_ref[...])
        output_ref[part, :] = value.astype(jnp.bfloat16)

    def store_q(i):
        return [
            pltpu.make_async_copy(
                done_q.at[i, :, pl.ds(which * LANES, LANES)],
                qkv_out.at[:, span(which * width + i * LANES, LANES)],
                out_sem.at[which, i],
            )
            for which in range(3)
        ]

    def store_o(n):
        return pltpu.make_async_copy(
            done_o.at[n], out_out.at[:, span(n * tile_o, tile_o)], out_sem.at[3, n]
        )

    stages_o, stages_q = reduce_o.stages(), reduce_q.stages()
    depth = len(stages_q)

    def slot_step(slot):
        for s in range(depth - 1, -1, -1):
            n = slot - 1 - s

            @pl.when((n >= 0) & (n < pairs))
            def _(s=s, n=n):
                stages_q[s](n)
                if s == depth - 1:
                    for copy in store_q(n):
                        copy.start()

            @pl.when(slot == s)
            def _(s=s):
                for n in range(out_chunks):
                    stages_o[s](n)
                    if s == depth - 1:
                        store_o(n).start()

        @pl.when(slot < pairs)
        def _():
            attend_pair(slot)

        @pl.when(slot == pairs)
        def _():
            loads[4].wait()
            every(0, rows // band // 2, input_band)

        @pl.when(slot == pairs + 1)
        def _():
            every(rows // band // 2, rows // band, input_band)

        @pl.when(slot == pairs + 2)
        def _():
            smalls.swap()
            every(0, rows // band, output_band)

        @pl.when(slot == pairs + 3)
        def _():
            smalls.cross()

        @pl.when(slot == pairs + 4)
        def _():
            smalls.spread()

        @pl.when(slot == pairs + 5)
        def _():
            smalls.finish()

    every(0, pairs + depth, slot_step)

    def stored(i):
        for copy in store_q(i):
            copy.wait()

    every(0, pairs, stored)
    for n in range(out_chunks):
        store_o(n).wait()
    reduce_o.drain()
    reduce_q.drain()
    smalls.drain()


def run_back(
    owners, lead, home_grad, home_out, back, hidden, cotangent, tokens, vectors, router_grad,
    act_t, merged_t, qkv, weight, w_out, low, high,
):
    rows, width = tokens.shape
    shard = width // 4
    pairs = width // LANES
    tile_o = min(512, width)
    out_chunks = width // tile_o
    count = owners // 2
    half = shard // 2
    mid = rows // 2
    any_spec = pl.BlockSpec(memory_space=pl.ANY)
    vmem_spec = pl.BlockSpec(memory_space=pltpu.VMEM)
    bf16, f32 = jnp.bfloat16, jnp.float32
    dma = pltpu.SemaphoreType.DMA

    def vm(*shape):
        return pltpu.VMEM(shape, bf16)

    def fm(*shape):
        return pltpu.VMEM(shape, f32)

    def reduce_buffers(chunks, tile):
        return [
            vm(chunks, 2, 2, shard, tile),
            vm(chunks, 2, shard, tile),
            vm(chunks, shard, tile),
            vm(chunks, half, tile),
            vm(chunks, count, half // count, tile),
            vm(chunks, shard, tile),
        ]

    def reduce_sems(chunks):
        return [dma((4, chunks)), dma((4, chunks)), dma((2, chunks, count)), dma((2, chunks, count))]

    return pl.pallas_call(
        functools.partial(back_kernel, (owners,)),
        out_shape=(
            jax.ShapeDtypeStruct((rows, width), bf16),
            jax.ShapeDtypeStruct((rows, width), f32),
            jax.ShapeDtypeStruct((lead, shard), f32),
            jax.ShapeDtypeStruct((shard, 3 * width), bf16),
            jax.ShapeDtypeStruct((shard, width), bf16),
        ),
        in_specs=[vmem_spec] * 8 + [any_spec] * 7,
        out_specs=(vmem_spec,) * 3 + (any_spec,) * 2,
        scratch_shapes=[
            vm(width, rows),
            vm(width, rows),
            vm(rows, 3 * width),
            vm(width, 3 * width),
            vm(width, width),
            vm(2, 2, mid, mid),
            vm(2, 2, mid, rows),
            vm(rows, width),
            vm(rows, width),
            vm(rows, 3 * width),
        ]
        + reduce_buffers(pairs, 3 * LANES)
        + reduce_buffers(out_chunks, tile_o)
        + [
            fm(lead, width),
            fm(2, 2, lead, shard),
            fm(2, lead, shard),
            fm(lead, shard),
            fm(lead, shard),
            fm(lead, shard),
            fm(owners, lead, shard),
            dma((5,)),
            dma((2, 2)),
        ]
        + reduce_sems(pairs)
        + reduce_sems(out_chunks)
        + [dma((2,)), dma((2,)), dma((owners,)), dma((owners,)), dma((4, pairs))],
        compiler_params=pltpu.CompilerParams(
            collective_id=2, has_side_effects=True, vmem_limit_bytes=VMEM_LIMIT
        ),
        name="back",
    )(
        home_grad, home_out, back, hidden, cotangent, tokens, vectors, router_grad,
        act_t, merged_t, qkv, weight, w_out, low, high,
    )


def on_device_plain(
    tokens,
    norm1_gain,
    norm1_shift,
    w_qkv,
    w_out,
    norm2_gain,
    norm2_shift,
    w_router,
    w_up,
    w_down,
    routes,
    priority,
    prefix,
    cotangent,
):
    row_count, model_width = tokens.shape
    expert_count = w_router.shape[1]
    capacity = row_count // expert_count
    owners = lax.axis_size("expert")
    local_experts = w_up.shape[0]
    slot_count = expert_count * capacity
    prefix_len = prefix[0]
    small = jnp.concatenate(
        [
            norm1_gain[None],
            norm1_shift[None],
            norm2_gain[None],
            norm2_shift[None],
            w_router.T,
        ],
        axis=0,
    )
    qkv_full = lax.all_gather(w_qkv, "wshard", axis=0, tiled=True)
    small_full = lax.all_gather(small, "wshard", axis=1, tiled=True)
    out_full = lax.all_gather(w_out, "wshard", axis=0, tiled=True)
    gain_one, shift_one, gain_two, shift_two = (small_full[i] for i in range(4))
    router_full = small_full[4:].T
    gain_one = gain_one.astype(jnp.float32)
    gain_two = gain_two.astype(jnp.float32)
    inputs = tokens.astype(jnp.float32)
    normed_one, scaled_one, inverse_one = normalize(inputs, gain_one, shift_one.astype(jnp.float32))
    act_one = normed_one.astype(jnp.bfloat16)
    qkv = jnp.dot(act_one, qkv_full, preferred_element_type=jnp.float32).astype(jnp.bfloat16)
    query_heads = qkv[:, :model_width]
    key_heads = qkv[:, model_width : 2 * model_width]
    value_heads = qkv[:, 2 * model_width :]
    merged, log_totals = attend_forward(query_heads, key_heads, value_heads, prefix_len)
    attn_out = jnp.dot(merged, out_full, preferred_element_type=jnp.float32)
    hidden = inputs + attn_out
    normed_two, scaled_two, inverse_two = normalize(hidden, gain_two, shift_two.astype(jnp.float32))
    act_two = normed_two.astype(jnp.bfloat16)
    logits = jnp.dot(act_two, router_full, preferred_element_type=jnp.float32)
    row_max = jnp.max(logits, axis=-1, keepdims=True)
    exponent = jnp.exp(logits - row_max)
    gate_prob = exponent / jnp.sum(exponent, axis=-1, keepdims=True)
    route_ids = routes[:, 0]
    chosen = route_ids[:, None] == jnp.arange(expert_count, dtype=jnp.int32)[None, :]
    gate_value = jnp.sum(jnp.where(chosen, gate_prob, 0.0), axis=1)
    slot_index, slot_source = assign_slots(route_ids, priority[0], expert_count, capacity)
    zero_row = jnp.zeros((1, model_width), jnp.bfloat16)
    padded = jnp.concatenate([act_two, zero_row], axis=0)
    send_rows = padded[slot_source].reshape(owners, local_experts * capacity, model_width)
    arrived = lax.all_to_all(send_rows, "expert", split_axis=0, concat_axis=0, tiled=True).reshape(
        owners, local_experts, capacity, model_width
    )
    group = lax.axis_size("wshard")
    local_rows = owners * capacity

    def by_expert(chunk):
        rows = jnp.transpose(chunk, (1, 0, 2, 3)).reshape(local_experts, local_rows, model_width)
        return lax.all_gather(rows, "wshard", axis=1, tiled=True)

    def home_rows(rows):
        own = lax.psum_scatter(rows.astype(jnp.bfloat16), "wshard", scatter_dimension=1, tiled=True)
        own = own.reshape(local_experts, owners, capacity, model_width)
        return jnp.transpose(own, (1, 0, 2, 3)).reshape(
            owners, local_experts * capacity, model_width
        )

    grad_output = cotangent.astype(jnp.float32)
    grad_combined = (gate_value[:, None] * grad_output).astype(jnp.bfloat16)
    grad_padded = jnp.concatenate([grad_combined, zero_row], axis=0)
    grad_send = grad_padded[slot_source].reshape(owners, local_experts * capacity, model_width)
    grad_arrived = lax.all_to_all(
        grad_send, "expert", split_axis=0, concat_axis=0, tiled=True
    ).reshape(owners, local_experts, capacity, model_width)
    rows_in = by_expert(arrived)
    grad_rows = by_expert(grad_arrived)
    pre_act = jnp.einsum("erd,edf->erf", rows_in, w_up, preferred_element_type=jnp.float32)
    activated, gelu_pull = jax.vjp(gelu_tanh, pre_act)
    act_hidden = activated.astype(jnp.bfloat16)
    produced = jnp.einsum(
        "erf,efd->erd", act_hidden, w_down, preferred_element_type=jnp.float32
    )
    expert_out = home_rows(produced)
    returned = lax.all_to_all(expert_out, "expert", split_axis=0, concat_axis=0, tiled=True)
    slots_back = jnp.concatenate([returned.reshape(slot_count, model_width), zero_row], axis=0)
    combined = slots_back[slot_index].astype(jnp.float32)
    output = (hidden + gate_value[:, None] * combined).astype(jnp.bfloat16)
    grad_gate = jnp.sum(grad_output * combined, axis=1)
    grad_down = jnp.einsum(
        "erf,erd->efd", act_hidden, grad_rows, preferred_element_type=jnp.float32
    )
    grad_hidden_units = jnp.einsum(
        "erd,efd->erf", grad_rows, w_down, preferred_element_type=jnp.float32
    )
    grad_pre = gelu_pull(grad_hidden_units)[0].astype(jnp.bfloat16)
    grad_up = jnp.einsum("erd,erf->edf", rows_in, grad_pre, preferred_element_type=jnp.float32)
    grad_expert_in = jnp.einsum(
        "erf,edf->erd", grad_pre, w_up, preferred_element_type=jnp.float32
    )
    grad_send_back = home_rows(grad_expert_in)
    grad_back = lax.all_to_all(grad_send_back, "expert", split_axis=0, concat_axis=0, tiled=True)
    grad_slots = jnp.concatenate([grad_back.reshape(slot_count, model_width), zero_row], axis=0)
    grad_act_two = grad_slots[slot_index].astype(jnp.float32)
    grad_logits = (
        gate_prob * (jnp.where(chosen, grad_gate[:, None], 0.0) - (gate_value * grad_gate)[:, None])
    ).astype(jnp.bfloat16)
    grad_router = contract_rows(act_two, grad_logits)
    grad_act_two = grad_act_two + times_transpose(grad_logits, router_full)
    grad_from_two, grad_gain_two, grad_shift_two = norm_back(
        grad_act_two, scaled_two, inverse_two, gain_two
    )
    grad_hidden = grad_output + grad_from_two
    grad_attn = grad_hidden.astype(jnp.bfloat16)
    grad_out_w = contract_rows(merged, grad_attn)
    grad_merged = times_transpose(grad_attn, out_full).astype(jnp.bfloat16)
    grad_qkv = attend_backward(
        query_heads, key_heads, value_heads, grad_merged, log_totals, prefix_len
    )
    grad_qkv_w = contract_rows(act_one, grad_qkv)
    grad_act_one = times_transpose(grad_qkv, qkv_full)
    grad_from_one, grad_gain_one, grad_shift_one = norm_back(
        grad_act_one, scaled_one, inverse_one, gain_one
    )
    grad_tokens = grad_hidden + grad_from_one
    small_grad = jnp.concatenate(
        [
            grad_gain_one[None],
            grad_shift_one[None],
            grad_gain_two[None],
            grad_shift_two[None],
            grad_router.T,
        ],
        axis=0,
    )
    out_share = lax.psum_scatter(
        grad_out_w.astype(jnp.bfloat16), "wshard", scatter_dimension=0, tiled=True
    )
    qkv_share = lax.psum_scatter(
        grad_qkv_w.astype(jnp.bfloat16), "wshard", scatter_dimension=0, tiled=True
    )
    small_share = lax.psum_scatter(small_grad, "wshard", scatter_dimension=1, tiled=True)
    out_total = lax.psum(out_share, "expert").astype(jnp.float32)
    qkv_total = lax.psum(qkv_share, "expert").astype(jnp.float32)
    small_total = lax.psum(small_share, "expert")
    totals = (
        small_total[0],
        small_total[1],
        qkv_total,
        out_total,
        small_total[2],
        small_total[3],
        small_total[4:].T,
    )
    return (
        output,
        grad_tokens,
        totals[0],
        totals[1],
        totals[2],
        totals[3],
        totals[4],
        totals[5],
        totals[6],
        grad_up,
        grad_down,
    )


def on_device(
    tokens,
    norm1_gain,
    norm1_shift,
    w_qkv,
    w_out,
    norm2_gain,
    norm2_shift,
    w_router,
    w_up,
    w_down,
    routes,
    priority,
    prefix,
    cotangent,
):
    row_count, model_width = tokens.shape
    expert_count = w_router.shape[1]
    capacity = row_count // expert_count
    owners = lax.axis_size("expert")
    experts = w_up.shape[0]
    small = jnp.concatenate(
        [norm1_gain[None], norm1_shift[None], norm2_gain[None], norm2_shift[None], w_router.T],
        axis=0,
    )
    lead = small.shape[0]
    small = jnp.pad(small, ((0, -lead % 16), (0, 0)))
    (
        qkv, act_t, merged_t, back, weight, out_full, low, high, grad_rows, hidden, send_rows,
        vectors,
    ) = run_front(
        owners, experts, capacity, prefix, routes, priority, tokens, cotangent, small, w_qkv, w_out
    )
    router = jnp.transpose(vectors[:, 4:lead], (0, 2, 1)).reshape(model_width, expert_count)
    router = jnp.pad(router, ((0, 0), (0, LANES - expert_count)))
    home_out, home_grad, rows, scaled, act_hidden, grad_pre, grad_router = run_experts(
        owners, capacity, expert_count, send_rows, grad_rows, w_up, w_down, router
    )
    grad_down = jnp.einsum("erf,erd->efd", act_hidden, scaled, preferred_element_type=jnp.float32)
    grad_up = jnp.einsum("erd,erf->edf", rows, grad_pre, preferred_element_type=jnp.float32)
    output, grad_tokens, small_total, qkv_total, out_total = run_back(
        owners, lead + -lead % 8, home_grad.reshape(-1, model_width),
        home_out.reshape(-1, model_width), back, hidden, cotangent, tokens, vectors, grad_router,
        act_t, merged_t, qkv, weight, out_full, low, high,
    )
    return (
        output,
        grad_tokens,
        small_total[0],
        small_total[1],
        qkv_total.astype(jnp.float32),
        out_total.astype(jnp.float32),
        small_total[2],
        small_total[3],
        small_total[4:lead].T,
        grad_up,
        grad_down,
    )


def solution(mesh):
    placed = (
        P(("expert", "wshard"), None),
        P("wshard"),
        P("wshard"),
        P("wshard", None),
        P("wshard", None),
        P("wshard"),
        P("wshard"),
        P("wshard", None),
        P("expert", None, "wshard"),
        P("expert", "wshard", None),
        P(("expert", "wshard"), None),
        P(("expert", "wshard"), None),
        P(("expert", "wshard")),
        P(("expert", "wshard"), None),
    )
    owners, group = mesh.shape["expert"], mesh.shape["wshard"]

    def body(*args):
        capacity = args[0].shape[0] // args[7].shape[1]
        fits = group == 4 and owners % 2 == 0 and capacity % 16 == 0
        return (on_device if fits else on_device_plain)(*args)

    return jax.shard_map(
        body,
        mesh=mesh,
        in_specs=placed,
        out_specs=(
            P(("expert", "wshard"), None),
            P(("expert", "wshard"), None),
            P("wshard"),
            P("wshard"),
            P("wshard", None),
            P("wshard", None),
            P("wshard"),
            P("wshard"),
            P("wshard", None),
            P("expert", None, "wshard"),
            P("expert", "wshard", None),
        ),
        check_vma=False,
    )
```

```python
import functools
import math

import jax
import jax.numpy as jnp
from jax import lax
from jax.experimental import pallas as pl
from jax.experimental.pallas import tpu as pltpu
from jax.sharding import PartitionSpec as P

HEADS = 16
HEAD_DIM = 64


epsilon = 1e-05
VMEM_LIMIT = 66_000_000
TILE = 512


def normalize(values, gain_vec, shift_vec):
    row_mean = jnp.mean(values, axis=-1, keepdims=True)
    centered = values - row_mean
    inverse = lax.rsqrt(jnp.mean(centered * centered, axis=-1, keepdims=True) + epsilon)
    scaled = centered * inverse
    return (scaled * gain_vec + shift_vec, scaled, inverse)


def norm_back(grad_rows, scaled, inverse, gain_vec):
    weighted = grad_rows * gain_vec
    mean_one = jnp.mean(weighted, axis=-1, keepdims=True)
    mean_two = jnp.mean(weighted * scaled, axis=-1, keepdims=True)
    grad_inputs = inverse * (weighted - mean_one - scaled * mean_two)
    return (grad_inputs, jnp.sum(grad_rows * scaled, axis=0), jnp.sum(grad_rows, axis=0))


def contract_rows(left, right):
    return lax.dot_general(
        left, right, (((0,), (0,)), ((), ())), preferred_element_type=jnp.float32
    )


def times_transpose(left, right):
    return lax.dot_general(
        left, right, (((1,), (1,)), ((), ())), preferred_element_type=jnp.float32
    )


def gelu_tanh(values):
    return jax.nn.gelu(values, approximate=True)


def assign_slots(route_ids, order_ids, expert_count, capacity):
    token_count = route_ids.shape[0]
    same_expert = route_ids[:, None] == route_ids[None, :]
    earlier = order_ids[None, :] < order_ids[:, None]
    rank_ids = jnp.sum((same_expert & earlier).astype(jnp.int32), axis=1)
    is_kept = rank_ids < capacity
    slot_index = jnp.where(is_kept, route_ids * capacity + rank_ids, expert_count * capacity)
    slot_ids = jnp.arange(expert_count * capacity, dtype=jnp.int32)
    match_table = slot_index[None, :] == slot_ids[:, None]
    token_ids = jnp.arange(token_count, dtype=jnp.int32)
    filled = jnp.any(match_table, axis=1)
    picked = jnp.sum(jnp.where(match_table, token_ids[None, :], 0), axis=1)
    slot_source = jnp.where(filled, picked, token_count)
    return (slot_index, slot_source)


def group_heads(values, groups):
    token_count = values.shape[0]
    return jnp.transpose(values.reshape(token_count, groups, -1, HEAD_DIM), (1, 0, 2, 3))


def block_scores(query_block, key_group, block_start, prefix_len):
    block_rows = query_block.shape[0]
    key_count = key_group.shape[0]
    scores = jnp.einsum(
        "qgd,kgd->gqk", query_block, key_group, preferred_element_type=jnp.float32
    ) * (1.0 / math.sqrt(HEAD_DIM))
    query_pos = block_start + jnp.arange(block_rows, dtype=jnp.int32)
    key_pos = jnp.arange(key_count, dtype=jnp.int32)
    allowed = (key_pos[None, :] <= query_pos[:, None]) | (key_pos[None, :] < prefix_len)
    return jnp.where(allowed[None], scores, -1e30)


def attend_forward(query_heads, key_heads, value_heads, prefix_len):
    token_count = query_heads.shape[0]
    group_size = min(4, HEADS)
    groups = HEADS // group_size
    block_rows = min(512, token_count)
    blocks = token_count // block_rows
    starts = jnp.arange(blocks, dtype=jnp.int32) * block_rows

    def one_group(group_item):
        query_group, key_group, value_group = group_item
        query_blocks = query_group.reshape(blocks, block_rows, group_size, HEAD_DIM)

        def one_block(block_item):
            query_block, block_start = block_item
            scores = block_scores(query_block, key_group, block_start, prefix_len)
            row_max = jnp.max(scores, axis=-1, keepdims=True)
            exponent = jnp.exp(scores - row_max)
            row_total = jnp.sum(exponent, axis=-1, keepdims=True)
            attn_probs = (exponent / row_total).astype(jnp.bfloat16)
            result = jnp.einsum(
                "gqk,kgd->qgd", attn_probs, value_group, preferred_element_type=jnp.float32
            )
            return (result, (row_max + jnp.log(row_total))[..., 0])

        return lax.map(one_block, (query_blocks, starts))

    attended, log_totals = lax.map(
        one_group,
        (
            group_heads(query_heads, groups),
            group_heads(key_heads, groups),
            group_heads(value_heads, groups),
        ),
    )
    merged = (
        jnp.transpose(attended, (1, 2, 0, 3, 4))
        .reshape(token_count, HEADS * HEAD_DIM)
        .astype(jnp.bfloat16)
    )
    return (merged, log_totals)


def attend_backward(query_heads, key_heads, value_heads, grad_merged, log_totals, prefix_len):
    token_count = query_heads.shape[0]
    group_size = min(4, HEADS)
    groups = HEADS // group_size
    block_rows = min(512, token_count)
    blocks = token_count // block_rows
    starts = jnp.arange(blocks, dtype=jnp.int32) * block_rows
    score_scale = 1.0 / math.sqrt(HEAD_DIM)

    def one_group(group_item):
        query_group, key_group, value_group, grad_group, total_group = group_item
        query_blocks = query_group.reshape(blocks, block_rows, group_size, HEAD_DIM)
        grad_blocks = grad_group.reshape(blocks, block_rows, group_size, HEAD_DIM)

        def one_block(carry, block_item):
            grad_keys, grad_vals = carry
            query_block, grad_block, total_block, block_start = block_item
            scores = block_scores(query_block, key_group, block_start, prefix_len)
            attn_probs = jnp.exp(scores - total_block[..., None])
            grad_probs = jnp.einsum(
                "qgd,kgd->gqk", grad_block, value_group, preferred_element_type=jnp.float32
            )
            row_delta = jnp.sum(attn_probs * grad_probs, axis=-1, keepdims=True)
            grad_scores = (attn_probs * (grad_probs - row_delta)).astype(jnp.bfloat16)
            grad_vals = grad_vals + jnp.einsum(
                "gqk,qgd->kgd",
                attn_probs.astype(jnp.bfloat16),
                grad_block,
                preferred_element_type=jnp.float32,
            )
            grad_keys = (
                grad_keys
                + jnp.einsum(
                    "gqk,qgd->kgd", grad_scores, query_block, preferred_element_type=jnp.float32
                )
                * score_scale
            )
            grad_query = (
                jnp.einsum(
                    "gqk,kgd->qgd", grad_scores, key_group, preferred_element_type=jnp.float32
                )
                * score_scale
            )
            return ((grad_keys, grad_vals), grad_query)

        zero_keys = jnp.zeros(key_group.shape, jnp.float32)
        carried, grad_queries = lax.scan(
            one_block, (zero_keys, zero_keys), (query_blocks, grad_blocks, total_group, starts)
        )
        return (grad_queries, carried[0], carried[1])

    grad_queries, grad_keys, grad_vals = lax.map(
        one_group,
        (
            group_heads(query_heads, groups),
            group_heads(key_heads, groups),
            group_heads(value_heads, groups),
            group_heads(grad_merged, groups),
            log_totals,
        ),
    )
    query_part = jnp.transpose(grad_queries, (1, 2, 0, 3, 4)).reshape(token_count, HEADS * HEAD_DIM)
    key_part = jnp.transpose(grad_keys, (1, 0, 2, 3)).reshape(token_count, HEADS * HEAD_DIM)
    value_part = jnp.transpose(grad_vals, (1, 0, 2, 3)).reshape(token_count, HEADS * HEAD_DIM)
    return jnp.concatenate([query_part, key_part, value_part], axis=1).astype(jnp.bfloat16)


MESH = pl.DeviceIdType.MESH
LANES = 128


def dot_nn(left, right):
    return lax.dot_general(
        left, right, (((1,), (0,)), ((), ())), preferred_element_type=jnp.float32
    )


def dot_nt(left, right):
    return lax.dot_general(
        left, right, (((1,), (1,)), ((), ())), preferred_element_type=jnp.float32
    )


def dot_tn(left, right):
    return lax.dot_general(
        left, right, (((0,), (0,)), ((), ())), preferred_element_type=jnp.float32
    )


def span(start, size):
    return pl.ds(pl.multiple_of(start, size), size)


def every(start, stop, step):
    def body(i, carry):
        step(i)
        return carry

    lax.fori_loop(start, stop, body, 0)


class Place:
    def __init__(self, owners):
        self.owners = owners
        self.e = lax.axis_index("expert")
        self.w = lax.axis_index("wshard")
        self.c = lax.rem(self.w, 2)
        self.x = lax.div(self.w, 2)
        self.sib = self.w + 1 - 2 * self.c
        self.far = lax.rem(self.w + 2, 4)
        self.diag = 3 - self.w
        self.pair = self.e + 1 - 2 * lax.rem(self.e, 2)

    def ahead(self, k):
        return lax.rem(self.e + k, self.owners)

    def peer(self, n):
        other = lax.div(n, 2) + lax.rem(n, 2) * (self.owners // 2)
        result, bit = 0, 1
        while bit < self.owners:
            result = result + bit * lax.rem(lax.div(self.e, bit) + lax.div(other, bit), 2)
            bit *= 2
        return result


def remote(src, dst, send, recv, device):
    return pltpu.make_async_remote_copy(
        src_ref=src,
        dst_ref=dst,
        send_sem=send,
        recv_sem=recv,
        device_id=device,
        device_id_type=MESH,
    )


def greet(peers):
    barrier = pltpu.get_barrier_semaphore()
    for peer in peers:
        pl.semaphore_signal(barrier, inc=1, device_id=peer, device_id_type=MESH)
    pl.semaphore_wait(barrier, len(peers))


def either(test, yes, no):
    pl.when(test)(yes)
    pl.when(jnp.logical_not(test))(no)


class Dispatch:
    def __init__(self, place, capacity, send_ref, rows_ref, sems):
        self.p, self.cap, self.src, self.rows = place, capacity, send_ref, rows_ref
        self.own_sem, self.send, self.recv = sems

    def slice(self, k, core, side):
        start = (((lax.div(k, 2) * 2 + core) * 2 + side) * 2 + lax.rem(k, 2)) * self.cap
        return self.rows.at[:, span(start, self.cap)]

    def own(self):
        return pltpu.make_async_copy(
            self.src.at[self.p.e], self.slice(0, self.p.c, self.p.x), self.own_sem
        )

    def direct(self, k):
        return remote(
            self.src.at[self.p.peer(k)],
            self.slice(k, self.p.c, self.p.x),
            self.send.at[0, k],
            self.recv.at[0, k],
            (self.p.peer(k), self.p.w),
        )

    def hop(self, k, side, which, peer):
        part = self.slice(k, self.p.c, side)
        return remote(
            part, part, self.send.at[which, k], self.recv.at[which, k], (self.p.e, peer)
        )

    def to_sib(self, k):
        return self.hop(k, self.p.x, 1, self.p.sib)

    def to_far(self, k):
        return self.hop(k, self.p.x, 2, self.p.far)

    def relayed(self, k):
        return self.hop(k, 1 - self.p.x, 3, self.p.sib)

    def start(self):
        self.own().start()
        every(1, self.p.owners, lambda k: self.direct(k).start())

    def forward(self, k):
        k = jnp.int32(k)

        @pl.when(k == 0)
        def _():
            self.own().wait()

        @pl.when(k > 0)
        def _():
            self.direct(k).wait_recv()

        self.to_far(k).start()
        self.to_sib(k).start()

    def relay(self, k):
        self.to_far(k).wait_recv()
        self.relayed(k).start()

    def ready(self, k):
        self.to_sib(k).wait_recv()
        self.relayed(k).wait_recv()

    def drain(self):
        every(1, self.p.owners, lambda k: self.direct(k).wait_send())

        def rest(k):
            self.to_sib(k).wait_send()
            self.to_far(k).wait_send()
            self.relayed(k).wait_send()

        every(0, self.p.owners, rest)


class Return:
    def __init__(self, place, capacity, experts, part, got, mid, far, done, home, sems):
        self.p, self.cap, self.experts = place, capacity, experts
        self.part, self.got, self.mid, self.far, self.done, self.home = (
            part, got, mid, far, done, home,
        )
        self.own_sem, self.send, self.recv, self.home_send, self.home_recv = sems

    def swapped(self, j):
        size = 4 * self.cap
        return remote(
            self.part.at[:, span((j * 2 + 1 - self.p.c) * size, size)],
            self.got.at[:, span(j * size, size)],
            self.send.at[0, j],
            self.recv.at[0, j],
            (self.p.e, self.p.sib),
        )

    def crossed(self, j):
        part = span(j * 2 * self.cap, 2 * self.cap)
        return remote(
            self.mid.at[:, part],
            self.far.at[:, part],
            self.send.at[1, j],
            self.recv.at[1, j],
            (self.p.e, self.p.far),
        )

    def own(self):
        return pltpu.make_async_copy(self.done.at[0], self.home.at[self.p.e], self.own_sem)

    def homed(self, n):
        return remote(
            self.done.at[n],
            self.home.at[self.p.e],
            self.home_send.at[n],
            self.home_recv.at[n],
            (self.p.peer(n), self.p.w),
        )

    def pair_sum(self, expert, j, side):
        size = 2 * self.cap
        mine = self.part[expert, span(((j * 2 + self.p.c) * 2 + side) * size, size), :]
        theirs = self.got[expert, span((j * 2 + side) * size, size), :]
        return mine.astype(jnp.float32) + theirs.astype(jnp.float32)

    def swap(self, j):
        self.swapped(j).start()

    def cross(self, j):
        self.swapped(j).wait_recv()
        size = 2 * self.cap
        for expert in range(self.experts):
            self.mid[expert, span(j * size, size), :] = self.pair_sum(
                expert, j, 1 - self.p.x
            ).astype(jnp.bfloat16)
        self.crossed(j).start()

    def finish(self, j):
        self.crossed(j).wait_recv()
        size = 2 * self.cap
        for expert in range(self.experts):
            total = self.pair_sum(expert, j, self.p.x) + self.far[
                expert, span(j * size, size), :
            ].astype(jnp.float32)
            total = total.astype(jnp.bfloat16)
            self.done[2 * j, expert] = total[: self.cap]
            self.done[2 * j + 1, expert] = total[self.cap :]
        j = jnp.int32(j)
        self.homed(2 * j + 1).start()
        either(j == 0, lambda: self.own().start(), lambda: self.homed(2 * j).start())

    def drain(self, chunks):
        def one(j):
            self.swapped(j).wait_send()
            self.crossed(j).wait_send()

        every(0, chunks, one)
        self.own().wait()
        every(1, self.p.owners, lambda n: self.homed(n).wait())


def gelu_pair(v):
    root = math.sqrt(2.0 / math.pi)
    square = v * v
    t = jnp.tanh(v * (root + (root * 0.044715) * square))
    half = 0.5 + 0.5 * t
    slope = half + (half * (1.0 - t)) * (v * (root + (3.0 * root * 0.044715) * square))
    return v * half, slope


def expert_kernel(
    dims,
    send_ref, grads_hbm, up_hbm, down_hbm, router_ref,
    home_out, home_grad, up_out, down_out, router_grad,
    rows, grads, scaled, hidden, pre, up, down, grad_up, grad_down,
    part_out, part_grad, got_out, got_grad, mid_out, mid_grad,
    far_out, far_grad, done_out, done_grad,
    load_sem, own_sem, disp_send, disp_recv, red_send, red_recv, home_send, home_recv,
):
    owners, experts, capacity, width, units, expert_count = dims
    place = Place(owners)
    loads = [
        pltpu.make_async_copy(src, dst, load_sem.at[i])
        for i, (src, dst) in enumerate(
            [(up_hbm, up), (grads_hbm, grads), (down_hbm, down)]
        )
    ]
    for load in loads:
        load.start()
    greet(
        [(place.ahead(k), place.w) for k in range(1, owners)]
        + [(place.e, place.sib), (place.e, place.far)]
    )
    dispatch = Dispatch(
        place, capacity, send_ref, rows, (own_sem.at[0], disp_send, disp_recv)
    )
    ret_grad, ret_out = [
        Return(
            place, capacity, experts, part, got, mid, far, done, home,
            (own_sem.at[1 + i], red_send.at[i], red_recv.at[i], home_send.at[i], home_recv.at[i]),
        )
        for i, (part, got, mid, far, done, home) in enumerate(
            [
                (part_grad, got_grad, mid_grad, far_grad, done_grad, home_grad),
                (part_out, got_out, mid_out, far_out, done_out, home_out),
            ]
        )
    ]
    dispatch.start()
    router_grad[...] = jnp.zeros_like(router_grad)
    tile = min(TILE, units)
    wide = min(TILE, width)
    chunks = owners // 2
    size = 8 * capacity
    lane = lax.broadcasted_iota(jnp.int32, (size, LANES), 1)

    def compute(j, expert):
        here = span(j * size, size)
        logits = dot_nn(rows[expert, here, :], router_ref[...])
        logits = jnp.where(lane < expert_count, logits, -1e30)
        exponent = jnp.exp(logits - jnp.max(logits, axis=1, keepdims=True))
        prob = exponent * (1.0 / jnp.sum(exponent, axis=1, keepdims=True))
        mine = lane == place.e * experts + expert
        gate = jnp.sum(jnp.where(mine, prob, 0.0), axis=1, keepdims=True)
        scaled[expert, here, :] = (
            gate * grads[expert, here, :].astype(jnp.float32)
        ).astype(jnp.bfloat16)

        def one_tile(n):
            cols = span(n * tile, tile)
            value, slope = gelu_pair(dot_nn(rows[expert, here, :], up[expert, :, cols]))
            hidden[expert, here, cols] = value.astype(jnp.bfloat16)
            back = dot_nt(scaled[expert, here, :], down[expert, cols, :])
            pre[expert, here, cols] = (back * slope).astype(jnp.bfloat16)

        every(0, units // tile, one_tile)

        def one_out(n, total):
            cols = span(n * wide, wide)
            value = dot_nn(hidden[expert, here, :], down[expert, :, cols])
            part_out[expert, here, cols] = (gate * value).astype(jnp.bfloat16)
            weighted = value * grads[expert, here, cols].astype(jnp.float32)
            for start in range(0, wide, LANES):
                total = total + weighted[:, start : start + LANES]
            return total

        total = lax.fori_loop(
            0, width // wide, one_out, jnp.zeros((size, LANES), jnp.float32)
        )
        grad_gate = jnp.sum(total, axis=1, keepdims=True)
        grad_logits = (
            prob * ((jnp.where(mine, 1.0, 0.0) - gate) * grad_gate)
        ).astype(jnp.bfloat16)

        def one_in(n):
            cols = span(n * wide, wide)
            value = dot_nt(pre[expert, here, :], up[expert, cols, :]) + dot_nt(
                grad_logits, router_ref[cols, :]
            )
            part_grad[expert, here, cols] = value.astype(jnp.bfloat16)
            router_grad[:, cols] += dot_tn(grad_logits, rows[expert, here, cols])

        every(0, width // wide, one_in)

    block = min(256, width)

    def weight_grads(expert, first, last):
        def one(n):
            part = span(n * block, block)
            grad_down[expert, part, :] = dot_tn(
                hidden[expert, :, part], scaled[expert]
            ).astype(jnp.bfloat16)
            grad_up[expert, part, :] = dot_tn(rows[expert, :, part], pre[expert]).astype(
                jnp.bfloat16
            )

        every(first * width // block // 4, last * width // block // 4, one)

    def keep(expert):
        return [
            pltpu.make_async_copy(src.at[expert], dst.at[expert], load_sem.at[2 * expert + i])
            for i, (src, dst) in enumerate(((grad_up, up_out), (grad_down, down_out)))
        ]

    def arrive(j):
        for n in (2 * j, 2 * j + 1):
            dispatch.relay(n)
        for n in (2 * j, 2 * j + 1):
            dispatch.ready(n)

    def forward(j):
        dispatch.forward(2 * j)
        dispatch.forward(2 * j + 1)

    forward(0)
    forward(1)
    for load in loads:
        load.wait()

    def step(j):
        arrive(j)
        compute(j, 0)
        pl.when(j + 2 < chunks)(lambda: forward(j + 2))
        pl.when(j >= 1)(lambda: ret_grad.cross(j - 1))

        @pl.when(j >= 2)
        def _():
            ret_grad.finish(j - 2)
            ret_out.cross(j - 2)

        for expert in range(1, experts):
            compute(j, expert)
        ret_grad.swap(j)
        ret_out.swap(j)

    every(0, chunks, step)
    weight_grads(0, 0, 1)
    ret_grad.cross(chunks - 1)
    ret_out.cross(chunks - 2)
    ret_grad.finish(chunks - 2)
    ret_out.cross(chunks - 1)
    weight_grads(0, 1, 3)
    every(0, chunks - 2, ret_out.finish)
    weight_grads(0, 3, 4)
    for store in keep(0):
        store.start()
    ret_grad.finish(chunks - 1)
    for expert in range(1, experts):
        weight_grads(expert, 0, 2)
        if expert == 1:
            ret_out.finish(chunks - 2)
        weight_grads(expert, 2, 4)
        for store in keep(expert):
            store.start()
    ret_out.finish(chunks - 1)
    for expert in range(experts):
        for store in keep(expert):
            store.wait()
    dispatch.drain()
    ret_grad.drain(chunks)
    ret_out.drain(chunks)


def run_experts(owners, capacity, expert_count, send_rows, grads, w_up, w_down, router):
    experts, width, units = w_up.shape
    slots = owners * 4 * capacity
    chunks = owners // 2
    dims = (owners, experts, capacity, width, units, expert_count)
    any_spec = pl.BlockSpec(memory_space=pl.ANY)
    vmem_spec = pl.BlockSpec(memory_space=pltpu.VMEM)
    bf16 = jnp.bfloat16
    home = jax.ShapeDtypeStruct((owners, experts, capacity, width), bf16)
    dma = pltpu.SemaphoreType.DMA

    def vm(*shape):
        return pltpu.VMEM(shape, bf16)

    return pl.pallas_call(
        functools.partial(expert_kernel, dims),
        out_shape=(
            home, home,
            jax.ShapeDtypeStruct(w_up.shape, bf16),
            jax.ShapeDtypeStruct(w_down.shape, bf16),
            jax.ShapeDtypeStruct((LANES, width), jnp.float32),
        ),
        in_specs=[any_spec] * 4 + [vmem_spec],
        out_specs=(any_spec,) * 4 + (vmem_spec,),
        scratch_shapes=[
            vm(experts, slots, width),
            vm(experts, slots, width),
            vm(experts, slots, width),
            vm(experts, slots, units),
            vm(experts, slots, units),
            vm(experts, width, units),
            vm(experts, units, width),
            vm(experts, width, units),
            vm(experts, units, width),
            vm(experts, slots, width),
            vm(experts, slots, width),
            vm(experts, slots // 2, width),
            vm(experts, slots // 2, width),
            vm(experts, slots // 4, width),
            vm(experts, slots // 4, width),
            vm(experts, slots // 4, width),
            vm(experts, slots // 4, width),
            vm(owners, experts, capacity, width),
            vm(owners, experts, capacity, width),
            dma((4,)),
            dma((3,)),
            dma((4, owners)),
            dma((4, owners)),
            dma((2, 2, chunks)),
            dma((2, 2, chunks)),
            dma((2, owners)),
            dma((2, owners)),
        ],
        compiler_params=pltpu.CompilerParams(
            collective_id=1, has_side_effects=True, vmem_limit_bytes=VMEM_LIMIT
        ),
        name="experts",
    )(send_rows, grads, w_up, w_down, router)


def masked_softmax(scores):
    exponent = jnp.exp(scores - jnp.max(scores, axis=1, keepdims=True))
    return exponent * (1.0 / jnp.sum(exponent, axis=1, keepdims=True))


def attend_head(query, key, value, prefix_len):
    half = query.shape[0] // 2
    query = query * (1.0 / math.sqrt(HEAD_DIM))
    row = lax.broadcasted_iota(jnp.int32, (half, half), 0)
    col = lax.broadcasted_iota(jnp.int32, (half, half), 1)
    low = dot_nt(query[:half], key[:half])
    low = jnp.where((col <= row) | (col < prefix_len), low, -1e30)
    low = masked_softmax(low).astype(jnp.bfloat16)
    high = dot_nt(query[half:], key)
    high = jnp.concatenate(
        [high[:, :half], jnp.where(col <= row, high[:, half:], -1e30)], axis=1
    )
    high = masked_softmax(high).astype(jnp.bfloat16)
    return low, high, dot_nn(low, value[:half]), dot_nn(high, value)


def score_grads(probs, grad_probs):
    probs = probs.astype(jnp.float32)
    weighted = probs * grad_probs
    total = jnp.sum(weighted, axis=1, keepdims=True)
    return (weighted - probs * total).astype(jnp.bfloat16)


def attend_back_head(query, key, value, low, high, grad):
    half = query.shape[0] // 2
    scale = 1.0 / math.sqrt(HEAD_DIM)
    query = query * scale
    grad_low = score_grads(low, dot_nt(grad[:half], value[:half]))
    grad_high = score_grads(high, dot_nt(grad[half:], value))
    grad_query = jnp.concatenate(
        [dot_nn(grad_low, key[:half]), dot_nn(grad_high, key)], axis=0
    )
    value_all = dot_tn(high, grad[half:])
    key_all = dot_tn(grad_high, query[half:])
    grad_value = jnp.concatenate(
        [value_all[:half] + dot_tn(low, grad[:half]), value_all[half:]], axis=0
    )
    grad_key = jnp.concatenate(
        [key_all[:half] + dot_tn(grad_low, query[:half]), key_all[half:]], axis=0
    )
    return (
        (grad_query * scale).astype(jnp.bfloat16),
        grad_key.astype(jnp.bfloat16),
        grad_value.astype(jnp.bfloat16),
    )


class Gather:
    def __init__(self, place, pieces, src, dst, sems):
        self.p, self.src, self.dst = place, src, dst
        self.send, self.recv, self.near_send, self.near_recv, self.own_sem = sems
        self.shard = src.shape[0]
        self.half = self.shard // 2
        self.step = self.half // pieces
        self.pieces = pieces
        self.first = lax.rem(place.e, 2) * self.half
        self.second = self.half - self.first

    def block(self, owner, start, size):
        return self.dst.at[pl.ds(pl.multiple_of(owner * self.shard + start, self.step), size)]

    def own(self):
        return pltpu.make_async_copy(self.src, self.block(self.p.w, 0, self.shard), self.own_sem)

    def near(self):
        return remote(
            self.src, self.block(self.p.w, 0, self.shard), self.near_send, self.near_recv,
            (self.p.e, self.p.sib),
        )

    def hop(self, n):
        return remote(
            self.src.at[span(self.first + n * self.step, self.step)],
            self.block(self.p.w, self.first + n * self.step, self.step),
            self.send.at[0, n], self.recv.at[0, n], (self.p.e, self.p.far),
        )

    def pass_from(self, start, n, which, device):
        part = self.block(self.p.far, start + n * self.step, self.step)
        return remote(part, part, self.send.at[which, n], self.recv.at[which, n], device)

    def pairs(self, n):
        return self.pass_from(self.first, n, 1, (self.p.pair, self.p.w))

    def relay(self, n):
        return self.pass_from(self.first, n, 2, (self.p.e, self.p.sib))

    def pair_relay(self, n):
        return self.pass_from(self.second, n, 3, (self.p.e, self.p.sib))

    def start(self):
        every(0, self.pieces, lambda n: self.hop(n).start())
        self.near().start()

    def pass_on(self, n):
        self.hop(n).wait_recv()
        self.pairs(n).start()
        self.relay(n).start()

    def pass_pair(self, n):
        self.pairs(n).wait_recv()
        self.pair_relay(n).start()

    def near_ready(self):
        self.own().wait()
        self.near().wait_recv()

    def far_ready(self):
        def one(n):
            self.relay(n).wait_recv()
            self.pair_relay(n).wait_recv()

        every(0, self.pieces, one)

    def drain(self):
        self.near().wait_send()

        def one(n):
            for copy in (self.hop(n), self.pairs(n), self.relay(n), self.pair_relay(n)):
                copy.wait_send()

        every(0, self.pieces, one)


def slot_tables(routes_ref, priority_ref, capacity, pick_ref, back_ref):
    count = routes_ref.shape[0]
    row = lax.broadcasted_iota(jnp.int32, (count, count), 0).astype(jnp.float32)
    col = lax.broadcasted_iota(jnp.int32, (count, count), 1).astype(jnp.float32)
    eye = row == col
    route_col = routes_ref[...].astype(jnp.float32)
    order_row = priority_ref[...].astype(jnp.float32)
    route_row = jnp.sum(jnp.where(eye, route_col, 0.0), axis=0, keepdims=True)
    order_col = jnp.sum(jnp.where(eye, order_row, 0.0), axis=1, keepdims=True)
    same = route_col == route_row
    rank_row = jnp.sum(
        jnp.where(same & (order_col < order_row), 1.0, 0.0), axis=0, keepdims=True
    )
    rank_col = jnp.sum(
        jnp.where(same & (order_row < order_col), 1.0, 0.0), axis=1, keepdims=True
    )
    slots = float(count)
    slot_row = jnp.where(rank_row < capacity, route_row * capacity + rank_row, slots)
    slot_col = jnp.where(rank_col < capacity, route_col * capacity + rank_col, slots)
    pick_ref[...] = jnp.where(slot_row == row, 1.0, 0.0).astype(jnp.bfloat16)
    back_ref[...] = jnp.where(slot_col == col, 1.0, 0.0).astype(jnp.bfloat16)


def norm_stats(value):
    centered = value - jnp.mean(value, axis=1, keepdims=True)
    inverse = lax.rsqrt(jnp.mean(centered * centered, axis=1, keepdims=True) + epsilon)
    return centered * inverse, inverse


def front_kernel(
    dims,
    prefix_ref, routes_ref, priority_ref, tokens_ref, cot_ref, small_hbm, qkv_hbm, out_hbm,
    qkv_out, act_out, merged_out, back_out, weight_out, out_full, low_out, high_out, grads_rows,
    hidden_ref, send_ref, small_out,
    small, weight, out_w, total, qkv, act, merged, act_two, turned, pick, back, grads_send, low_buf, high_buf,
    own_sem, disp_send, disp_recv, small_send, small_recv, near_send, near_recv,
    gat_send, gat_recv, store_sem, prob_sem,
):
    owners, capacity, pieces = dims
    place = Place(owners)
    rows, width = tokens_ref.shape
    shard = qkv_hbm.shape[0]
    gathers = [
        Gather(
            place, pieces, src, dst,
            (gat_send.at[i], gat_recv.at[i], near_send.at[i], near_recv.at[i], own_sem.at[1 + i]),
        )
        for i, (src, dst) in enumerate(((qkv_hbm, weight), (out_hbm, out_w)))
    ]
    for gather in gathers:
        gather.own().start()
    own_small = pltpu.make_async_copy(small_hbm, small.at[place.w], own_sem.at[3])
    own_small.start()
    greet(
        [(place.ahead(k), place.w) for k in range(1, owners)]
        + [(place.e, place.sib), (place.e, place.far), (place.e, place.diag)]
    )
    smalls = [
        remote(small_hbm, small.at[place.w], small_send.at[i], small_recv.at[i], (place.e, peer))
        for i, peer in enumerate((place.sib, place.far, place.diag))
    ]
    for copy in smalls:
        copy.start()
    for gather in gathers:
        gather.start()
    slot_tables(routes_ref, priority_ref, capacity, pick, back)
    tile = min(256, width)
    shape = grads_send.shape[:3]

    def to_slots(values_ref, slots_ref):
        def one(n):
            cols = span(n * tile, tile)
            value = dot_nn(pick[...], values_ref[:, cols]).astype(jnp.bfloat16)
            slots_ref[:, :, :, cols] = value.reshape(shape + (tile,))

        every(0, width // tile, one)

    to_slots(cot_ref, grads_send)
    dispatch = Dispatch(
        place, capacity, grads_send, grads_rows, (own_sem.at[0], disp_send, disp_recv)
    )
    dispatch.start()
    own_small.wait()
    for copy in smalls:
        copy.wait_recv()
    small_out[...] = small[...]

    def vector(which):
        parts = [small[i, which : which + 1, :] for i in range(4)]
        return jnp.concatenate(parts, axis=1).astype(jnp.float32)

    band = min(64, rows)
    gain, shift = vector(0), vector(1)

    def norm_band(i):
        part = span(i * band, band)
        scaled, _ = norm_stats(tokens_ref[part, :].astype(jnp.float32))
        act[part, :] = (scaled * gain + shift).astype(jnp.bfloat16)

    columns = weight.shape[1]
    wide = min(512, columns)

    def multiply(owner, cols):
        depth = span(owner * shard, shard)
        return dot_nn(act[:, depth], weight[depth, cols])

    def first_tile(n):
        cols = span(n * wide, wide)
        total[:, cols] = multiply(place.w, cols) + multiply(place.sib, cols)

    def last_tile(n):
        cols = span(n * wide, wide)
        value = total[:, cols] + multiply(place.far, cols) + multiply(place.diag, cols)
        qkv[:, cols] = value.astype(jnp.bfloat16)

    def pass_piece(gather, n):
        @pl.when(n < pieces)
        def _():
            gather.pass_on(n)

        @pl.when(n >= 1)
        def _():
            gather.pass_pair(n - 1)

    gathers[0].pass_on(0)
    every(0, rows // band, norm_band)
    pass_piece(gathers[0], jnp.int32(1))
    dispatch.forward(0)
    turned[0] = act[...].T
    gathers[0].near_ready()
    every(0, columns // wide, first_tile)
    early = max(pieces - 1, owners // 2)

    def pass_step(n):
        @pl.when(n <= pieces)
        def _():
            pass_piece(gathers[0], n)

        @pl.when(n - 1 < owners)
        def _():
            dispatch.forward(n - 1)

    every(2, early + 2, pass_step)
    gathers[0].far_ready()
    every(0, columns // wide, last_tile)
    stores = [
        pltpu.make_async_copy(src, dst, store_sem.at[i])
        for i, (src, dst) in enumerate(
            [(qkv, qkv_out), (turned.at[0], act_out), (back, back_out), (weight, weight_out),
             (turned.at[1], merged_out), (out_w, out_full)]
        )
    ]
    for store in stores[:4]:
        store.start()
    half = rows // 2
    pairs = width // LANES

    def keep_probs(i):
        slot = lax.rem(i, 2)
        return (
            pltpu.make_async_copy(
                low_buf.at[slot], low_out.at[pl.ds(2 * i, 2)], prob_sem.at[0, slot]
            ),
            pltpu.make_async_copy(
                high_buf.at[slot], high_out.at[pl.ds(2 * i, 2)], prob_sem.at[1, slot]
            ),
        )

    def attend_pair(i):
        slot = lax.rem(i, 2)

        @pl.when(i >= 2)
        def _():
            for copy in keep_probs(i - 2):
                copy.wait()

        query, key, value = (
            qkv[:, span(part * width + i * LANES, LANES)] for part in range(3)
        )
        tops, bottoms = [], []
        for head in range(2):
            part = slice(head * HEAD_DIM, (head + 1) * HEAD_DIM)
            low, high, top, bottom = attend_head(
                query[:, part], key[:, part], value[:, part], prefix_ref[0]
            )
            low_buf[slot, head] = low
            high_buf[slot, head] = high
            tops.append(top)
            bottoms.append(bottom)
        cols = span(i * LANES, LANES)
        merged[:half, cols] = jnp.concatenate(tops, axis=1).astype(jnp.bfloat16)
        merged[half:, cols] = jnp.concatenate(bottoms, axis=1).astype(jnp.bfloat16)
        for copy in keep_probs(i):
            copy.start()

    def attend_step(i):
        @pl.when(i < pairs)
        def _():
            attend_pair(i)

        @pl.when(i + early + 1 < owners)
        def _():
            dispatch.forward(i + early + 1)

        @pl.when((i >= 1) & (i < pieces + 2))
        def _():
            pass_piece(gathers[1], i - 1)

        @pl.when(i < owners)
        def _():
            dispatch.relay(i)

    every(0, max(pairs, owners, pieces + 2), attend_step)
    turned[1] = merged[...].T
    stores[4].start()
    gathers[1].near_ready()
    gathers[1].far_ready()
    stores[5].start()
    gain_two, shift_two = vector(2), vector(3)
    band_two = min(128, rows)

    def middle(i):
        part = span(i * band_two, band_two)
        value = tokens_ref[part, :].astype(jnp.float32) + dot_nn(merged[part, :], out_w[...])
        hidden_ref[part, :] = value
        scaled, _ = norm_stats(value)
        act_two[part, :] = (scaled * gain_two + shift_two).astype(jnp.bfloat16)

    every(0, rows // band_two, middle)
    to_slots(act_two, send_ref)
    for i in (pairs - 2, pairs - 1):
        for copy in keep_probs(i):
            copy.wait()
    every(0, owners, dispatch.ready)
    for store in stores:
        store.wait()
    for copy in smalls:
        copy.wait_send()
    for gather in gathers:
        gather.drain()
    dispatch.drain()


def run_front(owners, experts, capacity, prefix, routes, priority, tokens, cotangent, small, w_qkv, w_out):
    rows, width = tokens.shape
    shard, columns = w_qkv.shape
    half = rows // 2
    heads = width // HEAD_DIM
    pieces = 4
    any_spec = pl.BlockSpec(memory_space=pl.ANY)
    vmem_spec = pl.BlockSpec(memory_space=pltpu.VMEM)
    bf16, f32 = jnp.bfloat16, jnp.float32
    dma = pltpu.SemaphoreType.DMA

    def out(*shape):
        return jax.ShapeDtypeStruct(shape, bf16)

    def vm(*shape):
        return pltpu.VMEM(shape, bf16)

    return pl.pallas_call(
        functools.partial(front_kernel, (owners, capacity, pieces)),
        out_shape=(
            out(rows, columns),
            out(width, rows),
            out(width, rows),
            out(rows, rows),
            out(4 * shard, columns),
            out(4 * shard, width),
            out(heads, half, half),
            out(heads, half, rows),
            out(experts, owners * 4 * capacity, width),
            jax.ShapeDtypeStruct((rows, width), f32),
            out(owners, experts, capacity, width),
            out(4, *small.shape),
        ),
        in_specs=[pl.BlockSpec(memory_space=pltpu.SMEM)] + [vmem_spec] * 4 + [any_spec] * 3,
        out_specs=(any_spec,) * 9 + (vmem_spec,) * 3,
        scratch_shapes=[
            vm(4, *small.shape),
            vm(4 * shard, columns),
            vm(4 * shard, width),
            pltpu.VMEM((rows, columns), f32),
            vm(rows, columns),
            vm(rows, width),
            vm(rows, width),
            vm(rows, width),
            vm(2, width, rows),
            vm(rows, rows),
            vm(rows, rows),
            vm(owners, experts, capacity, width),
            vm(2, 2, half, half),
            vm(2, 2, half, rows),
            dma((4,)),
            dma((4, owners)),
            dma((4, owners)),
            dma((3,)),
            dma((3,)),
            dma((2,)),
            dma((2,)),
            dma((2, 4, pieces)),
            dma((2, 4, pieces)),
            dma((6,)),
            dma((2, 2)),
        ],
        compiler_params=pltpu.CompilerParams(
            collective_id=0, has_side_effects=True, vmem_limit_bytes=VMEM_LIMIT
        ),
        name="front",
    )(prefix, routes, priority, tokens, cotangent, small, w_qkv, w_out)


class Reduce:
    def __init__(self, place, part, got, far, pair, lines, done, sems):
        self.p = place
        self.part, self.got, self.far = part, got, far
        self.pair, self.lines, self.done = pair, lines, done
        self.send, self.recv, self.line_send, self.line_recv = sems
        self.chunks = part.shape[0]
        self.halves = done.shape[1] // 2
        self.count = place.owners // 2
        self.slice = self.halves // self.count
        self.bit = lax.rem(place.e, 2)
        self.level = lax.div(place.e, 2)

    def step(self, which, n, src, dst, device):
        return remote(src, dst, self.send.at[which, n], self.recv.at[which, n], device)

    def swapped(self, n):
        return self.step(
            0, n, self.part.at[n, :, 1 - self.p.c], self.got.at[n], (self.p.e, self.p.sib)
        )

    def crossed(self, n):
        return self.step(
            1, n, self.part.at[n, 1 - self.p.x, self.p.c], self.far.at[n], (self.p.e, self.p.far)
        )

    def folded(self, n):
        other = span((1 - self.bit) * self.halves, self.halves)
        return self.step(
            2, n, self.part.at[n, self.p.x, self.p.c, other], self.pair.at[n],
            (self.p.pair, self.p.w),
        )

    def shared(self, n):
        part = self.done.at[n, span(self.bit * self.halves, self.halves)]
        return self.step(3, n, part, part, (self.p.pair, self.p.w))

    def line(self, which, n, k, src, dst):
        return remote(
            src, dst, self.line_send.at[which, n, k], self.line_recv.at[which, n, k],
            (self.p.ahead(2 * k), self.p.w),
        )

    def row(self, level):
        return span(self.bit * self.halves + level * self.slice, self.slice)

    def spreads(self, n, k):
        target = lax.rem(self.level + k, self.count)
        return self.line(
            0, n, k, self.part.at[n, self.p.x, self.p.c, self.row(target)], self.lines.at[n, k]
        )

    def collects(self, n, k):
        part = self.done.at[n, self.row(self.level)]
        return self.line(1, n, k, part, part)

    def pair_sum(self, n, side):
        return self.part[n, side, self.p.c].astype(jnp.float32) + self.got[n, side].astype(
            jnp.float32
        )

    def swap(self, n):
        self.swapped(n).start()

    def cross(self, n):
        self.swapped(n).wait_recv()
        side = 1 - self.p.x
        self.part[n, side, self.p.c] = self.pair_sum(n, side).astype(jnp.bfloat16)
        self.crossed(n).start()

    def fold(self, n):
        self.crossed(n).wait_recv()
        total = self.pair_sum(n, self.p.x) + self.far[n].astype(jnp.float32)
        self.part[n, self.p.x, self.p.c] = total.astype(jnp.bfloat16)
        self.folded(n).start()

    def spread(self, n):
        self.folded(n).wait_recv()
        own = span(self.bit * self.halves, self.halves)
        total = self.part[n, self.p.x, self.p.c, own, :].astype(jnp.float32) + self.pair[
            n
        ].astype(jnp.float32)
        self.part[n, self.p.x, self.p.c, own, :] = total.astype(jnp.bfloat16)
        for k in range(1, self.count):
            self.spreads(n, k).start()

    def collect(self, n):
        total = self.part[n, self.p.x, self.p.c, self.row(self.level), :].astype(jnp.float32)
        for k in range(1, self.count):
            self.spreads(n, k).wait_recv()
            total = total + self.lines[n, k].astype(jnp.float32)
        self.done[n, self.row(self.level), :] = total.astype(jnp.bfloat16)
        for k in range(1, self.count):
            self.collects(n, k).start()

    def share(self, n):
        for k in range(1, self.count):
            self.collects(n, k).wait_recv()
        self.shared(n).start()

    def finish(self, n):
        self.shared(n).wait_recv()

    def stages(self):
        return (self.cross, self.fold, self.spread, self.collect, self.share, self.finish)

    def drain(self):
        def one(n):
            for copy in (self.swapped(n), self.crossed(n), self.folded(n), self.shared(n)):
                copy.wait_send()
            for k in range(1, self.count):
                self.spreads(n, k).wait_send()
                self.collects(n, k).wait_send()

        every(0, self.chunks, one)


class Small:
    def __init__(self, place, value, part, got, mid, far, total, others, out, sems):
        self.p, self.value, self.part, self.got, self.mid = place, value, part, got, mid
        self.far, self.total, self.others, self.out = far, total, others, out
        self.send, self.recv, self.all_send, self.all_recv = sems

    def swapped(self):
        return remote(
            self.part.at[:, 1 - self.p.c], self.got, self.send.at[0], self.recv.at[0],
            (self.p.e, self.p.sib),
        )

    def crossed(self):
        return remote(
            self.mid, self.far, self.send.at[1], self.recv.at[1], (self.p.e, self.p.far)
        )

    def spreads(self, k):
        return remote(
            self.total, self.others.at[k], self.all_send.at[k], self.all_recv.at[k],
            (self.p.ahead(k), self.p.w),
        )

    def swap(self):
        size = self.part.shape[-1]
        for owner in range(4):
            self.part[owner // 2, owner % 2] = self.value[:, owner * size : (owner + 1) * size]
        self.swapped().start()

    def cross(self):
        self.swapped().wait_recv()
        self.mid[...] = self.part[1 - self.p.x, self.p.c] + self.got[1 - self.p.x]
        self.crossed().start()

    def spread(self):
        self.crossed().wait_recv()
        self.total[...] = self.part[self.p.x, self.p.c] + self.got[self.p.x] + self.far[...]
        for k in range(1, self.p.owners):
            self.spreads(k).start()

    def finish(self):
        total = self.total[...]
        for k in range(1, self.p.owners):
            self.spreads(k).wait_recv()
            total = total + self.others[k]
        self.out[...] = total

    def drain(self):
        self.swapped().wait_send()
        self.crossed().wait_send()
        for k in range(1, self.p.owners):
            self.spreads(k).wait_send()


def norm_back_rows(grad, scaled, inverse, gain):
    weighted = grad * gain
    mean_one = jnp.mean(weighted, axis=1, keepdims=True)
    mean_two = jnp.mean(weighted * scaled, axis=1, keepdims=True)
    return inverse * (weighted - mean_one - scaled * mean_two)


def back_kernel(
    dims,
    home_grad_ref, home_out_ref, back_ref, hidden_ref, cot_ref, tokens_ref, vectors_ref, router_ref,
    act_hbm, merged_hbm, qkv_hbm, weight_hbm, out_hbm, low_hbm, high_hbm,
    output_ref, tokens_out, small_out, qkv_out, out_out,
    act_t, merged_t, qkv, weight, out_w, low_buf, high_buf, attn, grad_merged, grad_qkv,
    part_q, got_q, far_q, pair_q, lines_q, done_q,
    part_o, got_o, far_o, pair_o, lines_o, done_o,
    small, small_part, small_got, small_mid, small_far, small_sum, small_all,
    load_sem, prob_sem, send_q, recv_q, lsend_q, lrecv_q, send_o, recv_o, lsend_o, lrecv_o,
    small_send, small_recv, all_send, all_recv, out_sem,
):
    (owners,) = dims
    place = Place(owners)
    loads = [
        pltpu.make_async_copy(src, dst, load_sem.at[i])
        for i, (src, dst) in enumerate(
            [(merged_hbm, merged_t), (out_hbm, out_w), (qkv_hbm, qkv), (act_hbm, act_t),
             (weight_hbm, weight)]
        )
    ]

    def load_probs(i):
        slot = lax.rem(i, 2)
        return (
            pltpu.make_async_copy(
                low_hbm.at[pl.ds(2 * i, 2)], low_buf.at[slot], prob_sem.at[0, slot]
            ),
            pltpu.make_async_copy(
                high_hbm.at[pl.ds(2 * i, 2)], high_buf.at[slot], prob_sem.at[1, slot]
            ),
        )

    for load in loads:
        load.start()
    for load in load_probs(0):
        load.start()
    greet(
        [(place.ahead(k), place.w) for k in range(1, owners)]
        + [(place.e, place.sib), (place.e, place.far)]
    )
    reduce_o = Reduce(
        place, part_o, got_o, far_o, pair_o, lines_o, done_o, (send_o, recv_o, lsend_o, lrecv_o)
    )
    reduce_q = Reduce(
        place, part_q, got_q, far_q, pair_q, lines_q, done_q, (send_q, recv_q, lsend_q, lrecv_q)
    )
    smalls = Small(
        place, small, small_part, small_got, small_mid, small_far, small_sum, small_all, small_out,
        (small_send, small_recv, all_send, all_recv),
    )
    rows, width = tokens_ref.shape
    shard = width // 4
    band = min(128, rows)
    lead = small.shape[0]

    def vector(which):
        parts = [vectors_ref[i, which : which + 1, :] for i in range(4)]
        return jnp.concatenate(parts, axis=1).astype(jnp.float32)

    gain_one, gain_two = vector(0), vector(2)
    small[0:4, :] = jnp.zeros((4, width), jnp.float32)
    small[4:lead, :] = router_ref[0 : lead - 4, :]

    def post(i):
        part = span(i * band, band)
        grad = dot_nn(back_ref[part, :], home_grad_ref[...])
        scaled, inverse = norm_stats(hidden_ref[part, :])
        value = cot_ref[part, :].astype(jnp.float32) + norm_back_rows(
            grad, scaled, inverse, gain_two
        )
        tokens_out[part, :] = value
        attn[part, :] = value.astype(jnp.bfloat16)
        small[2:3, :] += jnp.sum(grad * scaled, axis=0, keepdims=True)
        small[3:4, :] += jnp.sum(grad, axis=0, keepdims=True)

    every(0, rows // band, post)
    loads[0].wait()

    def weight_grad(part, n, left, right):
        def one(owner):
            value = dot_nn(left[span(owner * shard, shard), :], right)
            part[n, lax.div(owner, 2), lax.rem(owner, 2)] = value.astype(jnp.bfloat16)

        every(0, 4, one)

    tile_o = part_o.shape[-1]
    out_chunks = part_o.shape[0]
    for n in range(out_chunks):
        weight_grad(part_o, n, merged_t, attn[:, n * tile_o : (n + 1) * tile_o])
        reduce_o.swap(n)
    loads[1].wait()

    def merged_band(i):
        part = span(i * band, band)
        grad_merged[part, :] = dot_nt(attn[part, :], out_w[...]).astype(jnp.bfloat16)

    every(0, rows // band, merged_band)
    for load in loads[2:4]:
        load.wait()
    pairs = part_q.shape[0]

    def attend_pair(i):
        slot = lax.rem(i, 2)
        for load in load_probs(i):
            load.wait()

        @pl.when(i + 1 < pairs)
        def _():
            for load in load_probs(i + 1):
                load.start()

        cols = span(i * LANES, LANES)
        query, key, value = (
            qkv[:, span(part * width + i * LANES, LANES)] for part in range(3)
        )
        grad = grad_merged[:, cols]
        results = []
        for head in range(2):
            part = slice(head * HEAD_DIM, (head + 1) * HEAD_DIM)
            results.append(
                attend_back_head(
                    query[:, part], key[:, part], value[:, part],
                    low_buf[slot, head], high_buf[slot, head], grad[:, part],
                )
            )
        for which in range(3):
            grad_qkv[:, span(which * width + i * LANES, LANES)] = jnp.concatenate(
                [results[0][which], results[1][which]], axis=1
            )
        right = jnp.concatenate(
            [grad_qkv[:, span(which * width + i * LANES, LANES)] for which in range(3)], axis=1
        )
        weight_grad(part_q, i, act_t, right)
        reduce_q.swap(i)

    def input_band(i):
        part = span(i * band, band)
        grad = dot_nt(grad_qkv[part, :], weight[...])
        scaled, inverse = norm_stats(tokens_ref[part, :].astype(jnp.float32))
        tokens_out[part, :] += norm_back_rows(grad, scaled, inverse, gain_one)
        small[0:1, :] += jnp.sum(grad * scaled, axis=0, keepdims=True)
        small[1:2, :] += jnp.sum(grad, axis=0, keepdims=True)

    def output_band(i):
        part = span(i * band, band)
        value = hidden_ref[part, :] + dot_nn(back_ref[part, :], home_out_ref[...])
        output_ref[part, :] = value.astype(jnp.bfloat16)

    def store_q(i):
        return [
            pltpu.make_async_copy(
                done_q.at[i, :, pl.ds(which * LANES, LANES)],
                qkv_out.at[:, span(which * width + i * LANES, LANES)],
                out_sem.at[which, i],
            )
            for which in range(3)
        ]

    def store_o(n):
        return pltpu.make_async_copy(
            done_o.at[n], out_out.at[:, span(n * tile_o, tile_o)], out_sem.at[3, n]
        )

    stages_o, stages_q = reduce_o.stages(), reduce_q.stages()
    depth = len(stages_q)

    def slot_step(slot):
        for s in range(depth - 1, -1, -1):
            n = slot - 1 - s

            @pl.when((n >= 0) & (n < pairs))
            def _(s=s, n=n):
                stages_q[s](n)
                if s == depth - 1:
                    for copy in store_q(n):
                        copy.start()

            @pl.when(slot == s)
            def _(s=s):
                for n in range(out_chunks):
                    stages_o[s](n)
                    if s == depth - 1:
                        store_o(n).start()

        @pl.when(slot < pairs)
        def _():
            attend_pair(slot)

        @pl.when(slot == pairs)
        def _():
            loads[4].wait()
            every(0, rows // band // 2, input_band)

        @pl.when(slot == pairs + 1)
        def _():
            every(rows // band // 2, rows // band, input_band)

        @pl.when(slot == pairs + 2)
        def _():
            smalls.swap()
            every(0, rows // band, output_band)

        @pl.when(slot == pairs + 3)
        def _():
            smalls.cross()

        @pl.when(slot == pairs + 4)
        def _():
            smalls.spread()

        @pl.when(slot == pairs + 5)
        def _():
            smalls.finish()

    every(0, pairs + depth, slot_step)

    def stored(i):
        for copy in store_q(i):
            copy.wait()

    every(0, pairs, stored)
    for n in range(out_chunks):
        store_o(n).wait()
    reduce_o.drain()
    reduce_q.drain()
    smalls.drain()


def run_back(
    owners, lead, home_grad, home_out, back, hidden, cotangent, tokens, vectors, router_grad,
    act_t, merged_t, qkv, weight, w_out, low, high,
):
    rows, width = tokens.shape
    shard = width // 4
    pairs = width // LANES
    tile_o = min(512, width)
    out_chunks = width // tile_o
    count = owners // 2
    half = shard // 2
    mid = rows // 2
    any_spec = pl.BlockSpec(memory_space=pl.ANY)
    vmem_spec = pl.BlockSpec(memory_space=pltpu.VMEM)
    bf16, f32 = jnp.bfloat16, jnp.float32
    dma = pltpu.SemaphoreType.DMA

    def vm(*shape):
        return pltpu.VMEM(shape, bf16)

    def fm(*shape):
        return pltpu.VMEM(shape, f32)

    def reduce_buffers(chunks, tile):
        return [
            vm(chunks, 2, 2, shard, tile),
            vm(chunks, 2, shard, tile),
            vm(chunks, shard, tile),
            vm(chunks, half, tile),
            vm(chunks, count, half // count, tile),
            vm(chunks, shard, tile),
        ]

    def reduce_sems(chunks):
        return [dma((4, chunks)), dma((4, chunks)), dma((2, chunks, count)), dma((2, chunks, count))]

    return pl.pallas_call(
        functools.partial(back_kernel, (owners,)),
        out_shape=(
            jax.ShapeDtypeStruct((rows, width), bf16),
            jax.ShapeDtypeStruct((rows, width), f32),
            jax.ShapeDtypeStruct((lead, shard), f32),
            jax.ShapeDtypeStruct((shard, 3 * width), bf16),
            jax.ShapeDtypeStruct((shard, width), bf16),
        ),
        in_specs=[vmem_spec] * 8 + [any_spec] * 7,
        out_specs=(vmem_spec,) * 3 + (any_spec,) * 2,
        scratch_shapes=[
            vm(width, rows),
            vm(width, rows),
            vm(rows, 3 * width),
            vm(width, 3 * width),
            vm(width, width),
            vm(2, 2, mid, mid),
            vm(2, 2, mid, rows),
            vm(rows, width),
            vm(rows, width),
            vm(rows, 3 * width),
        ]
        + reduce_buffers(pairs, 3 * LANES)
        + reduce_buffers(out_chunks, tile_o)
        + [
            fm(lead, width),
            fm(2, 2, lead, shard),
            fm(2, lead, shard),
            fm(lead, shard),
            fm(lead, shard),
            fm(lead, shard),
            fm(owners, lead, shard),
            dma((5,)),
            dma((2, 2)),
        ]
        + reduce_sems(pairs)
        + reduce_sems(out_chunks)
        + [dma((2,)), dma((2,)), dma((owners,)), dma((owners,)), dma((4, pairs))],
        compiler_params=pltpu.CompilerParams(
            collective_id=2, has_side_effects=True, vmem_limit_bytes=VMEM_LIMIT
        ),
        name="back",
    )(
        home_grad, home_out, back, hidden, cotangent, tokens, vectors, router_grad,
        act_t, merged_t, qkv, weight, w_out, low, high,
    )


def on_device_plain(
    tokens,
    norm1_gain,
    norm1_shift,
    w_qkv,
    w_out,
    norm2_gain,
    norm2_shift,
    w_router,
    w_up,
    w_down,
    routes,
    priority,
    prefix,
    cotangent,
):
    row_count, model_width = tokens.shape
    expert_count = w_router.shape[1]
    capacity = row_count // expert_count
    owners = lax.axis_size("expert")
    local_experts = w_up.shape[0]
    slot_count = expert_count * capacity
    prefix_len = prefix[0]
    small = jnp.concatenate(
        [
            norm1_gain[None],
            norm1_shift[None],
            norm2_gain[None],
            norm2_shift[None],
            w_router.T,
        ],
        axis=0,
    )
    qkv_full = lax.all_gather(w_qkv, "wshard", axis=0, tiled=True)
    small_full = lax.all_gather(small, "wshard", axis=1, tiled=True)
    out_full = lax.all_gather(w_out, "wshard", axis=0, tiled=True)
    gain_one, shift_one, gain_two, shift_two = (small_full[i] for i in range(4))
    router_full = small_full[4:].T
    gain_one = gain_one.astype(jnp.float32)
    gain_two = gain_two.astype(jnp.float32)
    inputs = tokens.astype(jnp.float32)
    normed_one, scaled_one, inverse_one = normalize(inputs, gain_one, shift_one.astype(jnp.float32))
    act_one = normed_one.astype(jnp.bfloat16)
    qkv = jnp.dot(act_one, qkv_full, preferred_element_type=jnp.float32).astype(jnp.bfloat16)
    query_heads = qkv[:, :model_width]
    key_heads = qkv[:, model_width : 2 * model_width]
    value_heads = qkv[:, 2 * model_width :]
    merged, log_totals = attend_forward(query_heads, key_heads, value_heads, prefix_len)
    attn_out = jnp.dot(merged, out_full, preferred_element_type=jnp.float32)
    hidden = inputs + attn_out
    normed_two, scaled_two, inverse_two = normalize(hidden, gain_two, shift_two.astype(jnp.float32))
    act_two = normed_two.astype(jnp.bfloat16)
    logits = jnp.dot(act_two, router_full, preferred_element_type=jnp.float32)
    row_max = jnp.max(logits, axis=-1, keepdims=True)
    exponent = jnp.exp(logits - row_max)
    gate_prob = exponent / jnp.sum(exponent, axis=-1, keepdims=True)
    route_ids = routes[:, 0]
    chosen = route_ids[:, None] == jnp.arange(expert_count, dtype=jnp.int32)[None, :]
    gate_value = jnp.sum(jnp.where(chosen, gate_prob, 0.0), axis=1)
    slot_index, slot_source = assign_slots(route_ids, priority[0], expert_count, capacity)
    zero_row = jnp.zeros((1, model_width), jnp.bfloat16)
    padded = jnp.concatenate([act_two, zero_row], axis=0)
    send_rows = padded[slot_source].reshape(owners, local_experts * capacity, model_width)
    arrived = lax.all_to_all(send_rows, "expert", split_axis=0, concat_axis=0, tiled=True).reshape(
        owners, local_experts, capacity, model_width
    )
    group = lax.axis_size("wshard")
    local_rows = owners * capacity

    def by_expert(chunk):
        rows = jnp.transpose(chunk, (1, 0, 2, 3)).reshape(local_experts, local_rows, model_width)
        return lax.all_gather(rows, "wshard", axis=1, tiled=True)

    def home_rows(rows):
        own = lax.psum_scatter(rows.astype(jnp.bfloat16), "wshard", scatter_dimension=1, tiled=True)
        own = own.reshape(local_experts, owners, capacity, model_width)
        return jnp.transpose(own, (1, 0, 2, 3)).reshape(
            owners, local_experts * capacity, model_width
        )

    grad_output = cotangent.astype(jnp.float32)
    grad_combined = (gate_value[:, None] * grad_output).astype(jnp.bfloat16)
    grad_padded = jnp.concatenate([grad_combined, zero_row], axis=0)
    grad_send = grad_padded[slot_source].reshape(owners, local_experts * capacity, model_width)
    grad_arrived = lax.all_to_all(
        grad_send, "expert", split_axis=0, concat_axis=0, tiled=True
    ).reshape(owners, local_experts, capacity, model_width)
    rows_in = by_expert(arrived)
    grad_rows = by_expert(grad_arrived)
    pre_act = jnp.einsum("erd,edf->erf", rows_in, w_up, preferred_element_type=jnp.float32)
    activated, gelu_pull = jax.vjp(gelu_tanh, pre_act)
    act_hidden = activated.astype(jnp.bfloat16)
    produced = jnp.einsum(
        "erf,efd->erd", act_hidden, w_down, preferred_element_type=jnp.float32
    )
    expert_out = home_rows(produced)
    returned = lax.all_to_all(expert_out, "expert", split_axis=0, concat_axis=0, tiled=True)
    slots_back = jnp.concatenate([returned.reshape(slot_count, model_width), zero_row], axis=0)
    combined = slots_back[slot_index].astype(jnp.float32)
    output = (hidden + gate_value[:, None] * combined).astype(jnp.bfloat16)
    grad_gate = jnp.sum(grad_output * combined, axis=1)
    grad_down = jnp.einsum(
        "erf,erd->efd", act_hidden, grad_rows, preferred_element_type=jnp.float32
    )
    grad_hidden_units = jnp.einsum(
        "erd,efd->erf", grad_rows, w_down, preferred_element_type=jnp.float32
    )
    grad_pre = gelu_pull(grad_hidden_units)[0].astype(jnp.bfloat16)
    grad_up = jnp.einsum("erd,erf->edf", rows_in, grad_pre, preferred_element_type=jnp.float32)
    grad_expert_in = jnp.einsum(
        "erf,edf->erd", grad_pre, w_up, preferred_element_type=jnp.float32
    )
    grad_send_back = home_rows(grad_expert_in)
    grad_back = lax.all_to_all(grad_send_back, "expert", split_axis=0, concat_axis=0, tiled=True)
    grad_slots = jnp.concatenate([grad_back.reshape(slot_count, model_width), zero_row], axis=0)
    grad_act_two = grad_slots[slot_index].astype(jnp.float32)
    grad_logits = (
        gate_prob * (jnp.where(chosen, grad_gate[:, None], 0.0) - (gate_value * grad_gate)[:, None])
    ).astype(jnp.bfloat16)
    grad_router = contract_rows(act_two, grad_logits)
    grad_act_two = grad_act_two + times_transpose(grad_logits, router_full)
    grad_from_two, grad_gain_two, grad_shift_two = norm_back(
        grad_act_two, scaled_two, inverse_two, gain_two
    )
    grad_hidden = grad_output + grad_from_two
    grad_attn = grad_hidden.astype(jnp.bfloat16)
    grad_out_w = contract_rows(merged, grad_attn)
    grad_merged = times_transpose(grad_attn, out_full).astype(jnp.bfloat16)
    grad_qkv = attend_backward(
        query_heads, key_heads, value_heads, grad_merged, log_totals, prefix_len
    )
    grad_qkv_w = contract_rows(act_one, grad_qkv)
    grad_act_one = times_transpose(grad_qkv, qkv_full)
    grad_from_one, grad_gain_one, grad_shift_one = norm_back(
        grad_act_one, scaled_one, inverse_one, gain_one
    )
    grad_tokens = grad_hidden + grad_from_one
    small_grad = jnp.concatenate(
        [
            grad_gain_one[None],
            grad_shift_one[None],
            grad_gain_two[None],
            grad_shift_two[None],
            grad_router.T,
        ],
        axis=0,
    )
    out_share = lax.psum_scatter(
        grad_out_w.astype(jnp.bfloat16), "wshard", scatter_dimension=0, tiled=True
    )
    qkv_share = lax.psum_scatter(
        grad_qkv_w.astype(jnp.bfloat16), "wshard", scatter_dimension=0, tiled=True
    )
    small_share = lax.psum_scatter(small_grad, "wshard", scatter_dimension=1, tiled=True)
    out_total = lax.psum(out_share, "expert").astype(jnp.float32)
    qkv_total = lax.psum(qkv_share, "expert").astype(jnp.float32)
    small_total = lax.psum(small_share, "expert")
    totals = (
        small_total[0],
        small_total[1],
        qkv_total,
        out_total,
        small_total[2],
        small_total[3],
        small_total[4:].T,
    )
    return (
        output,
        grad_tokens,
        totals[0],
        totals[1],
        totals[2],
        totals[3],
        totals[4],
        totals[5],
        totals[6],
        grad_up,
        grad_down,
    )


def on_device(
    tokens,
    norm1_gain,
    norm1_shift,
    w_qkv,
    w_out,
    norm2_gain,
    norm2_shift,
    w_router,
    w_up,
    w_down,
    routes,
    priority,
    prefix,
    cotangent,
):
    row_count, model_width = tokens.shape
    expert_count = w_router.shape[1]
    capacity = row_count // expert_count
    owners = lax.axis_size("expert")
    experts = w_up.shape[0]
    small = jnp.concatenate(
        [norm1_gain[None], norm1_shift[None], norm2_gain[None], norm2_shift[None], w_router.T],
        axis=0,
    )
    lead = small.shape[0]
    small = jnp.pad(small, ((0, -lead % 16), (0, 0)))
    (
        qkv, act_t, merged_t, back, weight, out_full, low, high, grad_rows, hidden, send_rows,
        vectors,
    ) = run_front(
        owners, experts, capacity, prefix, routes, priority, tokens, cotangent, small, w_qkv, w_out
    )
    router = jnp.transpose(vectors[:, 4:lead], (0, 2, 1)).reshape(model_width, expert_count)
    router = jnp.pad(router, ((0, 0), (0, LANES - expert_count)))
    home_out, home_grad, grad_up, grad_down, grad_router = run_experts(
        owners, capacity, expert_count, send_rows, grad_rows, w_up, w_down, router
    )
    output, grad_tokens, small_total, qkv_total, out_total = run_back(
        owners, lead + -lead % 8, home_grad.reshape(-1, model_width),
        home_out.reshape(-1, model_width), back, hidden, cotangent, tokens, vectors, grad_router,
        act_t, merged_t, qkv, weight, out_full, low, high,
    )
    return (
        output,
        grad_tokens,
        small_total[0],
        small_total[1],
        qkv_total.astype(jnp.float32),
        out_total.astype(jnp.float32),
        small_total[2],
        small_total[3],
        small_total[4:lead].T,
        grad_up.astype(jnp.float32),
        grad_down.astype(jnp.float32),
    )


def solution(mesh):
    placed = (
        P(("expert", "wshard"), None),
        P("wshard"),
        P("wshard"),
        P("wshard", None),
        P("wshard", None),
        P("wshard"),
        P("wshard"),
        P("wshard", None),
        P("expert", None, "wshard"),
        P("expert", "wshard", None),
        P(("expert", "wshard"), None),
        P(("expert", "wshard"), None),
        P(("expert", "wshard")),
        P(("expert", "wshard"), None),
    )
    owners, group = mesh.shape["expert"], mesh.shape["wshard"]

    def body(*args):
        capacity = args[0].shape[0] // args[7].shape[1]
        fits = group == 4 and owners in (4, 8, 16) and capacity % 16 == 0
        return (on_device if fits else on_device_plain)(*args)

    return jax.shard_map(
        body,
        mesh=mesh,
        in_specs=placed,
        out_specs=(
            P(("expert", "wshard"), None),
            P(("expert", "wshard"), None),
            P("wshard"),
            P("wshard"),
            P("wshard", None),
            P("wshard", None),
            P("wshard"),
            P("wshard"),
            P("wshard", None),
            P("expert", None, "wshard"),
            P("expert", "wshard", None),
        ),
        check_vma=False,
    )
```

```python
import functools
import math

import jax
import jax.numpy as jnp
from jax import lax
from jax.experimental import pallas as pl
from jax.experimental.pallas import tpu as pltpu
from jax.sharding import PartitionSpec as P

HEADS = 16
HEAD_DIM = 64


epsilon = 1e-05
VMEM_LIMIT = 66_000_000
TILE = 512


def normalize(values, gain_vec, shift_vec):
    row_mean = jnp.mean(values, axis=-1, keepdims=True)
    centered = values - row_mean
    inverse = lax.rsqrt(jnp.mean(centered * centered, axis=-1, keepdims=True) + epsilon)
    scaled = centered * inverse
    return (scaled * gain_vec + shift_vec, scaled, inverse)


def norm_back(grad_rows, scaled, inverse, gain_vec):
    weighted = grad_rows * gain_vec
    mean_one = jnp.mean(weighted, axis=-1, keepdims=True)
    mean_two = jnp.mean(weighted * scaled, axis=-1, keepdims=True)
    grad_inputs = inverse * (weighted - mean_one - scaled * mean_two)
    return (grad_inputs, jnp.sum(grad_rows * scaled, axis=0), jnp.sum(grad_rows, axis=0))


def contract_rows(left, right):
    return lax.dot_general(
        left, right, (((0,), (0,)), ((), ())), preferred_element_type=jnp.float32
    )


def times_transpose(left, right):
    return lax.dot_general(
        left, right, (((1,), (1,)), ((), ())), preferred_element_type=jnp.float32
    )


def gelu_tanh(values):
    return jax.nn.gelu(values, approximate=True)


def assign_slots(route_ids, order_ids, expert_count, capacity):
    token_count = route_ids.shape[0]
    same_expert = route_ids[:, None] == route_ids[None, :]
    earlier = order_ids[None, :] < order_ids[:, None]
    rank_ids = jnp.sum((same_expert & earlier).astype(jnp.int32), axis=1)
    is_kept = rank_ids < capacity
    slot_index = jnp.where(is_kept, route_ids * capacity + rank_ids, expert_count * capacity)
    slot_ids = jnp.arange(expert_count * capacity, dtype=jnp.int32)
    match_table = slot_index[None, :] == slot_ids[:, None]
    token_ids = jnp.arange(token_count, dtype=jnp.int32)
    filled = jnp.any(match_table, axis=1)
    picked = jnp.sum(jnp.where(match_table, token_ids[None, :], 0), axis=1)
    slot_source = jnp.where(filled, picked, token_count)
    return (slot_index, slot_source)


def group_heads(values, groups):
    token_count = values.shape[0]
    return jnp.transpose(values.reshape(token_count, groups, -1, HEAD_DIM), (1, 0, 2, 3))


def block_scores(query_block, key_group, block_start, prefix_len):
    block_rows = query_block.shape[0]
    key_count = key_group.shape[0]
    scores = jnp.einsum(
        "qgd,kgd->gqk", query_block, key_group, preferred_element_type=jnp.float32
    ) * (1.0 / math.sqrt(HEAD_DIM))
    query_pos = block_start + jnp.arange(block_rows, dtype=jnp.int32)
    key_pos = jnp.arange(key_count, dtype=jnp.int32)
    allowed = (key_pos[None, :] <= query_pos[:, None]) | (key_pos[None, :] < prefix_len)
    return jnp.where(allowed[None], scores, -1e30)


def attend_forward(query_heads, key_heads, value_heads, prefix_len):
    token_count = query_heads.shape[0]
    group_size = min(4, HEADS)
    groups = HEADS // group_size
    block_rows = min(512, token_count)
    blocks = token_count // block_rows
    starts = jnp.arange(blocks, dtype=jnp.int32) * block_rows

    def one_group(group_item):
        query_group, key_group, value_group = group_item
        query_blocks = query_group.reshape(blocks, block_rows, group_size, HEAD_DIM)

        def one_block(block_item):
            query_block, block_start = block_item
            scores = block_scores(query_block, key_group, block_start, prefix_len)
            row_max = jnp.max(scores, axis=-1, keepdims=True)
            exponent = jnp.exp(scores - row_max)
            row_total = jnp.sum(exponent, axis=-1, keepdims=True)
            attn_probs = (exponent / row_total).astype(jnp.bfloat16)
            result = jnp.einsum(
                "gqk,kgd->qgd", attn_probs, value_group, preferred_element_type=jnp.float32
            )
            return (result, (row_max + jnp.log(row_total))[..., 0])

        return lax.map(one_block, (query_blocks, starts))

    attended, log_totals = lax.map(
        one_group,
        (
            group_heads(query_heads, groups),
            group_heads(key_heads, groups),
            group_heads(value_heads, groups),
        ),
    )
    merged = (
        jnp.transpose(attended, (1, 2, 0, 3, 4))
        .reshape(token_count, HEADS * HEAD_DIM)
        .astype(jnp.bfloat16)
    )
    return (merged, log_totals)


def attend_backward(query_heads, key_heads, value_heads, grad_merged, log_totals, prefix_len):
    token_count = query_heads.shape[0]
    group_size = min(4, HEADS)
    groups = HEADS // group_size
    block_rows = min(512, token_count)
    blocks = token_count // block_rows
    starts = jnp.arange(blocks, dtype=jnp.int32) * block_rows
    score_scale = 1.0 / math.sqrt(HEAD_DIM)

    def one_group(group_item):
        query_group, key_group, value_group, grad_group, total_group = group_item
        query_blocks = query_group.reshape(blocks, block_rows, group_size, HEAD_DIM)
        grad_blocks = grad_group.reshape(blocks, block_rows, group_size, HEAD_DIM)

        def one_block(carry, block_item):
            grad_keys, grad_vals = carry
            query_block, grad_block, total_block, block_start = block_item
            scores = block_scores(query_block, key_group, block_start, prefix_len)
            attn_probs = jnp.exp(scores - total_block[..., None])
            grad_probs = jnp.einsum(
                "qgd,kgd->gqk", grad_block, value_group, preferred_element_type=jnp.float32
            )
            row_delta = jnp.sum(attn_probs * grad_probs, axis=-1, keepdims=True)
            grad_scores = (attn_probs * (grad_probs - row_delta)).astype(jnp.bfloat16)
            grad_vals = grad_vals + jnp.einsum(
                "gqk,qgd->kgd",
                attn_probs.astype(jnp.bfloat16),
                grad_block,
                preferred_element_type=jnp.float32,
            )
            grad_keys = (
                grad_keys
                + jnp.einsum(
                    "gqk,qgd->kgd", grad_scores, query_block, preferred_element_type=jnp.float32
                )
                * score_scale
            )
            grad_query = (
                jnp.einsum(
                    "gqk,kgd->qgd", grad_scores, key_group, preferred_element_type=jnp.float32
                )
                * score_scale
            )
            return ((grad_keys, grad_vals), grad_query)

        zero_keys = jnp.zeros(key_group.shape, jnp.float32)
        carried, grad_queries = lax.scan(
            one_block, (zero_keys, zero_keys), (query_blocks, grad_blocks, total_group, starts)
        )
        return (grad_queries, carried[0], carried[1])

    grad_queries, grad_keys, grad_vals = lax.map(
        one_group,
        (
            group_heads(query_heads, groups),
            group_heads(key_heads, groups),
            group_heads(value_heads, groups),
            group_heads(grad_merged, groups),
            log_totals,
        ),
    )
    query_part = jnp.transpose(grad_queries, (1, 2, 0, 3, 4)).reshape(token_count, HEADS * HEAD_DIM)
    key_part = jnp.transpose(grad_keys, (1, 0, 2, 3)).reshape(token_count, HEADS * HEAD_DIM)
    value_part = jnp.transpose(grad_vals, (1, 0, 2, 3)).reshape(token_count, HEADS * HEAD_DIM)
    return jnp.concatenate([query_part, key_part, value_part], axis=1).astype(jnp.bfloat16)


MESH = pl.DeviceIdType.MESH
LANES = 128


def dot_nn(left, right):
    return lax.dot_general(
        left, right, (((1,), (0,)), ((), ())), preferred_element_type=jnp.float32
    )


def dot_nt(left, right):
    return lax.dot_general(
        left, right, (((1,), (1,)), ((), ())), preferred_element_type=jnp.float32
    )


def dot_tn(left, right):
    return lax.dot_general(
        left, right, (((0,), (0,)), ((), ())), preferred_element_type=jnp.float32
    )


def span(start, size):
    return pl.ds(pl.multiple_of(start, size), size)


def every(start, stop, step):
    def body(i, carry):
        step(i)
        return carry

    lax.fori_loop(start, stop, body, 0)


class Place:
    def __init__(self, owners):
        self.owners = owners
        self.e = lax.axis_index("expert")
        self.w = lax.axis_index("wshard")
        self.c = lax.rem(self.w, 2)
        self.x = lax.div(self.w, 2)
        self.sib = self.w + 1 - 2 * self.c
        self.far = lax.rem(self.w + 2, 4)
        self.diag = 3 - self.w
        self.pair = self.e + 1 - 2 * lax.rem(self.e, 2)

    def ahead(self, k):
        return lax.rem(self.e + k, self.owners)

    def peer(self, n):
        other = lax.div(n, 2) + lax.rem(n, 2) * (self.owners // 2)
        result, bit = 0, 1
        while bit < self.owners:
            result = result + bit * lax.rem(lax.div(self.e, bit) + lax.div(other, bit), 2)
            bit *= 2
        return result


def remote(src, dst, send, recv, device):
    return pltpu.make_async_remote_copy(
        src_ref=src,
        dst_ref=dst,
        send_sem=send,
        recv_sem=recv,
        device_id=device,
        device_id_type=MESH,
    )


def greet(peers):
    barrier = pltpu.get_barrier_semaphore()
    for peer in peers:
        pl.semaphore_signal(barrier, inc=1, device_id=peer, device_id_type=MESH)
    pl.semaphore_wait(barrier, len(peers))


def either(test, yes, no):
    pl.when(test)(yes)
    pl.when(jnp.logical_not(test))(no)


class Dispatch:
    def __init__(self, place, capacity, send_ref, rows_ref, sems):
        self.p, self.cap, self.src, self.rows = place, capacity, send_ref, rows_ref
        self.own_sem, self.send, self.recv = sems

    def slice(self, k, core, side):
        start = (((lax.div(k, 2) * 2 + core) * 2 + side) * 2 + lax.rem(k, 2)) * self.cap
        return self.rows.at[:, span(start, self.cap)]

    def own(self):
        return pltpu.make_async_copy(
            self.src.at[self.p.e], self.slice(0, self.p.c, self.p.x), self.own_sem
        )

    def direct(self, k):
        return remote(
            self.src.at[self.p.peer(k)],
            self.slice(k, self.p.c, self.p.x),
            self.send.at[0, k],
            self.recv.at[0, k],
            (self.p.peer(k), self.p.w),
        )

    def hop(self, k, side, which, peer):
        part = self.slice(k, self.p.c, side)
        return remote(
            part, part, self.send.at[which, k], self.recv.at[which, k], (self.p.e, peer)
        )

    def to_sib(self, k):
        return self.hop(k, self.p.x, 1, self.p.sib)

    def to_far(self, k):
        return self.hop(k, self.p.x, 2, self.p.far)

    def relayed(self, k):
        return self.hop(k, 1 - self.p.x, 3, self.p.sib)

    def start(self):
        self.own().start()
        every(1, self.p.owners, lambda k: self.direct(k).start())

    def forward(self, k):
        k = jnp.int32(k)

        @pl.when(k == 0)
        def _():
            self.own().wait()

        @pl.when(k > 0)
        def _():
            self.direct(k).wait_recv()

        self.to_far(k).start()
        self.to_sib(k).start()

    def relay(self, k):
        self.to_far(k).wait_recv()
        self.relayed(k).start()

    def ready(self, k):
        self.to_sib(k).wait_recv()
        self.relayed(k).wait_recv()

    def drain(self):
        every(1, self.p.owners, lambda k: self.direct(k).wait_send())

        def rest(k):
            self.to_sib(k).wait_send()
            self.to_far(k).wait_send()
            self.relayed(k).wait_send()

        every(0, self.p.owners, rest)


class Return:
    def __init__(self, place, capacity, experts, part, got, mid, far, done, home, sems):
        self.p, self.cap, self.experts = place, capacity, experts
        self.part, self.got, self.mid, self.far, self.done, self.home = (
            part, got, mid, far, done, home,
        )
        self.own_sem, self.send, self.recv, self.home_send, self.home_recv = sems

    def swapped(self, j):
        size = 4 * self.cap
        return remote(
            self.part.at[:, span((j * 2 + 1 - self.p.c) * size, size)],
            self.got.at[:, span(j * size, size)],
            self.send.at[0, j],
            self.recv.at[0, j],
            (self.p.e, self.p.sib),
        )

    def crossed(self, j):
        part = span(j * 2 * self.cap, 2 * self.cap)
        return remote(
            self.mid.at[:, part],
            self.far.at[:, part],
            self.send.at[1, j],
            self.recv.at[1, j],
            (self.p.e, self.p.far),
        )

    def own(self):
        return pltpu.make_async_copy(self.done.at[0], self.home.at[self.p.e], self.own_sem)

    def homed(self, n):
        return remote(
            self.done.at[n],
            self.home.at[self.p.e],
            self.home_send.at[n],
            self.home_recv.at[n],
            (self.p.peer(n), self.p.w),
        )

    def pair_sum(self, expert, j, side):
        size = 2 * self.cap
        mine = self.part[expert, span(((j * 2 + self.p.c) * 2 + side) * size, size), :]
        theirs = self.got[expert, span((j * 2 + side) * size, size), :]
        return mine.astype(jnp.float32) + theirs.astype(jnp.float32)

    def swap(self, j):
        self.swapped(j).start()

    def split(self, j):
        self.swapped(j).wait_recv()
        here = span(j * 2 * self.cap, 2 * self.cap)
        for expert in range(self.experts):
            self.mid[expert, here, :] = self.pair_sum(expert, j, 1 - self.p.x).astype(jnp.bfloat16)
            self.far[expert, here, :] = self.pair_sum(expert, j, self.p.x).astype(jnp.bfloat16)

    def cross(self, j):
        self.swapped(j).wait_recv()
        size = 2 * self.cap
        for expert in range(self.experts):
            self.mid[expert, span(j * size, size), :] = self.pair_sum(
                expert, j, 1 - self.p.x
            ).astype(jnp.bfloat16)
        self.crossed(j).start()

    def this_side(self, expert, j):
        return self.pair_sum(expert, j, self.p.x)

    def finish(self, j):
        self.crossed(j).wait_recv()
        size = 2 * self.cap
        for expert in range(self.experts):
            total = self.this_side(expert, j) + self.far[
                expert, span(j * size, size), :
            ].astype(jnp.float32)
            total = total.astype(jnp.bfloat16)
            self.done[2 * j, expert] = total[: self.cap]
            self.done[2 * j + 1, expert] = total[self.cap :]
        j = jnp.int32(j)
        self.homed(2 * j + 1).start()
        either(j == 0, lambda: self.own().start(), lambda: self.homed(2 * j).start())

    def drain_swaps(self, chunks):
        every(0, chunks, lambda j: self.swapped(j).wait_send())

    def drain(self, chunks):
        every(0, chunks, lambda j: self.crossed(j).wait_send())
        every(1, self.p.owners, lambda n: self.homed(n).wait_send())

    def arrived(self):
        self.own().wait()
        every(1, self.p.owners, lambda n: self.homed(n).wait_recv())


class LateReturn(Return):
    def crossed(self, j):
        part = span(j * 2 * self.cap, 2 * self.cap)
        return remote(
            self.mid.at[:, part],
            self.far.at[:, part],
            self.send.at[j],
            self.recv.at[j],
            (self.p.e, self.p.far),
        )

    def this_side(self, expert, j):
        size = 2 * self.cap
        return self.part[expert, span(j * size, size), :].astype(jnp.float32)


def gelu_pair(v):
    root = math.sqrt(2.0 / math.pi)
    square = v * v
    t = jnp.tanh(v * (root + (root * 0.044715) * square))
    half = 0.5 + 0.5 * t
    slope = half + (half * (1.0 - t)) * (v * (root + (3.0 * root * 0.044715) * square))
    return v * half, slope


def expert_kernel(
    dims,
    send_ref, grads_hbm, up_hbm, down_hbm, router_ref,
    far_sums, near_sums, home_grad, up_out, down_out, router_grad,
    rows, grads, scaled, hidden, pre, up, down, grad_up, grad_down,
    part_out, part_grad, got_out, got_grad, mid_out, mid_grad,
    keep_out, far_grad, done_grad,
    load_sem, own_sem, disp_send, disp_recv, red_send, red_recv, home_send, home_recv,
):
    owners, experts, capacity, width, units, expert_count = dims
    place = Place(owners)
    loads = [
        pltpu.make_async_copy(src, dst, load_sem.at[i])
        for i, (src, dst) in enumerate(
            [(up_hbm, up), (grads_hbm, grads), (down_hbm, down)]
        )
    ]
    for load in loads:
        load.start()
    greet(
        [(place.ahead(k), place.w) for k in range(1, owners)]
        + [(place.e, place.sib), (place.e, place.far)]
    )
    dispatch = Dispatch(
        place, capacity, send_ref, rows, (own_sem.at[0], disp_send, disp_recv)
    )
    ret_grad = Return(
        place, capacity, experts, part_grad, got_grad, mid_grad, far_grad, done_grad, home_grad,
        (own_sem.at[1], red_send.at[0], red_recv.at[0], home_send, home_recv),
    )
    ret_out = Return(
        place, capacity, experts, part_out, got_out, mid_out, keep_out, None, None,
        (None, red_send.at[1], red_recv.at[1], None, None),
    )
    dispatch.start()
    router_grad[...] = jnp.zeros_like(router_grad)
    tile = min(TILE, units)
    wide = min(TILE, width)
    chunks = owners // 2
    size = 8 * capacity
    lane = lax.broadcasted_iota(jnp.int32, (size, LANES), 1)

    def compute(j, expert):
        here = span(j * size, size)
        logits = dot_nt(rows[expert, here, :], router_ref[...])
        logits = jnp.where(lane < expert_count, logits, -1e30)
        exponent = jnp.exp(logits - jnp.max(logits, axis=1, keepdims=True))
        prob = exponent * (1.0 / jnp.sum(exponent, axis=1, keepdims=True))
        mine = lane == place.e * experts + expert
        gate = jnp.sum(jnp.where(mine, prob, 0.0), axis=1, keepdims=True)
        scaled[expert, here, :] = (
            gate * grads[expert, here, :].astype(jnp.float32)
        ).astype(jnp.bfloat16)

        def one_tile(n):
            cols = span(n * tile, tile)
            value, slope = gelu_pair(dot_nn(rows[expert, here, :], up[expert, :, cols]))
            hidden[expert, here, cols] = value.astype(jnp.bfloat16)
            back = dot_nt(scaled[expert, here, :], down[expert, cols, :])
            pre[expert, here, cols] = (back * slope).astype(jnp.bfloat16)

        every(0, units // tile, one_tile)

        def one_out(n, total):
            cols = span(n * wide, wide)
            value = dot_nn(hidden[expert, here, :], down[expert, :, cols])
            part_out[expert, here, cols] = (gate * value).astype(jnp.bfloat16)
            weighted = value * grads[expert, here, cols].astype(jnp.float32)
            for start in range(0, wide, LANES):
                total = total + weighted[:, start : start + LANES]
            return total

        total = lax.fori_loop(
            0, width // wide, one_out, jnp.zeros((size, LANES), jnp.float32)
        )
        grad_gate = jnp.sum(total, axis=1, keepdims=True)
        grad_logits = (
            prob * ((jnp.where(mine, 1.0, 0.0) - gate) * grad_gate)
        ).astype(jnp.bfloat16)

        def one_in(n):
            cols = span(n * wide, wide)
            value = dot_nt(pre[expert, here, :], up[expert, cols, :]) + dot_nn(
                grad_logits, router_ref[:, cols]
            )
            part_grad[expert, here, cols] = value.astype(jnp.bfloat16)
            router_grad[:, cols] += dot_tn(grad_logits, rows[expert, here, cols])

        every(0, width // wide, one_in)

    block = min(256, width)

    def weight_grads(expert, first, last):
        def one(n):
            part = span(n * block, block)
            grad_down[expert, part, :] = dot_tn(
                hidden[expert, :, part], scaled[expert]
            ).astype(jnp.bfloat16)
            grad_up[expert, part, :] = dot_tn(rows[expert, :, part], pre[expert]).astype(
                jnp.bfloat16
            )

        every(first * width // block // 4, last * width // block // 4, one)

    def keep(expert):
        return [
            pltpu.make_async_copy(src.at[expert], dst.at[expert], load_sem.at[2 * expert + i])
            for i, (src, dst) in enumerate(((grad_up, up_out), (grad_down, down_out)))
        ]

    def arrive(j):
        for n in (2 * j, 2 * j + 1):
            dispatch.relay(n)
        for n in (2 * j, 2 * j + 1):
            dispatch.ready(n)

    def forward(j):
        dispatch.forward(2 * j)
        dispatch.forward(2 * j + 1)

    forward(0)
    forward(1)
    for load in loads:
        load.wait()

    def step(j):
        arrive(j)
        compute(j, 0)
        pl.when(j + 2 < chunks)(lambda: forward(j + 2))

        @pl.when(j >= 1)
        def _():
            ret_grad.cross(j - 1)
            ret_out.split(j - 1)

        pl.when(j >= 2)(lambda: ret_grad.finish(j - 2))

        for expert in range(1, experts):
            compute(j, expert)
        ret_grad.swap(j)
        ret_out.swap(j)

    every(0, chunks, step)
    weight_grads(0, 0, 1)
    ret_grad.cross(chunks - 1)
    ret_out.split(chunks - 1)
    sums = [
        pltpu.make_async_copy(src, dst, load_sem.at[4 + i])
        for i, (src, dst) in enumerate(((mid_out, far_sums), (keep_out, near_sums)))
    ]
    for store in sums:
        store.start()
    ret_grad.finish(chunks - 2)
    weight_grads(0, 1, 3)
    ret_grad.finish(chunks - 1)
    weight_grads(0, 3, 4)
    for store in keep(0):
        store.start()
    for expert in range(1, experts):
        weight_grads(expert, 0, 4)
        for store in keep(expert):
            store.start()
    for expert in range(experts):
        for store in keep(expert):
            store.wait()
    for store in sums:
        store.wait()
    dispatch.drain()
    ret_grad.drain_swaps(chunks)
    ret_grad.drain(chunks)
    ret_grad.arrived()
    ret_out.drain_swaps(chunks)


def run_experts(owners, capacity, expert_count, send_rows, grads, w_up, w_down, router):
    experts, width, units = w_up.shape
    slots = owners * 4 * capacity
    chunks = owners // 2
    dims = (owners, experts, capacity, width, units, expert_count)
    any_spec = pl.BlockSpec(memory_space=pl.ANY)
    vmem_spec = pl.BlockSpec(memory_space=pltpu.VMEM)
    bf16 = jnp.bfloat16
    home = jax.ShapeDtypeStruct((owners, experts, capacity, width), bf16)
    dma = pltpu.SemaphoreType.DMA

    def vm(*shape):
        return pltpu.VMEM(shape, bf16)

    return pl.pallas_call(
        functools.partial(expert_kernel, dims),
        out_shape=(
            jax.ShapeDtypeStruct((experts, slots // 4, width), bf16),
            jax.ShapeDtypeStruct((experts, slots // 4, width), bf16),
            home,
            jax.ShapeDtypeStruct(w_up.shape, bf16),
            jax.ShapeDtypeStruct(w_down.shape, bf16),
            jax.ShapeDtypeStruct((LANES, width), jnp.float32),
        ),
        in_specs=[any_spec] * 4 + [vmem_spec],
        out_specs=(any_spec,) * 5 + (vmem_spec,),
        scratch_shapes=[
            vm(experts, slots, width),
            vm(experts, slots, width),
            vm(experts, slots, width),
            vm(experts, slots, units),
            vm(experts, slots, units),
            vm(experts, width, units),
            vm(experts, units, width),
            vm(experts, width, units),
            vm(experts, units, width),
            vm(experts, slots, width),
            vm(experts, slots, width),
            vm(experts, slots // 2, width),
            vm(experts, slots // 2, width),
            vm(experts, slots // 4, width),
            vm(experts, slots // 4, width),
            vm(experts, slots // 4, width),
            vm(experts, slots // 4, width),
            vm(owners, experts, capacity, width),
            dma((6,)),
            dma((2,)),
            dma((4, owners)),
            dma((4, owners)),
            dma((2, 2, chunks)),
            dma((2, 2, chunks)),
            dma((owners,)),
            dma((owners,)),
        ],
        compiler_params=pltpu.CompilerParams(
            collective_id=1, has_side_effects=True, vmem_limit_bytes=VMEM_LIMIT
        ),
        name="experts",
    )(send_rows, grads, w_up, w_down, router)


def masked_softmax(scores):
    exponent = jnp.exp(scores - jnp.max(scores, axis=1, keepdims=True))
    return exponent * (1.0 / jnp.sum(exponent, axis=1, keepdims=True))


def attend_head(query, key, value, prefix_len):
    half = query.shape[0] // 2
    query = query * (1.0 / math.sqrt(HEAD_DIM))
    row = lax.broadcasted_iota(jnp.int32, (half, half), 0)
    col = lax.broadcasted_iota(jnp.int32, (half, half), 1)
    low = dot_nt(query[:half], key[:half])
    low = jnp.where((col <= row) | (col < prefix_len), low, -1e30)
    low = masked_softmax(low).astype(jnp.bfloat16)
    high = dot_nt(query[half:], key)
    high = jnp.concatenate(
        [high[:, :half], jnp.where(col <= row, high[:, half:], -1e30)], axis=1
    )
    high = masked_softmax(high).astype(jnp.bfloat16)
    return low, high, dot_nn(low, value[:half]), dot_nn(high, value)


def score_grads(probs, grad_probs):
    probs = probs.astype(jnp.float32)
    weighted = probs * grad_probs
    total = jnp.sum(weighted, axis=1, keepdims=True)
    return (weighted - probs * total).astype(jnp.bfloat16)


def attend_back_head(query, key, value, low, high, grad):
    half = query.shape[0] // 2
    scale = 1.0 / math.sqrt(HEAD_DIM)
    query = query * scale
    grad_low = score_grads(low, dot_nt(grad[:half], value[:half]))
    grad_high = score_grads(high, dot_nt(grad[half:], value))
    grad_query = jnp.concatenate(
        [dot_nn(grad_low, key[:half]), dot_nn(grad_high, key)], axis=0
    )
    value_all = dot_tn(high, grad[half:])
    key_all = dot_tn(grad_high, query[half:])
    grad_value = jnp.concatenate(
        [value_all[:half] + dot_tn(low, grad[:half]), value_all[half:]], axis=0
    )
    grad_key = jnp.concatenate(
        [key_all[:half] + dot_tn(grad_low, query[:half]), key_all[half:]], axis=0
    )
    return (
        (grad_query * scale).astype(jnp.bfloat16),
        grad_key.astype(jnp.bfloat16),
        grad_value.astype(jnp.bfloat16),
    )


class Gather:
    def __init__(self, place, pieces, src, dst, sems):
        self.p, self.src, self.dst = place, src, dst
        self.send, self.recv, self.near_send, self.near_recv, self.own_sem = sems
        self.shard = src.shape[0]
        self.half = self.shard // 2
        self.step = self.half // pieces
        self.pieces = pieces
        self.first = lax.rem(place.e, 2) * self.half
        self.second = self.half - self.first

    def block(self, owner, start, size):
        return self.dst.at[pl.ds(pl.multiple_of(owner * self.shard + start, self.step), size)]

    def own(self):
        return pltpu.make_async_copy(self.src, self.block(self.p.w, 0, self.shard), self.own_sem)

    def near(self):
        return remote(
            self.src, self.block(self.p.w, 0, self.shard), self.near_send, self.near_recv,
            (self.p.e, self.p.sib),
        )

    def hop(self, n):
        return remote(
            self.src.at[span(self.first + n * self.step, self.step)],
            self.block(self.p.w, self.first + n * self.step, self.step),
            self.send.at[0, n], self.recv.at[0, n], (self.p.e, self.p.far),
        )

    def pass_from(self, start, n, which, device):
        part = self.block(self.p.far, start + n * self.step, self.step)
        return remote(part, part, self.send.at[which, n], self.recv.at[which, n], device)

    def pairs(self, n):
        return self.pass_from(self.first, n, 1, (self.p.pair, self.p.w))

    def relay(self, n):
        return self.pass_from(self.first, n, 2, (self.p.e, self.p.sib))

    def pair_relay(self, n):
        return self.pass_from(self.second, n, 3, (self.p.e, self.p.sib))

    def start(self):
        every(0, self.pieces, lambda n: self.hop(n).start())
        self.near().start()

    def pass_on(self, n):
        self.hop(n).wait_recv()
        self.pairs(n).start()
        self.relay(n).start()

    def pass_pair(self, n):
        self.pairs(n).wait_recv()
        self.pair_relay(n).start()

    def near_ready(self):
        self.own().wait()
        self.near().wait_recv()

    def far_ready(self):
        def one(n):
            self.relay(n).wait_recv()
            self.pair_relay(n).wait_recv()

        every(0, self.pieces, one)

    def drain(self):
        self.near().wait_send()

        def one(n):
            for copy in (self.hop(n), self.pairs(n), self.relay(n), self.pair_relay(n)):
                copy.wait_send()

        every(0, self.pieces, one)


def slot_tables(routes_ref, priority_ref, capacity, pick_ref, back_ref):
    count = routes_ref.shape[1]
    row = lax.broadcasted_iota(jnp.int32, (count, count), 0).astype(jnp.float32)
    col = lax.broadcasted_iota(jnp.int32, (count, count), 1).astype(jnp.float32)
    eye = row == col
    route_row = routes_ref[...].astype(jnp.float32)
    order_row = priority_ref[...].astype(jnp.float32)
    route_col = jnp.sum(jnp.where(eye, route_row, 0.0), axis=1, keepdims=True)
    order_col = jnp.sum(jnp.where(eye, order_row, 0.0), axis=1, keepdims=True)
    same = route_col == route_row
    rank_row = jnp.sum(
        jnp.where(same & (order_col < order_row), 1.0, 0.0), axis=0, keepdims=True
    )
    rank_col = jnp.sum(
        jnp.where(same & (order_row < order_col), 1.0, 0.0), axis=1, keepdims=True
    )
    slots = float(count)
    slot_row = jnp.where(rank_row < capacity, route_row * capacity + rank_row, slots)
    slot_col = jnp.where(rank_col < capacity, route_col * capacity + rank_col, slots)
    pick_ref[...] = jnp.where(slot_row == row, 1.0, 0.0).astype(jnp.bfloat16)
    back_ref[...] = jnp.where(slot_col == col, 1.0, 0.0).astype(jnp.bfloat16)


def norm_stats(value):
    centered = value - jnp.mean(value, axis=1, keepdims=True)
    inverse = lax.rsqrt(jnp.mean(centered * centered, axis=1, keepdims=True) + epsilon)
    return centered * inverse, inverse


def front_kernel(
    dims,
    prefix_ref, routes_ref, priority_ref, tokens_ref, cot_ref, small_hbm, router_hbm, qkv_hbm, out_hbm,
    qkv_out, act_out, merged_out, back_out, weight_out, out_full, low_out, high_out, grads_rows,
    hidden_ref, send_ref, small_out, router_out,
    small, weight, out_w, total, qkv, act, merged, act_two, turned, pick, back, grads_send, low_buf, high_buf,
    own_sem, disp_send, disp_recv, small_send, small_recv, near_send, near_recv,
    gat_send, gat_recv, store_sem, prob_sem,
):
    owners, capacity, pieces = dims
    place = Place(owners)
    rows, width = tokens_ref.shape
    shard = qkv_hbm.shape[0]
    gathers = [
        Gather(
            place, pieces, src, dst,
            (gat_send.at[i], gat_recv.at[i], near_send.at[i], near_recv.at[i], own_sem.at[1 + i]),
        )
        for i, (src, dst) in enumerate(((qkv_hbm, weight), (out_hbm, out_w)))
    ]
    for gather in gathers:
        gather.own().start()
    vectors, gates = small_hbm.shape[0], router_hbm.shape[0]
    small_parts = [
        (small_hbm, small.at[place.w, pl.ds(0, vectors)]),
        (router_hbm, small.at[place.w, pl.ds(vectors, gates)]),
    ]
    own_smalls = [
        pltpu.make_async_copy(src, dst, own_sem.at[3 + i])
        for i, (src, dst) in enumerate(small_parts)
    ]
    for copy in own_smalls:
        copy.start()
    greet(
        [(place.ahead(k), place.w) for k in range(1, owners)]
        + [(place.e, place.sib), (place.e, place.far), (place.e, place.diag)]
    )
    smalls = [
        remote(src, dst, small_send.at[n, i], small_recv.at[n, i], (place.e, peer))
        for i, peer in enumerate((place.sib, place.far, place.diag))
        for n, (src, dst) in enumerate(small_parts)
    ]
    for copy in smalls:
        copy.start()
    for gather in gathers:
        gather.start()
    slot_tables(routes_ref, priority_ref, capacity, pick, back)
    tile = min(256, width)
    shape = grads_send.shape[:3]

    def to_slots(values_ref, slots_ref):
        def one(n):
            cols = span(n * tile, tile)
            value = dot_nn(pick[...], values_ref[:, cols]).astype(jnp.bfloat16)
            slots_ref[:, :, :, cols] = value.reshape(shape + (tile,))

        every(0, width // tile, one)

    to_slots(cot_ref, grads_send)
    dispatch = Dispatch(
        place, capacity, grads_send, grads_rows, (own_sem.at[0], disp_send, disp_recv)
    )
    dispatch.start()
    for copy in own_smalls:
        copy.wait()
    for copy in smalls:
        copy.wait_recv()
    small_out[...] = small[:, :vectors, :]
    router_out[...] = jnp.zeros_like(router_out)
    router_out[:gates, :] = jnp.concatenate(
        [small[i, vectors:, :] for i in range(4)], axis=1
    )

    def vector(which):
        parts = [small[i, which : which + 1, :] for i in range(4)]
        return jnp.concatenate(parts, axis=1).astype(jnp.float32)

    band = min(64, rows)
    gain, shift = vector(0), vector(1)

    def norm_band(i):
        part = span(i * band, band)
        scaled, _ = norm_stats(tokens_ref[part, :].astype(jnp.float32))
        act[part, :] = (scaled * gain + shift).astype(jnp.bfloat16)

    columns = weight.shape[1]
    wide = min(512, columns)

    def multiply(owner, cols):
        depth = span(owner * shard, shard)
        return dot_nn(act[:, depth], weight[depth, cols])

    def first_tile(n):
        cols = span(n * wide, wide)
        total[:, cols] = multiply(place.w, cols) + multiply(place.sib, cols)

    def last_tile(n):
        cols = span(n * wide, wide)
        value = total[:, cols] + multiply(place.far, cols) + multiply(place.diag, cols)
        qkv[:, cols] = value.astype(jnp.bfloat16)

    def pass_piece(gather, n):
        @pl.when(n < pieces)
        def _():
            gather.pass_on(n)

        @pl.when(n >= 1)
        def _():
            gather.pass_pair(n - 1)

    gathers[0].pass_on(0)
    every(0, rows // band, norm_band)
    pass_piece(gathers[0], jnp.int32(1))
    dispatch.forward(0)
    turned[0] = act[...].T
    gathers[0].near_ready()
    every(0, columns // wide, first_tile)
    early = max(pieces - 1, owners // 2)

    def pass_step(n):
        @pl.when(n <= pieces)
        def _():
            pass_piece(gathers[0], n)

        @pl.when(n - 1 < owners)
        def _():
            dispatch.forward(n - 1)

    every(2, early + 2, pass_step)
    gathers[0].far_ready()
    every(0, columns // wide, last_tile)
    stores = [
        pltpu.make_async_copy(src, dst, store_sem.at[i])
        for i, (src, dst) in enumerate(
            [(qkv, qkv_out), (turned.at[0], act_out), (back, back_out), (weight, weight_out),
             (turned.at[1], merged_out), (out_w, out_full)]
        )
    ]
    for store in stores[:4]:
        store.start()
    half = rows // 2
    pairs = width // LANES

    def keep_probs(i):
        slot = lax.rem(i, 2)
        return (
            pltpu.make_async_copy(
                low_buf.at[slot], low_out.at[pl.ds(2 * i, 2)], prob_sem.at[0, slot]
            ),
            pltpu.make_async_copy(
                high_buf.at[slot], high_out.at[pl.ds(2 * i, 2)], prob_sem.at[1, slot]
            ),
        )

    def attend_pair(i):
        slot = lax.rem(i, 2)

        @pl.when(i >= 2)
        def _():
            for copy in keep_probs(i - 2):
                copy.wait()

        query, key, value = (
            qkv[:, span(part * width + i * LANES, LANES)] for part in range(3)
        )
        tops, bottoms = [], []
        for head in range(2):
            part = slice(head * HEAD_DIM, (head + 1) * HEAD_DIM)
            low, high, top, bottom = attend_head(
                query[:, part], key[:, part], value[:, part], prefix_ref[0]
            )
            low_buf[slot, head] = low
            high_buf[slot, head] = high
            tops.append(top)
            bottoms.append(bottom)
        cols = span(i * LANES, LANES)
        merged[:half, cols] = jnp.concatenate(tops, axis=1).astype(jnp.bfloat16)
        merged[half:, cols] = jnp.concatenate(bottoms, axis=1).astype(jnp.bfloat16)
        for copy in keep_probs(i):
            copy.start()

    def attend_step(i):
        @pl.when(i < pairs)
        def _():
            attend_pair(i)

        @pl.when(i + early + 1 < owners)
        def _():
            dispatch.forward(i + early + 1)

        @pl.when((i >= 1) & (i < pieces + 2))
        def _():
            pass_piece(gathers[1], i - 1)

        @pl.when(i < owners)
        def _():
            dispatch.relay(i)

    every(0, max(pairs, owners, pieces + 2), attend_step)
    turned[1] = merged[...].T
    stores[4].start()
    gathers[1].near_ready()
    gathers[1].far_ready()
    stores[5].start()
    gain_two, shift_two = vector(2), vector(3)
    band_two = min(128, rows)

    def middle(i):
        part = span(i * band_two, band_two)
        value = tokens_ref[part, :].astype(jnp.float32) + dot_nn(merged[part, :], out_w[...])
        hidden_ref[part, :] = value
        scaled, _ = norm_stats(value)
        act_two[part, :] = (scaled * gain_two + shift_two).astype(jnp.bfloat16)

    every(0, rows // band_two, middle)
    to_slots(act_two, send_ref)
    for i in (pairs - 2, pairs - 1):
        for copy in keep_probs(i):
            copy.wait()
    every(0, owners, dispatch.ready)
    for store in stores:
        store.wait()
    for copy in smalls:
        copy.wait_send()
    for gather in gathers:
        gather.drain()
    dispatch.drain()


def run_front(
    owners, experts, capacity, prefix, routes, priority, tokens, cotangent, small, router, w_qkv, w_out
):
    rows, width = tokens.shape
    shard, columns = w_qkv.shape
    half = rows // 2
    heads = width // HEAD_DIM
    pieces = 4
    any_spec = pl.BlockSpec(memory_space=pl.ANY)
    vmem_spec = pl.BlockSpec(memory_space=pltpu.VMEM)
    bf16, f32 = jnp.bfloat16, jnp.float32
    dma = pltpu.SemaphoreType.DMA

    def out(*shape):
        return jax.ShapeDtypeStruct(shape, bf16)

    def vm(*shape):
        return pltpu.VMEM(shape, bf16)

    return pl.pallas_call(
        functools.partial(front_kernel, (owners, capacity, pieces)),
        out_shape=(
            out(rows, columns),
            out(width, rows),
            out(width, rows),
            out(rows, rows),
            out(4 * shard, columns),
            out(4 * shard, width),
            out(heads, half, half),
            out(heads, half, rows),
            out(experts, owners * 4 * capacity, width),
            jax.ShapeDtypeStruct((rows, width), f32),
            out(owners, experts, capacity, width),
            out(4, *small.shape),
            out(LANES, width),
        ),
        in_specs=[pl.BlockSpec(memory_space=pltpu.SMEM)] + [vmem_spec] * 4 + [any_spec] * 4,
        out_specs=(any_spec,) * 9 + (vmem_spec,) * 4,
        scratch_shapes=[
            vm(4, small.shape[0] + router.shape[0], shard),
            vm(4 * shard, columns),
            vm(4 * shard, width),
            pltpu.VMEM((rows, columns), f32),
            vm(rows, columns),
            vm(rows, width),
            vm(rows, width),
            vm(rows, width),
            vm(2, width, rows),
            vm(rows, rows),
            vm(rows, rows),
            vm(owners, experts, capacity, width),
            vm(2, 2, half, half),
            vm(2, 2, half, rows),
            dma((5,)),
            dma((4, owners)),
            dma((4, owners)),
            dma((2, 3)),
            dma((2, 3)),
            dma((2,)),
            dma((2,)),
            dma((2, 4, pieces)),
            dma((2, 4, pieces)),
            dma((6,)),
            dma((2, 2)),
        ],
        compiler_params=pltpu.CompilerParams(
            collective_id=0, has_side_effects=True, vmem_limit_bytes=VMEM_LIMIT
        ),
        name="front",
    )(prefix, routes, priority, tokens, cotangent, small, router, w_qkv, w_out)


class Reduce:
    def __init__(self, place, part, got, far, pair, lines, done, sems):
        self.p = place
        self.part, self.got, self.far = part, got, far
        self.pair, self.lines, self.done = pair, lines, done
        self.send, self.recv, self.line_send, self.line_recv = sems
        self.chunks = part.shape[0]
        self.halves = done.shape[1] // 2
        self.count = place.owners // 2
        self.slice = self.halves // self.count
        self.bit = lax.rem(place.e, 2)
        self.level = lax.div(place.e, 2)

    def step(self, which, n, src, dst, device):
        return remote(src, dst, self.send.at[which, n], self.recv.at[which, n], device)

    def swapped(self, n):
        return self.step(
            0, n, self.part.at[n, :, 1 - self.p.c], self.got.at[n], (self.p.e, self.p.sib)
        )

    def crossed(self, n):
        return self.step(
            1, n, self.part.at[n, 1 - self.p.x, self.p.c], self.far.at[n], (self.p.e, self.p.far)
        )

    def folded(self, n):
        other = span((1 - self.bit) * self.halves, self.halves)
        return self.step(
            2, n, self.part.at[n, self.p.x, self.p.c, other], self.pair.at[n],
            (self.p.pair, self.p.w),
        )

    def shared(self, n):
        part = self.done.at[n, span(self.bit * self.halves, self.halves)]
        return self.step(3, n, part, part, (self.p.pair, self.p.w))

    def line(self, which, n, k, src, dst):
        return remote(
            src, dst, self.line_send.at[which, n, k], self.line_recv.at[which, n, k],
            (self.p.ahead(2 * k), self.p.w),
        )

    def row(self, level):
        return span(self.bit * self.halves + level * self.slice, self.slice)

    def spreads(self, n, k):
        target = lax.rem(self.level + k, self.count)
        return self.line(
            0, n, k, self.part.at[n, self.p.x, self.p.c, self.row(target)], self.lines.at[n, k]
        )

    def collects(self, n, k):
        part = self.done.at[n, self.row(self.level)]
        return self.line(1, n, k, part, part)

    def pair_sum(self, n, side):
        return self.part[n, side, self.p.c].astype(jnp.float32) + self.got[n, side].astype(
            jnp.float32
        )

    def swap(self, n):
        self.swapped(n).start()

    def cross(self, n):
        self.swapped(n).wait_recv()
        side = 1 - self.p.x
        self.part[n, side, self.p.c] = self.pair_sum(n, side).astype(jnp.bfloat16)
        self.crossed(n).start()

    def fold(self, n):
        self.crossed(n).wait_recv()
        total = self.pair_sum(n, self.p.x) + self.far[n].astype(jnp.float32)
        self.part[n, self.p.x, self.p.c] = total.astype(jnp.bfloat16)
        self.folded(n).start()

    def spread(self, n):
        self.folded(n).wait_recv()
        own = span(self.bit * self.halves, self.halves)
        total = self.part[n, self.p.x, self.p.c, own, :].astype(jnp.float32) + self.pair[
            n
        ].astype(jnp.float32)
        self.part[n, self.p.x, self.p.c, own, :] = total.astype(jnp.bfloat16)
        for k in range(1, self.count):
            self.spreads(n, k).start()

    def collect(self, n):
        total = self.part[n, self.p.x, self.p.c, self.row(self.level), :].astype(jnp.float32)
        for k in range(1, self.count):
            self.spreads(n, k).wait_recv()
            total = total + self.lines[n, k].astype(jnp.float32)
        self.done[n, self.row(self.level), :] = total.astype(jnp.bfloat16)
        for k in range(1, self.count):
            self.collects(n, k).start()

    def share(self, n):
        for k in range(1, self.count):
            self.collects(n, k).wait_recv()
        self.shared(n).start()

    def finish(self, n):
        self.shared(n).wait_recv()

    def stages(self):
        return (self.cross, self.fold, self.spread, self.collect, self.share, self.finish)

    def drain(self):
        def one(n):
            for copy in (self.swapped(n), self.crossed(n), self.folded(n), self.shared(n)):
                copy.wait_send()
            for k in range(1, self.count):
                self.spreads(n, k).wait_send()
                self.collects(n, k).wait_send()

        every(0, self.chunks, one)


class Small:
    def __init__(self, place, value, part, got, mid, far, total, others, out, sems):
        self.p, self.value, self.part, self.got, self.mid = place, value, part, got, mid
        self.far, self.total, self.others, self.out = far, total, others, out
        self.send, self.recv, self.all_send, self.all_recv = sems

    def swapped(self):
        return remote(
            self.part.at[:, 1 - self.p.c], self.got, self.send.at[0], self.recv.at[0],
            (self.p.e, self.p.sib),
        )

    def crossed(self):
        return remote(
            self.mid, self.far, self.send.at[1], self.recv.at[1], (self.p.e, self.p.far)
        )

    def spreads(self, k):
        return remote(
            self.total, self.others.at[k], self.all_send.at[k], self.all_recv.at[k],
            (self.p.ahead(k), self.p.w),
        )

    def swap(self):
        size = self.part.shape[-1]
        for owner in range(4):
            self.part[owner // 2, owner % 2] = self.value[:, owner * size : (owner + 1) * size]
        self.swapped().start()

    def cross(self):
        self.swapped().wait_recv()
        self.mid[...] = self.part[1 - self.p.x, self.p.c] + self.got[1 - self.p.x]
        self.crossed().start()

    def spread(self):
        self.crossed().wait_recv()
        self.total[...] = self.part[self.p.x, self.p.c] + self.got[self.p.x] + self.far[...]
        for k in range(1, self.p.owners):
            self.spreads(k).start()

    def finish(self):
        total = self.total[...]
        for k in range(1, self.p.owners):
            self.spreads(k).wait_recv()
            total = total + self.others[k]
        vectors_out, gates_out = self.out
        vectors_out[...] = total[: vectors_out.shape[0]]
        gates_out[...] = total[vectors_out.shape[0] :]

    def drain(self):
        self.swapped().wait_send()
        self.crossed().wait_send()
        for k in range(1, self.p.owners):
            self.spreads(k).wait_send()


def norm_back_rows(grad, scaled, inverse, gain):
    weighted = grad * gain
    mean_one = jnp.mean(weighted, axis=1, keepdims=True)
    mean_two = jnp.mean(weighted * scaled, axis=1, keepdims=True)
    return inverse * (weighted - mean_one - scaled * mean_two)


def back_kernel(
    dims,
    home_grad_ref, back_ref, hidden_ref, cot_ref, tokens_ref, vectors_ref, router_ref,
    far_hbm, near_hbm, act_hbm, merged_hbm, qkv_hbm, weight_hbm, out_hbm, low_hbm, high_hbm,
    output_ref, tokens_out, vectors_out, gates_out, qkv_out, out_out,
    near_sums, far_sums, done_rows, home_out,
    act_t, merged_t, qkv, weight, out_w, low_buf, high_buf, attn, grad_merged, wide_q, wide_o,
    part_q, got_q, far_q, pair_q, lines_q, done_q,
    part_o, got_o, far_o, pair_o, lines_o, done_o,
    small, small_part, small_got, small_mid, small_far, small_sum, small_all,
    load_sem, prob_sem, own_sem, cross_send, cross_recv, home_send, home_recv, send_q, recv_q, lsend_q, lrecv_q, send_o, recv_o, lsend_o, lrecv_o,
    small_send, small_recv, all_send, all_recv, out_sem,
):
    owners, capacity, gates = dims
    grad_qkv = qkv
    place = Place(owners)
    loads = [
        pltpu.make_async_copy(src, dst, load_sem.at[i])
        for i, (src, dst) in enumerate(
            [(merged_hbm, merged_t), (out_hbm, out_w), (qkv_hbm, qkv), (act_hbm, act_t),
             (weight_hbm, weight), (near_hbm, near_sums)]
        )
    ]

    def load_probs(i):
        slot = lax.rem(i, 2)
        return (
            pltpu.make_async_copy(
                low_hbm.at[pl.ds(2 * i, 2)], low_buf.at[slot], prob_sem.at[0, slot]
            ),
            pltpu.make_async_copy(
                high_hbm.at[pl.ds(2 * i, 2)], high_buf.at[slot], prob_sem.at[1, slot]
            ),
        )

    for load in loads:
        load.start()
    for load in load_probs(0):
        load.start()
    greet(
        [(place.ahead(k), place.w) for k in range(1, owners)]
        + [(place.e, place.sib), (place.e, place.far)]
    )
    experts = near_sums.shape[0]
    groups = owners // 2
    late = LateReturn(
        place, capacity, experts, near_sums, None, far_hbm, far_sums, done_rows, home_out,
        (own_sem, cross_send, cross_recv, home_send, home_recv),
    )
    every(0, groups, lambda j: late.crossed(j).start())
    reduce_o = Reduce(
        place, part_o, got_o, far_o, pair_o, lines_o, done_o, (send_o, recv_o, lsend_o, lrecv_o)
    )
    reduce_q = Reduce(
        place, part_q, got_q, far_q, pair_q, lines_q, done_q, (send_q, recv_q, lsend_q, lrecv_q)
    )
    smalls = Small(
        place, small, small_part, small_got, small_mid, small_far, small_sum, small_all, (vectors_out, gates_out),
        (small_send, small_recv, all_send, all_recv),
    )
    rows, width = tokens_ref.shape
    shard = width // 4
    band = min(128, rows)
    lead = small.shape[0]

    def vector(which):
        parts = [vectors_ref[i, which : which + 1, :] for i in range(4)]
        return jnp.concatenate(parts, axis=1).astype(jnp.float32)

    gain_one, gain_two = vector(0), vector(2)
    small[: lead - gates, :] = jnp.zeros((lead - gates, width), jnp.float32)
    small[lead - gates :, :] = router_ref[:gates, :]

    def post(i):
        part = span(i * band, band)
        grad = dot_nn(back_ref[part, :], home_grad_ref.reshape(rows, width)[...])
        scaled, inverse = norm_stats(hidden_ref[part, :])
        value = cot_ref[part, :].astype(jnp.float32) + norm_back_rows(
            grad, scaled, inverse, gain_two
        )
        tokens_out[part, :] = value
        attn[part, :] = value.astype(jnp.bfloat16)
        small[2:3, :] += jnp.sum(grad * scaled, axis=0, keepdims=True)
        small[3:4, :] += jnp.sum(grad, axis=0, keepdims=True)

    every(0, rows // band, post)
    loads[0].wait()

    def weight_grad(part, n, left, right):
        def one(owner):
            value = dot_nn(left[span(owner * shard, shard), :], right)
            part[n, lax.div(owner, 2), lax.rem(owner, 2)] = value.astype(jnp.bfloat16)

        every(0, 4, one)

    tile_o = part_o.shape[-1]
    out_chunks = part_o.shape[0]
    for n in range(out_chunks):
        weight_grad(part_o, n, merged_t, attn[:, n * tile_o : (n + 1) * tile_o])
        reduce_o.swap(n)
    loads[1].wait()

    def merged_band(i):
        part = span(i * band, band)
        grad_merged[part, :] = dot_nt(attn[part, :], out_w[...]).astype(jnp.bfloat16)

    every(0, rows // band, merged_band)
    for load in loads[2:4] + loads[5:]:
        load.wait()
    pairs = part_q.shape[0]

    def attend_pair(i):
        slot = lax.rem(i, 2)
        for load in load_probs(i):
            load.wait()

        @pl.when(i + 1 < pairs)
        def _():
            for load in load_probs(i + 1):
                load.start()

        cols = span(i * LANES, LANES)
        query, key, value = (
            qkv[:, span(part * width + i * LANES, LANES)] for part in range(3)
        )
        grad = grad_merged[:, cols]
        results = []
        for head in range(2):
            part = slice(head * HEAD_DIM, (head + 1) * HEAD_DIM)
            results.append(
                attend_back_head(
                    query[:, part], key[:, part], value[:, part],
                    low_buf[slot, head], high_buf[slot, head], grad[:, part],
                )
            )
        for which in range(3):
            grad_qkv[:, span(which * width + i * LANES, LANES)] = jnp.concatenate(
                [results[0][which], results[1][which]], axis=1
            )
        right = jnp.concatenate(
            [grad_qkv[:, span(which * width + i * LANES, LANES)] for which in range(3)], axis=1
        )
        weight_grad(part_q, i, act_t, right)
        reduce_q.swap(i)

    def input_band(i):
        part = span(i * band, band)
        grad = dot_nt(grad_qkv[part, :], weight[...])
        scaled, inverse = norm_stats(tokens_ref[part, :].astype(jnp.float32))
        tokens_out[part, :] += norm_back_rows(grad, scaled, inverse, gain_one)
        small[0:1, :] += jnp.sum(grad * scaled, axis=0, keepdims=True)
        small[1:2, :] += jnp.sum(grad, axis=0, keepdims=True)

    def output_band(i):
        part = span(i * band, band)
        slots = home_out.reshape(rows, width)
        value = hidden_ref[part, :] + dot_nn(back_ref[part, :], slots[...])
        output_ref[part, :] = value.astype(jnp.bfloat16)

    def store_q(i):
        return [
            pltpu.make_async_copy(
                wide_q.at[i, :, pl.ds(which * LANES, LANES)],
                qkv_out.at[:, span(which * width + i * LANES, LANES)],
                out_sem.at[which, i],
            )
            for which in range(3)
        ]

    def store_o(n):
        return pltpu.make_async_copy(
            wide_o.at[n], out_out.at[:, span(n * tile_o, tile_o)], out_sem.at[3, n]
        )

    stages_o, stages_q = reduce_o.stages(), reduce_q.stages()
    delays = (1, 3, 4, 5, 6, 7)
    last = len(delays) - 1
    half = rows // band // 2

    def slot_step(slot):
        pl.when(slot < groups)(lambda: late.finish(slot))
        pl.when(slot < pairs)(lambda: attend_pair(slot))
        for s in range(last, -1, -1):
            n = slot - delays[s]

            @pl.when((n >= 0) & (n < pairs))
            def _(s=s, n=n):
                stages_q[s](n)
                if s == last:
                    wide_q[n] = done_q[n].astype(jnp.float32)
                    for copy in store_q(n):
                        copy.start()

            @pl.when(slot == delays[s] - 1)
            def _(s=s):
                for n in range(out_chunks):
                    stages_o[s](n)
                    if s == last:
                        wide_o[n] = done_o[n].astype(jnp.float32)
                        store_o(n).start()

        @pl.when(slot == pairs)
        def _():
            loads[4].wait()
            every(0, half, input_band)

        pl.when(slot == pairs + 1)(lambda: every(half, 2 * half, input_band))
        pl.when(slot == pairs + 2)(smalls.swap)
        pl.when(slot == pairs + 3)(smalls.cross)
        pl.when(slot == pairs + 4)(smalls.spread)

        @pl.when(slot == pairs + 3)
        def _():
            late.arrived()
            every(0, rows // band, output_band)

    every(0, pairs + delays[-1], slot_step)
    smalls.finish()

    def stored(i):
        for copy in store_q(i):
            copy.wait()

    every(0, pairs, stored)
    for n in range(out_chunks):
        store_o(n).wait()
    late.drain(groups)
    reduce_o.drain()
    reduce_q.drain()
    smalls.drain()


def run_back(
    owners, capacity, gates, home_grad, far_sums, near_sums, back, hidden, cotangent, tokens,
    vectors, router_grad, act_t, merged_t, qkv, weight, w_out, low, high,
):
    rows, width = tokens.shape
    shard = width // 4
    lead = 8 + gates
    groups = owners // 2
    pairs = width // LANES
    tile_o = min(512, width)
    out_chunks = width // tile_o
    count = owners // 2
    half = shard // 2
    mid = rows // 2
    any_spec = pl.BlockSpec(memory_space=pl.ANY)
    vmem_spec = pl.BlockSpec(memory_space=pltpu.VMEM)
    bf16, f32 = jnp.bfloat16, jnp.float32
    dma = pltpu.SemaphoreType.DMA

    def vm(*shape):
        return pltpu.VMEM(shape, bf16)

    def fm(*shape):
        return pltpu.VMEM(shape, f32)

    def reduce_buffers(chunks, tile):
        return [
            vm(chunks, 2, 2, shard, tile),
            vm(chunks, 2, shard, tile),
            vm(chunks, shard, tile),
            vm(chunks, half, tile),
            vm(chunks, count, half // count, tile),
            vm(chunks, shard, tile),
        ]

    def reduce_sems(chunks):
        return [dma((4, chunks)), dma((4, chunks)), dma((2, chunks, count)), dma((2, chunks, count))]

    return pl.pallas_call(
        functools.partial(back_kernel, (owners, capacity, gates)),
        out_shape=(
            jax.ShapeDtypeStruct((rows, width), bf16),
            jax.ShapeDtypeStruct((rows, width), f32),
            jax.ShapeDtypeStruct((8, shard), f32),
            jax.ShapeDtypeStruct((gates, shard), f32),
            jax.ShapeDtypeStruct((shard, 3 * width), f32),
            jax.ShapeDtypeStruct((shard, width), f32),
        ),
        in_specs=[vmem_spec] * 7 + [any_spec] * 9,
        out_specs=(vmem_spec,) * 4 + (any_spec,) * 2,
        scratch_shapes=[
            vm(*near_sums.shape),
            vm(*near_sums.shape),
            vm(*home_grad.shape),
            vm(*home_grad.shape),
            vm(width, rows),
            vm(width, rows),
            vm(rows, 3 * width),
            vm(width, 3 * width),
            vm(width, width),
            vm(2, 2, mid, mid),
            vm(2, 2, mid, rows),
            vm(rows, width),
            vm(rows, width),
            fm(pairs, shard, 3 * LANES),
            fm(out_chunks, shard, tile_o),
        ]
        + reduce_buffers(pairs, 3 * LANES)
        + reduce_buffers(out_chunks, tile_o)
        + [
            fm(lead, width),
            fm(2, 2, lead, shard),
            fm(2, lead, shard),
            fm(lead, shard),
            fm(lead, shard),
            fm(lead, shard),
            fm(owners, lead, shard),
            dma((6,)),
            dma((2, 2)),
            dma(()),
            dma((groups,)),
            dma((groups,)),
            dma((owners,)),
            dma((owners,)),
        ]
        + reduce_sems(pairs)
        + reduce_sems(out_chunks)
        + [dma((2,)), dma((2,)), dma((owners,)), dma((owners,)), dma((4, pairs))],
        compiler_params=pltpu.CompilerParams(
            collective_id=2, has_side_effects=True, vmem_limit_bytes=VMEM_LIMIT
        ),
        name="back",
    )(
        home_grad, back, hidden, cotangent, tokens, vectors, router_grad,
        far_sums, near_sums, act_t, merged_t, qkv, weight, w_out, low, high,
    )


def on_device_plain(
    tokens,
    norm1_gain,
    norm1_shift,
    w_qkv,
    w_out,
    norm2_gain,
    norm2_shift,
    w_router,
    w_up,
    w_down,
    routes,
    priority,
    prefix,
    cotangent,
):
    row_count, model_width = tokens.shape
    expert_count = w_router.shape[1]
    capacity = row_count // expert_count
    owners = lax.axis_size("expert")
    local_experts = w_up.shape[0]
    slot_count = expert_count * capacity
    prefix_len = prefix[0]
    small = jnp.concatenate(
        [
            norm1_gain[None],
            norm1_shift[None],
            norm2_gain[None],
            norm2_shift[None],
            w_router.T,
        ],
        axis=0,
    )
    qkv_full = lax.all_gather(w_qkv, "wshard", axis=0, tiled=True)
    small_full = lax.all_gather(small, "wshard", axis=1, tiled=True)
    out_full = lax.all_gather(w_out, "wshard", axis=0, tiled=True)
    gain_one, shift_one, gain_two, shift_two = (small_full[i] for i in range(4))
    router_full = small_full[4:].T
    gain_one = gain_one.astype(jnp.float32)
    gain_two = gain_two.astype(jnp.float32)
    inputs = tokens.astype(jnp.float32)
    normed_one, scaled_one, inverse_one = normalize(inputs, gain_one, shift_one.astype(jnp.float32))
    act_one = normed_one.astype(jnp.bfloat16)
    qkv = jnp.dot(act_one, qkv_full, preferred_element_type=jnp.float32).astype(jnp.bfloat16)
    query_heads = qkv[:, :model_width]
    key_heads = qkv[:, model_width : 2 * model_width]
    value_heads = qkv[:, 2 * model_width :]
    merged, log_totals = attend_forward(query_heads, key_heads, value_heads, prefix_len)
    attn_out = jnp.dot(merged, out_full, preferred_element_type=jnp.float32)
    hidden = inputs + attn_out
    normed_two, scaled_two, inverse_two = normalize(hidden, gain_two, shift_two.astype(jnp.float32))
    act_two = normed_two.astype(jnp.bfloat16)
    logits = jnp.dot(act_two, router_full, preferred_element_type=jnp.float32)
    row_max = jnp.max(logits, axis=-1, keepdims=True)
    exponent = jnp.exp(logits - row_max)
    gate_prob = exponent / jnp.sum(exponent, axis=-1, keepdims=True)
    route_ids = routes[:, 0]
    chosen = route_ids[:, None] == jnp.arange(expert_count, dtype=jnp.int32)[None, :]
    gate_value = jnp.sum(jnp.where(chosen, gate_prob, 0.0), axis=1)
    slot_index, slot_source = assign_slots(route_ids, priority[0], expert_count, capacity)
    zero_row = jnp.zeros((1, model_width), jnp.bfloat16)
    padded = jnp.concatenate([act_two, zero_row], axis=0)
    send_rows = padded[slot_source].reshape(owners, local_experts * capacity, model_width)
    arrived = lax.all_to_all(send_rows, "expert", split_axis=0, concat_axis=0, tiled=True).reshape(
        owners, local_experts, capacity, model_width
    )
    group = lax.axis_size("wshard")
    local_rows = owners * capacity

    def by_expert(chunk):
        rows = jnp.transpose(chunk, (1, 0, 2, 3)).reshape(local_experts, local_rows, model_width)
        return lax.all_gather(rows, "wshard", axis=1, tiled=True)

    def home_rows(rows):
        own = lax.psum_scatter(rows.astype(jnp.bfloat16), "wshard", scatter_dimension=1, tiled=True)
        own = own.reshape(local_experts, owners, capacity, model_width)
        return jnp.transpose(own, (1, 0, 2, 3)).reshape(
            owners, local_experts * capacity, model_width
        )

    grad_output = cotangent.astype(jnp.float32)
    grad_combined = (gate_value[:, None] * grad_output).astype(jnp.bfloat16)
    grad_padded = jnp.concatenate([grad_combined, zero_row], axis=0)
    grad_send = grad_padded[slot_source].reshape(owners, local_experts * capacity, model_width)
    grad_arrived = lax.all_to_all(
        grad_send, "expert", split_axis=0, concat_axis=0, tiled=True
    ).reshape(owners, local_experts, capacity, model_width)
    rows_in = by_expert(arrived)
    grad_rows = by_expert(grad_arrived)
    pre_act = jnp.einsum("erd,edf->erf", rows_in, w_up, preferred_element_type=jnp.float32)
    activated, gelu_pull = jax.vjp(gelu_tanh, pre_act)
    act_hidden = activated.astype(jnp.bfloat16)
    produced = jnp.einsum(
        "erf,efd->erd", act_hidden, w_down, preferred_element_type=jnp.float32
    )
    expert_out = home_rows(produced)
    returned = lax.all_to_all(expert_out, "expert", split_axis=0, concat_axis=0, tiled=True)
    slots_back = jnp.concatenate([returned.reshape(slot_count, model_width), zero_row], axis=0)
    combined = slots_back[slot_index].astype(jnp.float32)
    output = (hidden + gate_value[:, None] * combined).astype(jnp.bfloat16)
    grad_gate = jnp.sum(grad_output * combined, axis=1)
    grad_down = jnp.einsum(
        "erf,erd->efd", act_hidden, grad_rows, preferred_element_type=jnp.float32
    )
    grad_hidden_units = jnp.einsum(
        "erd,efd->erf", grad_rows, w_down, preferred_element_type=jnp.float32
    )
    grad_pre = gelu_pull(grad_hidden_units)[0].astype(jnp.bfloat16)
    grad_up = jnp.einsum("erd,erf->edf", rows_in, grad_pre, preferred_element_type=jnp.float32)
    grad_expert_in = jnp.einsum(
        "erf,edf->erd", grad_pre, w_up, preferred_element_type=jnp.float32
    )
    grad_send_back = home_rows(grad_expert_in)
    grad_back = lax.all_to_all(grad_send_back, "expert", split_axis=0, concat_axis=0, tiled=True)
    grad_slots = jnp.concatenate([grad_back.reshape(slot_count, model_width), zero_row], axis=0)
    grad_act_two = grad_slots[slot_index].astype(jnp.float32)
    grad_logits = (
        gate_prob * (jnp.where(chosen, grad_gate[:, None], 0.0) - (gate_value * grad_gate)[:, None])
    ).astype(jnp.bfloat16)
    grad_router = contract_rows(act_two, grad_logits)
    grad_act_two = grad_act_two + times_transpose(grad_logits, router_full)
    grad_from_two, grad_gain_two, grad_shift_two = norm_back(
        grad_act_two, scaled_two, inverse_two, gain_two
    )
    grad_hidden = grad_output + grad_from_two
    grad_attn = grad_hidden.astype(jnp.bfloat16)
    grad_out_w = contract_rows(merged, grad_attn)
    grad_merged = times_transpose(grad_attn, out_full).astype(jnp.bfloat16)
    grad_qkv = attend_backward(
        query_heads, key_heads, value_heads, grad_merged, log_totals, prefix_len
    )
    grad_qkv_w = contract_rows(act_one, grad_qkv)
    grad_act_one = times_transpose(grad_qkv, qkv_full)
    grad_from_one, grad_gain_one, grad_shift_one = norm_back(
        grad_act_one, scaled_one, inverse_one, gain_one
    )
    grad_tokens = grad_hidden + grad_from_one
    small_grad = jnp.concatenate(
        [
            grad_gain_one[None],
            grad_shift_one[None],
            grad_gain_two[None],
            grad_shift_two[None],
            grad_router.T,
        ],
        axis=0,
    )
    out_share = lax.psum_scatter(
        grad_out_w.astype(jnp.bfloat16), "wshard", scatter_dimension=0, tiled=True
    )
    qkv_share = lax.psum_scatter(
        grad_qkv_w.astype(jnp.bfloat16), "wshard", scatter_dimension=0, tiled=True
    )
    small_share = lax.psum_scatter(small_grad, "wshard", scatter_dimension=1, tiled=True)
    out_total = lax.psum(out_share, "expert").astype(jnp.float32)
    qkv_total = lax.psum(qkv_share, "expert").astype(jnp.float32)
    small_total = lax.psum(small_share, "expert")
    totals = (
        small_total[0],
        small_total[1],
        qkv_total,
        out_total,
        small_total[2],
        small_total[3],
        small_total[4:].T,
    )
    return (
        output,
        grad_tokens,
        totals[0],
        totals[1],
        totals[2],
        totals[3],
        totals[4],
        totals[5],
        totals[6],
        grad_up,
        grad_down,
    )


def on_device(
    tokens,
    norm1_gain,
    norm1_shift,
    w_qkv,
    w_out,
    norm2_gain,
    norm2_shift,
    w_router,
    w_up,
    w_down,
    routes,
    priority,
    prefix,
    cotangent,
):
    row_count, model_width = tokens.shape
    expert_count = w_router.shape[1]
    capacity = row_count // expert_count
    owners = lax.axis_size("expert")
    experts = w_up.shape[0]
    which = lax.broadcasted_iota(jnp.int32, (16, norm1_gain.shape[0]), 0)
    small = jnp.zeros(which.shape, jnp.bfloat16)
    for i, vector in enumerate((norm1_gain, norm1_shift, norm2_gain, norm2_shift)):
        small = jnp.where(which == i, vector[None], small)
    (
        qkv, act_t, merged_t, back, weight, out_full, low, high, grad_rows, hidden, send_rows,
        vectors, router,
    ) = run_front(
        owners, experts, capacity, prefix, routes.reshape(1, row_count), priority, tokens,
        cotangent, small, w_router.T, w_qkv, w_out,
    )
    far_sums, near_sums, home_grad, grad_up, grad_down, grad_router = run_experts(
        owners, capacity, expert_count, send_rows, grad_rows, w_up, w_down, router
    )
    output, grad_tokens, grad_vectors, grad_gates, grad_qkv, grad_out = run_back(
        owners, capacity, expert_count, home_grad, far_sums, near_sums, back, hidden, cotangent,
        tokens, vectors, grad_router, act_t, merged_t, qkv, weight, out_full, low, high,
    )
    return (
        output,
        grad_tokens,
        grad_vectors[0],
        grad_vectors[1],
        grad_qkv,
        grad_out,
        grad_vectors[2],
        grad_vectors[3],
        grad_gates.T,
        grad_up.astype(jnp.float32),
        grad_down.astype(jnp.float32),
    )


def solution(mesh):
    placed = (
        P(("expert", "wshard"), None),
        P("wshard"),
        P("wshard"),
        P("wshard", None),
        P("wshard", None),
        P("wshard"),
        P("wshard"),
        P("wshard", None),
        P("expert", None, "wshard"),
        P("expert", "wshard", None),
        P(("expert", "wshard"), None),
        P(("expert", "wshard"), None),
        P(("expert", "wshard")),
        P(("expert", "wshard"), None),
    )
    owners, group = mesh.shape["expert"], mesh.shape["wshard"]

    def body(*args):
        capacity = args[0].shape[0] // args[7].shape[1]
        fits = group == 4 and owners in (4, 8, 16) and capacity % 16 == 0 and args[7].shape[1] % 16 == 0
        return (on_device if fits else on_device_plain)(*args)

    return jax.shard_map(
        body,
        mesh=mesh,
        in_specs=placed,
        out_specs=(
            P(("expert", "wshard"), None),
            P(("expert", "wshard"), None),
            P("wshard"),
            P("wshard"),
            P("wshard", None),
            P("wshard", None),
            P("wshard"),
            P("wshard"),
            P("wshard", None),
            P("expert", None, "wshard"),
            P("expert", "wshard", None),
        ),
        check_vma=False,
    )
```

```python
import functools
import math

import jax
import jax.numpy as jnp
from jax import lax
from jax.experimental import pallas as pl
from jax.experimental.pallas import tpu as pltpu
from jax.sharding import PartitionSpec as P

HEADS = 16
HEAD_DIM = 64


epsilon = 1e-05
VMEM_LIMIT = 66_000_000
TILE = 1024
EARLY_CHUNKS = 2


def normalize(values, gain_vec, shift_vec):
    row_mean = jnp.mean(values, axis=-1, keepdims=True)
    centered = values - row_mean
    inverse = lax.rsqrt(jnp.mean(centered * centered, axis=-1, keepdims=True) + epsilon)
    scaled = centered * inverse
    return (scaled * gain_vec + shift_vec, scaled, inverse)


def norm_back(grad_rows, scaled, inverse, gain_vec):
    weighted = grad_rows * gain_vec
    mean_one = jnp.mean(weighted, axis=-1, keepdims=True)
    mean_two = jnp.mean(weighted * scaled, axis=-1, keepdims=True)
    grad_inputs = inverse * (weighted - mean_one - scaled * mean_two)
    return (grad_inputs, jnp.sum(grad_rows * scaled, axis=0), jnp.sum(grad_rows, axis=0))


def contract_rows(left, right):
    return lax.dot_general(
        left, right, (((0,), (0,)), ((), ())), preferred_element_type=jnp.float32
    )


def times_transpose(left, right):
    return lax.dot_general(
        left, right, (((1,), (1,)), ((), ())), preferred_element_type=jnp.float32
    )


def gelu_tanh(values):
    return jax.nn.gelu(values, approximate=True)


def assign_slots(route_ids, order_ids, expert_count, capacity):
    token_count = route_ids.shape[0]
    same_expert = route_ids[:, None] == route_ids[None, :]
    earlier = order_ids[None, :] < order_ids[:, None]
    rank_ids = jnp.sum((same_expert & earlier).astype(jnp.int32), axis=1)
    is_kept = rank_ids < capacity
    slot_index = jnp.where(is_kept, route_ids * capacity + rank_ids, expert_count * capacity)
    slot_ids = jnp.arange(expert_count * capacity, dtype=jnp.int32)
    match_table = slot_index[None, :] == slot_ids[:, None]
    token_ids = jnp.arange(token_count, dtype=jnp.int32)
    filled = jnp.any(match_table, axis=1)
    picked = jnp.sum(jnp.where(match_table, token_ids[None, :], 0), axis=1)
    slot_source = jnp.where(filled, picked, token_count)
    return (slot_index, slot_source)


def group_heads(values, groups):
    token_count = values.shape[0]
    return jnp.transpose(values.reshape(token_count, groups, -1, HEAD_DIM), (1, 0, 2, 3))


def block_scores(query_block, key_group, block_start, prefix_len):
    block_rows = query_block.shape[0]
    key_count = key_group.shape[0]
    scores = jnp.einsum(
        "qgd,kgd->gqk", query_block, key_group, preferred_element_type=jnp.float32
    ) * (1.0 / math.sqrt(HEAD_DIM))
    query_pos = block_start + jnp.arange(block_rows, dtype=jnp.int32)
    key_pos = jnp.arange(key_count, dtype=jnp.int32)
    allowed = (key_pos[None, :] <= query_pos[:, None]) | (key_pos[None, :] < prefix_len)
    return jnp.where(allowed[None], scores, -1e30)


def attend_forward(query_heads, key_heads, value_heads, prefix_len):
    token_count = query_heads.shape[0]
    group_size = min(4, HEADS)
    groups = HEADS // group_size
    block_rows = min(512, token_count)
    blocks = token_count // block_rows
    starts = jnp.arange(blocks, dtype=jnp.int32) * block_rows

    def one_group(group_item):
        query_group, key_group, value_group = group_item
        query_blocks = query_group.reshape(blocks, block_rows, group_size, HEAD_DIM)

        def one_block(block_item):
            query_block, block_start = block_item
            scores = block_scores(query_block, key_group, block_start, prefix_len)
            row_max = jnp.max(scores, axis=-1, keepdims=True)
            exponent = jnp.exp(scores - row_max)
            row_total = jnp.sum(exponent, axis=-1, keepdims=True)
            attn_probs = (exponent / row_total).astype(jnp.bfloat16)
            result = jnp.einsum(
                "gqk,kgd->qgd", attn_probs, value_group, preferred_element_type=jnp.float32
            )
            return (result, (row_max + jnp.log(row_total))[..., 0])

        return lax.map(one_block, (query_blocks, starts))

    attended, log_totals = lax.map(
        one_group,
        (
            group_heads(query_heads, groups),
            group_heads(key_heads, groups),
            group_heads(value_heads, groups),
        ),
    )
    merged = (
        jnp.transpose(attended, (1, 2, 0, 3, 4))
        .reshape(token_count, HEADS * HEAD_DIM)
        .astype(jnp.bfloat16)
    )
    return (merged, log_totals)


def attend_backward(query_heads, key_heads, value_heads, grad_merged, log_totals, prefix_len):
    token_count = query_heads.shape[0]
    group_size = min(4, HEADS)
    groups = HEADS // group_size
    block_rows = min(512, token_count)
    blocks = token_count // block_rows
    starts = jnp.arange(blocks, dtype=jnp.int32) * block_rows
    score_scale = 1.0 / math.sqrt(HEAD_DIM)

    def one_group(group_item):
        query_group, key_group, value_group, grad_group, total_group = group_item
        query_blocks = query_group.reshape(blocks, block_rows, group_size, HEAD_DIM)
        grad_blocks = grad_group.reshape(blocks, block_rows, group_size, HEAD_DIM)

        def one_block(carry, block_item):
            grad_keys, grad_vals = carry
            query_block, grad_block, total_block, block_start = block_item
            scores = block_scores(query_block, key_group, block_start, prefix_len)
            attn_probs = jnp.exp(scores - total_block[..., None])
            grad_probs = jnp.einsum(
                "qgd,kgd->gqk", grad_block, value_group, preferred_element_type=jnp.float32
            )
            row_delta = jnp.sum(attn_probs * grad_probs, axis=-1, keepdims=True)
            grad_scores = (attn_probs * (grad_probs - row_delta)).astype(jnp.bfloat16)
            grad_vals = grad_vals + jnp.einsum(
                "gqk,qgd->kgd",
                attn_probs.astype(jnp.bfloat16),
                grad_block,
                preferred_element_type=jnp.float32,
            )
            grad_keys = (
                grad_keys
                + jnp.einsum(
                    "gqk,qgd->kgd", grad_scores, query_block, preferred_element_type=jnp.float32
                )
                * score_scale
            )
            grad_query = (
                jnp.einsum(
                    "gqk,kgd->qgd", grad_scores, key_group, preferred_element_type=jnp.float32
                )
                * score_scale
            )
            return ((grad_keys, grad_vals), grad_query)

        zero_keys = jnp.zeros(key_group.shape, jnp.float32)
        carried, grad_queries = lax.scan(
            one_block, (zero_keys, zero_keys), (query_blocks, grad_blocks, total_group, starts)
        )
        return (grad_queries, carried[0], carried[1])

    grad_queries, grad_keys, grad_vals = lax.map(
        one_group,
        (
            group_heads(query_heads, groups),
            group_heads(key_heads, groups),
            group_heads(value_heads, groups),
            group_heads(grad_merged, groups),
            log_totals,
        ),
    )
    query_part = jnp.transpose(grad_queries, (1, 2, 0, 3, 4)).reshape(token_count, HEADS * HEAD_DIM)
    key_part = jnp.transpose(grad_keys, (1, 0, 2, 3)).reshape(token_count, HEADS * HEAD_DIM)
    value_part = jnp.transpose(grad_vals, (1, 0, 2, 3)).reshape(token_count, HEADS * HEAD_DIM)
    return jnp.concatenate([query_part, key_part, value_part], axis=1).astype(jnp.bfloat16)


MESH = pl.DeviceIdType.MESH
LANES = 128


def dot_nn(left, right):
    return lax.dot_general(
        left, right, (((1,), (0,)), ((), ())), preferred_element_type=jnp.float32
    )


def dot_nt(left, right):
    return lax.dot_general(
        left, right, (((1,), (1,)), ((), ())), preferred_element_type=jnp.float32
    )


def dot_tn(left, right):
    return lax.dot_general(
        left, right, (((0,), (0,)), ((), ())), preferred_element_type=jnp.float32
    )


def span(start, size):
    return pl.ds(pl.multiple_of(start, size), size)


def every(start, stop, step):
    def body(i, carry):
        step(i)
        return carry

    lax.fori_loop(start, stop, body, 0)


class Place:
    def __init__(self, owners):
        self.owners = owners
        self.e = lax.axis_index("expert")
        self.w = lax.axis_index("wshard")
        self.c = lax.rem(self.w, 2)
        self.x = lax.div(self.w, 2)
        self.sib = self.w + 1 - 2 * self.c
        self.far = lax.rem(self.w + 2, 4)
        self.diag = 3 - self.w
        self.pair = self.e + 1 - 2 * lax.rem(self.e, 2)

    def ahead(self, k):
        return lax.rem(self.e + k, self.owners)

    def peer(self, n):
        other = lax.div(n, 2) + lax.rem(n, 2) * (self.owners // 2)
        result, bit = 0, 1
        while bit < self.owners:
            result = result + bit * lax.rem(lax.div(self.e, bit) + lax.div(other, bit), 2)
            bit *= 2
        return result


def remote(src, dst, send, recv, device):
    return pltpu.make_async_remote_copy(
        src_ref=src,
        dst_ref=dst,
        send_sem=send,
        recv_sem=recv,
        device_id=device,
        device_id_type=MESH,
    )


def greet(peers):
    barrier = pltpu.get_barrier_semaphore()
    for peer in peers:
        pl.semaphore_signal(barrier, inc=1, device_id=peer, device_id_type=MESH)
    pl.semaphore_wait(barrier, len(peers))


def either(test, yes, no):
    pl.when(test)(yes)
    pl.when(jnp.logical_not(test))(no)


class Dispatch:
    def __init__(self, place, capacity, send_ref, rows_ref, sems):
        self.p, self.cap, self.src, self.rows = place, capacity, send_ref, rows_ref
        self.own_sem, self.send, self.recv = sems

    def slice(self, k, core, side):
        start = (((lax.div(k, 2) * 2 + core) * 2 + side) * 2 + lax.rem(k, 2)) * self.cap
        return self.rows.at[:, span(start, self.cap)]

    def own(self):
        return pltpu.make_async_copy(
            self.src.at[self.p.e], self.slice(0, self.p.c, self.p.x), self.own_sem
        )

    def direct(self, k):
        return remote(
            self.src.at[self.p.peer(k)],
            self.slice(k, self.p.c, self.p.x),
            self.send.at[0, k],
            self.recv.at[0, k],
            (self.p.peer(k), self.p.w),
        )

    def hop(self, k, side, which, peer):
        part = self.slice(k, self.p.c, side)
        return remote(
            part, part, self.send.at[which, k], self.recv.at[which, k], (self.p.e, peer)
        )

    def to_sib(self, k):
        return self.hop(k, self.p.x, 1, self.p.sib)

    def to_far(self, k):
        return self.hop(k, self.p.x, 2, self.p.far)

    def relayed(self, k):
        return self.hop(k, 1 - self.p.x, 3, self.p.sib)

    def start(self):
        self.own().start()
        every(1, self.p.owners, lambda k: self.direct(k).start())

    def forward(self, k):
        k = jnp.int32(k)

        @pl.when(k == 0)
        def _():
            self.own().wait()

        @pl.when(k > 0)
        def _():
            self.direct(k).wait_recv()

        self.to_far(k).start()
        self.to_sib(k).start()

    def relay(self, k):
        self.to_far(k).wait_recv()
        self.relayed(k).start()

    def ready(self, k):
        self.to_sib(k).wait_recv()
        self.relayed(k).wait_recv()

    def drain(self):
        every(1, self.p.owners, lambda k: self.direct(k).wait_send())

        def rest(k):
            self.to_sib(k).wait_send()
            self.to_far(k).wait_send()
            self.relayed(k).wait_send()

        every(0, self.p.owners, rest)


class Return:
    def __init__(self, place, capacity, experts, part, got, mid, far, done, home, sems):
        self.p, self.cap, self.experts = place, capacity, experts
        self.part, self.got, self.mid, self.far, self.done, self.home = (
            part, got, mid, far, done, home,
        )
        self.own_sem, self.send, self.recv, self.home_send, self.home_recv = sems

    def swapped(self, j):
        size = 4 * self.cap
        return remote(
            self.part.at[:, span((j * 2 + 1 - self.p.c) * size, size)],
            self.got.at[:, span(j * size, size)],
            self.send.at[0, j],
            self.recv.at[0, j],
            (self.p.e, self.p.sib),
        )

    def crossed(self, j):
        part = span(j * 2 * self.cap, 2 * self.cap)
        return remote(
            self.mid.at[:, part],
            self.far.at[:, part],
            self.send.at[1, j],
            self.recv.at[1, j],
            (self.p.e, self.p.far),
        )

    def own(self):
        return pltpu.make_async_copy(self.done.at[0], self.home.at[self.p.e], self.own_sem)

    def homed(self, n):
        return remote(
            self.done.at[n],
            self.home.at[self.p.e],
            self.home_send.at[n],
            self.home_recv.at[n],
            (self.p.peer(n), self.p.w),
        )

    def pair_sum(self, expert, j, side):
        size = 2 * self.cap
        mine = self.part[expert, span(((j * 2 + self.p.c) * 2 + side) * size, size), :]
        theirs = self.got[expert, span((j * 2 + side) * size, size), :]
        return mine.astype(jnp.float32) + theirs.astype(jnp.float32)

    def swap(self, j):
        self.swapped(j).start()

    def split(self, j):
        self.swapped(j).wait_recv()
        here = span(j * 2 * self.cap, 2 * self.cap)
        for expert in range(self.experts):
            self.mid[expert, here, :] = self.pair_sum(expert, j, 1 - self.p.x).astype(jnp.bfloat16)
            self.keep[expert, here, :] = self.pair_sum(expert, j, self.p.x).astype(jnp.bfloat16)

    def cross(self, j):
        self.swapped(j).wait_recv()
        size = 2 * self.cap
        for expert in range(self.experts):
            self.mid[expert, span(j * size, size), :] = self.pair_sum(
                expert, j, 1 - self.p.x
            ).astype(jnp.bfloat16)
        self.crossed(j).start()

    def this_side(self, expert, j):
        return self.pair_sum(expert, j, self.p.x)

    def finish(self, j):
        self.crossed(j).wait_recv()
        size = 2 * self.cap
        for expert in range(self.experts):
            total = self.this_side(expert, j) + self.far[
                expert, span(j * size, size), :
            ].astype(jnp.float32)
            total = total.astype(jnp.bfloat16)
            self.done[2 * j, expert] = total[: self.cap]
            self.done[2 * j + 1, expert] = total[self.cap :]
        j = jnp.int32(j)
        self.homed(2 * j + 1).start()
        either(j == 0, lambda: self.own().start(), lambda: self.homed(2 * j).start())

    def drain_swaps(self, chunks):
        every(0, chunks, lambda j: self.swapped(j).wait_send())

    def drain(self, first, last):
        every(first, last, lambda j: self.crossed(j).wait_send())
        every(max(1, 2 * first), 2 * last, lambda n: self.homed(n).wait_send())

    def arrived(self, first, last):
        if first == 0:
            self.own().wait()
        every(max(1, 2 * first), 2 * last, lambda n: self.homed(n).wait_recv())


class LateReturn(Return):
    def crossed(self, j):
        part = span(j * 2 * self.cap, 2 * self.cap)
        return remote(
            self.mid.at[:, part],
            self.far.at[:, part],
            self.send.at[j],
            self.recv.at[j],
            (self.p.e, self.p.far),
        )

    def this_side(self, expert, j):
        size = 2 * self.cap
        return self.part[expert, span(j * size, size), :].astype(jnp.float32)


def gelu_pair(v):
    root = math.sqrt(2.0 / math.pi)
    square = v * v
    t = jnp.tanh(v * (root + (root * 0.044715) * square))
    half = 0.5 + 0.5 * t
    slope = half + (half * (1.0 - t)) * (v * (root + (3.0 * root * 0.044715) * square))
    return v * half, slope


def expert_kernel(
    dims,
    send_ref, grads_hbm, up_hbm, down_hbm, router_ref,
    far_sums, near_sums, home_out, home_grad, up_out, down_out, router_grad,
    rows, grads, scaled, hidden, pre, up, down, grad_up, grad_down,
    part_out, part_grad, got_out, got_grad, mid_out, mid_grad,
    keep_out, far_grad, far_out, done_grad, done_out,
    load_sem, own_sem, disp_send, disp_recv, red_send, red_recv, home_send, home_recv,
):
    owners, experts, capacity, width, units, expert_count = dims
    place = Place(owners)
    loads = [
        pltpu.make_async_copy(src, dst, load_sem.at[i])
        for i, (src, dst) in enumerate(
            [(up_hbm, up), (grads_hbm, grads), (down_hbm, down)]
        )
    ]
    for load in loads:
        load.start()
    greet(
        [(place.ahead(k), place.w) for k in range(1, owners)]
        + [(place.e, place.sib), (place.e, place.far)]
    )
    dispatch = Dispatch(
        place, capacity, send_ref, rows, (own_sem.at[0], disp_send, disp_recv)
    )
    ret_grad = Return(
        place, capacity, experts, part_grad, got_grad, mid_grad, far_grad, done_grad, home_grad,
        (own_sem.at[1], red_send.at[0], red_recv.at[0], home_send.at[0], home_recv.at[0]),
    )
    ret_out = Return(
        place, capacity, experts, part_out, got_out, mid_out, far_out, done_out, home_out,
        (own_sem.at[2], red_send.at[1], red_recv.at[1], home_send.at[1], home_recv.at[1]),
    )
    dispatch.start()
    router_grad[...] = jnp.zeros_like(router_grad)
    tile = min(TILE, units)
    wide = min(TILE, width)
    chunks = owners // 2
    early = EARLY_CHUNKS
    size = 8 * capacity
    lane = lax.broadcasted_iota(jnp.int32, (size, LANES), 1)

    def compute(j, expert):
        here = span(j * size, size)
        logits = dot_nt(rows[expert, here, :], router_ref[...])
        logits = jnp.where(lane < expert_count, logits, -1e30)
        exponent = jnp.exp(logits - jnp.max(logits, axis=1, keepdims=True))
        prob = exponent * (1.0 / jnp.sum(exponent, axis=1, keepdims=True))
        mine = lane == place.e * experts + expert
        gate = jnp.sum(jnp.where(mine, prob, 0.0), axis=1, keepdims=True)
        scaled[expert, here, :] = (
            gate * grads[expert, here, :].astype(jnp.float32)
        ).astype(jnp.bfloat16)

        def one_tile(n):
            cols = span(n * tile, tile)
            value, slope = gelu_pair(dot_nn(rows[expert, here, :], up[expert, :, cols]))
            hidden[expert, here, cols] = value.astype(jnp.bfloat16)
            back = dot_nt(scaled[expert, here, :], down[expert, cols, :])
            pre[expert, here, cols] = (back * slope).astype(jnp.bfloat16)

        every(0, units // tile, one_tile)

        def one_out(n, total):
            cols = span(n * wide, wide)
            value = dot_nn(hidden[expert, here, :], down[expert, :, cols])
            part_out[expert, here, cols] = (gate * value).astype(jnp.bfloat16)
            weighted = value * grads[expert, here, cols].astype(jnp.float32)
            for start in range(0, wide, LANES):
                total = total + weighted[:, start : start + LANES]
            return total

        total = lax.fori_loop(
            0, width // wide, one_out, jnp.zeros((size, LANES), jnp.float32)
        )
        grad_gate = jnp.sum(total, axis=1, keepdims=True)
        grad_logits = (
            prob * ((jnp.where(mine, 1.0, 0.0) - gate) * grad_gate)
        ).astype(jnp.bfloat16)

        def one_in(n):
            cols = span(n * wide, wide)
            value = dot_nt(pre[expert, here, :], up[expert, cols, :]) + dot_nn(
                grad_logits, router_ref[:, cols]
            )
            part_grad[expert, here, cols] = value.astype(jnp.bfloat16)
            router_grad[:, cols] += dot_tn(grad_logits, rows[expert, here, cols])

        every(0, width // wide, one_in)

    block = min(256, width)

    def weight_grads(expert, first, last):
        def one(n):
            part = span(n * block, block)
            grad_down[expert, part, :] = dot_tn(
                hidden[expert, :, part], scaled[expert]
            ).astype(jnp.bfloat16)
            grad_up[expert, part, :] = dot_tn(rows[expert, :, part], pre[expert]).astype(
                jnp.bfloat16
            )

        every(first * width // block // 4, last * width // block // 4, one)

    def keep(expert):
        return [
            pltpu.make_async_copy(src.at[expert], dst.at[expert], load_sem.at[2 * expert + i])
            for i, (src, dst) in enumerate(((grad_up, up_out), (grad_down, down_out)))
        ]

    def arrive(j):
        for n in (2 * j, 2 * j + 1):
            dispatch.relay(n)
        for n in (2 * j, 2 * j + 1):
            dispatch.ready(n)

    def forward(j):
        dispatch.forward(2 * j)
        dispatch.forward(2 * j + 1)

    forward(0)
    forward(1)
    for load in loads:
        load.wait()

    def step(j):
        arrive(j)
        compute(j, 0)
        pl.when(j + 2 < chunks)(lambda: forward(j + 2))

        @pl.when(j >= 1)
        def _():
            ret_grad.cross(j - 1)
            either(
                j - 1 < early, lambda: ret_out.cross(j - 1), lambda: ret_out.split(j - 1)
            )

        pl.when(j >= 2)(lambda: ret_grad.finish(j - 2))

        for expert in range(1, experts):
            compute(j, expert)
        ret_grad.swap(j)
        ret_out.swap(j)

    ret_out.keep = keep_out
    every(0, chunks, step)
    weight_grads(0, 0, 1)
    ret_grad.cross(chunks - 1)
    ret_out.split(chunks - 1)
    sums = [
        pltpu.make_async_copy(src, dst, load_sem.at[4 + i])
        for i, (src, dst) in enumerate(((mid_out, far_sums), (keep_out, near_sums)))
    ]
    for store in sums:
        store.start()
    ret_grad.finish(chunks - 2)
    every(0, early, ret_out.finish)
    weight_grads(0, 1, 3)
    ret_grad.finish(chunks - 1)
    weight_grads(0, 3, 4)
    for store in keep(0):
        store.start()
    for expert in range(1, experts):
        weight_grads(expert, 0, 4)
        for store in keep(expert):
            store.start()
    for expert in range(experts):
        for store in keep(expert):
            store.wait()
    for store in sums:
        store.wait()
    dispatch.drain()
    ret_grad.drain_swaps(chunks)
    ret_grad.drain(0, chunks)
    ret_grad.arrived(0, chunks)
    ret_out.drain(0, early)
    ret_out.arrived(0, early)
    ret_out.drain_swaps(chunks)


def run_experts(owners, capacity, expert_count, send_rows, grads, w_up, w_down, router):
    experts, width, units = w_up.shape
    slots = owners * 4 * capacity
    chunks = owners // 2
    dims = (owners, experts, capacity, width, units, expert_count)
    any_spec = pl.BlockSpec(memory_space=pl.ANY)
    vmem_spec = pl.BlockSpec(memory_space=pltpu.VMEM)
    bf16 = jnp.bfloat16
    home = jax.ShapeDtypeStruct((owners, experts, capacity, width), bf16)
    dma = pltpu.SemaphoreType.DMA

    def vm(*shape):
        return pltpu.VMEM(shape, bf16)

    return pl.pallas_call(
        functools.partial(expert_kernel, dims),
        out_shape=(
            jax.ShapeDtypeStruct((experts, slots // 4, width), bf16),
            jax.ShapeDtypeStruct((experts, slots // 4, width), bf16),
            home, home,
            jax.ShapeDtypeStruct(w_up.shape, bf16),
            jax.ShapeDtypeStruct(w_down.shape, bf16),
            jax.ShapeDtypeStruct((LANES, width), jnp.float32),
        ),
        in_specs=[any_spec] * 4 + [vmem_spec],
        out_specs=(any_spec,) * 6 + (vmem_spec,),
        scratch_shapes=[
            vm(experts, slots, width),
            vm(experts, slots, width),
            vm(experts, slots, width),
            vm(experts, slots, units),
            vm(experts, slots, units),
            vm(experts, width, units),
            vm(experts, units, width),
            vm(experts, width, units),
            vm(experts, units, width),
            vm(experts, slots, width),
            vm(experts, slots, width),
            vm(experts, slots // 2, width),
            vm(experts, slots // 2, width),
            vm(experts, slots // 4, width),
            vm(experts, slots // 4, width),
            vm(experts, slots // 4, width),
            vm(experts, slots // 4, width),
            vm(experts, slots // 4, width),
            vm(owners, experts, capacity, width),
            vm(owners, experts, capacity, width),
            dma((6,)),
            dma((3,)),
            dma((4, owners)),
            dma((4, owners)),
            dma((2, 2, chunks)),
            dma((2, 2, chunks)),
            dma((2, owners)),
            dma((2, owners)),
        ],
        compiler_params=pltpu.CompilerParams(
            collective_id=1, has_side_effects=True, vmem_limit_bytes=VMEM_LIMIT
        ),
        name="experts",
    )(send_rows, grads, w_up, w_down, router)


def masked_softmax(scores):
    exponent = jnp.exp(scores - jnp.max(scores, axis=1, keepdims=True))
    return exponent * (1.0 / jnp.sum(exponent, axis=1, keepdims=True))


def attend_head(query, key, value, prefix_len):
    half = query.shape[0] // 2
    query = query * (1.0 / math.sqrt(HEAD_DIM))
    row = lax.broadcasted_iota(jnp.int32, (half, half), 0)
    col = lax.broadcasted_iota(jnp.int32, (half, half), 1)
    low = dot_nt(query[:half], key[:half])
    low = jnp.where((col <= row) | (col < prefix_len), low, -1e30)
    low = masked_softmax(low).astype(jnp.bfloat16)
    high = dot_nt(query[half:], key)
    high = jnp.concatenate(
        [high[:, :half], jnp.where(col <= row, high[:, half:], -1e30)], axis=1
    )
    high = masked_softmax(high).astype(jnp.bfloat16)
    return low, high, dot_nn(low, value[:half]), dot_nn(high, value)


def score_grads(probs, grad_probs):
    probs = probs.astype(jnp.float32)
    weighted = probs * grad_probs
    total = jnp.sum(weighted, axis=1, keepdims=True)
    return (weighted - probs * total).astype(jnp.bfloat16)


def attend_back_head(query, key, value, low, high, grad):
    half = query.shape[0] // 2
    scale = 1.0 / math.sqrt(HEAD_DIM)
    query = query * scale
    grad_low = score_grads(low, dot_nt(grad[:half], value[:half]))
    grad_high = score_grads(high, dot_nt(grad[half:], value))
    grad_query = jnp.concatenate(
        [dot_nn(grad_low, key[:half]), dot_nn(grad_high, key)], axis=0
    )
    value_all = dot_tn(high, grad[half:])
    key_all = dot_tn(grad_high, query[half:])
    grad_value = jnp.concatenate(
        [value_all[:half] + dot_tn(low, grad[:half]), value_all[half:]], axis=0
    )
    grad_key = jnp.concatenate(
        [key_all[:half] + dot_tn(grad_low, query[:half]), key_all[half:]], axis=0
    )
    return (
        (grad_query * scale).astype(jnp.bfloat16),
        grad_key.astype(jnp.bfloat16),
        grad_value.astype(jnp.bfloat16),
    )


class Gather:
    def __init__(self, place, pieces, parts, src, dst, sems):
        self.p, self.src, self.dst, self.pieces, self.parts = place, src, dst, pieces, parts
        self.send, self.recv = sems
        self.shard = src.shape[0]
        self.half = self.shard // 2
        self.width = src.shape[1] // parts
        self.step = self.width // pieces
        self.first = lax.rem(place.e, 2) * self.half
        self.second = self.half - self.first

    def cols(self, n, part):
        return span(part * self.width + n * self.step, self.step)

    def block(self, owner, start, size, n, part):
        rows = pl.ds(pl.multiple_of(owner * self.shard + start, self.half), size)
        return self.dst.at[rows, self.cols(n, part)]

    def move(self, which, n, part, src, dst, device):
        return remote(
            src, dst, self.send.at[which, n, part], self.recv.at[which, n, part], device
        )

    def own(self, n, part):
        return pltpu.make_async_copy(
            self.src.at[:, self.cols(n, part)],
            self.block(self.p.w, 0, self.shard, n, part),
            self.recv.at[5, n, part],
        )

    def near(self, n, part):
        return self.move(
            4, n, part, self.src.at[:, self.cols(n, part)],
            self.block(self.p.w, 0, self.shard, n, part), (self.p.e, self.p.sib),
        )

    def hop(self, n, part):
        return self.move(
            0, n, part, self.src.at[span(self.first, self.half), self.cols(n, part)],
            self.block(self.p.w, self.first, self.half, n, part), (self.p.e, self.p.far),
        )

    def pass_from(self, which, start, n, part, device):
        block = self.block(self.p.far, start, self.half, n, part)
        return self.move(which, n, part, block, block, device)

    def pairs(self, n, part):
        return self.pass_from(1, self.first, n, part, (self.p.pair, self.p.w))

    def relay(self, n, part):
        return self.pass_from(2, self.first, n, part, (self.p.e, self.p.sib))

    def pair_relay(self, n, part):
        return self.pass_from(3, self.second, n, part, (self.p.e, self.p.sib))

    def all_parts(self, n, act):
        for part in range(self.parts):
            act(n, part)

    def start_own(self):
        every(
            0, self.pieces, lambda n: self.all_parts(n, lambda n, part: self.own(n, part).start())
        )

    def start(self):
        def hop(n, part):
            self.hop(n, part).start()

        def near(n, part):
            self.near(n, part).start()

        every(0, self.pieces, lambda n: self.all_parts(n, hop))
        every(0, self.pieces, lambda n: self.all_parts(n, near))

    def pass_on(self, n):
        def one(n, part):
            self.hop(n, part).wait_recv()
            self.pairs(n, part).start()
            self.relay(n, part).start()

        self.all_parts(n, one)

    def pass_pair(self, n):
        def one(n, part):
            self.pairs(n, part).wait_recv()
            self.pair_relay(n, part).start()

        self.all_parts(n, one)

    def ready(self, n):
        def one(n, part):
            self.own(n, part).wait()
            for copy in (self.near(n, part), self.relay(n, part), self.pair_relay(n, part)):
                copy.wait_recv()

        self.all_parts(n, one)

    def drain(self):
        def one(n, part):
            for copy in (
                self.hop(n, part), self.pairs(n, part), self.relay(n, part),
                self.pair_relay(n, part), self.near(n, part),
            ):
                copy.wait_send()

        every(0, self.pieces, lambda n: self.all_parts(n, one))


def slot_tables(routes_ref, priority_ref, capacity, pick_ref, back_ref):
    count = routes_ref.shape[1]
    row = lax.broadcasted_iota(jnp.int32, (count, count), 0).astype(jnp.float32)
    col = lax.broadcasted_iota(jnp.int32, (count, count), 1).astype(jnp.float32)
    eye = row == col
    route_row = routes_ref[...].astype(jnp.float32)
    order_row = priority_ref[...].astype(jnp.float32)
    route_col = jnp.sum(jnp.where(eye, route_row, 0.0), axis=1, keepdims=True)
    order_col = jnp.sum(jnp.where(eye, order_row, 0.0), axis=1, keepdims=True)
    same = route_col == route_row
    rank_row = jnp.sum(
        jnp.where(same & (order_col < order_row), 1.0, 0.0), axis=0, keepdims=True
    )
    rank_col = jnp.sum(
        jnp.where(same & (order_row < order_col), 1.0, 0.0), axis=1, keepdims=True
    )
    slots = float(count)
    slot_row = jnp.where(rank_row < capacity, route_row * capacity + rank_row, slots)
    slot_col = jnp.where(rank_col < capacity, route_col * capacity + rank_col, slots)
    pick_ref[...] = jnp.where(slot_row == row, 1.0, 0.0).astype(jnp.bfloat16)
    back_ref[...] = jnp.where(slot_col == col, 1.0, 0.0).astype(jnp.bfloat16)


def norm_stats(value):
    centered = value - jnp.mean(value, axis=1, keepdims=True)
    inverse = lax.rsqrt(jnp.mean(centered * centered, axis=1, keepdims=True) + epsilon)
    return centered * inverse, inverse


def front_kernel(
    dims,
    prefix_ref, routes_ref, priority_ref, tokens_ref, cot_ref, small_hbm, router_hbm, qkv_hbm, out_hbm,
    qkv_out, act_out, merged_out, back_out, weight_out, out_full, low_out, high_out, grads_rows,
    hidden_ref, send_ref, small_out, router_out,
    small, weight, out_w, qkv, act, merged, act_two, turned, pick, back, grads_send, low_buf, high_buf,
    own_sem, disp_send, disp_recv, small_send, small_recv, gat_send, gat_recv, store_sem, prob_sem,
):
    owners, capacity, pieces = dims
    place = Place(owners)
    rows, width = tokens_ref.shape
    shard = qkv_hbm.shape[0]
    gathers = [
        Gather(place, pieces, parts, src, dst, (gat_send.at[i], gat_recv.at[i]))
        for i, (parts, src, dst) in enumerate(((3, qkv_hbm, weight), (1, out_hbm, out_w)))
    ]
    for gather in gathers:
        gather.start_own()
    vectors, gates = small_hbm.shape[0], router_hbm.shape[0]
    small_parts = [
        (small_hbm, small.at[place.w, pl.ds(0, vectors)]),
        (router_hbm, small.at[place.w, pl.ds(vectors, gates)]),
    ]
    own_smalls = [
        pltpu.make_async_copy(src, dst, own_sem.at[3 + i])
        for i, (src, dst) in enumerate(small_parts)
    ]
    for copy in own_smalls:
        copy.start()
    greet(
        [(place.ahead(k), place.w) for k in range(1, owners)]
        + [(place.e, place.sib), (place.e, place.far), (place.e, place.diag)]
    )
    smalls = [
        remote(src, dst, small_send.at[n, i], small_recv.at[n, i], (place.e, peer))
        for i, peer in enumerate((place.sib, place.far, place.diag))
        for n, (src, dst) in enumerate(small_parts)
    ]
    for copy in smalls:
        copy.start()
    for gather in gathers:
        gather.start()
    slot_tables(routes_ref, priority_ref, capacity, pick, back)
    tile = min(256, width)
    shape = grads_send.shape[:3]

    def to_slots(values_ref, slots_ref):
        def one(n):
            cols = span(n * tile, tile)
            value = dot_nn(pick[...], values_ref[:, cols]).astype(jnp.bfloat16)
            slots_ref[:, :, :, cols] = value.reshape(shape + (tile,))

        every(0, width // tile, one)

    to_slots(cot_ref, grads_send)
    dispatch = Dispatch(
        place, capacity, grads_send, grads_rows, (own_sem.at[0], disp_send, disp_recv)
    )
    dispatch.start()
    for copy in own_smalls:
        copy.wait()
    for copy in smalls:
        copy.wait_recv()
    small_out[...] = small[:, :vectors, :]
    router_out[...] = jnp.zeros_like(router_out)
    router_out[:gates, :] = jnp.concatenate(
        [small[i, vectors:, :] for i in range(4)], axis=1
    )

    def vector(which):
        parts = [small[i, which : which + 1, :] for i in range(4)]
        return jnp.concatenate(parts, axis=1).astype(jnp.float32)

    band = min(64, rows)
    gain, shift = vector(0), vector(1)

    def norm_band(i):
        part = span(i * band, band)
        scaled, _ = norm_stats(tokens_ref[part, :].astype(jnp.float32))
        act[part, :] = (scaled * gain + shift).astype(jnp.bfloat16)

    def project(n):
        for part in range(3):
            cols = gathers[0].cols(n, part)
            qkv[:, cols] = dot_nn(act[...], weight[:, cols]).astype(jnp.bfloat16)

    gathers[0].pass_on(0)
    every(0, rows // band, norm_band)
    turned[0] = act[...].T
    stores = [
        pltpu.make_async_copy(src, dst, store_sem.at[i])
        for i, (src, dst) in enumerate(
            [(qkv, qkv_out), (turned.at[0], act_out), (back, back_out), (weight, weight_out),
             (turned.at[1], merged_out), (out_w, out_full)]
        )
    ]
    for store in stores[1:3]:
        store.start()
    half = rows // 2
    pairs = width // LANES

    def keep_probs(i):
        slot = lax.rem(i, 2)
        return (
            pltpu.make_async_copy(
                low_buf.at[slot], low_out.at[pl.ds(2 * i, 2)], prob_sem.at[0, slot]
            ),
            pltpu.make_async_copy(
                high_buf.at[slot], high_out.at[pl.ds(2 * i, 2)], prob_sem.at[1, slot]
            ),
        )

    def attend_pair(i):
        slot = lax.rem(i, 2)

        @pl.when(i >= 2)
        def _():
            for copy in keep_probs(i - 2):
                copy.wait()

        query, key, value = (
            qkv[:, span(part * width + i * LANES, LANES)] for part in range(3)
        )
        tops, bottoms = [], []
        for head in range(2):
            part = slice(head * HEAD_DIM, (head + 1) * HEAD_DIM)
            low, high, top, bottom = attend_head(
                query[:, part], key[:, part], value[:, part], prefix_ref[0]
            )
            low_buf[slot, head] = low
            high_buf[slot, head] = high
            tops.append(top)
            bottoms.append(bottom)
        cols = span(i * LANES, LANES)
        merged[:half, cols] = jnp.concatenate(tops, axis=1).astype(jnp.bfloat16)
        merged[half:, cols] = jnp.concatenate(bottoms, axis=1).astype(jnp.bfloat16)
        for copy in keep_probs(i):
            copy.start()

    group = pairs // pieces
    share = -(-owners // pieces)

    def front_step(n):
        @pl.when(n + 1 < pieces)
        def _():
            gathers[0].pass_on(n + 1)

        gathers[0].pass_pair(n)
        for i in range(share):
            pl.when(n * share + i < owners)(lambda: dispatch.forward(n * share + i))
        gathers[0].ready(n)
        project(n)
        for i in range(group):
            attend_pair(n * group + i)

    every(0, pieces, front_step)
    turned[1] = merged[...].T
    for i in (0, 3, 4):
        stores[i].start()
    every(0, pieces, gathers[1].pass_on)
    every(0, pieces, gathers[1].pass_pair)
    dispatch.relay(0)
    every(0, pieces, gathers[1].ready)
    stores[5].start()
    gain_two, shift_two = vector(2), vector(3)
    band_two = min(128, rows)

    def middle(i):
        part = span(i * band_two, band_two)
        value = tokens_ref[part, :].astype(jnp.float32) + dot_nn(merged[part, :], out_w[...])
        hidden_ref[part, :] = value
        scaled, _ = norm_stats(value)
        act_two[part, :] = (scaled * gain_two + shift_two).astype(jnp.bfloat16)
        pl.when(i + 1 < owners)(lambda: dispatch.relay(i + 1))

    every(0, rows // band_two, middle)
    to_slots(act_two, send_ref)
    every(1 + min(rows // band_two, owners - 1), owners, dispatch.relay)
    for i in (pairs - 2, pairs - 1):
        for copy in keep_probs(i):
            copy.wait()
    every(0, owners, dispatch.ready)
    for store in stores:
        store.wait()
    for copy in smalls:
        copy.wait_send()
    for gather in gathers:
        gather.drain()
    dispatch.drain()


def run_front(
    owners, experts, capacity, prefix, routes, priority, tokens, cotangent, small, router, w_qkv, w_out
):
    rows, width = tokens.shape
    shard, columns = w_qkv.shape
    half = rows // 2
    heads = width // HEAD_DIM
    pieces = 4
    any_spec = pl.BlockSpec(memory_space=pl.ANY)
    vmem_spec = pl.BlockSpec(memory_space=pltpu.VMEM)
    bf16, f32 = jnp.bfloat16, jnp.float32
    dma = pltpu.SemaphoreType.DMA

    def out(*shape):
        return jax.ShapeDtypeStruct(shape, bf16)

    def vm(*shape):
        return pltpu.VMEM(shape, bf16)

    return pl.pallas_call(
        functools.partial(front_kernel, (owners, capacity, pieces)),
        out_shape=(
            out(rows, columns),
            out(width, rows),
            out(width, rows),
            out(rows, rows),
            out(4 * shard, columns),
            out(4 * shard, width),
            out(heads, half, half),
            out(heads, half, rows),
            out(experts, owners * 4 * capacity, width),
            jax.ShapeDtypeStruct((rows, width), f32),
            out(owners, experts, capacity, width),
            out(4, *small.shape),
            out(LANES, width),
        ),
        in_specs=[pl.BlockSpec(memory_space=pltpu.SMEM)] + [vmem_spec] * 4 + [any_spec] * 4,
        out_specs=(any_spec,) * 9 + (vmem_spec,) * 4,
        scratch_shapes=[
            vm(4, small.shape[0] + router.shape[0], shard),
            vm(4 * shard, columns),
            vm(4 * shard, width),
            vm(rows, columns),
            vm(rows, width),
            vm(rows, width),
            vm(rows, width),
            vm(2, width, rows),
            vm(rows, rows),
            vm(rows, rows),
            vm(owners, experts, capacity, width),
            vm(2, 2, half, half),
            vm(2, 2, half, rows),
            dma((5,)),
            dma((4, owners)),
            dma((4, owners)),
            dma((2, 3)),
            dma((2, 3)),
            dma((2, 6, pieces, 3)),
            dma((2, 6, pieces, 3)),
            dma((6,)),
            dma((2, 2)),
        ],
        compiler_params=pltpu.CompilerParams(
            collective_id=0, has_side_effects=True, vmem_limit_bytes=VMEM_LIMIT
        ),
        name="front",
    )(prefix, routes, priority, tokens, cotangent, small, router, w_qkv, w_out)


class Reduce:
    def __init__(self, place, part, got, far, pair, lines, done, sems):
        self.p = place
        self.part, self.got, self.far = part, got, far
        self.pair, self.lines, self.done = pair, lines, done
        self.send, self.recv, self.line_send, self.line_recv = sems
        self.chunks = part.shape[0]
        self.halves = done.shape[1] // 2
        self.count = place.owners // 2
        self.slice = self.halves // self.count
        self.bit = lax.rem(place.e, 2)
        self.level = lax.div(place.e, 2)

    def step(self, which, n, src, dst, device):
        return remote(src, dst, self.send.at[which, n], self.recv.at[which, n], device)

    def swapped(self, n):
        return self.step(
            0, n, self.part.at[n, :, 1 - self.p.c], self.got.at[n], (self.p.e, self.p.sib)
        )

    def crossed(self, n):
        return self.step(
            1, n, self.part.at[n, 1 - self.p.x, self.p.c], self.far.at[n], (self.p.e, self.p.far)
        )

    def folded(self, n):
        other = span((1 - self.bit) * self.halves, self.halves)
        return self.step(
            2, n, self.part.at[n, self.p.x, self.p.c, other], self.pair.at[n],
            (self.p.pair, self.p.w),
        )

    def shared(self, n):
        part = self.done.at[n, span(self.bit * self.halves, self.halves)]
        return self.step(3, n, part, part, (self.p.pair, self.p.w))

    def line(self, which, n, k, src, dst):
        return remote(
            src, dst, self.line_send.at[which, n, k], self.line_recv.at[which, n, k],
            (self.p.ahead(2 * k), self.p.w),
        )

    def row(self, level):
        return span(self.bit * self.halves + level * self.slice, self.slice)

    def spreads(self, n, k):
        target = lax.rem(self.level + k, self.count)
        return self.line(
            0, n, k, self.part.at[n, self.p.x, self.p.c, self.row(target)], self.lines.at[n, k]
        )

    def collects(self, n, k):
        part = self.done.at[n, self.row(self.level)]
        return self.line(1, n, k, part, part)

    def pair_sum(self, n, side):
        return self.part[n, side, self.p.c].astype(jnp.float32) + self.got[n, side].astype(
            jnp.float32
        )

    def swap(self, n):
        self.swapped(n).start()

    def cross(self, n):
        self.swapped(n).wait_recv()
        side = 1 - self.p.x
        self.part[n, side, self.p.c] = self.pair_sum(n, side).astype(jnp.bfloat16)
        self.crossed(n).start()

    def fold(self, n):
        self.crossed(n).wait_recv()
        total = self.pair_sum(n, self.p.x) + self.far[n].astype(jnp.float32)
        self.part[n, self.p.x, self.p.c] = total.astype(jnp.bfloat16)
        self.folded(n).start()

    def spread(self, n):
        self.folded(n).wait_recv()
        own = span(self.bit * self.halves, self.halves)
        total = self.part[n, self.p.x, self.p.c, own, :].astype(jnp.float32) + self.pair[
            n
        ].astype(jnp.float32)
        self.part[n, self.p.x, self.p.c, own, :] = total.astype(jnp.bfloat16)
        for k in range(1, self.count):
            self.spreads(n, k).start()

    def collect(self, n):
        total = self.part[n, self.p.x, self.p.c, self.row(self.level), :].astype(jnp.float32)
        for k in range(1, self.count):
            self.spreads(n, k).wait_recv()
            total = total + self.lines[n, k].astype(jnp.float32)
        self.done[n, self.row(self.level), :] = total.astype(jnp.bfloat16)
        for k in range(1, self.count):
            self.collects(n, k).start()

    def share(self, n):
        for k in range(1, self.count):
            self.collects(n, k).wait_recv()
        self.shared(n).start()

    def finish(self, n):
        self.shared(n).wait_recv()

    def stages(self):
        return (self.cross, self.fold, self.spread, self.collect, self.share, self.finish)

    def drain(self):
        def one(n):
            for copy in (self.swapped(n), self.crossed(n), self.folded(n), self.shared(n)):
                copy.wait_send()
            for k in range(1, self.count):
                self.spreads(n, k).wait_send()
                self.collects(n, k).wait_send()

        every(0, self.chunks, one)


class Small:
    def __init__(self, place, value, part, got, mid, far, total, others, out, sems):
        self.p, self.value, self.part, self.got, self.mid = place, value, part, got, mid
        self.far, self.total, self.others, self.out = far, total, others, out
        self.send, self.recv, self.all_send, self.all_recv = sems

    def swapped(self):
        return remote(
            self.part.at[:, 1 - self.p.c], self.got, self.send.at[0], self.recv.at[0],
            (self.p.e, self.p.sib),
        )

    def crossed(self):
        return remote(
            self.mid, self.far, self.send.at[1], self.recv.at[1], (self.p.e, self.p.far)
        )

    def spreads(self, k):
        return remote(
            self.total, self.others.at[k], self.all_send.at[k], self.all_recv.at[k],
            (self.p.ahead(k), self.p.w),
        )

    def swap(self):
        size = self.part.shape[-1]
        for owner in range(4):
            self.part[owner // 2, owner % 2] = self.value[:, owner * size : (owner + 1) * size]
        self.swapped().start()

    def cross(self):
        self.swapped().wait_recv()
        self.mid[...] = self.part[1 - self.p.x, self.p.c] + self.got[1 - self.p.x]
        self.crossed().start()

    def spread(self):
        self.crossed().wait_recv()
        self.total[...] = self.part[self.p.x, self.p.c] + self.got[self.p.x] + self.far[...]
        for k in range(1, self.p.owners):
            self.spreads(k).start()

    def finish(self):
        total = self.total[...]
        for k in range(1, self.p.owners):
            self.spreads(k).wait_recv()
            total = total + self.others[k]
        vectors_out, gates_out = self.out
        vectors_out[...] = total[: vectors_out.shape[0]]
        gates_out[...] = total[vectors_out.shape[0] :]

    def drain(self):
        self.swapped().wait_send()
        self.crossed().wait_send()
        for k in range(1, self.p.owners):
            self.spreads(k).wait_send()


def norm_back_rows(grad, scaled, inverse, gain):
    weighted = grad * gain
    mean_one = jnp.mean(weighted, axis=1, keepdims=True)
    mean_two = jnp.mean(weighted * scaled, axis=1, keepdims=True)
    return inverse * (weighted - mean_one - scaled * mean_two)


def back_kernel(
    dims,
    home_grad_ref, back_ref, hidden_ref, cot_ref, tokens_ref, vectors_ref, router_ref,
    far_hbm, near_hbm, home_hbm, act_hbm, merged_hbm, qkv_hbm, weight_hbm, out_hbm, low_hbm, high_hbm,
    output_ref, tokens_out, vectors_out, gates_out, qkv_out, out_out,
    near_sums, far_sums, done_rows, home_out,
    act_t, merged_t, qkv, weight, out_w, low_buf, high_buf, attn, grad_merged, wide_q, wide_o,
    part_q, got_q, far_q, pair_q, lines_q, done_q,
    part_o, got_o, far_o, pair_o, lines_o, done_o,
    small, small_part, small_got, small_mid, small_far, small_sum, small_all,
    load_sem, prob_sem, own_sem, early_sem, cross_send, cross_recv, home_send, home_recv, send_q, recv_q, lsend_q, lrecv_q, send_o, recv_o, lsend_o, lrecv_o,
    small_send, small_recv, all_send, all_recv, out_sem,
):
    owners, capacity, gates = dims
    grad_qkv = qkv
    place = Place(owners)
    loads = [
        pltpu.make_async_copy(src, dst, load_sem.at[i])
        for i, (src, dst) in enumerate(
            [(merged_hbm, merged_t), (out_hbm, out_w), (qkv_hbm, qkv), (act_hbm, act_t),
             (weight_hbm, weight), (near_hbm, near_sums)]
        )
    ]

    def load_probs(i):
        slot = lax.rem(i, 2)
        return (
            pltpu.make_async_copy(
                low_hbm.at[pl.ds(2 * i, 2)], low_buf.at[slot], prob_sem.at[0, slot]
            ),
            pltpu.make_async_copy(
                high_hbm.at[pl.ds(2 * i, 2)], high_buf.at[slot], prob_sem.at[1, slot]
            ),
        )

    for load in loads:
        load.start()
    for load in load_probs(0):
        load.start()
    greet(
        [(place.ahead(k), place.w) for k in range(1, owners)]
        + [(place.e, place.sib), (place.e, place.far)]
    )
    experts = near_sums.shape[0]
    groups = owners // 2
    late = LateReturn(
        place, capacity, experts, near_sums, None, far_hbm, far_sums, done_rows, home_out,
        (own_sem, cross_send, cross_recv, home_send, home_recv),
    )
    every(EARLY_CHUNKS, groups, lambda j: late.crossed(j).start())

    def early_rows(n):
        row = place.peer(n)
        return pltpu.make_async_copy(home_hbm.at[row], home_out.at[row], early_sem.at[n])

    every(0, 2 * EARLY_CHUNKS, lambda n: early_rows(n).start())
    reduce_o = Reduce(
        place, part_o, got_o, far_o, pair_o, lines_o, done_o, (send_o, recv_o, lsend_o, lrecv_o)
    )
    reduce_q = Reduce(
        place, part_q, got_q, far_q, pair_q, lines_q, done_q, (send_q, recv_q, lsend_q, lrecv_q)
    )
    smalls = Small(
        place, small, small_part, small_got, small_mid, small_far, small_sum, small_all, (vectors_out, gates_out),
        (small_send, small_recv, all_send, all_recv),
    )
    rows, width = tokens_ref.shape
    shard = width // 4
    band = min(128, rows)
    lead = small.shape[0]

    def vector(which):
        parts = [vectors_ref[i, which : which + 1, :] for i in range(4)]
        return jnp.concatenate(parts, axis=1).astype(jnp.float32)

    gain_one, gain_two = vector(0), vector(2)
    small[: lead - gates, :] = jnp.zeros((lead - gates, width), jnp.float32)
    small[lead - gates :, :] = router_ref[:gates, :]

    def post(i):
        part = span(i * band, band)
        grad = dot_nn(back_ref[part, :], home_grad_ref.reshape(rows, width)[...])
        scaled, inverse = norm_stats(hidden_ref[part, :])
        value = cot_ref[part, :].astype(jnp.float32) + norm_back_rows(
            grad, scaled, inverse, gain_two
        )
        tokens_out[part, :] = value
        attn[part, :] = value.astype(jnp.bfloat16)
        small[2:3, :] += jnp.sum(grad * scaled, axis=0, keepdims=True)
        small[3:4, :] += jnp.sum(grad, axis=0, keepdims=True)

    every(0, rows // band, post)
    loads[0].wait()

    def weight_grad(part, n, left, right):
        def one(owner):
            value = dot_nn(left[span(owner * shard, shard), :], right)
            part[n, lax.div(owner, 2), lax.rem(owner, 2)] = value.astype(jnp.bfloat16)

        every(0, 4, one)

    tile_o = part_o.shape[-1]
    out_chunks = part_o.shape[0]
    for n in range(out_chunks):
        weight_grad(part_o, n, merged_t, attn[:, n * tile_o : (n + 1) * tile_o])
        reduce_o.swap(n)
    loads[1].wait()

    def merged_band(i):
        part = span(i * band, band)
        grad_merged[part, :] = dot_nt(attn[part, :], out_w[...]).astype(jnp.bfloat16)

    every(0, rows // band, merged_band)
    for load in loads[2:4] + loads[5:]:
        load.wait()
    pairs = part_q.shape[0]

    def attend_pair(i):
        slot = lax.rem(i, 2)
        for load in load_probs(i):
            load.wait()

        @pl.when(i + 1 < pairs)
        def _():
            for load in load_probs(i + 1):
                load.start()

        cols = span(i * LANES, LANES)
        query, key, value = (
            qkv[:, span(part * width + i * LANES, LANES)] for part in range(3)
        )
        grad = grad_merged[:, cols]
        results = []
        for head in range(2):
            part = slice(head * HEAD_DIM, (head + 1) * HEAD_DIM)
            results.append(
                attend_back_head(
                    query[:, part], key[:, part], value[:, part],
                    low_buf[slot, head], high_buf[slot, head], grad[:, part],
                )
            )
        for which in range(3):
            grad_qkv[:, span(which * width + i * LANES, LANES)] = jnp.concatenate(
                [results[0][which], results[1][which]], axis=1
            )
        right = jnp.concatenate(
            [grad_qkv[:, span(which * width + i * LANES, LANES)] for which in range(3)], axis=1
        )
        weight_grad(part_q, i, act_t, right)
        reduce_q.swap(i)

    def input_band(i):
        part = span(i * band, band)
        grad = dot_nt(grad_qkv[part, :], weight[...])
        scaled, inverse = norm_stats(tokens_ref[part, :].astype(jnp.float32))
        tokens_out[part, :] += norm_back_rows(grad, scaled, inverse, gain_one)
        small[0:1, :] += jnp.sum(grad * scaled, axis=0, keepdims=True)
        small[1:2, :] += jnp.sum(grad, axis=0, keepdims=True)

    def output_band(i):
        part = span(i * band, band)
        slots = home_out.reshape(rows, width)
        value = hidden_ref[part, :] + dot_nn(back_ref[part, :], slots[...])
        output_ref[part, :] = value.astype(jnp.bfloat16)

    def store_q(i):
        return [
            pltpu.make_async_copy(
                wide_q.at[i, :, pl.ds(which * LANES, LANES)],
                qkv_out.at[:, span(which * width + i * LANES, LANES)],
                out_sem.at[which, i],
            )
            for which in range(3)
        ]

    def store_o(n):
        return pltpu.make_async_copy(
            wide_o.at[n], out_out.at[:, span(n * tile_o, tile_o)], out_sem.at[3, n]
        )

    stages_o, stages_q = reduce_o.stages(), reduce_q.stages()
    delays = (1, 3, 4, 5, 6, 7)
    last = len(delays) - 1
    half = rows // band // 2

    def slot_step(slot):
        pl.when(slot + EARLY_CHUNKS < groups)(lambda: late.finish(slot + EARLY_CHUNKS))
        pl.when(slot < pairs)(lambda: attend_pair(slot))
        for s in range(last, -1, -1):
            n = slot - delays[s]

            @pl.when((n >= 0) & (n < pairs))
            def _(s=s, n=n):
                stages_q[s](n)
                if s == last:
                    wide_q[n] = done_q[n].astype(jnp.float32)
                    for copy in store_q(n):
                        copy.start()

            @pl.when(slot == delays[s] - 1)
            def _(s=s):
                for n in range(out_chunks):
                    stages_o[s](n)
                    if s == last:
                        wide_o[n] = done_o[n].astype(jnp.float32)
                        store_o(n).start()

        @pl.when(slot == pairs)
        def _():
            loads[4].wait()
            every(0, half, input_band)

        pl.when(slot == pairs + 1)(lambda: every(half, 2 * half, input_band))
        pl.when(slot == pairs + 2)(smalls.swap)
        pl.when(slot == pairs + 3)(smalls.cross)
        pl.when(slot == pairs + 4)(smalls.spread)

        @pl.when(slot == pairs + 3)
        def _():
            late.arrived(EARLY_CHUNKS, groups)
            every(0, 2 * EARLY_CHUNKS, lambda n: early_rows(n).wait())
            every(0, rows // band, output_band)

    every(0, pairs + delays[-1], slot_step)
    smalls.finish()

    def stored(i):
        for copy in store_q(i):
            copy.wait()

    every(0, pairs, stored)
    for n in range(out_chunks):
        store_o(n).wait()
    late.drain(EARLY_CHUNKS, groups)
    reduce_o.drain()
    reduce_q.drain()
    smalls.drain()


def run_back(
    owners, capacity, gates, home_grad, far_sums, near_sums, home_out, back, hidden, cotangent, tokens,
    vectors, router_grad, act_t, merged_t, qkv, weight, w_out, low, high,
):
    rows, width = tokens.shape
    shard = width // 4
    lead = 8 + gates
    groups = owners // 2
    pairs = width // LANES
    tile_o = min(512, width)
    out_chunks = width // tile_o
    count = owners // 2
    half = shard // 2
    mid = rows // 2
    any_spec = pl.BlockSpec(memory_space=pl.ANY)
    vmem_spec = pl.BlockSpec(memory_space=pltpu.VMEM)
    bf16, f32 = jnp.bfloat16, jnp.float32
    dma = pltpu.SemaphoreType.DMA

    def vm(*shape):
        return pltpu.VMEM(shape, bf16)

    def fm(*shape):
        return pltpu.VMEM(shape, f32)

    def reduce_buffers(chunks, tile):
        return [
            vm(chunks, 2, 2, shard, tile),
            vm(chunks, 2, shard, tile),
            vm(chunks, shard, tile),
            vm(chunks, half, tile),
            vm(chunks, count, half // count, tile),
            vm(chunks, shard, tile),
        ]

    def reduce_sems(chunks):
        return [dma((4, chunks)), dma((4, chunks)), dma((2, chunks, count)), dma((2, chunks, count))]

    return pl.pallas_call(
        functools.partial(back_kernel, (owners, capacity, gates)),
        out_shape=(
            jax.ShapeDtypeStruct((rows, width), bf16),
            jax.ShapeDtypeStruct((rows, width), f32),
            jax.ShapeDtypeStruct((8, shard), f32),
            jax.ShapeDtypeStruct((gates, shard), f32),
            jax.ShapeDtypeStruct((shard, 3 * width), f32),
            jax.ShapeDtypeStruct((shard, width), f32),
        ),
        in_specs=[vmem_spec] * 7 + [any_spec] * 10,
        out_specs=(vmem_spec,) * 4 + (any_spec,) * 2,
        scratch_shapes=[
            vm(*near_sums.shape),
            vm(*near_sums.shape),
            vm(*home_grad.shape),
            vm(*home_grad.shape),
            vm(width, rows),
            vm(width, rows),
            vm(rows, 3 * width),
            vm(width, 3 * width),
            vm(width, width),
            vm(2, 2, mid, mid),
            vm(2, 2, mid, rows),
            vm(rows, width),
            vm(rows, width),
            fm(pairs, shard, 3 * LANES),
            fm(out_chunks, shard, tile_o),
        ]
        + reduce_buffers(pairs, 3 * LANES)
        + reduce_buffers(out_chunks, tile_o)
        + [
            fm(lead, width),
            fm(2, 2, lead, shard),
            fm(2, lead, shard),
            fm(lead, shard),
            fm(lead, shard),
            fm(lead, shard),
            fm(owners, lead, shard),
            dma((6,)),
            dma((2, 2)),
            dma(()),
            dma((owners,)),
            dma((groups,)),
            dma((groups,)),
            dma((owners,)),
            dma((owners,)),
        ]
        + reduce_sems(pairs)
        + reduce_sems(out_chunks)
        + [dma((2,)), dma((2,)), dma((owners,)), dma((owners,)), dma((4, pairs))],
        compiler_params=pltpu.CompilerParams(
            collective_id=2, has_side_effects=True, vmem_limit_bytes=VMEM_LIMIT
        ),
        name="back",
    )(
        home_grad, back, hidden, cotangent, tokens, vectors, router_grad,
        far_sums, near_sums, home_out, act_t, merged_t, qkv, weight, w_out, low, high,
    )


def on_device_plain(
    tokens,
    norm1_gain,
    norm1_shift,
    w_qkv,
    w_out,
    norm2_gain,
    norm2_shift,
    w_router,
    w_up,
    w_down,
    routes,
    priority,
    prefix,
    cotangent,
):
    row_count, model_width = tokens.shape
    expert_count = w_router.shape[1]
    capacity = row_count // expert_count
    owners = lax.axis_size("expert")
    local_experts = w_up.shape[0]
    slot_count = expert_count * capacity
    prefix_len = prefix[0]
    small = jnp.concatenate(
        [
            norm1_gain[None],
            norm1_shift[None],
            norm2_gain[None],
            norm2_shift[None],
            w_router.T,
        ],
        axis=0,
    )
    qkv_full = lax.all_gather(w_qkv, "wshard", axis=0, tiled=True)
    small_full = lax.all_gather(small, "wshard", axis=1, tiled=True)
    out_full = lax.all_gather(w_out, "wshard", axis=0, tiled=True)
    gain_one, shift_one, gain_two, shift_two = (small_full[i] for i in range(4))
    router_full = small_full[4:].T
    gain_one = gain_one.astype(jnp.float32)
    gain_two = gain_two.astype(jnp.float32)
    inputs = tokens.astype(jnp.float32)
    normed_one, scaled_one, inverse_one = normalize(inputs, gain_one, shift_one.astype(jnp.float32))
    act_one = normed_one.astype(jnp.bfloat16)
    qkv = jnp.dot(act_one, qkv_full, preferred_element_type=jnp.float32).astype(jnp.bfloat16)
    query_heads = qkv[:, :model_width]
    key_heads = qkv[:, model_width : 2 * model_width]
    value_heads = qkv[:, 2 * model_width :]
    merged, log_totals = attend_forward(query_heads, key_heads, value_heads, prefix_len)
    attn_out = jnp.dot(merged, out_full, preferred_element_type=jnp.float32)
    hidden = inputs + attn_out
    normed_two, scaled_two, inverse_two = normalize(hidden, gain_two, shift_two.astype(jnp.float32))
    act_two = normed_two.astype(jnp.bfloat16)
    logits = jnp.dot(act_two, router_full, preferred_element_type=jnp.float32)
    row_max = jnp.max(logits, axis=-1, keepdims=True)
    exponent = jnp.exp(logits - row_max)
    gate_prob = exponent / jnp.sum(exponent, axis=-1, keepdims=True)
    route_ids = routes[:, 0]
    chosen = route_ids[:, None] == jnp.arange(expert_count, dtype=jnp.int32)[None, :]
    gate_value = jnp.sum(jnp.where(chosen, gate_prob, 0.0), axis=1)
    slot_index, slot_source = assign_slots(route_ids, priority[0], expert_count, capacity)
    zero_row = jnp.zeros((1, model_width), jnp.bfloat16)
    padded = jnp.concatenate([act_two, zero_row], axis=0)
    send_rows = padded[slot_source].reshape(owners, local_experts * capacity, model_width)
    arrived = lax.all_to_all(send_rows, "expert", split_axis=0, concat_axis=0, tiled=True).reshape(
        owners, local_experts, capacity, model_width
    )
    group = lax.axis_size("wshard")
    local_rows = owners * capacity

    def by_expert(chunk):
        rows = jnp.transpose(chunk, (1, 0, 2, 3)).reshape(local_experts, local_rows, model_width)
        return lax.all_gather(rows, "wshard", axis=1, tiled=True)

    def home_rows(rows):
        own = lax.psum_scatter(rows.astype(jnp.bfloat16), "wshard", scatter_dimension=1, tiled=True)
        own = own.reshape(local_experts, owners, capacity, model_width)
        return jnp.transpose(own, (1, 0, 2, 3)).reshape(
            owners, local_experts * capacity, model_width
        )

    grad_output = cotangent.astype(jnp.float32)
    grad_combined = (gate_value[:, None] * grad_output).astype(jnp.bfloat16)
    grad_padded = jnp.concatenate([grad_combined, zero_row], axis=0)
    grad_send = grad_padded[slot_source].reshape(owners, local_experts * capacity, model_width)
    grad_arrived = lax.all_to_all(
        grad_send, "expert", split_axis=0, concat_axis=0, tiled=True
    ).reshape(owners, local_experts, capacity, model_width)
    rows_in = by_expert(arrived)
    grad_rows = by_expert(grad_arrived)
    pre_act = jnp.einsum("erd,edf->erf", rows_in, w_up, preferred_element_type=jnp.float32)
    activated, gelu_pull = jax.vjp(gelu_tanh, pre_act)
    act_hidden = activated.astype(jnp.bfloat16)
    produced = jnp.einsum(
        "erf,efd->erd", act_hidden, w_down, preferred_element_type=jnp.float32
    )
    expert_out = home_rows(produced)
    returned = lax.all_to_all(expert_out, "expert", split_axis=0, concat_axis=0, tiled=True)
    slots_back = jnp.concatenate([returned.reshape(slot_count, model_width), zero_row], axis=0)
    combined = slots_back[slot_index].astype(jnp.float32)
    output = (hidden + gate_value[:, None] * combined).astype(jnp.bfloat16)
    grad_gate = jnp.sum(grad_output * combined, axis=1)
    grad_down = jnp.einsum(
        "erf,erd->efd", act_hidden, grad_rows, preferred_element_type=jnp.float32
    )
    grad_hidden_units = jnp.einsum(
        "erd,efd->erf", grad_rows, w_down, preferred_element_type=jnp.float32
    )
    grad_pre = gelu_pull(grad_hidden_units)[0].astype(jnp.bfloat16)
    grad_up = jnp.einsum("erd,erf->edf", rows_in, grad_pre, preferred_element_type=jnp.float32)
    grad_expert_in = jnp.einsum(
        "erf,edf->erd", grad_pre, w_up, preferred_element_type=jnp.float32
    )
    grad_send_back = home_rows(grad_expert_in)
    grad_back = lax.all_to_all(grad_send_back, "expert", split_axis=0, concat_axis=0, tiled=True)
    grad_slots = jnp.concatenate([grad_back.reshape(slot_count, model_width), zero_row], axis=0)
    grad_act_two = grad_slots[slot_index].astype(jnp.float32)
    grad_logits = (
        gate_prob * (jnp.where(chosen, grad_gate[:, None], 0.0) - (gate_value * grad_gate)[:, None])
    ).astype(jnp.bfloat16)
    grad_router = contract_rows(act_two, grad_logits)
    grad_act_two = grad_act_two + times_transpose(grad_logits, router_full)
    grad_from_two, grad_gain_two, grad_shift_two = norm_back(
        grad_act_two, scaled_two, inverse_two, gain_two
    )
    grad_hidden = grad_output + grad_from_two
    grad_attn = grad_hidden.astype(jnp.bfloat16)
    grad_out_w = contract_rows(merged, grad_attn)
    grad_merged = times_transpose(grad_attn, out_full).astype(jnp.bfloat16)
    grad_qkv = attend_backward(
        query_heads, key_heads, value_heads, grad_merged, log_totals, prefix_len
    )
    grad_qkv_w = contract_rows(act_one, grad_qkv)
    grad_act_one = times_transpose(grad_qkv, qkv_full)
    grad_from_one, grad_gain_one, grad_shift_one = norm_back(
        grad_act_one, scaled_one, inverse_one, gain_one
    )
    grad_tokens = grad_hidden + grad_from_one
    small_grad = jnp.concatenate(
        [
            grad_gain_one[None],
            grad_shift_one[None],
            grad_gain_two[None],
            grad_shift_two[None],
            grad_router.T,
        ],
        axis=0,
    )
    out_share = lax.psum_scatter(
        grad_out_w.astype(jnp.bfloat16), "wshard", scatter_dimension=0, tiled=True
    )
    qkv_share = lax.psum_scatter(
        grad_qkv_w.astype(jnp.bfloat16), "wshard", scatter_dimension=0, tiled=True
    )
    small_share = lax.psum_scatter(small_grad, "wshard", scatter_dimension=1, tiled=True)
    out_total = lax.psum(out_share, "expert").astype(jnp.float32)
    qkv_total = lax.psum(qkv_share, "expert").astype(jnp.float32)
    small_total = lax.psum(small_share, "expert")
    totals = (
        small_total[0],
        small_total[1],
        qkv_total,
        out_total,
        small_total[2],
        small_total[3],
        small_total[4:].T,
    )
    return (
        output,
        grad_tokens,
        totals[0],
        totals[1],
        totals[2],
        totals[3],
        totals[4],
        totals[5],
        totals[6],
        grad_up,
        grad_down,
    )


def on_device(
    tokens,
    norm1_gain,
    norm1_shift,
    w_qkv,
    w_out,
    norm2_gain,
    norm2_shift,
    w_router,
    w_up,
    w_down,
    routes,
    priority,
    prefix,
    cotangent,
):
    row_count, model_width = tokens.shape
    expert_count = w_router.shape[1]
    capacity = row_count // expert_count
    owners = lax.axis_size("expert")
    experts = w_up.shape[0]
    which = lax.broadcasted_iota(jnp.int32, (16, norm1_gain.shape[0]), 0)
    small = jnp.zeros(which.shape, jnp.bfloat16)
    for i, vector in enumerate((norm1_gain, norm1_shift, norm2_gain, norm2_shift)):
        small = jnp.where(which == i, vector[None], small)
    (
        qkv, act_t, merged_t, back, weight, out_full, low, high, grad_rows, hidden, send_rows,
        vectors, router,
    ) = run_front(
        owners, experts, capacity, prefix, routes.reshape(1, row_count), priority, tokens,
        cotangent, small, w_router.T, w_qkv, w_out,
    )
    far_sums, near_sums, home_out, home_grad, grad_up, grad_down, grad_router = run_experts(
        owners, capacity, expert_count, send_rows, grad_rows, w_up, w_down, router
    )
    output, grad_tokens, grad_vectors, grad_gates, grad_qkv, grad_out = run_back(
        owners, capacity, expert_count, home_grad, far_sums, near_sums, home_out, back, hidden, cotangent,
        tokens, vectors, grad_router, act_t, merged_t, qkv, weight, out_full, low, high,
    )
    return (
        output,
        grad_tokens,
        grad_vectors[0],
        grad_vectors[1],
        grad_qkv,
        grad_out,
        grad_vectors[2],
        grad_vectors[3],
        grad_gates.T,
        grad_up.astype(jnp.float32),
        grad_down.astype(jnp.float32),
    )


def solution(mesh):
    placed = (
        P(("expert", "wshard"), None),
        P("wshard"),
        P("wshard"),
        P("wshard", None),
        P("wshard", None),
        P("wshard"),
        P("wshard"),
        P("wshard", None),
        P("expert", None, "wshard"),
        P("expert", "wshard", None),
        P(("expert", "wshard"), None),
        P(("expert", "wshard"), None),
        P(("expert", "wshard")),
        P(("expert", "wshard"), None),
    )
    owners, group = mesh.shape["expert"], mesh.shape["wshard"]

    def body(*args):
        capacity = args[0].shape[0] // args[7].shape[1]
        fits = group == 4 and owners in (4, 8, 16) and capacity % 16 == 0 and args[7].shape[1] % 16 == 0
        return (on_device if fits else on_device_plain)(*args)

    return jax.shard_map(
        body,
        mesh=mesh,
        in_specs=placed,
        out_specs=(
            P(("expert", "wshard"), None),
            P(("expert", "wshard"), None),
            P("wshard"),
            P("wshard"),
            P("wshard", None),
            P("wshard", None),
            P("wshard"),
            P("wshard"),
            P("wshard", None),
            P("expert", None, "wshard"),
            P("expert", "wshard", None),
        ),
        check_vma=False,
    )
```

```python
import functools
import math

import jax
import jax.numpy as jnp
from jax import lax
from jax.experimental import pallas as pl
from jax.experimental.pallas import tpu as pltpu
from jax.sharding import PartitionSpec as P

HEADS = 16
HEAD_DIM = 64


epsilon = 1e-05
VMEM_LIMIT = 66_000_000
TILE = 1024
EARLY_CHUNKS = 2


def normalize(values, gain_vec, shift_vec):
    row_mean = jnp.mean(values, axis=-1, keepdims=True)
    centered = values - row_mean
    inverse = lax.rsqrt(jnp.mean(centered * centered, axis=-1, keepdims=True) + epsilon)
    scaled = centered * inverse
    return (scaled * gain_vec + shift_vec, scaled, inverse)


def norm_back(grad_rows, scaled, inverse, gain_vec):
    weighted = grad_rows * gain_vec
    mean_one = jnp.mean(weighted, axis=-1, keepdims=True)
    mean_two = jnp.mean(weighted * scaled, axis=-1, keepdims=True)
    grad_inputs = inverse * (weighted - mean_one - scaled * mean_two)
    return (grad_inputs, jnp.sum(grad_rows * scaled, axis=0), jnp.sum(grad_rows, axis=0))


def contract_rows(left, right):
    return lax.dot_general(
        left, right, (((0,), (0,)), ((), ())), preferred_element_type=jnp.float32
    )


def times_transpose(left, right):
    return lax.dot_general(
        left, right, (((1,), (1,)), ((), ())), preferred_element_type=jnp.float32
    )


def gelu_tanh(values):
    return jax.nn.gelu(values, approximate=True)


def assign_slots(route_ids, order_ids, expert_count, capacity):
    token_count = route_ids.shape[0]
    same_expert = route_ids[:, None] == route_ids[None, :]
    earlier = order_ids[None, :] < order_ids[:, None]
    rank_ids = jnp.sum((same_expert & earlier).astype(jnp.int32), axis=1)
    is_kept = rank_ids < capacity
    slot_index = jnp.where(is_kept, route_ids * capacity + rank_ids, expert_count * capacity)
    slot_ids = jnp.arange(expert_count * capacity, dtype=jnp.int32)
    match_table = slot_index[None, :] == slot_ids[:, None]
    token_ids = jnp.arange(token_count, dtype=jnp.int32)
    filled = jnp.any(match_table, axis=1)
    picked = jnp.sum(jnp.where(match_table, token_ids[None, :], 0), axis=1)
    slot_source = jnp.where(filled, picked, token_count)
    return (slot_index, slot_source)


def group_heads(values, groups):
    token_count = values.shape[0]
    return jnp.transpose(values.reshape(token_count, groups, -1, HEAD_DIM), (1, 0, 2, 3))


def block_scores(query_block, key_group, block_start, prefix_len):
    block_rows = query_block.shape[0]
    key_count = key_group.shape[0]
    scores = jnp.einsum(
        "qgd,kgd->gqk", query_block, key_group, preferred_element_type=jnp.float32
    ) * (1.0 / math.sqrt(HEAD_DIM))
    query_pos = block_start + jnp.arange(block_rows, dtype=jnp.int32)
    key_pos = jnp.arange(key_count, dtype=jnp.int32)
    allowed = (key_pos[None, :] <= query_pos[:, None]) | (key_pos[None, :] < prefix_len)
    return jnp.where(allowed[None], scores, -1e30)


def attend_forward(query_heads, key_heads, value_heads, prefix_len):
    token_count = query_heads.shape[0]
    group_size = min(4, HEADS)
    groups = HEADS // group_size
    block_rows = min(512, token_count)
    blocks = token_count // block_rows
    starts = jnp.arange(blocks, dtype=jnp.int32) * block_rows

    def one_group(group_item):
        query_group, key_group, value_group = group_item
        query_blocks = query_group.reshape(blocks, block_rows, group_size, HEAD_DIM)

        def one_block(block_item):
            query_block, block_start = block_item
            scores = block_scores(query_block, key_group, block_start, prefix_len)
            row_max = jnp.max(scores, axis=-1, keepdims=True)
            exponent = jnp.exp(scores - row_max)
            row_total = jnp.sum(exponent, axis=-1, keepdims=True)
            attn_probs = (exponent / row_total).astype(jnp.bfloat16)
            result = jnp.einsum(
                "gqk,kgd->qgd", attn_probs, value_group, preferred_element_type=jnp.float32
            )
            return (result, (row_max + jnp.log(row_total))[..., 0])

        return lax.map(one_block, (query_blocks, starts))

    attended, log_totals = lax.map(
        one_group,
        (
            group_heads(query_heads, groups),
            group_heads(key_heads, groups),
            group_heads(value_heads, groups),
        ),
    )
    merged = (
        jnp.transpose(attended, (1, 2, 0, 3, 4))
        .reshape(token_count, HEADS * HEAD_DIM)
        .astype(jnp.bfloat16)
    )
    return (merged, log_totals)


def attend_backward(query_heads, key_heads, value_heads, grad_merged, log_totals, prefix_len):
    token_count = query_heads.shape[0]
    group_size = min(4, HEADS)
    groups = HEADS // group_size
    block_rows = min(512, token_count)
    blocks = token_count // block_rows
    starts = jnp.arange(blocks, dtype=jnp.int32) * block_rows
    score_scale = 1.0 / math.sqrt(HEAD_DIM)

    def one_group(group_item):
        query_group, key_group, value_group, grad_group, total_group = group_item
        query_blocks = query_group.reshape(blocks, block_rows, group_size, HEAD_DIM)
        grad_blocks = grad_group.reshape(blocks, block_rows, group_size, HEAD_DIM)

        def one_block(carry, block_item):
            grad_keys, grad_vals = carry
            query_block, grad_block, total_block, block_start = block_item
            scores = block_scores(query_block, key_group, block_start, prefix_len)
            attn_probs = jnp.exp(scores - total_block[..., None])
            grad_probs = jnp.einsum(
                "qgd,kgd->gqk", grad_block, value_group, preferred_element_type=jnp.float32
            )
            row_delta = jnp.sum(attn_probs * grad_probs, axis=-1, keepdims=True)
            grad_scores = (attn_probs * (grad_probs - row_delta)).astype(jnp.bfloat16)
            grad_vals = grad_vals + jnp.einsum(
                "gqk,qgd->kgd",
                attn_probs.astype(jnp.bfloat16),
                grad_block,
                preferred_element_type=jnp.float32,
            )
            grad_keys = (
                grad_keys
                + jnp.einsum(
                    "gqk,qgd->kgd", grad_scores, query_block, preferred_element_type=jnp.float32
                )
                * score_scale
            )
            grad_query = (
                jnp.einsum(
                    "gqk,kgd->qgd", grad_scores, key_group, preferred_element_type=jnp.float32
                )
                * score_scale
            )
            return ((grad_keys, grad_vals), grad_query)

        zero_keys = jnp.zeros(key_group.shape, jnp.float32)
        carried, grad_queries = lax.scan(
            one_block, (zero_keys, zero_keys), (query_blocks, grad_blocks, total_group, starts)
        )
        return (grad_queries, carried[0], carried[1])

    grad_queries, grad_keys, grad_vals = lax.map(
        one_group,
        (
            group_heads(query_heads, groups),
            group_heads(key_heads, groups),
            group_heads(value_heads, groups),
            group_heads(grad_merged, groups),
            log_totals,
        ),
    )
    query_part = jnp.transpose(grad_queries, (1, 2, 0, 3, 4)).reshape(token_count, HEADS * HEAD_DIM)
    key_part = jnp.transpose(grad_keys, (1, 0, 2, 3)).reshape(token_count, HEADS * HEAD_DIM)
    value_part = jnp.transpose(grad_vals, (1, 0, 2, 3)).reshape(token_count, HEADS * HEAD_DIM)
    return jnp.concatenate([query_part, key_part, value_part], axis=1).astype(jnp.bfloat16)


MESH = pl.DeviceIdType.MESH
LANES = 128


def dot_nn(left, right):
    return lax.dot_general(
        left, right, (((1,), (0,)), ((), ())), preferred_element_type=jnp.float32
    )


def dot_nt(left, right):
    return lax.dot_general(
        left, right, (((1,), (1,)), ((), ())), preferred_element_type=jnp.float32
    )


def dot_tn(left, right):
    return lax.dot_general(
        left, right, (((0,), (0,)), ((), ())), preferred_element_type=jnp.float32
    )


def span(start, size):
    return pl.ds(pl.multiple_of(start, size), size)


def every(start, stop, step):
    def body(i, carry):
        step(i)
        return carry

    lax.fori_loop(start, stop, body, 0)


class Place:
    def __init__(self, owners):
        self.owners = owners
        self.e = lax.axis_index("expert")
        self.w = lax.axis_index("wshard")
        self.c = lax.rem(self.w, 2)
        self.x = lax.div(self.w, 2)
        self.sib = self.w + 1 - 2 * self.c
        self.far = lax.rem(self.w + 2, 4)
        self.diag = 3 - self.w
        self.pair = self.e + 1 - 2 * lax.rem(self.e, 2)

    def ahead(self, k):
        return lax.rem(self.e + k, self.owners)

    def peer(self, n):
        other = lax.div(n, 2) + lax.rem(n, 2) * (self.owners // 2)
        result, bit = 0, 1
        while bit < self.owners:
            result = result + bit * lax.rem(lax.div(self.e, bit) + lax.div(other, bit), 2)
            bit *= 2
        return result


def remote(src, dst, send, recv, device):
    return pltpu.make_async_remote_copy(
        src_ref=src,
        dst_ref=dst,
        send_sem=send,
        recv_sem=recv,
        device_id=device,
        device_id_type=MESH,
    )


def greet(peers):
    barrier = pltpu.get_barrier_semaphore()
    for peer in peers:
        pl.semaphore_signal(barrier, inc=1, device_id=peer, device_id_type=MESH)
    pl.semaphore_wait(barrier, len(peers))


def either(test, yes, no):
    pl.when(test)(yes)
    pl.when(jnp.logical_not(test))(no)


class Dispatch:
    def __init__(self, place, capacity, send_ref, rows_ref, sems):
        self.p, self.cap, self.src, self.rows = place, capacity, send_ref, rows_ref
        self.own_sem, self.send, self.recv = sems

    def slice(self, k, core, side):
        start = (((lax.div(k, 2) * 2 + core) * 2 + side) * 2 + lax.rem(k, 2)) * self.cap
        return self.rows.at[:, span(start, self.cap)]

    def own(self):
        return pltpu.make_async_copy(
            self.src.at[self.p.e], self.slice(0, self.p.c, self.p.x), self.own_sem
        )

    def direct(self, k):
        return remote(
            self.src.at[self.p.peer(k)],
            self.slice(k, self.p.c, self.p.x),
            self.send.at[0, k],
            self.recv.at[0, k],
            (self.p.peer(k), self.p.w),
        )

    def hop(self, k, side, which, peer):
        part = self.slice(k, self.p.c, side)
        return remote(
            part, part, self.send.at[which, k], self.recv.at[which, k], (self.p.e, peer)
        )

    def to_sib(self, k):
        return self.hop(k, self.p.x, 1, self.p.sib)

    def to_far(self, k):
        return self.hop(k, self.p.x, 2, self.p.far)

    def relayed(self, k):
        return self.hop(k, 1 - self.p.x, 3, self.p.sib)

    def start(self):
        self.own().start()
        every(1, self.p.owners, lambda k: self.direct(k).start())

    def forward(self, k):
        k = jnp.int32(k)

        @pl.when(k == 0)
        def _():
            self.own().wait()

        @pl.when(k > 0)
        def _():
            self.direct(k).wait_recv()

        self.to_far(k).start()
        self.to_sib(k).start()

    def relay(self, k):
        self.to_far(k).wait_recv()
        self.relayed(k).start()

    def ready(self, k):
        self.to_sib(k).wait_recv()
        self.relayed(k).wait_recv()

    def order(self):
        near, far = list(range(0, self.p.owners, 2)), list(range(1, self.p.owners, 2))
        return near[:3] + far[:1] + near[3:] + far[1:]

    def drain(self):
        every(1, self.p.owners, lambda k: self.direct(k).wait_send())

        def rest(k):
            self.to_sib(k).wait_send()
            self.to_far(k).wait_send()
            self.relayed(k).wait_send()

        every(0, self.p.owners, rest)


class Return:
    def __init__(self, place, capacity, part, got, mid, far, done, home, sems):
        self.p, self.cap = place, capacity
        self.part, self.got, self.mid, self.far, self.done, self.home = (
            part, got, mid, far, done, home,
        )
        self.own_sem, self.send, self.recv, self.home_send, self.home_recv = sems

    def swapped(self, j, expert):
        size = 4 * self.cap
        return remote(
            self.part.at[expert, span((j * 2 + 1 - self.p.c) * size, size)],
            self.got.at[expert, span(j * size, size)],
            self.send.at[0, j, expert],
            self.recv.at[0, j, expert],
            (self.p.e, self.p.sib),
        )

    def crossed(self, j, expert):
        part = span(j * 2 * self.cap, 2 * self.cap)
        return remote(
            self.mid.at[expert, part],
            self.far.at[expert, part],
            self.send.at[1, j, expert],
            self.recv.at[1, j, expert],
            (self.p.e, self.p.far),
        )

    def own(self, expert):
        return pltpu.make_async_copy(
            self.done.at[0, expert], self.home.at[self.p.e, expert], self.own_sem.at[expert]
        )

    def homed(self, n, expert):
        return remote(
            self.done.at[n, expert],
            self.home.at[self.p.e, expert],
            self.home_send.at[n, expert],
            self.home_recv.at[n, expert],
            (self.p.peer(n), self.p.w),
        )

    def pair_sum(self, j, expert, side):
        size = 2 * self.cap
        mine = self.part[expert, span(((j * 2 + self.p.c) * 2 + side) * size, size), :]
        theirs = self.got[expert, span((j * 2 + side) * size, size), :]
        return mine.astype(jnp.float32) + theirs.astype(jnp.float32)

    def swap(self, j, expert):
        self.swapped(j, expert).start()

    def split(self, j, expert):
        self.swapped(j, expert).wait_recv()
        here = span(j * 2 * self.cap, 2 * self.cap)
        self.mid[expert, here, :] = self.pair_sum(j, expert, 1 - self.p.x).astype(jnp.bfloat16)
        self.keep[expert, here, :] = self.pair_sum(j, expert, self.p.x).astype(jnp.bfloat16)

    def cross(self, j, expert):
        self.swapped(j, expert).wait_recv()
        here = span(j * 2 * self.cap, 2 * self.cap)
        self.mid[expert, here, :] = self.pair_sum(j, expert, 1 - self.p.x).astype(jnp.bfloat16)
        self.crossed(j, expert).start()

    def this_side(self, j, expert):
        return self.pair_sum(j, expert, self.p.x)

    def finish(self, j, expert):
        self.crossed(j, expert).wait_recv()
        here = span(j * 2 * self.cap, 2 * self.cap)
        total = self.this_side(j, expert) + self.far[expert, here, :].astype(jnp.float32)
        total = total.astype(jnp.bfloat16)
        self.done[2 * j, expert] = total[: self.cap]
        self.done[2 * j + 1, expert] = total[self.cap :]
        j = jnp.int32(j)
        self.homed(2 * j + 1, expert).start()
        either(
            j == 0,
            lambda: self.own(expert).start(),
            lambda: self.homed(2 * j, expert).start(),
        )

    def drain_swaps(self, chunks, experts):
        for expert in range(experts):
            every(0, chunks, lambda j: self.swapped(j, expert).wait_send())

    def drain(self, first, last, experts):
        for expert in range(experts):
            every(first, last, lambda j: self.crossed(j, expert).wait_send())
            every(
                max(1, 2 * first), 2 * last, lambda n: self.homed(n, expert).wait_send()
            )

    def arrived(self, first, last, experts):
        for expert in range(experts):
            if first == 0 and last > 0:
                self.own(expert).wait()
            every(
                max(1, 2 * first), 2 * last, lambda n: self.homed(n, expert).wait_recv()
            )


class LateReturn(Return):
    def crossed(self, j, expert):
        part = span(j * 2 * self.cap, 2 * self.cap)
        return remote(
            self.mid.at[expert, part],
            self.far.at[expert, part],
            self.send.at[j, expert],
            self.recv.at[j, expert],
            (self.p.e, self.p.far),
        )

    def this_side(self, j, expert):
        here = span(j * 2 * self.cap, 2 * self.cap)
        return self.part[expert, here, :].astype(jnp.float32)


def gelu_pair(v):
    root = math.sqrt(2.0 / math.pi)
    square = v * v
    t = jnp.tanh(v * (root + (root * 0.044715) * square))
    half = 0.5 + 0.5 * t
    slope = half + (half * (1.0 - t)) * (v * (root + (3.0 * root * 0.044715) * square))
    return v * half, slope


def expert_kernel(
    dims,
    send_ref, grads_hbm, up_hbm, down_hbm, router_ref,
    far_sums, near_sums, home_out, home_grad, up_out, down_out, router_grad,
    rows, grads, scaled, hidden, pre, up, down, grad_up, grad_down,
    part_out, part_grad, got_out, got_grad, mid_out, mid_grad,
    keep_out, far_grad, far_out, done_grad, done_out,
    load_sem, own_sem, disp_send, disp_recv, red_send, red_recv, home_send, home_recv,
):
    owners, experts, capacity, width, units, expert_count = dims
    place = Place(owners)
    loads = [
        pltpu.make_async_copy(src, dst, load_sem.at[i])
        for i, (src, dst) in enumerate(
            [(up_hbm, up), (grads_hbm, grads), (down_hbm, down)]
        )
    ]
    for load in loads:
        load.start()
    greet(
        [(place.ahead(k), place.w) for k in range(1, owners)]
        + [(place.e, place.sib), (place.e, place.far)]
    )
    dispatch = Dispatch(
        place, capacity, send_ref, rows, (own_sem.at[0, 0], disp_send, disp_recv)
    )
    ret_grad = Return(
        place, capacity, part_grad, got_grad, mid_grad, far_grad, done_grad, home_grad,
        (own_sem.at[1], red_send.at[0], red_recv.at[0], home_send.at[0], home_recv.at[0]),
    )
    ret_out = Return(
        place, capacity, part_out, got_out, mid_out, far_out, done_out, home_out,
        (own_sem.at[2], red_send.at[1], red_recv.at[1], home_send.at[1], home_recv.at[1]),
    )
    dispatch.start()
    router_grad[...] = jnp.zeros_like(router_grad)
    tile = min(TILE, units)
    wide = min(TILE, width)
    chunks = owners // 2
    early = EARLY_CHUNKS
    size = 8 * capacity
    lane = lax.broadcasted_iota(jnp.int32, (size, LANES), 1)

    def compute(j, expert):
        here = span(j * size, size)
        logits = dot_nt(rows[expert, here, :], router_ref[...])
        logits = jnp.where(lane < expert_count, logits, -1e30)
        exponent = jnp.exp(logits - jnp.max(logits, axis=1, keepdims=True))
        prob = exponent * (1.0 / jnp.sum(exponent, axis=1, keepdims=True))
        mine = lane == place.e * experts + expert
        gate = jnp.sum(jnp.where(mine, prob, 0.0), axis=1, keepdims=True)
        scaled[expert, here, :] = (
            gate * grads[expert, here, :].astype(jnp.float32)
        ).astype(jnp.bfloat16)

        def one_tile(n):
            cols = span(n * tile, tile)
            value, slope = gelu_pair(dot_nn(rows[expert, here, :], up[expert, :, cols]))
            hidden[expert, here, cols] = value.astype(jnp.bfloat16)
            back = pre[expert, here, cols].astype(jnp.float32)
            pre[expert, here, cols] = (gate * back * slope).astype(jnp.bfloat16)

        every(0, units // tile, one_tile)

        def one_out(n, total):
            cols = span(n * wide, wide)
            value = dot_nn(hidden[expert, here, :], down[expert, :, cols])
            part_out[expert, here, cols] = (gate * value).astype(jnp.bfloat16)
            weighted = value * grads[expert, here, cols].astype(jnp.float32)
            for start in range(0, wide, LANES):
                total = total + weighted[:, start : start + LANES]
            return total

        total = lax.fori_loop(
            0, width // wide, one_out, jnp.zeros((size, LANES), jnp.float32)
        )
        grad_gate = jnp.sum(total, axis=1, keepdims=True)
        grad_logits = (
            prob * ((jnp.where(mine, 1.0, 0.0) - gate) * grad_gate)
        ).astype(jnp.bfloat16)

        def one_in(n):
            cols = span(n * wide, wide)
            value = dot_nt(pre[expert, here, :], up[expert, cols, :]) + dot_nn(
                grad_logits, router_ref[:, cols]
            )
            part_grad[expert, here, cols] = value.astype(jnp.bfloat16)
            router_grad[:, cols] += dot_tn(grad_logits, rows[expert, here, cols])

        every(0, width // wide, one_in)

    def unscaled(j, expert):
        here = span(j * size, size)
        pre[expert, here, :] = dot_nt(grads[expert, here, :], down[expert]).astype(jnp.bfloat16)

    block = min(256, width)

    def weight_grads(expert, first, last):
        def one(n):
            part = span(n * block, block)
            grad_down[expert, part, :] = dot_tn(
                hidden[expert, :, part], scaled[expert]
            ).astype(jnp.bfloat16)
            grad_up[expert, part, :] = dot_tn(rows[expert, :, part], pre[expert]).astype(
                jnp.bfloat16
            )

        every(first * width // block // 4, last * width // block // 4, one)

    def keep(expert):
        return [
            pltpu.make_async_copy(src.at[expert], dst.at[expert], load_sem.at[2 * expert + i])
            for i, (src, dst) in enumerate(((grad_up, up_out), (grad_down, down_out)))
        ]

    turns = [(j, expert) for j in range(chunks) for expert in range(experts)]
    order = dispatch.order()
    waiting, moved = order[4:], set(order[:4])
    plan = [[] for _ in turns]

    def forward_to(acts, count):
        for _ in range(min(count, len(waiting))):
            n = waiting.pop(0)
            moved.add(n)
            acts.append((dispatch.forward, n))

    for u, (j, expert) in enumerate(turns):
        acts = plan[u]
        pair = (2 * j, 2 * j + 1)
        if expert == 0:
            if j > 0:
                while not moved.issuperset(pair):
                    forward_to(acts, 1)
                for n in pair:
                    acts.append((dispatch.relay, n))
            for n in pair:
                acts.append((dispatch.ready, n))
        if u > 0:
            forward_to(acts, 2)
        if u >= 2:
            last = turns[u - 2]
            acts.append((ret_grad.cross,) + last)
            acts.append((ret_out.cross if last[0] < early else ret_out.split,) + last)
        if u >= 4:
            last = turns[u - 4]
            acts.append((ret_grad.finish,) + last)
            if last[0] < early:
                acts.append((ret_out.finish,) + last)
    ret_out.keep = keep_out
    for load in loads:
        load.wait()
    for n in order[:4]:
        dispatch.forward(n)
        j = n // 2 if n % 2 == 0 else chunks - 1
        for expert in range(experts):
            unscaled(j, expert)
    dispatch.relay(0)
    dispatch.relay(1)

    def step(unit):
        for u, acts in enumerate(plan):

            @pl.when(unit == u)
            def _(acts=acts):
                for act, *at in acts:
                    act(*at)

        j, expert = lax.div(unit, experts), lax.rem(unit, experts)
        compute(j, expert)
        ret_grad.swap(j, expert)
        ret_out.swap(j, expert)

    every(0, len(turns), step)
    ret_grad.cross(*turns[-2])
    ret_out.split(*turns[-2])
    ret_grad.finish(*turns[-4])
    weight_grads(0, 0, 1)
    ret_grad.cross(*turns[-1])
    ret_out.split(*turns[-1])
    sums = [
        pltpu.make_async_copy(src, dst, load_sem.at[4 + i])
        for i, (src, dst) in enumerate(((mid_out, far_sums), (keep_out, near_sums)))
    ]
    for store in sums:
        store.start()
    ret_grad.finish(*turns[-3])
    weight_grads(0, 1, 2)
    ret_grad.finish(*turns[-2])
    weight_grads(0, 2, 3)
    ret_grad.finish(*turns[-1])
    weight_grads(0, 3, 4)
    for store in keep(0):
        store.start()
    for expert in range(1, experts):
        weight_grads(expert, 0, 4)
        for store in keep(expert):
            store.start()
    for expert in range(experts):
        for store in keep(expert):
            store.wait()
    for store in sums:
        store.wait()
    dispatch.drain()
    ret_grad.drain_swaps(chunks, experts)
    ret_grad.drain(0, chunks, experts)
    ret_grad.arrived(0, chunks, experts)
    ret_out.drain_swaps(chunks, experts)
    ret_out.drain(0, early, experts)
    ret_out.arrived(0, early, experts)


def run_experts(owners, capacity, expert_count, send_rows, grads, w_up, w_down, router):
    experts, width, units = w_up.shape
    slots = owners * 4 * capacity
    chunks = owners // 2
    dims = (owners, experts, capacity, width, units, expert_count)
    any_spec = pl.BlockSpec(memory_space=pl.ANY)
    vmem_spec = pl.BlockSpec(memory_space=pltpu.VMEM)
    bf16 = jnp.bfloat16
    home = jax.ShapeDtypeStruct((owners, experts, capacity, width), bf16)
    dma = pltpu.SemaphoreType.DMA

    def vm(*shape):
        return pltpu.VMEM(shape, bf16)

    return pl.pallas_call(
        functools.partial(expert_kernel, dims),
        out_shape=(
            jax.ShapeDtypeStruct((experts, slots // 4, width), bf16),
            jax.ShapeDtypeStruct((experts, slots // 4, width), bf16),
            home, home,
            jax.ShapeDtypeStruct(w_up.shape, bf16),
            jax.ShapeDtypeStruct(w_down.shape, bf16),
            jax.ShapeDtypeStruct((LANES, width), jnp.float32),
        ),
        in_specs=[any_spec] * 4 + [vmem_spec],
        out_specs=(any_spec,) * 6 + (vmem_spec,),
        scratch_shapes=[
            vm(experts, slots, width),
            vm(experts, slots, width),
            vm(experts, slots, width),
            vm(experts, slots, units),
            vm(experts, slots, units),
            vm(experts, width, units),
            vm(experts, units, width),
            vm(experts, width, units),
            vm(experts, units, width),
            vm(experts, slots, width),
            vm(experts, slots, width),
            vm(experts, slots // 2, width),
            vm(experts, slots // 2, width),
            vm(experts, slots // 4, width),
            vm(experts, slots // 4, width),
            vm(experts, slots // 4, width),
            vm(experts, slots // 4, width),
            vm(experts, slots // 4, width),
            vm(owners, experts, capacity, width),
            vm(owners, experts, capacity, width),
            dma((6,)),
            dma((3, experts)),
            dma((4, owners)),
            dma((4, owners)),
            dma((2, 2, chunks, experts)),
            dma((2, 2, chunks, experts)),
            dma((2, owners, experts)),
            dma((2, owners, experts)),
        ],
        compiler_params=pltpu.CompilerParams(
            collective_id=1, has_side_effects=True, vmem_limit_bytes=VMEM_LIMIT
        ),
        name="experts",
    )(send_rows, grads, w_up, w_down, router)


def masked_softmax(scores):
    exponent = jnp.exp(scores - jnp.max(scores, axis=1, keepdims=True))
    return exponent * (1.0 / jnp.sum(exponent, axis=1, keepdims=True))


def attend_head(query, key, value, prefix_len):
    half = query.shape[0] // 2
    query = query * (1.0 / math.sqrt(HEAD_DIM))
    row = lax.broadcasted_iota(jnp.int32, (half, half), 0)
    col = lax.broadcasted_iota(jnp.int32, (half, half), 1)
    low = dot_nt(query[:half], key[:half])
    low = jnp.where((col <= row) | (col < prefix_len), low, -1e30)
    low = masked_softmax(low).astype(jnp.bfloat16)
    high = dot_nt(query[half:], key)
    high = jnp.concatenate(
        [high[:, :half], jnp.where(col <= row, high[:, half:], -1e30)], axis=1
    )
    high = masked_softmax(high).astype(jnp.bfloat16)
    return low, high, dot_nn(low, value[:half]), dot_nn(high, value)


def score_grads(probs, grad_probs):
    probs = probs.astype(jnp.float32)
    weighted = probs * grad_probs
    total = jnp.sum(weighted, axis=1, keepdims=True)
    return (weighted - probs * total).astype(jnp.bfloat16)


def attend_back_head(query, key, value, low, high, grad):
    half = query.shape[0] // 2
    scale = 1.0 / math.sqrt(HEAD_DIM)
    query = query * scale
    grad_low = score_grads(low, dot_nt(grad[:half], value[:half]))
    grad_high = score_grads(high, dot_nt(grad[half:], value))
    grad_query = jnp.concatenate(
        [dot_nn(grad_low, key[:half]), dot_nn(grad_high, key)], axis=0
    )
    value_all = dot_tn(high, grad[half:])
    key_all = dot_tn(grad_high, query[half:])
    grad_value = jnp.concatenate(
        [value_all[:half] + dot_tn(low, grad[:half]), value_all[half:]], axis=0
    )
    grad_key = jnp.concatenate(
        [key_all[:half] + dot_tn(grad_low, query[:half]), key_all[half:]], axis=0
    )
    return (
        (grad_query * scale).astype(jnp.bfloat16),
        grad_key.astype(jnp.bfloat16),
        grad_value.astype(jnp.bfloat16),
    )


class Gather:
    def __init__(self, place, pieces, parts, src, dst, sems):
        self.p, self.src, self.dst, self.pieces, self.parts = place, src, dst, pieces, parts
        self.send, self.recv = sems
        self.shard = src.shape[0]
        self.half = self.shard // 2
        self.width = src.shape[1] // parts
        self.step = self.width // pieces
        self.first = lax.rem(place.e, 2) * self.half
        self.second = self.half - self.first

    def cols(self, n, part):
        return span(part * self.width + n * self.step, self.step)

    def block(self, owner, start, size, n, part):
        rows = pl.ds(pl.multiple_of(owner * self.shard + start, self.half), size)
        return self.dst.at[rows, self.cols(n, part)]

    def move(self, which, n, part, src, dst, device):
        return remote(
            src, dst, self.send.at[which, n, part], self.recv.at[which, n, part], device
        )

    def own(self, n, part):
        return pltpu.make_async_copy(
            self.src.at[:, self.cols(n, part)],
            self.block(self.p.w, 0, self.shard, n, part),
            self.recv.at[5, n, part],
        )

    def near(self, n, part):
        return self.move(
            4, n, part, self.src.at[:, self.cols(n, part)],
            self.block(self.p.w, 0, self.shard, n, part), (self.p.e, self.p.sib),
        )

    def hop(self, n, part):
        return self.move(
            0, n, part, self.src.at[span(self.first, self.half), self.cols(n, part)],
            self.block(self.p.w, self.first, self.half, n, part), (self.p.e, self.p.far),
        )

    def pass_from(self, which, start, n, part, device):
        block = self.block(self.p.far, start, self.half, n, part)
        return self.move(which, n, part, block, block, device)

    def pairs(self, n, part):
        return self.pass_from(1, self.first, n, part, (self.p.pair, self.p.w))

    def relay(self, n, part):
        return self.pass_from(2, self.first, n, part, (self.p.e, self.p.sib))

    def pair_relay(self, n, part):
        return self.pass_from(3, self.second, n, part, (self.p.e, self.p.sib))

    def all_parts(self, n, act):
        for part in range(self.parts):
            act(n, part)

    def start_own(self):
        every(
            0, self.pieces, lambda n: self.all_parts(n, lambda n, part: self.own(n, part).start())
        )

    def start(self):
        def hop(n, part):
            self.hop(n, part).start()

        def near(n, part):
            self.near(n, part).start()

        every(0, self.pieces, lambda n: self.all_parts(n, hop))
        every(0, self.pieces, lambda n: self.all_parts(n, near))

    def pass_on(self, n):
        def one(n, part):
            self.hop(n, part).wait_recv()
            self.pairs(n, part).start()
            self.relay(n, part).start()

        self.all_parts(n, one)

    def pass_pair(self, n):
        def one(n, part):
            self.pairs(n, part).wait_recv()
            self.pair_relay(n, part).start()

        self.all_parts(n, one)

    def ready(self, n):
        def one(n, part):
            self.own(n, part).wait()
            for copy in (self.near(n, part), self.relay(n, part), self.pair_relay(n, part)):
                copy.wait_recv()

        self.all_parts(n, one)

    def drain(self):
        def one(n, part):
            for copy in (
                self.hop(n, part), self.pairs(n, part), self.relay(n, part),
                self.pair_relay(n, part), self.near(n, part),
            ):
                copy.wait_send()

        every(0, self.pieces, lambda n: self.all_parts(n, one))


def slot_tables(routes_ref, priority_ref, capacity, pick_ref, back_ref):
    count = routes_ref.shape[1]
    row = lax.broadcasted_iota(jnp.int32, (count, count), 0).astype(jnp.float32)
    col = lax.broadcasted_iota(jnp.int32, (count, count), 1).astype(jnp.float32)
    eye = row == col
    route_row = routes_ref[...].astype(jnp.float32)
    order_row = priority_ref[...].astype(jnp.float32)
    route_col = jnp.sum(jnp.where(eye, route_row, 0.0), axis=1, keepdims=True)
    order_col = jnp.sum(jnp.where(eye, order_row, 0.0), axis=1, keepdims=True)
    same = route_col == route_row
    rank_row = jnp.sum(
        jnp.where(same & (order_col < order_row), 1.0, 0.0), axis=0, keepdims=True
    )
    rank_col = jnp.sum(
        jnp.where(same & (order_row < order_col), 1.0, 0.0), axis=1, keepdims=True
    )
    slots = float(count)
    slot_row = jnp.where(rank_row < capacity, route_row * capacity + rank_row, slots)
    slot_col = jnp.where(rank_col < capacity, route_col * capacity + rank_col, slots)
    pick_ref[...] = jnp.where(slot_row == row, 1.0, 0.0).astype(jnp.bfloat16)
    back_ref[...] = jnp.where(slot_col == col, 1.0, 0.0).astype(jnp.bfloat16)


def norm_stats(value):
    centered = value - jnp.mean(value, axis=1, keepdims=True)
    inverse = lax.rsqrt(jnp.mean(centered * centered, axis=1, keepdims=True) + epsilon)
    return centered * inverse, inverse


def front_kernel(
    dims,
    prefix_ref, routes_ref, priority_ref, tokens_ref, cot_ref, small_hbm, router_hbm, qkv_hbm, out_hbm,
    qkv_out, act_out, merged_out, back_out, weight_out, out_full, low_out, high_out, grads_rows,
    hidden_ref, send_ref, small_out, router_out,
    small, weight, out_w, qkv, act, merged, act_two, turned, pick, back, grads_send, low_buf, high_buf,
    own_sem, disp_send, disp_recv, small_send, small_recv, gat_send, gat_recv, store_sem, prob_sem,
):
    owners, capacity, pieces = dims
    place = Place(owners)
    rows, width = tokens_ref.shape
    shard = qkv_hbm.shape[0]
    gathers = [
        Gather(place, pieces, parts, src, dst, (gat_send.at[i], gat_recv.at[i]))
        for i, (parts, src, dst) in enumerate(((3, qkv_hbm, weight), (1, out_hbm, out_w)))
    ]
    for gather in gathers:
        gather.start_own()
    vectors, gates = small_hbm.shape[0], router_hbm.shape[0]
    small_parts = [
        (small_hbm, small.at[place.w, pl.ds(0, vectors)]),
        (router_hbm, small.at[place.w, pl.ds(vectors, gates)]),
    ]
    own_smalls = [
        pltpu.make_async_copy(src, dst, own_sem.at[3 + i])
        for i, (src, dst) in enumerate(small_parts)
    ]
    for copy in own_smalls:
        copy.start()
    greet(
        [(place.ahead(k), place.w) for k in range(1, owners)]
        + [(place.e, place.sib), (place.e, place.far), (place.e, place.diag)]
    )
    smalls = [
        remote(src, dst, small_send.at[n, i], small_recv.at[n, i], (place.e, peer))
        for i, peer in enumerate((place.sib, place.far, place.diag))
        for n, (src, dst) in enumerate(small_parts)
    ]
    for copy in smalls:
        copy.start()
    for gather in gathers:
        gather.start()
    slot_tables(routes_ref, priority_ref, capacity, pick, back)
    tile = min(256, width)
    shape = grads_send.shape[:3]

    def to_slots(values_ref, slots_ref):
        def one(n):
            cols = span(n * tile, tile)
            value = dot_nn(pick[...], values_ref[:, cols]).astype(jnp.bfloat16)
            slots_ref[:, :, :, cols] = value.reshape(shape + (tile,))

        every(0, width // tile, one)

    to_slots(cot_ref, grads_send)
    dispatch = Dispatch(
        place, capacity, grads_send, grads_rows, (own_sem.at[0], disp_send, disp_recv)
    )
    dispatch.start()
    for copy in own_smalls:
        copy.wait()
    for copy in smalls:
        copy.wait_recv()
    small_out[...] = small[:, :vectors, :]
    router_out[...] = jnp.zeros_like(router_out)
    router_out[:gates, :] = jnp.concatenate(
        [small[i, vectors:, :] for i in range(4)], axis=1
    )

    def vector(which):
        parts = [small[i, which : which + 1, :] for i in range(4)]
        return jnp.concatenate(parts, axis=1).astype(jnp.float32)

    band = min(64, rows)
    gain, shift = vector(0), vector(1)

    def norm_band(i):
        part = span(i * band, band)
        scaled, _ = norm_stats(tokens_ref[part, :].astype(jnp.float32))
        act[part, :] = (scaled * gain + shift).astype(jnp.bfloat16)

    def project(n):
        for part in range(3):
            cols = gathers[0].cols(n, part)
            qkv[:, cols] = dot_nn(act[...], weight[:, cols]).astype(jnp.bfloat16)

    gathers[0].pass_on(0)
    every(0, rows // band, norm_band)
    turned[0] = act[...].T
    stores = [
        pltpu.make_async_copy(src, dst, store_sem.at[i])
        for i, (src, dst) in enumerate(
            [(qkv, qkv_out), (turned.at[0], act_out), (back, back_out), (weight, weight_out),
             (turned.at[1], merged_out), (out_w, out_full)]
        )
    ]
    for store in stores[1:3]:
        store.start()
    half = rows // 2
    pairs = width // LANES

    def keep_probs(i):
        slot = lax.rem(i, 2)
        return (
            pltpu.make_async_copy(
                low_buf.at[slot], low_out.at[pl.ds(2 * i, 2)], prob_sem.at[0, slot]
            ),
            pltpu.make_async_copy(
                high_buf.at[slot], high_out.at[pl.ds(2 * i, 2)], prob_sem.at[1, slot]
            ),
        )

    def attend_pair(i):
        slot = lax.rem(i, 2)

        @pl.when(i >= 2)
        def _():
            for copy in keep_probs(i - 2):
                copy.wait()

        query, key, value = (
            qkv[:, span(part * width + i * LANES, LANES)] for part in range(3)
        )
        tops, bottoms = [], []
        for head in range(2):
            part = slice(head * HEAD_DIM, (head + 1) * HEAD_DIM)
            low, high, top, bottom = attend_head(
                query[:, part], key[:, part], value[:, part], prefix_ref[0]
            )
            low_buf[slot, head] = low
            high_buf[slot, head] = high
            tops.append(top)
            bottoms.append(bottom)
        cols = span(i * LANES, LANES)
        merged[:half, cols] = jnp.concatenate(tops, axis=1).astype(jnp.bfloat16)
        merged[half:, cols] = jnp.concatenate(bottoms, axis=1).astype(jnp.bfloat16)
        for copy in keep_probs(i):
            copy.start()

    group = pairs // pieces
    share = -(-owners // pieces)

    def front_step(n):
        @pl.when(n + 1 < pieces)
        def _():
            gathers[0].pass_on(n + 1)

        gathers[0].pass_pair(n)
        for i, partner in enumerate(dispatch.order()):
            pl.when(n == i // share)(functools.partial(dispatch.forward, partner))
        gathers[0].ready(n)
        project(n)
        for i in range(group):
            attend_pair(n * group + i)

    every(0, pieces, front_step)
    turned[1] = merged[...].T
    for i in (0, 3, 4):
        stores[i].start()
    every(0, pieces, gathers[1].pass_on)
    every(0, pieces, gathers[1].pass_pair)
    order = dispatch.order()
    dispatch.relay(order[0])
    every(0, pieces, gathers[1].ready)
    stores[5].start()
    gain_two, shift_two = vector(2), vector(3)
    band_two = min(128, rows)

    def middle(i):
        part = span(i * band_two, band_two)
        value = tokens_ref[part, :].astype(jnp.float32) + dot_nn(merged[part, :], out_w[...])
        hidden_ref[part, :] = value
        scaled, _ = norm_stats(value)
        act_two[part, :] = (scaled * gain_two + shift_two).astype(jnp.bfloat16)
        for n, partner in enumerate(order[1 : 1 + bands]):
            pl.when(i == n)(functools.partial(dispatch.relay, partner))

    bands = rows // band_two
    every(0, bands, middle)
    to_slots(act_two, send_ref)
    for partner in order[1 + bands :]:
        dispatch.relay(partner)
    for i in (pairs - 2, pairs - 1):
        for copy in keep_probs(i):
            copy.wait()
    every(0, owners, dispatch.ready)
    for store in stores:
        store.wait()
    for copy in smalls:
        copy.wait_send()
    for gather in gathers:
        gather.drain()
    dispatch.drain()


def run_front(
    owners, experts, capacity, prefix, routes, priority, tokens, cotangent, small, router, w_qkv, w_out
):
    rows, width = tokens.shape
    shard, columns = w_qkv.shape
    half = rows // 2
    heads = width // HEAD_DIM
    pieces = 4
    any_spec = pl.BlockSpec(memory_space=pl.ANY)
    vmem_spec = pl.BlockSpec(memory_space=pltpu.VMEM)
    bf16, f32 = jnp.bfloat16, jnp.float32
    dma = pltpu.SemaphoreType.DMA

    def out(*shape):
        return jax.ShapeDtypeStruct(shape, bf16)

    def vm(*shape):
        return pltpu.VMEM(shape, bf16)

    return pl.pallas_call(
        functools.partial(front_kernel, (owners, capacity, pieces)),
        out_shape=(
            out(rows, columns),
            out(width, rows),
            out(width, rows),
            out(rows, rows),
            out(4 * shard, columns),
            out(4 * shard, width),
            out(heads, half, half),
            out(heads, half, rows),
            out(experts, owners * 4 * capacity, width),
            jax.ShapeDtypeStruct((rows, width), f32),
            out(owners, experts, capacity, width),
            out(4, *small.shape),
            out(LANES, width),
        ),
        in_specs=[pl.BlockSpec(memory_space=pltpu.SMEM)] + [vmem_spec] * 4 + [any_spec] * 4,
        out_specs=(any_spec,) * 9 + (vmem_spec,) * 4,
        scratch_shapes=[
            vm(4, small.shape[0] + router.shape[0], shard),
            vm(4 * shard, columns),
            vm(4 * shard, width),
            vm(rows, columns),
            vm(rows, width),
            vm(rows, width),
            vm(rows, width),
            vm(2, width, rows),
            vm(rows, rows),
            vm(rows, rows),
            vm(owners, experts, capacity, width),
            vm(2, 2, half, half),
            vm(2, 2, half, rows),
            dma((5,)),
            dma((4, owners)),
            dma((4, owners)),
            dma((2, 3)),
            dma((2, 3)),
            dma((2, 6, pieces, 3)),
            dma((2, 6, pieces, 3)),
            dma((6,)),
            dma((2, 2)),
        ],
        compiler_params=pltpu.CompilerParams(
            collective_id=0, has_side_effects=True, vmem_limit_bytes=VMEM_LIMIT
        ),
        name="front",
    )(prefix, routes, priority, tokens, cotangent, small, router, w_qkv, w_out)


class Reduce:
    def __init__(self, place, part, got, far, pair, lines, done, sems):
        self.p = place
        self.part, self.got, self.far = part, got, far
        self.pair, self.lines, self.done = pair, lines, done
        self.send, self.recv, self.line_send, self.line_recv = sems
        self.chunks = part.shape[0]
        self.halves = done.shape[1] // 2
        self.count = place.owners // 2
        self.slice = self.halves // self.count
        self.bit = lax.rem(place.e, 2)
        self.level = lax.div(place.e, 2)

    def step(self, which, n, src, dst, device):
        return remote(src, dst, self.send.at[which, n], self.recv.at[which, n], device)

    def swapped(self, n):
        return self.step(
            0, n, self.part.at[n, :, 1 - self.p.c], self.got.at[n], (self.p.e, self.p.sib)
        )

    def crossed(self, n):
        return self.step(
            1, n, self.part.at[n, 1 - self.p.x, self.p.c], self.far.at[n], (self.p.e, self.p.far)
        )

    def folded(self, n):
        other = span((1 - self.bit) * self.halves, self.halves)
        return self.step(
            2, n, self.part.at[n, self.p.x, self.p.c, other], self.pair.at[n],
            (self.p.pair, self.p.w),
        )

    def shared(self, n):
        part = self.done.at[n, span(self.bit * self.halves, self.halves)]
        return self.step(3, n, part, part, (self.p.pair, self.p.w))

    def line(self, which, n, k, src, dst):
        return remote(
            src, dst, self.line_send.at[which, n, k], self.line_recv.at[which, n, k],
            (self.p.ahead(2 * k), self.p.w),
        )

    def row(self, level):
        return span(self.bit * self.halves + level * self.slice, self.slice)

    def spreads(self, n, k):
        target = lax.rem(self.level + k, self.count)
        return self.line(
            0, n, k, self.part.at[n, self.p.x, self.p.c, self.row(target)], self.lines.at[n, k]
        )

    def collects(self, n, k):
        part = self.done.at[n, self.row(self.level)]
        return self.line(1, n, k, part, part)

    def pair_sum(self, n, side):
        return self.part[n, side, self.p.c].astype(jnp.float32) + self.got[n, side].astype(
            jnp.float32
        )

    def swap(self, n):
        self.swapped(n).start()

    def cross(self, n):
        self.swapped(n).wait_recv()
        side = 1 - self.p.x
        self.part[n, side, self.p.c] = self.pair_sum(n, side).astype(jnp.bfloat16)
        self.crossed(n).start()

    def fold(self, n):
        self.crossed(n).wait_recv()
        total = self.pair_sum(n, self.p.x) + self.far[n].astype(jnp.float32)
        self.part[n, self.p.x, self.p.c] = total.astype(jnp.bfloat16)
        self.folded(n).start()

    def spread(self, n):
        self.folded(n).wait_recv()
        own = span(self.bit * self.halves, self.halves)
        total = self.part[n, self.p.x, self.p.c, own, :].astype(jnp.float32) + self.pair[
            n
        ].astype(jnp.float32)
        self.part[n, self.p.x, self.p.c, own, :] = total.astype(jnp.bfloat16)
        for k in range(1, self.count):
            self.spreads(n, k).start()

    def collect(self, n):
        total = self.part[n, self.p.x, self.p.c, self.row(self.level), :].astype(jnp.float32)
        for k in range(1, self.count):
            self.spreads(n, k).wait_recv()
            total = total + self.lines[n, k].astype(jnp.float32)
        self.done[n, self.row(self.level), :] = total.astype(jnp.bfloat16)
        for k in range(1, self.count):
            self.collects(n, k).start()

    def share(self, n):
        for k in range(1, self.count):
            self.collects(n, k).wait_recv()
        self.shared(n).start()

    def finish(self, n):
        self.shared(n).wait_recv()

    def stages(self):
        return (self.cross, self.fold, self.spread, self.collect, self.share, self.finish)

    def drain(self):
        def one(n):
            for copy in (self.swapped(n), self.crossed(n), self.folded(n), self.shared(n)):
                copy.wait_send()
            for k in range(1, self.count):
                self.spreads(n, k).wait_send()
                self.collects(n, k).wait_send()

        every(0, self.chunks, one)


class Small:
    def __init__(self, place, value, part, got, mid, far, total, others, out, sems):
        self.p, self.value, self.part, self.got, self.mid = place, value, part, got, mid
        self.far, self.total, self.others, self.out = far, total, others, out
        self.send, self.recv, self.all_send, self.all_recv = sems

    def swapped(self):
        return remote(
            self.part.at[:, 1 - self.p.c], self.got, self.send.at[0], self.recv.at[0],
            (self.p.e, self.p.sib),
        )

    def crossed(self):
        return remote(
            self.mid, self.far, self.send.at[1], self.recv.at[1], (self.p.e, self.p.far)
        )

    def spreads(self, k):
        return remote(
            self.total, self.others.at[k], self.all_send.at[k], self.all_recv.at[k],
            (self.p.ahead(k), self.p.w),
        )

    def swap(self):
        size = self.part.shape[-1]
        for owner in range(4):
            self.part[owner // 2, owner % 2] = self.value[:, owner * size : (owner + 1) * size]
        self.swapped().start()

    def cross(self):
        self.swapped().wait_recv()
        self.mid[...] = self.part[1 - self.p.x, self.p.c] + self.got[1 - self.p.x]
        self.crossed().start()

    def spread(self):
        self.crossed().wait_recv()
        self.total[...] = self.part[self.p.x, self.p.c] + self.got[self.p.x] + self.far[...]
        for k in range(1, self.p.owners):
            self.spreads(k).start()

    def finish(self):
        total = self.total[...]
        for k in range(1, self.p.owners):
            self.spreads(k).wait_recv()
            total = total + self.others[k]
        vectors_out, gates_out = self.out
        vectors_out[...] = total[: vectors_out.shape[0]]
        gates_out[...] = total[vectors_out.shape[0] :]

    def drain(self):
        self.swapped().wait_send()
        self.crossed().wait_send()
        for k in range(1, self.p.owners):
            self.spreads(k).wait_send()


def norm_back_rows(grad, scaled, inverse, gain):
    weighted = grad * gain
    mean_one = jnp.mean(weighted, axis=1, keepdims=True)
    mean_two = jnp.mean(weighted * scaled, axis=1, keepdims=True)
    return inverse * (weighted - mean_one - scaled * mean_two)


def back_kernel(
    dims,
    home_grad_ref, back_ref, hidden_ref, cot_ref, tokens_ref, vectors_ref, router_ref,
    far_hbm, near_hbm, home_hbm, act_hbm, merged_hbm, qkv_hbm, weight_hbm, out_hbm, low_hbm, high_hbm,
    output_ref, tokens_out, vectors_out, gates_out, qkv_out, out_out,
    near_sums, far_sums, done_rows, home_out,
    act_t, merged_t, qkv, weight, out_w, low_buf, high_buf, attn, grad_merged,
    part_q, got_q, far_q, pair_q, lines_q, done_q,
    part_o, got_o, far_o, pair_o, lines_o, done_o,
    small, small_part, small_got, small_mid, small_far, small_sum, small_all,
    load_sem, prob_sem, own_sem, early_sem, cross_send, cross_recv, home_send, home_recv, send_q, recv_q, lsend_q, lrecv_q, send_o, recv_o, lsend_o, lrecv_o,
    small_send, small_recv, all_send, all_recv, out_sem,
):
    owners, capacity, gates = dims
    grad_qkv = qkv
    place = Place(owners)
    loads = [
        pltpu.make_async_copy(src, dst, load_sem.at[i])
        for i, (src, dst) in enumerate(
            [(merged_hbm, merged_t), (out_hbm, out_w), (qkv_hbm, qkv), (act_hbm, act_t),
             (weight_hbm, weight), (near_hbm, near_sums)]
        )
    ]

    def load_probs(i):
        slot = lax.rem(i, 2)
        return (
            pltpu.make_async_copy(
                low_hbm.at[pl.ds(2 * i, 2)], low_buf.at[slot], prob_sem.at[0, slot]
            ),
            pltpu.make_async_copy(
                high_hbm.at[pl.ds(2 * i, 2)], high_buf.at[slot], prob_sem.at[1, slot]
            ),
        )

    for load in loads:
        load.start()
    for load in load_probs(0):
        load.start()
    greet(
        [(place.ahead(k), place.w) for k in range(1, owners)]
        + [(place.e, place.sib), (place.e, place.far)]
    )
    experts = near_sums.shape[0]
    groups = owners // 2
    late = LateReturn(
        place, capacity, near_sums, None, far_hbm, far_sums, done_rows, home_out,
        (own_sem, cross_send, cross_recv, home_send, home_recv),
    )
    for expert in range(experts):
        every(EARLY_CHUNKS, groups, lambda j: late.crossed(j, expert).start())

    def early_rows(n):
        row = place.peer(n)
        return pltpu.make_async_copy(home_hbm.at[row], home_out.at[row], early_sem.at[n])

    every(0, 2 * EARLY_CHUNKS, lambda n: early_rows(n).start())
    reduce_o = Reduce(
        place, part_o, got_o, far_o, pair_o, lines_o, done_o, (send_o, recv_o, lsend_o, lrecv_o)
    )
    reduce_q = Reduce(
        place, part_q, got_q, far_q, pair_q, lines_q, done_q, (send_q, recv_q, lsend_q, lrecv_q)
    )
    smalls = Small(
        place, small, small_part, small_got, small_mid, small_far, small_sum, small_all, (vectors_out, gates_out),
        (small_send, small_recv, all_send, all_recv),
    )
    rows, width = tokens_ref.shape
    shard = width // 4
    band = min(128, rows)
    lead = small.shape[0]

    def vector(which):
        parts = [vectors_ref[i, which : which + 1, :] for i in range(4)]
        return jnp.concatenate(parts, axis=1).astype(jnp.float32)

    gain_one, gain_two = vector(0), vector(2)
    small[: lead - gates, :] = jnp.zeros((lead - gates, width), jnp.float32)
    small[lead - gates :, :] = router_ref[:gates, :]

    def post(i):
        part = span(i * band, band)
        grad = dot_nn(back_ref[part, :], home_grad_ref.reshape(rows, width)[...])
        scaled, inverse = norm_stats(hidden_ref[part, :])
        value = cot_ref[part, :].astype(jnp.float32) + norm_back_rows(
            grad, scaled, inverse, gain_two
        )
        tokens_out[part, :] = value
        attn[part, :] = value.astype(jnp.bfloat16)
        small[2:3, :] += jnp.sum(grad * scaled, axis=0, keepdims=True)
        small[3:4, :] += jnp.sum(grad, axis=0, keepdims=True)

    every(0, rows // band, post)
    loads[0].wait()

    def weight_grad(part, n, left, right):
        def one(owner):
            value = dot_nn(left[span(owner * shard, shard), :], right)
            part[n, lax.div(owner, 2), lax.rem(owner, 2)] = value.astype(jnp.bfloat16)

        every(0, 4, one)

    tile_o = part_o.shape[-1]
    out_chunks = part_o.shape[0]
    for n in range(out_chunks):
        weight_grad(part_o, n, merged_t, attn[:, n * tile_o : (n + 1) * tile_o])
        reduce_o.swap(n)
    loads[1].wait()

    def merged_band(i):
        part = span(i * band, band)
        grad_merged[part, :] = dot_nt(attn[part, :], out_w[...]).astype(jnp.bfloat16)

    every(0, rows // band, merged_band)
    for load in loads[2:4] + loads[5:]:
        load.wait()
    pairs = part_q.shape[0]

    def attend_pair(i):
        slot = lax.rem(i, 2)
        for load in load_probs(i):
            load.wait()

        @pl.when(i + 1 < pairs)
        def _():
            for load in load_probs(i + 1):
                load.start()

        cols = span(i * LANES, LANES)
        query, key, value = (
            qkv[:, span(part * width + i * LANES, LANES)] for part in range(3)
        )
        grad = grad_merged[:, cols]
        results = []
        for head in range(2):
            part = slice(head * HEAD_DIM, (head + 1) * HEAD_DIM)
            results.append(
                attend_back_head(
                    query[:, part], key[:, part], value[:, part],
                    low_buf[slot, head], high_buf[slot, head], grad[:, part],
                )
            )
        for which in range(3):
            grad_qkv[:, span(which * width + i * LANES, LANES)] = jnp.concatenate(
                [results[0][which], results[1][which]], axis=1
            )
        right = jnp.concatenate(
            [grad_qkv[:, span(which * width + i * LANES, LANES)] for which in range(3)], axis=1
        )
        weight_grad(part_q, i, act_t, right)
        reduce_q.swap(i)

    def input_band(i):
        part = span(i * band, band)
        grad = dot_nt(grad_qkv[part, :], weight[...])
        scaled, inverse = norm_stats(tokens_ref[part, :].astype(jnp.float32))
        tokens_out[part, :] += norm_back_rows(grad, scaled, inverse, gain_one)
        small[0:1, :] += jnp.sum(grad * scaled, axis=0, keepdims=True)
        small[1:2, :] += jnp.sum(grad, axis=0, keepdims=True)

    def output_band(i):
        part = span(i * band, band)
        slots = home_out.reshape(rows, width)
        value = hidden_ref[part, :] + dot_nn(back_ref[part, :], slots[...])
        output_ref[part, :] = value.astype(jnp.bfloat16)

    def store_q(i):
        return [
            pltpu.make_async_copy(
                done_q.at[i, :, pl.ds(which * LANES, LANES)],
                qkv_out.at[:, span(which * width + i * LANES, LANES)],
                out_sem.at[which, i],
            )
            for which in range(3)
        ]

    def store_o(n):
        return pltpu.make_async_copy(
            done_o.at[n], out_out.at[:, span(n * tile_o, tile_o)], out_sem.at[3, n]
        )

    stages_o, stages_q = reduce_o.stages(), reduce_q.stages()
    delays = (1, 3, 4, 5, 6, 7)
    last = len(delays) - 1
    half = rows // band // 2

    def slot_step(slot):
        @pl.when(slot + EARLY_CHUNKS < groups)
        def _():
            for expert in range(experts):
                late.finish(slot + EARLY_CHUNKS, expert)

        pl.when(slot < pairs)(lambda: attend_pair(slot))
        for s in range(last, -1, -1):
            n = slot - delays[s]

            @pl.when((n >= 0) & (n < pairs))
            def _(s=s, n=n):
                stages_q[s](n)
                if s == last:
                    for copy in store_q(n):
                        copy.start()

            @pl.when(slot == delays[s] - 1)
            def _(s=s):
                for n in range(out_chunks):
                    stages_o[s](n)
                    if s == last:
                        store_o(n).start()

        @pl.when(slot == pairs)
        def _():
            loads[4].wait()
            every(0, half, input_band)

        pl.when(slot == pairs + 1)(lambda: every(half, 2 * half, input_band))
        pl.when(slot == pairs + 2)(smalls.swap)
        pl.when(slot == pairs + 3)(smalls.cross)
        pl.when(slot == pairs + 4)(smalls.spread)

        @pl.when(slot == pairs + 3)
        def _():
            late.arrived(EARLY_CHUNKS, groups, experts)
            every(0, 2 * EARLY_CHUNKS, lambda n: early_rows(n).wait())
            every(0, rows // band, output_band)

    every(0, pairs + delays[-1], slot_step)
    smalls.finish()

    def stored(i):
        for copy in store_q(i):
            copy.wait()

    every(0, pairs, stored)
    for n in range(out_chunks):
        store_o(n).wait()
    late.drain(EARLY_CHUNKS, groups, experts)
    reduce_o.drain()
    reduce_q.drain()
    smalls.drain()


def run_back(
    owners, capacity, gates, home_grad, far_sums, near_sums, home_out, back, hidden, cotangent, tokens,
    vectors, router_grad, act_t, merged_t, qkv, weight, w_out, low, high,
):
    rows, width = tokens.shape
    shard = width // 4
    lead = 8 + gates
    groups = owners // 2
    pairs = width // LANES
    tile_o = min(512, width)
    out_chunks = width // tile_o
    count = owners // 2
    half = shard // 2
    mid = rows // 2
    any_spec = pl.BlockSpec(memory_space=pl.ANY)
    vmem_spec = pl.BlockSpec(memory_space=pltpu.VMEM)
    bf16, f32 = jnp.bfloat16, jnp.float32
    dma = pltpu.SemaphoreType.DMA

    def vm(*shape):
        return pltpu.VMEM(shape, bf16)

    def fm(*shape):
        return pltpu.VMEM(shape, f32)

    def reduce_buffers(chunks, tile):
        return [
            vm(chunks, 2, 2, shard, tile),
            vm(chunks, 2, shard, tile),
            vm(chunks, shard, tile),
            vm(chunks, half, tile),
            vm(chunks, count, half // count, tile),
            vm(chunks, shard, tile),
        ]

    def reduce_sems(chunks):
        return [dma((4, chunks)), dma((4, chunks)), dma((2, chunks, count)), dma((2, chunks, count))]

    return pl.pallas_call(
        functools.partial(back_kernel, (owners, capacity, gates)),
        out_shape=(
            jax.ShapeDtypeStruct((rows, width), bf16),
            jax.ShapeDtypeStruct((rows, width), f32),
            jax.ShapeDtypeStruct((8, shard), f32),
            jax.ShapeDtypeStruct((gates, shard), f32),
            jax.ShapeDtypeStruct((shard, 3 * width), bf16),
            jax.ShapeDtypeStruct((shard, width), bf16),
        ),
        in_specs=[vmem_spec] * 7 + [any_spec] * 10,
        out_specs=(vmem_spec,) * 4 + (any_spec,) * 2,
        scratch_shapes=[
            vm(*near_sums.shape),
            vm(*near_sums.shape),
            vm(*home_grad.shape),
            vm(*home_grad.shape),
            vm(width, rows),
            vm(width, rows),
            vm(rows, 3 * width),
            vm(width, 3 * width),
            vm(width, width),
            vm(2, 2, mid, mid),
            vm(2, 2, mid, rows),
            vm(rows, width),
            vm(rows, width),
        ]
        + reduce_buffers(pairs, 3 * LANES)
        + reduce_buffers(out_chunks, tile_o)
        + [
            fm(lead, width),
            fm(2, 2, lead, shard),
            fm(2, lead, shard),
            fm(lead, shard),
            fm(lead, shard),
            fm(lead, shard),
            fm(owners, lead, shard),
            dma((6,)),
            dma((2, 2)),
            dma((near_sums.shape[0],)),
            dma((owners,)),
            dma((groups, near_sums.shape[0])),
            dma((groups, near_sums.shape[0])),
            dma((owners, near_sums.shape[0])),
            dma((owners, near_sums.shape[0])),
        ]
        + reduce_sems(pairs)
        + reduce_sems(out_chunks)
        + [dma((2,)), dma((2,)), dma((owners,)), dma((owners,)), dma((4, pairs))],
        compiler_params=pltpu.CompilerParams(
            collective_id=2, has_side_effects=True, vmem_limit_bytes=VMEM_LIMIT
        ),
        name="back",
    )(
        home_grad, back, hidden, cotangent, tokens, vectors, router_grad,
        far_sums, near_sums, home_out, act_t, merged_t, qkv, weight, w_out, low, high,
    )


def widen_kernel(*refs):
    count = len(refs) // 2
    for src, dst in zip(refs[:count], refs[count:]):
        dst[...] = src[...].astype(dst.dtype)


def widen(steps, values, kinds):
    def spec(value):
        if value.shape[0] % (16 * steps):
            return pl.BlockSpec(value.shape, lambda i: (0, 0))
        return pl.BlockSpec((value.shape[0] // steps, value.shape[1]), lambda i: (i, 0))

    return pl.pallas_call(
        widen_kernel,
        grid=(steps,),
        in_specs=[spec(value) for value in values],
        out_specs=[spec(value) for value in values],
        out_shape=[
            jax.ShapeDtypeStruct(value.shape, kind) for value, kind in zip(values, kinds)
        ],
        name="widen",
    )(*values)


def on_device_plain(
    tokens,
    norm1_gain,
    norm1_shift,
    w_qkv,
    w_out,
    norm2_gain,
    norm2_shift,
    w_router,
    w_up,
    w_down,
    routes,
    priority,
    prefix,
    cotangent,
):
    row_count, model_width = tokens.shape
    expert_count = w_router.shape[1]
    capacity = row_count // expert_count
    owners = lax.axis_size("expert")
    local_experts = w_up.shape[0]
    slot_count = expert_count * capacity
    prefix_len = prefix[0]
    small = jnp.concatenate(
        [
            norm1_gain[None],
            norm1_shift[None],
            norm2_gain[None],
            norm2_shift[None],
            w_router.T,
        ],
        axis=0,
    )
    qkv_full = lax.all_gather(w_qkv, "wshard", axis=0, tiled=True)
    small_full = lax.all_gather(small, "wshard", axis=1, tiled=True)
    out_full = lax.all_gather(w_out, "wshard", axis=0, tiled=True)
    gain_one, shift_one, gain_two, shift_two = (small_full[i] for i in range(4))
    router_full = small_full[4:].T
    gain_one = gain_one.astype(jnp.float32)
    gain_two = gain_two.astype(jnp.float32)
    inputs = tokens.astype(jnp.float32)
    normed_one, scaled_one, inverse_one = normalize(inputs, gain_one, shift_one.astype(jnp.float32))
    act_one = normed_one.astype(jnp.bfloat16)
    qkv = jnp.dot(act_one, qkv_full, preferred_element_type=jnp.float32).astype(jnp.bfloat16)
    query_heads = qkv[:, :model_width]
    key_heads = qkv[:, model_width : 2 * model_width]
    value_heads = qkv[:, 2 * model_width :]
    merged, log_totals = attend_forward(query_heads, key_heads, value_heads, prefix_len)
    attn_out = jnp.dot(merged, out_full, preferred_element_type=jnp.float32)
    hidden = inputs + attn_out
    normed_two, scaled_two, inverse_two = normalize(hidden, gain_two, shift_two.astype(jnp.float32))
    act_two = normed_two.astype(jnp.bfloat16)
    logits = jnp.dot(act_two, router_full, preferred_element_type=jnp.float32)
    row_max = jnp.max(logits, axis=-1, keepdims=True)
    exponent = jnp.exp(logits - row_max)
    gate_prob = exponent / jnp.sum(exponent, axis=-1, keepdims=True)
    route_ids = routes[:, 0]
    chosen = route_ids[:, None] == jnp.arange(expert_count, dtype=jnp.int32)[None, :]
    gate_value = jnp.sum(jnp.where(chosen, gate_prob, 0.0), axis=1)
    slot_index, slot_source = assign_slots(route_ids, priority[0], expert_count, capacity)
    zero_row = jnp.zeros((1, model_width), jnp.bfloat16)
    padded = jnp.concatenate([act_two, zero_row], axis=0)
    send_rows = padded[slot_source].reshape(owners, local_experts * capacity, model_width)
    arrived = lax.all_to_all(send_rows, "expert", split_axis=0, concat_axis=0, tiled=True).reshape(
        owners, local_experts, capacity, model_width
    )
    group = lax.axis_size("wshard")
    local_rows = owners * capacity

    def by_expert(chunk):
        rows = jnp.transpose(chunk, (1, 0, 2, 3)).reshape(local_experts, local_rows, model_width)
        return lax.all_gather(rows, "wshard", axis=1, tiled=True)

    def home_rows(rows):
        own = lax.psum_scatter(rows.astype(jnp.bfloat16), "wshard", scatter_dimension=1, tiled=True)
        own = own.reshape(local_experts, owners, capacity, model_width)
        return jnp.transpose(own, (1, 0, 2, 3)).reshape(
            owners, local_experts * capacity, model_width
        )

    grad_output = cotangent.astype(jnp.float32)
    grad_combined = (gate_value[:, None] * grad_output).astype(jnp.bfloat16)
    grad_padded = jnp.concatenate([grad_combined, zero_row], axis=0)
    grad_send = grad_padded[slot_source].reshape(owners, local_experts * capacity, model_width)
    grad_arrived = lax.all_to_all(
        grad_send, "expert", split_axis=0, concat_axis=0, tiled=True
    ).reshape(owners, local_experts, capacity, model_width)
    rows_in = by_expert(arrived)
    grad_rows = by_expert(grad_arrived)
    pre_act = jnp.einsum("erd,edf->erf", rows_in, w_up, preferred_element_type=jnp.float32)
    activated, gelu_pull = jax.vjp(gelu_tanh, pre_act)
    act_hidden = activated.astype(jnp.bfloat16)
    produced = jnp.einsum(
        "erf,efd->erd", act_hidden, w_down, preferred_element_type=jnp.float32
    )
    expert_out = home_rows(produced)
    returned = lax.all_to_all(expert_out, "expert", split_axis=0, concat_axis=0, tiled=True)
    slots_back = jnp.concatenate([returned.reshape(slot_count, model_width), zero_row], axis=0)
    combined = slots_back[slot_index].astype(jnp.float32)
    output = (hidden + gate_value[:, None] * combined).astype(jnp.bfloat16)
    grad_gate = jnp.sum(grad_output * combined, axis=1)
    grad_down = jnp.einsum(
        "erf,erd->efd", act_hidden, grad_rows, preferred_element_type=jnp.float32
    )
    grad_hidden_units = jnp.einsum(
        "erd,efd->erf", grad_rows, w_down, preferred_element_type=jnp.float32
    )
    grad_pre = gelu_pull(grad_hidden_units)[0].astype(jnp.bfloat16)
    grad_up = jnp.einsum("erd,erf->edf", rows_in, grad_pre, preferred_element_type=jnp.float32)
    grad_expert_in = jnp.einsum(
        "erf,edf->erd", grad_pre, w_up, preferred_element_type=jnp.float32
    )
    grad_send_back = home_rows(grad_expert_in)
    grad_back = lax.all_to_all(grad_send_back, "expert", split_axis=0, concat_axis=0, tiled=True)
    grad_slots = jnp.concatenate([grad_back.reshape(slot_count, model_width), zero_row], axis=0)
    grad_act_two = grad_slots[slot_index].astype(jnp.float32)
    grad_logits = (
        gate_prob * (jnp.where(chosen, grad_gate[:, None], 0.0) - (gate_value * grad_gate)[:, None])
    ).astype(jnp.bfloat16)
    grad_router = contract_rows(act_two, grad_logits)
    grad_act_two = grad_act_two + times_transpose(grad_logits, router_full)
    grad_from_two, grad_gain_two, grad_shift_two = norm_back(
        grad_act_two, scaled_two, inverse_two, gain_two
    )
    grad_hidden = grad_output + grad_from_two
    grad_attn = grad_hidden.astype(jnp.bfloat16)
    grad_out_w = contract_rows(merged, grad_attn)
    grad_merged = times_transpose(grad_attn, out_full).astype(jnp.bfloat16)
    grad_qkv = attend_backward(
        query_heads, key_heads, value_heads, grad_merged, log_totals, prefix_len
    )
    grad_qkv_w = contract_rows(act_one, grad_qkv)
    grad_act_one = times_transpose(grad_qkv, qkv_full)
    grad_from_one, grad_gain_one, grad_shift_one = norm_back(
        grad_act_one, scaled_one, inverse_one, gain_one
    )
    grad_tokens = grad_hidden + grad_from_one
    small_grad = jnp.concatenate(
        [
            grad_gain_one[None],
            grad_shift_one[None],
            grad_gain_two[None],
            grad_shift_two[None],
            grad_router.T,
        ],
        axis=0,
    )
    out_share = lax.psum_scatter(
        grad_out_w.astype(jnp.bfloat16), "wshard", scatter_dimension=0, tiled=True
    )
    qkv_share = lax.psum_scatter(
        grad_qkv_w.astype(jnp.bfloat16), "wshard", scatter_dimension=0, tiled=True
    )
    small_share = lax.psum_scatter(small_grad, "wshard", scatter_dimension=1, tiled=True)
    out_total = lax.psum(out_share, "expert").astype(jnp.float32)
    qkv_total = lax.psum(qkv_share, "expert").astype(jnp.float32)
    small_total = lax.psum(small_share, "expert")
    totals = (
        small_total[0],
        small_total[1],
        qkv_total,
        out_total,
        small_total[2],
        small_total[3],
        small_total[4:].T,
    )
    return (
        output,
        grad_tokens,
        totals[0],
        totals[1],
        totals[2],
        totals[3],
        totals[4],
        totals[5],
        totals[6],
        grad_up,
        grad_down,
    )


def on_device(
    tokens,
    norm1_gain,
    norm1_shift,
    w_qkv,
    w_out,
    norm2_gain,
    norm2_shift,
    w_router,
    w_up,
    w_down,
    routes,
    priority,
    prefix,
    cotangent,
):
    row_count, model_width = tokens.shape
    expert_count = w_router.shape[1]
    capacity = row_count // expert_count
    owners = lax.axis_size("expert")
    experts = w_up.shape[0]
    which = lax.broadcasted_iota(jnp.int32, (16, norm1_gain.shape[0]), 0)
    small = jnp.zeros(which.shape, jnp.bfloat16)
    for i, vector in enumerate((norm1_gain, norm1_shift, norm2_gain, norm2_shift)):
        small = jnp.where(which == i, vector[None], small)
    (
        qkv, act_t, merged_t, back, weight, out_full, low, high, grad_rows, hidden, send_rows,
        vectors, router,
    ) = run_front(
        owners, experts, capacity, prefix, routes.reshape(1, row_count), priority, tokens,
        cotangent, small, w_router.T, w_qkv, w_out,
    )
    far_sums, near_sums, home_out, home_grad, grad_up, grad_down, grad_router = run_experts(
        owners, capacity, expert_count, send_rows, grad_rows, w_up, w_down, router
    )
    output, grad_tokens, grad_vectors, grad_gates, grad_qkv, grad_out = run_back(
        owners, capacity, expert_count, home_grad, far_sums, near_sums, home_out, back, hidden, cotangent,
        tokens, vectors, grad_router, act_t, merged_t, qkv, weight, out_full, low, high,
    )
    f32 = jnp.float32
    units = w_up.shape[2]
    output, grad_tokens, grad_vectors, grad_gates, grad_qkv, grad_out, grad_up, grad_down = widen(
        16,
        (
            output, grad_tokens, grad_vectors, grad_gates, grad_qkv, grad_out,
            grad_up.reshape(-1, units), grad_down.reshape(-1, model_width),
        ),
        (output.dtype,) + (f32,) * 7,
    )
    return (
        output,
        grad_tokens,
        grad_vectors[0],
        grad_vectors[1],
        grad_qkv,
        grad_out,
        grad_vectors[2],
        grad_vectors[3],
        grad_gates.T,
        grad_up.reshape(w_up.shape),
        grad_down.reshape(w_down.shape),
    )


def solution(mesh):
    placed = (
        P(("expert", "wshard"), None),
        P("wshard"),
        P("wshard"),
        P("wshard", None),
        P("wshard", None),
        P("wshard"),
        P("wshard"),
        P("wshard", None),
        P("expert", None, "wshard"),
        P("expert", "wshard", None),
        P(("expert", "wshard"), None),
        P(("expert", "wshard"), None),
        P(("expert", "wshard")),
        P(("expert", "wshard"), None),
    )
    owners, group = mesh.shape["expert"], mesh.shape["wshard"]

    def body(*args):
        capacity = args[0].shape[0] // args[7].shape[1]
        fits = group == 4 and owners == 8 and capacity % 16 == 0 and args[7].shape[1] % 16 == 0
        return (on_device if fits else on_device_plain)(*args)

    return jax.shard_map(
        body,
        mesh=mesh,
        in_specs=placed,
        out_specs=(
            P(("expert", "wshard"), None),
            P(("expert", "wshard"), None),
            P("wshard"),
            P("wshard"),
            P("wshard", None),
            P("wshard", None),
            P("wshard"),
            P("wshard"),
            P("wshard", None),
            P("expert", None, "wshard"),
            P("expert", "wshard", None),
        ),
        check_vma=False,
    )
```

```python
import functools
import math

import jax
import jax.numpy as jnp
from jax import lax
from jax.experimental import pallas as pl
from jax.experimental.pallas import tpu as pltpu
from jax.sharding import PartitionSpec as P

HEADS = 16
HEAD_DIM = 64


epsilon = 1e-05
VMEM_LIMIT = 66_000_000
TILE = 1024
EARLY_CHUNKS = 1


def normalize(values, gain_vec, shift_vec):
    row_mean = jnp.mean(values, axis=-1, keepdims=True)
    centered = values - row_mean
    inverse = lax.rsqrt(jnp.mean(centered * centered, axis=-1, keepdims=True) + epsilon)
    scaled = centered * inverse
    return (scaled * gain_vec + shift_vec, scaled, inverse)


def norm_back(grad_rows, scaled, inverse, gain_vec):
    weighted = grad_rows * gain_vec
    mean_one = jnp.mean(weighted, axis=-1, keepdims=True)
    mean_two = jnp.mean(weighted * scaled, axis=-1, keepdims=True)
    grad_inputs = inverse * (weighted - mean_one - scaled * mean_two)
    return (grad_inputs, jnp.sum(grad_rows * scaled, axis=0), jnp.sum(grad_rows, axis=0))


def contract_rows(left, right):
    return lax.dot_general(
        left, right, (((0,), (0,)), ((), ())), preferred_element_type=jnp.float32
    )


def times_transpose(left, right):
    return lax.dot_general(
        left, right, (((1,), (1,)), ((), ())), preferred_element_type=jnp.float32
    )


def gelu_tanh(values):
    return jax.nn.gelu(values, approximate=True)


def assign_slots(route_ids, order_ids, expert_count, capacity):
    token_count = route_ids.shape[0]
    same_expert = route_ids[:, None] == route_ids[None, :]
    earlier = order_ids[None, :] < order_ids[:, None]
    rank_ids = jnp.sum((same_expert & earlier).astype(jnp.int32), axis=1)
    is_kept = rank_ids < capacity
    slot_index = jnp.where(is_kept, route_ids * capacity + rank_ids, expert_count * capacity)
    slot_ids = jnp.arange(expert_count * capacity, dtype=jnp.int32)
    match_table = slot_index[None, :] == slot_ids[:, None]
    token_ids = jnp.arange(token_count, dtype=jnp.int32)
    filled = jnp.any(match_table, axis=1)
    picked = jnp.sum(jnp.where(match_table, token_ids[None, :], 0), axis=1)
    slot_source = jnp.where(filled, picked, token_count)
    return (slot_index, slot_source)


def group_heads(values, groups):
    token_count = values.shape[0]
    return jnp.transpose(values.reshape(token_count, groups, -1, HEAD_DIM), (1, 0, 2, 3))


def block_scores(query_block, key_group, block_start, prefix_len):
    block_rows = query_block.shape[0]
    key_count = key_group.shape[0]
    scores = jnp.einsum(
        "qgd,kgd->gqk", query_block, key_group, preferred_element_type=jnp.float32
    ) * (1.0 / math.sqrt(HEAD_DIM))
    query_pos = block_start + jnp.arange(block_rows, dtype=jnp.int32)
    key_pos = jnp.arange(key_count, dtype=jnp.int32)
    allowed = (key_pos[None, :] <= query_pos[:, None]) | (key_pos[None, :] < prefix_len)
    return jnp.where(allowed[None], scores, -1e30)


def attend_forward(query_heads, key_heads, value_heads, prefix_len):
    token_count = query_heads.shape[0]
    group_size = min(4, HEADS)
    groups = HEADS // group_size
    block_rows = min(512, token_count)
    blocks = token_count // block_rows
    starts = jnp.arange(blocks, dtype=jnp.int32) * block_rows

    def one_group(group_item):
        query_group, key_group, value_group = group_item
        query_blocks = query_group.reshape(blocks, block_rows, group_size, HEAD_DIM)

        def one_block(block_item):
            query_block, block_start = block_item
            scores = block_scores(query_block, key_group, block_start, prefix_len)
            row_max = jnp.max(scores, axis=-1, keepdims=True)
            exponent = jnp.exp(scores - row_max)
            row_total = jnp.sum(exponent, axis=-1, keepdims=True)
            attn_probs = (exponent / row_total).astype(jnp.bfloat16)
            result = jnp.einsum(
                "gqk,kgd->qgd", attn_probs, value_group, preferred_element_type=jnp.float32
            )
            return (result, (row_max + jnp.log(row_total))[..., 0])

        return lax.map(one_block, (query_blocks, starts))

    attended, log_totals = lax.map(
        one_group,
        (
            group_heads(query_heads, groups),
            group_heads(key_heads, groups),
            group_heads(value_heads, groups),
        ),
    )
    merged = (
        jnp.transpose(attended, (1, 2, 0, 3, 4))
        .reshape(token_count, HEADS * HEAD_DIM)
        .astype(jnp.bfloat16)
    )
    return (merged, log_totals)


def attend_backward(query_heads, key_heads, value_heads, grad_merged, log_totals, prefix_len):
    token_count = query_heads.shape[0]
    group_size = min(4, HEADS)
    groups = HEADS // group_size
    block_rows = min(512, token_count)
    blocks = token_count // block_rows
    starts = jnp.arange(blocks, dtype=jnp.int32) * block_rows
    score_scale = 1.0 / math.sqrt(HEAD_DIM)

    def one_group(group_item):
        query_group, key_group, value_group, grad_group, total_group = group_item
        query_blocks = query_group.reshape(blocks, block_rows, group_size, HEAD_DIM)
        grad_blocks = grad_group.reshape(blocks, block_rows, group_size, HEAD_DIM)

        def one_block(carry, block_item):
            grad_keys, grad_vals = carry
            query_block, grad_block, total_block, block_start = block_item
            scores = block_scores(query_block, key_group, block_start, prefix_len)
            attn_probs = jnp.exp(scores - total_block[..., None])
            grad_probs = jnp.einsum(
                "qgd,kgd->gqk", grad_block, value_group, preferred_element_type=jnp.float32
            )
            row_delta = jnp.sum(attn_probs * grad_probs, axis=-1, keepdims=True)
            grad_scores = (attn_probs * (grad_probs - row_delta)).astype(jnp.bfloat16)
            grad_vals = grad_vals + jnp.einsum(
                "gqk,qgd->kgd",
                attn_probs.astype(jnp.bfloat16),
                grad_block,
                preferred_element_type=jnp.float32,
            )
            grad_keys = (
                grad_keys
                + jnp.einsum(
                    "gqk,qgd->kgd", grad_scores, query_block, preferred_element_type=jnp.float32
                )
                * score_scale
            )
            grad_query = (
                jnp.einsum(
                    "gqk,kgd->qgd", grad_scores, key_group, preferred_element_type=jnp.float32
                )
                * score_scale
            )
            return ((grad_keys, grad_vals), grad_query)

        zero_keys = jnp.zeros(key_group.shape, jnp.float32)
        carried, grad_queries = lax.scan(
            one_block, (zero_keys, zero_keys), (query_blocks, grad_blocks, total_group, starts)
        )
        return (grad_queries, carried[0], carried[1])

    grad_queries, grad_keys, grad_vals = lax.map(
        one_group,
        (
            group_heads(query_heads, groups),
            group_heads(key_heads, groups),
            group_heads(value_heads, groups),
            group_heads(grad_merged, groups),
            log_totals,
        ),
    )
    query_part = jnp.transpose(grad_queries, (1, 2, 0, 3, 4)).reshape(token_count, HEADS * HEAD_DIM)
    key_part = jnp.transpose(grad_keys, (1, 0, 2, 3)).reshape(token_count, HEADS * HEAD_DIM)
    value_part = jnp.transpose(grad_vals, (1, 0, 2, 3)).reshape(token_count, HEADS * HEAD_DIM)
    return jnp.concatenate([query_part, key_part, value_part], axis=1).astype(jnp.bfloat16)


MESH = pl.DeviceIdType.MESH
LANES = 128


def dot_nn(left, right):
    return lax.dot_general(
        left, right, (((1,), (0,)), ((), ())), preferred_element_type=jnp.float32
    )


def dot_nt(left, right):
    return lax.dot_general(
        left, right, (((1,), (1,)), ((), ())), preferred_element_type=jnp.float32
    )


def dot_tn(left, right):
    return lax.dot_general(
        left, right, (((0,), (0,)), ((), ())), preferred_element_type=jnp.float32
    )


def span(start, size):
    return pl.ds(pl.multiple_of(start, size), size)


def every(start, stop, step):
    def body(i, carry):
        step(i)
        return carry

    lax.fori_loop(start, stop, body, 0)


class Place:
    def __init__(self, owners):
        self.owners = owners
        self.e = lax.axis_index("expert")
        self.w = lax.axis_index("wshard")
        self.c = lax.rem(self.w, 2)
        self.x = lax.div(self.w, 2)
        self.sib = self.w + 1 - 2 * self.c
        self.far = lax.rem(self.w + 2, 4)
        self.diag = 3 - self.w
        self.pair = self.e + 1 - 2 * lax.rem(self.e, 2)

    def ahead(self, k):
        return lax.rem(self.e + k, self.owners)

    def peer(self, n):
        other = lax.div(n, 2) + lax.rem(n, 2) * (self.owners // 2)
        result, bit = 0, 1
        while bit < self.owners:
            result = result + bit * lax.rem(lax.div(self.e, bit) + lax.div(other, bit), 2)
            bit *= 2
        return result


def remote(src, dst, send, recv, device):
    return pltpu.make_async_remote_copy(
        src_ref=src,
        dst_ref=dst,
        send_sem=send,
        recv_sem=recv,
        device_id=device,
        device_id_type=MESH,
    )


def greet(peers):
    barrier = pltpu.get_barrier_semaphore()
    for peer in peers:
        pl.semaphore_signal(barrier, inc=1, device_id=peer, device_id_type=MESH)
    pl.semaphore_wait(barrier, len(peers))


def either(test, yes, no):
    pl.when(test)(yes)
    pl.when(jnp.logical_not(test))(no)


class Dispatch:
    def __init__(self, place, capacity, send_ref, rows_ref, sems):
        self.p, self.cap, self.src, self.rows = place, capacity, send_ref, rows_ref
        self.own_sem, self.send, self.recv = sems

    def slice(self, k, core, side):
        start = (((lax.div(k, 2) * 2 + core) * 2 + side) * 2 + lax.rem(k, 2)) * self.cap
        return self.rows.at[:, span(start, self.cap)]

    def own(self):
        return pltpu.make_async_copy(
            self.src.at[self.p.e], self.slice(0, self.p.c, self.p.x), self.own_sem
        )

    def direct(self, k):
        return remote(
            self.src.at[self.p.peer(k)],
            self.slice(k, self.p.c, self.p.x),
            self.send.at[0, k],
            self.recv.at[0, k],
            (self.p.peer(k), self.p.w),
        )

    def hop(self, k, side, which, peer):
        part = self.slice(k, self.p.c, side)
        return remote(
            part, part, self.send.at[which, k], self.recv.at[which, k], (self.p.e, peer)
        )

    def to_sib(self, k):
        return self.hop(k, self.p.x, 1, self.p.sib)

    def to_far(self, k):
        return self.hop(k, self.p.x, 2, self.p.far)

    def relayed(self, k):
        return self.hop(k, 1 - self.p.x, 3, self.p.sib)

    def start(self):
        self.own().start()
        every(1, self.p.owners, lambda k: self.direct(k).start())

    def forward(self, k):
        k = jnp.int32(k)

        @pl.when(k == 0)
        def _():
            self.own().wait()

        @pl.when(k > 0)
        def _():
            self.direct(k).wait_recv()

        self.to_far(k).start()
        self.to_sib(k).start()

    def relay(self, k):
        self.to_far(k).wait_recv()
        self.relayed(k).start()

    def ready(self, k):
        self.to_sib(k).wait_recv()
        self.relayed(k).wait_recv()

    def order(self):
        return (0, 2, 4, 1, 6, 3, 5, 7)

    def drain(self):
        every(1, self.p.owners, lambda k: self.direct(k).wait_send())

        def rest(k):
            self.to_sib(k).wait_send()
            self.to_far(k).wait_send()
            self.relayed(k).wait_send()

        every(0, self.p.owners, rest)


class Return:
    def __init__(self, place, capacity, part, got, mid, far, done, home, sems):
        self.p, self.cap = place, capacity
        self.part, self.got, self.mid, self.far, self.done, self.home = (
            part, got, mid, far, done, home,
        )
        self.own_sem, self.send, self.recv, self.home_send, self.home_recv = sems

    def swapped(self, j, expert):
        size = 4 * self.cap
        return remote(
            self.part.at[expert, span((j * 2 + 1 - self.p.c) * size, size)],
            self.got.at[expert, span(j * size, size)],
            self.send.at[0, j, expert],
            self.recv.at[0, j, expert],
            (self.p.e, self.p.sib),
        )

    def crossed(self, j, expert):
        part = span(j * 2 * self.cap, 2 * self.cap)
        return remote(
            self.mid.at[expert, part],
            self.far.at[expert, part],
            self.send.at[1, j, expert],
            self.recv.at[1, j, expert],
            (self.p.e, self.p.far),
        )

    def own(self, expert):
        return pltpu.make_async_copy(
            self.done.at[0, expert], self.home.at[self.p.e, expert], self.own_sem.at[expert]
        )

    def homed(self, n, expert):
        return remote(
            self.done.at[n, expert],
            self.home.at[self.p.e, expert],
            self.home_send.at[n, expert],
            self.home_recv.at[n, expert],
            (self.p.peer(n), self.p.w),
        )

    def pair_sum(self, j, expert, side):
        size = 2 * self.cap
        mine = self.part[expert, span(((j * 2 + self.p.c) * 2 + side) * size, size), :]
        theirs = self.got[expert, span((j * 2 + side) * size, size), :]
        return mine.astype(jnp.float32) + theirs.astype(jnp.float32)

    def swap(self, j, expert):
        self.swapped(j, expert).start()

    def split(self, j, expert):
        self.swapped(j, expert).wait_recv()
        here = span(j * 2 * self.cap, 2 * self.cap)
        self.mid[expert, here, :] = self.pair_sum(j, expert, 1 - self.p.x).astype(jnp.bfloat16)
        self.keep[expert, here, :] = self.pair_sum(j, expert, self.p.x).astype(jnp.bfloat16)

    def cross(self, j, expert):
        self.swapped(j, expert).wait_recv()
        here = span(j * 2 * self.cap, 2 * self.cap)
        self.mid[expert, here, :] = self.pair_sum(j, expert, 1 - self.p.x).astype(jnp.bfloat16)
        self.crossed(j, expert).start()

    def this_side(self, j, expert):
        return self.pair_sum(j, expert, self.p.x)

    def finish(self, j, expert):
        self.crossed(j, expert).wait_recv()
        here = span(j * 2 * self.cap, 2 * self.cap)
        total = self.this_side(j, expert) + self.far[expert, here, :].astype(jnp.float32)
        total = total.astype(jnp.bfloat16)
        self.done[2 * j, expert] = total[: self.cap]
        self.done[2 * j + 1, expert] = total[self.cap :]
        j = jnp.int32(j)
        self.homed(2 * j + 1, expert).start()
        either(
            j == 0,
            lambda: self.own(expert).start(),
            lambda: self.homed(2 * j, expert).start(),
        )

    def drain_swaps(self, chunks, experts):
        for expert in range(experts):
            every(0, chunks, lambda j: self.swapped(j, expert).wait_send())

    def drain(self, first, last, experts):
        for expert in range(experts):
            every(first, last, lambda j: self.crossed(j, expert).wait_send())
            every(
                max(1, 2 * first), 2 * last, lambda n: self.homed(n, expert).wait_send()
            )

    def arrived(self, first, last, experts):
        for expert in range(experts):
            if first == 0 and last > 0:
                self.own(expert).wait()
            every(
                max(1, 2 * first), 2 * last, lambda n: self.homed(n, expert).wait_recv()
            )


class LateReturn(Return):
    def crossed(self, j, expert):
        part = span(j * 2 * self.cap, 2 * self.cap)
        return remote(
            self.mid.at[expert, part],
            self.far.at[expert, part],
            self.send.at[j, expert],
            self.recv.at[j, expert],
            (self.p.e, self.p.far),
        )

    def this_side(self, j, expert):
        here = span(j * 2 * self.cap, 2 * self.cap)
        return self.part[expert, here, :].astype(jnp.float32)


def gelu_pair(v):
    root = math.sqrt(2.0 / math.pi)
    square = v * v
    t = jnp.tanh(v * (root + (root * 0.044715) * square))
    half = 0.5 + 0.5 * t
    slope = half + (half * (1.0 - t)) * (v * (root + (3.0 * root * 0.044715) * square))
    return v * half, slope


def expert_kernel(
    dims,
    send_ref, grads_hbm, up_hbm, down_hbm, router_ref,
    far_sums, near_sums, home_out, home_grad, up_out, down_out, router_grad,
    rows, grads, scaled, hidden, pre, up, down, grad_up, grad_down,
    part_out, part_grad, got_out, got_grad, mid_out, mid_grad,
    keep_out, far_grad, far_out, done_grad, done_out,
    load_sem, own_sem, disp_send, disp_recv, red_send, red_recv, home_send, home_recv,
):
    owners, experts, capacity, width, units, expert_count = dims
    place = Place(owners)
    loads = [
        pltpu.make_async_copy(src, dst, load_sem.at[i])
        for i, (src, dst) in enumerate(
            [(up_hbm, up), (grads_hbm, grads), (down_hbm, down)]
        )
    ]
    for load in loads:
        load.start()
    greet(
        [(place.ahead(k), place.w) for k in range(1, owners)]
        + [(place.e, place.sib), (place.e, place.far)]
    )
    dispatch = Dispatch(
        place, capacity, send_ref, rows, (own_sem.at[0, 0], disp_send, disp_recv)
    )
    ret_grad = Return(
        place, capacity, part_grad, got_grad, mid_grad, far_grad, done_grad, home_grad,
        (own_sem.at[1], red_send.at[0], red_recv.at[0], home_send.at[0], home_recv.at[0]),
    )
    ret_out = Return(
        place, capacity, part_out, got_out, mid_out, far_out, done_out, home_out,
        (own_sem.at[2], red_send.at[1], red_recv.at[1], home_send.at[1], home_recv.at[1]),
    )
    dispatch.start()
    router_grad[...] = jnp.zeros_like(router_grad)
    tile = min(TILE, units)
    wide = min(TILE, width)
    chunks = owners // 2
    early = EARLY_CHUNKS
    size = 8 * capacity
    lane = lax.broadcasted_iota(jnp.int32, (size, LANES), 1)

    def compute(j, expert):
        here = span(j * size, size)
        logits = dot_nt(rows[expert, here, :], router_ref[...])
        logits = jnp.where(lane < expert_count, logits, -1e30)
        exponent = jnp.exp(logits - jnp.max(logits, axis=1, keepdims=True))
        prob = exponent * (1.0 / jnp.sum(exponent, axis=1, keepdims=True))
        mine = lane == place.e * experts + expert
        gate = jnp.sum(jnp.where(mine, prob, 0.0), axis=1, keepdims=True)
        scaled[expert, here, :] = (
            gate * grads[expert, here, :].astype(jnp.float32)
        ).astype(jnp.bfloat16)

        def one_tile(n):
            cols = span(n * tile, tile)
            value, slope = gelu_pair(dot_nn(rows[expert, here, :], up[expert, :, cols]))
            hidden[expert, here, cols] = value.astype(jnp.bfloat16)
            back = pre[expert, here, cols].astype(jnp.float32)
            pre[expert, here, cols] = (gate * back * slope).astype(jnp.bfloat16)

        every(0, units // tile, one_tile)

        def one_out(n, total):
            cols = span(n * wide, wide)
            value = dot_nn(hidden[expert, here, :], down[expert, :, cols])
            part_out[expert, here, cols] = (gate * value).astype(jnp.bfloat16)
            weighted = value * grads[expert, here, cols].astype(jnp.float32)
            for start in range(0, wide, LANES):
                total = total + weighted[:, start : start + LANES]
            return total

        total = lax.fori_loop(
            0, width // wide, one_out, jnp.zeros((size, LANES), jnp.float32)
        )
        grad_gate = jnp.sum(total, axis=1, keepdims=True)
        grad_logits = (
            prob * ((jnp.where(mine, 1.0, 0.0) - gate) * grad_gate)
        ).astype(jnp.bfloat16)

        def one_in(n):
            cols = span(n * wide, wide)
            value = dot_nt(pre[expert, here, :], up[expert, cols, :]) + dot_nn(
                grad_logits, router_ref[:, cols]
            )
            part_grad[expert, here, cols] = value.astype(jnp.bfloat16)
            router_grad[:, cols] += dot_tn(grad_logits, rows[expert, here, cols])

        every(0, width // wide, one_in)

    def unscaled(j, expert):
        here = span(j * size, size)
        pre[expert, here, :] = dot_nt(grads[expert, here, :], down[expert]).astype(jnp.bfloat16)

    block = min(256, width)

    def weight_grads(expert, first, last):
        def one(n):
            part = span(n * block, block)
            grad_down[expert, part, :] = dot_tn(
                hidden[expert, :, part], scaled[expert]
            ).astype(jnp.bfloat16)
            grad_up[expert, part, :] = dot_tn(rows[expert, :, part], pre[expert]).astype(
                jnp.bfloat16
            )

        every(first * width // block // 4, last * width // block // 4, one)

    def keep(expert):
        return [
            pltpu.make_async_copy(src.at[expert], dst.at[expert], load_sem.at[2 * expert + i])
            for i, (src, dst) in enumerate(((grad_up, up_out), (grad_down, down_out)))
        ]

    turns = [(j, expert) for j in range(chunks) for expert in range(experts)]
    ahead, through, here = dispatch.forward, dispatch.relay, dispatch.ready
    plan = [[] for _ in turns]
    for unit, acts in (
        (0, ((here, 0), (here, 1), (ahead, 5))),
        (1, ((through, 6), (ahead, 7))),
        (2, ((through, 3), (here, 2), (here, 3))),
        (3, ((through, 5),)),
        (4, ((through, 7), (here, 4), (here, 5))),
        (6, ((here, 6), (here, 7))),
    ):
        plan[unit].extend(acts)
    for u in range(2, len(turns)):
        done = turns[u - 2]
        plan[u].append((ret_grad.cross,) + done)
        plan[u].append((ret_out.cross if done[0] < early else ret_out.split,) + done)
        if u >= 4:
            done = turns[u - 4]
            plan[u].append((ret_grad.finish,) + done)
            if done[0] < early:
                plan[u].append((ret_out.finish,) + done)
    ret_out.keep = keep_out
    for load in loads:
        load.wait()

    def unscaled_pair(j):
        for expert in range(experts):
            unscaled(j, expert)

    ahead(0)
    unscaled_pair(0)
    unscaled_pair(1)
    ahead(2)
    ahead(4)
    ahead(1)
    unscaled_pair(2)
    through(0)
    unscaled_pair(3)
    through(2)
    ahead(6)
    through(4)
    through(1)
    ahead(3)

    def step(unit):
        for u, acts in enumerate(plan):

            @pl.when(unit == u)
            def _(acts=acts):
                for act, *at in acts:
                    act(*at)

        j, expert = lax.div(unit, experts), lax.rem(unit, experts)
        compute(j, expert)
        ret_grad.swap(j, expert)
        ret_out.swap(j, expert)

    every(0, len(turns), step)
    ret_grad.cross(*turns[-2])
    ret_out.split(*turns[-2])
    ret_grad.finish(*turns[-4])
    weight_grads(0, 0, 1)
    ret_grad.cross(*turns[-1])
    ret_out.split(*turns[-1])
    sums = [
        pltpu.make_async_copy(src, dst, load_sem.at[4 + i])
        for i, (src, dst) in enumerate(((mid_out, far_sums), (keep_out, near_sums)))
    ]
    for store in sums:
        store.start()
    ret_grad.finish(*turns[-3])
    weight_grads(0, 1, 2)
    ret_grad.finish(*turns[-2])
    weight_grads(0, 2, 3)
    ret_grad.finish(*turns[-1])
    weight_grads(0, 3, 4)
    for store in keep(0):
        store.start()
    for expert in range(1, experts):
        weight_grads(expert, 0, 4)
        for store in keep(expert):
            store.start()
    for expert in range(experts):
        for store in keep(expert):
            store.wait()
    for store in sums:
        store.wait()
    dispatch.drain()
    ret_grad.drain_swaps(chunks, experts)
    ret_grad.drain(0, chunks, experts)
    ret_grad.arrived(0, chunks, experts)
    ret_out.drain_swaps(chunks, experts)
    ret_out.drain(0, early, experts)
    ret_out.arrived(0, early, experts)


def run_experts(owners, capacity, expert_count, send_rows, grads, w_up, w_down, router):
    experts, width, units = w_up.shape
    slots = owners * 4 * capacity
    chunks = owners // 2
    dims = (owners, experts, capacity, width, units, expert_count)
    any_spec = pl.BlockSpec(memory_space=pl.ANY)
    vmem_spec = pl.BlockSpec(memory_space=pltpu.VMEM)
    bf16 = jnp.bfloat16
    home = jax.ShapeDtypeStruct((owners, experts, capacity, width), bf16)
    dma = pltpu.SemaphoreType.DMA

    def vm(*shape):
        return pltpu.VMEM(shape, bf16)

    return pl.pallas_call(
        functools.partial(expert_kernel, dims),
        out_shape=(
            jax.ShapeDtypeStruct((experts, slots // 4, width), bf16),
            jax.ShapeDtypeStruct((experts, slots // 4, width), bf16),
            home, home,
            jax.ShapeDtypeStruct(w_up.shape, bf16),
            jax.ShapeDtypeStruct(w_down.shape, bf16),
            jax.ShapeDtypeStruct((LANES, width), jnp.float32),
        ),
        in_specs=[any_spec] * 4 + [vmem_spec],
        out_specs=(any_spec,) * 6 + (vmem_spec,),
        scratch_shapes=[
            vm(experts, slots, width),
            vm(experts, slots, width),
            vm(experts, slots, width),
            vm(experts, slots, units),
            vm(experts, slots, units),
            vm(experts, width, units),
            vm(experts, units, width),
            vm(experts, width, units),
            vm(experts, units, width),
            vm(experts, slots, width),
            vm(experts, slots, width),
            vm(experts, slots // 2, width),
            vm(experts, slots // 2, width),
            vm(experts, slots // 4, width),
            vm(experts, slots // 4, width),
            vm(experts, slots // 4, width),
            vm(experts, slots // 4, width),
            vm(experts, slots // 4, width),
            vm(owners, experts, capacity, width),
            vm(owners, experts, capacity, width),
            dma((6,)),
            dma((3, experts)),
            dma((4, owners)),
            dma((4, owners)),
            dma((2, 2, chunks, experts)),
            dma((2, 2, chunks, experts)),
            dma((2, owners, experts)),
            dma((2, owners, experts)),
        ],
        compiler_params=pltpu.CompilerParams(
            collective_id=1, has_side_effects=True, vmem_limit_bytes=VMEM_LIMIT
        ),
        name="experts",
    )(send_rows, grads, w_up, w_down, router)


def masked_softmax(scores):
    exponent = jnp.exp(scores - jnp.max(scores, axis=1, keepdims=True))
    return exponent * (1.0 / jnp.sum(exponent, axis=1, keepdims=True))


def attend_head(query, key, value, prefix_len):
    half = query.shape[0] // 2
    query = query * (1.0 / math.sqrt(HEAD_DIM))
    row = lax.broadcasted_iota(jnp.int32, (half, half), 0)
    col = lax.broadcasted_iota(jnp.int32, (half, half), 1)
    low = dot_nt(query[:half], key[:half])
    low = jnp.where((col <= row) | (col < prefix_len), low, -1e30)
    low = masked_softmax(low).astype(jnp.bfloat16)
    high = dot_nt(query[half:], key)
    high = jnp.concatenate(
        [high[:, :half], jnp.where(col <= row, high[:, half:], -1e30)], axis=1
    )
    high = masked_softmax(high).astype(jnp.bfloat16)
    return low, high, dot_nn(low, value[:half]), dot_nn(high, value)


def score_grads(probs, grad_probs):
    probs = probs.astype(jnp.float32)
    weighted = probs * grad_probs
    total = jnp.sum(weighted, axis=1, keepdims=True)
    return (weighted - probs * total).astype(jnp.bfloat16)


def attend_back_head(query, key, value, low, high, grad):
    half = query.shape[0] // 2
    scale = 1.0 / math.sqrt(HEAD_DIM)
    query = query * scale
    grad_low = score_grads(low, dot_nt(grad[:half], value[:half]))
    grad_high = score_grads(high, dot_nt(grad[half:], value))
    grad_query = jnp.concatenate(
        [dot_nn(grad_low, key[:half]), dot_nn(grad_high, key)], axis=0
    )
    value_all = dot_tn(high, grad[half:])
    key_all = dot_tn(grad_high, query[half:])
    grad_value = jnp.concatenate(
        [value_all[:half] + dot_tn(low, grad[:half]), value_all[half:]], axis=0
    )
    grad_key = jnp.concatenate(
        [key_all[:half] + dot_tn(grad_low, query[:half]), key_all[half:]], axis=0
    )
    return (
        (grad_query * scale).astype(jnp.bfloat16),
        grad_key.astype(jnp.bfloat16),
        grad_value.astype(jnp.bfloat16),
    )


class Gather:
    def __init__(self, place, pieces, parts, src, dst, sems):
        self.p, self.src, self.dst, self.pieces, self.parts = place, src, dst, pieces, parts
        self.send, self.recv = sems
        self.shard = src.shape[0]
        self.half = self.shard // 2
        self.width = src.shape[1] // parts
        self.step = self.width // pieces
        self.first = lax.rem(place.e, 2) * self.half
        self.second = self.half - self.first

    def cols(self, n, part):
        return span(part * self.width + n * self.step, self.step)

    def block(self, owner, start, size, n, part):
        rows = pl.ds(pl.multiple_of(owner * self.shard + start, self.half), size)
        return self.dst.at[rows, self.cols(n, part)]

    def move(self, which, n, part, src, dst, device):
        return remote(
            src, dst, self.send.at[which, n, part], self.recv.at[which, n, part], device
        )

    def own(self, n, part):
        return pltpu.make_async_copy(
            self.src.at[:, self.cols(n, part)],
            self.block(self.p.w, 0, self.shard, n, part),
            self.recv.at[5, n, part],
        )

    def near(self, n, part):
        return self.move(
            4, n, part, self.src.at[:, self.cols(n, part)],
            self.block(self.p.w, 0, self.shard, n, part), (self.p.e, self.p.sib),
        )

    def hop(self, n, part):
        return self.move(
            0, n, part, self.src.at[span(self.first, self.half), self.cols(n, part)],
            self.block(self.p.w, self.first, self.half, n, part), (self.p.e, self.p.far),
        )

    def pass_from(self, which, start, n, part, device):
        block = self.block(self.p.far, start, self.half, n, part)
        return self.move(which, n, part, block, block, device)

    def pairs(self, n, part):
        return self.pass_from(1, self.first, n, part, (self.p.pair, self.p.w))

    def relay(self, n, part):
        return self.pass_from(2, self.first, n, part, (self.p.e, self.p.sib))

    def pair_relay(self, n, part):
        return self.pass_from(3, self.second, n, part, (self.p.e, self.p.sib))

    def all_parts(self, n, act):
        for part in range(self.parts):
            act(n, part)

    def start_own(self):
        every(
            0, self.pieces, lambda n: self.all_parts(n, lambda n, part: self.own(n, part).start())
        )

    def start(self):
        def hop(n, part):
            self.hop(n, part).start()

        def near(n, part):
            self.near(n, part).start()

        every(0, self.pieces, lambda n: self.all_parts(n, hop))
        every(0, self.pieces, lambda n: self.all_parts(n, near))

    def pass_on(self, n):
        def one(n, part):
            self.hop(n, part).wait_recv()
            self.pairs(n, part).start()
            self.relay(n, part).start()

        self.all_parts(n, one)

    def pass_pair(self, n):
        def one(n, part):
            self.pairs(n, part).wait_recv()
            self.pair_relay(n, part).start()

        self.all_parts(n, one)

    def ready(self, n):
        def one(n, part):
            self.own(n, part).wait()
            for copy in (self.near(n, part), self.relay(n, part), self.pair_relay(n, part)):
                copy.wait_recv()

        self.all_parts(n, one)

    def drain(self):
        def one(n, part):
            for copy in (
                self.hop(n, part), self.pairs(n, part), self.relay(n, part),
                self.pair_relay(n, part), self.near(n, part),
            ):
                copy.wait_send()

        every(0, self.pieces, lambda n: self.all_parts(n, one))


def slot_tables(routes_ref, priority_ref, capacity, pick_ref, back_ref):
    count = routes_ref.shape[1]
    row = lax.broadcasted_iota(jnp.int32, (count, count), 0).astype(jnp.float32)
    col = lax.broadcasted_iota(jnp.int32, (count, count), 1).astype(jnp.float32)
    eye = row == col
    route_row = routes_ref[...].astype(jnp.float32)
    order_row = priority_ref[...].astype(jnp.float32)
    route_col = jnp.sum(jnp.where(eye, route_row, 0.0), axis=1, keepdims=True)
    order_col = jnp.sum(jnp.where(eye, order_row, 0.0), axis=1, keepdims=True)
    same = route_col == route_row
    rank_row = jnp.sum(
        jnp.where(same & (order_col < order_row), 1.0, 0.0), axis=0, keepdims=True
    )
    rank_col = jnp.sum(
        jnp.where(same & (order_row < order_col), 1.0, 0.0), axis=1, keepdims=True
    )
    slots = float(count)
    slot_row = jnp.where(rank_row < capacity, route_row * capacity + rank_row, slots)
    slot_col = jnp.where(rank_col < capacity, route_col * capacity + rank_col, slots)
    pick_ref[...] = jnp.where(slot_row == row, 1.0, 0.0).astype(jnp.bfloat16)
    back_ref[...] = jnp.where(slot_col == col, 1.0, 0.0).astype(jnp.bfloat16)


def norm_stats(value):
    centered = value - jnp.mean(value, axis=1, keepdims=True)
    inverse = lax.rsqrt(jnp.mean(centered * centered, axis=1, keepdims=True) + epsilon)
    return centered * inverse, inverse


def front_kernel(
    dims,
    prefix_ref, routes_ref, priority_ref, tokens_ref, cot_ref, small_hbm, router_hbm, qkv_hbm, out_hbm,
    qkv_out, act_out, merged_out, back_out, weight_out, out_full, low_out, high_out, grads_rows,
    hidden_ref, send_ref, small_out, router_out,
    small, weight, out_w, qkv, act, merged, act_two, turned, pick, back, grads_send, low_buf, high_buf,
    own_sem, disp_send, disp_recv, small_send, small_recv, gat_send, gat_recv, store_sem, prob_sem,
):
    owners, capacity, pieces = dims
    place = Place(owners)
    rows, width = tokens_ref.shape
    shard = qkv_hbm.shape[0]
    gathers = [
        Gather(place, pieces, parts, src, dst, (gat_send.at[i], gat_recv.at[i]))
        for i, (parts, src, dst) in enumerate(((3, qkv_hbm, weight), (1, out_hbm, out_w)))
    ]
    for gather in gathers:
        gather.start_own()
    vectors, gates = small_hbm.shape[0], router_hbm.shape[0]
    small_parts = [
        (small_hbm, small.at[place.w, pl.ds(0, vectors)]),
        (router_hbm, small.at[place.w, pl.ds(vectors, gates)]),
    ]
    own_smalls = [
        pltpu.make_async_copy(src, dst, own_sem.at[3 + i])
        for i, (src, dst) in enumerate(small_parts)
    ]
    for copy in own_smalls:
        copy.start()
    greet(
        [(place.ahead(k), place.w) for k in range(1, owners)]
        + [(place.e, place.sib), (place.e, place.far), (place.e, place.diag)]
    )
    smalls = [
        remote(src, dst, small_send.at[n, i], small_recv.at[n, i], (place.e, peer))
        for i, peer in enumerate((place.sib, place.far, place.diag))
        for n, (src, dst) in enumerate(small_parts)
    ]
    for copy in smalls:
        copy.start()
    for gather in gathers:
        gather.start()
    slot_tables(routes_ref, priority_ref, capacity, pick, back)
    tile = min(256, width)
    shape = grads_send.shape[:3]

    def to_slots(values_ref, slots_ref):
        def one(n):
            cols = span(n * tile, tile)
            value = dot_nn(pick[...], values_ref[:, cols]).astype(jnp.bfloat16)
            slots_ref[:, :, :, cols] = value.reshape(shape + (tile,))

        every(0, width // tile, one)

    to_slots(cot_ref, grads_send)
    dispatch = Dispatch(
        place, capacity, grads_send, grads_rows, (own_sem.at[0], disp_send, disp_recv)
    )
    dispatch.start()
    for copy in own_smalls:
        copy.wait()
    for copy in smalls:
        copy.wait_recv()
    small_out[...] = small[:, :vectors, :]
    router_out[...] = jnp.zeros_like(router_out)
    router_out[:gates, :] = jnp.concatenate(
        [small[i, vectors:, :] for i in range(4)], axis=1
    )

    def vector(which):
        parts = [small[i, which : which + 1, :] for i in range(4)]
        return jnp.concatenate(parts, axis=1).astype(jnp.float32)

    band = min(64, rows)
    gain, shift = vector(0), vector(1)

    def norm_band(i):
        part = span(i * band, band)
        scaled, _ = norm_stats(tokens_ref[part, :].astype(jnp.float32))
        act[part, :] = (scaled * gain + shift).astype(jnp.bfloat16)

    def project(n):
        for part in range(3):
            cols = gathers[0].cols(n, part)
            qkv[:, cols] = dot_nn(act[...], weight[:, cols]).astype(jnp.bfloat16)

    gathers[0].pass_on(0)
    every(0, rows // band, norm_band)
    turned[0] = act[...].T
    stores = [
        pltpu.make_async_copy(src, dst, store_sem.at[i])
        for i, (src, dst) in enumerate(
            [(qkv, qkv_out), (turned.at[0], act_out), (back, back_out), (weight, weight_out),
             (turned.at[1], merged_out), (out_w, out_full)]
        )
    ]
    for store in stores[1:3]:
        store.start()
    half = rows // 2
    pairs = width // LANES

    def keep_probs(i):
        slot = lax.rem(i, 2)
        return (
            pltpu.make_async_copy(
                low_buf.at[slot], low_out.at[pl.ds(2 * i, 2)], prob_sem.at[0, slot]
            ),
            pltpu.make_async_copy(
                high_buf.at[slot], high_out.at[pl.ds(2 * i, 2)], prob_sem.at[1, slot]
            ),
        )

    def attend_pair(i):
        slot = lax.rem(i, 2)

        @pl.when(i >= 2)
        def _():
            for copy in keep_probs(i - 2):
                copy.wait()

        query, key, value = (
            qkv[:, span(part * width + i * LANES, LANES)] for part in range(3)
        )
        tops, bottoms = [], []
        for head in range(2):
            part = slice(head * HEAD_DIM, (head + 1) * HEAD_DIM)
            low, high, top, bottom = attend_head(
                query[:, part], key[:, part], value[:, part], prefix_ref[0]
            )
            low_buf[slot, head] = low
            high_buf[slot, head] = high
            tops.append(top)
            bottoms.append(bottom)
        cols = span(i * LANES, LANES)
        merged[:half, cols] = jnp.concatenate(tops, axis=1).astype(jnp.bfloat16)
        merged[half:, cols] = jnp.concatenate(bottoms, axis=1).astype(jnp.bfloat16)
        for copy in keep_probs(i):
            copy.start()

    group = pairs // pieces
    share = -(-owners // pieces)

    def front_step(n):
        @pl.when(n + 1 < pieces)
        def _():
            gathers[0].pass_on(n + 1)

        gathers[0].pass_pair(n)
        for i, partner in enumerate(dispatch.order()):
            pl.when(n == i // share)(functools.partial(dispatch.forward, partner))
        gathers[0].ready(n)
        project(n)
        for i in range(group):
            attend_pair(n * group + i)

    every(0, pieces, front_step)
    turned[1] = merged[...].T
    for i in (0, 3, 4):
        stores[i].start()
    every(0, pieces, gathers[1].pass_on)
    every(0, pieces, gathers[1].pass_pair)
    order = dispatch.order()
    dispatch.relay(order[0])
    every(0, pieces, gathers[1].ready)
    stores[5].start()
    gain_two, shift_two = vector(2), vector(3)
    band_two = min(128, rows)

    def middle(i):
        part = span(i * band_two, band_two)
        value = tokens_ref[part, :].astype(jnp.float32) + dot_nn(merged[part, :], out_w[...])
        hidden_ref[part, :] = value
        scaled, _ = norm_stats(value)
        act_two[part, :] = (scaled * gain_two + shift_two).astype(jnp.bfloat16)
        for n, partner in enumerate(order[1 : 1 + bands]):
            pl.when(i == n)(functools.partial(dispatch.relay, partner))

    bands = rows // band_two
    every(0, bands, middle)
    to_slots(act_two, send_ref)
    for partner in order[1 + bands :]:
        dispatch.relay(partner)
    for i in (pairs - 2, pairs - 1):
        for copy in keep_probs(i):
            copy.wait()
    every(0, owners, dispatch.ready)
    for store in stores:
        store.wait()
    for copy in smalls:
        copy.wait_send()
    for gather in gathers:
        gather.drain()
    dispatch.drain()


def run_front(
    owners, experts, capacity, prefix, routes, priority, tokens, cotangent, small, router, w_qkv, w_out
):
    rows, width = tokens.shape
    shard, columns = w_qkv.shape
    half = rows // 2
    heads = width // HEAD_DIM
    pieces = 4
    any_spec = pl.BlockSpec(memory_space=pl.ANY)
    vmem_spec = pl.BlockSpec(memory_space=pltpu.VMEM)
    bf16, f32 = jnp.bfloat16, jnp.float32
    dma = pltpu.SemaphoreType.DMA

    def out(*shape):
        return jax.ShapeDtypeStruct(shape, bf16)

    def vm(*shape):
        return pltpu.VMEM(shape, bf16)

    return pl.pallas_call(
        functools.partial(front_kernel, (owners, capacity, pieces)),
        out_shape=(
            out(rows, columns),
            out(width, rows),
            out(width, rows),
            out(rows, rows),
            out(4 * shard, columns),
            out(4 * shard, width),
            out(heads, half, half),
            out(heads, half, rows),
            out(experts, owners * 4 * capacity, width),
            jax.ShapeDtypeStruct((rows, width), f32),
            out(owners, experts, capacity, width),
            out(4, *small.shape),
            out(LANES, width),
        ),
        in_specs=[pl.BlockSpec(memory_space=pltpu.SMEM)] + [vmem_spec] * 4 + [any_spec] * 4,
        out_specs=(any_spec,) * 9 + (vmem_spec,) * 4,
        scratch_shapes=[
            vm(4, small.shape[0] + router.shape[0], shard),
            vm(4 * shard, columns),
            vm(4 * shard, width),
            vm(rows, columns),
            vm(rows, width),
            vm(rows, width),
            vm(rows, width),
            vm(2, width, rows),
            vm(rows, rows),
            vm(rows, rows),
            vm(owners, experts, capacity, width),
            vm(2, 2, half, half),
            vm(2, 2, half, rows),
            dma((5,)),
            dma((4, owners)),
            dma((4, owners)),
            dma((2, 3)),
            dma((2, 3)),
            dma((2, 6, pieces, 3)),
            dma((2, 6, pieces, 3)),
            dma((6,)),
            dma((2, 2)),
        ],
        compiler_params=pltpu.CompilerParams(
            collective_id=0, has_side_effects=True, vmem_limit_bytes=VMEM_LIMIT
        ),
        name="front",
    )(prefix, routes, priority, tokens, cotangent, small, router, w_qkv, w_out)


class Reduce:
    def __init__(self, place, part, got, far, pair, lines, done, sems):
        self.p = place
        self.part, self.got, self.far = part, got, far
        self.pair, self.lines, self.done = pair, lines, done
        self.send, self.recv, self.line_send, self.line_recv = sems
        self.chunks = part.shape[0]
        self.halves = done.shape[1] // 2
        self.count = place.owners // 2
        self.slice = self.halves // self.count
        self.bit = lax.rem(place.e, 2)
        self.level = lax.div(place.e, 2)

    def step(self, which, n, src, dst, device):
        return remote(src, dst, self.send.at[which, n], self.recv.at[which, n], device)

    def swapped(self, n):
        return self.step(
            0, n, self.part.at[n, :, 1 - self.p.c], self.got.at[n], (self.p.e, self.p.sib)
        )

    def crossed(self, n):
        return self.step(
            1, n, self.part.at[n, 1 - self.p.x, self.p.c], self.far.at[n], (self.p.e, self.p.far)
        )

    def folded(self, n):
        other = span((1 - self.bit) * self.halves, self.halves)
        return self.step(
            2, n, self.part.at[n, self.p.x, self.p.c, other], self.pair.at[n],
            (self.p.pair, self.p.w),
        )

    def shared(self, n):
        part = self.done.at[n, span(self.bit * self.halves, self.halves)]
        return self.step(3, n, part, part, (self.p.pair, self.p.w))

    def line(self, which, n, k, src, dst):
        return remote(
            src, dst, self.line_send.at[which, n, k], self.line_recv.at[which, n, k],
            (self.p.ahead(2 * k), self.p.w),
        )

    def row(self, level):
        return span(self.bit * self.halves + level * self.slice, self.slice)

    def spreads(self, n, k):
        target = lax.rem(self.level + k, self.count)
        return self.line(
            0, n, k, self.part.at[n, self.p.x, self.p.c, self.row(target)], self.lines.at[n, k]
        )

    def collects(self, n, k):
        part = self.done.at[n, self.row(self.level)]
        return self.line(1, n, k, part, part)

    def pair_sum(self, n, side):
        return self.part[n, side, self.p.c].astype(jnp.float32) + self.got[n, side].astype(
            jnp.float32
        )

    def swap(self, n):
        self.swapped(n).start()

    def cross(self, n):
        self.swapped(n).wait_recv()
        side = 1 - self.p.x
        self.part[n, side, self.p.c] = self.pair_sum(n, side).astype(jnp.bfloat16)
        self.crossed(n).start()

    def fold(self, n):
        self.crossed(n).wait_recv()
        total = self.pair_sum(n, self.p.x) + self.far[n].astype(jnp.float32)
        self.part[n, self.p.x, self.p.c] = total.astype(jnp.bfloat16)
        self.folded(n).start()

    def spread(self, n):
        self.folded(n).wait_recv()
        own = span(self.bit * self.halves, self.halves)
        total = self.part[n, self.p.x, self.p.c, own, :].astype(jnp.float32) + self.pair[
            n
        ].astype(jnp.float32)
        self.part[n, self.p.x, self.p.c, own, :] = total.astype(jnp.bfloat16)
        for k in range(1, self.count):
            self.spreads(n, k).start()

    def collect(self, n):
        total = self.part[n, self.p.x, self.p.c, self.row(self.level), :].astype(jnp.float32)
        for k in range(1, self.count):
            self.spreads(n, k).wait_recv()
            total = total + self.lines[n, k].astype(jnp.float32)
        self.done[n, self.row(self.level), :] = total.astype(jnp.bfloat16)
        for k in range(1, self.count):
            self.collects(n, k).start()

    def share(self, n):
        for k in range(1, self.count):
            self.collects(n, k).wait_recv()
        self.shared(n).start()

    def finish(self, n):
        self.shared(n).wait_recv()

    def stages(self):
        return (self.cross, self.fold, self.spread, self.collect, self.share, self.finish)

    def drain(self):
        def one(n):
            for copy in (self.swapped(n), self.crossed(n), self.folded(n), self.shared(n)):
                copy.wait_send()
            for k in range(1, self.count):
                self.spreads(n, k).wait_send()
                self.collects(n, k).wait_send()

        every(0, self.chunks, one)


class PairFirst(Reduce):
    def folded(self, n):
        other = span((1 - self.bit) * self.halves, self.halves)
        return self.step(
            2, n, self.part.at[n, :, self.p.c, other], self.pair.at[n], (self.p.pair, self.p.w)
        )

    def crossed(self, n):
        own = span(self.bit * self.halves, self.halves)
        return self.step(
            1, n, self.part.at[n, 1 - self.p.x, self.p.c, own], self.far.at[n],
            (self.p.e, self.p.far),
        )

    def fold(self, n):
        self.swapped(n).wait_recv()
        for side in range(2):
            self.part[n, side, self.p.c] = self.pair_sum(n, side).astype(jnp.bfloat16)
        self.folded(n).start()

    def cross(self, n):
        self.folded(n).wait_recv()
        own = span(self.bit * self.halves, self.halves)
        for side in range(2):
            total = self.part[n, side, self.p.c, own, :].astype(jnp.float32) + self.pair[
                n, side
            ].astype(jnp.float32)
            self.part[n, side, self.p.c, own, :] = total.astype(jnp.bfloat16)
        self.crossed(n).start()

    def spread(self, n):
        self.crossed(n).wait_recv()
        own = span(self.bit * self.halves, self.halves)
        total = self.part[n, self.p.x, self.p.c, own, :].astype(jnp.float32) + self.far[
            n
        ].astype(jnp.float32)
        self.part[n, self.p.x, self.p.c, own, :] = total.astype(jnp.bfloat16)
        for k in range(1, self.count):
            self.spreads(n, k).start()

    def stages(self):
        return (self.fold, self.cross, self.spread, self.collect, self.share, self.finish)


class Small:
    def __init__(self, place, value, part, got, mid, far, total, others, out, sems):
        self.p, self.value, self.part, self.got, self.mid = place, value, part, got, mid
        self.far, self.total, self.others, self.out = far, total, others, out
        self.send, self.recv, self.all_send, self.all_recv = sems

    def swapped(self):
        return remote(
            self.part.at[:, 1 - self.p.c], self.got, self.send.at[0], self.recv.at[0],
            (self.p.e, self.p.sib),
        )

    def crossed(self):
        return remote(
            self.mid, self.far, self.send.at[1], self.recv.at[1], (self.p.e, self.p.far)
        )

    def spreads(self, k):
        return remote(
            self.total, self.others.at[k], self.all_send.at[k], self.all_recv.at[k],
            (self.p.ahead(k), self.p.w),
        )

    def swap(self):
        size = self.part.shape[-1]
        for owner in range(4):
            self.part[owner // 2, owner % 2] = self.value[:, owner * size : (owner + 1) * size]
        self.swapped().start()

    def cross(self):
        self.swapped().wait_recv()
        self.mid[...] = self.part[1 - self.p.x, self.p.c] + self.got[1 - self.p.x]
        self.crossed().start()

    def spread(self):
        self.crossed().wait_recv()
        self.total[...] = self.part[self.p.x, self.p.c] + self.got[self.p.x] + self.far[...]
        for k in range(1, self.p.owners):
            self.spreads(k).start()

    def finish(self):
        total = self.total[...]
        for k in range(1, self.p.owners):
            self.spreads(k).wait_recv()
            total = total + self.others[k]
        vectors_out, gates_out = self.out
        vectors_out[...] = total[: vectors_out.shape[0]]
        gates_out[...] = total[vectors_out.shape[0] :]

    def drain(self):
        self.swapped().wait_send()
        self.crossed().wait_send()
        for k in range(1, self.p.owners):
            self.spreads(k).wait_send()


def norm_back_rows(grad, scaled, inverse, gain):
    weighted = grad * gain
    mean_one = jnp.mean(weighted, axis=1, keepdims=True)
    mean_two = jnp.mean(weighted * scaled, axis=1, keepdims=True)
    return inverse * (weighted - mean_one - scaled * mean_two)


def back_kernel(
    dims,
    home_grad_ref, back_ref, hidden_ref, cot_ref, tokens_ref, vectors_ref, router_ref,
    far_hbm, near_hbm, home_hbm, act_hbm, merged_hbm, qkv_hbm, weight_hbm, out_hbm, low_hbm, high_hbm,
    output_ref, tokens_out, vectors_out, gates_out, qkv_out, out_out,
    near_sums, far_sums, done_rows, home_out,
    act_t, merged_t, qkv, weight, out_w, low_buf, high_buf, attn, grad_merged, grad_act,
    part_q, got_q, far_q, pair_q, lines_q, done_q,
    part_o, got_o, far_o, pair_o, lines_o, done_o,
    small, small_part, small_got, small_mid, small_far, small_sum, small_all,
    load_sem, prob_sem, own_sem, early_sem, cross_send, cross_recv, home_send, home_recv, send_q, recv_q, lsend_q, lrecv_q, send_o, recv_o, lsend_o, lrecv_o,
    small_send, small_recv, all_send, all_recv, out_sem,
):
    owners, capacity, gates = dims
    grad_qkv = qkv
    place = Place(owners)
    loads = [
        pltpu.make_async_copy(src, dst, load_sem.at[i])
        for i, (src, dst) in enumerate(
            [(merged_hbm, merged_t), (out_hbm, out_w), (qkv_hbm, qkv), (act_hbm, act_t),
             (weight_hbm, weight), (near_hbm, near_sums)]
        )
    ]

    def load_probs(i):
        slot = lax.rem(i, 2)
        return (
            pltpu.make_async_copy(
                low_hbm.at[pl.ds(2 * i, 2)], low_buf.at[slot], prob_sem.at[0, slot]
            ),
            pltpu.make_async_copy(
                high_hbm.at[pl.ds(2 * i, 2)], high_buf.at[slot], prob_sem.at[1, slot]
            ),
        )

    for load in loads:
        load.start()
    for load in load_probs(0):
        load.start()
    greet(
        [(place.ahead(k), place.w) for k in range(1, owners)]
        + [(place.e, place.sib), (place.e, place.far)]
    )
    experts = near_sums.shape[0]
    groups = owners // 2
    late = LateReturn(
        place, capacity, near_sums, None, far_hbm, far_sums, done_rows, home_out,
        (own_sem, cross_send, cross_recv, home_send, home_recv),
    )

    def start_late(j):
        for expert in range(experts):
            late.crossed(j, expert).start()

    every(EARLY_CHUNKS, groups, start_late)

    def early_rows(n):
        row = place.peer(n)
        return pltpu.make_async_copy(home_hbm.at[row], home_out.at[row], early_sem.at[n])

    every(0, 2 * EARLY_CHUNKS, lambda n: early_rows(n).start())
    reduce_o = PairFirst(
        place, part_o, got_o, far_o, pair_o, lines_o, done_o, (send_o, recv_o, lsend_o, lrecv_o)
    )
    reduce_q = Reduce(
        place, part_q, got_q, far_q, pair_q, lines_q, done_q, (send_q, recv_q, lsend_q, lrecv_q)
    )
    smalls = Small(
        place, small, small_part, small_got, small_mid, small_far, small_sum, small_all, (vectors_out, gates_out),
        (small_send, small_recv, all_send, all_recv),
    )
    rows, width = tokens_ref.shape
    shard = width // 4
    band = min(128, rows)
    lead = small.shape[0]

    def vector(which):
        parts = [vectors_ref[i, which : which + 1, :] for i in range(4)]
        return jnp.concatenate(parts, axis=1).astype(jnp.float32)

    gain_one, gain_two = vector(0), vector(2)
    small[: lead - gates, :] = jnp.zeros((lead - gates, width), jnp.float32)
    small[lead - gates :, :] = router_ref[:gates, :]

    def post(i):
        part = span(i * band, band)
        grad = dot_nn(back_ref[part, :], home_grad_ref.reshape(rows, width)[...])
        scaled, inverse = norm_stats(hidden_ref[part, :])
        value = cot_ref[part, :].astype(jnp.float32) + norm_back_rows(
            grad, scaled, inverse, gain_two
        )
        tokens_out[part, :] = value
        attn[part, :] = value.astype(jnp.bfloat16)
        small[2:3, :] += jnp.sum(grad * scaled, axis=0, keepdims=True)
        small[3:4, :] += jnp.sum(grad, axis=0, keepdims=True)

    every(0, rows // band, post)
    loads[0].wait()

    def weight_grad(part, n, left, right):
        def one(owner):
            value = dot_nn(left[span(owner * shard, shard), :], right)
            part[n, lax.div(owner, 2), lax.rem(owner, 2)] = value.astype(jnp.bfloat16)

        every(0, 4, one)

    tile_o = part_o.shape[-1]
    out_chunks = part_o.shape[0]
    for n in range(out_chunks):
        weight_grad(part_o, n, merged_t, attn[:, n * tile_o : (n + 1) * tile_o])
        reduce_o.swap(n)
    loads[1].wait()

    def merged_band(i):
        part = span(i * band, band)
        grad_merged[part, :] = dot_nt(attn[part, :], out_w[...]).astype(jnp.bfloat16)

    every(0, rows // band, merged_band)
    stages_o, stages_q = reduce_o.stages(), reduce_q.stages()
    for n in range(out_chunks):
        stages_o[0](n)
    for load in loads[2:]:
        load.wait()
    grad_act[...] = jnp.zeros_like(grad_act)
    pairs = part_q.shape[0]

    def attend_pair(i):
        slot = lax.rem(i, 2)
        for load in load_probs(i):
            load.wait()

        @pl.when(i + 1 < pairs)
        def _():
            for load in load_probs(i + 1):
                load.start()

        cols = span(i * LANES, LANES)
        query, key, value = (
            qkv[:, span(part * width + i * LANES, LANES)] for part in range(3)
        )
        grad = grad_merged[:, cols]
        results = []
        for head in range(2):
            part = slice(head * HEAD_DIM, (head + 1) * HEAD_DIM)
            results.append(
                attend_back_head(
                    query[:, part], key[:, part], value[:, part],
                    low_buf[slot, head], high_buf[slot, head], grad[:, part],
                )
            )
        for which in range(3):
            grad_qkv[:, span(which * width + i * LANES, LANES)] = jnp.concatenate(
                [results[0][which], results[1][which]], axis=1
            )
        right = jnp.concatenate(
            [grad_qkv[:, span(which * width + i * LANES, LANES)] for which in range(3)], axis=1
        )
        weight_grad(part_q, i, act_t, right)
        reduce_q.swap(i)
        columns = jnp.concatenate(
            [weight[:, span(which * width + i * LANES, LANES)] for which in range(3)], axis=1
        )
        grad_act[...] += dot_nt(right, columns)

    def input_band(i):
        part = span(i * band, band)
        grad = grad_act[part, :]
        scaled, inverse = norm_stats(tokens_ref[part, :].astype(jnp.float32))
        tokens_out[part, :] += norm_back_rows(grad, scaled, inverse, gain_one)
        small[0:1, :] += jnp.sum(grad * scaled, axis=0, keepdims=True)
        small[1:2, :] += jnp.sum(grad, axis=0, keepdims=True)

    def output_band(i):
        part = span(i * band, band)
        slots = home_out.reshape(rows, width)
        value = hidden_ref[part, :] + dot_nn(back_ref[part, :], slots[...])
        output_ref[part, :] = value.astype(jnp.bfloat16)

    def store_q(i):
        return [
            pltpu.make_async_copy(
                done_q.at[i, :, pl.ds(which * LANES, LANES)],
                qkv_out.at[:, span(which * width + i * LANES, LANES)],
                out_sem.at[which, i],
            )
            for which in range(3)
        ]

    def store_o(n):
        return pltpu.make_async_copy(
            done_o.at[n], out_out.at[:, span(n * tile_o, tile_o)], out_sem.at[3, n]
        )

    delays = (1, 3, 4, 5, 6, 7)
    last = len(delays) - 1
    half = rows // band // 2

    def slot_step(slot):
        @pl.when(slot + EARLY_CHUNKS < groups)
        def _():
            for expert in range(experts):
                late.finish(slot + EARLY_CHUNKS, expert)

        pl.when(slot < pairs)(lambda: attend_pair(slot))
        for s in range(last, -1, -1):
            n = slot - delays[s]

            @pl.when((n >= 0) & (n < pairs))
            def _(s=s, n=n):
                stages_q[s](n)
                if s == last:
                    for copy in store_q(n):
                        copy.start()

            @pl.when(slot == (delays[s] - 2 if s else -1))
            def _(s=s):
                for n in range(out_chunks):
                    stages_o[s](n)
                    if s == last:
                        store_o(n).start()

        @pl.when(slot == pairs)
        def _():
            every(0, half, input_band)

        pl.when(slot == pairs + 1)(lambda: every(half, 2 * half, input_band))
        pl.when(slot == pairs + 2)(smalls.swap)
        pl.when(slot == pairs + 3)(smalls.cross)
        pl.when(slot == pairs + 4)(smalls.spread)

        @pl.when(slot == pairs + 3)
        def _():
            late.arrived(EARLY_CHUNKS, groups, experts)
            every(0, 2 * EARLY_CHUNKS, lambda n: early_rows(n).wait())
            every(0, rows // band, output_band)

    every(0, pairs + delays[-1], slot_step)
    smalls.finish()

    def stored(i):
        for copy in store_q(i):
            copy.wait()

    every(0, pairs, stored)
    for n in range(out_chunks):
        store_o(n).wait()
    late.drain(EARLY_CHUNKS, groups, experts)
    reduce_o.drain()
    reduce_q.drain()
    smalls.drain()


def run_back(
    owners, capacity, gates, home_grad, far_sums, near_sums, home_out, back, hidden, cotangent, tokens,
    vectors, router_grad, act_t, merged_t, qkv, weight, w_out, low, high,
):
    rows, width = tokens.shape
    shard = width // 4
    lead = 8 + gates
    groups = owners // 2
    pairs = width // LANES
    tile_o = min(512, width)
    out_chunks = width // tile_o
    count = owners // 2
    half = shard // 2
    mid = rows // 2
    any_spec = pl.BlockSpec(memory_space=pl.ANY)
    vmem_spec = pl.BlockSpec(memory_space=pltpu.VMEM)
    bf16, f32 = jnp.bfloat16, jnp.float32
    dma = pltpu.SemaphoreType.DMA

    def vm(*shape):
        return pltpu.VMEM(shape, bf16)

    def fm(*shape):
        return pltpu.VMEM(shape, f32)

    def reduce_buffers(chunks, tile, pair_first):
        far, pair = ((half,), (2, half)) if pair_first else ((shard,), (half,))
        return [
            vm(chunks, 2, 2, shard, tile),
            vm(chunks, 2, shard, tile),
            vm(chunks, *far, tile),
            vm(chunks, *pair, tile),
            vm(chunks, count, half // count, tile),
            vm(chunks, shard, tile),
        ]

    def reduce_sems(chunks):
        return [dma((4, chunks)), dma((4, chunks)), dma((2, chunks, count)), dma((2, chunks, count))]

    return pl.pallas_call(
        functools.partial(back_kernel, (owners, capacity, gates)),
        out_shape=(
            jax.ShapeDtypeStruct((rows, width), bf16),
            jax.ShapeDtypeStruct((rows, width), f32),
            jax.ShapeDtypeStruct((8, shard), f32),
            jax.ShapeDtypeStruct((gates, shard), f32),
            jax.ShapeDtypeStruct((shard, 3 * width), bf16),
            jax.ShapeDtypeStruct((shard, width), bf16),
        ),
        in_specs=[vmem_spec] * 7 + [any_spec] * 10,
        out_specs=(vmem_spec,) * 4 + (any_spec,) * 2,
        scratch_shapes=[
            vm(*near_sums.shape),
            vm(*near_sums.shape),
            vm(*home_grad.shape),
            vm(*home_grad.shape),
            vm(width, rows),
            vm(width, rows),
            vm(rows, 3 * width),
            vm(width, 3 * width),
            vm(width, width),
            vm(2, 2, mid, mid),
            vm(2, 2, mid, rows),
            vm(rows, width),
            vm(rows, width),
            fm(rows, width),
        ]
        + reduce_buffers(pairs, 3 * LANES, False)
        + reduce_buffers(out_chunks, tile_o, True)
        + [
            fm(lead, width),
            fm(2, 2, lead, shard),
            fm(2, lead, shard),
            fm(lead, shard),
            fm(lead, shard),
            fm(lead, shard),
            fm(owners, lead, shard),
            dma((6,)),
            dma((2, 2)),
            dma((near_sums.shape[0],)),
            dma((owners,)),
            dma((groups, near_sums.shape[0])),
            dma((groups, near_sums.shape[0])),
            dma((owners, near_sums.shape[0])),
            dma((owners, near_sums.shape[0])),
        ]
        + reduce_sems(pairs)
        + reduce_sems(out_chunks)
        + [dma((2,)), dma((2,)), dma((owners,)), dma((owners,)), dma((4, pairs))],
        compiler_params=pltpu.CompilerParams(
            collective_id=2, has_side_effects=True, vmem_limit_bytes=VMEM_LIMIT
        ),
        name="back",
    )(
        home_grad, back, hidden, cotangent, tokens, vectors, router_grad,
        far_sums, near_sums, home_out, act_t, merged_t, qkv, weight, w_out, low, high,
    )


def widen_kernel(*refs):
    count = len(refs) // 2
    for src, dst in zip(refs[:count], refs[count:]):
        dst[...] = src[...].astype(dst.dtype)


def widen(steps, values, kinds):
    def spec(value):
        if value.shape[0] % (16 * steps):
            return pl.BlockSpec(value.shape, lambda i: (0, 0))
        return pl.BlockSpec((value.shape[0] // steps, value.shape[1]), lambda i: (i, 0))

    return pl.pallas_call(
        widen_kernel,
        grid=(steps,),
        in_specs=[spec(value) for value in values],
        out_specs=[spec(value) for value in values],
        out_shape=[
            jax.ShapeDtypeStruct(value.shape, kind) for value, kind in zip(values, kinds)
        ],
        name="widen",
    )(*values)


def on_device_plain(
    tokens,
    norm1_gain,
    norm1_shift,
    w_qkv,
    w_out,
    norm2_gain,
    norm2_shift,
    w_router,
    w_up,
    w_down,
    routes,
    priority,
    prefix,
    cotangent,
):
    row_count, model_width = tokens.shape
    expert_count = w_router.shape[1]
    capacity = row_count // expert_count
    owners = lax.axis_size("expert")
    local_experts = w_up.shape[0]
    slot_count = expert_count * capacity
    prefix_len = prefix[0]
    small = jnp.concatenate(
        [
            norm1_gain[None],
            norm1_shift[None],
            norm2_gain[None],
            norm2_shift[None],
            w_router.T,
        ],
        axis=0,
    )
    qkv_full = lax.all_gather(w_qkv, "wshard", axis=0, tiled=True)
    small_full = lax.all_gather(small, "wshard", axis=1, tiled=True)
    out_full = lax.all_gather(w_out, "wshard", axis=0, tiled=True)
    gain_one, shift_one, gain_two, shift_two = (small_full[i] for i in range(4))
    router_full = small_full[4:].T
    gain_one = gain_one.astype(jnp.float32)
    gain_two = gain_two.astype(jnp.float32)
    inputs = tokens.astype(jnp.float32)
    normed_one, scaled_one, inverse_one = normalize(inputs, gain_one, shift_one.astype(jnp.float32))
    act_one = normed_one.astype(jnp.bfloat16)
    qkv = jnp.dot(act_one, qkv_full, preferred_element_type=jnp.float32).astype(jnp.bfloat16)
    query_heads = qkv[:, :model_width]
    key_heads = qkv[:, model_width : 2 * model_width]
    value_heads = qkv[:, 2 * model_width :]
    merged, log_totals = attend_forward(query_heads, key_heads, value_heads, prefix_len)
    attn_out = jnp.dot(merged, out_full, preferred_element_type=jnp.float32)
    hidden = inputs + attn_out
    normed_two, scaled_two, inverse_two = normalize(hidden, gain_two, shift_two.astype(jnp.float32))
    act_two = normed_two.astype(jnp.bfloat16)
    logits = jnp.dot(act_two, router_full, preferred_element_type=jnp.float32)
    row_max = jnp.max(logits, axis=-1, keepdims=True)
    exponent = jnp.exp(logits - row_max)
    gate_prob = exponent / jnp.sum(exponent, axis=-1, keepdims=True)
    route_ids = routes[:, 0]
    chosen = route_ids[:, None] == jnp.arange(expert_count, dtype=jnp.int32)[None, :]
    gate_value = jnp.sum(jnp.where(chosen, gate_prob, 0.0), axis=1)
    slot_index, slot_source = assign_slots(route_ids, priority[0], expert_count, capacity)
    zero_row = jnp.zeros((1, model_width), jnp.bfloat16)
    padded = jnp.concatenate([act_two, zero_row], axis=0)
    send_rows = padded[slot_source].reshape(owners, local_experts * capacity, model_width)
    arrived = lax.all_to_all(send_rows, "expert", split_axis=0, concat_axis=0, tiled=True).reshape(
        owners, local_experts, capacity, model_width
    )
    group = lax.axis_size("wshard")
    local_rows = owners * capacity

    def by_expert(chunk):
        rows = jnp.transpose(chunk, (1, 0, 2, 3)).reshape(local_experts, local_rows, model_width)
        return lax.all_gather(rows, "wshard", axis=1, tiled=True)

    def home_rows(rows):
        own = lax.psum_scatter(rows.astype(jnp.bfloat16), "wshard", scatter_dimension=1, tiled=True)
        own = own.reshape(local_experts, owners, capacity, model_width)
        return jnp.transpose(own, (1, 0, 2, 3)).reshape(
            owners, local_experts * capacity, model_width
        )

    grad_output = cotangent.astype(jnp.float32)
    grad_combined = (gate_value[:, None] * grad_output).astype(jnp.bfloat16)
    grad_padded = jnp.concatenate([grad_combined, zero_row], axis=0)
    grad_send = grad_padded[slot_source].reshape(owners, local_experts * capacity, model_width)
    grad_arrived = lax.all_to_all(
        grad_send, "expert", split_axis=0, concat_axis=0, tiled=True
    ).reshape(owners, local_experts, capacity, model_width)
    rows_in = by_expert(arrived)
    grad_rows = by_expert(grad_arrived)
    pre_act = jnp.einsum("erd,edf->erf", rows_in, w_up, preferred_element_type=jnp.float32)
    activated, gelu_pull = jax.vjp(gelu_tanh, pre_act)
    act_hidden = activated.astype(jnp.bfloat16)
    produced = jnp.einsum(
        "erf,efd->erd", act_hidden, w_down, preferred_element_type=jnp.float32
    )
    expert_out = home_rows(produced)
    returned = lax.all_to_all(expert_out, "expert", split_axis=0, concat_axis=0, tiled=True)
    slots_back = jnp.concatenate([returned.reshape(slot_count, model_width), zero_row], axis=0)
    combined = slots_back[slot_index].astype(jnp.float32)
    output = (hidden + gate_value[:, None] * combined).astype(jnp.bfloat16)
    grad_gate = jnp.sum(grad_output * combined, axis=1)
    grad_down = jnp.einsum(
        "erf,erd->efd", act_hidden, grad_rows, preferred_element_type=jnp.float32
    )
    grad_hidden_units = jnp.einsum(
        "erd,efd->erf", grad_rows, w_down, preferred_element_type=jnp.float32
    )
    grad_pre = gelu_pull(grad_hidden_units)[0].astype(jnp.bfloat16)
    grad_up = jnp.einsum("erd,erf->edf", rows_in, grad_pre, preferred_element_type=jnp.float32)
    grad_expert_in = jnp.einsum(
        "erf,edf->erd", grad_pre, w_up, preferred_element_type=jnp.float32
    )
    grad_send_back = home_rows(grad_expert_in)
    grad_back = lax.all_to_all(grad_send_back, "expert", split_axis=0, concat_axis=0, tiled=True)
    grad_slots = jnp.concatenate([grad_back.reshape(slot_count, model_width), zero_row], axis=0)
    grad_act_two = grad_slots[slot_index].astype(jnp.float32)
    grad_logits = (
        gate_prob * (jnp.where(chosen, grad_gate[:, None], 0.0) - (gate_value * grad_gate)[:, None])
    ).astype(jnp.bfloat16)
    grad_router = contract_rows(act_two, grad_logits)
    grad_act_two = grad_act_two + times_transpose(grad_logits, router_full)
    grad_from_two, grad_gain_two, grad_shift_two = norm_back(
        grad_act_two, scaled_two, inverse_two, gain_two
    )
    grad_hidden = grad_output + grad_from_two
    grad_attn = grad_hidden.astype(jnp.bfloat16)
    grad_out_w = contract_rows(merged, grad_attn)
    grad_merged = times_transpose(grad_attn, out_full).astype(jnp.bfloat16)
    grad_qkv = attend_backward(
        query_heads, key_heads, value_heads, grad_merged, log_totals, prefix_len
    )
    grad_qkv_w = contract_rows(act_one, grad_qkv)
    grad_act_one = times_transpose(grad_qkv, qkv_full)
    grad_from_one, grad_gain_one, grad_shift_one = norm_back(
        grad_act_one, scaled_one, inverse_one, gain_one
    )
    grad_tokens = grad_hidden + grad_from_one
    small_grad = jnp.concatenate(
        [
            grad_gain_one[None],
            grad_shift_one[None],
            grad_gain_two[None],
            grad_shift_two[None],
            grad_router.T,
        ],
        axis=0,
    )
    out_share = lax.psum_scatter(
        grad_out_w.astype(jnp.bfloat16), "wshard", scatter_dimension=0, tiled=True
    )
    qkv_share = lax.psum_scatter(
        grad_qkv_w.astype(jnp.bfloat16), "wshard", scatter_dimension=0, tiled=True
    )
    small_share = lax.psum_scatter(small_grad, "wshard", scatter_dimension=1, tiled=True)
    out_total = lax.psum(out_share, "expert").astype(jnp.float32)
    qkv_total = lax.psum(qkv_share, "expert").astype(jnp.float32)
    small_total = lax.psum(small_share, "expert")
    totals = (
        small_total[0],
        small_total[1],
        qkv_total,
        out_total,
        small_total[2],
        small_total[3],
        small_total[4:].T,
    )
    return (
        output,
        grad_tokens,
        totals[0],
        totals[1],
        totals[2],
        totals[3],
        totals[4],
        totals[5],
        totals[6],
        grad_up,
        grad_down,
    )


def on_device(
    tokens,
    norm1_gain,
    norm1_shift,
    w_qkv,
    w_out,
    norm2_gain,
    norm2_shift,
    w_router,
    w_up,
    w_down,
    routes,
    priority,
    prefix,
    cotangent,
):
    row_count, model_width = tokens.shape
    expert_count = w_router.shape[1]
    capacity = row_count // expert_count
    owners = lax.axis_size("expert")
    experts = w_up.shape[0]
    which = lax.broadcasted_iota(jnp.int32, (16, norm1_gain.shape[0]), 0)
    small = jnp.zeros(which.shape, jnp.bfloat16)
    for i, vector in enumerate((norm1_gain, norm1_shift, norm2_gain, norm2_shift)):
        small = jnp.where(which == i, vector[None], small)
    (
        qkv, act_t, merged_t, back, weight, out_full, low, high, grad_rows, hidden, send_rows,
        vectors, router,
    ) = run_front(
        owners, experts, capacity, prefix, routes.reshape(1, row_count), priority, tokens,
        cotangent, small, w_router.T, w_qkv, w_out,
    )
    far_sums, near_sums, home_out, home_grad, grad_up, grad_down, grad_router = run_experts(
        owners, capacity, expert_count, send_rows, grad_rows, w_up, w_down, router
    )
    output, grad_tokens, grad_vectors, grad_gates, grad_qkv, grad_out = run_back(
        owners, capacity, expert_count, home_grad, far_sums, near_sums, home_out, back, hidden, cotangent,
        tokens, vectors, grad_router, act_t, merged_t, qkv, weight, out_full, low, high,
    )
    f32 = jnp.float32
    units = w_up.shape[2]
    output, grad_tokens, grad_gates, grad_qkv, grad_out, grad_up, grad_down = widen(
        2,
        (
            output, grad_tokens, grad_gates, grad_qkv, grad_out,
            grad_up.reshape(-1, units), grad_down.reshape(-1, model_width),
        ),
        (output.dtype,) + (f32,) * 6,
    )
    return (
        output,
        grad_tokens,
        grad_vectors[0],
        grad_vectors[1],
        grad_qkv,
        grad_out,
        grad_vectors[2],
        grad_vectors[3],
        grad_gates.T,
        grad_up.reshape(w_up.shape),
        grad_down.reshape(w_down.shape),
    )


def solution(mesh):
    placed = (
        P(("expert", "wshard"), None),
        P("wshard"),
        P("wshard"),
        P("wshard", None),
        P("wshard", None),
        P("wshard"),
        P("wshard"),
        P("wshard", None),
        P("expert", None, "wshard"),
        P("expert", "wshard", None),
        P(("expert", "wshard"), None),
        P(("expert", "wshard"), None),
        P(("expert", "wshard")),
        P(("expert", "wshard"), None),
    )
    owners, group = mesh.shape["expert"], mesh.shape["wshard"]

    def body(*args):
        capacity = args[0].shape[0] // args[7].shape[1]
        fits = group == 4 and owners == 8 and capacity % 16 == 0 and args[7].shape[1] % 16 == 0
        return (on_device if fits else on_device_plain)(*args)

    return jax.shard_map(
        body,
        mesh=mesh,
        in_specs=placed,
        out_specs=(
            P(("expert", "wshard"), None),
            P(("expert", "wshard"), None),
            P("wshard"),
            P("wshard"),
            P("wshard", None),
            P("wshard", None),
            P("wshard"),
            P("wshard"),
            P("wshard", None),
            P("expert", None, "wshard"),
            P("expert", "wshard", None),
        ),
        check_vma=False,
    )
```

```python
import functools
import math

import jax
import jax.numpy as jnp
from jax import lax
from jax.experimental import pallas as pl
from jax.experimental.pallas import tpu as pltpu
from jax.sharding import PartitionSpec as P

HEADS = 16
HEAD_DIM = 64


epsilon = 1e-05
VMEM_LIMIT = 66_000_000
TILE = 1024
EARLY_CHUNKS = 1


def normalize(values, gain_vec, shift_vec):
    row_mean = jnp.mean(values, axis=-1, keepdims=True)
    centered = values - row_mean
    inverse = lax.rsqrt(jnp.mean(centered * centered, axis=-1, keepdims=True) + epsilon)
    scaled = centered * inverse
    return (scaled * gain_vec + shift_vec, scaled, inverse)


def norm_back(grad_rows, scaled, inverse, gain_vec):
    weighted = grad_rows * gain_vec
    mean_one = jnp.mean(weighted, axis=-1, keepdims=True)
    mean_two = jnp.mean(weighted * scaled, axis=-1, keepdims=True)
    grad_inputs = inverse * (weighted - mean_one - scaled * mean_two)
    return (grad_inputs, jnp.sum(grad_rows * scaled, axis=0), jnp.sum(grad_rows, axis=0))


def contract_rows(left, right):
    return lax.dot_general(
        left, right, (((0,), (0,)), ((), ())), preferred_element_type=jnp.float32
    )


def times_transpose(left, right):
    return lax.dot_general(
        left, right, (((1,), (1,)), ((), ())), preferred_element_type=jnp.float32
    )


def gelu_tanh(values):
    return jax.nn.gelu(values, approximate=True)


def assign_slots(route_ids, order_ids, expert_count, capacity):
    token_count = route_ids.shape[0]
    same_expert = route_ids[:, None] == route_ids[None, :]
    earlier = order_ids[None, :] < order_ids[:, None]
    rank_ids = jnp.sum((same_expert & earlier).astype(jnp.int32), axis=1)
    is_kept = rank_ids < capacity
    slot_index = jnp.where(is_kept, route_ids * capacity + rank_ids, expert_count * capacity)
    slot_ids = jnp.arange(expert_count * capacity, dtype=jnp.int32)
    match_table = slot_index[None, :] == slot_ids[:, None]
    token_ids = jnp.arange(token_count, dtype=jnp.int32)
    filled = jnp.any(match_table, axis=1)
    picked = jnp.sum(jnp.where(match_table, token_ids[None, :], 0), axis=1)
    slot_source = jnp.where(filled, picked, token_count)
    return (slot_index, slot_source)


def group_heads(values, groups):
    token_count = values.shape[0]
    return jnp.transpose(values.reshape(token_count, groups, -1, HEAD_DIM), (1, 0, 2, 3))


def block_scores(query_block, key_group, block_start, prefix_len):
    block_rows = query_block.shape[0]
    key_count = key_group.shape[0]
    scores = jnp.einsum(
        "qgd,kgd->gqk", query_block, key_group, preferred_element_type=jnp.float32
    ) * (1.0 / math.sqrt(HEAD_DIM))
    query_pos = block_start + jnp.arange(block_rows, dtype=jnp.int32)
    key_pos = jnp.arange(key_count, dtype=jnp.int32)
    allowed = (key_pos[None, :] <= query_pos[:, None]) | (key_pos[None, :] < prefix_len)
    return jnp.where(allowed[None], scores, -1e30)


def attend_forward(query_heads, key_heads, value_heads, prefix_len):
    token_count = query_heads.shape[0]
    group_size = min(4, HEADS)
    groups = HEADS // group_size
    block_rows = min(512, token_count)
    blocks = token_count // block_rows
    starts = jnp.arange(blocks, dtype=jnp.int32) * block_rows

    def one_group(group_item):
        query_group, key_group, value_group = group_item
        query_blocks = query_group.reshape(blocks, block_rows, group_size, HEAD_DIM)

        def one_block(block_item):
            query_block, block_start = block_item
            scores = block_scores(query_block, key_group, block_start, prefix_len)
            row_max = jnp.max(scores, axis=-1, keepdims=True)
            exponent = jnp.exp(scores - row_max)
            row_total = jnp.sum(exponent, axis=-1, keepdims=True)
            attn_probs = (exponent / row_total).astype(jnp.bfloat16)
            result = jnp.einsum(
                "gqk,kgd->qgd", attn_probs, value_group, preferred_element_type=jnp.float32
            )
            return (result, (row_max + jnp.log(row_total))[..., 0])

        return lax.map(one_block, (query_blocks, starts))

    attended, log_totals = lax.map(
        one_group,
        (
            group_heads(query_heads, groups),
            group_heads(key_heads, groups),
            group_heads(value_heads, groups),
        ),
    )
    merged = (
        jnp.transpose(attended, (1, 2, 0, 3, 4))
        .reshape(token_count, HEADS * HEAD_DIM)
        .astype(jnp.bfloat16)
    )
    return (merged, log_totals)


def attend_backward(query_heads, key_heads, value_heads, grad_merged, log_totals, prefix_len):
    token_count = query_heads.shape[0]
    group_size = min(4, HEADS)
    groups = HEADS // group_size
    block_rows = min(512, token_count)
    blocks = token_count // block_rows
    starts = jnp.arange(blocks, dtype=jnp.int32) * block_rows
    score_scale = 1.0 / math.sqrt(HEAD_DIM)

    def one_group(group_item):
        query_group, key_group, value_group, grad_group, total_group = group_item
        query_blocks = query_group.reshape(blocks, block_rows, group_size, HEAD_DIM)
        grad_blocks = grad_group.reshape(blocks, block_rows, group_size, HEAD_DIM)

        def one_block(carry, block_item):
            grad_keys, grad_vals = carry
            query_block, grad_block, total_block, block_start = block_item
            scores = block_scores(query_block, key_group, block_start, prefix_len)
            attn_probs = jnp.exp(scores - total_block[..., None])
            grad_probs = jnp.einsum(
                "qgd,kgd->gqk", grad_block, value_group, preferred_element_type=jnp.float32
            )
            row_delta = jnp.sum(attn_probs * grad_probs, axis=-1, keepdims=True)
            grad_scores = (attn_probs * (grad_probs - row_delta)).astype(jnp.bfloat16)
            grad_vals = grad_vals + jnp.einsum(
                "gqk,qgd->kgd",
                attn_probs.astype(jnp.bfloat16),
                grad_block,
                preferred_element_type=jnp.float32,
            )
            grad_keys = (
                grad_keys
                + jnp.einsum(
                    "gqk,qgd->kgd", grad_scores, query_block, preferred_element_type=jnp.float32
                )
                * score_scale
            )
            grad_query = (
                jnp.einsum(
                    "gqk,kgd->qgd", grad_scores, key_group, preferred_element_type=jnp.float32
                )
                * score_scale
            )
            return ((grad_keys, grad_vals), grad_query)

        zero_keys = jnp.zeros(key_group.shape, jnp.float32)
        carried, grad_queries = lax.scan(
            one_block, (zero_keys, zero_keys), (query_blocks, grad_blocks, total_group, starts)
        )
        return (grad_queries, carried[0], carried[1])

    grad_queries, grad_keys, grad_vals = lax.map(
        one_group,
        (
            group_heads(query_heads, groups),
            group_heads(key_heads, groups),
            group_heads(value_heads, groups),
            group_heads(grad_merged, groups),
            log_totals,
        ),
    )
    query_part = jnp.transpose(grad_queries, (1, 2, 0, 3, 4)).reshape(token_count, HEADS * HEAD_DIM)
    key_part = jnp.transpose(grad_keys, (1, 0, 2, 3)).reshape(token_count, HEADS * HEAD_DIM)
    value_part = jnp.transpose(grad_vals, (1, 0, 2, 3)).reshape(token_count, HEADS * HEAD_DIM)
    return jnp.concatenate([query_part, key_part, value_part], axis=1).astype(jnp.bfloat16)


MESH = pl.DeviceIdType.MESH
LANES = 128


def dot_nn(left, right):
    return lax.dot_general(
        left, right, (((1,), (0,)), ((), ())), preferred_element_type=jnp.float32
    )


def dot_nt(left, right):
    return lax.dot_general(
        left, right, (((1,), (1,)), ((), ())), preferred_element_type=jnp.float32
    )


def dot_tn(left, right):
    return lax.dot_general(
        left, right, (((0,), (0,)), ((), ())), preferred_element_type=jnp.float32
    )


def span(start, size):
    return pl.ds(pl.multiple_of(start, size), size)


def every(start, stop, step):
    def body(i, carry):
        step(i)
        return carry

    lax.fori_loop(start, stop, body, 0)


class Place:
    def __init__(self, owners):
        self.owners = owners
        self.e = lax.axis_index("expert")
        self.w = lax.axis_index("wshard")
        self.c = lax.rem(self.w, 2)
        self.x = lax.div(self.w, 2)
        self.sib = self.w + 1 - 2 * self.c
        self.far = lax.rem(self.w + 2, 4)
        self.diag = 3 - self.w
        self.pair = self.e + 1 - 2 * lax.rem(self.e, 2)

    def ahead(self, k):
        return lax.rem(self.e + k, self.owners)

    def flip(self, bit):
        return self.e + bit * (1 - 2 * lax.rem(lax.div(self.e, bit), 2))

    def peer(self, n):
        other = lax.div(n, 2) + lax.rem(n, 2) * (self.owners // 2)
        result, bit = 0, 1
        while bit < self.owners:
            result = result + bit * lax.rem(lax.div(self.e, bit) + lax.div(other, bit), 2)
            bit *= 2
        return result


def remote(src, dst, send, recv, device):
    return pltpu.make_async_remote_copy(
        src_ref=src,
        dst_ref=dst,
        send_sem=send,
        recv_sem=recv,
        device_id=device,
        device_id_type=MESH,
    )


def greet(peers):
    barrier = pltpu.get_barrier_semaphore()
    for peer in peers:
        pl.semaphore_signal(barrier, inc=1, device_id=peer, device_id_type=MESH)
    pl.semaphore_wait(barrier, len(peers))


def either(test, yes, no):
    pl.when(test)(yes)
    pl.when(jnp.logical_not(test))(no)


class Dispatch:
    def __init__(self, place, capacity, send_ref, rows_ref, sems):
        self.p, self.cap, self.src, self.rows = place, capacity, send_ref, rows_ref
        self.own_sem, self.send, self.recv = sems

    def slice(self, k, core, side):
        start = (((lax.div(k, 2) * 2 + core) * 2 + side) * 2 + lax.rem(k, 2)) * self.cap
        return self.rows.at[:, span(start, self.cap)]

    def own(self):
        return pltpu.make_async_copy(
            self.src.at[self.p.e], self.slice(0, self.p.c, self.p.x), self.own_sem
        )

    def direct(self, k):
        return remote(
            self.src.at[self.p.peer(k)],
            self.slice(k, self.p.c, self.p.x),
            self.send.at[0, k],
            self.recv.at[0, k],
            (self.p.peer(k), self.p.w),
        )

    def hop(self, k, side, which, peer):
        part = self.slice(k, self.p.c, side)
        return remote(
            part, part, self.send.at[which, k], self.recv.at[which, k], (self.p.e, peer)
        )

    def to_sib(self, k):
        return self.hop(k, self.p.x, 1, self.p.sib)

    def to_far(self, k):
        return self.hop(k, self.p.x, 2, self.p.far)

    def relayed(self, k):
        return self.hop(k, 1 - self.p.x, 3, self.p.sib)

    def start(self):
        self.own().start()
        every(1, self.p.owners, lambda k: self.direct(k).start())

    def forward(self, k):
        k = jnp.int32(k)

        @pl.when(k == 0)
        def _():
            self.own().wait()

        @pl.when(k > 0)
        def _():
            self.direct(k).wait_recv()

        self.to_far(k).start()
        self.to_sib(k).start()

    def relay(self, k):
        self.to_far(k).wait_recv()
        self.relayed(k).start()

    def ready(self, k):
        self.to_sib(k).wait_recv()
        self.relayed(k).wait_recv()

    def order(self):
        return (0, 2, 4, 1, 6, 3, 5, 7)

    def drain(self):
        every(1, self.p.owners, lambda k: self.direct(k).wait_send())

        def rest(k):
            self.to_sib(k).wait_send()
            self.to_far(k).wait_send()
            self.relayed(k).wait_send()

        every(0, self.p.owners, rest)


class Return:
    def __init__(self, place, capacity, part, got, mid, far, done, home, sems):
        self.p, self.cap = place, capacity
        self.part, self.got, self.mid, self.far, self.done, self.home = (
            part, got, mid, far, done, home,
        )
        self.own_sem, self.send, self.recv, self.home_send, self.home_recv = sems

    def swapped(self, j, expert):
        size = 4 * self.cap
        return remote(
            self.part.at[expert, span((j * 2 + 1 - self.p.c) * size, size)],
            self.got.at[expert, span(j * size, size)],
            self.send.at[0, j, expert],
            self.recv.at[0, j, expert],
            (self.p.e, self.p.sib),
        )

    def crossed(self, j, expert):
        part = span(j * 2 * self.cap, 2 * self.cap)
        return remote(
            self.mid.at[expert, part],
            self.far.at[expert, part],
            self.send.at[1, j, expert],
            self.recv.at[1, j, expert],
            (self.p.e, self.p.far),
        )

    def own(self, expert):
        return pltpu.make_async_copy(
            self.done.at[0, expert], self.home.at[self.p.e, expert], self.own_sem.at[expert]
        )

    def homed(self, n, expert):
        return remote(
            self.done.at[n, expert],
            self.home.at[self.p.e, expert],
            self.home_send.at[n, expert],
            self.home_recv.at[n, expert],
            (self.p.peer(n), self.p.w),
        )

    def pair_sum(self, j, expert, side):
        size = 2 * self.cap
        mine = self.part[expert, span(((j * 2 + self.p.c) * 2 + side) * size, size), :]
        theirs = self.got[expert, span((j * 2 + side) * size, size), :]
        return mine.astype(jnp.float32) + theirs.astype(jnp.float32)

    def swap(self, j, expert):
        self.swapped(j, expert).start()

    def split(self, j, expert):
        self.swapped(j, expert).wait_recv()
        here = span(j * 2 * self.cap, 2 * self.cap)
        self.mid[expert, here, :] = self.pair_sum(j, expert, 1 - self.p.x).astype(jnp.bfloat16)
        self.keep[expert, here, :] = self.pair_sum(j, expert, self.p.x).astype(jnp.bfloat16)

    def cross(self, j, expert):
        self.swapped(j, expert).wait_recv()
        here = span(j * 2 * self.cap, 2 * self.cap)
        self.mid[expert, here, :] = self.pair_sum(j, expert, 1 - self.p.x).astype(jnp.bfloat16)
        self.crossed(j, expert).start()

    def this_side(self, j, expert):
        return self.pair_sum(j, expert, self.p.x)

    def finish(self, j, expert):
        self.crossed(j, expert).wait_recv()
        here = span(j * 2 * self.cap, 2 * self.cap)
        total = self.this_side(j, expert) + self.far[expert, here, :].astype(jnp.float32)
        total = total.astype(jnp.bfloat16)
        self.done[2 * j, expert] = total[: self.cap]
        self.done[2 * j + 1, expert] = total[self.cap :]
        j = jnp.int32(j)
        self.homed(2 * j + 1, expert).start()
        either(
            j == 0,
            lambda: self.own(expert).start(),
            lambda: self.homed(2 * j, expert).start(),
        )

    def drain_swaps(self, chunks, experts):
        for expert in range(experts):
            every(0, chunks, lambda j: self.swapped(j, expert).wait_send())

    def drain(self, first, last, experts):
        for expert in range(experts):
            every(first, last, lambda j: self.crossed(j, expert).wait_send())
            every(
                max(1, 2 * first), 2 * last, lambda n: self.homed(n, expert).wait_send()
            )

    def arrived(self, first, last, experts):
        for expert in range(experts):
            if first == 0 and last > 0:
                self.own(expert).wait()
            every(
                max(1, 2 * first), 2 * last, lambda n: self.homed(n, expert).wait_recv()
            )


class LateReturn(Return):
    def crossed(self, j, expert):
        part = span(j * 2 * self.cap, 2 * self.cap)
        return remote(
            self.mid.at[expert, part],
            self.far.at[expert, part],
            self.send.at[j, expert],
            self.recv.at[j, expert],
            (self.p.e, self.p.far),
        )

    def this_side(self, j, expert):
        here = span(j * 2 * self.cap, 2 * self.cap)
        return self.part[expert, here, :].astype(jnp.float32)


def gelu_pair(v):
    root = math.sqrt(2.0 / math.pi)
    square = v * v
    t = jnp.tanh(v * (root + (root * 0.044715) * square))
    half = 0.5 + 0.5 * t
    slope = half + (half * (1.0 - t)) * (v * (root + (3.0 * root * 0.044715) * square))
    return v * half, slope


def expert_kernel(
    dims,
    send_ref, grads_hbm, up_hbm, down_hbm, router_ref,
    far_sums, near_sums, home_out, home_grad, up_out, down_out, router_grad,
    rows, grads, scaled, hidden, pre, up, down, grad_up, grad_down,
    part_out, part_grad, got_out, got_grad, mid_out, mid_grad,
    keep_out, far_grad, far_out, done_grad, done_out,
    load_sem, own_sem, disp_send, disp_recv, red_send, red_recv, home_send, home_recv,
):
    owners, experts, capacity, width, units, expert_count = dims
    place = Place(owners)
    loads = [
        pltpu.make_async_copy(src, dst, load_sem.at[i])
        for i, (src, dst) in enumerate(
            [(up_hbm, up), (grads_hbm, grads), (down_hbm, down)]
        )
    ]
    for load in loads:
        load.start()
    greet(
        [(place.ahead(k), place.w) for k in range(1, owners)]
        + [(place.e, place.sib), (place.e, place.far)]
    )
    dispatch = Dispatch(
        place, capacity, send_ref, rows, (own_sem.at[0, 0], disp_send, disp_recv)
    )
    ret_grad = Return(
        place, capacity, part_grad, got_grad, mid_grad, far_grad, done_grad, home_grad,
        (own_sem.at[1], red_send.at[0], red_recv.at[0], home_send.at[0], home_recv.at[0]),
    )
    ret_out = Return(
        place, capacity, part_out, got_out, mid_out, far_out, done_out, home_out,
        (own_sem.at[2], red_send.at[1], red_recv.at[1], home_send.at[1], home_recv.at[1]),
    )
    dispatch.start()
    router_grad[...] = jnp.zeros_like(router_grad)
    tile = min(TILE, units)
    wide = min(TILE, width)
    chunks = owners // 2
    early = EARLY_CHUNKS
    size = 8 * capacity
    lane = lax.broadcasted_iota(jnp.int32, (size, LANES), 1)

    def compute(j, expert):
        here = span(j * size, size)
        logits = dot_nt(rows[expert, here, :], router_ref[...])
        logits = jnp.where(lane < expert_count, logits, -1e30)
        exponent = jnp.exp(logits - jnp.max(logits, axis=1, keepdims=True))
        prob = exponent * (1.0 / jnp.sum(exponent, axis=1, keepdims=True))
        mine = lane == place.e * experts + expert
        gate = jnp.sum(jnp.where(mine, prob, 0.0), axis=1, keepdims=True)
        scaled[expert, here, :] = (
            gate * grads[expert, here, :].astype(jnp.float32)
        ).astype(jnp.bfloat16)

        def one_tile(n):
            cols = span(n * tile, tile)
            value, slope = gelu_pair(dot_nn(rows[expert, here, :], up[expert, :, cols]))
            hidden[expert, here, cols] = value.astype(jnp.bfloat16)
            back = pre[expert, here, cols].astype(jnp.float32)
            pre[expert, here, cols] = (gate * back * slope).astype(jnp.bfloat16)

        every(0, units // tile, one_tile)

        def one_out(n, total):
            cols = span(n * wide, wide)
            value = dot_nn(hidden[expert, here, :], down[expert, :, cols])
            part_out[expert, here, cols] = (gate * value).astype(jnp.bfloat16)
            weighted = value * grads[expert, here, cols].astype(jnp.float32)
            for start in range(0, wide, LANES):
                total = total + weighted[:, start : start + LANES]
            return total

        total = lax.fori_loop(
            0, width // wide, one_out, jnp.zeros((size, LANES), jnp.float32)
        )
        grad_gate = jnp.sum(total, axis=1, keepdims=True)
        grad_logits = (
            prob * ((jnp.where(mine, 1.0, 0.0) - gate) * grad_gate)
        ).astype(jnp.bfloat16)

        def one_in(n):
            cols = span(n * wide, wide)
            value = dot_nt(pre[expert, here, :], up[expert, cols, :]) + dot_nn(
                grad_logits, router_ref[:, cols]
            )
            part_grad[expert, here, cols] = value.astype(jnp.bfloat16)
            router_grad[:, cols] += dot_tn(grad_logits, rows[expert, here, cols])

        every(0, width // wide, one_in)

    def unscaled(j, expert):
        here = span(j * size, size)
        pre[expert, here, :] = dot_nt(grads[expert, here, :], down[expert]).astype(jnp.bfloat16)

    block = min(256, width)

    def weight_grads(expert, first, last):
        def one(n):
            part = span(n * block, block)
            grad_down[expert, part, :] = dot_tn(
                hidden[expert, :, part], scaled[expert]
            ).astype(jnp.bfloat16)
            grad_up[expert, part, :] = dot_tn(rows[expert, :, part], pre[expert]).astype(
                jnp.bfloat16
            )

        every(first * width // block // 4, last * width // block // 4, one)

    def keep(expert):
        return [
            pltpu.make_async_copy(src.at[expert], dst.at[expert], load_sem.at[2 * expert + i])
            for i, (src, dst) in enumerate(((grad_up, up_out), (grad_down, down_out)))
        ]

    turns = [(j, expert) for j in range(chunks) for expert in range(experts)]
    ahead, through, here = dispatch.forward, dispatch.relay, dispatch.ready
    plan = [[] for _ in turns]
    for unit, acts in (
        (0, ((here, 0), (here, 1), (ahead, 5))),
        (1, ((through, 6), (ahead, 7))),
        (2, ((through, 3), (here, 2), (here, 3))),
        (3, ((through, 5),)),
        (4, ((through, 7), (here, 4), (here, 5))),
        (6, ((here, 6), (here, 7))),
    ):
        plan[unit].extend(acts)
    for u in range(2, len(turns)):
        done = turns[u - 2]
        plan[u].append((ret_grad.cross,) + done)
        plan[u].append((ret_out.cross if done[0] < early else ret_out.split,) + done)
        if u >= 4:
            done = turns[u - 4]
            plan[u].append((ret_grad.finish,) + done)
            if done[0] < early:
                plan[u].append((ret_out.finish,) + done)
    ret_out.keep = keep_out
    for load in loads:
        load.wait()

    def unscaled_pair(j):
        for expert in range(experts):
            unscaled(j, expert)

    ahead(0)
    unscaled_pair(0)
    unscaled_pair(1)
    ahead(2)
    ahead(4)
    ahead(1)
    unscaled_pair(2)
    through(0)
    unscaled_pair(3)
    through(2)
    ahead(6)
    through(4)
    through(1)
    ahead(3)

    def step(unit):
        for u, acts in enumerate(plan):

            @pl.when(unit == u)
            def _(acts=acts):
                for act, *at in acts:
                    act(*at)

        j, expert = lax.div(unit, experts), lax.rem(unit, experts)
        compute(j, expert)
        ret_grad.swap(j, expert)
        ret_out.swap(j, expert)

    every(0, len(turns), step)
    ret_grad.cross(*turns[-2])
    ret_out.split(*turns[-2])
    ret_grad.finish(*turns[-4])
    weight_grads(0, 0, 1)
    ret_grad.cross(*turns[-1])
    ret_out.split(*turns[-1])
    sums = [
        pltpu.make_async_copy(src, dst, load_sem.at[4 + i])
        for i, (src, dst) in enumerate(((mid_out, far_sums), (keep_out, near_sums)))
    ]
    for store in sums:
        store.start()
    ret_grad.finish(*turns[-3])
    weight_grads(0, 1, 2)
    ret_grad.finish(*turns[-2])
    weight_grads(0, 2, 3)
    ret_grad.finish(*turns[-1])
    weight_grads(0, 3, 4)
    for store in keep(0):
        store.start()
    for expert in range(1, experts):
        weight_grads(expert, 0, 4)
        for store in keep(expert):
            store.start()
    for expert in range(experts):
        for store in keep(expert):
            store.wait()
    for store in sums:
        store.wait()
    dispatch.drain()
    ret_grad.drain_swaps(chunks, experts)
    ret_grad.drain(0, chunks, experts)
    ret_grad.arrived(0, chunks, experts)
    ret_out.drain_swaps(chunks, experts)
    ret_out.drain(0, early, experts)
    ret_out.arrived(0, early, experts)


def run_experts(owners, capacity, expert_count, send_rows, grads, w_up, w_down, router):
    experts, width, units = w_up.shape
    slots = owners * 4 * capacity
    chunks = owners // 2
    dims = (owners, experts, capacity, width, units, expert_count)
    any_spec = pl.BlockSpec(memory_space=pl.ANY)
    vmem_spec = pl.BlockSpec(memory_space=pltpu.VMEM)
    bf16 = jnp.bfloat16
    home = jax.ShapeDtypeStruct((owners, experts, capacity, width), bf16)
    dma = pltpu.SemaphoreType.DMA

    def vm(*shape):
        return pltpu.VMEM(shape, bf16)

    return pl.pallas_call(
        functools.partial(expert_kernel, dims),
        out_shape=(
            jax.ShapeDtypeStruct((experts, slots // 4, width), bf16),
            jax.ShapeDtypeStruct((experts, slots // 4, width), bf16),
            home, home,
            jax.ShapeDtypeStruct(w_up.shape, bf16),
            jax.ShapeDtypeStruct(w_down.shape, bf16),
            jax.ShapeDtypeStruct((LANES, width), jnp.float32),
        ),
        in_specs=[any_spec] * 4 + [vmem_spec],
        out_specs=(any_spec,) * 6 + (vmem_spec,),
        scratch_shapes=[
            vm(experts, slots, width),
            vm(experts, slots, width),
            vm(experts, slots, width),
            vm(experts, slots, units),
            vm(experts, slots, units),
            vm(experts, width, units),
            vm(experts, units, width),
            vm(experts, width, units),
            vm(experts, units, width),
            vm(experts, slots, width),
            vm(experts, slots, width),
            vm(experts, slots // 2, width),
            vm(experts, slots // 2, width),
            vm(experts, slots // 4, width),
            vm(experts, slots // 4, width),
            vm(experts, slots // 4, width),
            vm(experts, slots // 4, width),
            vm(experts, slots // 4, width),
            vm(owners, experts, capacity, width),
            vm(owners, experts, capacity, width),
            dma((6,)),
            dma((3, experts)),
            dma((4, owners)),
            dma((4, owners)),
            dma((2, 2, chunks, experts)),
            dma((2, 2, chunks, experts)),
            dma((2, owners, experts)),
            dma((2, owners, experts)),
        ],
        compiler_params=pltpu.CompilerParams(
            collective_id=1, has_side_effects=True, vmem_limit_bytes=VMEM_LIMIT
        ),
        name="experts",
    )(send_rows, grads, w_up, w_down, router)


def masked_softmax(scores):
    exponent = jnp.exp(scores - jnp.max(scores, axis=1, keepdims=True))
    return exponent * (1.0 / jnp.sum(exponent, axis=1, keepdims=True))


def attend_head(query, key, value, prefix_len):
    half = query.shape[0] // 2
    query = query * (1.0 / math.sqrt(HEAD_DIM))
    row = lax.broadcasted_iota(jnp.int32, (half, half), 0)
    col = lax.broadcasted_iota(jnp.int32, (half, half), 1)
    low = dot_nt(query[:half], key[:half])
    low = jnp.where((col <= row) | (col < prefix_len), low, -1e30)
    low = masked_softmax(low).astype(jnp.bfloat16)
    high = dot_nt(query[half:], key)
    high = jnp.concatenate(
        [high[:, :half], jnp.where(col <= row, high[:, half:], -1e30)], axis=1
    )
    high = masked_softmax(high).astype(jnp.bfloat16)
    return low, high, dot_nn(low, value[:half]), dot_nn(high, value)


def score_grads(probs, grad_probs):
    probs = probs.astype(jnp.float32)
    weighted = probs * grad_probs
    total = jnp.sum(weighted, axis=1, keepdims=True)
    return (weighted - probs * total).astype(jnp.bfloat16)


def attend_back_head(query, key, value, low, high, grad):
    half = query.shape[0] // 2
    scale = 1.0 / math.sqrt(HEAD_DIM)
    query = query * scale
    grad_low = score_grads(low, dot_nt(grad[:half], value[:half]))
    grad_high = score_grads(high, dot_nt(grad[half:], value))
    grad_query = jnp.concatenate(
        [dot_nn(grad_low, key[:half]), dot_nn(grad_high, key)], axis=0
    )
    value_all = dot_tn(high, grad[half:])
    key_all = dot_tn(grad_high, query[half:])
    grad_value = jnp.concatenate(
        [value_all[:half] + dot_tn(low, grad[:half]), value_all[half:]], axis=0
    )
    grad_key = jnp.concatenate(
        [key_all[:half] + dot_tn(grad_low, query[:half]), key_all[half:]], axis=0
    )
    return (
        (grad_query * scale).astype(jnp.bfloat16),
        grad_key.astype(jnp.bfloat16),
        grad_value.astype(jnp.bfloat16),
    )


class Gather:
    def __init__(self, place, pieces, parts, src, dst, sems):
        self.p, self.src, self.dst, self.pieces, self.parts = place, src, dst, pieces, parts
        self.send, self.recv = sems
        self.shard = src.shape[0]
        self.half = self.shard // 2
        self.width = src.shape[1] // parts
        self.step = self.width // pieces
        self.first = lax.rem(place.e, 2) * self.half
        self.second = self.half - self.first

    def cols(self, n, part):
        return span(part * self.width + n * self.step, self.step)

    def block(self, owner, start, size, n, part):
        rows = pl.ds(pl.multiple_of(owner * self.shard + start, self.half), size)
        return self.dst.at[rows, self.cols(n, part)]

    def move(self, which, n, part, src, dst, device):
        return remote(
            src, dst, self.send.at[which, n, part], self.recv.at[which, n, part], device
        )

    def own(self, n, part):
        return pltpu.make_async_copy(
            self.src.at[:, self.cols(n, part)],
            self.block(self.p.w, 0, self.shard, n, part),
            self.recv.at[5, n, part],
        )

    def near(self, n, part):
        return self.move(
            4, n, part, self.src.at[:, self.cols(n, part)],
            self.block(self.p.w, 0, self.shard, n, part), (self.p.e, self.p.sib),
        )

    def hop(self, n, part):
        return self.move(
            0, n, part, self.src.at[span(self.first, self.half), self.cols(n, part)],
            self.block(self.p.w, self.first, self.half, n, part), (self.p.e, self.p.far),
        )

    def pass_from(self, which, start, n, part, device):
        block = self.block(self.p.far, start, self.half, n, part)
        return self.move(which, n, part, block, block, device)

    def pairs(self, n, part):
        return self.pass_from(1, self.first, n, part, (self.p.pair, self.p.w))

    def relay(self, n, part):
        return self.pass_from(2, self.first, n, part, (self.p.e, self.p.sib))

    def pair_relay(self, n, part):
        return self.pass_from(3, self.second, n, part, (self.p.e, self.p.sib))

    def all_parts(self, n, act):
        for part in range(self.parts):
            act(n, part)

    def start_own(self):
        every(
            0, self.pieces, lambda n: self.all_parts(n, lambda n, part: self.own(n, part).start())
        )

    def start(self):
        def hop(n, part):
            self.hop(n, part).start()

        def near(n, part):
            self.near(n, part).start()

        every(0, self.pieces, lambda n: self.all_parts(n, hop))
        every(0, self.pieces, lambda n: self.all_parts(n, near))

    def pass_on(self, n):
        def one(n, part):
            self.hop(n, part).wait_recv()
            self.pairs(n, part).start()
            self.relay(n, part).start()

        self.all_parts(n, one)

    def pass_pair(self, n):
        def one(n, part):
            self.pairs(n, part).wait_recv()
            self.pair_relay(n, part).start()

        self.all_parts(n, one)

    def ready(self, n):
        def one(n, part):
            self.own(n, part).wait()
            for copy in (self.near(n, part), self.relay(n, part), self.pair_relay(n, part)):
                copy.wait_recv()

        self.all_parts(n, one)

    def drain(self):
        def one(n, part):
            for copy in (
                self.hop(n, part), self.pairs(n, part), self.relay(n, part),
                self.pair_relay(n, part), self.near(n, part),
            ):
                copy.wait_send()

        every(0, self.pieces, lambda n: self.all_parts(n, one))


def slot_tables(routes_ref, priority_ref, capacity, pick_ref, back_ref):
    count = routes_ref.shape[1]
    row = lax.broadcasted_iota(jnp.int32, (count, count), 0).astype(jnp.float32)
    col = lax.broadcasted_iota(jnp.int32, (count, count), 1).astype(jnp.float32)
    eye = row == col
    route_row = routes_ref[...].astype(jnp.float32)
    order_row = priority_ref[...].astype(jnp.float32)
    route_col = jnp.sum(jnp.where(eye, route_row, 0.0), axis=1, keepdims=True)
    order_col = jnp.sum(jnp.where(eye, order_row, 0.0), axis=1, keepdims=True)
    same = route_col == route_row
    rank_row = jnp.sum(
        jnp.where(same & (order_col < order_row), 1.0, 0.0), axis=0, keepdims=True
    )
    rank_col = jnp.sum(
        jnp.where(same & (order_row < order_col), 1.0, 0.0), axis=1, keepdims=True
    )
    slots = float(count)
    slot_row = jnp.where(rank_row < capacity, route_row * capacity + rank_row, slots)
    slot_col = jnp.where(rank_col < capacity, route_col * capacity + rank_col, slots)
    pick_ref[...] = jnp.where(slot_row == row, 1.0, 0.0).astype(jnp.bfloat16)
    back_ref[...] = jnp.where(slot_col == col, 1.0, 0.0).astype(jnp.bfloat16)


def norm_stats(value):
    centered = value - jnp.mean(value, axis=1, keepdims=True)
    inverse = lax.rsqrt(jnp.mean(centered * centered, axis=1, keepdims=True) + epsilon)
    return centered * inverse, inverse


def front_kernel(
    dims,
    prefix_ref, routes_ref, priority_ref, tokens_ref, cot_ref, small_hbm, router_hbm, qkv_hbm, out_hbm,
    qkv_out, act_out, merged_out, back_out, weight_out, out_full, low_out, high_out, grads_rows,
    hidden_ref, send_ref, small_out, router_out,
    small, weight, out_w, qkv, act, merged, act_two, turned, pick, back, grads_send, low_buf, high_buf,
    own_sem, disp_send, disp_recv, small_send, small_recv, gat_send, gat_recv, store_sem, prob_sem,
):
    owners, capacity, pieces = dims
    place = Place(owners)
    rows, width = tokens_ref.shape
    shard = qkv_hbm.shape[0]
    gathers = [
        Gather(place, pieces, parts, src, dst, (gat_send.at[i], gat_recv.at[i]))
        for i, (parts, src, dst) in enumerate(((3, qkv_hbm, weight), (1, out_hbm, out_w)))
    ]
    for gather in gathers:
        gather.start_own()
    vectors, gates = small_hbm.shape[0], router_hbm.shape[0]
    small_parts = [
        (small_hbm, small.at[place.w, pl.ds(0, vectors)]),
        (router_hbm, small.at[place.w, pl.ds(vectors, gates)]),
    ]
    own_smalls = [
        pltpu.make_async_copy(src, dst, own_sem.at[3 + i])
        for i, (src, dst) in enumerate(small_parts)
    ]
    for copy in own_smalls:
        copy.start()
    greet(
        [(place.ahead(k), place.w) for k in range(1, owners)]
        + [(place.e, place.sib), (place.e, place.far), (place.e, place.diag)]
    )
    smalls = [
        remote(src, dst, small_send.at[n, i], small_recv.at[n, i], (place.e, peer))
        for i, peer in enumerate((place.sib, place.far, place.diag))
        for n, (src, dst) in enumerate(small_parts)
    ]
    for copy in smalls:
        copy.start()
    for gather in gathers:
        gather.start()
    slot_tables(routes_ref, priority_ref, capacity, pick, back)
    tile = min(256, width)
    shape = grads_send.shape[:3]

    def to_slots(values_ref, slots_ref):
        def one(n):
            cols = span(n * tile, tile)
            value = dot_nn(pick[...], values_ref[:, cols]).astype(jnp.bfloat16)
            slots_ref[:, :, :, cols] = value.reshape(shape + (tile,))

        every(0, width // tile, one)

    to_slots(cot_ref, grads_send)
    dispatch = Dispatch(
        place, capacity, grads_send, grads_rows, (own_sem.at[0], disp_send, disp_recv)
    )
    dispatch.start()
    for copy in own_smalls:
        copy.wait()
    for copy in smalls:
        copy.wait_recv()
    small_out[...] = small[:, :vectors, :]
    router_out[...] = jnp.zeros_like(router_out)
    router_out[:gates, :] = jnp.concatenate(
        [small[i, vectors:, :] for i in range(4)], axis=1
    )

    def vector(which):
        parts = [small[i, which : which + 1, :] for i in range(4)]
        return jnp.concatenate(parts, axis=1).astype(jnp.float32)

    band = min(64, rows)
    gain, shift = vector(0), vector(1)

    def norm_band(i):
        part = span(i * band, band)
        scaled, _ = norm_stats(tokens_ref[part, :].astype(jnp.float32))
        act[part, :] = (scaled * gain + shift).astype(jnp.bfloat16)

    def project(n):
        for part in range(3):
            cols = gathers[0].cols(n, part)
            qkv[:, cols] = dot_nn(act[...], weight[:, cols]).astype(jnp.bfloat16)

    gathers[0].pass_on(0)
    every(0, rows // band, norm_band)
    turned[0] = act[...].T
    stores = [
        pltpu.make_async_copy(src, dst, store_sem.at[i])
        for i, (src, dst) in enumerate(
            [(qkv, qkv_out), (turned.at[0], act_out), (back, back_out), (weight, weight_out),
             (turned.at[1], merged_out), (out_w, out_full)]
        )
    ]
    for store in stores[1:3]:
        store.start()
    half = rows // 2
    pairs = width // LANES

    def keep_probs(i):
        slot = lax.rem(i, 2)
        return (
            pltpu.make_async_copy(
                low_buf.at[slot], low_out.at[pl.ds(2 * i, 2)], prob_sem.at[0, slot]
            ),
            pltpu.make_async_copy(
                high_buf.at[slot], high_out.at[pl.ds(2 * i, 2)], prob_sem.at[1, slot]
            ),
        )

    def attend_pair(i):
        slot = lax.rem(i, 2)

        @pl.when(i >= 2)
        def _():
            for copy in keep_probs(i - 2):
                copy.wait()

        query, key, value = (
            qkv[:, span(part * width + i * LANES, LANES)] for part in range(3)
        )
        tops, bottoms = [], []
        for head in range(2):
            part = slice(head * HEAD_DIM, (head + 1) * HEAD_DIM)
            low, high, top, bottom = attend_head(
                query[:, part], key[:, part], value[:, part], prefix_ref[0]
            )
            low_buf[slot, head] = low
            high_buf[slot, head] = high
            tops.append(top)
            bottoms.append(bottom)
        cols = span(i * LANES, LANES)
        merged[:half, cols] = jnp.concatenate(tops, axis=1).astype(jnp.bfloat16)
        merged[half:, cols] = jnp.concatenate(bottoms, axis=1).astype(jnp.bfloat16)
        for copy in keep_probs(i):
            copy.start()

    group = pairs // pieces
    share = -(-owners // pieces)

    def front_step(n):
        @pl.when(n + 1 < pieces)
        def _():
            gathers[0].pass_on(n + 1)

        gathers[0].pass_pair(n)
        for i, partner in enumerate(dispatch.order()):
            pl.when(n == i // share)(functools.partial(dispatch.forward, partner))
        gathers[0].ready(n)
        project(n)
        for i in range(group):
            attend_pair(n * group + i)

    every(0, pieces, front_step)
    turned[1] = merged[...].T
    for i in (0, 3, 4):
        stores[i].start()
    every(0, pieces, gathers[1].pass_on)
    every(0, pieces, gathers[1].pass_pair)
    order = dispatch.order()
    dispatch.relay(order[0])
    every(0, pieces, gathers[1].ready)
    stores[5].start()
    gain_two, shift_two = vector(2), vector(3)
    band_two = min(128, rows)

    def middle(i):
        part = span(i * band_two, band_two)
        value = tokens_ref[part, :].astype(jnp.float32) + dot_nn(merged[part, :], out_w[...])
        hidden_ref[part, :] = value
        scaled, _ = norm_stats(value)
        act_two[part, :] = (scaled * gain_two + shift_two).astype(jnp.bfloat16)
        for n, partner in enumerate(order[1 : 1 + bands]):
            pl.when(i == n)(functools.partial(dispatch.relay, partner))

    bands = rows // band_two
    every(0, bands, middle)
    to_slots(act_two, send_ref)
    for partner in order[1 + bands :]:
        dispatch.relay(partner)
    for i in (pairs - 2, pairs - 1):
        for copy in keep_probs(i):
            copy.wait()
    every(0, owners, dispatch.ready)
    for store in stores:
        store.wait()
    for copy in smalls:
        copy.wait_send()
    for gather in gathers:
        gather.drain()
    dispatch.drain()


def run_front(
    owners, experts, capacity, prefix, routes, priority, tokens, cotangent, small, router, w_qkv, w_out
):
    rows, width = tokens.shape
    shard, columns = w_qkv.shape
    half = rows // 2
    heads = width // HEAD_DIM
    pieces = 4
    any_spec = pl.BlockSpec(memory_space=pl.ANY)
    vmem_spec = pl.BlockSpec(memory_space=pltpu.VMEM)
    bf16, f32 = jnp.bfloat16, jnp.float32
    dma = pltpu.SemaphoreType.DMA

    def out(*shape):
        return jax.ShapeDtypeStruct(shape, bf16)

    def vm(*shape):
        return pltpu.VMEM(shape, bf16)

    return pl.pallas_call(
        functools.partial(front_kernel, (owners, capacity, pieces)),
        out_shape=(
            out(rows, columns),
            out(width, rows),
            out(width, rows),
            out(rows, rows),
            out(4 * shard, columns),
            out(4 * shard, width),
            out(heads, half, half),
            out(heads, half, rows),
            out(experts, owners * 4 * capacity, width),
            jax.ShapeDtypeStruct((rows, width), f32),
            out(owners, experts, capacity, width),
            out(4, *small.shape),
            out(LANES, width),
        ),
        in_specs=[pl.BlockSpec(memory_space=pltpu.SMEM)] + [vmem_spec] * 4 + [any_spec] * 4,
        out_specs=(any_spec,) * 9 + (vmem_spec,) * 4,
        scratch_shapes=[
            vm(4, small.shape[0] + router.shape[0], shard),
            vm(4 * shard, columns),
            vm(4 * shard, width),
            vm(rows, columns),
            vm(rows, width),
            vm(rows, width),
            vm(rows, width),
            vm(2, width, rows),
            vm(rows, rows),
            vm(rows, rows),
            vm(owners, experts, capacity, width),
            vm(2, 2, half, half),
            vm(2, 2, half, rows),
            dma((5,)),
            dma((4, owners)),
            dma((4, owners)),
            dma((2, 3)),
            dma((2, 3)),
            dma((2, 6, pieces, 3)),
            dma((2, 6, pieces, 3)),
            dma((6,)),
            dma((2, 2)),
        ],
        compiler_params=pltpu.CompilerParams(
            collective_id=0, has_side_effects=True, vmem_limit_bytes=VMEM_LIMIT
        ),
        name="front",
    )(prefix, routes, priority, tokens, cotangent, small, router, w_qkv, w_out)


class Reduce:
    def __init__(self, place, part, got, far, pair, near, line, done, sems):
        self.p = place
        self.part, self.got, self.far = part, got, far
        self.pair, self.near, self.line, self.done = pair, near, line, done
        self.send, self.recv = sems
        self.chunks = part.shape[0]
        self.halves = done.shape[1] // 2
        self.bit = lax.rem(place.e, 2)
        self.low = lax.rem(lax.div(place.e, 2), 2)
        self.high = lax.div(place.e, 4)

    def step(self, which, n, src, dst, device):
        return remote(src, dst, self.send.at[which, n], self.recv.at[which, n], device)

    def swapped(self, n):
        return self.step(
            0, n, self.part.at[n, :, 1 - self.p.c], self.got.at[n], (self.p.e, self.p.sib)
        )

    def crossed(self, n):
        return self.step(
            1, n, self.part.at[n, 1 - self.p.x, self.p.c], self.far.at[n], (self.p.e, self.p.far)
        )

    def folded(self, n):
        other = span((1 - self.bit) * self.halves, self.halves)
        return self.step(
            2, n, self.part.at[n, self.p.x, self.p.c, other], self.pair.at[n],
            (self.p.pair, self.p.w),
        )

    def shared(self, n):
        part = self.done.at[n, span(self.bit * self.halves, self.halves)]
        return self.step(3, n, part, part, (self.p.pair, self.p.w))

    def quarter(self, low):
        size = self.halves // 2
        return span(self.bit * self.halves + low * size, size)

    def eighth(self, high):
        size = self.halves // 4
        return span(self.bit * self.halves + (self.low * 2 + high) * size, size)

    def nears(self, n):
        return self.step(
            4, n, self.part.at[n, self.p.x, self.p.c, self.quarter(1 - self.low)],
            self.near.at[n], (self.p.flip(2), self.p.w),
        )

    def lines(self, n):
        return self.step(
            5, n, self.part.at[n, self.p.x, self.p.c, self.eighth(1 - self.high)],
            self.line.at[n], (self.p.flip(4), self.p.w),
        )

    def line_back(self, n):
        part = self.done.at[n, self.eighth(self.high)]
        return self.step(6, n, part, part, (self.p.flip(4), self.p.w))

    def near_back(self, n):
        part = self.done.at[n, self.quarter(self.low)]
        return self.step(7, n, part, part, (self.p.flip(2), self.p.w))

    def add(self, n, rows, other):
        total = self.part[n, self.p.x, self.p.c, rows, :].astype(jnp.float32) + other.astype(
            jnp.float32
        )
        return total.astype(jnp.bfloat16)

    def pair_sum(self, n, side):
        return self.part[n, side, self.p.c].astype(jnp.float32) + self.got[n, side].astype(
            jnp.float32
        )

    def swap(self, n):
        self.swapped(n).start()

    def cross(self, n):
        self.swapped(n).wait_recv()
        side = 1 - self.p.x
        self.part[n, side, self.p.c] = self.pair_sum(n, side).astype(jnp.bfloat16)
        self.crossed(n).start()

    def fold(self, n):
        self.crossed(n).wait_recv()
        total = self.pair_sum(n, self.p.x) + self.far[n].astype(jnp.float32)
        self.part[n, self.p.x, self.p.c] = total.astype(jnp.bfloat16)
        self.folded(n).start()

    def spread(self, n):
        self.folded(n).wait_recv()
        own = span(self.bit * self.halves, self.halves)
        self.part[n, self.p.x, self.p.c, own, :] = self.add(n, own, self.pair[n])
        self.nears(n).start()

    def reach(self, n):
        self.nears(n).wait_recv()
        own = self.quarter(self.low)
        self.part[n, self.p.x, self.p.c, own, :] = self.add(n, own, self.near[n])
        self.lines(n).start()

    def collect(self, n):
        self.lines(n).wait_recv()
        own = self.eighth(self.high)
        self.done[n, own, :] = self.add(n, own, self.line[n])
        self.line_back(n).start()

    def widen_back(self, n):
        self.line_back(n).wait_recv()
        self.near_back(n).start()

    def share(self, n):
        self.near_back(n).wait_recv()
        self.shared(n).start()

    def finish(self, n):
        self.shared(n).wait_recv()

    def line_stages(self):
        return (self.spread, self.reach, self.collect, self.widen_back, self.share, self.finish)

    def stages(self):
        return (self.cross, self.fold) + self.line_stages()

    def drain(self):
        def one(n):
            for copy in (
                self.swapped(n), self.crossed(n), self.folded(n), self.shared(n), self.nears(n),
                self.lines(n), self.line_back(n), self.near_back(n),
            ):
                copy.wait_send()

        every(0, self.chunks, one)


class PairFirst(Reduce):
    def folded(self, n):
        other = span((1 - self.bit) * self.halves, self.halves)
        return self.step(
            2, n, self.part.at[n, :, self.p.c, other], self.pair.at[n], (self.p.pair, self.p.w)
        )

    def crossed(self, n):
        own = span(self.bit * self.halves, self.halves)
        return self.step(
            1, n, self.part.at[n, 1 - self.p.x, self.p.c, own], self.far.at[n],
            (self.p.e, self.p.far),
        )

    def fold(self, n):
        self.swapped(n).wait_recv()
        for side in range(2):
            self.part[n, side, self.p.c] = self.pair_sum(n, side).astype(jnp.bfloat16)
        self.folded(n).start()

    def cross(self, n):
        self.folded(n).wait_recv()
        own = span(self.bit * self.halves, self.halves)
        for side in range(2):
            total = self.part[n, side, self.p.c, own, :].astype(jnp.float32) + self.pair[
                n, side
            ].astype(jnp.float32)
            self.part[n, side, self.p.c, own, :] = total.astype(jnp.bfloat16)
        self.crossed(n).start()

    def spread(self, n):
        self.crossed(n).wait_recv()
        own = span(self.bit * self.halves, self.halves)
        self.part[n, self.p.x, self.p.c, own, :] = self.add(n, own, self.far[n])
        self.nears(n).start()

    def stages(self):
        return (self.fold, self.cross) + self.line_stages()


class Small:
    def __init__(self, place, value, part, got, mid, far, total, others, out, sems):
        self.p, self.value, self.part, self.got, self.mid = place, value, part, got, mid
        self.far, self.total, self.others, self.out = far, total, others, out
        self.send, self.recv, self.all_send, self.all_recv = sems

    def swapped(self):
        return remote(
            self.part.at[:, 1 - self.p.c], self.got, self.send.at[0], self.recv.at[0],
            (self.p.e, self.p.sib),
        )

    def crossed(self):
        return remote(
            self.mid, self.far, self.send.at[1], self.recv.at[1], (self.p.e, self.p.far)
        )

    def spreads(self, k):
        return remote(
            self.total, self.others.at[k], self.all_send.at[k], self.all_recv.at[k],
            (self.p.ahead(k), self.p.w),
        )

    def swap(self):
        size = self.part.shape[-1]
        for owner in range(4):
            self.part[owner // 2, owner % 2] = self.value[:, owner * size : (owner + 1) * size]
        self.swapped().start()

    def cross(self):
        self.swapped().wait_recv()
        self.mid[...] = self.part[1 - self.p.x, self.p.c] + self.got[1 - self.p.x]
        self.crossed().start()

    def spread(self):
        self.crossed().wait_recv()
        self.total[...] = self.part[self.p.x, self.p.c] + self.got[self.p.x] + self.far[...]
        for k in range(1, self.p.owners):
            self.spreads(k).start()

    def finish(self):
        total = self.total[...]
        for k in range(1, self.p.owners):
            self.spreads(k).wait_recv()
            total = total + self.others[k]
        vectors_out, gates_out = self.out
        vectors_out[...] = total[: vectors_out.shape[0]]
        gates_out[...] = total[vectors_out.shape[0] :]

    def drain(self):
        self.swapped().wait_send()
        self.crossed().wait_send()
        for k in range(1, self.p.owners):
            self.spreads(k).wait_send()


def norm_back_rows(grad, scaled, inverse, gain):
    weighted = grad * gain
    mean_one = jnp.mean(weighted, axis=1, keepdims=True)
    mean_two = jnp.mean(weighted * scaled, axis=1, keepdims=True)
    return inverse * (weighted - mean_one - scaled * mean_two)


def back_kernel(
    dims,
    home_grad_ref, back_ref, hidden_ref, cot_ref, tokens_ref, vectors_ref, router_ref,
    far_hbm, near_hbm, home_hbm, act_hbm, merged_hbm, qkv_hbm, weight_hbm, out_hbm, low_hbm, high_hbm,
    output_ref, tokens_out, vectors_out, gates_out, qkv_out, out_out,
    near_sums, far_sums, done_rows, home_out,
    act_t, merged_t, qkv, weight, out_w, low_buf, high_buf, attn, grad_merged, grad_act,
    part_q, got_q, far_q, pair_q, near_q, line_q, done_q,
    part_o, got_o, far_o, pair_o, near_o, line_o, done_o,
    small, small_part, small_got, small_mid, small_far, small_sum, small_all,
    load_sem, prob_sem, own_sem, early_sem, cross_send, cross_recv, home_send, home_recv, send_q, recv_q, send_o, recv_o,
    small_send, small_recv, all_send, all_recv, out_sem,
):
    owners, capacity, gates = dims
    grad_qkv = qkv
    place = Place(owners)
    loads = [
        pltpu.make_async_copy(src, dst, load_sem.at[i])
        for i, (src, dst) in enumerate(
            [(merged_hbm, merged_t), (out_hbm, out_w), (qkv_hbm, qkv), (act_hbm, act_t),
             (weight_hbm, weight), (near_hbm, near_sums)]
        )
    ]

    def load_probs(i):
        slot = lax.rem(i, 2)
        return (
            pltpu.make_async_copy(
                low_hbm.at[pl.ds(2 * i, 2)], low_buf.at[slot], prob_sem.at[0, slot]
            ),
            pltpu.make_async_copy(
                high_hbm.at[pl.ds(2 * i, 2)], high_buf.at[slot], prob_sem.at[1, slot]
            ),
        )

    for load in loads:
        load.start()
    for load in load_probs(0):
        load.start()
    greet(
        [(place.ahead(k), place.w) for k in range(1, owners)]
        + [(place.e, place.sib), (place.e, place.far)]
    )
    experts = near_sums.shape[0]
    groups = owners // 2
    late = LateReturn(
        place, capacity, near_sums, None, far_hbm, far_sums, done_rows, home_out,
        (own_sem, cross_send, cross_recv, home_send, home_recv),
    )

    def start_late(j):
        for expert in range(experts):
            late.crossed(j, expert).start()

    every(EARLY_CHUNKS, groups, start_late)

    def early_rows(n):
        row = place.peer(n)
        return pltpu.make_async_copy(home_hbm.at[row], home_out.at[row], early_sem.at[n])

    every(0, 2 * EARLY_CHUNKS, lambda n: early_rows(n).start())
    reduce_o = PairFirst(
        place, part_o, got_o, far_o, pair_o, near_o, line_o, done_o, (send_o, recv_o)
    )
    reduce_q = Reduce(
        place, part_q, got_q, far_q, pair_q, near_q, line_q, done_q, (send_q, recv_q)
    )
    smalls = Small(
        place, small, small_part, small_got, small_mid, small_far, small_sum, small_all, (vectors_out, gates_out),
        (small_send, small_recv, all_send, all_recv),
    )
    rows, width = tokens_ref.shape
    shard = width // 4
    band = min(128, rows)
    lead = small.shape[0]

    def vector(which):
        parts = [vectors_ref[i, which : which + 1, :] for i in range(4)]
        return jnp.concatenate(parts, axis=1).astype(jnp.float32)

    gain_one, gain_two = vector(0), vector(2)
    small[: lead - gates, :] = jnp.zeros((lead - gates, width), jnp.float32)
    small[lead - gates :, :] = router_ref[:gates, :]

    def post(i):
        part = span(i * band, band)
        grad = dot_nn(back_ref[part, :], home_grad_ref.reshape(rows, width)[...])
        scaled, inverse = norm_stats(hidden_ref[part, :])
        value = cot_ref[part, :].astype(jnp.float32) + norm_back_rows(
            grad, scaled, inverse, gain_two
        )
        tokens_out[part, :] = value
        attn[part, :] = value.astype(jnp.bfloat16)
        small[2:3, :] += jnp.sum(grad * scaled, axis=0, keepdims=True)
        small[3:4, :] += jnp.sum(grad, axis=0, keepdims=True)

    every(0, rows // band, post)
    loads[0].wait()

    def weight_grad(part, n, left, right):
        value = dot_nn(left[...], right).astype(jnp.bfloat16)
        part[n] = value.reshape(part.shape[1:])

    tile_o = part_o.shape[-1]
    out_chunks = part_o.shape[0]
    for n in range(out_chunks):
        weight_grad(part_o, n, merged_t, attn[:, n * tile_o : (n + 1) * tile_o])
        reduce_o.swap(n)
    loads[1].wait()

    def merged_band(i):
        part = span(i * band, band)
        grad_merged[part, :] = dot_nt(attn[part, :], out_w[...]).astype(jnp.bfloat16)

    every(0, rows // band, merged_band)
    stages_o, stages_q = reduce_o.stages(), reduce_q.stages()
    for n in range(out_chunks):
        stages_o[0](n)
    for load in loads[2:]:
        load.wait()
    grad_act[...] = jnp.zeros_like(grad_act)
    pairs = part_q.shape[0]

    def attend_pair(i):
        slot = lax.rem(i, 2)
        for load in load_probs(i):
            load.wait()

        @pl.when(i + 1 < pairs)
        def _():
            for load in load_probs(i + 1):
                load.start()

        cols = span(i * LANES, LANES)
        query, key, value = (
            qkv[:, span(part * width + i * LANES, LANES)] for part in range(3)
        )
        grad = grad_merged[:, cols]
        results = []
        for head in range(2):
            part = slice(head * HEAD_DIM, (head + 1) * HEAD_DIM)
            results.append(
                attend_back_head(
                    query[:, part], key[:, part], value[:, part],
                    low_buf[slot, head], high_buf[slot, head], grad[:, part],
                )
            )
        for which in range(3):
            grad_qkv[:, span(which * width + i * LANES, LANES)] = jnp.concatenate(
                [results[0][which], results[1][which]], axis=1
            )
        right = jnp.concatenate(
            [grad_qkv[:, span(which * width + i * LANES, LANES)] for which in range(3)], axis=1
        )
        weight_grad(part_q, i, act_t, right)
        reduce_q.swap(i)
        columns = jnp.concatenate(
            [weight[:, span(which * width + i * LANES, LANES)] for which in range(3)], axis=1
        )
        grad_act[...] += dot_nt(right, columns)

    def input_band(i):
        part = span(i * band, band)
        grad = grad_act[part, :]
        scaled, inverse = norm_stats(tokens_ref[part, :].astype(jnp.float32))
        tokens_out[part, :] += norm_back_rows(grad, scaled, inverse, gain_one)
        small[0:1, :] += jnp.sum(grad * scaled, axis=0, keepdims=True)
        small[1:2, :] += jnp.sum(grad, axis=0, keepdims=True)

    def output_band(i):
        part = span(i * band, band)
        slots = home_out.reshape(rows, width)
        value = hidden_ref[part, :] + dot_nn(back_ref[part, :], slots[...])
        output_ref[part, :] = value.astype(jnp.bfloat16)

    def store_q(i):
        return [
            pltpu.make_async_copy(
                done_q.at[i, :, pl.ds(which * LANES, LANES)],
                qkv_out.at[:, span(which * width + i * LANES, LANES)],
                out_sem.at[which, i],
            )
            for which in range(3)
        ]

    def store_o(n):
        return pltpu.make_async_copy(
            done_o.at[n], out_out.at[:, span(n * tile_o, tile_o)], out_sem.at[3, n]
        )

    delays = (1, 3, 4, 5, 6, 7, 8, 9)
    turns_o = (-1, 3, 5, 6, 7, 8, 9, 10)
    last = len(delays) - 1
    half = rows // band // 2

    def slot_step(slot):
        @pl.when(slot + EARLY_CHUNKS < groups)
        def _():
            for expert in range(experts):
                late.finish(slot + EARLY_CHUNKS, expert)

        pl.when(slot < pairs)(lambda: attend_pair(slot))
        for s in range(last, -1, -1):
            n = slot - delays[s]

            @pl.when((n >= 0) & (n < pairs))
            def _(s=s, n=n):
                stages_q[s](n)
                if s == last:
                    for copy in store_q(n):
                        copy.start()

            @pl.when(slot == turns_o[s])
            def _(s=s):
                for n in range(out_chunks):
                    stages_o[s](n)
                    if s == last:
                        store_o(n).start()

        @pl.when(slot == pairs)
        def _():
            every(0, half, input_band)

        pl.when(slot == pairs + 1)(lambda: every(half, 2 * half, input_band))
        pl.when(slot == pairs + 2)(smalls.swap)
        pl.when(slot == pairs + 3)(smalls.cross)
        pl.when(slot == pairs + 4)(smalls.spread)

        @pl.when(slot == pairs + 3)
        def _():
            late.arrived(EARLY_CHUNKS, groups, experts)
            every(0, 2 * EARLY_CHUNKS, lambda n: early_rows(n).wait())
            every(0, rows // band, output_band)

    every(0, pairs + delays[-1], slot_step)
    smalls.finish()

    def stored(i):
        for copy in store_q(i):
            copy.wait()

    every(0, pairs, stored)
    for n in range(out_chunks):
        store_o(n).wait()
    late.drain(EARLY_CHUNKS, groups, experts)
    reduce_o.drain()
    reduce_q.drain()
    smalls.drain()


def run_back(
    owners, capacity, gates, home_grad, far_sums, near_sums, home_out, back, hidden, cotangent, tokens,
    vectors, router_grad, act_t, merged_t, qkv, weight, w_out, low, high,
):
    rows, width = tokens.shape
    shard = width // 4
    lead = 8 + gates
    groups = owners // 2
    pairs = width // LANES
    tile_o = min(512, width)
    out_chunks = width // tile_o
    half = shard // 2
    mid = rows // 2
    any_spec = pl.BlockSpec(memory_space=pl.ANY)
    vmem_spec = pl.BlockSpec(memory_space=pltpu.VMEM)
    bf16, f32 = jnp.bfloat16, jnp.float32
    dma = pltpu.SemaphoreType.DMA

    def vm(*shape):
        return pltpu.VMEM(shape, bf16)

    def fm(*shape):
        return pltpu.VMEM(shape, f32)

    def reduce_buffers(chunks, tile, pair_first):
        far, pair = ((half,), (2, half)) if pair_first else ((shard,), (half,))
        return [
            vm(chunks, 2, 2, shard, tile),
            vm(chunks, 2, shard, tile),
            vm(chunks, *far, tile),
            vm(chunks, *pair, tile),
            vm(chunks, half // 2, tile),
            vm(chunks, half // 4, tile),
            vm(chunks, shard, tile),
        ]

    def reduce_sems(chunks):
        return [dma((8, chunks)), dma((8, chunks))]

    return pl.pallas_call(
        functools.partial(back_kernel, (owners, capacity, gates)),
        out_shape=(
            jax.ShapeDtypeStruct((rows, width), bf16),
            jax.ShapeDtypeStruct((rows, width), f32),
            jax.ShapeDtypeStruct((8, shard), f32),
            jax.ShapeDtypeStruct((gates, shard), f32),
            jax.ShapeDtypeStruct((shard, 3 * width), bf16),
            jax.ShapeDtypeStruct((shard, width), bf16),
        ),
        in_specs=[vmem_spec] * 7 + [any_spec] * 10,
        out_specs=(vmem_spec,) * 4 + (any_spec,) * 2,
        scratch_shapes=[
            vm(*near_sums.shape),
            vm(*near_sums.shape),
            vm(*home_grad.shape),
            vm(*home_grad.shape),
            vm(width, rows),
            vm(width, rows),
            vm(rows, 3 * width),
            vm(width, 3 * width),
            vm(width, width),
            vm(2, 2, mid, mid),
            vm(2, 2, mid, rows),
            vm(rows, width),
            vm(rows, width),
            fm(rows, width),
        ]
        + reduce_buffers(pairs, 3 * LANES, False)
        + reduce_buffers(out_chunks, tile_o, True)
        + [
            fm(lead, width),
            fm(2, 2, lead, shard),
            fm(2, lead, shard),
            fm(lead, shard),
            fm(lead, shard),
            fm(lead, shard),
            fm(owners, lead, shard),
            dma((6,)),
            dma((2, 2)),
            dma((near_sums.shape[0],)),
            dma((owners,)),
            dma((groups, near_sums.shape[0])),
            dma((groups, near_sums.shape[0])),
            dma((owners, near_sums.shape[0])),
            dma((owners, near_sums.shape[0])),
        ]
        + reduce_sems(pairs)
        + reduce_sems(out_chunks)
        + [dma((2,)), dma((2,)), dma((owners,)), dma((owners,)), dma((4, pairs))],
        compiler_params=pltpu.CompilerParams(
            collective_id=2, has_side_effects=True, vmem_limit_bytes=VMEM_LIMIT
        ),
        name="back",
    )(
        home_grad, back, hidden, cotangent, tokens, vectors, router_grad,
        far_sums, near_sums, home_out, act_t, merged_t, qkv, weight, w_out, low, high,
    )


def widen_kernel(*refs):
    count = len(refs) // 2
    for src, dst in zip(refs[:count], refs[count:]):
        dst[...] = src[...].astype(dst.dtype)


def widen(steps, values, kinds):
    def spec(value):
        if value.shape[0] % (16 * steps):
            return pl.BlockSpec(value.shape, lambda i: (0, 0))
        return pl.BlockSpec((value.shape[0] // steps, value.shape[1]), lambda i: (i, 0))

    return pl.pallas_call(
        widen_kernel,
        grid=(steps,),
        in_specs=[spec(value) for value in values],
        out_specs=[spec(value) for value in values],
        out_shape=[
            jax.ShapeDtypeStruct(value.shape, kind) for value, kind in zip(values, kinds)
        ],
        name="widen",
    )(*values)


def on_device_plain(
    tokens,
    norm1_gain,
    norm1_shift,
    w_qkv,
    w_out,
    norm2_gain,
    norm2_shift,
    w_router,
    w_up,
    w_down,
    routes,
    priority,
    prefix,
    cotangent,
):
    row_count, model_width = tokens.shape
    expert_count = w_router.shape[1]
    capacity = row_count // expert_count
    owners = lax.axis_size("expert")
    local_experts = w_up.shape[0]
    slot_count = expert_count * capacity
    prefix_len = prefix[0]
    small = jnp.concatenate(
        [
            norm1_gain[None],
            norm1_shift[None],
            norm2_gain[None],
            norm2_shift[None],
            w_router.T,
        ],
        axis=0,
    )
    qkv_full = lax.all_gather(w_qkv, "wshard", axis=0, tiled=True)
    small_full = lax.all_gather(small, "wshard", axis=1, tiled=True)
    out_full = lax.all_gather(w_out, "wshard", axis=0, tiled=True)
    gain_one, shift_one, gain_two, shift_two = (small_full[i] for i in range(4))
    router_full = small_full[4:].T
    gain_one = gain_one.astype(jnp.float32)
    gain_two = gain_two.astype(jnp.float32)
    inputs = tokens.astype(jnp.float32)
    normed_one, scaled_one, inverse_one = normalize(inputs, gain_one, shift_one.astype(jnp.float32))
    act_one = normed_one.astype(jnp.bfloat16)
    qkv = jnp.dot(act_one, qkv_full, preferred_element_type=jnp.float32).astype(jnp.bfloat16)
    query_heads = qkv[:, :model_width]
    key_heads = qkv[:, model_width : 2 * model_width]
    value_heads = qkv[:, 2 * model_width :]
    merged, log_totals = attend_forward(query_heads, key_heads, value_heads, prefix_len)
    attn_out = jnp.dot(merged, out_full, preferred_element_type=jnp.float32)
    hidden = inputs + attn_out
    normed_two, scaled_two, inverse_two = normalize(hidden, gain_two, shift_two.astype(jnp.float32))
    act_two = normed_two.astype(jnp.bfloat16)
    logits = jnp.dot(act_two, router_full, preferred_element_type=jnp.float32)
    row_max = jnp.max(logits, axis=-1, keepdims=True)
    exponent = jnp.exp(logits - row_max)
    gate_prob = exponent / jnp.sum(exponent, axis=-1, keepdims=True)
    route_ids = routes[:, 0]
    chosen = route_ids[:, None] == jnp.arange(expert_count, dtype=jnp.int32)[None, :]
    gate_value = jnp.sum(jnp.where(chosen, gate_prob, 0.0), axis=1)
    slot_index, slot_source = assign_slots(route_ids, priority[0], expert_count, capacity)
    zero_row = jnp.zeros((1, model_width), jnp.bfloat16)
    padded = jnp.concatenate([act_two, zero_row], axis=0)
    send_rows = padded[slot_source].reshape(owners, local_experts * capacity, model_width)
    arrived = lax.all_to_all(send_rows, "expert", split_axis=0, concat_axis=0, tiled=True).reshape(
        owners, local_experts, capacity, model_width
    )
    group = lax.axis_size("wshard")
    local_rows = owners * capacity

    def by_expert(chunk):
        rows = jnp.transpose(chunk, (1, 0, 2, 3)).reshape(local_experts, local_rows, model_width)
        return lax.all_gather(rows, "wshard", axis=1, tiled=True)

    def home_rows(rows):
        own = lax.psum_scatter(rows.astype(jnp.bfloat16), "wshard", scatter_dimension=1, tiled=True)
        own = own.reshape(local_experts, owners, capacity, model_width)
        return jnp.transpose(own, (1, 0, 2, 3)).reshape(
            owners, local_experts * capacity, model_width
        )

    grad_output = cotangent.astype(jnp.float32)
    grad_combined = (gate_value[:, None] * grad_output).astype(jnp.bfloat16)
    grad_padded = jnp.concatenate([grad_combined, zero_row], axis=0)
    grad_send = grad_padded[slot_source].reshape(owners, local_experts * capacity, model_width)
    grad_arrived = lax.all_to_all(
        grad_send, "expert", split_axis=0, concat_axis=0, tiled=True
    ).reshape(owners, local_experts, capacity, model_width)
    rows_in = by_expert(arrived)
    grad_rows = by_expert(grad_arrived)
    pre_act = jnp.einsum("erd,edf->erf", rows_in, w_up, preferred_element_type=jnp.float32)
    activated, gelu_pull = jax.vjp(gelu_tanh, pre_act)
    act_hidden = activated.astype(jnp.bfloat16)
    produced = jnp.einsum(
        "erf,efd->erd", act_hidden, w_down, preferred_element_type=jnp.float32
    )
    expert_out = home_rows(produced)
    returned = lax.all_to_all(expert_out, "expert", split_axis=0, concat_axis=0, tiled=True)
    slots_back = jnp.concatenate([returned.reshape(slot_count, model_width), zero_row], axis=0)
    combined = slots_back[slot_index].astype(jnp.float32)
    output = (hidden + gate_value[:, None] * combined).astype(jnp.bfloat16)
    grad_gate = jnp.sum(grad_output * combined, axis=1)
    grad_down = jnp.einsum(
        "erf,erd->efd", act_hidden, grad_rows, preferred_element_type=jnp.float32
    )
    grad_hidden_units = jnp.einsum(
        "erd,efd->erf", grad_rows, w_down, preferred_element_type=jnp.float32
    )
    grad_pre = gelu_pull(grad_hidden_units)[0].astype(jnp.bfloat16)
    grad_up = jnp.einsum("erd,erf->edf", rows_in, grad_pre, preferred_element_type=jnp.float32)
    grad_expert_in = jnp.einsum(
        "erf,edf->erd", grad_pre, w_up, preferred_element_type=jnp.float32
    )
    grad_send_back = home_rows(grad_expert_in)
    grad_back = lax.all_to_all(grad_send_back, "expert", split_axis=0, concat_axis=0, tiled=True)
    grad_slots = jnp.concatenate([grad_back.reshape(slot_count, model_width), zero_row], axis=0)
    grad_act_two = grad_slots[slot_index].astype(jnp.float32)
    grad_logits = (
        gate_prob * (jnp.where(chosen, grad_gate[:, None], 0.0) - (gate_value * grad_gate)[:, None])
    ).astype(jnp.bfloat16)
    grad_router = contract_rows(act_two, grad_logits)
    grad_act_two = grad_act_two + times_transpose(grad_logits, router_full)
    grad_from_two, grad_gain_two, grad_shift_two = norm_back(
        grad_act_two, scaled_two, inverse_two, gain_two
    )
    grad_hidden = grad_output + grad_from_two
    grad_attn = grad_hidden.astype(jnp.bfloat16)
    grad_out_w = contract_rows(merged, grad_attn)
    grad_merged = times_transpose(grad_attn, out_full).astype(jnp.bfloat16)
    grad_qkv = attend_backward(
        query_heads, key_heads, value_heads, grad_merged, log_totals, prefix_len
    )
    grad_qkv_w = contract_rows(act_one, grad_qkv)
    grad_act_one = times_transpose(grad_qkv, qkv_full)
    grad_from_one, grad_gain_one, grad_shift_one = norm_back(
        grad_act_one, scaled_one, inverse_one, gain_one
    )
    grad_tokens = grad_hidden + grad_from_one
    small_grad = jnp.concatenate(
        [
            grad_gain_one[None],
            grad_shift_one[None],
            grad_gain_two[None],
            grad_shift_two[None],
            grad_router.T,
        ],
        axis=0,
    )
    out_share = lax.psum_scatter(
        grad_out_w.astype(jnp.bfloat16), "wshard", scatter_dimension=0, tiled=True
    )
    qkv_share = lax.psum_scatter(
        grad_qkv_w.astype(jnp.bfloat16), "wshard", scatter_dimension=0, tiled=True
    )
    small_share = lax.psum_scatter(small_grad, "wshard", scatter_dimension=1, tiled=True)
    out_total = lax.psum(out_share, "expert").astype(jnp.float32)
    qkv_total = lax.psum(qkv_share, "expert").astype(jnp.float32)
    small_total = lax.psum(small_share, "expert")
    totals = (
        small_total[0],
        small_total[1],
        qkv_total,
        out_total,
        small_total[2],
        small_total[3],
        small_total[4:].T,
    )
    return (
        output,
        grad_tokens,
        totals[0],
        totals[1],
        totals[2],
        totals[3],
        totals[4],
        totals[5],
        totals[6],
        grad_up,
        grad_down,
    )


def on_device(
    tokens,
    norm1_gain,
    norm1_shift,
    w_qkv,
    w_out,
    norm2_gain,
    norm2_shift,
    w_router,
    w_up,
    w_down,
    routes,
    priority,
    prefix,
    cotangent,
):
    row_count, model_width = tokens.shape
    expert_count = w_router.shape[1]
    capacity = row_count // expert_count
    owners = lax.axis_size("expert")
    experts = w_up.shape[0]
    which = lax.broadcasted_iota(jnp.int32, (16, norm1_gain.shape[0]), 0)
    small = jnp.zeros(which.shape, jnp.bfloat16)
    for i, vector in enumerate((norm1_gain, norm1_shift, norm2_gain, norm2_shift)):
        small = jnp.where(which == i, vector[None], small)
    (
        qkv, act_t, merged_t, back, weight, out_full, low, high, grad_rows, hidden, send_rows,
        vectors, router,
    ) = run_front(
        owners, experts, capacity, prefix, routes.reshape(1, row_count), priority, tokens,
        cotangent, small, w_router.T, w_qkv, w_out,
    )
    far_sums, near_sums, home_out, home_grad, grad_up, grad_down, grad_router = run_experts(
        owners, capacity, expert_count, send_rows, grad_rows, w_up, w_down, router
    )
    output, grad_tokens, grad_vectors, grad_gates, grad_qkv, grad_out = run_back(
        owners, capacity, expert_count, home_grad, far_sums, near_sums, home_out, back, hidden, cotangent,
        tokens, vectors, grad_router, act_t, merged_t, qkv, weight, out_full, low, high,
    )
    f32 = jnp.float32
    units = w_up.shape[2]
    output, grad_tokens, grad_gates, grad_qkv, grad_out, grad_up, grad_down = widen(
        2,
        (
            output, grad_tokens, grad_gates, grad_qkv, grad_out,
            grad_up.reshape(-1, units), grad_down.reshape(-1, model_width),
        ),
        (output.dtype,) + (f32,) * 6,
    )
    return (
        output,
        grad_tokens,
        grad_vectors[0],
        grad_vectors[1],
        grad_qkv,
        grad_out,
        grad_vectors[2],
        grad_vectors[3],
        grad_gates.T,
        grad_up.reshape(w_up.shape),
        grad_down.reshape(w_down.shape),
    )


def solution(mesh):
    placed = (
        P(("expert", "wshard"), None),
        P("wshard"),
        P("wshard"),
        P("wshard", None),
        P("wshard", None),
        P("wshard"),
        P("wshard"),
        P("wshard", None),
        P("expert", None, "wshard"),
        P("expert", "wshard", None),
        P(("expert", "wshard"), None),
        P(("expert", "wshard"), None),
        P(("expert", "wshard")),
        P(("expert", "wshard"), None),
    )
    owners, group = mesh.shape["expert"], mesh.shape["wshard"]

    def body(*args):
        capacity = args[0].shape[0] // args[7].shape[1]
        fits = group == 4 and owners == 8 and capacity % 16 == 0 and args[7].shape[1] % 16 == 0
        return (on_device if fits else on_device_plain)(*args)

    return jax.shard_map(
        body,
        mesh=mesh,
        in_specs=placed,
        out_specs=(
            P(("expert", "wshard"), None),
            P(("expert", "wshard"), None),
            P("wshard"),
            P("wshard"),
            P("wshard", None),
            P("wshard", None),
            P("wshard"),
            P("wshard"),
            P("wshard", None),
            P("expert", None, "wshard"),
            P("expert", "wshard", None),
        ),
        check_vma=False,
    )
```

```python
import functools
import math

import jax
import jax.numpy as jnp
from jax import lax
from jax.experimental import pallas as pl
from jax.experimental.pallas import tpu as pltpu
from jax.sharding import PartitionSpec as P

HEADS = 16
HEAD_DIM = 64


epsilon = 1e-05
VMEM_LIMIT = 66_000_000
TILE = 1024
EARLY_CHUNKS = 1


def normalize(values, gain_vec, shift_vec):
    row_mean = jnp.mean(values, axis=-1, keepdims=True)
    centered = values - row_mean
    inverse = lax.rsqrt(jnp.mean(centered * centered, axis=-1, keepdims=True) + epsilon)
    scaled = centered * inverse
    return (scaled * gain_vec + shift_vec, scaled, inverse)


def norm_back(grad_rows, scaled, inverse, gain_vec):
    weighted = grad_rows * gain_vec
    mean_one = jnp.mean(weighted, axis=-1, keepdims=True)
    mean_two = jnp.mean(weighted * scaled, axis=-1, keepdims=True)
    grad_inputs = inverse * (weighted - mean_one - scaled * mean_two)
    return (grad_inputs, jnp.sum(grad_rows * scaled, axis=0), jnp.sum(grad_rows, axis=0))


def contract_rows(left, right):
    return lax.dot_general(
        left, right, (((0,), (0,)), ((), ())), preferred_element_type=jnp.float32
    )


def times_transpose(left, right):
    return lax.dot_general(
        left, right, (((1,), (1,)), ((), ())), preferred_element_type=jnp.float32
    )


def gelu_tanh(values):
    return jax.nn.gelu(values, approximate=True)


def assign_slots(route_ids, order_ids, expert_count, capacity):
    token_count = route_ids.shape[0]
    same_expert = route_ids[:, None] == route_ids[None, :]
    earlier = order_ids[None, :] < order_ids[:, None]
    rank_ids = jnp.sum((same_expert & earlier).astype(jnp.int32), axis=1)
    is_kept = rank_ids < capacity
    slot_index = jnp.where(is_kept, route_ids * capacity + rank_ids, expert_count * capacity)
    slot_ids = jnp.arange(expert_count * capacity, dtype=jnp.int32)
    match_table = slot_index[None, :] == slot_ids[:, None]
    token_ids = jnp.arange(token_count, dtype=jnp.int32)
    filled = jnp.any(match_table, axis=1)
    picked = jnp.sum(jnp.where(match_table, token_ids[None, :], 0), axis=1)
    slot_source = jnp.where(filled, picked, token_count)
    return (slot_index, slot_source)


def group_heads(values, groups):
    token_count = values.shape[0]
    return jnp.transpose(values.reshape(token_count, groups, -1, HEAD_DIM), (1, 0, 2, 3))


def block_scores(query_block, key_group, block_start, prefix_len):
    block_rows = query_block.shape[0]
    key_count = key_group.shape[0]
    scores = jnp.einsum(
        "qgd,kgd->gqk", query_block, key_group, preferred_element_type=jnp.float32
    ) * (1.0 / math.sqrt(HEAD_DIM))
    query_pos = block_start + jnp.arange(block_rows, dtype=jnp.int32)
    key_pos = jnp.arange(key_count, dtype=jnp.int32)
    allowed = (key_pos[None, :] <= query_pos[:, None]) | (key_pos[None, :] < prefix_len)
    return jnp.where(allowed[None], scores, -1e30)


def attend_forward(query_heads, key_heads, value_heads, prefix_len):
    token_count = query_heads.shape[0]
    group_size = min(4, HEADS)
    groups = HEADS // group_size
    block_rows = min(512, token_count)
    blocks = token_count // block_rows
    starts = jnp.arange(blocks, dtype=jnp.int32) * block_rows

    def one_group(group_item):
        query_group, key_group, value_group = group_item
        query_blocks = query_group.reshape(blocks, block_rows, group_size, HEAD_DIM)

        def one_block(block_item):
            query_block, block_start = block_item
            scores = block_scores(query_block, key_group, block_start, prefix_len)
            row_max = jnp.max(scores, axis=-1, keepdims=True)
            exponent = jnp.exp(scores - row_max)
            row_total = jnp.sum(exponent, axis=-1, keepdims=True)
            attn_probs = (exponent / row_total).astype(jnp.bfloat16)
            result = jnp.einsum(
                "gqk,kgd->qgd", attn_probs, value_group, preferred_element_type=jnp.float32
            )
            return (result, (row_max + jnp.log(row_total))[..., 0])

        return lax.map(one_block, (query_blocks, starts))

    attended, log_totals = lax.map(
        one_group,
        (
            group_heads(query_heads, groups),
            group_heads(key_heads, groups),
            group_heads(value_heads, groups),
        ),
    )
    merged = (
        jnp.transpose(attended, (1, 2, 0, 3, 4))
        .reshape(token_count, HEADS * HEAD_DIM)
        .astype(jnp.bfloat16)
    )
    return (merged, log_totals)


def attend_backward(query_heads, key_heads, value_heads, grad_merged, log_totals, prefix_len):
    token_count = query_heads.shape[0]
    group_size = min(4, HEADS)
    groups = HEADS // group_size
    block_rows = min(512, token_count)
    blocks = token_count // block_rows
    starts = jnp.arange(blocks, dtype=jnp.int32) * block_rows
    score_scale = 1.0 / math.sqrt(HEAD_DIM)

    def one_group(group_item):
        query_group, key_group, value_group, grad_group, total_group = group_item
        query_blocks = query_group.reshape(blocks, block_rows, group_size, HEAD_DIM)
        grad_blocks = grad_group.reshape(blocks, block_rows, group_size, HEAD_DIM)

        def one_block(carry, block_item):
            grad_keys, grad_vals = carry
            query_block, grad_block, total_block, block_start = block_item
            scores = block_scores(query_block, key_group, block_start, prefix_len)
            attn_probs = jnp.exp(scores - total_block[..., None])
            grad_probs = jnp.einsum(
                "qgd,kgd->gqk", grad_block, value_group, preferred_element_type=jnp.float32
            )
            row_delta = jnp.sum(attn_probs * grad_probs, axis=-1, keepdims=True)
            grad_scores = (attn_probs * (grad_probs - row_delta)).astype(jnp.bfloat16)
            grad_vals = grad_vals + jnp.einsum(
                "gqk,qgd->kgd",
                attn_probs.astype(jnp.bfloat16),
                grad_block,
                preferred_element_type=jnp.float32,
            )
            grad_keys = (
                grad_keys
                + jnp.einsum(
                    "gqk,qgd->kgd", grad_scores, query_block, preferred_element_type=jnp.float32
                )
                * score_scale
            )
            grad_query = (
                jnp.einsum(
                    "gqk,kgd->qgd", grad_scores, key_group, preferred_element_type=jnp.float32
                )
                * score_scale
            )
            return ((grad_keys, grad_vals), grad_query)

        zero_keys = jnp.zeros(key_group.shape, jnp.float32)
        carried, grad_queries = lax.scan(
            one_block, (zero_keys, zero_keys), (query_blocks, grad_blocks, total_group, starts)
        )
        return (grad_queries, carried[0], carried[1])

    grad_queries, grad_keys, grad_vals = lax.map(
        one_group,
        (
            group_heads(query_heads, groups),
            group_heads(key_heads, groups),
            group_heads(value_heads, groups),
            group_heads(grad_merged, groups),
            log_totals,
        ),
    )
    query_part = jnp.transpose(grad_queries, (1, 2, 0, 3, 4)).reshape(token_count, HEADS * HEAD_DIM)
    key_part = jnp.transpose(grad_keys, (1, 0, 2, 3)).reshape(token_count, HEADS * HEAD_DIM)
    value_part = jnp.transpose(grad_vals, (1, 0, 2, 3)).reshape(token_count, HEADS * HEAD_DIM)
    return jnp.concatenate([query_part, key_part, value_part], axis=1).astype(jnp.bfloat16)


MESH = pl.DeviceIdType.MESH
LANES = 128


def dot_nn(left, right):
    return lax.dot_general(
        left, right, (((1,), (0,)), ((), ())), preferred_element_type=jnp.float32
    )


def dot_nt(left, right):
    return lax.dot_general(
        left, right, (((1,), (1,)), ((), ())), preferred_element_type=jnp.float32
    )


def dot_tn(left, right):
    return lax.dot_general(
        left, right, (((0,), (0,)), ((), ())), preferred_element_type=jnp.float32
    )


def span(start, size):
    return pl.ds(pl.multiple_of(start, size), size)


def every(start, stop, step):
    def body(i, carry):
        step(i)
        return carry

    lax.fori_loop(start, stop, body, 0)


class Place:
    def __init__(self, owners):
        self.owners = owners
        self.e = lax.axis_index("expert")
        self.w = lax.axis_index("wshard")
        self.c = lax.rem(self.w, 2)
        self.x = lax.div(self.w, 2)
        self.sib = self.w + 1 - 2 * self.c
        self.far = lax.rem(self.w + 2, 4)
        self.diag = 3 - self.w
        self.pair = self.e + 1 - 2 * lax.rem(self.e, 2)

    def ahead(self, k):
        return lax.rem(self.e + k, self.owners)

    def flip(self, bit):
        return self.e + bit * (1 - 2 * lax.rem(lax.div(self.e, bit), 2))

    def peer(self, n):
        other = lax.div(n, 2) + lax.rem(n, 2) * (self.owners // 2)
        result, bit = 0, 1
        while bit < self.owners:
            result = result + bit * lax.rem(lax.div(self.e, bit) + lax.div(other, bit), 2)
            bit *= 2
        return result


def remote(src, dst, send, recv, device):
    return pltpu.make_async_remote_copy(
        src_ref=src,
        dst_ref=dst,
        send_sem=send,
        recv_sem=recv,
        device_id=device,
        device_id_type=MESH,
    )


def greet(peers):
    barrier = pltpu.get_barrier_semaphore()
    for peer in peers:
        pl.semaphore_signal(barrier, inc=1, device_id=peer, device_id_type=MESH)
    pl.semaphore_wait(barrier, len(peers))


def either(test, yes, no):
    pl.when(test)(yes)
    pl.when(jnp.logical_not(test))(no)


class Dispatch:
    def __init__(self, place, capacity, send_ref, rows_ref, sems):
        self.p, self.cap, self.src, self.rows = place, capacity, send_ref, rows_ref
        self.own_sem, self.send, self.recv = sems

    def slice(self, k, core, side):
        start = (((lax.div(k, 2) * 2 + core) * 2 + side) * 2 + lax.rem(k, 2)) * self.cap
        return self.rows.at[:, span(start, self.cap)]

    def own(self):
        return pltpu.make_async_copy(
            self.src.at[self.p.e], self.slice(0, self.p.c, self.p.x), self.own_sem
        )

    def direct(self, k):
        return remote(
            self.src.at[self.p.peer(k)],
            self.slice(k, self.p.c, self.p.x),
            self.send.at[0, k],
            self.recv.at[0, k],
            (self.p.peer(k), self.p.w),
        )

    def hop(self, k, side, which, peer):
        part = self.slice(k, self.p.c, side)
        return remote(
            part, part, self.send.at[which, k], self.recv.at[which, k], (self.p.e, peer)
        )

    def to_sib(self, k):
        return self.hop(k, self.p.x, 1, self.p.sib)

    def to_far(self, k):
        return self.hop(k, self.p.x, 2, self.p.far)

    def relayed(self, k):
        return self.hop(k, 1 - self.p.x, 3, self.p.sib)

    def start(self):
        self.own().start()
        every(1, self.p.owners, lambda k: self.direct(k).start())

    def forward(self, k):
        k = jnp.int32(k)

        @pl.when(k == 0)
        def _():
            self.own().wait()

        @pl.when(k > 0)
        def _():
            self.direct(k).wait_recv()

        self.to_far(k).start()
        self.to_sib(k).start()

    def relay(self, k):
        self.to_far(k).wait_recv()
        self.relayed(k).start()

    def ready(self, k):
        self.to_sib(k).wait_recv()
        self.relayed(k).wait_recv()

    def order(self):
        return (0, 2, 4, 1, 6, 3, 5, 7)

    def drain(self):
        every(1, self.p.owners, lambda k: self.direct(k).wait_send())

        def rest(k):
            self.to_sib(k).wait_send()
            self.to_far(k).wait_send()
            self.relayed(k).wait_send()

        every(0, self.p.owners, rest)


class Return:
    def __init__(self, place, capacity, part, got, mid, far, done, home, sems):
        self.p, self.cap = place, capacity
        self.part, self.got, self.mid, self.far, self.done, self.home = (
            part, got, mid, far, done, home,
        )
        self.own_sem, self.send, self.recv, self.home_send, self.home_recv = sems

    def swapped(self, j, expert):
        size = 4 * self.cap
        return remote(
            self.part.at[expert, span((j * 2 + 1 - self.p.c) * size, size)],
            self.got.at[expert, span(j * size, size)],
            self.send.at[0, j, expert],
            self.recv.at[0, j, expert],
            (self.p.e, self.p.sib),
        )

    def crossed(self, j, expert):
        part = span(j * 2 * self.cap, 2 * self.cap)
        return remote(
            self.mid.at[expert, part],
            self.far.at[expert, part],
            self.send.at[1, j, expert],
            self.recv.at[1, j, expert],
            (self.p.e, self.p.far),
        )

    def own(self, expert):
        return pltpu.make_async_copy(
            self.done.at[0, expert], self.home.at[self.p.e, expert], self.own_sem.at[expert]
        )

    def homed(self, n, expert):
        return remote(
            self.done.at[n, expert],
            self.home.at[self.p.e, expert],
            self.home_send.at[n, expert],
            self.home_recv.at[n, expert],
            (self.p.peer(n), self.p.w),
        )

    def pair_sum(self, j, expert, side):
        size = 2 * self.cap
        mine = self.part[expert, span(((j * 2 + self.p.c) * 2 + side) * size, size), :]
        theirs = self.got[expert, span((j * 2 + side) * size, size), :]
        return mine.astype(jnp.float32) + theirs.astype(jnp.float32)

    def swap(self, j, expert):
        self.swapped(j, expert).start()

    def split(self, j, expert):
        self.swapped(j, expert).wait_recv()
        here = span(j * 2 * self.cap, 2 * self.cap)
        self.mid[expert, here, :] = self.pair_sum(j, expert, 1 - self.p.x).astype(jnp.bfloat16)
        self.keep[expert, here, :] = self.pair_sum(j, expert, self.p.x).astype(jnp.bfloat16)

    def cross(self, j, expert):
        self.swapped(j, expert).wait_recv()
        here = span(j * 2 * self.cap, 2 * self.cap)
        self.mid[expert, here, :] = self.pair_sum(j, expert, 1 - self.p.x).astype(jnp.bfloat16)
        self.crossed(j, expert).start()

    def this_side(self, j, expert):
        return self.pair_sum(j, expert, self.p.x)

    def finish(self, j, expert):
        self.crossed(j, expert).wait_recv()
        here = span(j * 2 * self.cap, 2 * self.cap)
        total = self.this_side(j, expert) + self.far[expert, here, :].astype(jnp.float32)
        total = total.astype(jnp.bfloat16)
        self.done[2 * j, expert] = total[: self.cap]
        self.done[2 * j + 1, expert] = total[self.cap :]
        j = jnp.int32(j)
        self.homed(2 * j + 1, expert).start()
        either(
            j == 0,
            lambda: self.own(expert).start(),
            lambda: self.homed(2 * j, expert).start(),
        )

    def drain_swaps(self, chunks, experts):
        for expert in range(experts):
            every(0, chunks, lambda j: self.swapped(j, expert).wait_send())

    def drain(self, first, last, experts):
        for expert in range(experts):
            every(first, last, lambda j: self.crossed(j, expert).wait_send())
            every(
                max(1, 2 * first), 2 * last, lambda n: self.homed(n, expert).wait_send()
            )

    def arrived(self, first, last, experts):
        for expert in range(experts):
            if first == 0 and last > 0:
                self.own(expert).wait()
            every(
                max(1, 2 * first), 2 * last, lambda n: self.homed(n, expert).wait_recv()
            )


class LateReturn(Return):
    def crossed(self, j, expert):
        part = span(j * 2 * self.cap, 2 * self.cap)
        return remote(
            self.mid.at[expert, part],
            self.far.at[expert, part],
            self.send.at[j, expert],
            self.recv.at[j, expert],
            (self.p.e, self.p.far),
        )

    def this_side(self, j, expert):
        here = span(j * 2 * self.cap, 2 * self.cap)
        return self.part[expert, here, :].astype(jnp.float32)


def gelu_pair(v):
    root = math.sqrt(2.0 / math.pi)
    square = v * v
    t = jnp.tanh(v * (root + (root * 0.044715) * square))
    half = 0.5 + 0.5 * t
    slope = half + (half * (1.0 - t)) * (v * (root + (3.0 * root * 0.044715) * square))
    return v * half, slope


def expert_kernel(
    dims,
    send_ref, grads_hbm, up_hbm, down_hbm, router_ref,
    far_sums, near_sums, home_out, home_grad, up_out, down_out, router_grad,
    rows, grads, scaled, hidden, pre, up, down, grad_up, grad_down,
    part_out, part_grad, got_out, got_grad, mid_out, mid_grad,
    keep_out, far_grad, far_out, done_grad, done_out,
    load_sem, own_sem, disp_send, disp_recv, red_send, red_recv, home_send, home_recv,
):
    owners, experts, capacity, width, units, expert_count = dims
    place = Place(owners)
    loads = [
        pltpu.make_async_copy(src, dst, load_sem.at[i])
        for i, (src, dst) in enumerate(
            [(up_hbm, up), (grads_hbm, grads), (down_hbm, down)]
        )
    ]
    for load in loads:
        load.start()
    greet(
        [(place.ahead(k), place.w) for k in range(1, owners)]
        + [(place.e, place.sib), (place.e, place.far)]
    )
    dispatch = Dispatch(
        place, capacity, send_ref, rows, (own_sem.at[0, 0], disp_send, disp_recv)
    )
    ret_grad = Return(
        place, capacity, part_grad, got_grad, mid_grad, far_grad, done_grad, home_grad,
        (own_sem.at[1], red_send.at[0], red_recv.at[0], home_send.at[0], home_recv.at[0]),
    )
    ret_out = Return(
        place, capacity, part_out, got_out, mid_out, far_out, done_out, home_out,
        (own_sem.at[2], red_send.at[1], red_recv.at[1], home_send.at[1], home_recv.at[1]),
    )
    dispatch.start()
    router_grad[...] = jnp.zeros_like(router_grad)
    tile = min(TILE, units)
    wide = min(TILE, width)
    chunks = owners // 2
    early = EARLY_CHUNKS
    size = 8 * capacity
    lane = lax.broadcasted_iota(jnp.int32, (size, LANES), 1)

    def compute(j, expert):
        here = span(j * size, size)
        logits = dot_nt(rows[expert, here, :], router_ref[...])
        logits = jnp.where(lane < expert_count, logits, -1e30)
        exponent = jnp.exp(logits - jnp.max(logits, axis=1, keepdims=True))
        prob = exponent * (1.0 / jnp.sum(exponent, axis=1, keepdims=True))
        mine = lane == place.e * experts + expert
        gate = jnp.sum(jnp.where(mine, prob, 0.0), axis=1, keepdims=True)
        scaled[expert, here, :] = (
            gate * grads[expert, here, :].astype(jnp.float32)
        ).astype(jnp.bfloat16)

        def one_tile(n):
            cols = span(n * tile, tile)
            value, slope = gelu_pair(dot_nn(rows[expert, here, :], up[expert, :, cols]))
            hidden[expert, here, cols] = value.astype(jnp.bfloat16)
            back = pre[expert, here, cols].astype(jnp.float32)
            pre[expert, here, cols] = (gate * back * slope).astype(jnp.bfloat16)

        every(0, units // tile, one_tile)

        def one_out(n, total):
            cols = span(n * wide, wide)
            value = dot_nn(hidden[expert, here, :], down[expert, :, cols])
            part_out[expert, here, cols] = (gate * value).astype(jnp.bfloat16)
            weighted = value * grads[expert, here, cols].astype(jnp.float32)
            for start in range(0, wide, LANES):
                total = total + weighted[:, start : start + LANES]
            return total

        total = lax.fori_loop(
            0, width // wide, one_out, jnp.zeros((size, LANES), jnp.float32)
        )
        grad_gate = jnp.sum(total, axis=1, keepdims=True)
        grad_logits = (
            prob * ((jnp.where(mine, 1.0, 0.0) - gate) * grad_gate)
        ).astype(jnp.bfloat16)

        def one_in(n):
            cols = span(n * wide, wide)
            value = dot_nt(pre[expert, here, :], up[expert, cols, :]) + dot_nn(
                grad_logits, router_ref[:, cols]
            )
            part_grad[expert, here, cols] = value.astype(jnp.bfloat16)
            router_grad[:, cols] += dot_tn(grad_logits, rows[expert, here, cols])

        every(0, width // wide, one_in)

    def unscaled(j, expert):
        here = span(j * size, size)
        pre[expert, here, :] = dot_nt(grads[expert, here, :], down[expert]).astype(jnp.bfloat16)

    block = min(256, width)

    def weight_grads(expert, first, last):
        def one(n):
            part = span(n * block, block)
            grad_down[expert, part, :] = dot_tn(
                hidden[expert, :, part], scaled[expert]
            ).astype(jnp.bfloat16)
            grad_up[expert, part, :] = dot_tn(rows[expert, :, part], pre[expert]).astype(
                jnp.bfloat16
            )

        every(first * width // block // 4, last * width // block // 4, one)

    def keep(expert):
        return [
            pltpu.make_async_copy(src.at[expert], dst.at[expert], load_sem.at[2 * expert + i])
            for i, (src, dst) in enumerate(((grad_up, up_out), (grad_down, down_out)))
        ]

    turns = [(j, expert) for j in range(chunks) for expert in range(experts)]
    ahead, through, here = dispatch.forward, dispatch.relay, dispatch.ready
    plan = [[] for _ in turns]
    for unit, acts in (
        (0, ((here, 0), (here, 1), (ahead, 5))),
        (1, ((through, 6), (ahead, 7))),
        (2, ((through, 3), (here, 2), (here, 3))),
        (3, ((through, 5),)),
        (4, ((through, 7), (here, 4), (here, 5))),
        (6, ((here, 6), (here, 7))),
    ):
        plan[unit].extend(acts)
    for u in range(2, len(turns)):
        done = turns[u - 2]
        plan[u].append((ret_grad.cross,) + done)
        plan[u].append((ret_out.cross if done[0] < early else ret_out.split,) + done)
        if u >= 4:
            done = turns[u - 4]
            plan[u].append((ret_grad.finish,) + done)
            if done[0] < early:
                plan[u].append((ret_out.finish,) + done)
    ret_out.keep = keep_out
    for load in loads:
        load.wait()

    def unscaled_pair(j):
        for expert in range(experts):
            unscaled(j, expert)

    ahead(0)
    unscaled_pair(0)
    unscaled_pair(1)
    ahead(2)
    ahead(4)
    ahead(1)
    unscaled_pair(2)
    through(0)
    unscaled_pair(3)
    through(2)
    ahead(6)
    through(4)
    through(1)
    ahead(3)

    def step(unit):
        for u, acts in enumerate(plan):

            @pl.when(unit == u)
            def _(acts=acts):
                for act, *at in acts:
                    act(*at)

        j, expert = lax.div(unit, experts), lax.rem(unit, experts)
        compute(j, expert)
        ret_grad.swap(j, expert)
        ret_out.swap(j, expert)

    every(0, len(turns), step)
    ret_grad.cross(*turns[-2])
    ret_out.split(*turns[-2])
    ret_grad.finish(*turns[-4])
    weight_grads(0, 0, 1)
    ret_grad.cross(*turns[-1])
    ret_out.split(*turns[-1])
    sums = [
        pltpu.make_async_copy(src, dst, load_sem.at[4 + i])
        for i, (src, dst) in enumerate(((mid_out, far_sums), (keep_out, near_sums)))
    ]
    for store in sums:
        store.start()
    ret_grad.finish(*turns[-3])
    weight_grads(0, 1, 2)
    ret_grad.finish(*turns[-2])
    weight_grads(0, 2, 3)
    ret_grad.finish(*turns[-1])
    weight_grads(0, 3, 4)
    for store in keep(0):
        store.start()
    for expert in range(1, experts):
        weight_grads(expert, 0, 4)
        for store in keep(expert):
            store.start()
    for expert in range(experts):
        for store in keep(expert):
            store.wait()
    for store in sums:
        store.wait()
    dispatch.drain()
    ret_grad.drain_swaps(chunks, experts)
    ret_grad.drain(0, chunks, experts)
    ret_grad.arrived(0, chunks, experts)
    ret_out.drain_swaps(chunks, experts)
    ret_out.drain(0, early, experts)
    ret_out.arrived(0, early, experts)


def run_experts(owners, capacity, expert_count, send_rows, grads, w_up, w_down, router):
    experts, width, units = w_up.shape
    slots = owners * 4 * capacity
    chunks = owners // 2
    dims = (owners, experts, capacity, width, units, expert_count)
    any_spec = pl.BlockSpec(memory_space=pl.ANY)
    vmem_spec = pl.BlockSpec(memory_space=pltpu.VMEM)
    bf16 = jnp.bfloat16
    home = jax.ShapeDtypeStruct((owners, experts, capacity, width), bf16)
    dma = pltpu.SemaphoreType.DMA

    def vm(*shape):
        return pltpu.VMEM(shape, bf16)

    return pl.pallas_call(
        functools.partial(expert_kernel, dims),
        out_shape=(
            jax.ShapeDtypeStruct((experts, slots // 4, width), bf16),
            jax.ShapeDtypeStruct((experts, slots // 4, width), bf16),
            home, home,
            jax.ShapeDtypeStruct(w_up.shape, bf16),
            jax.ShapeDtypeStruct(w_down.shape, bf16),
            jax.ShapeDtypeStruct((LANES, width), jnp.float32),
        ),
        in_specs=[any_spec] * 4 + [vmem_spec],
        out_specs=(any_spec,) * 6 + (vmem_spec,),
        scratch_shapes=[
            vm(experts, slots, width),
            vm(experts, slots, width),
            vm(experts, slots, width),
            vm(experts, slots, units),
            vm(experts, slots, units),
            vm(experts, width, units),
            vm(experts, units, width),
            vm(experts, width, units),
            vm(experts, units, width),
            vm(experts, slots, width),
            vm(experts, slots, width),
            vm(experts, slots // 2, width),
            vm(experts, slots // 2, width),
            vm(experts, slots // 4, width),
            vm(experts, slots // 4, width),
            vm(experts, slots // 4, width),
            vm(experts, slots // 4, width),
            vm(experts, slots // 4, width),
            vm(owners, experts, capacity, width),
            vm(owners, experts, capacity, width),
            dma((6,)),
            dma((3, experts)),
            dma((4, owners)),
            dma((4, owners)),
            dma((2, 2, chunks, experts)),
            dma((2, 2, chunks, experts)),
            dma((2, owners, experts)),
            dma((2, owners, experts)),
        ],
        compiler_params=pltpu.CompilerParams(
            collective_id=1, has_side_effects=True, vmem_limit_bytes=VMEM_LIMIT
        ),
        name="experts",
    )(send_rows, grads, w_up, w_down, router)


def masked_softmax(scores):
    exponent = jnp.exp(scores - jnp.max(scores, axis=1, keepdims=True))
    return exponent * (1.0 / jnp.sum(exponent, axis=1, keepdims=True))


def attend_head(query, key, value, prefix_len):
    half = query.shape[0] // 2
    query = query * (1.0 / math.sqrt(HEAD_DIM))
    row = lax.broadcasted_iota(jnp.int32, (half, half), 0)
    col = lax.broadcasted_iota(jnp.int32, (half, half), 1)
    low = dot_nt(query[:half], key[:half])
    low = jnp.where((col <= row) | (col < prefix_len), low, -1e30)
    low = masked_softmax(low).astype(jnp.bfloat16)
    high = dot_nt(query[half:], key)
    high = jnp.concatenate(
        [high[:, :half], jnp.where(col <= row, high[:, half:], -1e30)], axis=1
    )
    high = masked_softmax(high).astype(jnp.bfloat16)
    return low, high, dot_nn(low, value[:half]), dot_nn(high, value)


def score_grads(probs, grad_probs):
    probs = probs.astype(jnp.float32)
    weighted = probs * grad_probs
    total = jnp.sum(weighted, axis=1, keepdims=True)
    return (weighted - probs * total).astype(jnp.bfloat16)


def attend_back_head(query, key, value, low, high, grad):
    half = query.shape[0] // 2
    scale = 1.0 / math.sqrt(HEAD_DIM)
    query = query * scale
    grad_low = score_grads(low, dot_nt(grad[:half], value[:half]))
    grad_high = score_grads(high, dot_nt(grad[half:], value))
    grad_query = jnp.concatenate(
        [dot_nn(grad_low, key[:half]), dot_nn(grad_high, key)], axis=0
    )
    value_all = dot_tn(high, grad[half:])
    key_all = dot_tn(grad_high, query[half:])
    grad_value = jnp.concatenate(
        [value_all[:half] + dot_tn(low, grad[:half]), value_all[half:]], axis=0
    )
    grad_key = jnp.concatenate(
        [key_all[:half] + dot_tn(grad_low, query[:half]), key_all[half:]], axis=0
    )
    return (
        (grad_query * scale).astype(jnp.bfloat16),
        grad_key.astype(jnp.bfloat16),
        grad_value.astype(jnp.bfloat16),
    )


class Gather:
    def __init__(self, place, pieces, parts, src, dst, sems):
        self.p, self.src, self.dst, self.pieces, self.parts = place, src, dst, pieces, parts
        self.send, self.recv = sems
        self.shard = src.shape[0]
        self.half = self.shard // 2
        self.width = src.shape[1] // parts
        self.step = self.width // pieces
        self.first = lax.rem(place.e, 2) * self.half
        self.second = self.half - self.first

    def cols(self, n, part):
        return span(part * self.width + n * self.step, self.step)

    def block(self, owner, start, size, n, part):
        rows = pl.ds(pl.multiple_of(owner * self.shard + start, self.half), size)
        return self.dst.at[rows, self.cols(n, part)]

    def move(self, which, n, part, src, dst, device):
        return remote(
            src, dst, self.send.at[which, n, part], self.recv.at[which, n, part], device
        )

    def own(self, n, part):
        return pltpu.make_async_copy(
            self.src.at[:, self.cols(n, part)],
            self.block(self.p.w, 0, self.shard, n, part),
            self.recv.at[5, n, part],
        )

    def near(self, n, part):
        return self.move(
            4, n, part, self.src.at[:, self.cols(n, part)],
            self.block(self.p.w, 0, self.shard, n, part), (self.p.e, self.p.sib),
        )

    def hop(self, n, part):
        return self.move(
            0, n, part, self.src.at[span(self.first, self.half), self.cols(n, part)],
            self.block(self.p.w, self.first, self.half, n, part), (self.p.e, self.p.far),
        )

    def pass_from(self, which, start, n, part, device):
        block = self.block(self.p.far, start, self.half, n, part)
        return self.move(which, n, part, block, block, device)

    def pairs(self, n, part):
        return self.pass_from(1, self.first, n, part, (self.p.pair, self.p.w))

    def relay(self, n, part):
        return self.pass_from(2, self.first, n, part, (self.p.e, self.p.sib))

    def pair_relay(self, n, part):
        return self.pass_from(3, self.second, n, part, (self.p.e, self.p.sib))

    def all_parts(self, n, act):
        for part in range(self.parts):
            act(n, part)

    def start_own(self):
        every(
            0, self.pieces, lambda n: self.all_parts(n, lambda n, part: self.own(n, part).start())
        )

    def start(self):
        def hop(n, part):
            self.hop(n, part).start()

        def near(n, part):
            self.near(n, part).start()

        every(0, self.pieces, lambda n: self.all_parts(n, hop))
        every(0, self.pieces, lambda n: self.all_parts(n, near))

    def pass_on(self, n):
        def one(n, part):
            self.hop(n, part).wait_recv()
            self.pairs(n, part).start()
            self.relay(n, part).start()

        self.all_parts(n, one)

    def pass_pair(self, n):
        def one(n, part):
            self.pairs(n, part).wait_recv()
            self.pair_relay(n, part).start()

        self.all_parts(n, one)

    def ready(self, n):
        def one(n, part):
            self.own(n, part).wait()
            for copy in (self.near(n, part), self.relay(n, part), self.pair_relay(n, part)):
                copy.wait_recv()

        self.all_parts(n, one)

    def drain(self):
        def one(n, part):
            for copy in (
                self.hop(n, part), self.pairs(n, part), self.relay(n, part),
                self.pair_relay(n, part), self.near(n, part),
            ):
                copy.wait_send()

        every(0, self.pieces, lambda n: self.all_parts(n, one))


def slot_tables(routes_ref, priority_ref, capacity, pick_ref, back_ref):
    count = routes_ref.shape[1]
    row = lax.broadcasted_iota(jnp.int32, (count, count), 0).astype(jnp.float32)
    col = lax.broadcasted_iota(jnp.int32, (count, count), 1).astype(jnp.float32)
    eye = row == col
    route_row = routes_ref[...].astype(jnp.float32)
    order_row = priority_ref[...].astype(jnp.float32)
    route_col = jnp.sum(jnp.where(eye, route_row, 0.0), axis=1, keepdims=True)
    order_col = jnp.sum(jnp.where(eye, order_row, 0.0), axis=1, keepdims=True)
    same = route_col == route_row
    rank_row = jnp.sum(
        jnp.where(same & (order_col < order_row), 1.0, 0.0), axis=0, keepdims=True
    )
    rank_col = jnp.sum(
        jnp.where(same & (order_row < order_col), 1.0, 0.0), axis=1, keepdims=True
    )
    slots = float(count)
    slot_row = jnp.where(rank_row < capacity, route_row * capacity + rank_row, slots)
    slot_col = jnp.where(rank_col < capacity, route_col * capacity + rank_col, slots)
    pick_ref[...] = jnp.where(slot_row == row, 1.0, 0.0).astype(jnp.bfloat16)
    back_ref[...] = jnp.where(slot_col == col, 1.0, 0.0).astype(jnp.bfloat16)


def norm_stats(value):
    centered = value - jnp.mean(value, axis=1, keepdims=True)
    inverse = lax.rsqrt(jnp.mean(centered * centered, axis=1, keepdims=True) + epsilon)
    return centered * inverse, inverse


def front_kernel(
    dims,
    prefix_ref, routes_ref, priority_ref, tokens_ref, cot_ref, small_hbm, router_hbm, qkv_hbm, out_hbm,
    qkv_out, act_out, merged_out, back_out, weight_out, out_full, low_out, high_out, grads_rows,
    hidden_ref, send_ref, small_out, router_out,
    small, weight, out_w, qkv, act, merged, act_two, turned, pick, back, grads_send, low_buf, high_buf,
    own_sem, disp_send, disp_recv, small_send, small_recv, gat_send, gat_recv, store_sem, prob_sem,
):
    owners, capacity, pieces = dims
    place = Place(owners)
    rows, width = tokens_ref.shape
    shard = qkv_hbm.shape[0]
    gathers = [
        Gather(place, pieces, parts, src, dst, (gat_send.at[i], gat_recv.at[i]))
        for i, (parts, src, dst) in enumerate(((3, qkv_hbm, weight), (1, out_hbm, out_w)))
    ]
    for gather in gathers:
        gather.start_own()
    vectors, gates = small_hbm.shape[0], router_hbm.shape[0]
    small_parts = [
        (small_hbm, small.at[place.w, pl.ds(0, vectors)]),
        (router_hbm, small.at[place.w, pl.ds(vectors, gates)]),
    ]
    own_smalls = [
        pltpu.make_async_copy(src, dst, own_sem.at[3 + i])
        for i, (src, dst) in enumerate(small_parts)
    ]
    for copy in own_smalls:
        copy.start()
    greet(
        [(place.ahead(k), place.w) for k in range(1, owners)]
        + [(place.e, place.sib), (place.e, place.far), (place.e, place.diag)]
    )
    smalls = [
        remote(src, dst, small_send.at[n, i], small_recv.at[n, i], (place.e, peer))
        for i, peer in enumerate((place.sib, place.far, place.diag))
        for n, (src, dst) in enumerate(small_parts)
    ]
    for copy in smalls:
        copy.start()
    for gather in gathers:
        gather.start()
    slot_tables(routes_ref, priority_ref, capacity, pick, back)
    tile = min(256, width)
    shape = grads_send.shape[:3]

    def to_slots(values_ref, slots_ref):
        def one(n):
            cols = span(n * tile, tile)
            value = dot_nn(pick[...], values_ref[:, cols]).astype(jnp.bfloat16)
            slots_ref[:, :, :, cols] = value.reshape(shape + (tile,))

        every(0, width // tile, one)

    to_slots(cot_ref, grads_send)
    dispatch = Dispatch(
        place, capacity, grads_send, grads_rows, (own_sem.at[0], disp_send, disp_recv)
    )
    dispatch.start()
    for copy in own_smalls:
        copy.wait()
    for copy in smalls:
        copy.wait_recv()
    small_out[...] = small[:, :vectors, :]
    router_out[...] = jnp.zeros_like(router_out)
    router_out[:gates, :] = jnp.concatenate(
        [small[i, vectors:, :] for i in range(4)], axis=1
    )

    def vector(which):
        parts = [small[i, which : which + 1, :] for i in range(4)]
        return jnp.concatenate(parts, axis=1).astype(jnp.float32)

    band = min(64, rows)
    gain, shift = vector(0), vector(1)

    def norm_band(i):
        part = span(i * band, band)
        scaled, _ = norm_stats(tokens_ref[part, :].astype(jnp.float32))
        act[part, :] = (scaled * gain + shift).astype(jnp.bfloat16)

    def project(n):
        for part in range(3):
            cols = gathers[0].cols(n, part)
            qkv[:, cols] = dot_nn(act[...], weight[:, cols]).astype(jnp.bfloat16)

    gathers[0].pass_on(0)
    every(0, rows // band, norm_band)
    turned[0] = act[...].T
    stores = [
        pltpu.make_async_copy(src, dst, store_sem.at[i])
        for i, (src, dst) in enumerate(
            [(qkv, qkv_out), (turned.at[0], act_out), (back, back_out), (weight, weight_out),
             (turned.at[1], merged_out), (out_w, out_full)]
        )
    ]
    for store in stores[1:3]:
        store.start()
    half = rows // 2
    pairs = width // LANES

    def keep_probs(i):
        slot = lax.rem(i, 2)
        return (
            pltpu.make_async_copy(
                low_buf.at[slot], low_out.at[pl.ds(2 * i, 2)], prob_sem.at[0, slot]
            ),
            pltpu.make_async_copy(
                high_buf.at[slot], high_out.at[pl.ds(2 * i, 2)], prob_sem.at[1, slot]
            ),
        )

    def attend_pair(i):
        slot = lax.rem(i, 2)

        @pl.when(i >= 2)
        def _():
            for copy in keep_probs(i - 2):
                copy.wait()

        query, key, value = (
            qkv[:, span(part * width + i * LANES, LANES)] for part in range(3)
        )
        tops, bottoms = [], []
        for head in range(2):
            part = slice(head * HEAD_DIM, (head + 1) * HEAD_DIM)
            low, high, top, bottom = attend_head(
                query[:, part], key[:, part], value[:, part], prefix_ref[0]
            )
            low_buf[slot, head] = low
            high_buf[slot, head] = high
            tops.append(top)
            bottoms.append(bottom)
        cols = span(i * LANES, LANES)
        merged[:half, cols] = jnp.concatenate(tops, axis=1).astype(jnp.bfloat16)
        merged[half:, cols] = jnp.concatenate(bottoms, axis=1).astype(jnp.bfloat16)
        for copy in keep_probs(i):
            copy.start()

    group = pairs // pieces
    share = -(-owners // pieces)

    def front_step(n):
        @pl.when(n + 1 < pieces)
        def _():
            gathers[0].pass_on(n + 1)

        gathers[0].pass_pair(n)
        for i, partner in enumerate(dispatch.order()):
            pl.when(n == i // share)(functools.partial(dispatch.forward, partner))
        gathers[0].ready(n)
        project(n)
        pl.when(n >= 2)(lambda: gathers[1].pass_on(n - 2))

        @pl.when(n == pieces - 1)
        def _():
            gathers[1].pass_on(pieces - 2)
            gathers[1].pass_pair(0)

        for i in range(group):
            attend_pair(n * group + i)

    every(0, pieces, front_step)
    gathers[1].pass_on(pieces - 1)
    every(1, pieces, gathers[1].pass_pair)
    turned[1] = merged[...].T
    for i in (0, 3, 4):
        stores[i].start()
    order = dispatch.order()
    dispatch.relay(order[0])
    every(0, pieces, gathers[1].ready)
    stores[5].start()
    gain_two, shift_two = vector(2), vector(3)
    band_two = min(128, rows)

    def middle(i):
        part = span(i * band_two, band_two)
        value = tokens_ref[part, :].astype(jnp.float32) + dot_nn(merged[part, :], out_w[...])
        hidden_ref[part, :] = value
        scaled, _ = norm_stats(value)
        act_two[part, :] = (scaled * gain_two + shift_two).astype(jnp.bfloat16)
        for n, partner in enumerate(order[1 : 1 + bands]):
            pl.when(i == n)(functools.partial(dispatch.relay, partner))

    bands = rows // band_two
    every(0, bands, middle)
    to_slots(act_two, send_ref)
    for partner in order[1 + bands :]:
        dispatch.relay(partner)
    for i in (pairs - 2, pairs - 1):
        for copy in keep_probs(i):
            copy.wait()
    every(0, owners, dispatch.ready)
    for store in stores:
        store.wait()
    for copy in smalls:
        copy.wait_send()
    for gather in gathers:
        gather.drain()
    dispatch.drain()


def run_front(
    owners, experts, capacity, prefix, routes, priority, tokens, cotangent, small, router, w_qkv, w_out
):
    rows, width = tokens.shape
    shard, columns = w_qkv.shape
    half = rows // 2
    heads = width // HEAD_DIM
    pieces = 4
    any_spec = pl.BlockSpec(memory_space=pl.ANY)
    vmem_spec = pl.BlockSpec(memory_space=pltpu.VMEM)
    bf16, f32 = jnp.bfloat16, jnp.float32
    dma = pltpu.SemaphoreType.DMA

    def out(*shape):
        return jax.ShapeDtypeStruct(shape, bf16)

    def vm(*shape):
        return pltpu.VMEM(shape, bf16)

    return pl.pallas_call(
        functools.partial(front_kernel, (owners, capacity, pieces)),
        out_shape=(
            out(rows, columns),
            out(width, rows),
            out(width, rows),
            out(rows, rows),
            out(4 * shard, columns),
            out(4 * shard, width),
            out(heads, half, half),
            out(heads, half, rows),
            out(experts, owners * 4 * capacity, width),
            jax.ShapeDtypeStruct((rows, width), f32),
            out(owners, experts, capacity, width),
            out(4, *small.shape),
            out(LANES, width),
        ),
        in_specs=[pl.BlockSpec(memory_space=pltpu.SMEM)] + [vmem_spec] * 4 + [any_spec] * 4,
        out_specs=(any_spec,) * 9 + (vmem_spec,) * 4,
        scratch_shapes=[
            vm(4, small.shape[0] + router.shape[0], shard),
            vm(4 * shard, columns),
            vm(4 * shard, width),
            vm(rows, columns),
            vm(rows, width),
            vm(rows, width),
            vm(rows, width),
            vm(2, width, rows),
            vm(rows, rows),
            vm(rows, rows),
            vm(owners, experts, capacity, width),
            vm(2, 2, half, half),
            vm(2, 2, half, rows),
            dma((5,)),
            dma((4, owners)),
            dma((4, owners)),
            dma((2, 3)),
            dma((2, 3)),
            dma((2, 6, pieces, 3)),
            dma((2, 6, pieces, 3)),
            dma((6,)),
            dma((2, 2)),
        ],
        compiler_params=pltpu.CompilerParams(
            collective_id=0, has_side_effects=True, vmem_limit_bytes=VMEM_LIMIT
        ),
        name="front",
    )(prefix, routes, priority, tokens, cotangent, small, router, w_qkv, w_out)


class Reduce:
    def __init__(self, place, part, got, far, pair, near, line, done, sems):
        self.p = place
        self.part, self.got, self.far = part, got, far
        self.pair, self.near, self.line, self.done = pair, near, line, done
        self.send, self.recv = sems
        self.chunks = part.shape[0]
        self.halves = done.shape[1] // 2
        self.bit = lax.rem(place.e, 2)
        self.low = lax.rem(lax.div(place.e, 2), 2)
        self.high = lax.div(place.e, 4)

    def step(self, which, n, src, dst, device):
        return remote(src, dst, self.send.at[which, n], self.recv.at[which, n], device)

    def swapped(self, n):
        return self.step(
            0, n, self.part.at[n, :, 1 - self.p.c], self.got.at[n], (self.p.e, self.p.sib)
        )

    def crossed(self, n):
        return self.step(
            1, n, self.part.at[n, 1 - self.p.x, self.p.c], self.far.at[n], (self.p.e, self.p.far)
        )

    def folded(self, n):
        other = span((1 - self.bit) * self.halves, self.halves)
        return self.step(
            2, n, self.part.at[n, self.p.x, self.p.c, other], self.pair.at[n],
            (self.p.pair, self.p.w),
        )

    def shared(self, n):
        part = self.done.at[n, span(self.bit * self.halves, self.halves)]
        return self.step(3, n, part, part, (self.p.pair, self.p.w))

    def quarter(self, low):
        size = self.halves // 2
        return span(self.bit * self.halves + low * size, size)

    def eighth(self, high):
        size = self.halves // 4
        return span(self.bit * self.halves + (self.low * 2 + high) * size, size)

    def nears(self, n):
        return self.step(
            4, n, self.part.at[n, self.p.x, self.p.c, self.quarter(1 - self.low)],
            self.near.at[n], (self.p.flip(2), self.p.w),
        )

    def lines(self, n):
        return self.step(
            5, n, self.part.at[n, self.p.x, self.p.c, self.eighth(1 - self.high)],
            self.line.at[n], (self.p.flip(4), self.p.w),
        )

    def line_back(self, n):
        part = self.done.at[n, self.eighth(self.high)]
        return self.step(6, n, part, part, (self.p.flip(4), self.p.w))

    def near_back(self, n):
        part = self.done.at[n, self.quarter(self.low)]
        return self.step(7, n, part, part, (self.p.flip(2), self.p.w))

    def add(self, n, rows, other):
        total = self.part[n, self.p.x, self.p.c, rows, :].astype(jnp.float32) + other.astype(
            jnp.float32
        )
        return total.astype(jnp.bfloat16)

    def pair_sum(self, n, side):
        return self.part[n, side, self.p.c].astype(jnp.float32) + self.got[n, side].astype(
            jnp.float32
        )

    def swap(self, n):
        self.swapped(n).start()

    def cross(self, n):
        self.swapped(n).wait_recv()
        side = 1 - self.p.x
        self.part[n, side, self.p.c] = self.pair_sum(n, side).astype(jnp.bfloat16)
        self.crossed(n).start()

    def fold(self, n):
        self.crossed(n).wait_recv()
        total = self.pair_sum(n, self.p.x) + self.far[n].astype(jnp.float32)
        self.part[n, self.p.x, self.p.c] = total.astype(jnp.bfloat16)
        self.folded(n).start()

    def spread(self, n):
        self.folded(n).wait_recv()
        own = span(self.bit * self.halves, self.halves)
        self.part[n, self.p.x, self.p.c, own, :] = self.add(n, own, self.pair[n])
        self.nears(n).start()

    def reach(self, n):
        self.nears(n).wait_recv()
        own = self.quarter(self.low)
        self.part[n, self.p.x, self.p.c, own, :] = self.add(n, own, self.near[n])
        self.lines(n).start()

    def collect(self, n):
        self.lines(n).wait_recv()
        own = self.eighth(self.high)
        self.done[n, own, :] = self.add(n, own, self.line[n])
        self.line_back(n).start()

    def widen_back(self, n):
        self.line_back(n).wait_recv()
        self.near_back(n).start()

    def share(self, n):
        self.near_back(n).wait_recv()
        self.shared(n).start()

    def finish(self, n):
        self.shared(n).wait_recv()

    def line_stages(self):
        return (self.spread, self.reach, self.collect, self.widen_back, self.share, self.finish)

    def stages(self):
        return (self.cross, self.fold) + self.line_stages()

    def drain(self):
        def one(n):
            for copy in (
                self.swapped(n), self.crossed(n), self.folded(n), self.shared(n), self.nears(n),
                self.lines(n), self.line_back(n), self.near_back(n),
            ):
                copy.wait_send()

        every(0, self.chunks, one)


class PairFirst(Reduce):
    def folded(self, n):
        other = span((1 - self.bit) * self.halves, self.halves)
        return self.step(
            2, n, self.part.at[n, :, self.p.c, other], self.pair.at[n], (self.p.pair, self.p.w)
        )

    def crossed(self, n):
        own = span(self.bit * self.halves, self.halves)
        return self.step(
            1, n, self.part.at[n, 1 - self.p.x, self.p.c, own], self.far.at[n],
            (self.p.e, self.p.far),
        )

    def fold(self, n):
        self.swapped(n).wait_recv()
        for side in range(2):
            self.part[n, side, self.p.c] = self.pair_sum(n, side).astype(jnp.bfloat16)
        self.folded(n).start()

    def cross(self, n):
        self.folded(n).wait_recv()
        own = span(self.bit * self.halves, self.halves)
        for side in range(2):
            total = self.part[n, side, self.p.c, own, :].astype(jnp.float32) + self.pair[
                n, side
            ].astype(jnp.float32)
            self.part[n, side, self.p.c, own, :] = total.astype(jnp.bfloat16)
        self.crossed(n).start()

    def spread(self, n):
        self.crossed(n).wait_recv()
        own = span(self.bit * self.halves, self.halves)
        self.part[n, self.p.x, self.p.c, own, :] = self.add(n, own, self.far[n])
        self.nears(n).start()

    def stages(self):
        return (self.fold, self.cross) + self.line_stages()


class Small:
    def __init__(self, place, value, part, got, mid, far, total, others, out, sems):
        self.p, self.value, self.part, self.got, self.mid = place, value, part, got, mid
        self.far, self.total, self.others, self.out = far, total, others, out
        self.send, self.recv, self.all_send, self.all_recv = sems

    def swapped(self):
        return remote(
            self.part.at[:, 1 - self.p.c], self.got, self.send.at[0], self.recv.at[0],
            (self.p.e, self.p.sib),
        )

    def crossed(self):
        return remote(
            self.mid, self.far, self.send.at[1], self.recv.at[1], (self.p.e, self.p.far)
        )

    def spreads(self, k):
        return remote(
            self.total, self.others.at[k], self.all_send.at[k], self.all_recv.at[k],
            (self.p.ahead(k), self.p.w),
        )

    def swap(self):
        size = self.part.shape[-1]
        for owner in range(4):
            self.part[owner // 2, owner % 2] = self.value[:, owner * size : (owner + 1) * size]
        self.swapped().start()

    def cross(self):
        self.swapped().wait_recv()
        self.mid[...] = self.part[1 - self.p.x, self.p.c] + self.got[1 - self.p.x]
        self.crossed().start()

    def spread(self):
        self.crossed().wait_recv()
        self.total[...] = self.part[self.p.x, self.p.c] + self.got[self.p.x] + self.far[...]
        for k in range(1, self.p.owners):
            self.spreads(k).start()

    def finish(self):
        total = self.total[...]
        for k in range(1, self.p.owners):
            self.spreads(k).wait_recv()
            total = total + self.others[k]
        vectors_out, gates_out = self.out
        vectors_out[...] = total[: vectors_out.shape[0]]
        gates_out[...] = total[vectors_out.shape[0] :]

    def drain(self):
        self.swapped().wait_send()
        self.crossed().wait_send()
        for k in range(1, self.p.owners):
            self.spreads(k).wait_send()


def norm_back_rows(grad, scaled, inverse, gain):
    weighted = grad * gain
    mean_one = jnp.mean(weighted, axis=1, keepdims=True)
    mean_two = jnp.mean(weighted * scaled, axis=1, keepdims=True)
    return inverse * (weighted - mean_one - scaled * mean_two)


def back_kernel(
    dims,
    home_grad_ref, back_ref, hidden_ref, cot_ref, tokens_ref, vectors_ref, router_ref,
    far_hbm, near_hbm, home_hbm, act_hbm, merged_hbm, qkv_hbm, weight_hbm, out_hbm, low_hbm, high_hbm,
    output_ref, tokens_out, vectors_out, gates_out, qkv_out, out_out,
    near_sums, far_sums, done_rows, home_out,
    act_t, merged_t, qkv, weight, out_w, low_buf, high_buf, attn, grad_merged, grad_act,
    part_q, got_q, far_q, pair_q, near_q, line_q, done_q,
    part_o, got_o, far_o, pair_o, near_o, line_o, done_o,
    small, small_part, small_got, small_mid, small_far, small_sum, small_all,
    load_sem, prob_sem, own_sem, early_sem, cross_send, cross_recv, home_send, home_recv, send_q, recv_q, send_o, recv_o,
    small_send, small_recv, all_send, all_recv, out_sem,
):
    owners, capacity, gates = dims
    grad_qkv = qkv
    place = Place(owners)
    loads = [
        pltpu.make_async_copy(src, dst, load_sem.at[i])
        for i, (src, dst) in enumerate(
            [(merged_hbm, merged_t), (out_hbm, out_w), (qkv_hbm, qkv), (act_hbm, act_t),
             (weight_hbm, weight), (near_hbm, near_sums)]
        )
    ]

    def load_probs(i):
        slot = lax.rem(i, 2)
        return (
            pltpu.make_async_copy(
                low_hbm.at[pl.ds(2 * i, 2)], low_buf.at[slot], prob_sem.at[0, slot]
            ),
            pltpu.make_async_copy(
                high_hbm.at[pl.ds(2 * i, 2)], high_buf.at[slot], prob_sem.at[1, slot]
            ),
        )

    for load in loads:
        load.start()
    for load in load_probs(0):
        load.start()
    greet(
        [(place.ahead(k), place.w) for k in range(1, owners)]
        + [(place.e, place.sib), (place.e, place.far)]
    )
    experts = near_sums.shape[0]
    groups = owners // 2
    late = LateReturn(
        place, capacity, near_sums, None, far_hbm, far_sums, done_rows, home_out,
        (own_sem, cross_send, cross_recv, home_send, home_recv),
    )

    def start_late(j):
        for expert in range(experts):
            late.crossed(j, expert).start()

    every(EARLY_CHUNKS, groups, start_late)

    def early_rows(n):
        row = place.peer(n)
        return pltpu.make_async_copy(home_hbm.at[row], home_out.at[row], early_sem.at[n])

    every(0, 2 * EARLY_CHUNKS, lambda n: early_rows(n).start())
    reduce_o = PairFirst(
        place, part_o, got_o, far_o, pair_o, near_o, line_o, done_o, (send_o, recv_o)
    )
    reduce_q = Reduce(
        place, part_q, got_q, far_q, pair_q, near_q, line_q, done_q, (send_q, recv_q)
    )
    smalls = Small(
        place, small, small_part, small_got, small_mid, small_far, small_sum, small_all, (vectors_out, gates_out),
        (small_send, small_recv, all_send, all_recv),
    )
    rows, width = tokens_ref.shape
    shard = width // 4
    band = min(128, rows)
    lead = small.shape[0]

    def vector(which):
        parts = [vectors_ref[i, which : which + 1, :] for i in range(4)]
        return jnp.concatenate(parts, axis=1).astype(jnp.float32)

    gain_one, gain_two = vector(0), vector(2)
    small[: lead - gates, :] = jnp.zeros((lead - gates, width), jnp.float32)
    small[lead - gates :, :] = router_ref[:gates, :]

    def post(i):
        part = span(i * band, band)
        grad = dot_nn(back_ref[part, :], home_grad_ref.reshape(rows, width)[...])
        scaled, inverse = norm_stats(hidden_ref[part, :])
        value = cot_ref[part, :].astype(jnp.float32) + norm_back_rows(
            grad, scaled, inverse, gain_two
        )
        tokens_out[part, :] = value
        attn[part, :] = value.astype(jnp.bfloat16)
        small[2:3, :] += jnp.sum(grad * scaled, axis=0, keepdims=True)
        small[3:4, :] += jnp.sum(grad, axis=0, keepdims=True)

    every(0, rows // band, post)
    loads[0].wait()

    def weight_grad(part, n, left, right):
        value = dot_nn(left[...], right).astype(jnp.bfloat16)
        part[n] = value.reshape(part.shape[1:])

    tile_o = part_o.shape[-1]
    out_chunks = part_o.shape[0]
    for n in range(out_chunks):
        weight_grad(part_o, n, merged_t, attn[:, n * tile_o : (n + 1) * tile_o])
        reduce_o.swap(n)
    loads[1].wait()

    def merged_band(i):
        part = span(i * band, band)
        grad_merged[part, :] = dot_nt(attn[part, :], out_w[...]).astype(jnp.bfloat16)

    every(0, rows // band, merged_band)
    stages_o, stages_q = reduce_o.stages(), reduce_q.stages()
    for n in range(out_chunks):
        stages_o[0](n)
    for load in loads[2:]:
        load.wait()
    grad_act[...] = jnp.zeros_like(grad_act)
    pairs = part_q.shape[0]

    def attend_pair(i):
        slot = lax.rem(i, 2)
        for load in load_probs(i):
            load.wait()

        @pl.when(i + 1 < pairs)
        def _():
            for load in load_probs(i + 1):
                load.start()

        cols = span(i * LANES, LANES)
        query, key, value = (
            qkv[:, span(part * width + i * LANES, LANES)] for part in range(3)
        )
        grad = grad_merged[:, cols]
        results = []
        for head in range(2):
            part = slice(head * HEAD_DIM, (head + 1) * HEAD_DIM)
            results.append(
                attend_back_head(
                    query[:, part], key[:, part], value[:, part],
                    low_buf[slot, head], high_buf[slot, head], grad[:, part],
                )
            )
        for which in range(3):
            grad_qkv[:, span(which * width + i * LANES, LANES)] = jnp.concatenate(
                [results[0][which], results[1][which]], axis=1
            )
        right = jnp.concatenate(
            [grad_qkv[:, span(which * width + i * LANES, LANES)] for which in range(3)], axis=1
        )
        weight_grad(part_q, i, act_t, right)
        reduce_q.swap(i)
        columns = jnp.concatenate(
            [weight[:, span(which * width + i * LANES, LANES)] for which in range(3)], axis=1
        )
        grad_act[...] += dot_nt(right, columns)

    def input_band(i):
        part = span(i * band, band)
        grad = grad_act[part, :]
        scaled, inverse = norm_stats(tokens_ref[part, :].astype(jnp.float32))
        tokens_out[part, :] += norm_back_rows(grad, scaled, inverse, gain_one)
        small[0:1, :] += jnp.sum(grad * scaled, axis=0, keepdims=True)
        small[1:2, :] += jnp.sum(grad, axis=0, keepdims=True)

    def output_band(i):
        part = span(i * band, band)
        slots = home_out.reshape(rows, width)
        value = hidden_ref[part, :] + dot_nn(back_ref[part, :], slots[...])
        output_ref[part, :] = value.astype(jnp.bfloat16)

    def store_q(i):
        return [
            pltpu.make_async_copy(
                done_q.at[i, :, pl.ds(which * LANES, LANES)],
                qkv_out.at[:, span(which * width + i * LANES, LANES)],
                out_sem.at[which, i],
            )
            for which in range(3)
        ]

    def store_o(n):
        return pltpu.make_async_copy(
            done_o.at[n], out_out.at[:, span(n * tile_o, tile_o)], out_sem.at[3, n]
        )

    delays = (1, 3, 4, 5, 6, 7, 8, 9)
    turns_o = (-1, 3, 5, 6, 7, 8, 9, 10)
    last = len(delays) - 1
    half = rows // band // 2

    def slot_step(slot):
        @pl.when(slot + EARLY_CHUNKS < groups)
        def _():
            for expert in range(experts):
                late.finish(slot + EARLY_CHUNKS, expert)

        pl.when(slot < pairs)(lambda: attend_pair(slot))
        for s in range(last, -1, -1):
            n = slot - delays[s]

            @pl.when((n >= 0) & (n < pairs))
            def _(s=s, n=n):
                stages_q[s](n)
                if s == last:
                    for copy in store_q(n):
                        copy.start()

            @pl.when(slot == turns_o[s])
            def _(s=s):
                for n in range(out_chunks):
                    stages_o[s](n)
                    if s == last:
                        store_o(n).start()

        @pl.when(slot == pairs)
        def _():
            every(0, half, input_band)

        pl.when(slot == pairs + 1)(lambda: every(half, 2 * half, input_band))
        pl.when(slot == pairs + 2)(smalls.swap)
        pl.when(slot == pairs + 3)(smalls.cross)
        pl.when(slot == pairs + 4)(smalls.spread)

        @pl.when(slot == pairs + 3)
        def _():
            late.arrived(EARLY_CHUNKS, groups, experts)
            every(0, 2 * EARLY_CHUNKS, lambda n: early_rows(n).wait())
            every(0, rows // band, output_band)

    every(0, pairs + delays[-1], slot_step)
    smalls.finish()

    def stored(i):
        for copy in store_q(i):
            copy.wait()

    every(0, pairs, stored)
    for n in range(out_chunks):
        store_o(n).wait()
    late.drain(EARLY_CHUNKS, groups, experts)
    reduce_o.drain()
    reduce_q.drain()
    smalls.drain()


def run_back(
    owners, capacity, gates, home_grad, far_sums, near_sums, home_out, back, hidden, cotangent, tokens,
    vectors, router_grad, act_t, merged_t, qkv, weight, w_out, low, high,
):
    rows, width = tokens.shape
    shard = width // 4
    lead = 8 + gates
    groups = owners // 2
    pairs = width // LANES
    tile_o = min(512, width)
    out_chunks = width // tile_o
    half = shard // 2
    mid = rows // 2
    any_spec = pl.BlockSpec(memory_space=pl.ANY)
    vmem_spec = pl.BlockSpec(memory_space=pltpu.VMEM)
    bf16, f32 = jnp.bfloat16, jnp.float32
    dma = pltpu.SemaphoreType.DMA

    def vm(*shape):
        return pltpu.VMEM(shape, bf16)

    def fm(*shape):
        return pltpu.VMEM(shape, f32)

    def reduce_buffers(chunks, tile, pair_first):
        far, pair = ((half,), (2, half)) if pair_first else ((shard,), (half,))
        return [
            vm(chunks, 2, 2, shard, tile),
            vm(chunks, 2, shard, tile),
            vm(chunks, *far, tile),
            vm(chunks, *pair, tile),
            vm(chunks, half // 2, tile),
            vm(chunks, half // 4, tile),
            vm(chunks, shard, tile),
        ]

    def reduce_sems(chunks):
        return [dma((8, chunks)), dma((8, chunks))]

    return pl.pallas_call(
        functools.partial(back_kernel, (owners, capacity, gates)),
        out_shape=(
            jax.ShapeDtypeStruct((rows, width), bf16),
            jax.ShapeDtypeStruct((rows, width), f32),
            jax.ShapeDtypeStruct((8, shard), f32),
            jax.ShapeDtypeStruct((gates, shard), f32),
            jax.ShapeDtypeStruct((shard, 3 * width), bf16),
            jax.ShapeDtypeStruct((shard, width), bf16),
        ),
        in_specs=[vmem_spec] * 7 + [any_spec] * 10,
        out_specs=(vmem_spec,) * 4 + (any_spec,) * 2,
        scratch_shapes=[
            vm(*near_sums.shape),
            vm(*near_sums.shape),
            vm(*home_grad.shape),
            vm(*home_grad.shape),
            vm(width, rows),
            vm(width, rows),
            vm(rows, 3 * width),
            vm(width, 3 * width),
            vm(width, width),
            vm(2, 2, mid, mid),
            vm(2, 2, mid, rows),
            vm(rows, width),
            vm(rows, width),
            fm(rows, width),
        ]
        + reduce_buffers(pairs, 3 * LANES, False)
        + reduce_buffers(out_chunks, tile_o, True)
        + [
            fm(lead, width),
            fm(2, 2, lead, shard),
            fm(2, lead, shard),
            fm(lead, shard),
            fm(lead, shard),
            fm(lead, shard),
            fm(owners, lead, shard),
            dma((6,)),
            dma((2, 2)),
            dma((near_sums.shape[0],)),
            dma((owners,)),
            dma((groups, near_sums.shape[0])),
            dma((groups, near_sums.shape[0])),
            dma((owners, near_sums.shape[0])),
            dma((owners, near_sums.shape[0])),
        ]
        + reduce_sems(pairs)
        + reduce_sems(out_chunks)
        + [dma((2,)), dma((2,)), dma((owners,)), dma((owners,)), dma((4, pairs))],
        compiler_params=pltpu.CompilerParams(
            collective_id=2, has_side_effects=True, vmem_limit_bytes=VMEM_LIMIT
        ),
        name="back",
    )(
        home_grad, back, hidden, cotangent, tokens, vectors, router_grad,
        far_sums, near_sums, home_out, act_t, merged_t, qkv, weight, w_out, low, high,
    )


def widen_kernel(vectors_ref, *refs):
    count = (len(refs) - 4) // 2
    for src, dst in zip(refs[:count], refs[count:]):
        dst[...] = src[...].astype(dst.dtype)
    for i, dst in enumerate(refs[2 * count :]):
        dst[...] = vectors_ref[i, :]


def widen(steps, vectors, values, kinds):
    def spec(value):
        if value.shape[0] % (16 * steps):
            return pl.BlockSpec(value.shape, lambda i: (0, 0))
        return pl.BlockSpec((value.shape[0] // steps, value.shape[1]), lambda i: (i, 0))

    return pl.pallas_call(
        widen_kernel,
        grid=(steps,),
        in_specs=[pl.BlockSpec(vectors.shape, lambda i: (0, 0))]
        + [spec(value) for value in values],
        out_specs=[spec(value) for value in values]
        + [pl.BlockSpec((vectors.shape[1],), lambda i: (0,))] * 4,
        out_shape=[
            jax.ShapeDtypeStruct(value.shape, kind) for value, kind in zip(values, kinds)
        ]
        + [jax.ShapeDtypeStruct((vectors.shape[1],), jnp.float32)] * 4,
        name="widen",
    )(vectors, *values)


def on_device_plain(
    tokens,
    norm1_gain,
    norm1_shift,
    w_qkv,
    w_out,
    norm2_gain,
    norm2_shift,
    w_router,
    w_up,
    w_down,
    routes,
    priority,
    prefix,
    cotangent,
):
    row_count, model_width = tokens.shape
    expert_count = w_router.shape[1]
    capacity = row_count // expert_count
    owners = lax.axis_size("expert")
    local_experts = w_up.shape[0]
    slot_count = expert_count * capacity
    prefix_len = prefix[0]
    small = jnp.concatenate(
        [
            norm1_gain[None],
            norm1_shift[None],
            norm2_gain[None],
            norm2_shift[None],
            w_router.T,
        ],
        axis=0,
    )
    qkv_full = lax.all_gather(w_qkv, "wshard", axis=0, tiled=True)
    small_full = lax.all_gather(small, "wshard", axis=1, tiled=True)
    out_full = lax.all_gather(w_out, "wshard", axis=0, tiled=True)
    gain_one, shift_one, gain_two, shift_two = (small_full[i] for i in range(4))
    router_full = small_full[4:].T
    gain_one = gain_one.astype(jnp.float32)
    gain_two = gain_two.astype(jnp.float32)
    inputs = tokens.astype(jnp.float32)
    normed_one, scaled_one, inverse_one = normalize(inputs, gain_one, shift_one.astype(jnp.float32))
    act_one = normed_one.astype(jnp.bfloat16)
    qkv = jnp.dot(act_one, qkv_full, preferred_element_type=jnp.float32).astype(jnp.bfloat16)
    query_heads = qkv[:, :model_width]
    key_heads = qkv[:, model_width : 2 * model_width]
    value_heads = qkv[:, 2 * model_width :]
    merged, log_totals = attend_forward(query_heads, key_heads, value_heads, prefix_len)
    attn_out = jnp.dot(merged, out_full, preferred_element_type=jnp.float32)
    hidden = inputs + attn_out
    normed_two, scaled_two, inverse_two = normalize(hidden, gain_two, shift_two.astype(jnp.float32))
    act_two = normed_two.astype(jnp.bfloat16)
    logits = jnp.dot(act_two, router_full, preferred_element_type=jnp.float32)
    row_max = jnp.max(logits, axis=-1, keepdims=True)
    exponent = jnp.exp(logits - row_max)
    gate_prob = exponent / jnp.sum(exponent, axis=-1, keepdims=True)
    route_ids = routes[:, 0]
    chosen = route_ids[:, None] == jnp.arange(expert_count, dtype=jnp.int32)[None, :]
    gate_value = jnp.sum(jnp.where(chosen, gate_prob, 0.0), axis=1)
    slot_index, slot_source = assign_slots(route_ids, priority[0], expert_count, capacity)
    zero_row = jnp.zeros((1, model_width), jnp.bfloat16)
    padded = jnp.concatenate([act_two, zero_row], axis=0)
    send_rows = padded[slot_source].reshape(owners, local_experts * capacity, model_width)
    arrived = lax.all_to_all(send_rows, "expert", split_axis=0, concat_axis=0, tiled=True).reshape(
        owners, local_experts, capacity, model_width
    )
    group = lax.axis_size("wshard")
    local_rows = owners * capacity

    def by_expert(chunk):
        rows = jnp.transpose(chunk, (1, 0, 2, 3)).reshape(local_experts, local_rows, model_width)
        return lax.all_gather(rows, "wshard", axis=1, tiled=True)

    def home_rows(rows):
        own = lax.psum_scatter(rows.astype(jnp.bfloat16), "wshard", scatter_dimension=1, tiled=True)
        own = own.reshape(local_experts, owners, capacity, model_width)
        return jnp.transpose(own, (1, 0, 2, 3)).reshape(
            owners, local_experts * capacity, model_width
        )

    grad_output = cotangent.astype(jnp.float32)
    grad_combined = (gate_value[:, None] * grad_output).astype(jnp.bfloat16)
    grad_padded = jnp.concatenate([grad_combined, zero_row], axis=0)
    grad_send = grad_padded[slot_source].reshape(owners, local_experts * capacity, model_width)
    grad_arrived = lax.all_to_all(
        grad_send, "expert", split_axis=0, concat_axis=0, tiled=True
    ).reshape(owners, local_experts, capacity, model_width)
    rows_in = by_expert(arrived)
    grad_rows = by_expert(grad_arrived)
    pre_act = jnp.einsum("erd,edf->erf", rows_in, w_up, preferred_element_type=jnp.float32)
    activated, gelu_pull = jax.vjp(gelu_tanh, pre_act)
    act_hidden = activated.astype(jnp.bfloat16)
    produced = jnp.einsum(
        "erf,efd->erd", act_hidden, w_down, preferred_element_type=jnp.float32
    )
    expert_out = home_rows(produced)
    returned = lax.all_to_all(expert_out, "expert", split_axis=0, concat_axis=0, tiled=True)
    slots_back = jnp.concatenate([returned.reshape(slot_count, model_width), zero_row], axis=0)
    combined = slots_back[slot_index].astype(jnp.float32)
    output = (hidden + gate_value[:, None] * combined).astype(jnp.bfloat16)
    grad_gate = jnp.sum(grad_output * combined, axis=1)
    grad_down = jnp.einsum(
        "erf,erd->efd", act_hidden, grad_rows, preferred_element_type=jnp.float32
    )
    grad_hidden_units = jnp.einsum(
        "erd,efd->erf", grad_rows, w_down, preferred_element_type=jnp.float32
    )
    grad_pre = gelu_pull(grad_hidden_units)[0].astype(jnp.bfloat16)
    grad_up = jnp.einsum("erd,erf->edf", rows_in, grad_pre, preferred_element_type=jnp.float32)
    grad_expert_in = jnp.einsum(
        "erf,edf->erd", grad_pre, w_up, preferred_element_type=jnp.float32
    )
    grad_send_back = home_rows(grad_expert_in)
    grad_back = lax.all_to_all(grad_send_back, "expert", split_axis=0, concat_axis=0, tiled=True)
    grad_slots = jnp.concatenate([grad_back.reshape(slot_count, model_width), zero_row], axis=0)
    grad_act_two = grad_slots[slot_index].astype(jnp.float32)
    grad_logits = (
        gate_prob * (jnp.where(chosen, grad_gate[:, None], 0.0) - (gate_value * grad_gate)[:, None])
    ).astype(jnp.bfloat16)
    grad_router = contract_rows(act_two, grad_logits)
    grad_act_two = grad_act_two + times_transpose(grad_logits, router_full)
    grad_from_two, grad_gain_two, grad_shift_two = norm_back(
        grad_act_two, scaled_two, inverse_two, gain_two
    )
    grad_hidden = grad_output + grad_from_two
    grad_attn = grad_hidden.astype(jnp.bfloat16)
    grad_out_w = contract_rows(merged, grad_attn)
    grad_merged = times_transpose(grad_attn, out_full).astype(jnp.bfloat16)
    grad_qkv = attend_backward(
        query_heads, key_heads, value_heads, grad_merged, log_totals, prefix_len
    )
    grad_qkv_w = contract_rows(act_one, grad_qkv)
    grad_act_one = times_transpose(grad_qkv, qkv_full)
    grad_from_one, grad_gain_one, grad_shift_one = norm_back(
        grad_act_one, scaled_one, inverse_one, gain_one
    )
    grad_tokens = grad_hidden + grad_from_one
    small_grad = jnp.concatenate(
        [
            grad_gain_one[None],
            grad_shift_one[None],
            grad_gain_two[None],
            grad_shift_two[None],
            grad_router.T,
        ],
        axis=0,
    )
    out_share = lax.psum_scatter(
        grad_out_w.astype(jnp.bfloat16), "wshard", scatter_dimension=0, tiled=True
    )
    qkv_share = lax.psum_scatter(
        grad_qkv_w.astype(jnp.bfloat16), "wshard", scatter_dimension=0, tiled=True
    )
    small_share = lax.psum_scatter(small_grad, "wshard", scatter_dimension=1, tiled=True)
    out_total = lax.psum(out_share, "expert").astype(jnp.float32)
    qkv_total = lax.psum(qkv_share, "expert").astype(jnp.float32)
    small_total = lax.psum(small_share, "expert")
    totals = (
        small_total[0],
        small_total[1],
        qkv_total,
        out_total,
        small_total[2],
        small_total[3],
        small_total[4:].T,
    )
    return (
        output,
        grad_tokens,
        totals[0],
        totals[1],
        totals[2],
        totals[3],
        totals[4],
        totals[5],
        totals[6],
        grad_up,
        grad_down,
    )


def on_device(
    tokens,
    norm1_gain,
    norm1_shift,
    w_qkv,
    w_out,
    norm2_gain,
    norm2_shift,
    w_router,
    w_up,
    w_down,
    routes,
    priority,
    prefix,
    cotangent,
):
    row_count, model_width = tokens.shape
    expert_count = w_router.shape[1]
    capacity = row_count // expert_count
    owners = lax.axis_size("expert")
    experts = w_up.shape[0]
    which = lax.broadcasted_iota(jnp.int32, (16, norm1_gain.shape[0]), 0)
    small = jnp.zeros(which.shape, jnp.bfloat16)
    for i, vector in enumerate((norm1_gain, norm1_shift, norm2_gain, norm2_shift)):
        small = jnp.where(which == i, vector[None], small)
    (
        qkv, act_t, merged_t, back, weight, out_full, low, high, grad_rows, hidden, send_rows,
        vectors, router,
    ) = run_front(
        owners, experts, capacity, prefix, routes.reshape(1, row_count), priority, tokens,
        cotangent, small, w_router.T, w_qkv, w_out,
    )
    far_sums, near_sums, home_out, home_grad, grad_up, grad_down, grad_router = run_experts(
        owners, capacity, expert_count, send_rows, grad_rows, w_up, w_down, router
    )
    output, grad_tokens, grad_vectors, grad_gates, grad_qkv, grad_out = run_back(
        owners, capacity, expert_count, home_grad, far_sums, near_sums, home_out, back, hidden, cotangent,
        tokens, vectors, grad_router, act_t, merged_t, qkv, weight, out_full, low, high,
    )
    f32 = jnp.float32
    units = w_up.shape[2]
    (
        output, grad_tokens, grad_gates, grad_qkv, grad_out, grad_up, grad_down, *grad_vectors,
    ) = widen(
        2,
        grad_vectors,
        (
            output, grad_tokens, grad_gates, grad_qkv, grad_out,
            grad_up.reshape(-1, units), grad_down.reshape(-1, model_width),
        ),
        (output.dtype,) + (f32,) * 6,
    )
    return (
        output,
        grad_tokens,
        grad_vectors[0],
        grad_vectors[1],
        grad_qkv,
        grad_out,
        grad_vectors[2],
        grad_vectors[3],
        grad_gates.T,
        grad_up.reshape(w_up.shape),
        grad_down.reshape(w_down.shape),
    )


def solution(mesh):
    placed = (
        P(("expert", "wshard"), None),
        P("wshard"),
        P("wshard"),
        P("wshard", None),
        P("wshard", None),
        P("wshard"),
        P("wshard"),
        P("wshard", None),
        P("expert", None, "wshard"),
        P("expert", "wshard", None),
        P(("expert", "wshard"), None),
        P(("expert", "wshard"), None),
        P(("expert", "wshard")),
        P(("expert", "wshard"), None),
    )
    owners, group = mesh.shape["expert"], mesh.shape["wshard"]

    def body(*args):
        capacity = args[0].shape[0] // args[7].shape[1]
        fits = group == 4 and owners == 8 and capacity % 16 == 0 and args[7].shape[1] % 16 == 0
        return (on_device if fits else on_device_plain)(*args)

    return jax.shard_map(
        body,
        mesh=mesh,
        in_specs=placed,
        out_specs=(
            P(("expert", "wshard"), None),
            P(("expert", "wshard"), None),
            P("wshard"),
            P("wshard"),
            P("wshard", None),
            P("wshard", None),
            P("wshard"),
            P("wshard"),
            P("wshard", None),
            P("expert", None, "wshard"),
            P("expert", "wshard", None),
        ),
        check_vma=False,
    )
```

```python
import functools
import math

import jax
import jax.numpy as jnp
from jax import lax
from jax.experimental import pallas as pl
from jax.experimental.pallas import tpu as pltpu
from jax.sharding import PartitionSpec as P

HEADS = 16
HEAD_DIM = 64


epsilon = 1e-05
VMEM_LIMIT = 66_000_000
TILE = 1024
EARLY_CHUNKS = 1


def normalize(values, gain_vec, shift_vec):
    row_mean = jnp.mean(values, axis=-1, keepdims=True)
    centered = values - row_mean
    inverse = lax.rsqrt(jnp.mean(centered * centered, axis=-1, keepdims=True) + epsilon)
    scaled = centered * inverse
    return (scaled * gain_vec + shift_vec, scaled, inverse)


def norm_back(grad_rows, scaled, inverse, gain_vec):
    weighted = grad_rows * gain_vec
    mean_one = jnp.mean(weighted, axis=-1, keepdims=True)
    mean_two = jnp.mean(weighted * scaled, axis=-1, keepdims=True)
    grad_inputs = inverse * (weighted - mean_one - scaled * mean_two)
    return (grad_inputs, jnp.sum(grad_rows * scaled, axis=0), jnp.sum(grad_rows, axis=0))


def contract_rows(left, right):
    return lax.dot_general(
        left, right, (((0,), (0,)), ((), ())), preferred_element_type=jnp.float32
    )


def times_transpose(left, right):
    return lax.dot_general(
        left, right, (((1,), (1,)), ((), ())), preferred_element_type=jnp.float32
    )


def gelu_tanh(values):
    return jax.nn.gelu(values, approximate=True)


def assign_slots(route_ids, order_ids, expert_count, capacity):
    token_count = route_ids.shape[0]
    same_expert = route_ids[:, None] == route_ids[None, :]
    earlier = order_ids[None, :] < order_ids[:, None]
    rank_ids = jnp.sum((same_expert & earlier).astype(jnp.int32), axis=1)
    is_kept = rank_ids < capacity
    slot_index = jnp.where(is_kept, route_ids * capacity + rank_ids, expert_count * capacity)
    slot_ids = jnp.arange(expert_count * capacity, dtype=jnp.int32)
    match_table = slot_index[None, :] == slot_ids[:, None]
    token_ids = jnp.arange(token_count, dtype=jnp.int32)
    filled = jnp.any(match_table, axis=1)
    picked = jnp.sum(jnp.where(match_table, token_ids[None, :], 0), axis=1)
    slot_source = jnp.where(filled, picked, token_count)
    return (slot_index, slot_source)


def group_heads(values, groups):
    token_count = values.shape[0]
    return jnp.transpose(values.reshape(token_count, groups, -1, HEAD_DIM), (1, 0, 2, 3))


def block_scores(query_block, key_group, block_start, prefix_len):
    block_rows = query_block.shape[0]
    key_count = key_group.shape[0]
    scores = jnp.einsum(
        "qgd,kgd->gqk", query_block, key_group, preferred_element_type=jnp.float32
    ) * (1.0 / math.sqrt(HEAD_DIM))
    query_pos = block_start + jnp.arange(block_rows, dtype=jnp.int32)
    key_pos = jnp.arange(key_count, dtype=jnp.int32)
    allowed = (key_pos[None, :] <= query_pos[:, None]) | (key_pos[None, :] < prefix_len)
    return jnp.where(allowed[None], scores, -1e30)


def attend_forward(query_heads, key_heads, value_heads, prefix_len):
    token_count = query_heads.shape[0]
    group_size = min(4, HEADS)
    groups = HEADS // group_size
    block_rows = min(512, token_count)
    blocks = token_count // block_rows
    starts = jnp.arange(blocks, dtype=jnp.int32) * block_rows

    def one_group(group_item):
        query_group, key_group, value_group = group_item
        query_blocks = query_group.reshape(blocks, block_rows, group_size, HEAD_DIM)

        def one_block(block_item):
            query_block, block_start = block_item
            scores = block_scores(query_block, key_group, block_start, prefix_len)
            row_max = jnp.max(scores, axis=-1, keepdims=True)
            exponent = jnp.exp(scores - row_max)
            row_total = jnp.sum(exponent, axis=-1, keepdims=True)
            attn_probs = (exponent / row_total).astype(jnp.bfloat16)
            result = jnp.einsum(
                "gqk,kgd->qgd", attn_probs, value_group, preferred_element_type=jnp.float32
            )
            return (result, (row_max + jnp.log(row_total))[..., 0])

        return lax.map(one_block, (query_blocks, starts))

    attended, log_totals = lax.map(
        one_group,
        (
            group_heads(query_heads, groups),
            group_heads(key_heads, groups),
            group_heads(value_heads, groups),
        ),
    )
    merged = (
        jnp.transpose(attended, (1, 2, 0, 3, 4))
        .reshape(token_count, HEADS * HEAD_DIM)
        .astype(jnp.bfloat16)
    )
    return (merged, log_totals)


def attend_backward(query_heads, key_heads, value_heads, grad_merged, log_totals, prefix_len):
    token_count = query_heads.shape[0]
    group_size = min(4, HEADS)
    groups = HEADS // group_size
    block_rows = min(512, token_count)
    blocks = token_count // block_rows
    starts = jnp.arange(blocks, dtype=jnp.int32) * block_rows
    score_scale = 1.0 / math.sqrt(HEAD_DIM)

    def one_group(group_item):
        query_group, key_group, value_group, grad_group, total_group = group_item
        query_blocks = query_group.reshape(blocks, block_rows, group_size, HEAD_DIM)
        grad_blocks = grad_group.reshape(blocks, block_rows, group_size, HEAD_DIM)

        def one_block(carry, block_item):
            grad_keys, grad_vals = carry
            query_block, grad_block, total_block, block_start = block_item
            scores = block_scores(query_block, key_group, block_start, prefix_len)
            attn_probs = jnp.exp(scores - total_block[..., None])
            grad_probs = jnp.einsum(
                "qgd,kgd->gqk", grad_block, value_group, preferred_element_type=jnp.float32
            )
            row_delta = jnp.sum(attn_probs * grad_probs, axis=-1, keepdims=True)
            grad_scores = (attn_probs * (grad_probs - row_delta)).astype(jnp.bfloat16)
            grad_vals = grad_vals + jnp.einsum(
                "gqk,qgd->kgd",
                attn_probs.astype(jnp.bfloat16),
                grad_block,
                preferred_element_type=jnp.float32,
            )
            grad_keys = (
                grad_keys
                + jnp.einsum(
                    "gqk,qgd->kgd", grad_scores, query_block, preferred_element_type=jnp.float32
                )
                * score_scale
            )
            grad_query = (
                jnp.einsum(
                    "gqk,kgd->qgd", grad_scores, key_group, preferred_element_type=jnp.float32
                )
                * score_scale
            )
            return ((grad_keys, grad_vals), grad_query)

        zero_keys = jnp.zeros(key_group.shape, jnp.float32)
        carried, grad_queries = lax.scan(
            one_block, (zero_keys, zero_keys), (query_blocks, grad_blocks, total_group, starts)
        )
        return (grad_queries, carried[0], carried[1])

    grad_queries, grad_keys, grad_vals = lax.map(
        one_group,
        (
            group_heads(query_heads, groups),
            group_heads(key_heads, groups),
            group_heads(value_heads, groups),
            group_heads(grad_merged, groups),
            log_totals,
        ),
    )
    query_part = jnp.transpose(grad_queries, (1, 2, 0, 3, 4)).reshape(token_count, HEADS * HEAD_DIM)
    key_part = jnp.transpose(grad_keys, (1, 0, 2, 3)).reshape(token_count, HEADS * HEAD_DIM)
    value_part = jnp.transpose(grad_vals, (1, 0, 2, 3)).reshape(token_count, HEADS * HEAD_DIM)
    return jnp.concatenate([query_part, key_part, value_part], axis=1).astype(jnp.bfloat16)


MESH = pl.DeviceIdType.MESH
LANES = 128


def dot_nn(left, right):
    return lax.dot_general(
        left, right, (((1,), (0,)), ((), ())), preferred_element_type=jnp.float32
    )


def dot_nt(left, right):
    return lax.dot_general(
        left, right, (((1,), (1,)), ((), ())), preferred_element_type=jnp.float32
    )


def dot_tn(left, right):
    return lax.dot_general(
        left, right, (((0,), (0,)), ((), ())), preferred_element_type=jnp.float32
    )


def span(start, size):
    return pl.ds(pl.multiple_of(start, size), size)


def every(start, stop, step):
    def body(i, carry):
        step(i)
        return carry

    lax.fori_loop(start, stop, body, 0)


class Place:
    def __init__(self, owners):
        self.owners = owners
        self.e = lax.axis_index("expert")
        self.w = lax.axis_index("wshard")
        self.c = lax.rem(self.w, 2)
        self.x = lax.div(self.w, 2)
        self.sib = self.w + 1 - 2 * self.c
        self.far = lax.rem(self.w + 2, 4)
        self.diag = 3 - self.w
        self.pair = self.e + 1 - 2 * lax.rem(self.e, 2)

    def ahead(self, k):
        return lax.rem(self.e + k, self.owners)

    def flip(self, bit):
        return self.e + bit * (1 - 2 * lax.rem(lax.div(self.e, bit), 2))

    def peer(self, n):
        other = lax.div(n, 2) + lax.rem(n, 2) * (self.owners // 2)
        result, bit = 0, 1
        while bit < self.owners:
            result = result + bit * lax.rem(lax.div(self.e, bit) + lax.div(other, bit), 2)
            bit *= 2
        return result


def remote(src, dst, send, recv, device):
    return pltpu.make_async_remote_copy(
        src_ref=src,
        dst_ref=dst,
        send_sem=send,
        recv_sem=recv,
        device_id=device,
        device_id_type=MESH,
    )


def greet(peers):
    barrier = pltpu.get_barrier_semaphore()
    for peer in peers:
        pl.semaphore_signal(barrier, inc=1, device_id=peer, device_id_type=MESH)
    pl.semaphore_wait(barrier, len(peers))


def either(test, yes, no):
    pl.when(test)(yes)
    pl.when(jnp.logical_not(test))(no)


class Dispatch:
    def __init__(self, place, capacity, send_ref, rows_ref, sems):
        self.p, self.cap, self.src, self.rows = place, capacity, send_ref, rows_ref
        self.own_sem, self.send, self.recv = sems

    def slice(self, k, core, side):
        start = (((lax.div(k, 2) * 2 + core) * 2 + side) * 2 + lax.rem(k, 2)) * self.cap
        return self.rows.at[:, span(start, self.cap)]

    def own(self):
        return pltpu.make_async_copy(
            self.src.at[self.p.e], self.slice(0, self.p.c, self.p.x), self.own_sem
        )

    def direct(self, k):
        return remote(
            self.src.at[self.p.peer(k)],
            self.slice(k, self.p.c, self.p.x),
            self.send.at[0, k],
            self.recv.at[0, k],
            (self.p.peer(k), self.p.w),
        )

    def hop(self, k, side, which, peer):
        part = self.slice(k, self.p.c, side)
        return remote(
            part, part, self.send.at[which, k], self.recv.at[which, k], (self.p.e, peer)
        )

    def to_sib(self, k):
        return self.hop(k, self.p.x, 1, self.p.sib)

    def to_far(self, k):
        return self.hop(k, self.p.x, 2, self.p.far)

    def relayed(self, k):
        return self.hop(k, 1 - self.p.x, 3, self.p.sib)

    def start(self):
        self.own().start()
        every(1, self.p.owners, lambda k: self.direct(k).start())

    def forward(self, k):
        k = jnp.int32(k)

        @pl.when(k == 0)
        def _():
            self.own().wait()

        @pl.when(k > 0)
        def _():
            self.direct(k).wait_recv()

        self.to_far(k).start()
        self.to_sib(k).start()

    def relay(self, k):
        self.to_far(k).wait_recv()
        self.relayed(k).start()

    def ready(self, k):
        self.to_sib(k).wait_recv()
        self.relayed(k).wait_recv()

    def order(self):
        return (0, 2, 4, 1, 6, 3, 5, 7)

    def drain(self):
        every(1, self.p.owners, lambda k: self.direct(k).wait_send())

        def rest(k):
            self.to_sib(k).wait_send()
            self.to_far(k).wait_send()
            self.relayed(k).wait_send()

        every(0, self.p.owners, rest)


class Return:
    def __init__(self, place, capacity, part, got, mid, far, done, home, sems):
        self.p, self.cap = place, capacity
        self.part, self.got, self.mid, self.far, self.done, self.home = (
            part, got, mid, far, done, home,
        )
        self.own_sem, self.send, self.recv, self.home_send, self.home_recv = sems

    def swapped(self, j, expert):
        size = 4 * self.cap
        return remote(
            self.part.at[expert, span((j * 2 + 1 - self.p.c) * size, size)],
            self.got.at[expert, span(j * size, size)],
            self.send.at[0, j, expert],
            self.recv.at[0, j, expert],
            (self.p.e, self.p.sib),
        )

    def crossed(self, j, expert):
        part = span(j * 2 * self.cap, 2 * self.cap)
        return remote(
            self.mid.at[expert, part],
            self.far.at[expert, part],
            self.send.at[1, j, expert],
            self.recv.at[1, j, expert],
            (self.p.e, self.p.far),
        )

    def own(self, expert):
        return pltpu.make_async_copy(
            self.done.at[0, expert], self.home.at[self.p.e, expert], self.own_sem.at[expert]
        )

    def homed(self, n, expert):
        return remote(
            self.done.at[n, expert],
            self.home.at[self.p.e, expert],
            self.home_send.at[n, expert],
            self.home_recv.at[n, expert],
            (self.p.peer(n), self.p.w),
        )

    def pair_sum(self, j, expert, side):
        size = 2 * self.cap
        mine = self.part[expert, span(((j * 2 + self.p.c) * 2 + side) * size, size), :]
        theirs = self.got[expert, span((j * 2 + side) * size, size), :]
        return mine.astype(jnp.float32) + theirs.astype(jnp.float32)

    def swap(self, j, expert):
        self.swapped(j, expert).start()

    def split(self, j, expert):
        self.swapped(j, expert).wait_recv()
        here = span(j * 2 * self.cap, 2 * self.cap)
        self.mid[expert, here, :] = self.pair_sum(j, expert, 1 - self.p.x).astype(jnp.bfloat16)
        self.keep[expert, here, :] = self.pair_sum(j, expert, self.p.x).astype(jnp.bfloat16)

    def cross(self, j, expert):
        self.swapped(j, expert).wait_recv()
        here = span(j * 2 * self.cap, 2 * self.cap)
        self.mid[expert, here, :] = self.pair_sum(j, expert, 1 - self.p.x).astype(jnp.bfloat16)
        self.crossed(j, expert).start()

    def this_side(self, j, expert):
        return self.pair_sum(j, expert, self.p.x)

    def finish(self, j, expert):
        self.crossed(j, expert).wait_recv()
        here = span(j * 2 * self.cap, 2 * self.cap)
        total = self.this_side(j, expert) + self.far[expert, here, :].astype(jnp.float32)
        total = total.astype(jnp.bfloat16)
        self.done[2 * j, expert] = total[: self.cap]
        self.done[2 * j + 1, expert] = total[self.cap :]
        j = jnp.int32(j)
        self.homed(2 * j + 1, expert).start()
        either(
            j == 0,
            lambda: self.own(expert).start(),
            lambda: self.homed(2 * j, expert).start(),
        )

    def drain_swaps(self, chunks, experts):
        for expert in range(experts):
            every(0, chunks, lambda j: self.swapped(j, expert).wait_send())

    def drain(self, first, last, experts):
        for expert in range(experts):
            every(first, last, lambda j: self.crossed(j, expert).wait_send())
            every(
                max(1, 2 * first), 2 * last, lambda n: self.homed(n, expert).wait_send()
            )

    def arrived(self, first, last, experts):
        for expert in range(experts):
            if first == 0 and last > 0:
                self.own(expert).wait()
            every(
                max(1, 2 * first), 2 * last, lambda n: self.homed(n, expert).wait_recv()
            )


class LateReturn(Return):
    def crossed(self, j, expert):
        part = span(j * 2 * self.cap, 2 * self.cap)
        return remote(
            self.mid.at[expert, part],
            self.far.at[expert, part],
            self.send.at[j, expert],
            self.recv.at[j, expert],
            (self.p.e, self.p.far),
        )

    def this_side(self, j, expert):
        here = span(j * 2 * self.cap, 2 * self.cap)
        return self.part[expert, here, :].astype(jnp.float32)


def gelu_pair(v):
    root = math.sqrt(2.0 / math.pi)
    square = v * v
    t = jnp.tanh(v * (root + (root * 0.044715) * square))
    half = 0.5 + 0.5 * t
    slope = half + (half * (1.0 - t)) * (v * (root + (3.0 * root * 0.044715) * square))
    return v * half, slope


def expert_kernel(
    dims,
    send_ref, grads_hbm, up_hbm, down_hbm, router_ref,
    far_sums, near_sums, home_out, home_grad, up_out, down_out, router_grad,
    rows, grads, scaled, hidden, pre, up, down, grad_up, grad_down,
    part_out, part_grad, got_out, got_grad, mid_out, mid_grad,
    keep_out, far_grad, far_out, done_grad, done_out,
    load_sem, own_sem, disp_send, disp_recv, red_send, red_recv, home_send, home_recv,
):
    owners, experts, capacity, width, units, expert_count = dims
    place = Place(owners)
    loads = [
        pltpu.make_async_copy(src, dst, load_sem.at[i])
        for i, (src, dst) in enumerate(
            [(up_hbm, up), (grads_hbm, grads), (down_hbm, down)]
        )
    ]
    for load in loads:
        load.start()
    greet(
        [(place.ahead(k), place.w) for k in range(1, owners)]
        + [(place.e, place.sib), (place.e, place.far)]
    )
    dispatch = Dispatch(
        place, capacity, send_ref, rows, (own_sem.at[0, 0], disp_send, disp_recv)
    )
    ret_grad = Return(
        place, capacity, part_grad, got_grad, mid_grad, far_grad, done_grad, home_grad,
        (own_sem.at[1], red_send.at[0], red_recv.at[0], home_send.at[0], home_recv.at[0]),
    )
    ret_out = Return(
        place, capacity, part_out, got_out, mid_out, far_out, done_out, home_out,
        (own_sem.at[2], red_send.at[1], red_recv.at[1], home_send.at[1], home_recv.at[1]),
    )
    dispatch.start()
    router_grad[...] = jnp.zeros_like(router_grad)
    tile = min(TILE, units)
    wide = min(TILE, width)
    chunks = owners // 2
    early = EARLY_CHUNKS
    size = 8 * capacity
    lane = lax.broadcasted_iota(jnp.int32, (size, LANES), 1)

    def compute(j, expert):
        here = span(j * size, size)
        logits = dot_nt(rows[expert, here, :], router_ref[...])
        logits = jnp.where(lane < expert_count, logits, -1e30)
        exponent = jnp.exp(logits - jnp.max(logits, axis=1, keepdims=True))
        prob = exponent * (1.0 / jnp.sum(exponent, axis=1, keepdims=True))
        mine = lane == place.e * experts + expert
        gate = jnp.sum(jnp.where(mine, prob, 0.0), axis=1, keepdims=True)
        scaled[expert, here, :] = (
            gate * grads[expert, here, :].astype(jnp.float32)
        ).astype(jnp.bfloat16)

        def one_tile(n):
            cols = span(n * tile, tile)
            value, slope = gelu_pair(dot_nn(rows[expert, here, :], up[expert, :, cols]))
            hidden[expert, here, cols] = value.astype(jnp.bfloat16)
            back = pre[expert, here, cols].astype(jnp.float32)
            pre[expert, here, cols] = (gate * back * slope).astype(jnp.bfloat16)

        every(0, units // tile, one_tile)

        def one_out(n, total):
            cols = span(n * wide, wide)
            value = dot_nn(hidden[expert, here, :], down[expert, :, cols])
            part_out[expert, here, cols] = (gate * value).astype(jnp.bfloat16)
            weighted = value * grads[expert, here, cols].astype(jnp.float32)
            for start in range(0, wide, LANES):
                total = total + weighted[:, start : start + LANES]
            return total

        total = lax.fori_loop(
            0, width // wide, one_out, jnp.zeros((size, LANES), jnp.float32)
        )
        grad_gate = jnp.sum(total, axis=1, keepdims=True)
        grad_logits = (
            prob * ((jnp.where(mine, 1.0, 0.0) - gate) * grad_gate)
        ).astype(jnp.bfloat16)

        def one_in(n):
            cols = span(n * wide, wide)
            value = dot_nt(pre[expert, here, :], up[expert, cols, :]) + dot_nn(
                grad_logits, router_ref[:, cols]
            )
            part_grad[expert, here, cols] = value.astype(jnp.bfloat16)
            router_grad[:, cols] += dot_tn(grad_logits, rows[expert, here, cols])

        every(0, width // wide, one_in)

    def unscaled(j, expert):
        here = span(j * size, size)
        pre[expert, here, :] = dot_nt(grads[expert, here, :], down[expert]).astype(jnp.bfloat16)

    block = min(256, width)

    def weight_grads(expert, first, last):
        def one(n):
            part = span(n * block, block)
            grad_down[expert, part, :] = dot_tn(
                hidden[expert, :, part], scaled[expert]
            ).astype(jnp.bfloat16)
            grad_up[expert, part, :] = dot_tn(rows[expert, :, part], pre[expert]).astype(
                jnp.bfloat16
            )

        every(first * width // block // 4, last * width // block // 4, one)

    def keep(expert):
        return [
            pltpu.make_async_copy(src.at[expert], dst.at[expert], load_sem.at[2 * expert + i])
            for i, (src, dst) in enumerate(((grad_up, up_out), (grad_down, down_out)))
        ]

    turns = [(j, expert) for j in range(chunks) for expert in range(experts)]
    ahead, through, here = dispatch.forward, dispatch.relay, dispatch.ready
    plan = [[] for _ in turns]
    for unit, acts in (
        (0, ((here, 0), (here, 1), (ahead, 5))),
        (1, ((through, 6), (ahead, 7))),
        (2, ((through, 3), (here, 2), (here, 3))),
        (3, ((through, 5),)),
        (4, ((through, 7), (here, 4), (here, 5))),
        (6, ((here, 6), (here, 7))),
    ):
        plan[unit].extend(acts)
    for u in range(2, len(turns)):
        done = turns[u - 2]
        plan[u].append((ret_grad.cross,) + done)
        plan[u].append((ret_out.cross if done[0] < early else ret_out.split,) + done)
        if u >= 4:
            done = turns[u - 4]
            plan[u].append((ret_grad.finish,) + done)
            if done[0] < early:
                plan[u].append((ret_out.finish,) + done)
    ret_out.keep = keep_out
    for load in loads:
        load.wait()

    def unscaled_pair(j):
        for expert in range(experts):
            unscaled(j, expert)

    ahead(0)
    unscaled_pair(0)
    unscaled_pair(1)
    ahead(2)
    ahead(4)
    ahead(1)
    unscaled_pair(2)
    through(0)
    unscaled_pair(3)
    through(2)
    ahead(6)
    through(4)
    through(1)
    ahead(3)

    def step(unit):
        for u, acts in enumerate(plan):

            @pl.when(unit == u)
            def _(acts=acts):
                for act, *at in acts:
                    act(*at)

        j, expert = lax.div(unit, experts), lax.rem(unit, experts)
        compute(j, expert)
        ret_grad.swap(j, expert)
        ret_out.swap(j, expert)

    every(0, len(turns), step)
    ret_grad.cross(*turns[-2])
    ret_out.split(*turns[-2])
    ret_grad.finish(*turns[-4])
    weight_grads(0, 0, 1)
    ret_grad.cross(*turns[-1])
    ret_out.split(*turns[-1])
    sums = [
        pltpu.make_async_copy(src, dst, load_sem.at[4 + i])
        for i, (src, dst) in enumerate(((mid_out, far_sums), (keep_out, near_sums)))
    ]
    for store in sums:
        store.start()
    ret_grad.finish(*turns[-3])
    weight_grads(0, 1, 2)
    ret_grad.finish(*turns[-2])
    weight_grads(0, 2, 3)
    ret_grad.finish(*turns[-1])
    weight_grads(0, 3, 4)
    for store in keep(0):
        store.start()
    for expert in range(1, experts):
        weight_grads(expert, 0, 4)
        for store in keep(expert):
            store.start()
    for expert in range(experts):
        for store in keep(expert):
            store.wait()
    for store in sums:
        store.wait()
    dispatch.drain()
    ret_grad.drain_swaps(chunks, experts)
    ret_grad.drain(0, chunks, experts)
    ret_grad.arrived(0, chunks, experts)
    ret_out.drain_swaps(chunks, experts)
    ret_out.drain(0, early, experts)
    ret_out.arrived(0, early, experts)


def run_experts(owners, capacity, expert_count, send_rows, grads, w_up, w_down, router):
    experts, width, units = w_up.shape
    slots = owners * 4 * capacity
    chunks = owners // 2
    dims = (owners, experts, capacity, width, units, expert_count)
    any_spec = pl.BlockSpec(memory_space=pl.ANY)
    vmem_spec = pl.BlockSpec(memory_space=pltpu.VMEM)
    bf16 = jnp.bfloat16
    home = jax.ShapeDtypeStruct((owners, experts, capacity, width), bf16)
    dma = pltpu.SemaphoreType.DMA

    def vm(*shape):
        return pltpu.VMEM(shape, bf16)

    return pl.pallas_call(
        functools.partial(expert_kernel, dims),
        out_shape=(
            jax.ShapeDtypeStruct((experts, slots // 4, width), bf16),
            jax.ShapeDtypeStruct((experts, slots // 4, width), bf16),
            home, home,
            jax.ShapeDtypeStruct(w_up.shape, bf16),
            jax.ShapeDtypeStruct(w_down.shape, bf16),
            jax.ShapeDtypeStruct((LANES, width), jnp.float32),
        ),
        in_specs=[any_spec] * 4 + [vmem_spec],
        out_specs=(any_spec,) * 6 + (vmem_spec,),
        scratch_shapes=[
            vm(experts, slots, width),
            vm(experts, slots, width),
            vm(experts, slots, width),
            vm(experts, slots, units),
            vm(experts, slots, units),
            vm(experts, width, units),
            vm(experts, units, width),
            vm(experts, width, units),
            vm(experts, units, width),
            vm(experts, slots, width),
            vm(experts, slots, width),
            vm(experts, slots // 2, width),
            vm(experts, slots // 2, width),
            vm(experts, slots // 4, width),
            vm(experts, slots // 4, width),
            vm(experts, slots // 4, width),
            vm(experts, slots // 4, width),
            vm(experts, slots // 4, width),
            vm(owners, experts, capacity, width),
            vm(owners, experts, capacity, width),
            dma((6,)),
            dma((3, experts)),
            dma((4, owners)),
            dma((4, owners)),
            dma((2, 2, chunks, experts)),
            dma((2, 2, chunks, experts)),
            dma((2, owners, experts)),
            dma((2, owners, experts)),
        ],
        compiler_params=pltpu.CompilerParams(
            collective_id=1, has_side_effects=True, vmem_limit_bytes=VMEM_LIMIT
        ),
        name="experts",
    )(send_rows, grads, w_up, w_down, router)


def masked_softmax(scores):
    exponent = jnp.exp(scores - jnp.max(scores, axis=1, keepdims=True))
    return exponent * (1.0 / jnp.sum(exponent, axis=1, keepdims=True))


def attend_head(query, key, value, prefix_len):
    half = query.shape[0] // 2
    query = query * (1.0 / math.sqrt(HEAD_DIM))
    row = lax.broadcasted_iota(jnp.int32, (half, half), 0)
    col = lax.broadcasted_iota(jnp.int32, (half, half), 1)
    low = dot_nt(query[:half], key[:half])
    low = jnp.where((col <= row) | (col < prefix_len), low, -1e30)
    low = masked_softmax(low).astype(jnp.bfloat16)
    high = dot_nt(query[half:], key)
    high = jnp.concatenate(
        [high[:, :half], jnp.where(col <= row, high[:, half:], -1e30)], axis=1
    )
    high = masked_softmax(high).astype(jnp.bfloat16)
    return low, high, dot_nn(low, value[:half]), dot_nn(high, value)


def score_grads(probs, grad_probs):
    probs = probs.astype(jnp.float32)
    weighted = probs * grad_probs
    total = jnp.sum(weighted, axis=1, keepdims=True)
    return (weighted - probs * total).astype(jnp.bfloat16)


def attend_back_head(query, key, value, low, high, grad):
    half = query.shape[0] // 2
    scale = 1.0 / math.sqrt(HEAD_DIM)
    query = query * scale
    grad_low = score_grads(low, dot_nt(grad[:half], value[:half]))
    grad_high = score_grads(high, dot_nt(grad[half:], value))
    grad_query = jnp.concatenate(
        [dot_nn(grad_low, key[:half]), dot_nn(grad_high, key)], axis=0
    )
    value_all = dot_tn(high, grad[half:])
    key_all = dot_tn(grad_high, query[half:])
    grad_value = jnp.concatenate(
        [value_all[:half] + dot_tn(low, grad[:half]), value_all[half:]], axis=0
    )
    grad_key = jnp.concatenate(
        [key_all[:half] + dot_tn(grad_low, query[:half]), key_all[half:]], axis=0
    )
    return (
        (grad_query * scale).astype(jnp.bfloat16),
        grad_key.astype(jnp.bfloat16),
        grad_value.astype(jnp.bfloat16),
    )


class Gather:
    def __init__(self, place, pieces, parts, src, dst, sems):
        self.p, self.src, self.dst, self.pieces, self.parts = place, src, dst, pieces, parts
        self.send, self.recv = sems
        self.shard = src.shape[0]
        self.half = self.shard // 2
        self.width = src.shape[1] // parts
        self.step = self.width // pieces
        self.first = lax.rem(place.e, 2) * self.half
        self.second = self.half - self.first

    def cols(self, n, part):
        return span(part * self.width + n * self.step, self.step)

    def block(self, owner, start, size, n, part):
        rows = pl.ds(pl.multiple_of(owner * self.shard + start, self.half), size)
        return self.dst.at[rows, self.cols(n, part)]

    def move(self, which, n, part, src, dst, device):
        return remote(
            src, dst, self.send.at[which, n, part], self.recv.at[which, n, part], device
        )

    def own(self, n, part):
        return pltpu.make_async_copy(
            self.src.at[:, self.cols(n, part)],
            self.block(self.p.w, 0, self.shard, n, part),
            self.recv.at[5, n, part],
        )

    def near(self, n, part):
        return self.move(
            4, n, part, self.src.at[:, self.cols(n, part)],
            self.block(self.p.w, 0, self.shard, n, part), (self.p.e, self.p.sib),
        )

    def hop(self, n, part):
        return self.move(
            0, n, part, self.src.at[span(self.first, self.half), self.cols(n, part)],
            self.block(self.p.w, self.first, self.half, n, part), (self.p.e, self.p.far),
        )

    def pass_from(self, which, start, n, part, device):
        block = self.block(self.p.far, start, self.half, n, part)
        return self.move(which, n, part, block, block, device)

    def pairs(self, n, part):
        return self.pass_from(1, self.first, n, part, (self.p.pair, self.p.w))

    def relay(self, n, part):
        return self.pass_from(2, self.first, n, part, (self.p.e, self.p.sib))

    def pair_relay(self, n, part):
        return self.pass_from(3, self.second, n, part, (self.p.e, self.p.sib))

    def all_parts(self, n, act):
        for part in range(self.parts):
            act(n, part)

    def start_own(self):
        every(
            0, self.pieces, lambda n: self.all_parts(n, lambda n, part: self.own(n, part).start())
        )

    def start(self):
        def hop(n, part):
            self.hop(n, part).start()

        def near(n, part):
            self.near(n, part).start()

        every(0, self.pieces, lambda n: self.all_parts(n, hop))
        every(0, self.pieces, lambda n: self.all_parts(n, near))

    def pass_on(self, n):
        def one(n, part):
            self.hop(n, part).wait_recv()
            self.pairs(n, part).start()
            self.relay(n, part).start()

        self.all_parts(n, one)

    def pass_pair(self, n):
        def one(n, part):
            self.pairs(n, part).wait_recv()
            self.pair_relay(n, part).start()

        self.all_parts(n, one)

    def ready(self, n):
        def one(n, part):
            self.own(n, part).wait()
            for copy in (self.near(n, part), self.relay(n, part), self.pair_relay(n, part)):
                copy.wait_recv()

        self.all_parts(n, one)

    def drain(self):
        def one(n, part):
            for copy in (
                self.hop(n, part), self.pairs(n, part), self.relay(n, part),
                self.pair_relay(n, part), self.near(n, part),
            ):
                copy.wait_send()

        every(0, self.pieces, lambda n: self.all_parts(n, one))


def slot_tables(routes_ref, priority_ref, capacity, pick_ref, back_ref):
    count = routes_ref.shape[1]
    row = lax.broadcasted_iota(jnp.int32, (count, count), 0).astype(jnp.float32)
    col = lax.broadcasted_iota(jnp.int32, (count, count), 1).astype(jnp.float32)
    eye = row == col
    route_row = routes_ref[...].astype(jnp.float32)
    order_row = priority_ref[...].astype(jnp.float32)
    route_col = jnp.sum(jnp.where(eye, route_row, 0.0), axis=1, keepdims=True)
    order_col = jnp.sum(jnp.where(eye, order_row, 0.0), axis=1, keepdims=True)
    same = route_col == route_row
    rank_row = jnp.sum(
        jnp.where(same & (order_col < order_row), 1.0, 0.0), axis=0, keepdims=True
    )
    rank_col = jnp.sum(
        jnp.where(same & (order_row < order_col), 1.0, 0.0), axis=1, keepdims=True
    )
    slots = float(count)
    slot_row = jnp.where(rank_row < capacity, route_row * capacity + rank_row, slots)
    slot_col = jnp.where(rank_col < capacity, route_col * capacity + rank_col, slots)
    pick_ref[...] = jnp.where(slot_row == row, 1.0, 0.0).astype(jnp.bfloat16)
    back_ref[...] = jnp.where(slot_col == col, 1.0, 0.0).astype(jnp.bfloat16)


def norm_stats(value):
    centered = value - jnp.mean(value, axis=1, keepdims=True)
    inverse = lax.rsqrt(jnp.mean(centered * centered, axis=1, keepdims=True) + epsilon)
    return centered * inverse, inverse


def front_kernel(
    dims,
    prefix_ref, routes_ref, priority_ref, tokens_hbm, cot_hbm, small_hbm, router_hbm, qkv_hbm, out_hbm,
    qkv_out, act_out, merged_out, back_out, weight_out, out_full, low_out, high_out, grads_rows,
    hidden_hbm, send_hbm, small_out, router_out,
    tokens_ref, cot_ref, hidden_ref, send_ref,
    small, weight, out_w, qkv, act, merged, act_two, turned, pick, back, grads_send, low_buf, high_buf,
    own_sem, disp_send, disp_recv, small_send, small_recv, gat_send, gat_recv, store_sem, prob_sem, first_sem,
):
    owners, capacity, pieces = dims
    place = Place(owners)
    firsts = [
        pltpu.make_async_copy(src, dst, first_sem.at[i])
        for i, (src, dst) in enumerate(((cot_hbm, cot_ref), (tokens_hbm, tokens_ref)))
    ]
    for load in firsts:
        load.start()
    rows, width = tokens_ref.shape
    shard = qkv_hbm.shape[0]
    gathers = [
        Gather(place, pieces, parts, src, dst, (gat_send.at[i], gat_recv.at[i]))
        for i, (parts, src, dst) in enumerate(((3, qkv_hbm, weight), (1, out_hbm, out_w)))
    ]
    for gather in gathers:
        gather.start_own()
    vectors, gates = small_hbm.shape[0], router_hbm.shape[0]
    small_parts = [
        (small_hbm, small.at[place.w, pl.ds(0, vectors)]),
        (router_hbm, small.at[place.w, pl.ds(vectors, gates)]),
    ]
    own_smalls = [
        pltpu.make_async_copy(src, dst, own_sem.at[3 + i])
        for i, (src, dst) in enumerate(small_parts)
    ]
    for copy in own_smalls:
        copy.start()
    greet(
        [(place.ahead(k), place.w) for k in range(1, owners)]
        + [(place.e, place.sib), (place.e, place.far), (place.e, place.diag)]
    )
    smalls = [
        remote(src, dst, small_send.at[n, i], small_recv.at[n, i], (place.e, peer))
        for i, peer in enumerate((place.sib, place.far, place.diag))
        for n, (src, dst) in enumerate(small_parts)
    ]
    for copy in smalls:
        copy.start()
    for gather in gathers:
        gather.start()
    slot_tables(routes_ref, priority_ref, capacity, pick, back)
    tile = min(256, width)
    shape = grads_send.shape[:3]

    def to_slots(values_ref, slots_ref):
        def one(n):
            cols = span(n * tile, tile)
            value = dot_nn(pick[...], values_ref[:, cols]).astype(jnp.bfloat16)
            slots_ref[:, :, :, cols] = value.reshape(shape + (tile,))

        every(0, width // tile, one)

    firsts[0].wait()
    to_slots(cot_ref, grads_send)
    dispatch = Dispatch(
        place, capacity, grads_send, grads_rows, (own_sem.at[0], disp_send, disp_recv)
    )
    dispatch.start()
    for copy in own_smalls:
        copy.wait()
    for copy in smalls:
        copy.wait_recv()
    small_out[...] = small[:, :vectors, :]
    router_out[...] = jnp.zeros_like(router_out)
    router_out[:gates, :] = jnp.concatenate(
        [small[i, vectors:, :] for i in range(4)], axis=1
    )

    def vector(which):
        parts = [small[i, which : which + 1, :] for i in range(4)]
        return jnp.concatenate(parts, axis=1).astype(jnp.float32)

    band = min(64, rows)
    gain, shift = vector(0), vector(1)

    def norm_band(i):
        part = span(i * band, band)
        scaled, _ = norm_stats(tokens_ref[part, :].astype(jnp.float32))
        act[part, :] = (scaled * gain + shift).astype(jnp.bfloat16)

    def project(n):
        for part in range(3):
            cols = gathers[0].cols(n, part)
            qkv[:, cols] = dot_nn(act[...], weight[:, cols]).astype(jnp.bfloat16)

    gathers[0].pass_on(0)
    firsts[1].wait()
    every(0, rows // band, norm_band)
    turned[0] = act[...].T
    stores = [
        pltpu.make_async_copy(src, dst, store_sem.at[i])
        for i, (src, dst) in enumerate(
            [(qkv, qkv_out), (turned.at[0], act_out), (back, back_out), (weight, weight_out),
             (turned.at[1], merged_out), (out_w, out_full)]
        )
    ]
    for store in stores[1:3]:
        store.start()
    half = rows // 2
    pairs = width // LANES

    def keep_probs(i):
        slot = lax.rem(i, 2)
        return (
            pltpu.make_async_copy(
                low_buf.at[slot], low_out.at[pl.ds(2 * i, 2)], prob_sem.at[0, slot]
            ),
            pltpu.make_async_copy(
                high_buf.at[slot], high_out.at[pl.ds(2 * i, 2)], prob_sem.at[1, slot]
            ),
        )

    def attend_pair(i):
        slot = lax.rem(i, 2)

        @pl.when(i >= 2)
        def _():
            for copy in keep_probs(i - 2):
                copy.wait()

        query, key, value = (
            qkv[:, span(part * width + i * LANES, LANES)] for part in range(3)
        )
        tops, bottoms = [], []
        for head in range(2):
            part = slice(head * HEAD_DIM, (head + 1) * HEAD_DIM)
            low, high, top, bottom = attend_head(
                query[:, part], key[:, part], value[:, part], prefix_ref[0]
            )
            low_buf[slot, head] = low
            high_buf[slot, head] = high
            tops.append(top)
            bottoms.append(bottom)
        cols = span(i * LANES, LANES)
        merged[:half, cols] = jnp.concatenate(tops, axis=1).astype(jnp.bfloat16)
        merged[half:, cols] = jnp.concatenate(bottoms, axis=1).astype(jnp.bfloat16)
        for copy in keep_probs(i):
            copy.start()

    group = pairs // pieces
    share = -(-owners // pieces)

    def front_step(n):
        @pl.when(n + 1 < pieces)
        def _():
            gathers[0].pass_on(n + 1)

        gathers[0].pass_pair(n)
        for i, partner in enumerate(dispatch.order()):
            pl.when(n == i // share)(functools.partial(dispatch.forward, partner))
        gathers[0].ready(n)
        project(n)
        pl.when(n >= 2)(lambda: gathers[1].pass_on(n - 2))

        @pl.when(n == pieces - 1)
        def _():
            gathers[1].pass_on(pieces - 2)
            gathers[1].pass_pair(0)

        for i in range(group):
            attend_pair(n * group + i)

    every(0, pieces, front_step)
    gathers[1].pass_on(pieces - 1)
    every(1, pieces, gathers[1].pass_pair)
    turned[1] = merged[...].T
    for i in (0, 3, 4):
        stores[i].start()
    order = dispatch.order()
    dispatch.relay(order[0])
    every(0, pieces, gathers[1].ready)
    stores[5].start()
    gain_two, shift_two = vector(2), vector(3)
    band_two = min(128, rows)

    def middle(i):
        part = span(i * band_two, band_two)
        value = tokens_ref[part, :].astype(jnp.float32) + dot_nn(merged[part, :], out_w[...])
        hidden_ref[part, :] = value
        scaled, _ = norm_stats(value)
        act_two[part, :] = (scaled * gain_two + shift_two).astype(jnp.bfloat16)
        for n, partner in enumerate(order[1 : 1 + bands]):
            pl.when(i == n)(functools.partial(dispatch.relay, partner))

    bands = rows // band_two
    every(0, bands, middle)
    results = [
        pltpu.make_async_copy(src, dst, first_sem.at[2 + i])
        for i, (src, dst) in enumerate(((hidden_ref, hidden_hbm), (send_ref, send_hbm)))
    ]
    results[0].start()
    to_slots(act_two, send_ref)
    results[1].start()
    for partner in order[1 + bands :]:
        dispatch.relay(partner)
    for i in (pairs - 2, pairs - 1):
        for copy in keep_probs(i):
            copy.wait()
    every(0, owners, dispatch.ready)
    for store in stores + results:
        store.wait()
    for copy in smalls:
        copy.wait_send()
    for gather in gathers:
        gather.drain()
    dispatch.drain()


def run_front(
    owners, experts, capacity, prefix, routes, priority, tokens, cotangent, small, router, w_qkv, w_out
):
    rows, width = tokens.shape
    shard, columns = w_qkv.shape
    half = rows // 2
    heads = width // HEAD_DIM
    pieces = 4
    any_spec = pl.BlockSpec(memory_space=pl.ANY)
    vmem_spec = pl.BlockSpec(memory_space=pltpu.VMEM)
    bf16, f32 = jnp.bfloat16, jnp.float32
    dma = pltpu.SemaphoreType.DMA

    def out(*shape):
        return jax.ShapeDtypeStruct(shape, bf16)

    def vm(*shape):
        return pltpu.VMEM(shape, bf16)

    return pl.pallas_call(
        functools.partial(front_kernel, (owners, capacity, pieces)),
        out_shape=(
            out(rows, columns),
            out(width, rows),
            out(width, rows),
            out(rows, rows),
            out(4 * shard, columns),
            out(4 * shard, width),
            out(heads, half, half),
            out(heads, half, rows),
            out(experts, owners * 4 * capacity, width),
            jax.ShapeDtypeStruct((rows, width), f32),
            out(owners, experts, capacity, width),
            out(4, *small.shape),
            out(LANES, width),
        ),
        in_specs=[pl.BlockSpec(memory_space=pltpu.SMEM)] + [vmem_spec] * 2 + [any_spec] * 6,
        out_specs=(any_spec,) * 11 + (vmem_spec,) * 2,
        scratch_shapes=[
            vm(rows, width),
            vm(rows, width),
            pltpu.VMEM((rows, width), f32),
            vm(owners, experts, capacity, width),
            vm(4, small.shape[0] + router.shape[0], shard),
            vm(4 * shard, columns),
            vm(4 * shard, width),
            vm(rows, columns),
            vm(rows, width),
            vm(rows, width),
            vm(rows, width),
            vm(2, width, rows),
            vm(rows, rows),
            vm(rows, rows),
            vm(owners, experts, capacity, width),
            vm(2, 2, half, half),
            vm(2, 2, half, rows),
            dma((5,)),
            dma((4, owners)),
            dma((4, owners)),
            dma((2, 3)),
            dma((2, 3)),
            dma((2, 6, pieces, 3)),
            dma((2, 6, pieces, 3)),
            dma((6,)),
            dma((2, 2)),
            dma((4,)),
        ],
        compiler_params=pltpu.CompilerParams(
            collective_id=0, has_side_effects=True, vmem_limit_bytes=VMEM_LIMIT
        ),
        name="front",
    )(prefix, routes, priority, tokens, cotangent, small, router, w_qkv, w_out)


class Reduce:
    def __init__(self, place, part, got, far, pair, near, line, done, sems):
        self.p = place
        self.part, self.got, self.far = part, got, far
        self.pair, self.near, self.line, self.done = pair, near, line, done
        self.send, self.recv = sems
        self.chunks = part.shape[0]
        self.halves = done.shape[1] // 2
        self.bit = lax.rem(place.e, 2)
        self.low = lax.rem(lax.div(place.e, 2), 2)
        self.high = lax.div(place.e, 4)

    def step(self, which, n, src, dst, device):
        return remote(src, dst, self.send.at[which, n], self.recv.at[which, n], device)

    def swapped(self, n):
        return self.step(
            0, n, self.part.at[n, :, 1 - self.p.c], self.got.at[n], (self.p.e, self.p.sib)
        )

    def crossed(self, n):
        return self.step(
            1, n, self.part.at[n, 1 - self.p.x, self.p.c], self.far.at[n], (self.p.e, self.p.far)
        )

    def folded(self, n):
        other = span((1 - self.bit) * self.halves, self.halves)
        return self.step(
            2, n, self.part.at[n, self.p.x, self.p.c, other], self.pair.at[n],
            (self.p.pair, self.p.w),
        )

    def shared(self, n):
        part = self.done.at[n, span(self.bit * self.halves, self.halves)]
        return self.step(3, n, part, part, (self.p.pair, self.p.w))

    def quarter(self, low):
        size = self.halves // 2
        return span(self.bit * self.halves + low * size, size)

    def eighth(self, high):
        size = self.halves // 4
        return span(self.bit * self.halves + (self.low * 2 + high) * size, size)

    def nears(self, n):
        return self.step(
            4, n, self.part.at[n, self.p.x, self.p.c, self.quarter(1 - self.low)],
            self.near.at[n], (self.p.flip(2), self.p.w),
        )

    def lines(self, n):
        return self.step(
            5, n, self.part.at[n, self.p.x, self.p.c, self.eighth(1 - self.high)],
            self.line.at[n], (self.p.flip(4), self.p.w),
        )

    def line_back(self, n):
        part = self.done.at[n, self.eighth(self.high)]
        return self.step(6, n, part, part, (self.p.flip(4), self.p.w))

    def near_back(self, n):
        part = self.done.at[n, self.quarter(self.low)]
        return self.step(7, n, part, part, (self.p.flip(2), self.p.w))

    def add(self, n, rows, other):
        total = self.part[n, self.p.x, self.p.c, rows, :].astype(jnp.float32) + other.astype(
            jnp.float32
        )
        return total.astype(jnp.bfloat16)

    def pair_sum(self, n, side):
        return self.part[n, side, self.p.c].astype(jnp.float32) + self.got[n, side].astype(
            jnp.float32
        )

    def swap(self, n):
        self.swapped(n).start()

    def cross(self, n):
        self.swapped(n).wait_recv()
        side = 1 - self.p.x
        self.part[n, side, self.p.c] = self.pair_sum(n, side).astype(jnp.bfloat16)
        self.crossed(n).start()

    def fold(self, n):
        self.crossed(n).wait_recv()
        total = self.pair_sum(n, self.p.x) + self.far[n].astype(jnp.float32)
        self.part[n, self.p.x, self.p.c] = total.astype(jnp.bfloat16)
        self.folded(n).start()

    def spread(self, n):
        self.folded(n).wait_recv()
        own = span(self.bit * self.halves, self.halves)
        self.part[n, self.p.x, self.p.c, own, :] = self.add(n, own, self.pair[n])
        self.nears(n).start()

    def reach(self, n):
        self.nears(n).wait_recv()
        own = self.quarter(self.low)
        self.part[n, self.p.x, self.p.c, own, :] = self.add(n, own, self.near[n])
        self.lines(n).start()

    def collect(self, n):
        self.lines(n).wait_recv()
        own = self.eighth(self.high)
        self.done[n, own, :] = self.add(n, own, self.line[n])
        self.line_back(n).start()

    def widen_back(self, n):
        self.line_back(n).wait_recv()
        self.near_back(n).start()

    def share(self, n):
        self.near_back(n).wait_recv()
        self.shared(n).start()

    def finish(self, n):
        self.shared(n).wait_recv()

    def line_stages(self):
        return (self.spread, self.reach, self.collect, self.widen_back, self.share, self.finish)

    def stages(self):
        return (self.cross, self.fold) + self.line_stages()

    def drain(self):
        def one(n):
            for copy in (
                self.swapped(n), self.crossed(n), self.folded(n), self.shared(n), self.nears(n),
                self.lines(n), self.line_back(n), self.near_back(n),
            ):
                copy.wait_send()

        every(0, self.chunks, one)


class PairFirst(Reduce):
    def folded(self, n):
        other = span((1 - self.bit) * self.halves, self.halves)
        return self.step(
            2, n, self.part.at[n, :, self.p.c, other], self.pair.at[n], (self.p.pair, self.p.w)
        )

    def crossed(self, n):
        own = span(self.bit * self.halves, self.halves)
        return self.step(
            1, n, self.part.at[n, 1 - self.p.x, self.p.c, own], self.far.at[n],
            (self.p.e, self.p.far),
        )

    def fold(self, n):
        self.swapped(n).wait_recv()
        for side in range(2):
            self.part[n, side, self.p.c] = self.pair_sum(n, side).astype(jnp.bfloat16)
        self.folded(n).start()

    def cross(self, n):
        self.folded(n).wait_recv()
        own = span(self.bit * self.halves, self.halves)
        for side in range(2):
            total = self.part[n, side, self.p.c, own, :].astype(jnp.float32) + self.pair[
                n, side
            ].astype(jnp.float32)
            self.part[n, side, self.p.c, own, :] = total.astype(jnp.bfloat16)
        self.crossed(n).start()

    def spread(self, n):
        self.crossed(n).wait_recv()
        own = span(self.bit * self.halves, self.halves)
        self.part[n, self.p.x, self.p.c, own, :] = self.add(n, own, self.far[n])
        self.nears(n).start()

    def stages(self):
        return (self.fold, self.cross) + self.line_stages()


class Small:
    def __init__(self, place, value, part, got, mid, far, total, others, out, sems):
        self.p, self.value, self.part, self.got, self.mid = place, value, part, got, mid
        self.far, self.total, self.others, self.out = far, total, others, out
        self.send, self.recv, self.all_send, self.all_recv = sems

    def swapped(self):
        return remote(
            self.part.at[:, 1 - self.p.c], self.got, self.send.at[0], self.recv.at[0],
            (self.p.e, self.p.sib),
        )

    def crossed(self):
        return remote(
            self.mid, self.far, self.send.at[1], self.recv.at[1], (self.p.e, self.p.far)
        )

    def spreads(self, k):
        return remote(
            self.total, self.others.at[k], self.all_send.at[k], self.all_recv.at[k],
            (self.p.ahead(k), self.p.w),
        )

    def swap(self):
        size = self.part.shape[-1]
        for owner in range(4):
            self.part[owner // 2, owner % 2] = self.value[:, owner * size : (owner + 1) * size]
        self.swapped().start()

    def cross(self):
        self.swapped().wait_recv()
        self.mid[...] = self.part[1 - self.p.x, self.p.c] + self.got[1 - self.p.x]
        self.crossed().start()

    def spread(self):
        self.crossed().wait_recv()
        self.total[...] = self.part[self.p.x, self.p.c] + self.got[self.p.x] + self.far[...]
        for k in range(1, self.p.owners):
            self.spreads(k).start()

    def finish(self):
        total = self.total[...]
        for k in range(1, self.p.owners):
            self.spreads(k).wait_recv()
            total = total + self.others[k]
        vectors_out, gates_out = self.out
        vectors_out[...] = total[: vectors_out.shape[0]]
        gates_out[...] = total[vectors_out.shape[0] :]

    def drain(self):
        self.swapped().wait_send()
        self.crossed().wait_send()
        for k in range(1, self.p.owners):
            self.spreads(k).wait_send()


def norm_back_rows(grad, scaled, inverse, gain):
    weighted = grad * gain
    mean_one = jnp.mean(weighted, axis=1, keepdims=True)
    mean_two = jnp.mean(weighted * scaled, axis=1, keepdims=True)
    return inverse * (weighted - mean_one - scaled * mean_two)


def back_kernel(
    dims,
    home_grad_hbm, back_hbm, hidden_hbm, cot_hbm, tokens_hbm, vectors_ref, router_ref,
    far_hbm, near_hbm, home_hbm, act_hbm, merged_hbm, qkv_hbm, weight_hbm, out_hbm, low_hbm, high_hbm,
    output_hbm, grad_tokens_hbm, vectors_out, gates_out, qkv_out, out_out,
    home_grad_ref, back_ref, hidden_ref, cot_ref, tokens_ref, output_ref, tokens_out,
    near_sums, far_sums, done_rows, home_out,
    act_t, merged_t, qkv, weight, out_w, low_buf, high_buf, attn, grad_merged, grad_act,
    part_q, got_q, far_q, pair_q, near_q, line_q, done_q,
    part_o, got_o, far_o, pair_o, near_o, line_o, done_o,
    small, small_part, small_got, small_mid, small_far, small_sum, small_all,
    first_sem, load_sem, prob_sem, own_sem, early_sem, cross_send, cross_recv, home_send, home_recv, send_q, recv_q, send_o, recv_o,
    small_send, small_recv, all_send, all_recv, out_sem,
):
    owners, capacity, gates = dims
    grad_qkv = qkv
    place = Place(owners)
    loads = [
        pltpu.make_async_copy(src, dst, load_sem.at[i])
        for i, (src, dst) in enumerate(
            [(merged_hbm, merged_t), (out_hbm, out_w), (qkv_hbm, qkv), (act_hbm, act_t),
             (weight_hbm, weight), (near_hbm, near_sums)]
        )
    ]

    def load_probs(i):
        slot = lax.rem(i, 2)
        return (
            pltpu.make_async_copy(
                low_hbm.at[pl.ds(2 * i, 2)], low_buf.at[slot], prob_sem.at[0, slot]
            ),
            pltpu.make_async_copy(
                high_hbm.at[pl.ds(2 * i, 2)], high_buf.at[slot], prob_sem.at[1, slot]
            ),
        )

    firsts = [
        pltpu.make_async_copy(src, dst, first_sem.at[i])
        for i, (src, dst) in enumerate(
            [(home_grad_hbm, home_grad_ref), (back_hbm, back_ref), (hidden_hbm, hidden_ref),
             (cot_hbm, cot_ref), (tokens_hbm, tokens_ref)]
        )
    ]
    results = [
        pltpu.make_async_copy(src, dst, first_sem.at[5 + i])
        for i, (src, dst) in enumerate([(tokens_out, grad_tokens_hbm), (output_ref, output_hbm)])
    ]
    for load in firsts[:4] + loads + firsts[4:]:
        load.start()
    for load in load_probs(0):
        load.start()
    greet(
        [(place.ahead(k), place.w) for k in range(1, owners)]
        + [(place.e, place.sib), (place.e, place.far)]
    )
    experts = near_sums.shape[0]
    groups = owners // 2
    late = LateReturn(
        place, capacity, near_sums, None, far_hbm, far_sums, done_rows, home_out,
        (own_sem, cross_send, cross_recv, home_send, home_recv),
    )

    def start_late(j):
        for expert in range(experts):
            late.crossed(j, expert).start()

    every(EARLY_CHUNKS, groups, start_late)

    def early_rows(n):
        row = place.peer(n)
        return pltpu.make_async_copy(home_hbm.at[row], home_out.at[row], early_sem.at[n])

    every(0, 2 * EARLY_CHUNKS, lambda n: early_rows(n).start())
    reduce_o = PairFirst(
        place, part_o, got_o, far_o, pair_o, near_o, line_o, done_o, (send_o, recv_o)
    )
    reduce_q = Reduce(
        place, part_q, got_q, far_q, pair_q, near_q, line_q, done_q, (send_q, recv_q)
    )
    smalls = Small(
        place, small, small_part, small_got, small_mid, small_far, small_sum, small_all, (vectors_out, gates_out),
        (small_send, small_recv, all_send, all_recv),
    )
    rows, width = tokens_ref.shape
    shard = width // 4
    band = min(128, rows)
    lead = small.shape[0]

    def vector(which):
        parts = [vectors_ref[i, which : which + 1, :] for i in range(4)]
        return jnp.concatenate(parts, axis=1).astype(jnp.float32)

    gain_one, gain_two = vector(0), vector(2)
    small[: lead - gates, :] = jnp.zeros((lead - gates, width), jnp.float32)
    small[lead - gates :, :] = router_ref[:gates, :]

    def post(i):
        part = span(i * band, band)
        grad = dot_nn(back_ref[part, :], home_grad_ref.reshape(rows, width)[...])
        scaled, inverse = norm_stats(hidden_ref[part, :])
        value = cot_ref[part, :].astype(jnp.float32) + norm_back_rows(
            grad, scaled, inverse, gain_two
        )
        tokens_out[part, :] = value
        attn[part, :] = value.astype(jnp.bfloat16)
        small[2:3, :] += jnp.sum(grad * scaled, axis=0, keepdims=True)
        small[3:4, :] += jnp.sum(grad, axis=0, keepdims=True)

    for load in firsts[:4]:
        load.wait()
    every(0, rows // band, post)
    loads[0].wait()

    def weight_grad(part, n, left, right):
        value = dot_nn(left[...], right).astype(jnp.bfloat16)
        part[n] = value.reshape(part.shape[1:])

    tile_o = part_o.shape[-1]
    out_chunks = part_o.shape[0]
    for n in range(out_chunks):
        weight_grad(part_o, n, merged_t, attn[:, n * tile_o : (n + 1) * tile_o])
        reduce_o.swap(n)
    loads[1].wait()

    def merged_band(i):
        part = span(i * band, band)
        grad_merged[part, :] = dot_nt(attn[part, :], out_w[...]).astype(jnp.bfloat16)

    every(0, rows // band, merged_band)
    stages_o, stages_q = reduce_o.stages(), reduce_q.stages()
    for n in range(out_chunks):
        stages_o[0](n)
    for load in loads[2:] + firsts[4:]:
        load.wait()
    grad_act[...] = jnp.zeros_like(grad_act)
    pairs = part_q.shape[0]

    def attend_pair(i):
        slot = lax.rem(i, 2)
        for load in load_probs(i):
            load.wait()

        @pl.when(i + 1 < pairs)
        def _():
            for load in load_probs(i + 1):
                load.start()

        cols = span(i * LANES, LANES)
        query, key, value = (
            qkv[:, span(part * width + i * LANES, LANES)] for part in range(3)
        )
        grad = grad_merged[:, cols]
        results = []
        for head in range(2):
            part = slice(head * HEAD_DIM, (head + 1) * HEAD_DIM)
            results.append(
                attend_back_head(
                    query[:, part], key[:, part], value[:, part],
                    low_buf[slot, head], high_buf[slot, head], grad[:, part],
                )
            )
        for which in range(3):
            grad_qkv[:, span(which * width + i * LANES, LANES)] = jnp.concatenate(
                [results[0][which], results[1][which]], axis=1
            )
        right = jnp.concatenate(
            [grad_qkv[:, span(which * width + i * LANES, LANES)] for which in range(3)], axis=1
        )
        weight_grad(part_q, i, act_t, right)
        reduce_q.swap(i)
        columns = jnp.concatenate(
            [weight[:, span(which * width + i * LANES, LANES)] for which in range(3)], axis=1
        )
        grad_act[...] += dot_nt(right, columns)

    def input_band(i):
        part = span(i * band, band)
        grad = grad_act[part, :]
        scaled, inverse = norm_stats(tokens_ref[part, :].astype(jnp.float32))
        tokens_out[part, :] += norm_back_rows(grad, scaled, inverse, gain_one)
        small[0:1, :] += jnp.sum(grad * scaled, axis=0, keepdims=True)
        small[1:2, :] += jnp.sum(grad, axis=0, keepdims=True)

    def output_band(i):
        part = span(i * band, band)
        slots = home_out.reshape(rows, width)
        value = hidden_ref[part, :] + dot_nn(back_ref[part, :], slots[...])
        output_ref[part, :] = value.astype(jnp.bfloat16)

    def store_q(i):
        return [
            pltpu.make_async_copy(
                done_q.at[i, :, pl.ds(which * LANES, LANES)],
                qkv_out.at[:, span(which * width + i * LANES, LANES)],
                out_sem.at[which, i],
            )
            for which in range(3)
        ]

    def store_o(n):
        return pltpu.make_async_copy(
            done_o.at[n], out_out.at[:, span(n * tile_o, tile_o)], out_sem.at[3, n]
        )

    delays = (1, 3, 4, 5, 6, 7, 8, 9)
    turns_o = (-1, 3, 5, 6, 7, 8, 9, 10)
    last = len(delays) - 1
    half = rows // band // 2

    def slot_step(slot):
        @pl.when(slot + EARLY_CHUNKS < groups)
        def _():
            for expert in range(experts):
                late.finish(slot + EARLY_CHUNKS, expert)

        pl.when(slot < pairs)(lambda: attend_pair(slot))
        for s in range(last, -1, -1):
            n = slot - delays[s]

            @pl.when((n >= 0) & (n < pairs))
            def _(s=s, n=n):
                stages_q[s](n)
                if s == last:
                    for copy in store_q(n):
                        copy.start()

            @pl.when(slot == turns_o[s])
            def _(s=s):
                for n in range(out_chunks):
                    stages_o[s](n)
                    if s == last:
                        store_o(n).start()

        @pl.when(slot == pairs)
        def _():
            every(0, half, input_band)

        @pl.when(slot == pairs + 1)
        def _():
            every(half, 2 * half, input_band)
            results[0].start()

        pl.when(slot == pairs + 2)(smalls.swap)
        pl.when(slot == pairs + 3)(smalls.cross)
        pl.when(slot == pairs + 4)(smalls.spread)

        @pl.when(slot == pairs + 3)
        def _():
            late.arrived(EARLY_CHUNKS, groups, experts)
            every(0, 2 * EARLY_CHUNKS, lambda n: early_rows(n).wait())
            every(0, rows // band, output_band)
            results[1].start()

    every(0, pairs + delays[-1], slot_step)
    smalls.finish()

    def stored(i):
        for copy in store_q(i):
            copy.wait()

    every(0, pairs, stored)
    for result in results:
        result.wait()
    for n in range(out_chunks):
        store_o(n).wait()
    late.drain(EARLY_CHUNKS, groups, experts)
    reduce_o.drain()
    reduce_q.drain()
    smalls.drain()


def run_back(
    owners, capacity, gates, home_grad, far_sums, near_sums, home_out, back, hidden, cotangent, tokens,
    vectors, router_grad, act_t, merged_t, qkv, weight, w_out, low, high,
):
    rows, width = tokens.shape
    shard = width // 4
    lead = 8 + gates
    groups = owners // 2
    pairs = width // LANES
    tile_o = min(512, width)
    out_chunks = width // tile_o
    half = shard // 2
    mid = rows // 2
    any_spec = pl.BlockSpec(memory_space=pl.ANY)
    vmem_spec = pl.BlockSpec(memory_space=pltpu.VMEM)
    bf16, f32 = jnp.bfloat16, jnp.float32
    dma = pltpu.SemaphoreType.DMA

    def vm(*shape):
        return pltpu.VMEM(shape, bf16)

    def fm(*shape):
        return pltpu.VMEM(shape, f32)

    def reduce_buffers(chunks, tile, pair_first):
        far, pair = ((half,), (2, half)) if pair_first else ((shard,), (half,))
        return [
            vm(chunks, 2, 2, shard, tile),
            vm(chunks, 2, shard, tile),
            vm(chunks, *far, tile),
            vm(chunks, *pair, tile),
            vm(chunks, half // 2, tile),
            vm(chunks, half // 4, tile),
            vm(chunks, shard, tile),
        ]

    def reduce_sems(chunks):
        return [dma((8, chunks)), dma((8, chunks))]

    return pl.pallas_call(
        functools.partial(back_kernel, (owners, capacity, gates)),
        out_shape=(
            jax.ShapeDtypeStruct((rows, width), bf16),
            jax.ShapeDtypeStruct((rows, width), f32),
            jax.ShapeDtypeStruct((8, shard), f32),
            jax.ShapeDtypeStruct((gates, shard), f32),
            jax.ShapeDtypeStruct((shard, 3 * width), bf16),
            jax.ShapeDtypeStruct((shard, width), bf16),
        ),
        in_specs=[any_spec] * 5 + [vmem_spec] * 2 + [any_spec] * 10,
        out_specs=(any_spec,) * 2 + (vmem_spec,) * 2 + (any_spec,) * 2,
        scratch_shapes=[
            vm(*home_grad.shape),
            vm(rows, rows),
            fm(rows, width),
            vm(rows, width),
            vm(rows, width),
            vm(rows, width),
            fm(rows, width),
            vm(*near_sums.shape),
            vm(*near_sums.shape),
            vm(*home_grad.shape),
            vm(*home_grad.shape),
            vm(width, rows),
            vm(width, rows),
            vm(rows, 3 * width),
            vm(width, 3 * width),
            vm(width, width),
            vm(2, 2, mid, mid),
            vm(2, 2, mid, rows),
            vm(rows, width),
            vm(rows, width),
            fm(rows, width),
        ]
        + reduce_buffers(pairs, 3 * LANES, False)
        + reduce_buffers(out_chunks, tile_o, True)
        + [
            fm(lead, width),
            fm(2, 2, lead, shard),
            fm(2, lead, shard),
            fm(lead, shard),
            fm(lead, shard),
            fm(lead, shard),
            fm(owners, lead, shard),
            dma((7,)),
            dma((6,)),
            dma((2, 2)),
            dma((near_sums.shape[0],)),
            dma((owners,)),
            dma((groups, near_sums.shape[0])),
            dma((groups, near_sums.shape[0])),
            dma((owners, near_sums.shape[0])),
            dma((owners, near_sums.shape[0])),
        ]
        + reduce_sems(pairs)
        + reduce_sems(out_chunks)
        + [dma((2,)), dma((2,)), dma((owners,)), dma((owners,)), dma((4, pairs))],
        compiler_params=pltpu.CompilerParams(
            collective_id=2, has_side_effects=True, vmem_limit_bytes=VMEM_LIMIT
        ),
        name="back",
    )(
        home_grad, back, hidden, cotangent, tokens, vectors, router_grad,
        far_sums, near_sums, home_out, act_t, merged_t, qkv, weight, w_out, low, high,
    )


def widen_kernel(vectors_ref, *refs):
    count = (len(refs) - 4) // 2
    for src, dst in zip(refs[:count], refs[count:]):
        dst[...] = src[...].astype(dst.dtype)
    for i, dst in enumerate(refs[2 * count :]):
        dst[...] = vectors_ref[i, :]


def widen(steps, vectors, values, kinds):
    def spec(value):
        if value.shape[0] % (16 * steps):
            return pl.BlockSpec(value.shape, lambda i: (0, 0))
        return pl.BlockSpec((value.shape[0] // steps, value.shape[1]), lambda i: (i, 0))

    return pl.pallas_call(
        widen_kernel,
        grid=(steps,),
        in_specs=[pl.BlockSpec(vectors.shape, lambda i: (0, 0))]
        + [spec(value) for value in values],
        out_specs=[spec(value) for value in values]
        + [pl.BlockSpec((vectors.shape[1],), lambda i: (0,))] * 4,
        out_shape=[
            jax.ShapeDtypeStruct(value.shape, kind) for value, kind in zip(values, kinds)
        ]
        + [jax.ShapeDtypeStruct((vectors.shape[1],), jnp.float32)] * 4,
        name="widen",
    )(vectors, *values)


def on_device_plain(
    tokens,
    norm1_gain,
    norm1_shift,
    w_qkv,
    w_out,
    norm2_gain,
    norm2_shift,
    w_router,
    w_up,
    w_down,
    routes,
    priority,
    prefix,
    cotangent,
):
    row_count, model_width = tokens.shape
    expert_count = w_router.shape[1]
    capacity = row_count // expert_count
    owners = lax.axis_size("expert")
    local_experts = w_up.shape[0]
    slot_count = expert_count * capacity
    prefix_len = prefix[0]
    small = jnp.concatenate(
        [
            norm1_gain[None],
            norm1_shift[None],
            norm2_gain[None],
            norm2_shift[None],
            w_router.T,
        ],
        axis=0,
    )
    qkv_full = lax.all_gather(w_qkv, "wshard", axis=0, tiled=True)
    small_full = lax.all_gather(small, "wshard", axis=1, tiled=True)
    out_full = lax.all_gather(w_out, "wshard", axis=0, tiled=True)
    gain_one, shift_one, gain_two, shift_two = (small_full[i] for i in range(4))
    router_full = small_full[4:].T
    gain_one = gain_one.astype(jnp.float32)
    gain_two = gain_two.astype(jnp.float32)
    inputs = tokens.astype(jnp.float32)
    normed_one, scaled_one, inverse_one = normalize(inputs, gain_one, shift_one.astype(jnp.float32))
    act_one = normed_one.astype(jnp.bfloat16)
    qkv = jnp.dot(act_one, qkv_full, preferred_element_type=jnp.float32).astype(jnp.bfloat16)
    query_heads = qkv[:, :model_width]
    key_heads = qkv[:, model_width : 2 * model_width]
    value_heads = qkv[:, 2 * model_width :]
    merged, log_totals = attend_forward(query_heads, key_heads, value_heads, prefix_len)
    attn_out = jnp.dot(merged, out_full, preferred_element_type=jnp.float32)
    hidden = inputs + attn_out
    normed_two, scaled_two, inverse_two = normalize(hidden, gain_two, shift_two.astype(jnp.float32))
    act_two = normed_two.astype(jnp.bfloat16)
    logits = jnp.dot(act_two, router_full, preferred_element_type=jnp.float32)
    row_max = jnp.max(logits, axis=-1, keepdims=True)
    exponent = jnp.exp(logits - row_max)
    gate_prob = exponent / jnp.sum(exponent, axis=-1, keepdims=True)
    route_ids = routes[:, 0]
    chosen = route_ids[:, None] == jnp.arange(expert_count, dtype=jnp.int32)[None, :]
    gate_value = jnp.sum(jnp.where(chosen, gate_prob, 0.0), axis=1)
    slot_index, slot_source = assign_slots(route_ids, priority[0], expert_count, capacity)
    zero_row = jnp.zeros((1, model_width), jnp.bfloat16)
    padded = jnp.concatenate([act_two, zero_row], axis=0)
    send_rows = padded[slot_source].reshape(owners, local_experts * capacity, model_width)
    arrived = lax.all_to_all(send_rows, "expert", split_axis=0, concat_axis=0, tiled=True).reshape(
        owners, local_experts, capacity, model_width
    )
    group = lax.axis_size("wshard")
    local_rows = owners * capacity

    def by_expert(chunk):
        rows = jnp.transpose(chunk, (1, 0, 2, 3)).reshape(local_experts, local_rows, model_width)
        return lax.all_gather(rows, "wshard", axis=1, tiled=True)

    def home_rows(rows):
        own = lax.psum_scatter(rows.astype(jnp.bfloat16), "wshard", scatter_dimension=1, tiled=True)
        own = own.reshape(local_experts, owners, capacity, model_width)
        return jnp.transpose(own, (1, 0, 2, 3)).reshape(
            owners, local_experts * capacity, model_width
        )

    grad_output = cotangent.astype(jnp.float32)
    grad_combined = (gate_value[:, None] * grad_output).astype(jnp.bfloat16)
    grad_padded = jnp.concatenate([grad_combined, zero_row], axis=0)
    grad_send = grad_padded[slot_source].reshape(owners, local_experts * capacity, model_width)
    grad_arrived = lax.all_to_all(
        grad_send, "expert", split_axis=0, concat_axis=0, tiled=True
    ).reshape(owners, local_experts, capacity, model_width)
    rows_in = by_expert(arrived)
    grad_rows = by_expert(grad_arrived)
    pre_act = jnp.einsum("erd,edf->erf", rows_in, w_up, preferred_element_type=jnp.float32)
    activated, gelu_pull = jax.vjp(gelu_tanh, pre_act)
    act_hidden = activated.astype(jnp.bfloat16)
    produced = jnp.einsum(
        "erf,efd->erd", act_hidden, w_down, preferred_element_type=jnp.float32
    )
    expert_out = home_rows(produced)
    returned = lax.all_to_all(expert_out, "expert", split_axis=0, concat_axis=0, tiled=True)
    slots_back = jnp.concatenate([returned.reshape(slot_count, model_width), zero_row], axis=0)
    combined = slots_back[slot_index].astype(jnp.float32)
    output = (hidden + gate_value[:, None] * combined).astype(jnp.bfloat16)
    grad_gate = jnp.sum(grad_output * combined, axis=1)
    grad_down = jnp.einsum(
        "erf,erd->efd", act_hidden, grad_rows, preferred_element_type=jnp.float32
    )
    grad_hidden_units = jnp.einsum(
        "erd,efd->erf", grad_rows, w_down, preferred_element_type=jnp.float32
    )
    grad_pre = gelu_pull(grad_hidden_units)[0].astype(jnp.bfloat16)
    grad_up = jnp.einsum("erd,erf->edf", rows_in, grad_pre, preferred_element_type=jnp.float32)
    grad_expert_in = jnp.einsum(
        "erf,edf->erd", grad_pre, w_up, preferred_element_type=jnp.float32
    )
    grad_send_back = home_rows(grad_expert_in)
    grad_back = lax.all_to_all(grad_send_back, "expert", split_axis=0, concat_axis=0, tiled=True)
    grad_slots = jnp.concatenate([grad_back.reshape(slot_count, model_width), zero_row], axis=0)
    grad_act_two = grad_slots[slot_index].astype(jnp.float32)
    grad_logits = (
        gate_prob * (jnp.where(chosen, grad_gate[:, None], 0.0) - (gate_value * grad_gate)[:, None])
    ).astype(jnp.bfloat16)
    grad_router = contract_rows(act_two, grad_logits)
    grad_act_two = grad_act_two + times_transpose(grad_logits, router_full)
    grad_from_two, grad_gain_two, grad_shift_two = norm_back(
        grad_act_two, scaled_two, inverse_two, gain_two
    )
    grad_hidden = grad_output + grad_from_two
    grad_attn = grad_hidden.astype(jnp.bfloat16)
    grad_out_w = contract_rows(merged, grad_attn)
    grad_merged = times_transpose(grad_attn, out_full).astype(jnp.bfloat16)
    grad_qkv = attend_backward(
        query_heads, key_heads, value_heads, grad_merged, log_totals, prefix_len
    )
    grad_qkv_w = contract_rows(act_one, grad_qkv)
    grad_act_one = times_transpose(grad_qkv, qkv_full)
    grad_from_one, grad_gain_one, grad_shift_one = norm_back(
        grad_act_one, scaled_one, inverse_one, gain_one
    )
    grad_tokens = grad_hidden + grad_from_one
    small_grad = jnp.concatenate(
        [
            grad_gain_one[None],
            grad_shift_one[None],
            grad_gain_two[None],
            grad_shift_two[None],
            grad_router.T,
        ],
        axis=0,
    )
    out_share = lax.psum_scatter(
        grad_out_w.astype(jnp.bfloat16), "wshard", scatter_dimension=0, tiled=True
    )
    qkv_share = lax.psum_scatter(
        grad_qkv_w.astype(jnp.bfloat16), "wshard", scatter_dimension=0, tiled=True
    )
    small_share = lax.psum_scatter(small_grad, "wshard", scatter_dimension=1, tiled=True)
    out_total = lax.psum(out_share, "expert").astype(jnp.float32)
    qkv_total = lax.psum(qkv_share, "expert").astype(jnp.float32)
    small_total = lax.psum(small_share, "expert")
    totals = (
        small_total[0],
        small_total[1],
        qkv_total,
        out_total,
        small_total[2],
        small_total[3],
        small_total[4:].T,
    )
    return (
        output,
        grad_tokens,
        totals[0],
        totals[1],
        totals[2],
        totals[3],
        totals[4],
        totals[5],
        totals[6],
        grad_up,
        grad_down,
    )


def on_device(
    tokens,
    norm1_gain,
    norm1_shift,
    w_qkv,
    w_out,
    norm2_gain,
    norm2_shift,
    w_router,
    w_up,
    w_down,
    routes,
    priority,
    prefix,
    cotangent,
):
    row_count, model_width = tokens.shape
    expert_count = w_router.shape[1]
    capacity = row_count // expert_count
    owners = lax.axis_size("expert")
    experts = w_up.shape[0]
    which = lax.broadcasted_iota(jnp.int32, (16, norm1_gain.shape[0]), 0)
    small = jnp.zeros(which.shape, jnp.bfloat16)
    for i, vector in enumerate((norm1_gain, norm1_shift, norm2_gain, norm2_shift)):
        small = jnp.where(which == i, vector[None], small)
    (
        qkv, act_t, merged_t, back, weight, out_full, low, high, grad_rows, hidden, send_rows,
        vectors, router,
    ) = run_front(
        owners, experts, capacity, prefix, routes.reshape(1, row_count), priority, tokens,
        cotangent, small, w_router.T, w_qkv, w_out,
    )
    far_sums, near_sums, home_out, home_grad, grad_up, grad_down, grad_router = run_experts(
        owners, capacity, expert_count, send_rows, grad_rows, w_up, w_down, router
    )
    output, grad_tokens, grad_vectors, grad_gates, grad_qkv, grad_out = run_back(
        owners, capacity, expert_count, home_grad, far_sums, near_sums, home_out, back, hidden, cotangent,
        tokens, vectors, grad_router, act_t, merged_t, qkv, weight, out_full, low, high,
    )
    f32 = jnp.float32
    units = w_up.shape[2]
    (
        output, grad_tokens, grad_gates, grad_qkv, grad_out, grad_up, grad_down, *grad_vectors,
    ) = widen(
        2,
        grad_vectors,
        (
            output, grad_tokens, grad_gates, grad_qkv, grad_out,
            grad_up.reshape(-1, units), grad_down.reshape(-1, model_width),
        ),
        (output.dtype,) + (f32,) * 6,
    )
    return (
        output,
        grad_tokens,
        grad_vectors[0],
        grad_vectors[1],
        grad_qkv,
        grad_out,
        grad_vectors[2],
        grad_vectors[3],
        grad_gates.T,
        grad_up.reshape(w_up.shape),
        grad_down.reshape(w_down.shape),
    )


def solution(mesh):
    placed = (
        P(("expert", "wshard"), None),
        P("wshard"),
        P("wshard"),
        P("wshard", None),
        P("wshard", None),
        P("wshard"),
        P("wshard"),
        P("wshard", None),
        P("expert", None, "wshard"),
        P("expert", "wshard", None),
        P(("expert", "wshard"), None),
        P(("expert", "wshard"), None),
        P(("expert", "wshard")),
        P(("expert", "wshard"), None),
    )
    owners, group = mesh.shape["expert"], mesh.shape["wshard"]

    def body(*args):
        capacity = args[0].shape[0] // args[7].shape[1]
        fits = group == 4 and owners == 8 and capacity % 16 == 0 and args[7].shape[1] % 16 == 0
        return (on_device if fits else on_device_plain)(*args)

    return jax.shard_map(
        body,
        mesh=mesh,
        in_specs=placed,
        out_specs=(
            P(("expert", "wshard"), None),
            P(("expert", "wshard"), None),
            P("wshard"),
            P("wshard"),
            P("wshard", None),
            P("wshard", None),
            P("wshard"),
            P("wshard"),
            P("wshard", None),
            P("expert", None, "wshard"),
            P("expert", "wshard", None),
        ),
        check_vma=False,
    )
```

```python
import functools
import math

import jax
import jax.numpy as jnp
from jax import lax
from jax.experimental import pallas as pl
from jax.experimental.pallas import tpu as pltpu
from jax.sharding import PartitionSpec as P

HEADS = 16
HEAD_DIM = 64


epsilon = 1e-05
VMEM_LIMIT = 66_000_000
TILE = 1024
EARLY_CHUNKS = 1


def normalize(values, gain_vec, shift_vec):
    row_mean = jnp.mean(values, axis=-1, keepdims=True)
    centered = values - row_mean
    inverse = lax.rsqrt(jnp.mean(centered * centered, axis=-1, keepdims=True) + epsilon)
    scaled = centered * inverse
    return (scaled * gain_vec + shift_vec, scaled, inverse)


def norm_back(grad_rows, scaled, inverse, gain_vec):
    weighted = grad_rows * gain_vec
    mean_one = jnp.mean(weighted, axis=-1, keepdims=True)
    mean_two = jnp.mean(weighted * scaled, axis=-1, keepdims=True)
    grad_inputs = inverse * (weighted - mean_one - scaled * mean_two)
    return (grad_inputs, jnp.sum(grad_rows * scaled, axis=0), jnp.sum(grad_rows, axis=0))


def contract_rows(left, right):
    return lax.dot_general(
        left, right, (((0,), (0,)), ((), ())), preferred_element_type=jnp.float32
    )


def times_transpose(left, right):
    return lax.dot_general(
        left, right, (((1,), (1,)), ((), ())), preferred_element_type=jnp.float32
    )


def gelu_tanh(values):
    return jax.nn.gelu(values, approximate=True)


def assign_slots(route_ids, order_ids, expert_count, capacity):
    token_count = route_ids.shape[0]
    same_expert = route_ids[:, None] == route_ids[None, :]
    earlier = order_ids[None, :] < order_ids[:, None]
    rank_ids = jnp.sum((same_expert & earlier).astype(jnp.int32), axis=1)
    is_kept = rank_ids < capacity
    slot_index = jnp.where(is_kept, route_ids * capacity + rank_ids, expert_count * capacity)
    slot_ids = jnp.arange(expert_count * capacity, dtype=jnp.int32)
    match_table = slot_index[None, :] == slot_ids[:, None]
    token_ids = jnp.arange(token_count, dtype=jnp.int32)
    filled = jnp.any(match_table, axis=1)
    picked = jnp.sum(jnp.where(match_table, token_ids[None, :], 0), axis=1)
    slot_source = jnp.where(filled, picked, token_count)
    return (slot_index, slot_source)


def group_heads(values, groups):
    token_count = values.shape[0]
    return jnp.transpose(values.reshape(token_count, groups, -1, HEAD_DIM), (1, 0, 2, 3))


def block_scores(query_block, key_group, block_start, prefix_len):
    block_rows = query_block.shape[0]
    key_count = key_group.shape[0]
    scores = jnp.einsum(
        "qgd,kgd->gqk", query_block, key_group, preferred_element_type=jnp.float32
    ) * (1.0 / math.sqrt(HEAD_DIM))
    query_pos = block_start + jnp.arange(block_rows, dtype=jnp.int32)
    key_pos = jnp.arange(key_count, dtype=jnp.int32)
    allowed = (key_pos[None, :] <= query_pos[:, None]) | (key_pos[None, :] < prefix_len)
    return jnp.where(allowed[None], scores, -1e30)


def attend_forward(query_heads, key_heads, value_heads, prefix_len):
    token_count = query_heads.shape[0]
    group_size = min(4, HEADS)
    groups = HEADS // group_size
    block_rows = min(512, token_count)
    blocks = token_count // block_rows
    starts = jnp.arange(blocks, dtype=jnp.int32) * block_rows

    def one_group(group_item):
        query_group, key_group, value_group = group_item
        query_blocks = query_group.reshape(blocks, block_rows, group_size, HEAD_DIM)

        def one_block(block_item):
            query_block, block_start = block_item
            scores = block_scores(query_block, key_group, block_start, prefix_len)
            row_max = jnp.max(scores, axis=-1, keepdims=True)
            exponent = jnp.exp(scores - row_max)
            row_total = jnp.sum(exponent, axis=-1, keepdims=True)
            attn_probs = (exponent / row_total).astype(jnp.bfloat16)
            result = jnp.einsum(
                "gqk,kgd->qgd", attn_probs, value_group, preferred_element_type=jnp.float32
            )
            return (result, (row_max + jnp.log(row_total))[..., 0])

        return lax.map(one_block, (query_blocks, starts))

    attended, log_totals = lax.map(
        one_group,
        (
            group_heads(query_heads, groups),
            group_heads(key_heads, groups),
            group_heads(value_heads, groups),
        ),
    )
    merged = (
        jnp.transpose(attended, (1, 2, 0, 3, 4))
        .reshape(token_count, HEADS * HEAD_DIM)
        .astype(jnp.bfloat16)
    )
    return (merged, log_totals)


def attend_backward(query_heads, key_heads, value_heads, grad_merged, log_totals, prefix_len):
    token_count = query_heads.shape[0]
    group_size = min(4, HEADS)
    groups = HEADS // group_size
    block_rows = min(512, token_count)
    blocks = token_count // block_rows
    starts = jnp.arange(blocks, dtype=jnp.int32) * block_rows
    score_scale = 1.0 / math.sqrt(HEAD_DIM)

    def one_group(group_item):
        query_group, key_group, value_group, grad_group, total_group = group_item
        query_blocks = query_group.reshape(blocks, block_rows, group_size, HEAD_DIM)
        grad_blocks = grad_group.reshape(blocks, block_rows, group_size, HEAD_DIM)

        def one_block(carry, block_item):
            grad_keys, grad_vals = carry
            query_block, grad_block, total_block, block_start = block_item
            scores = block_scores(query_block, key_group, block_start, prefix_len)
            attn_probs = jnp.exp(scores - total_block[..., None])
            grad_probs = jnp.einsum(
                "qgd,kgd->gqk", grad_block, value_group, preferred_element_type=jnp.float32
            )
            row_delta = jnp.sum(attn_probs * grad_probs, axis=-1, keepdims=True)
            grad_scores = (attn_probs * (grad_probs - row_delta)).astype(jnp.bfloat16)
            grad_vals = grad_vals + jnp.einsum(
                "gqk,qgd->kgd",
                attn_probs.astype(jnp.bfloat16),
                grad_block,
                preferred_element_type=jnp.float32,
            )
            grad_keys = (
                grad_keys
                + jnp.einsum(
                    "gqk,qgd->kgd", grad_scores, query_block, preferred_element_type=jnp.float32
                )
                * score_scale
            )
            grad_query = (
                jnp.einsum(
                    "gqk,kgd->qgd", grad_scores, key_group, preferred_element_type=jnp.float32
                )
                * score_scale
            )
            return ((grad_keys, grad_vals), grad_query)

        zero_keys = jnp.zeros(key_group.shape, jnp.float32)
        carried, grad_queries = lax.scan(
            one_block, (zero_keys, zero_keys), (query_blocks, grad_blocks, total_group, starts)
        )
        return (grad_queries, carried[0], carried[1])

    grad_queries, grad_keys, grad_vals = lax.map(
        one_group,
        (
            group_heads(query_heads, groups),
            group_heads(key_heads, groups),
            group_heads(value_heads, groups),
            group_heads(grad_merged, groups),
            log_totals,
        ),
    )
    query_part = jnp.transpose(grad_queries, (1, 2, 0, 3, 4)).reshape(token_count, HEADS * HEAD_DIM)
    key_part = jnp.transpose(grad_keys, (1, 0, 2, 3)).reshape(token_count, HEADS * HEAD_DIM)
    value_part = jnp.transpose(grad_vals, (1, 0, 2, 3)).reshape(token_count, HEADS * HEAD_DIM)
    return jnp.concatenate([query_part, key_part, value_part], axis=1).astype(jnp.bfloat16)


MESH = pl.DeviceIdType.MESH
LANES = 128


def dot_nn(left, right):
    return lax.dot_general(
        left, right, (((1,), (0,)), ((), ())), preferred_element_type=jnp.float32
    )


def dot_nt(left, right):
    return lax.dot_general(
        left, right, (((1,), (1,)), ((), ())), preferred_element_type=jnp.float32
    )


def dot_tn(left, right):
    return lax.dot_general(
        left, right, (((0,), (0,)), ((), ())), preferred_element_type=jnp.float32
    )


def span(start, size):
    return pl.ds(pl.multiple_of(start, size), size)


def every(start, stop, step):
    def body(i, carry):
        step(i)
        return carry

    lax.fori_loop(start, stop, body, 0)


class Place:
    def __init__(self, owners):
        self.owners = owners
        self.e = lax.axis_index("expert")
        self.w = lax.axis_index("wshard")
        self.c = lax.rem(self.w, 2)
        self.x = lax.div(self.w, 2)
        self.sib = self.w + 1 - 2 * self.c
        self.far = lax.rem(self.w + 2, 4)
        self.diag = 3 - self.w
        self.pair = self.e + 1 - 2 * lax.rem(self.e, 2)

    def ahead(self, k):
        return lax.rem(self.e + k, self.owners)

    def flip(self, bit):
        return self.e + bit * (1 - 2 * lax.rem(lax.div(self.e, bit), 2))

    def peer(self, n):
        other = lax.div(n, 2) + lax.rem(n, 2) * (self.owners // 2)
        result, bit = 0, 1
        while bit < self.owners:
            result = result + bit * lax.rem(lax.div(self.e, bit) + lax.div(other, bit), 2)
            bit *= 2
        return result


def remote(src, dst, send, recv, device):
    return pltpu.make_async_remote_copy(
        src_ref=src,
        dst_ref=dst,
        send_sem=send,
        recv_sem=recv,
        device_id=device,
        device_id_type=MESH,
    )


def greet(peers):
    barrier = pltpu.get_barrier_semaphore()
    for peer in peers:
        pl.semaphore_signal(barrier, inc=1, device_id=peer, device_id_type=MESH)
    pl.semaphore_wait(barrier, len(peers))


def either(test, yes, no):
    pl.when(test)(yes)
    pl.when(jnp.logical_not(test))(no)


class Dispatch:
    def __init__(self, place, capacity, send_ref, rows_ref, sems):
        self.p, self.cap, self.src, self.rows = place, capacity, send_ref, rows_ref
        self.own_sem, self.send, self.recv = sems

    def slice(self, k, core, side):
        start = (((lax.div(k, 2) * 2 + core) * 2 + side) * 2 + lax.rem(k, 2)) * self.cap
        return self.rows.at[:, span(start, self.cap)]

    def own(self):
        return pltpu.make_async_copy(
            self.src.at[self.p.e], self.slice(0, self.p.c, self.p.x), self.own_sem
        )

    def direct(self, k):
        return remote(
            self.src.at[self.p.peer(k)],
            self.slice(k, self.p.c, self.p.x),
            self.send.at[0, k],
            self.recv.at[0, k],
            (self.p.peer(k), self.p.w),
        )

    def hop(self, k, side, which, peer):
        part = self.slice(k, self.p.c, side)
        return remote(
            part, part, self.send.at[which, k], self.recv.at[which, k], (self.p.e, peer)
        )

    def to_sib(self, k):
        return self.hop(k, self.p.x, 1, self.p.sib)

    def to_far(self, k):
        return self.hop(k, self.p.x, 2, self.p.far)

    def relayed(self, k):
        return self.hop(k, 1 - self.p.x, 3, self.p.sib)

    def start(self):
        self.own().start()
        every(1, self.p.owners, lambda k: self.direct(k).start())

    def forward(self, k):
        k = jnp.int32(k)

        @pl.when(k == 0)
        def _():
            self.own().wait()

        @pl.when(k > 0)
        def _():
            self.direct(k).wait_recv()

        self.to_far(k).start()
        self.to_sib(k).start()

    def relay(self, k):
        self.to_far(k).wait_recv()
        self.relayed(k).start()

    def ready(self, k):
        self.to_sib(k).wait_recv()
        self.relayed(k).wait_recv()

    def order(self):
        return (0, 2, 4, 1, 6, 3, 5, 7)

    def drain(self):
        every(1, self.p.owners, lambda k: self.direct(k).wait_send())

        def rest(k):
            self.to_sib(k).wait_send()
            self.to_far(k).wait_send()
            self.relayed(k).wait_send()

        every(0, self.p.owners, rest)


class Return:
    def __init__(self, place, capacity, part, got, mid, far, done, home, sems):
        self.p, self.cap = place, capacity
        self.part, self.got, self.mid, self.far, self.done, self.home = (
            part, got, mid, far, done, home,
        )
        self.own_sem, self.send, self.recv, self.home_send, self.home_recv = sems

    def swapped(self, j, expert):
        size = 4 * self.cap
        return remote(
            self.part.at[expert, span((j * 2 + 1 - self.p.c) * size, size)],
            self.got.at[expert, span(j * size, size)],
            self.send.at[0, j, expert],
            self.recv.at[0, j, expert],
            (self.p.e, self.p.sib),
        )

    def crossed(self, j, expert):
        part = span(j * 2 * self.cap, 2 * self.cap)
        return remote(
            self.mid.at[expert, part],
            self.far.at[expert, part],
            self.send.at[1, j, expert],
            self.recv.at[1, j, expert],
            (self.p.e, self.p.far),
        )

    def own(self, expert):
        return pltpu.make_async_copy(
            self.done.at[0, expert], self.home.at[self.p.e, expert], self.own_sem.at[expert]
        )

    def homed(self, n, expert):
        return remote(
            self.done.at[n, expert],
            self.home.at[self.p.e, expert],
            self.home_send.at[n, expert],
            self.home_recv.at[n, expert],
            (self.p.peer(n), self.p.w),
        )

    def pair_sum(self, j, expert, side):
        size = 2 * self.cap
        mine = self.part[expert, span(((j * 2 + self.p.c) * 2 + side) * size, size), :]
        theirs = self.got[expert, span((j * 2 + side) * size, size), :]
        return mine.astype(jnp.float32) + theirs.astype(jnp.float32)

    def swap(self, j, expert):
        self.swapped(j, expert).start()

    def split(self, j, expert):
        self.swapped(j, expert).wait_recv()
        here = span(j * 2 * self.cap, 2 * self.cap)
        self.mid[expert, here, :] = self.pair_sum(j, expert, 1 - self.p.x).astype(jnp.bfloat16)
        self.keep[expert, here, :] = self.pair_sum(j, expert, self.p.x).astype(jnp.bfloat16)

    def cross(self, j, expert):
        self.swapped(j, expert).wait_recv()
        here = span(j * 2 * self.cap, 2 * self.cap)
        self.mid[expert, here, :] = self.pair_sum(j, expert, 1 - self.p.x).astype(jnp.bfloat16)
        self.crossed(j, expert).start()

    def this_side(self, j, expert):
        return self.pair_sum(j, expert, self.p.x)

    def finish(self, j, expert):
        self.crossed(j, expert).wait_recv()
        here = span(j * 2 * self.cap, 2 * self.cap)
        total = self.this_side(j, expert) + self.far[expert, here, :].astype(jnp.float32)
        total = total.astype(jnp.bfloat16)
        self.done[2 * j, expert] = total[: self.cap]
        self.done[2 * j + 1, expert] = total[self.cap :]
        j = jnp.int32(j)
        self.homed(2 * j + 1, expert).start()
        either(
            j == 0,
            lambda: self.own(expert).start(),
            lambda: self.homed(2 * j, expert).start(),
        )

    def drain_swaps(self, chunks, experts):
        for expert in range(experts):
            every(0, chunks, lambda j: self.swapped(j, expert).wait_send())

    def drain(self, first, last, experts):
        for expert in range(experts):
            every(first, last, lambda j: self.crossed(j, expert).wait_send())
            every(
                max(1, 2 * first), 2 * last, lambda n: self.homed(n, expert).wait_send()
            )

    def arrived(self, first, last, experts):
        for expert in range(experts):
            if first == 0 and last > 0:
                self.own(expert).wait()
            every(
                max(1, 2 * first), 2 * last, lambda n: self.homed(n, expert).wait_recv()
            )


class LateReturn(Return):
    def crossed(self, j, expert):
        part = span(j * 2 * self.cap, 2 * self.cap)
        return remote(
            self.mid.at[expert, part],
            self.far.at[expert, part],
            self.send.at[j, expert],
            self.recv.at[j, expert],
            (self.p.e, self.p.far),
        )

    def this_side(self, j, expert):
        here = span(j * 2 * self.cap, 2 * self.cap)
        return self.part[expert, here, :].astype(jnp.float32)


def gelu_pair(v):
    root = math.sqrt(2.0 / math.pi)
    square = v * v
    t = jnp.tanh(v * (root + (root * 0.044715) * square))
    half = 0.5 + 0.5 * t
    slope = half + (half * (1.0 - t)) * (v * (root + (3.0 * root * 0.044715) * square))
    return v * half, slope


def expert_kernel(
    dims,
    send_ref, grads_hbm, up_hbm, down_hbm, router_ref,
    far_sums, near_sums, home_out, home_grad, up_out, down_out, router_grad,
    rows, grads, scaled, hidden, pre, up, down, grad_up, grad_down,
    part_out, part_grad, got_out, got_grad, mid_out, mid_grad,
    keep_out, far_grad, far_out, done_grad, done_out,
    load_sem, own_sem, disp_send, disp_recv, red_send, red_recv, home_send, home_recv,
):
    owners, experts, capacity, width, units, expert_count = dims
    place = Place(owners)
    loads = [
        pltpu.make_async_copy(src, dst, load_sem.at[i])
        for i, (src, dst) in enumerate(
            [(up_hbm, up), (grads_hbm, grads), (down_hbm, down)]
        )
    ]
    for load in loads:
        load.start()
    greet(
        [(place.ahead(k), place.w) for k in range(1, owners)]
        + [(place.e, place.sib), (place.e, place.far)]
    )
    dispatch = Dispatch(
        place, capacity, send_ref, rows, (own_sem.at[0, 0], disp_send, disp_recv)
    )
    ret_grad = Return(
        place, capacity, part_grad, got_grad, mid_grad, far_grad, done_grad, home_grad,
        (own_sem.at[1], red_send.at[0], red_recv.at[0], home_send.at[0], home_recv.at[0]),
    )
    ret_out = Return(
        place, capacity, part_out, got_out, mid_out, far_out, done_out, home_out,
        (own_sem.at[2], red_send.at[1], red_recv.at[1], home_send.at[1], home_recv.at[1]),
    )
    dispatch.start()
    router_grad[...] = jnp.zeros_like(router_grad)
    tile = min(TILE, units)
    wide = min(TILE, width)
    chunks = owners // 2
    early = EARLY_CHUNKS
    size = 8 * capacity
    lane = lax.broadcasted_iota(jnp.int32, (size, LANES), 1)

    def compute(j, expert):
        here = span(j * size, size)
        logits = dot_nt(rows[expert, here, :], router_ref[...])
        logits = jnp.where(lane < expert_count, logits, -1e30)
        exponent = jnp.exp(logits - jnp.max(logits, axis=1, keepdims=True))
        prob = exponent * (1.0 / jnp.sum(exponent, axis=1, keepdims=True))
        mine = lane == place.e * experts + expert
        gate = jnp.sum(jnp.where(mine, prob, 0.0), axis=1, keepdims=True)
        scaled[expert, here, :] = (
            gate * grads[expert, here, :].astype(jnp.float32)
        ).astype(jnp.bfloat16)

        def one_tile(n):
            cols = span(n * tile, tile)
            value, slope = gelu_pair(dot_nn(rows[expert, here, :], up[expert, :, cols]))
            hidden[expert, here, cols] = value.astype(jnp.bfloat16)
            back = pre[expert, here, cols].astype(jnp.float32)
            pre[expert, here, cols] = (gate * back * slope).astype(jnp.bfloat16)

        every(0, units // tile, one_tile)

        def one_out(n, total):
            cols = span(n * wide, wide)
            value = dot_nn(hidden[expert, here, :], down[expert, :, cols])
            part_out[expert, here, cols] = (gate * value).astype(jnp.bfloat16)
            weighted = value * grads[expert, here, cols].astype(jnp.float32)
            for start in range(0, wide, LANES):
                total = total + weighted[:, start : start + LANES]
            return total

        total = lax.fori_loop(
            0, width // wide, one_out, jnp.zeros((size, LANES), jnp.float32)
        )
        grad_gate = jnp.sum(total, axis=1, keepdims=True)
        grad_logits = (
            prob * ((jnp.where(mine, 1.0, 0.0) - gate) * grad_gate)
        ).astype(jnp.bfloat16)

        def one_in(n):
            cols = span(n * wide, wide)
            value = dot_nt(pre[expert, here, :], up[expert, cols, :]) + dot_nn(
                grad_logits, router_ref[:, cols]
            )
            part_grad[expert, here, cols] = value.astype(jnp.bfloat16)
            router_grad[:, cols] += dot_tn(grad_logits, rows[expert, here, cols])

        every(0, width // wide, one_in)

    def unscaled(j, expert):
        here = span(j * size, size)
        pre[expert, here, :] = dot_nt(grads[expert, here, :], down[expert]).astype(jnp.bfloat16)

    block = min(256, width)

    def weight_grads(expert, first, last):
        def one(n):
            part = span(n * block, block)
            grad_down[expert, part, :] = dot_tn(
                hidden[expert, :, part], scaled[expert]
            ).astype(jnp.bfloat16)
            grad_up[expert, part, :] = dot_tn(rows[expert, :, part], pre[expert]).astype(
                jnp.bfloat16
            )

        every(first * width // block // 4, last * width // block // 4, one)

    def keep(expert):
        return [
            pltpu.make_async_copy(src.at[expert], dst.at[expert], load_sem.at[2 * expert + i])
            for i, (src, dst) in enumerate(((grad_up, up_out), (grad_down, down_out)))
        ]

    turns = [(j, expert) for j in range(chunks) for expert in range(experts)]
    ahead, through, here = dispatch.forward, dispatch.relay, dispatch.ready
    plan = [[] for _ in turns]
    for unit, acts in (
        (0, ((here, 0), (here, 1), (ahead, 5))),
        (1, ((through, 6), (ahead, 7))),
        (2, ((through, 3), (here, 2), (here, 3))),
        (3, ((through, 5),)),
        (4, ((through, 7), (here, 4), (here, 5))),
        (6, ((here, 6), (here, 7))),
    ):
        plan[unit].extend(acts)
    for u in range(2, len(turns)):
        done = turns[u - 2]
        plan[u].append((ret_grad.cross,) + done)
        plan[u].append((ret_out.cross if done[0] < early else ret_out.split,) + done)
        if u >= 4:
            done = turns[u - 4]
            plan[u].append((ret_grad.finish,) + done)
            if done[0] < early:
                plan[u].append((ret_out.finish,) + done)
    ret_out.keep = keep_out
    for load in loads:
        load.wait()

    def unscaled_pair(j):
        for expert in range(experts):
            unscaled(j, expert)

    ahead(0)
    unscaled_pair(0)
    unscaled_pair(1)
    ahead(2)
    ahead(4)
    ahead(1)
    unscaled_pair(2)
    through(0)
    unscaled_pair(3)
    through(2)
    ahead(6)
    through(4)
    through(1)
    ahead(3)

    def step(unit):
        for u, acts in enumerate(plan):

            @pl.when(unit == u)
            def _(acts=acts):
                for act, *at in acts:
                    act(*at)

        j, expert = lax.div(unit, experts), lax.rem(unit, experts)
        compute(j, expert)
        ret_grad.swap(j, expert)
        ret_out.swap(j, expert)

    every(0, len(turns), step)
    ret_grad.cross(*turns[-2])
    ret_out.split(*turns[-2])
    ret_grad.finish(*turns[-4])
    weight_grads(0, 0, 1)
    ret_grad.cross(*turns[-1])
    ret_out.split(*turns[-1])
    sums = [
        pltpu.make_async_copy(src, dst, load_sem.at[4 + i])
        for i, (src, dst) in enumerate(((mid_out, far_sums), (keep_out, near_sums)))
    ]
    for store in sums:
        store.start()
    ret_grad.finish(*turns[-3])
    weight_grads(0, 1, 2)
    ret_grad.finish(*turns[-2])
    weight_grads(0, 2, 3)
    ret_grad.finish(*turns[-1])
    weight_grads(0, 3, 4)
    for store in keep(0):
        store.start()
    for expert in range(1, experts):
        weight_grads(expert, 0, 4)
        for store in keep(expert):
            store.start()
    for expert in range(experts):
        for store in keep(expert):
            store.wait()
    for store in sums:
        store.wait()
    dispatch.drain()
    ret_grad.drain_swaps(chunks, experts)
    ret_grad.drain(0, chunks, experts)
    ret_grad.arrived(0, chunks, experts)
    ret_out.drain_swaps(chunks, experts)
    ret_out.drain(0, early, experts)
    ret_out.arrived(0, early, experts)


def run_experts(owners, capacity, expert_count, send_rows, grads, w_up, w_down, router):
    experts, width, units = w_up.shape
    slots = owners * 4 * capacity
    chunks = owners // 2
    dims = (owners, experts, capacity, width, units, expert_count)
    any_spec = pl.BlockSpec(memory_space=pl.ANY)
    vmem_spec = pl.BlockSpec(memory_space=pltpu.VMEM)
    bf16 = jnp.bfloat16
    home = jax.ShapeDtypeStruct((owners, experts, capacity, width), bf16)
    dma = pltpu.SemaphoreType.DMA

    def vm(*shape):
        return pltpu.VMEM(shape, bf16)

    return pl.pallas_call(
        functools.partial(expert_kernel, dims),
        out_shape=(
            jax.ShapeDtypeStruct((experts, slots // 4, width), bf16),
            jax.ShapeDtypeStruct((experts, slots // 4, width), bf16),
            home, home,
            jax.ShapeDtypeStruct(w_up.shape, bf16),
            jax.ShapeDtypeStruct(w_down.shape, bf16),
            jax.ShapeDtypeStruct((LANES, width), jnp.float32),
        ),
        in_specs=[any_spec] * 4 + [vmem_spec],
        out_specs=(any_spec,) * 6 + (vmem_spec,),
        scratch_shapes=[
            vm(experts, slots, width),
            vm(experts, slots, width),
            vm(experts, slots, width),
            vm(experts, slots, units),
            vm(experts, slots, units),
            vm(experts, width, units),
            vm(experts, units, width),
            vm(experts, width, units),
            vm(experts, units, width),
            vm(experts, slots, width),
            vm(experts, slots, width),
            vm(experts, slots // 2, width),
            vm(experts, slots // 2, width),
            vm(experts, slots // 4, width),
            vm(experts, slots // 4, width),
            vm(experts, slots // 4, width),
            vm(experts, slots // 4, width),
            vm(experts, slots // 4, width),
            vm(owners, experts, capacity, width),
            vm(owners, experts, capacity, width),
            dma((6,)),
            dma((3, experts)),
            dma((4, owners)),
            dma((4, owners)),
            dma((2, 2, chunks, experts)),
            dma((2, 2, chunks, experts)),
            dma((2, owners, experts)),
            dma((2, owners, experts)),
        ],
        compiler_params=pltpu.CompilerParams(
            collective_id=1, has_side_effects=True, vmem_limit_bytes=VMEM_LIMIT
        ),
        name="experts",
    )(send_rows, grads, w_up, w_down, router)


def masked_softmax(scores):
    exponent = jnp.exp(scores - jnp.max(scores, axis=1, keepdims=True))
    return exponent * (1.0 / jnp.sum(exponent, axis=1, keepdims=True))


def attend_head(query, key, value, prefix_len):
    half = query.shape[0] // 2
    query = query * (1.0 / math.sqrt(HEAD_DIM))
    row = lax.broadcasted_iota(jnp.int32, (half, half), 0)
    col = lax.broadcasted_iota(jnp.int32, (half, half), 1)
    low = dot_nt(query[:half], key[:half])
    low = jnp.where((col <= row) | (col < prefix_len), low, -1e30)
    low = masked_softmax(low).astype(jnp.bfloat16)
    high = dot_nt(query[half:], key)
    high = jnp.concatenate(
        [high[:, :half], jnp.where(col <= row, high[:, half:], -1e30)], axis=1
    )
    high = masked_softmax(high).astype(jnp.bfloat16)
    return low, high, dot_nn(low, value[:half]), dot_nn(high, value)


def score_grads(probs, grad_probs):
    probs = probs.astype(jnp.float32)
    weighted = probs * grad_probs
    total = jnp.sum(weighted, axis=1, keepdims=True)
    return (weighted - probs * total).astype(jnp.bfloat16)


def attend_back_head(query, key, value, low, high, grad):
    half = query.shape[0] // 2
    scale = 1.0 / math.sqrt(HEAD_DIM)
    query = query * scale
    grad_low = score_grads(low, dot_nt(grad[:half], value[:half]))
    grad_high = score_grads(high, dot_nt(grad[half:], value))
    grad_query = jnp.concatenate(
        [dot_nn(grad_low, key[:half]), dot_nn(grad_high, key)], axis=0
    )
    value_all = dot_tn(high, grad[half:])
    key_all = dot_tn(grad_high, query[half:])
    grad_value = jnp.concatenate(
        [value_all[:half] + dot_tn(low, grad[:half]), value_all[half:]], axis=0
    )
    grad_key = jnp.concatenate(
        [key_all[:half] + dot_tn(grad_low, query[:half]), key_all[half:]], axis=0
    )
    return (
        (grad_query * scale).astype(jnp.bfloat16),
        grad_key.astype(jnp.bfloat16),
        grad_value.astype(jnp.bfloat16),
    )


class Gather:
    def __init__(self, place, pieces, parts, src, dst, sems):
        self.p, self.src, self.dst, self.pieces, self.parts = place, src, dst, pieces, parts
        self.send, self.recv = sems
        self.shard = src.shape[0]
        self.half = self.shard // 2
        self.width = src.shape[1] // parts
        self.step = self.width // pieces
        self.first = lax.rem(place.e, 2) * self.half
        self.second = self.half - self.first

    def cols(self, n, part):
        return span(part * self.width + n * self.step, self.step)

    def block(self, owner, start, size, n, part):
        rows = pl.ds(pl.multiple_of(owner * self.shard + start, self.half), size)
        return self.dst.at[rows, self.cols(n, part)]

    def move(self, which, n, part, src, dst, device):
        return remote(
            src, dst, self.send.at[which, n, part], self.recv.at[which, n, part], device
        )

    def own(self, n, part):
        return pltpu.make_async_copy(
            self.src.at[:, self.cols(n, part)],
            self.block(self.p.w, 0, self.shard, n, part),
            self.recv.at[5, n, part],
        )

    def near(self, n, part):
        return self.move(
            4, n, part, self.src.at[:, self.cols(n, part)],
            self.block(self.p.w, 0, self.shard, n, part), (self.p.e, self.p.sib),
        )

    def hop(self, n, part):
        return self.move(
            0, n, part, self.src.at[span(self.first, self.half), self.cols(n, part)],
            self.block(self.p.w, self.first, self.half, n, part), (self.p.e, self.p.far),
        )

    def pass_from(self, which, start, n, part, device):
        block = self.block(self.p.far, start, self.half, n, part)
        return self.move(which, n, part, block, block, device)

    def pairs(self, n, part):
        return self.pass_from(1, self.first, n, part, (self.p.pair, self.p.w))

    def relay(self, n, part):
        return self.pass_from(2, self.first, n, part, (self.p.e, self.p.sib))

    def pair_relay(self, n, part):
        return self.pass_from(3, self.second, n, part, (self.p.e, self.p.sib))

    def all_parts(self, n, act):
        for part in range(self.parts):
            act(n, part)

    def start_own(self):
        every(
            0, self.pieces, lambda n: self.all_parts(n, lambda n, part: self.own(n, part).start())
        )

    def start(self):
        def hop(n, part):
            self.hop(n, part).start()

        def near(n, part):
            self.near(n, part).start()

        every(0, self.pieces, lambda n: self.all_parts(n, hop))
        every(0, self.pieces, lambda n: self.all_parts(n, near))

    def pass_on(self, n):
        def one(n, part):
            self.hop(n, part).wait_recv()
            self.pairs(n, part).start()
            self.relay(n, part).start()

        self.all_parts(n, one)

    def pass_pair(self, n):
        def one(n, part):
            self.pairs(n, part).wait_recv()
            self.pair_relay(n, part).start()

        self.all_parts(n, one)

    def ready(self, n):
        def one(n, part):
            self.own(n, part).wait()
            for copy in (self.near(n, part), self.relay(n, part), self.pair_relay(n, part)):
                copy.wait_recv()

        self.all_parts(n, one)

    def drain(self):
        def one(n, part):
            for copy in (
                self.hop(n, part), self.pairs(n, part), self.relay(n, part),
                self.pair_relay(n, part), self.near(n, part),
            ):
                copy.wait_send()

        every(0, self.pieces, lambda n: self.all_parts(n, one))


def slot_tables(routes_ref, priority_ref, capacity, pick_ref, back_ref):
    count = routes_ref.shape[1]
    row = lax.broadcasted_iota(jnp.int32, (count, count), 0).astype(jnp.float32)
    col = lax.broadcasted_iota(jnp.int32, (count, count), 1).astype(jnp.float32)
    eye = row == col
    route_row = routes_ref[...].astype(jnp.float32)
    order_row = priority_ref[...].astype(jnp.float32)
    route_col = jnp.sum(jnp.where(eye, route_row, 0.0), axis=1, keepdims=True)
    order_col = jnp.sum(jnp.where(eye, order_row, 0.0), axis=1, keepdims=True)
    same = route_col == route_row
    rank_row = jnp.sum(
        jnp.where(same & (order_col < order_row), 1.0, 0.0), axis=0, keepdims=True
    )
    rank_col = jnp.sum(
        jnp.where(same & (order_row < order_col), 1.0, 0.0), axis=1, keepdims=True
    )
    slots = float(count)
    slot_row = jnp.where(rank_row < capacity, route_row * capacity + rank_row, slots)
    slot_col = jnp.where(rank_col < capacity, route_col * capacity + rank_col, slots)
    pick_ref[...] = jnp.where(slot_row == row, 1.0, 0.0).astype(jnp.bfloat16)
    back_ref[...] = jnp.where(slot_col == col, 1.0, 0.0).astype(jnp.bfloat16)


def norm_stats(value):
    centered = value - jnp.mean(value, axis=1, keepdims=True)
    inverse = lax.rsqrt(jnp.mean(centered * centered, axis=1, keepdims=True) + epsilon)
    return centered * inverse, inverse


def front_kernel(
    dims,
    prefix_ref, routes_ref, priority_ref, gain_one_ref, shift_one_ref, gain_two_ref, shift_two_ref,
    tokens_hbm, cot_hbm, router_hbm, qkv_hbm, out_hbm,
    qkv_out, act_out, merged_out, back_out, weight_out, out_full, low_out, high_out, grads_rows,
    hidden_hbm, send_hbm, small_out, router_out,
    small_own, tokens_ref, cot_ref, hidden_ref, send_ref,
    small, weight, out_w, qkv, act, merged, act_two, turned, pick, back, grads_send, low_buf, high_buf,
    own_sem, disp_send, disp_recv, small_send, small_recv, gat_send, gat_recv, store_sem, prob_sem, first_sem,
):
    owners, capacity, pieces = dims
    place = Place(owners)
    firsts = [
        pltpu.make_async_copy(src, dst, first_sem.at[i])
        for i, (src, dst) in enumerate(((cot_hbm, cot_ref), (tokens_hbm, tokens_ref)))
    ]
    for load in firsts:
        load.start()
    small_own[...] = jnp.zeros_like(small_own)
    for i, vector_ref in enumerate((gain_one_ref, shift_one_ref, gain_two_ref, shift_two_ref)):
        small_own[i, :] = vector_ref[...]
    rows, width = tokens_ref.shape
    shard = qkv_hbm.shape[0]
    gathers = [
        Gather(place, pieces, parts, src, dst, (gat_send.at[i], gat_recv.at[i]))
        for i, (parts, src, dst) in enumerate(((3, qkv_hbm, weight), (1, out_hbm, out_w)))
    ]
    for gather in gathers:
        gather.start_own()
    vectors, gates = small_own.shape[0], router_hbm.shape[0]
    small_parts = [
        (small_own, small.at[place.w, pl.ds(0, vectors)]),
        (router_hbm, small.at[place.w, pl.ds(vectors, gates)]),
    ]
    own_smalls = [
        pltpu.make_async_copy(src, dst, own_sem.at[3 + i])
        for i, (src, dst) in enumerate(small_parts)
    ]
    for copy in own_smalls:
        copy.start()
    greet(
        [(place.ahead(k), place.w) for k in range(1, owners)]
        + [(place.e, place.sib), (place.e, place.far), (place.e, place.diag)]
    )
    smalls = [
        remote(src, dst, small_send.at[n, i], small_recv.at[n, i], (place.e, peer))
        for i, peer in enumerate((place.sib, place.far, place.diag))
        for n, (src, dst) in enumerate(small_parts)
    ]
    for copy in smalls:
        copy.start()
    for gather in gathers:
        gather.start()
    slot_tables(routes_ref, priority_ref, capacity, pick, back)
    tile = min(256, width)
    shape = grads_send.shape[:3]

    def to_slots(values_ref, slots_ref):
        def one(n):
            cols = span(n * tile, tile)
            value = dot_nn(pick[...], values_ref[:, cols]).astype(jnp.bfloat16)
            slots_ref[:, :, :, cols] = value.reshape(shape + (tile,))

        every(0, width // tile, one)

    firsts[0].wait()
    to_slots(cot_ref, grads_send)
    dispatch = Dispatch(
        place, capacity, grads_send, grads_rows, (own_sem.at[0], disp_send, disp_recv)
    )
    dispatch.start()
    for copy in own_smalls:
        copy.wait()
    for copy in smalls:
        copy.wait_recv()
    small_out[...] = small[:, :vectors, :]
    router_out[...] = jnp.zeros_like(router_out)
    router_out[:gates, :] = jnp.concatenate(
        [small[i, vectors:, :] for i in range(4)], axis=1
    )

    def vector(which):
        parts = [small[i, which : which + 1, :] for i in range(4)]
        return jnp.concatenate(parts, axis=1).astype(jnp.float32)

    band = min(64, rows)
    gain, shift = vector(0), vector(1)

    def norm_band(i):
        part = span(i * band, band)
        scaled, _ = norm_stats(tokens_ref[part, :].astype(jnp.float32))
        act[part, :] = (scaled * gain + shift).astype(jnp.bfloat16)

    def project(n):
        for part in range(3):
            cols = gathers[0].cols(n, part)
            qkv[:, cols] = dot_nn(act[...], weight[:, cols]).astype(jnp.bfloat16)

    gathers[0].pass_on(0)
    firsts[1].wait()
    every(0, rows // band, norm_band)
    turned[0] = act[...].T
    stores = [
        pltpu.make_async_copy(src, dst, store_sem.at[i])
        for i, (src, dst) in enumerate(
            [(qkv, qkv_out), (turned.at[0], act_out), (back, back_out), (weight, weight_out),
             (turned.at[1], merged_out), (out_w, out_full)]
        )
    ]
    for store in stores[1:3]:
        store.start()
    half = rows // 2
    pairs = width // LANES

    def keep_probs(i):
        slot = lax.rem(i, 2)
        return (
            pltpu.make_async_copy(
                low_buf.at[slot], low_out.at[pl.ds(2 * i, 2)], prob_sem.at[0, slot]
            ),
            pltpu.make_async_copy(
                high_buf.at[slot], high_out.at[pl.ds(2 * i, 2)], prob_sem.at[1, slot]
            ),
        )

    def attend_pair(i):
        slot = lax.rem(i, 2)

        @pl.when(i >= 2)
        def _():
            for copy in keep_probs(i - 2):
                copy.wait()

        query, key, value = (
            qkv[:, span(part * width + i * LANES, LANES)] for part in range(3)
        )
        tops, bottoms = [], []
        for head in range(2):
            part = slice(head * HEAD_DIM, (head + 1) * HEAD_DIM)
            low, high, top, bottom = attend_head(
                query[:, part], key[:, part], value[:, part], prefix_ref[0]
            )
            low_buf[slot, head] = low
            high_buf[slot, head] = high
            tops.append(top)
            bottoms.append(bottom)
        cols = span(i * LANES, LANES)
        merged[:half, cols] = jnp.concatenate(tops, axis=1).astype(jnp.bfloat16)
        merged[half:, cols] = jnp.concatenate(bottoms, axis=1).astype(jnp.bfloat16)
        for copy in keep_probs(i):
            copy.start()

    group = pairs // pieces
    share = -(-owners // pieces)

    def front_step(n):
        @pl.when(n + 1 < pieces)
        def _():
            gathers[0].pass_on(n + 1)

        gathers[0].pass_pair(n)
        for i, partner in enumerate(dispatch.order()):
            pl.when(n == i // share)(functools.partial(dispatch.forward, partner))
        gathers[0].ready(n)
        project(n)
        pl.when(n >= 2)(lambda: gathers[1].pass_on(n - 2))

        @pl.when(n == pieces - 1)
        def _():
            gathers[1].pass_on(pieces - 2)
            gathers[1].pass_pair(0)

        for i in range(group):
            attend_pair(n * group + i)

    every(0, pieces, front_step)
    gathers[1].pass_on(pieces - 1)
    every(1, pieces, gathers[1].pass_pair)
    turned[1] = merged[...].T
    for i in (0, 3, 4):
        stores[i].start()
    order = dispatch.order()
    dispatch.relay(order[0])
    every(0, pieces, gathers[1].ready)
    stores[5].start()
    gain_two, shift_two = vector(2), vector(3)
    band_two = min(128, rows)

    def middle(i):
        part = span(i * band_two, band_two)
        value = tokens_ref[part, :].astype(jnp.float32) + dot_nn(merged[part, :], out_w[...])
        hidden_ref[part, :] = value
        scaled, _ = norm_stats(value)
        act_two[part, :] = (scaled * gain_two + shift_two).astype(jnp.bfloat16)
        for n, partner in enumerate(order[1 : 1 + bands]):
            pl.when(i == n)(functools.partial(dispatch.relay, partner))

    bands = rows // band_two
    every(0, bands, middle)
    results = [
        pltpu.make_async_copy(src, dst, first_sem.at[2 + i])
        for i, (src, dst) in enumerate(((hidden_ref, hidden_hbm), (send_ref, send_hbm)))
    ]
    results[0].start()
    to_slots(act_two, send_ref)
    results[1].start()
    for partner in order[1 + bands :]:
        dispatch.relay(partner)
    for i in (pairs - 2, pairs - 1):
        for copy in keep_probs(i):
            copy.wait()
    every(0, owners, dispatch.ready)
    for store in stores + results:
        store.wait()
    for copy in smalls:
        copy.wait_send()
    for gather in gathers:
        gather.drain()
    dispatch.drain()


def run_front(
    owners, experts, capacity, prefix, routes, priority, vectors, tokens, cotangent, router, w_qkv, w_out
):
    rows, width = tokens.shape
    shard, columns = w_qkv.shape
    half = rows // 2
    heads = width // HEAD_DIM
    pieces = 4
    any_spec = pl.BlockSpec(memory_space=pl.ANY)
    vmem_spec = pl.BlockSpec(memory_space=pltpu.VMEM)
    bf16, f32 = jnp.bfloat16, jnp.float32
    dma = pltpu.SemaphoreType.DMA

    def out(*shape):
        return jax.ShapeDtypeStruct(shape, bf16)

    def vm(*shape):
        return pltpu.VMEM(shape, bf16)

    return pl.pallas_call(
        functools.partial(front_kernel, (owners, capacity, pieces)),
        out_shape=(
            out(rows, columns),
            out(width, rows),
            out(width, rows),
            out(rows, rows),
            out(4 * shard, columns),
            out(4 * shard, width),
            out(heads, half, half),
            out(heads, half, rows),
            out(experts, owners * 4 * capacity, width),
            jax.ShapeDtypeStruct((rows, width), f32),
            out(owners, experts, capacity, width),
            out(4, 16, shard),
            out(LANES, width),
        ),
        in_specs=[pl.BlockSpec(memory_space=pltpu.SMEM)] + [vmem_spec] * 6 + [any_spec] * 5,
        out_specs=(any_spec,) * 11 + (vmem_spec,) * 2,
        scratch_shapes=[
            vm(16, shard),
            vm(rows, width),
            vm(rows, width),
            pltpu.VMEM((rows, width), f32),
            vm(owners, experts, capacity, width),
            vm(4, 16 + router.shape[0], shard),
            vm(4 * shard, columns),
            vm(4 * shard, width),
            vm(rows, columns),
            vm(rows, width),
            vm(rows, width),
            vm(rows, width),
            vm(2, width, rows),
            vm(rows, rows),
            vm(rows, rows),
            vm(owners, experts, capacity, width),
            vm(2, 2, half, half),
            vm(2, 2, half, rows),
            dma((5,)),
            dma((4, owners)),
            dma((4, owners)),
            dma((2, 3)),
            dma((2, 3)),
            dma((2, 6, pieces, 3)),
            dma((2, 6, pieces, 3)),
            dma((6,)),
            dma((2, 2)),
            dma((4,)),
        ],
        compiler_params=pltpu.CompilerParams(
            collective_id=0, has_side_effects=True, vmem_limit_bytes=VMEM_LIMIT
        ),
        name="front",
    )(prefix, routes, priority, *vectors, tokens, cotangent, router, w_qkv, w_out)


class Reduce:
    def __init__(self, place, part, got, far, pair, near, line, done, sems):
        self.p = place
        self.part, self.got, self.far = part, got, far
        self.pair, self.near, self.line, self.done = pair, near, line, done
        self.send, self.recv = sems
        self.chunks = part.shape[0]
        self.halves = done.shape[1] // 2
        self.bit = lax.rem(place.e, 2)
        self.low = lax.rem(lax.div(place.e, 2), 2)
        self.high = lax.div(place.e, 4)

    def step(self, which, n, src, dst, device):
        return remote(src, dst, self.send.at[which, n], self.recv.at[which, n], device)

    def swapped(self, n):
        return self.step(
            0, n, self.part.at[n, :, 1 - self.p.c], self.got.at[n], (self.p.e, self.p.sib)
        )

    def crossed(self, n):
        return self.step(
            1, n, self.part.at[n, 1 - self.p.x, self.p.c], self.far.at[n], (self.p.e, self.p.far)
        )

    def folded(self, n):
        other = span((1 - self.bit) * self.halves, self.halves)
        return self.step(
            2, n, self.part.at[n, self.p.x, self.p.c, other], self.pair.at[n],
            (self.p.pair, self.p.w),
        )

    def shared(self, n):
        part = self.done.at[n, span(self.bit * self.halves, self.halves)]
        return self.step(3, n, part, part, (self.p.pair, self.p.w))

    def quarter(self, low):
        size = self.halves // 2
        return span(self.bit * self.halves + low * size, size)

    def eighth(self, high):
        size = self.halves // 4
        return span(self.bit * self.halves + (self.low * 2 + high) * size, size)

    def nears(self, n):
        return self.step(
            4, n, self.part.at[n, self.p.x, self.p.c, self.quarter(1 - self.low)],
            self.near.at[n], (self.p.flip(2), self.p.w),
        )

    def lines(self, n):
        return self.step(
            5, n, self.part.at[n, self.p.x, self.p.c, self.eighth(1 - self.high)],
            self.line.at[n], (self.p.flip(4), self.p.w),
        )

    def line_back(self, n):
        part = self.done.at[n, self.eighth(self.high)]
        return self.step(6, n, part, part, (self.p.flip(4), self.p.w))

    def near_back(self, n):
        part = self.done.at[n, self.quarter(self.low)]
        return self.step(7, n, part, part, (self.p.flip(2), self.p.w))

    def add(self, n, rows, other):
        total = self.part[n, self.p.x, self.p.c, rows, :].astype(jnp.float32) + other.astype(
            jnp.float32
        )
        return total.astype(jnp.bfloat16)

    def pair_sum(self, n, side):
        return self.part[n, side, self.p.c].astype(jnp.float32) + self.got[n, side].astype(
            jnp.float32
        )

    def swap(self, n):
        self.swapped(n).start()

    def cross(self, n):
        self.swapped(n).wait_recv()
        side = 1 - self.p.x
        self.part[n, side, self.p.c] = self.pair_sum(n, side).astype(jnp.bfloat16)
        self.crossed(n).start()

    def fold(self, n):
        self.crossed(n).wait_recv()
        total = self.pair_sum(n, self.p.x) + self.far[n].astype(jnp.float32)
        self.part[n, self.p.x, self.p.c] = total.astype(jnp.bfloat16)
        self.folded(n).start()

    def spread(self, n):
        self.folded(n).wait_recv()
        own = span(self.bit * self.halves, self.halves)
        self.part[n, self.p.x, self.p.c, own, :] = self.add(n, own, self.pair[n])
        self.nears(n).start()

    def reach(self, n):
        self.nears(n).wait_recv()
        own = self.quarter(self.low)
        self.part[n, self.p.x, self.p.c, own, :] = self.add(n, own, self.near[n])
        self.lines(n).start()

    def collect(self, n):
        self.lines(n).wait_recv()
        own = self.eighth(self.high)
        self.done[n, own, :] = self.add(n, own, self.line[n])
        self.line_back(n).start()

    def widen_back(self, n):
        self.line_back(n).wait_recv()
        self.near_back(n).start()

    def share(self, n):
        self.near_back(n).wait_recv()
        self.shared(n).start()

    def finish(self, n):
        self.shared(n).wait_recv()

    def line_stages(self):
        return (self.spread, self.reach, self.collect, self.widen_back, self.share, self.finish)

    def stages(self):
        return (self.cross, self.fold) + self.line_stages()

    def drain(self):
        def one(n):
            for copy in (
                self.swapped(n), self.crossed(n), self.folded(n), self.shared(n), self.nears(n),
                self.lines(n), self.line_back(n), self.near_back(n),
            ):
                copy.wait_send()

        every(0, self.chunks, one)


class PairFirst(Reduce):
    def folded(self, n):
        other = span((1 - self.bit) * self.halves, self.halves)
        return self.step(
            2, n, self.part.at[n, :, self.p.c, other], self.pair.at[n], (self.p.pair, self.p.w)
        )

    def crossed(self, n):
        own = span(self.bit * self.halves, self.halves)
        return self.step(
            1, n, self.part.at[n, 1 - self.p.x, self.p.c, own], self.far.at[n],
            (self.p.e, self.p.far),
        )

    def fold(self, n):
        self.swapped(n).wait_recv()
        for side in range(2):
            self.part[n, side, self.p.c] = self.pair_sum(n, side).astype(jnp.bfloat16)
        self.folded(n).start()

    def cross(self, n):
        self.folded(n).wait_recv()
        own = span(self.bit * self.halves, self.halves)
        for side in range(2):
            total = self.part[n, side, self.p.c, own, :].astype(jnp.float32) + self.pair[
                n, side
            ].astype(jnp.float32)
            self.part[n, side, self.p.c, own, :] = total.astype(jnp.bfloat16)
        self.crossed(n).start()

    def spread(self, n):
        self.crossed(n).wait_recv()
        own = span(self.bit * self.halves, self.halves)
        self.part[n, self.p.x, self.p.c, own, :] = self.add(n, own, self.far[n])
        self.nears(n).start()

    def stages(self):
        return (self.fold, self.cross) + self.line_stages()


class Small:
    def __init__(self, place, value, part, got, mid, far, total, others, out, sems):
        self.p, self.value, self.part, self.got, self.mid = place, value, part, got, mid
        self.far, self.total, self.others, self.out = far, total, others, out
        self.send, self.recv, self.all_send, self.all_recv = sems

    def swapped(self):
        return remote(
            self.part.at[:, 1 - self.p.c], self.got, self.send.at[0], self.recv.at[0],
            (self.p.e, self.p.sib),
        )

    def crossed(self):
        return remote(
            self.mid, self.far, self.send.at[1], self.recv.at[1], (self.p.e, self.p.far)
        )

    def spreads(self, k):
        return remote(
            self.total, self.others.at[k], self.all_send.at[k], self.all_recv.at[k],
            (self.p.ahead(k), self.p.w),
        )

    def swap(self):
        size = self.part.shape[-1]
        for owner in range(4):
            self.part[owner // 2, owner % 2] = self.value[:, owner * size : (owner + 1) * size]
        self.swapped().start()

    def cross(self):
        self.swapped().wait_recv()
        self.mid[...] = self.part[1 - self.p.x, self.p.c] + self.got[1 - self.p.x]
        self.crossed().start()

    def spread(self):
        self.crossed().wait_recv()
        self.total[...] = self.part[self.p.x, self.p.c] + self.got[self.p.x] + self.far[...]
        for k in range(1, self.p.owners):
            self.spreads(k).start()

    def finish(self):
        total = self.total[...]
        for k in range(1, self.p.owners):
            self.spreads(k).wait_recv()
            total = total + self.others[k]
        vectors_out, gates_out = self.out
        vectors_out[...] = total[: vectors_out.shape[0]]
        gates_out[...] = total[vectors_out.shape[0] :]

    def drain(self):
        self.swapped().wait_send()
        self.crossed().wait_send()
        for k in range(1, self.p.owners):
            self.spreads(k).wait_send()


def norm_back_rows(grad, scaled, inverse, gain):
    weighted = grad * gain
    mean_one = jnp.mean(weighted, axis=1, keepdims=True)
    mean_two = jnp.mean(weighted * scaled, axis=1, keepdims=True)
    return inverse * (weighted - mean_one - scaled * mean_two)


def back_kernel(
    dims,
    home_grad_hbm, back_hbm, hidden_hbm, cot_hbm, tokens_hbm, vectors_ref, router_ref,
    far_hbm, near_hbm, home_hbm, act_hbm, merged_hbm, qkv_hbm, weight_hbm, out_hbm, low_hbm, high_hbm,
    output_hbm, grad_tokens_hbm, vectors_out, gates_out, qkv_out, out_out,
    home_grad_ref, back_ref, hidden_ref, cot_ref, tokens_ref, output_ref, tokens_out,
    near_sums, far_sums, done_rows, home_out,
    act_t, merged_t, qkv, weight, out_w, low_buf, high_buf, attn, grad_merged, grad_act,
    part_q, got_q, far_q, pair_q, near_q, line_q, done_q,
    part_o, got_o, far_o, pair_o, near_o, line_o, done_o,
    small, small_part, small_got, small_mid, small_far, small_sum, small_all,
    first_sem, load_sem, prob_sem, own_sem, early_sem, cross_send, cross_recv, home_send, home_recv, send_q, recv_q, send_o, recv_o,
    small_send, small_recv, all_send, all_recv, out_sem,
):
    owners, capacity, gates = dims
    grad_qkv = qkv
    place = Place(owners)
    loads = [
        pltpu.make_async_copy(src, dst, load_sem.at[i])
        for i, (src, dst) in enumerate(
            [(merged_hbm, merged_t), (out_hbm, out_w), (qkv_hbm, qkv), (act_hbm, act_t),
             (weight_hbm, weight), (near_hbm, near_sums)]
        )
    ]

    def load_probs(i):
        slot = lax.rem(i, 2)
        return (
            pltpu.make_async_copy(
                low_hbm.at[pl.ds(2 * i, 2)], low_buf.at[slot], prob_sem.at[0, slot]
            ),
            pltpu.make_async_copy(
                high_hbm.at[pl.ds(2 * i, 2)], high_buf.at[slot], prob_sem.at[1, slot]
            ),
        )

    firsts = [
        pltpu.make_async_copy(src, dst, first_sem.at[i])
        for i, (src, dst) in enumerate(
            [(home_grad_hbm, home_grad_ref), (back_hbm, back_ref), (hidden_hbm, hidden_ref),
             (cot_hbm, cot_ref), (tokens_hbm, tokens_ref)]
        )
    ]
    results = [
        pltpu.make_async_copy(src, dst, first_sem.at[5 + i])
        for i, (src, dst) in enumerate([(tokens_out, grad_tokens_hbm), (output_ref, output_hbm)])
    ]
    for load in firsts[:4] + loads + firsts[4:]:
        load.start()
    for load in load_probs(0):
        load.start()
    greet(
        [(place.ahead(k), place.w) for k in range(1, owners)]
        + [(place.e, place.sib), (place.e, place.far)]
    )
    experts = near_sums.shape[0]
    groups = owners // 2
    late = LateReturn(
        place, capacity, near_sums, None, far_hbm, far_sums, done_rows, home_out,
        (own_sem, cross_send, cross_recv, home_send, home_recv),
    )

    def start_late(j):
        for expert in range(experts):
            late.crossed(j, expert).start()

    every(EARLY_CHUNKS, groups, start_late)

    def early_rows(n):
        row = place.peer(n)
        return pltpu.make_async_copy(home_hbm.at[row], home_out.at[row], early_sem.at[n])

    every(0, 2 * EARLY_CHUNKS, lambda n: early_rows(n).start())
    reduce_o = PairFirst(
        place, part_o, got_o, far_o, pair_o, near_o, line_o, done_o, (send_o, recv_o)
    )
    reduce_q = Reduce(
        place, part_q, got_q, far_q, pair_q, near_q, line_q, done_q, (send_q, recv_q)
    )
    smalls = Small(
        place, small, small_part, small_got, small_mid, small_far, small_sum, small_all, (vectors_out, gates_out),
        (small_send, small_recv, all_send, all_recv),
    )
    rows, width = tokens_ref.shape
    shard = width // 4
    band = min(128, rows)
    lead = small.shape[0]

    def vector(which):
        parts = [vectors_ref[i, which : which + 1, :] for i in range(4)]
        return jnp.concatenate(parts, axis=1).astype(jnp.float32)

    gain_one, gain_two = vector(0), vector(2)
    small[: lead - gates, :] = jnp.zeros((lead - gates, width), jnp.float32)
    small[lead - gates :, :] = router_ref[:gates, :]

    def post(i):
        part = span(i * band, band)
        grad = dot_nn(back_ref[part, :], home_grad_ref.reshape(rows, width)[...])
        scaled, inverse = norm_stats(hidden_ref[part, :])
        value = cot_ref[part, :].astype(jnp.float32) + norm_back_rows(
            grad, scaled, inverse, gain_two
        )
        tokens_out[part, :] = value
        attn[part, :] = value.astype(jnp.bfloat16)
        small[2:3, :] += jnp.sum(grad * scaled, axis=0, keepdims=True)
        small[3:4, :] += jnp.sum(grad, axis=0, keepdims=True)

    for load in firsts[:4]:
        load.wait()
    every(0, rows // band, post)
    loads[0].wait()

    def weight_grad(part, n, left, right):
        value = dot_nn(left[...], right).astype(jnp.bfloat16)
        part[n] = value.reshape(part.shape[1:])

    tile_o = part_o.shape[-1]
    out_chunks = part_o.shape[0]
    for n in range(out_chunks):
        weight_grad(part_o, n, merged_t, attn[:, n * tile_o : (n + 1) * tile_o])
        reduce_o.swap(n)
    loads[1].wait()

    def merged_band(i):
        part = span(i * band, band)
        grad_merged[part, :] = dot_nt(attn[part, :], out_w[...]).astype(jnp.bfloat16)

    every(0, rows // band, merged_band)
    stages_o, stages_q = reduce_o.stages(), reduce_q.stages()
    for n in range(out_chunks):
        stages_o[0](n)
    for load in loads[2:] + firsts[4:]:
        load.wait()
    grad_act[...] = jnp.zeros_like(grad_act)
    pairs = part_q.shape[0]

    def attend_pair(i):
        slot = lax.rem(i, 2)
        for load in load_probs(i):
            load.wait()

        @pl.when(i + 1 < pairs)
        def _():
            for load in load_probs(i + 1):
                load.start()

        cols = span(i * LANES, LANES)
        query, key, value = (
            qkv[:, span(part * width + i * LANES, LANES)] for part in range(3)
        )
        grad = grad_merged[:, cols]
        results = []
        for head in range(2):
            part = slice(head * HEAD_DIM, (head + 1) * HEAD_DIM)
            results.append(
                attend_back_head(
                    query[:, part], key[:, part], value[:, part],
                    low_buf[slot, head], high_buf[slot, head], grad[:, part],
                )
            )
        for which in range(3):
            grad_qkv[:, span(which * width + i * LANES, LANES)] = jnp.concatenate(
                [results[0][which], results[1][which]], axis=1
            )
        right = jnp.concatenate(
            [grad_qkv[:, span(which * width + i * LANES, LANES)] for which in range(3)], axis=1
        )
        weight_grad(part_q, i, act_t, right)
        reduce_q.swap(i)
        columns = jnp.concatenate(
            [weight[:, span(which * width + i * LANES, LANES)] for which in range(3)], axis=1
        )
        grad_act[...] += dot_nt(right, columns)

    def input_band(i):
        part = span(i * band, band)
        grad = grad_act[part, :]
        scaled, inverse = norm_stats(tokens_ref[part, :].astype(jnp.float32))
        tokens_out[part, :] += norm_back_rows(grad, scaled, inverse, gain_one)
        small[0:1, :] += jnp.sum(grad * scaled, axis=0, keepdims=True)
        small[1:2, :] += jnp.sum(grad, axis=0, keepdims=True)

    def output_band(i):
        part = span(i * band, band)
        slots = home_out.reshape(rows, width)
        value = hidden_ref[part, :] + dot_nn(back_ref[part, :], slots[...])
        output_ref[part, :] = value.astype(jnp.bfloat16)

    def store_q(i):
        return [
            pltpu.make_async_copy(
                done_q.at[i, :, pl.ds(which * LANES, LANES)],
                qkv_out.at[:, span(which * width + i * LANES, LANES)],
                out_sem.at[which, i],
            )
            for which in range(3)
        ]

    def store_o(n):
        return pltpu.make_async_copy(
            done_o.at[n], out_out.at[:, span(n * tile_o, tile_o)], out_sem.at[3, n]
        )

    delays = (1, 3, 4, 5, 6, 7, 8, 9)
    turns_o = (-1, 3, 5, 6, 7, 8, 9, 10)
    last = len(delays) - 1
    half = rows // band // 2

    def slot_step(slot):
        @pl.when(slot + EARLY_CHUNKS < groups)
        def _():
            for expert in range(experts):
                late.finish(slot + EARLY_CHUNKS, expert)

        pl.when(slot < pairs)(lambda: attend_pair(slot))
        for s in range(last, -1, -1):
            n = slot - delays[s]

            @pl.when((n >= 0) & (n < pairs))
            def _(s=s, n=n):
                stages_q[s](n)
                if s == last:
                    for copy in store_q(n):
                        copy.start()

            @pl.when(slot == turns_o[s])
            def _(s=s):
                for n in range(out_chunks):
                    stages_o[s](n)
                    if s == last:
                        store_o(n).start()

        @pl.when(slot == pairs)
        def _():
            every(0, half, input_band)

        @pl.when(slot == pairs + 1)
        def _():
            every(half, 2 * half, input_band)
            results[0].start()

        pl.when(slot == pairs + 2)(smalls.swap)
        pl.when(slot == pairs + 3)(smalls.cross)
        pl.when(slot == pairs + 4)(smalls.spread)

        @pl.when(slot == pairs + 3)
        def _():
            late.arrived(EARLY_CHUNKS, groups, experts)
            every(0, 2 * EARLY_CHUNKS, lambda n: early_rows(n).wait())
            every(0, rows // band, output_band)
            results[1].start()

    every(0, pairs + delays[-1], slot_step)
    smalls.finish()

    def stored(i):
        for copy in store_q(i):
            copy.wait()

    every(0, pairs, stored)
    for result in results:
        result.wait()
    for n in range(out_chunks):
        store_o(n).wait()
    late.drain(EARLY_CHUNKS, groups, experts)
    reduce_o.drain()
    reduce_q.drain()
    smalls.drain()


def run_back(
    owners, capacity, gates, home_grad, far_sums, near_sums, home_out, back, hidden, cotangent, tokens,
    vectors, router_grad, act_t, merged_t, qkv, weight, w_out, low, high,
):
    rows, width = tokens.shape
    shard = width // 4
    lead = 8 + gates
    groups = owners // 2
    pairs = width // LANES
    tile_o = min(512, width)
    out_chunks = width // tile_o
    half = shard // 2
    mid = rows // 2
    any_spec = pl.BlockSpec(memory_space=pl.ANY)
    vmem_spec = pl.BlockSpec(memory_space=pltpu.VMEM)
    bf16, f32 = jnp.bfloat16, jnp.float32
    dma = pltpu.SemaphoreType.DMA

    def vm(*shape):
        return pltpu.VMEM(shape, bf16)

    def fm(*shape):
        return pltpu.VMEM(shape, f32)

    def reduce_buffers(chunks, tile, pair_first):
        far, pair = ((half,), (2, half)) if pair_first else ((shard,), (half,))
        return [
            vm(chunks, 2, 2, shard, tile),
            vm(chunks, 2, shard, tile),
            vm(chunks, *far, tile),
            vm(chunks, *pair, tile),
            vm(chunks, half // 2, tile),
            vm(chunks, half // 4, tile),
            vm(chunks, shard, tile),
        ]

    def reduce_sems(chunks):
        return [dma((8, chunks)), dma((8, chunks))]

    return pl.pallas_call(
        functools.partial(back_kernel, (owners, capacity, gates)),
        out_shape=(
            jax.ShapeDtypeStruct((rows, width), bf16),
            jax.ShapeDtypeStruct((rows, width), f32),
            jax.ShapeDtypeStruct((8, shard), f32),
            jax.ShapeDtypeStruct((gates, shard), f32),
            jax.ShapeDtypeStruct((shard, 3 * width), bf16),
            jax.ShapeDtypeStruct((shard, width), bf16),
        ),
        in_specs=[any_spec] * 5 + [vmem_spec] * 2 + [any_spec] * 10,
        out_specs=(any_spec,) * 2 + (vmem_spec,) * 2 + (any_spec,) * 2,
        scratch_shapes=[
            vm(*home_grad.shape),
            vm(rows, rows),
            fm(rows, width),
            vm(rows, width),
            vm(rows, width),
            vm(rows, width),
            fm(rows, width),
            vm(*near_sums.shape),
            vm(*near_sums.shape),
            vm(*home_grad.shape),
            vm(*home_grad.shape),
            vm(width, rows),
            vm(width, rows),
            vm(rows, 3 * width),
            vm(width, 3 * width),
            vm(width, width),
            vm(2, 2, mid, mid),
            vm(2, 2, mid, rows),
            vm(rows, width),
            vm(rows, width),
            fm(rows, width),
        ]
        + reduce_buffers(pairs, 3 * LANES, False)
        + reduce_buffers(out_chunks, tile_o, True)
        + [
            fm(lead, width),
            fm(2, 2, lead, shard),
            fm(2, lead, shard),
            fm(lead, shard),
            fm(lead, shard),
            fm(lead, shard),
            fm(owners, lead, shard),
            dma((7,)),
            dma((6,)),
            dma((2, 2)),
            dma((near_sums.shape[0],)),
            dma((owners,)),
            dma((groups, near_sums.shape[0])),
            dma((groups, near_sums.shape[0])),
            dma((owners, near_sums.shape[0])),
            dma((owners, near_sums.shape[0])),
        ]
        + reduce_sems(pairs)
        + reduce_sems(out_chunks)
        + [dma((2,)), dma((2,)), dma((owners,)), dma((owners,)), dma((4, pairs))],
        compiler_params=pltpu.CompilerParams(
            collective_id=2, has_side_effects=True, vmem_limit_bytes=VMEM_LIMIT
        ),
        name="back",
    )(
        home_grad, back, hidden, cotangent, tokens, vectors, router_grad,
        far_sums, near_sums, home_out, act_t, merged_t, qkv, weight, w_out, low, high,
    )


def widen_kernel(vectors_ref, *refs):
    count = (len(refs) - 4) // 2
    for src, dst in zip(refs[:count], refs[count:]):
        dst[...] = src[...].astype(dst.dtype)
    for i, dst in enumerate(refs[2 * count :]):
        dst[...] = vectors_ref[i, :]


def widen(steps, vectors, values, kinds):
    def spec(value):
        if value.shape[0] % (16 * steps):
            return pl.BlockSpec(value.shape, lambda i: (0, 0))
        return pl.BlockSpec((value.shape[0] // steps, value.shape[1]), lambda i: (i, 0))

    return pl.pallas_call(
        widen_kernel,
        grid=(steps,),
        in_specs=[pl.BlockSpec(vectors.shape, lambda i: (0, 0))]
        + [spec(value) for value in values],
        out_specs=[spec(value) for value in values]
        + [pl.BlockSpec((vectors.shape[1],), lambda i: (0,))] * 4,
        out_shape=[
            jax.ShapeDtypeStruct(value.shape, kind) for value, kind in zip(values, kinds)
        ]
        + [jax.ShapeDtypeStruct((vectors.shape[1],), jnp.float32)] * 4,
        name="widen",
    )(vectors, *values)


def on_device_plain(
    tokens,
    norm1_gain,
    norm1_shift,
    w_qkv,
    w_out,
    norm2_gain,
    norm2_shift,
    w_router,
    w_up,
    w_down,
    routes,
    priority,
    prefix,
    cotangent,
):
    row_count, model_width = tokens.shape
    expert_count = w_router.shape[1]
    capacity = row_count // expert_count
    owners = lax.axis_size("expert")
    local_experts = w_up.shape[0]
    slot_count = expert_count * capacity
    prefix_len = prefix[0]
    small = jnp.concatenate(
        [
            norm1_gain[None],
            norm1_shift[None],
            norm2_gain[None],
            norm2_shift[None],
            w_router.T,
        ],
        axis=0,
    )
    qkv_full = lax.all_gather(w_qkv, "wshard", axis=0, tiled=True)
    small_full = lax.all_gather(small, "wshard", axis=1, tiled=True)
    out_full = lax.all_gather(w_out, "wshard", axis=0, tiled=True)
    gain_one, shift_one, gain_two, shift_two = (small_full[i] for i in range(4))
    router_full = small_full[4:].T
    gain_one = gain_one.astype(jnp.float32)
    gain_two = gain_two.astype(jnp.float32)
    inputs = tokens.astype(jnp.float32)
    normed_one, scaled_one, inverse_one = normalize(inputs, gain_one, shift_one.astype(jnp.float32))
    act_one = normed_one.astype(jnp.bfloat16)
    qkv = jnp.dot(act_one, qkv_full, preferred_element_type=jnp.float32).astype(jnp.bfloat16)
    query_heads = qkv[:, :model_width]
    key_heads = qkv[:, model_width : 2 * model_width]
    value_heads = qkv[:, 2 * model_width :]
    merged, log_totals = attend_forward(query_heads, key_heads, value_heads, prefix_len)
    attn_out = jnp.dot(merged, out_full, preferred_element_type=jnp.float32)
    hidden = inputs + attn_out
    normed_two, scaled_two, inverse_two = normalize(hidden, gain_two, shift_two.astype(jnp.float32))
    act_two = normed_two.astype(jnp.bfloat16)
    logits = jnp.dot(act_two, router_full, preferred_element_type=jnp.float32)
    row_max = jnp.max(logits, axis=-1, keepdims=True)
    exponent = jnp.exp(logits - row_max)
    gate_prob = exponent / jnp.sum(exponent, axis=-1, keepdims=True)
    route_ids = routes[:, 0]
    chosen = route_ids[:, None] == jnp.arange(expert_count, dtype=jnp.int32)[None, :]
    gate_value = jnp.sum(jnp.where(chosen, gate_prob, 0.0), axis=1)
    slot_index, slot_source = assign_slots(route_ids, priority[0], expert_count, capacity)
    zero_row = jnp.zeros((1, model_width), jnp.bfloat16)
    padded = jnp.concatenate([act_two, zero_row], axis=0)
    send_rows = padded[slot_source].reshape(owners, local_experts * capacity, model_width)
    arrived = lax.all_to_all(send_rows, "expert", split_axis=0, concat_axis=0, tiled=True).reshape(
        owners, local_experts, capacity, model_width
    )
    group = lax.axis_size("wshard")
    local_rows = owners * capacity

    def by_expert(chunk):
        rows = jnp.transpose(chunk, (1, 0, 2, 3)).reshape(local_experts, local_rows, model_width)
        return lax.all_gather(rows, "wshard", axis=1, tiled=True)

    def home_rows(rows):
        own = lax.psum_scatter(rows.astype(jnp.bfloat16), "wshard", scatter_dimension=1, tiled=True)
        own = own.reshape(local_experts, owners, capacity, model_width)
        return jnp.transpose(own, (1, 0, 2, 3)).reshape(
            owners, local_experts * capacity, model_width
        )

    grad_output = cotangent.astype(jnp.float32)
    grad_combined = (gate_value[:, None] * grad_output).astype(jnp.bfloat16)
    grad_padded = jnp.concatenate([grad_combined, zero_row], axis=0)
    grad_send = grad_padded[slot_source].reshape(owners, local_experts * capacity, model_width)
    grad_arrived = lax.all_to_all(
        grad_send, "expert", split_axis=0, concat_axis=0, tiled=True
    ).reshape(owners, local_experts, capacity, model_width)
    rows_in = by_expert(arrived)
    grad_rows = by_expert(grad_arrived)
    pre_act = jnp.einsum("erd,edf->erf", rows_in, w_up, preferred_element_type=jnp.float32)
    activated, gelu_pull = jax.vjp(gelu_tanh, pre_act)
    act_hidden = activated.astype(jnp.bfloat16)
    produced = jnp.einsum(
        "erf,efd->erd", act_hidden, w_down, preferred_element_type=jnp.float32
    )
    expert_out = home_rows(produced)
    returned = lax.all_to_all(expert_out, "expert", split_axis=0, concat_axis=0, tiled=True)
    slots_back = jnp.concatenate([returned.reshape(slot_count, model_width), zero_row], axis=0)
    combined = slots_back[slot_index].astype(jnp.float32)
    output = (hidden + gate_value[:, None] * combined).astype(jnp.bfloat16)
    grad_gate = jnp.sum(grad_output * combined, axis=1)
    grad_down = jnp.einsum(
        "erf,erd->efd", act_hidden, grad_rows, preferred_element_type=jnp.float32
    )
    grad_hidden_units = jnp.einsum(
        "erd,efd->erf", grad_rows, w_down, preferred_element_type=jnp.float32
    )
    grad_pre = gelu_pull(grad_hidden_units)[0].astype(jnp.bfloat16)
    grad_up = jnp.einsum("erd,erf->edf", rows_in, grad_pre, preferred_element_type=jnp.float32)
    grad_expert_in = jnp.einsum(
        "erf,edf->erd", grad_pre, w_up, preferred_element_type=jnp.float32
    )
    grad_send_back = home_rows(grad_expert_in)
    grad_back = lax.all_to_all(grad_send_back, "expert", split_axis=0, concat_axis=0, tiled=True)
    grad_slots = jnp.concatenate([grad_back.reshape(slot_count, model_width), zero_row], axis=0)
    grad_act_two = grad_slots[slot_index].astype(jnp.float32)
    grad_logits = (
        gate_prob * (jnp.where(chosen, grad_gate[:, None], 0.0) - (gate_value * grad_gate)[:, None])
    ).astype(jnp.bfloat16)
    grad_router = contract_rows(act_two, grad_logits)
    grad_act_two = grad_act_two + times_transpose(grad_logits, router_full)
    grad_from_two, grad_gain_two, grad_shift_two = norm_back(
        grad_act_two, scaled_two, inverse_two, gain_two
    )
    grad_hidden = grad_output + grad_from_two
    grad_attn = grad_hidden.astype(jnp.bfloat16)
    grad_out_w = contract_rows(merged, grad_attn)
    grad_merged = times_transpose(grad_attn, out_full).astype(jnp.bfloat16)
    grad_qkv = attend_backward(
        query_heads, key_heads, value_heads, grad_merged, log_totals, prefix_len
    )
    grad_qkv_w = contract_rows(act_one, grad_qkv)
    grad_act_one = times_transpose(grad_qkv, qkv_full)
    grad_from_one, grad_gain_one, grad_shift_one = norm_back(
        grad_act_one, scaled_one, inverse_one, gain_one
    )
    grad_tokens = grad_hidden + grad_from_one
    small_grad = jnp.concatenate(
        [
            grad_gain_one[None],
            grad_shift_one[None],
            grad_gain_two[None],
            grad_shift_two[None],
            grad_router.T,
        ],
        axis=0,
    )
    out_share = lax.psum_scatter(
        grad_out_w.astype(jnp.bfloat16), "wshard", scatter_dimension=0, tiled=True
    )
    qkv_share = lax.psum_scatter(
        grad_qkv_w.astype(jnp.bfloat16), "wshard", scatter_dimension=0, tiled=True
    )
    small_share = lax.psum_scatter(small_grad, "wshard", scatter_dimension=1, tiled=True)
    out_total = lax.psum(out_share, "expert").astype(jnp.float32)
    qkv_total = lax.psum(qkv_share, "expert").astype(jnp.float32)
    small_total = lax.psum(small_share, "expert")
    totals = (
        small_total[0],
        small_total[1],
        qkv_total,
        out_total,
        small_total[2],
        small_total[3],
        small_total[4:].T,
    )
    return (
        output,
        grad_tokens,
        totals[0],
        totals[1],
        totals[2],
        totals[3],
        totals[4],
        totals[5],
        totals[6],
        grad_up,
        grad_down,
    )


def on_device(
    tokens,
    norm1_gain,
    norm1_shift,
    w_qkv,
    w_out,
    norm2_gain,
    norm2_shift,
    w_router,
    w_up,
    w_down,
    routes,
    priority,
    prefix,
    cotangent,
):
    row_count, model_width = tokens.shape
    expert_count = w_router.shape[1]
    capacity = row_count // expert_count
    owners = lax.axis_size("expert")
    experts = w_up.shape[0]
    (
        qkv, act_t, merged_t, back, weight, out_full, low, high, grad_rows, hidden, send_rows,
        vectors, router,
    ) = run_front(
        owners, experts, capacity, prefix, routes.reshape(1, row_count), priority,
        (norm1_gain, norm1_shift, norm2_gain, norm2_shift), tokens, cotangent, w_router.T, w_qkv,
        w_out,
    )
    far_sums, near_sums, home_out, home_grad, grad_up, grad_down, grad_router = run_experts(
        owners, capacity, expert_count, send_rows, grad_rows, w_up, w_down, router
    )
    output, grad_tokens, grad_vectors, grad_gates, grad_qkv, grad_out = run_back(
        owners, capacity, expert_count, home_grad, far_sums, near_sums, home_out, back, hidden, cotangent,
        tokens, vectors, grad_router, act_t, merged_t, qkv, weight, out_full, low, high,
    )
    f32 = jnp.float32
    units = w_up.shape[2]
    (
        output, grad_tokens, grad_gates, grad_qkv, grad_out, grad_up, grad_down, *grad_vectors,
    ) = widen(
        2,
        grad_vectors,
        (
            output, grad_tokens, grad_gates, grad_qkv, grad_out,
            grad_up.reshape(-1, units), grad_down.reshape(-1, model_width),
        ),
        (output.dtype,) + (f32,) * 6,
    )
    return (
        output,
        grad_tokens,
        grad_vectors[0],
        grad_vectors[1],
        grad_qkv,
        grad_out,
        grad_vectors[2],
        grad_vectors[3],
        grad_gates.T,
        grad_up.reshape(w_up.shape),
        grad_down.reshape(w_down.shape),
    )


def solution(mesh):
    placed = (
        P(("expert", "wshard"), None),
        P("wshard"),
        P("wshard"),
        P("wshard", None),
        P("wshard", None),
        P("wshard"),
        P("wshard"),
        P("wshard", None),
        P("expert", None, "wshard"),
        P("expert", "wshard", None),
        P(("expert", "wshard"), None),
        P(("expert", "wshard"), None),
        P(("expert", "wshard")),
        P(("expert", "wshard"), None),
    )
    owners, group = mesh.shape["expert"], mesh.shape["wshard"]

    def body(*args):
        capacity = args[0].shape[0] // args[7].shape[1]
        fits = group == 4 and owners == 8 and capacity % 16 == 0 and args[7].shape[1] % 16 == 0
        return (on_device if fits else on_device_plain)(*args)

    return jax.shard_map(
        body,
        mesh=mesh,
        in_specs=placed,
        out_specs=(
            P(("expert", "wshard"), None),
            P(("expert", "wshard"), None),
            P("wshard"),
            P("wshard"),
            P("wshard", None),
            P("wshard", None),
            P("wshard"),
            P("wshard"),
            P("wshard", None),
            P("expert", None, "wshard"),
            P("expert", "wshard", None),
        ),
        check_vma=False,
    )
```

```python
import functools
import math

import jax
import jax.numpy as jnp
from jax import lax
from jax.experimental import pallas as pl
from jax.experimental.pallas import tpu as pltpu
from jax.sharding import PartitionSpec as P

HEADS = 16
HEAD_DIM = 64


epsilon = 1e-05
VMEM_LIMIT = 66_000_000
TILE = 1024
EARLY_CHUNKS = 1


def normalize(values, gain_vec, shift_vec):
    row_mean = jnp.mean(values, axis=-1, keepdims=True)
    centered = values - row_mean
    inverse = lax.rsqrt(jnp.mean(centered * centered, axis=-1, keepdims=True) + epsilon)
    scaled = centered * inverse
    return (scaled * gain_vec + shift_vec, scaled, inverse)


def norm_back(grad_rows, scaled, inverse, gain_vec):
    weighted = grad_rows * gain_vec
    mean_one = jnp.mean(weighted, axis=-1, keepdims=True)
    mean_two = jnp.mean(weighted * scaled, axis=-1, keepdims=True)
    grad_inputs = inverse * (weighted - mean_one - scaled * mean_two)
    return (grad_inputs, jnp.sum(grad_rows * scaled, axis=0), jnp.sum(grad_rows, axis=0))


def contract_rows(left, right):
    return lax.dot_general(
        left, right, (((0,), (0,)), ((), ())), preferred_element_type=jnp.float32
    )


def times_transpose(left, right):
    return lax.dot_general(
        left, right, (((1,), (1,)), ((), ())), preferred_element_type=jnp.float32
    )


def gelu_tanh(values):
    return jax.nn.gelu(values, approximate=True)


def assign_slots(route_ids, order_ids, expert_count, capacity):
    token_count = route_ids.shape[0]
    same_expert = route_ids[:, None] == route_ids[None, :]
    earlier = order_ids[None, :] < order_ids[:, None]
    rank_ids = jnp.sum((same_expert & earlier).astype(jnp.int32), axis=1)
    is_kept = rank_ids < capacity
    slot_index = jnp.where(is_kept, route_ids * capacity + rank_ids, expert_count * capacity)
    slot_ids = jnp.arange(expert_count * capacity, dtype=jnp.int32)
    match_table = slot_index[None, :] == slot_ids[:, None]
    token_ids = jnp.arange(token_count, dtype=jnp.int32)
    filled = jnp.any(match_table, axis=1)
    picked = jnp.sum(jnp.where(match_table, token_ids[None, :], 0), axis=1)
    slot_source = jnp.where(filled, picked, token_count)
    return (slot_index, slot_source)


def group_heads(values, groups):
    token_count = values.shape[0]
    return jnp.transpose(values.reshape(token_count, groups, -1, HEAD_DIM), (1, 0, 2, 3))


def block_scores(query_block, key_group, block_start, prefix_len):
    block_rows = query_block.shape[0]
    key_count = key_group.shape[0]
    scores = jnp.einsum(
        "qgd,kgd->gqk", query_block, key_group, preferred_element_type=jnp.float32
    ) * (1.0 / math.sqrt(HEAD_DIM))
    query_pos = block_start + jnp.arange(block_rows, dtype=jnp.int32)
    key_pos = jnp.arange(key_count, dtype=jnp.int32)
    allowed = (key_pos[None, :] <= query_pos[:, None]) | (key_pos[None, :] < prefix_len)
    return jnp.where(allowed[None], scores, -1e30)


def attend_forward(query_heads, key_heads, value_heads, prefix_len):
    token_count = query_heads.shape[0]
    group_size = min(4, HEADS)
    groups = HEADS // group_size
    block_rows = min(512, token_count)
    blocks = token_count // block_rows
    starts = jnp.arange(blocks, dtype=jnp.int32) * block_rows

    def one_group(group_item):
        query_group, key_group, value_group = group_item
        query_blocks = query_group.reshape(blocks, block_rows, group_size, HEAD_DIM)

        def one_block(block_item):
            query_block, block_start = block_item
            scores = block_scores(query_block, key_group, block_start, prefix_len)
            row_max = jnp.max(scores, axis=-1, keepdims=True)
            exponent = jnp.exp(scores - row_max)
            row_total = jnp.sum(exponent, axis=-1, keepdims=True)
            attn_probs = (exponent / row_total).astype(jnp.bfloat16)
            result = jnp.einsum(
                "gqk,kgd->qgd", attn_probs, value_group, preferred_element_type=jnp.float32
            )
            return (result, (row_max + jnp.log(row_total))[..., 0])

        return lax.map(one_block, (query_blocks, starts))

    attended, log_totals = lax.map(
        one_group,
        (
            group_heads(query_heads, groups),
            group_heads(key_heads, groups),
            group_heads(value_heads, groups),
        ),
    )
    merged = (
        jnp.transpose(attended, (1, 2, 0, 3, 4))
        .reshape(token_count, HEADS * HEAD_DIM)
        .astype(jnp.bfloat16)
    )
    return (merged, log_totals)


def attend_backward(query_heads, key_heads, value_heads, grad_merged, log_totals, prefix_len):
    token_count = query_heads.shape[0]
    group_size = min(4, HEADS)
    groups = HEADS // group_size
    block_rows = min(512, token_count)
    blocks = token_count // block_rows
    starts = jnp.arange(blocks, dtype=jnp.int32) * block_rows
    score_scale = 1.0 / math.sqrt(HEAD_DIM)

    def one_group(group_item):
        query_group, key_group, value_group, grad_group, total_group = group_item
        query_blocks = query_group.reshape(blocks, block_rows, group_size, HEAD_DIM)
        grad_blocks = grad_group.reshape(blocks, block_rows, group_size, HEAD_DIM)

        def one_block(carry, block_item):
            grad_keys, grad_vals = carry
            query_block, grad_block, total_block, block_start = block_item
            scores = block_scores(query_block, key_group, block_start, prefix_len)
            attn_probs = jnp.exp(scores - total_block[..., None])
            grad_probs = jnp.einsum(
                "qgd,kgd->gqk", grad_block, value_group, preferred_element_type=jnp.float32
            )
            row_delta = jnp.sum(attn_probs * grad_probs, axis=-1, keepdims=True)
            grad_scores = (attn_probs * (grad_probs - row_delta)).astype(jnp.bfloat16)
            grad_vals = grad_vals + jnp.einsum(
                "gqk,qgd->kgd",
                attn_probs.astype(jnp.bfloat16),
                grad_block,
                preferred_element_type=jnp.float32,
            )
            grad_keys = (
                grad_keys
                + jnp.einsum(
                    "gqk,qgd->kgd", grad_scores, query_block, preferred_element_type=jnp.float32
                )
                * score_scale
            )
            grad_query = (
                jnp.einsum(
                    "gqk,kgd->qgd", grad_scores, key_group, preferred_element_type=jnp.float32
                )
                * score_scale
            )
            return ((grad_keys, grad_vals), grad_query)

        zero_keys = jnp.zeros(key_group.shape, jnp.float32)
        carried, grad_queries = lax.scan(
            one_block, (zero_keys, zero_keys), (query_blocks, grad_blocks, total_group, starts)
        )
        return (grad_queries, carried[0], carried[1])

    grad_queries, grad_keys, grad_vals = lax.map(
        one_group,
        (
            group_heads(query_heads, groups),
            group_heads(key_heads, groups),
            group_heads(value_heads, groups),
            group_heads(grad_merged, groups),
            log_totals,
        ),
    )
    query_part = jnp.transpose(grad_queries, (1, 2, 0, 3, 4)).reshape(token_count, HEADS * HEAD_DIM)
    key_part = jnp.transpose(grad_keys, (1, 0, 2, 3)).reshape(token_count, HEADS * HEAD_DIM)
    value_part = jnp.transpose(grad_vals, (1, 0, 2, 3)).reshape(token_count, HEADS * HEAD_DIM)
    return jnp.concatenate([query_part, key_part, value_part], axis=1).astype(jnp.bfloat16)


MESH = pl.DeviceIdType.MESH
LANES = 128


def dot_nn(left, right):
    return lax.dot_general(
        left, right, (((1,), (0,)), ((), ())), preferred_element_type=jnp.float32
    )


def dot_nt(left, right):
    return lax.dot_general(
        left, right, (((1,), (1,)), ((), ())), preferred_element_type=jnp.float32
    )


def dot_tn(left, right):
    return lax.dot_general(
        left, right, (((0,), (0,)), ((), ())), preferred_element_type=jnp.float32
    )


def span(start, size):
    return pl.ds(pl.multiple_of(start, size), size)


def every(start, stop, step):
    def body(i, carry):
        step(i)
        return carry

    lax.fori_loop(start, stop, body, 0)


class Place:
    def __init__(self, owners):
        self.owners = owners
        self.e = lax.axis_index("expert")
        self.w = lax.axis_index("wshard")
        self.c = lax.rem(self.w, 2)
        self.x = lax.div(self.w, 2)
        self.sib = self.w + 1 - 2 * self.c
        self.far = lax.rem(self.w + 2, 4)
        self.diag = 3 - self.w
        self.pair = self.e + 1 - 2 * lax.rem(self.e, 2)

    def ahead(self, k):
        return lax.rem(self.e + k, self.owners)

    def flip(self, bit):
        return self.e + bit * (1 - 2 * lax.rem(lax.div(self.e, bit), 2))

    def peer(self, n):
        other = lax.div(n, 2) + lax.rem(n, 2) * (self.owners // 2)
        result, bit = 0, 1
        while bit < self.owners:
            result = result + bit * lax.rem(lax.div(self.e, bit) + lax.div(other, bit), 2)
            bit *= 2
        return result


def remote(src, dst, send, recv, device):
    return pltpu.make_async_remote_copy(
        src_ref=src,
        dst_ref=dst,
        send_sem=send,
        recv_sem=recv,
        device_id=device,
        device_id_type=MESH,
    )


def greet(peers):
    barrier = pltpu.get_barrier_semaphore()
    for peer in peers:
        pl.semaphore_signal(barrier, inc=1, device_id=peer, device_id_type=MESH)
    pl.semaphore_wait(barrier, len(peers))


def either(test, yes, no):
    pl.when(test)(yes)
    pl.when(jnp.logical_not(test))(no)


class Dispatch:
    def __init__(self, place, capacity, send_ref, rows_ref, sems):
        self.p, self.cap, self.src, self.rows = place, capacity, send_ref, rows_ref
        self.own_sem, self.send, self.recv = sems

    def slice(self, k, core, side):
        start = (((lax.div(k, 2) * 2 + core) * 2 + side) * 2 + lax.rem(k, 2)) * self.cap
        return self.rows.at[:, span(start, self.cap)]

    def own(self):
        return pltpu.make_async_copy(
            self.src.at[self.p.e], self.slice(0, self.p.c, self.p.x), self.own_sem
        )

    def direct(self, k):
        return remote(
            self.src.at[self.p.peer(k)],
            self.slice(k, self.p.c, self.p.x),
            self.send.at[0, k],
            self.recv.at[0, k],
            (self.p.peer(k), self.p.w),
        )

    def hop(self, k, side, which, peer):
        part = self.slice(k, self.p.c, side)
        return remote(
            part, part, self.send.at[which, k], self.recv.at[which, k], (self.p.e, peer)
        )

    def to_sib(self, k):
        return self.hop(k, self.p.x, 1, self.p.sib)

    def to_far(self, k):
        return self.hop(k, self.p.x, 2, self.p.far)

    def relayed(self, k):
        return self.hop(k, 1 - self.p.x, 3, self.p.sib)

    def start(self):
        self.own().start()
        every(1, self.p.owners, lambda k: self.direct(k).start())

    def forward(self, k):
        k = jnp.int32(k)

        @pl.when(k == 0)
        def _():
            self.own().wait()

        @pl.when(k > 0)
        def _():
            self.direct(k).wait_recv()

        self.to_far(k).start()
        self.to_sib(k).start()

    def relay(self, k):
        self.to_far(k).wait_recv()
        self.relayed(k).start()

    def ready(self, k):
        self.to_sib(k).wait_recv()
        self.relayed(k).wait_recv()

    def order(self):
        return (0, 2, 4, 1, 6, 3, 5, 7)

    def drain(self):
        every(1, self.p.owners, lambda k: self.direct(k).wait_send())

        def rest(k):
            self.to_sib(k).wait_send()
            self.to_far(k).wait_send()
            self.relayed(k).wait_send()

        every(0, self.p.owners, rest)


class Return:
    def __init__(self, place, capacity, part, got, mid, far, done, home, sems):
        self.p, self.cap = place, capacity
        self.part, self.got, self.mid, self.far, self.done, self.home = (
            part, got, mid, far, done, home,
        )
        self.own_sem, self.send, self.recv, self.home_send, self.home_recv = sems

    def swapped(self, j, expert):
        size = 4 * self.cap
        return remote(
            self.part.at[expert, span((j * 2 + 1 - self.p.c) * size, size)],
            self.got.at[expert, span(j * size, size)],
            self.send.at[0, j, expert],
            self.recv.at[0, j, expert],
            (self.p.e, self.p.sib),
        )

    def crossed(self, j, expert):
        part = span(j * 2 * self.cap, 2 * self.cap)
        return remote(
            self.mid.at[expert, part],
            self.far.at[expert, part],
            self.send.at[1, j, expert],
            self.recv.at[1, j, expert],
            (self.p.e, self.p.far),
        )

    def own(self, expert):
        return pltpu.make_async_copy(
            self.done.at[0, expert], self.home.at[self.p.e, expert], self.own_sem.at[expert]
        )

    def homed(self, n, expert):
        return remote(
            self.done.at[n, expert],
            self.home.at[self.p.e, expert],
            self.home_send.at[n, expert],
            self.home_recv.at[n, expert],
            (self.p.peer(n), self.p.w),
        )

    def pair_sum(self, j, expert, side):
        size = 2 * self.cap
        mine = self.part[expert, span(((j * 2 + self.p.c) * 2 + side) * size, size), :]
        theirs = self.got[expert, span((j * 2 + side) * size, size), :]
        return mine.astype(jnp.float32) + theirs.astype(jnp.float32)

    def swap(self, j, expert):
        self.swapped(j, expert).start()

    def split(self, j, expert):
        self.swapped(j, expert).wait_recv()
        here = span(j * 2 * self.cap, 2 * self.cap)
        self.mid[expert, here, :] = self.pair_sum(j, expert, 1 - self.p.x).astype(jnp.bfloat16)
        self.keep[expert, here, :] = self.pair_sum(j, expert, self.p.x).astype(jnp.bfloat16)

    def cross(self, j, expert):
        self.swapped(j, expert).wait_recv()
        here = span(j * 2 * self.cap, 2 * self.cap)
        self.mid[expert, here, :] = self.pair_sum(j, expert, 1 - self.p.x).astype(jnp.bfloat16)
        self.crossed(j, expert).start()

    def this_side(self, j, expert):
        return self.pair_sum(j, expert, self.p.x)

    def finish(self, j, expert):
        self.crossed(j, expert).wait_recv()
        here = span(j * 2 * self.cap, 2 * self.cap)
        total = self.this_side(j, expert) + self.far[expert, here, :].astype(jnp.float32)
        total = total.astype(jnp.bfloat16)
        self.done[2 * j, expert] = total[: self.cap]
        self.done[2 * j + 1, expert] = total[self.cap :]
        j = jnp.int32(j)
        self.homed(2 * j + 1, expert).start()
        either(
            j == 0,
            lambda: self.own(expert).start(),
            lambda: self.homed(2 * j, expert).start(),
        )

    def drain_swaps(self, chunks, experts):
        for expert in range(experts):
            every(0, chunks, lambda j: self.swapped(j, expert).wait_send())

    def drain(self, first, last, experts):
        for expert in range(experts):
            every(first, last, lambda j: self.crossed(j, expert).wait_send())
            every(
                max(1, 2 * first), 2 * last, lambda n: self.homed(n, expert).wait_send()
            )

    def arrived(self, first, last, experts):
        for expert in range(experts):
            if first == 0 and last > 0:
                self.own(expert).wait()
            every(
                max(1, 2 * first), 2 * last, lambda n: self.homed(n, expert).wait_recv()
            )


class LateReturn(Return):
    def crossed(self, j, expert):
        part = span(j * 2 * self.cap, 2 * self.cap)
        return remote(
            self.mid.at[expert, part],
            self.far.at[expert, part],
            self.send.at[j, expert],
            self.recv.at[j, expert],
            (self.p.e, self.p.far),
        )

    def this_side(self, j, expert):
        here = span(j * 2 * self.cap, 2 * self.cap)
        return self.part[expert, here, :].astype(jnp.float32)


def gelu_pair(v):
    root = math.sqrt(2.0 / math.pi)
    square = v * v
    t = jnp.tanh(v * (root + (root * 0.044715) * square))
    half = 0.5 + 0.5 * t
    slope = half + (half * (1.0 - t)) * (v * (root + (3.0 * root * 0.044715) * square))
    return v * half, slope


def expert_kernel(
    dims,
    send_ref, grads_hbm, up_hbm, down_hbm, router_ref,
    far_sums, near_sums, home_out, home_grad, up_out, down_out, router_grad,
    rows, grads, scaled, hidden, pre, up, down, grad_up, grad_down,
    part_out, part_grad, got_out, got_grad, mid_out, mid_grad,
    keep_out, far_grad, far_out, done_grad, done_out,
    load_sem, own_sem, disp_send, disp_recv, red_send, red_recv, home_send, home_recv,
):
    owners, experts, capacity, width, units, expert_count = dims
    place = Place(owners)
    loads = [
        pltpu.make_async_copy(src, dst, load_sem.at[i])
        for i, (src, dst) in enumerate(
            [(up_hbm, up), (grads_hbm, grads), (down_hbm, down)]
        )
    ]
    for load in loads:
        load.start()
    greet(
        [(place.ahead(k), place.w) for k in range(1, owners)]
        + [(place.e, place.sib), (place.e, place.far)]
    )
    dispatch = Dispatch(
        place, capacity, send_ref, rows, (own_sem.at[0, 0], disp_send, disp_recv)
    )
    ret_grad = Return(
        place, capacity, part_grad, got_grad, mid_grad, far_grad, done_grad, home_grad,
        (own_sem.at[1], red_send.at[0], red_recv.at[0], home_send.at[0], home_recv.at[0]),
    )
    ret_out = Return(
        place, capacity, part_out, got_out, mid_out, far_out, done_out, home_out,
        (own_sem.at[2], red_send.at[1], red_recv.at[1], home_send.at[1], home_recv.at[1]),
    )
    dispatch.start()
    router_grad[...] = jnp.zeros_like(router_grad)
    tile = min(TILE, units)
    wide = min(TILE, width)
    chunks = owners // 2
    early = EARLY_CHUNKS
    size = 8 * capacity
    lane = lax.broadcasted_iota(jnp.int32, (size, LANES), 1)

    def compute(j, expert):
        here = span(j * size, size)
        logits = dot_nt(rows[expert, here, :], router_ref[...])
        logits = jnp.where(lane < expert_count, logits, -1e30)
        exponent = jnp.exp(logits - jnp.max(logits, axis=1, keepdims=True))
        prob = exponent * (1.0 / jnp.sum(exponent, axis=1, keepdims=True))
        mine = lane == place.e * experts + expert
        gate = jnp.sum(jnp.where(mine, prob, 0.0), axis=1, keepdims=True)
        scaled[expert, here, :] = (
            gate * grads[expert, here, :].astype(jnp.float32)
        ).astype(jnp.bfloat16)

        def one_tile(n):
            cols = span(n * tile, tile)
            value, slope = gelu_pair(dot_nn(rows[expert, here, :], up[expert, :, cols]))
            hidden[expert, here, cols] = value.astype(jnp.bfloat16)
            back = pre[expert, here, cols].astype(jnp.float32)
            pre[expert, here, cols] = (gate * back * slope).astype(jnp.bfloat16)

        every(0, units // tile, one_tile)

        def one_out(n, total):
            cols = span(n * wide, wide)
            value = dot_nn(hidden[expert, here, :], down[expert, :, cols])
            part_out[expert, here, cols] = (gate * value).astype(jnp.bfloat16)
            weighted = value * grads[expert, here, cols].astype(jnp.float32)
            for start in range(0, wide, LANES):
                total = total + weighted[:, start : start + LANES]
            return total

        total = lax.fori_loop(
            0, width // wide, one_out, jnp.zeros((size, LANES), jnp.float32)
        )
        grad_gate = jnp.sum(total, axis=1, keepdims=True)
        grad_logits = (
            prob * ((jnp.where(mine, 1.0, 0.0) - gate) * grad_gate)
        ).astype(jnp.bfloat16)

        def one_in(n):
            cols = span(n * wide, wide)
            value = dot_nt(pre[expert, here, :], up[expert, cols, :]) + dot_nn(
                grad_logits, router_ref[:, cols]
            )
            part_grad[expert, here, cols] = value.astype(jnp.bfloat16)
            router_grad[:, cols] += dot_tn(grad_logits, rows[expert, here, cols])

        every(0, width // wide, one_in)

    def unscaled(j, expert):
        here = span(j * size, size)
        pre[expert, here, :] = dot_nt(grads[expert, here, :], down[expert]).astype(jnp.bfloat16)

    block = min(256, width)

    def weight_grads(expert, first, last):
        def one(n):
            part = span(n * block, block)
            grad_down[expert, part, :] = dot_tn(
                hidden[expert, :, part], scaled[expert]
            ).astype(jnp.bfloat16)
            grad_up[expert, part, :] = dot_tn(rows[expert, :, part], pre[expert]).astype(
                jnp.bfloat16
            )

        every(first * width // block // 4, last * width // block // 4, one)

    def keep(expert):
        return [
            pltpu.make_async_copy(src.at[expert], dst.at[expert], load_sem.at[2 * expert + i])
            for i, (src, dst) in enumerate(((grad_up, up_out), (grad_down, down_out)))
        ]

    turns = [(j, expert) for j in range(chunks) for expert in range(experts)]
    ahead, through, here = dispatch.forward, dispatch.relay, dispatch.ready
    plan = [[] for _ in turns]
    for unit, acts in (
        (0, ((here, 0), (here, 1), (ahead, 5))),
        (1, ((through, 6), (ahead, 7))),
        (2, ((through, 3), (here, 2), (here, 3))),
        (3, ((through, 5),)),
        (4, ((through, 7), (here, 4), (here, 5))),
        (6, ((here, 6), (here, 7))),
    ):
        plan[unit].extend(acts)
    for u in range(2, len(turns)):
        done = turns[u - 2]
        plan[u].append((ret_grad.cross,) + done)
        plan[u].append((ret_out.cross if done[0] < early else ret_out.split,) + done)
        if u >= 4:
            done = turns[u - 4]
            plan[u].append((ret_grad.finish,) + done)
            if done[0] < early:
                plan[u].append((ret_out.finish,) + done)
    ret_out.keep = keep_out
    for load in loads:
        load.wait()

    def unscaled_pair(j):
        for expert in range(experts):
            unscaled(j, expert)

    ahead(0)
    unscaled_pair(0)
    unscaled_pair(1)
    ahead(2)
    ahead(4)
    ahead(1)
    unscaled_pair(2)
    through(0)
    unscaled_pair(3)
    through(2)
    ahead(6)
    through(4)
    through(1)
    ahead(3)

    def step(unit):
        for u, acts in enumerate(plan):

            @pl.when(unit == u)
            def _(acts=acts):
                for act, *at in acts:
                    act(*at)

        j, expert = lax.div(unit, experts), lax.rem(unit, experts)
        compute(j, expert)
        ret_grad.swap(j, expert)
        ret_out.swap(j, expert)

    every(0, len(turns), step)
    ret_grad.cross(*turns[-2])
    ret_grad.cross(*turns[-1])
    ret_grad.finish(*turns[-4])
    ret_out.split(*turns[-2])
    ret_out.split(*turns[-1])
    weight_grads(0, 0, 1)
    sums = [
        pltpu.make_async_copy(src, dst, load_sem.at[4 + i])
        for i, (src, dst) in enumerate(((mid_out, far_sums), (keep_out, near_sums)))
    ]
    for store in sums:
        store.start()
    ret_grad.finish(*turns[-3])
    weight_grads(0, 1, 2)
    ret_grad.finish(*turns[-2])
    weight_grads(0, 2, 3)
    ret_grad.finish(*turns[-1])
    weight_grads(0, 3, 4)
    for store in keep(0):
        store.start()
    for expert in range(1, experts):
        weight_grads(expert, 0, 4)
        for store in keep(expert):
            store.start()
    for expert in range(experts):
        for store in keep(expert):
            store.wait()
    for store in sums:
        store.wait()
    dispatch.drain()
    ret_grad.drain_swaps(chunks, experts)
    ret_grad.drain(0, chunks, experts)
    ret_grad.arrived(0, chunks, experts)
    ret_out.drain_swaps(chunks, experts)
    ret_out.drain(0, early, experts)
    ret_out.arrived(0, early, experts)


def run_experts(owners, capacity, expert_count, send_rows, grads, w_up, w_down, router):
    experts, width, units = w_up.shape
    slots = owners * 4 * capacity
    chunks = owners // 2
    dims = (owners, experts, capacity, width, units, expert_count)
    any_spec = pl.BlockSpec(memory_space=pl.ANY)
    vmem_spec = pl.BlockSpec(memory_space=pltpu.VMEM)
    bf16 = jnp.bfloat16
    home = jax.ShapeDtypeStruct((owners, experts, capacity, width), bf16)
    dma = pltpu.SemaphoreType.DMA

    def vm(*shape):
        return pltpu.VMEM(shape, bf16)

    return pl.pallas_call(
        functools.partial(expert_kernel, dims),
        out_shape=(
            jax.ShapeDtypeStruct((experts, slots // 4, width), bf16),
            jax.ShapeDtypeStruct((experts, slots // 4, width), bf16),
            home, home,
            jax.ShapeDtypeStruct(w_up.shape, bf16),
            jax.ShapeDtypeStruct(w_down.shape, bf16),
            jax.ShapeDtypeStruct((LANES, width), jnp.float32),
        ),
        in_specs=[any_spec] * 4 + [vmem_spec],
        out_specs=(any_spec,) * 6 + (vmem_spec,),
        scratch_shapes=[
            vm(experts, slots, width),
            vm(experts, slots, width),
            vm(experts, slots, width),
            vm(experts, slots, units),
            vm(experts, slots, units),
            vm(experts, width, units),
            vm(experts, units, width),
            vm(experts, width, units),
            vm(experts, units, width),
            vm(experts, slots, width),
            vm(experts, slots, width),
            vm(experts, slots // 2, width),
            vm(experts, slots // 2, width),
            vm(experts, slots // 4, width),
            vm(experts, slots // 4, width),
            vm(experts, slots // 4, width),
            vm(experts, slots // 4, width),
            vm(experts, slots // 4, width),
            vm(owners, experts, capacity, width),
            vm(owners, experts, capacity, width),
            dma((6,)),
            dma((3, experts)),
            dma((4, owners)),
            dma((4, owners)),
            dma((2, 2, chunks, experts)),
            dma((2, 2, chunks, experts)),
            dma((2, owners, experts)),
            dma((2, owners, experts)),
        ],
        compiler_params=pltpu.CompilerParams(
            collective_id=1, has_side_effects=True, vmem_limit_bytes=VMEM_LIMIT
        ),
        name="experts",
    )(send_rows, grads, w_up, w_down, router)


def masked_softmax(scores):
    exponent = jnp.exp(scores - jnp.max(scores, axis=1, keepdims=True))
    return exponent * (1.0 / jnp.sum(exponent, axis=1, keepdims=True))


def attend_head(query, key, value, prefix_len):
    half = query.shape[0] // 2
    query = query * (1.0 / math.sqrt(HEAD_DIM))
    row = lax.broadcasted_iota(jnp.int32, (half, half), 0)
    col = lax.broadcasted_iota(jnp.int32, (half, half), 1)
    low = dot_nt(query[:half], key[:half])
    low = jnp.where((col <= row) | (col < prefix_len), low, -1e30)
    low = masked_softmax(low).astype(jnp.bfloat16)
    high = dot_nt(query[half:], key)
    high = jnp.concatenate(
        [high[:, :half], jnp.where(col <= row, high[:, half:], -1e30)], axis=1
    )
    high = masked_softmax(high).astype(jnp.bfloat16)
    return low, high, dot_nn(low, value[:half]), dot_nn(high, value)


def score_grads(probs, grad_probs):
    probs = probs.astype(jnp.float32)
    weighted = probs * grad_probs
    total = jnp.sum(weighted, axis=1, keepdims=True)
    return (weighted - probs * total).astype(jnp.bfloat16)


def attend_back_head(query, key, value, low, high, grad):
    half = query.shape[0] // 2
    scale = 1.0 / math.sqrt(HEAD_DIM)
    query = query * scale
    grad_low = score_grads(low, dot_nt(grad[:half], value[:half]))
    grad_high = score_grads(high, dot_nt(grad[half:], value))
    grad_query = jnp.concatenate(
        [dot_nn(grad_low, key[:half]), dot_nn(grad_high, key)], axis=0
    )
    value_all = dot_tn(high, grad[half:])
    key_all = dot_tn(grad_high, query[half:])
    grad_value = jnp.concatenate(
        [value_all[:half] + dot_tn(low, grad[:half]), value_all[half:]], axis=0
    )
    grad_key = jnp.concatenate(
        [key_all[:half] + dot_tn(grad_low, query[:half]), key_all[half:]], axis=0
    )
    return (
        (grad_query * scale).astype(jnp.bfloat16),
        grad_key.astype(jnp.bfloat16),
        grad_value.astype(jnp.bfloat16),
    )


class Gather:
    def __init__(self, place, pieces, parts, src, dst, sems):
        self.p, self.src, self.dst, self.pieces, self.parts = place, src, dst, pieces, parts
        self.send, self.recv = sems
        self.shard = src.shape[0]
        self.half = self.shard // 2
        self.width = src.shape[1] // parts
        self.step = self.width // pieces
        self.first = lax.rem(place.e, 2) * self.half
        self.second = self.half - self.first

    def cols(self, n, part):
        return span(part * self.width + n * self.step, self.step)

    def block(self, owner, start, size, n, part):
        rows = pl.ds(pl.multiple_of(owner * self.shard + start, self.half), size)
        return self.dst.at[rows, self.cols(n, part)]

    def move(self, which, n, part, src, dst, device):
        return remote(
            src, dst, self.send.at[which, n, part], self.recv.at[which, n, part], device
        )

    def own(self, n, part):
        return pltpu.make_async_copy(
            self.src.at[:, self.cols(n, part)],
            self.block(self.p.w, 0, self.shard, n, part),
            self.recv.at[5, n, part],
        )

    def near(self, n, part):
        return self.move(
            4, n, part, self.src.at[:, self.cols(n, part)],
            self.block(self.p.w, 0, self.shard, n, part), (self.p.e, self.p.sib),
        )

    def hop(self, n, part):
        return self.move(
            0, n, part, self.src.at[span(self.first, self.half), self.cols(n, part)],
            self.block(self.p.w, self.first, self.half, n, part), (self.p.e, self.p.far),
        )

    def pass_from(self, which, start, n, part, device):
        block = self.block(self.p.far, start, self.half, n, part)
        return self.move(which, n, part, block, block, device)

    def pairs(self, n, part):
        return self.pass_from(1, self.first, n, part, (self.p.pair, self.p.w))

    def relay(self, n, part):
        return self.pass_from(2, self.first, n, part, (self.p.e, self.p.sib))

    def pair_relay(self, n, part):
        return self.pass_from(3, self.second, n, part, (self.p.e, self.p.sib))

    def all_parts(self, n, act):
        for part in range(self.parts):
            act(n, part)

    def start_own(self):
        every(
            0, self.pieces, lambda n: self.all_parts(n, lambda n, part: self.own(n, part).start())
        )

    def start(self):
        def hop(n, part):
            self.hop(n, part).start()

        def near(n, part):
            self.near(n, part).start()

        every(0, self.pieces, lambda n: self.all_parts(n, hop))
        every(0, self.pieces, lambda n: self.all_parts(n, near))

    def pass_on(self, n):
        def one(n, part):
            self.hop(n, part).wait_recv()
            self.pairs(n, part).start()
            self.relay(n, part).start()

        self.all_parts(n, one)

    def pass_pair(self, n):
        def one(n, part):
            self.pairs(n, part).wait_recv()
            self.pair_relay(n, part).start()

        self.all_parts(n, one)

    def ready(self, n):
        def one(n, part):
            self.own(n, part).wait()
            for copy in (self.near(n, part), self.relay(n, part), self.pair_relay(n, part)):
                copy.wait_recv()

        self.all_parts(n, one)

    def drain(self):
        def one(n, part):
            for copy in (
                self.hop(n, part), self.pairs(n, part), self.relay(n, part),
                self.pair_relay(n, part), self.near(n, part),
            ):
                copy.wait_send()

        every(0, self.pieces, lambda n: self.all_parts(n, one))


def slot_tables(routes_ref, priority_ref, capacity, pick_ref, back_ref):
    count = routes_ref.shape[1]
    row = lax.broadcasted_iota(jnp.int32, (count, count), 0).astype(jnp.float32)
    col = lax.broadcasted_iota(jnp.int32, (count, count), 1).astype(jnp.float32)
    eye = row == col
    route_row = routes_ref[...].astype(jnp.float32)
    order_row = priority_ref[...].astype(jnp.float32)
    route_col = jnp.sum(jnp.where(eye, route_row, 0.0), axis=1, keepdims=True)
    order_col = jnp.sum(jnp.where(eye, order_row, 0.0), axis=1, keepdims=True)
    same = route_col == route_row
    rank_row = jnp.sum(
        jnp.where(same & (order_col < order_row), 1.0, 0.0), axis=0, keepdims=True
    )
    rank_col = jnp.sum(
        jnp.where(same & (order_row < order_col), 1.0, 0.0), axis=1, keepdims=True
    )
    slots = float(count)
    slot_row = jnp.where(rank_row < capacity, route_row * capacity + rank_row, slots)
    slot_col = jnp.where(rank_col < capacity, route_col * capacity + rank_col, slots)
    pick_ref[...] = jnp.where(slot_row == row, 1.0, 0.0).astype(jnp.bfloat16)
    back_ref[...] = jnp.where(slot_col == col, 1.0, 0.0).astype(jnp.bfloat16)


def norm_stats(value):
    centered = value - jnp.mean(value, axis=1, keepdims=True)
    inverse = lax.rsqrt(jnp.mean(centered * centered, axis=1, keepdims=True) + epsilon)
    return centered * inverse, inverse


def front_kernel(
    dims,
    prefix_ref, routes_ref, priority_ref, gain_one_ref, shift_one_ref, gain_two_ref, shift_two_ref,
    tokens_hbm, cot_hbm, router_hbm, qkv_hbm, out_hbm,
    qkv_out, act_out, merged_out, back_out, weight_out, out_full, low_out, high_out, grads_rows,
    hidden_hbm, send_hbm, small_out, router_out,
    small_own, tokens_ref, cot_ref, hidden_ref, send_ref,
    small, weight, out_w, qkv, act, merged, act_two, turned, pick, back, grads_send, low_buf, high_buf,
    own_sem, disp_send, disp_recv, small_send, small_recv, gat_send, gat_recv, store_sem, prob_sem, first_sem,
):
    owners, capacity, pieces = dims
    place = Place(owners)
    firsts = [
        pltpu.make_async_copy(src, dst, first_sem.at[i])
        for i, (src, dst) in enumerate(((cot_hbm, cot_ref), (tokens_hbm, tokens_ref)))
    ]
    for load in firsts:
        load.start()
    small_own[...] = jnp.zeros_like(small_own)
    for i, vector_ref in enumerate((gain_one_ref, shift_one_ref, gain_two_ref, shift_two_ref)):
        small_own[i, :] = vector_ref[...]
    rows, width = tokens_ref.shape
    shard = qkv_hbm.shape[0]
    gathers = [
        Gather(place, pieces, parts, src, dst, (gat_send.at[i], gat_recv.at[i]))
        for i, (parts, src, dst) in enumerate(((3, qkv_hbm, weight), (1, out_hbm, out_w)))
    ]
    for gather in gathers:
        gather.start_own()
    vectors, gates = small_own.shape[0], router_hbm.shape[0]
    small_parts = [
        (small_own, small.at[place.w, pl.ds(0, vectors)]),
        (router_hbm, small.at[place.w, pl.ds(vectors, gates)]),
    ]
    own_smalls = [
        pltpu.make_async_copy(src, dst, own_sem.at[3 + i])
        for i, (src, dst) in enumerate(small_parts)
    ]
    for copy in own_smalls:
        copy.start()
    greet(
        [(place.ahead(k), place.w) for k in range(1, owners)]
        + [(place.e, place.sib), (place.e, place.far), (place.e, place.diag)]
    )
    smalls = [
        remote(src, dst, small_send.at[n, i], small_recv.at[n, i], (place.e, peer))
        for i, peer in enumerate((place.sib, place.far, place.diag))
        for n, (src, dst) in enumerate(small_parts)
    ]
    for copy in smalls:
        copy.start()
    for gather in gathers:
        gather.start()
    slot_tables(routes_ref, priority_ref, capacity, pick, back)
    tile = min(256, width)
    shape = grads_send.shape[:3]

    def to_slots(values_ref, slots_ref):
        def one(n):
            cols = span(n * tile, tile)
            value = dot_nn(pick[...], values_ref[:, cols]).astype(jnp.bfloat16)
            slots_ref[:, :, :, cols] = value.reshape(shape + (tile,))

        every(0, width // tile, one)

    firsts[0].wait()
    to_slots(cot_ref, grads_send)
    dispatch = Dispatch(
        place, capacity, grads_send, grads_rows, (own_sem.at[0], disp_send, disp_recv)
    )
    dispatch.start()
    for copy in own_smalls:
        copy.wait()
    for copy in smalls:
        copy.wait_recv()
    small_out[...] = small[:, :vectors, :]
    router_out[...] = jnp.zeros_like(router_out)
    router_out[:gates, :] = jnp.concatenate(
        [small[i, vectors:, :] for i in range(4)], axis=1
    )

    def vector(which):
        parts = [small[i, which : which + 1, :] for i in range(4)]
        return jnp.concatenate(parts, axis=1).astype(jnp.float32)

    band = min(64, rows)
    gain, shift = vector(0), vector(1)

    def norm_band(i):
        part = span(i * band, band)
        scaled, _ = norm_stats(tokens_ref[part, :].astype(jnp.float32))
        act[part, :] = (scaled * gain + shift).astype(jnp.bfloat16)

    def project(n):
        for part in range(3):
            cols = gathers[0].cols(n, part)
            qkv[:, cols] = dot_nn(act[...], weight[:, cols]).astype(jnp.bfloat16)

    gathers[0].pass_on(0)
    firsts[1].wait()
    every(0, rows // band, norm_band)
    turned[0] = act[...].T
    stores = [
        pltpu.make_async_copy(src, dst, store_sem.at[i])
        for i, (src, dst) in enumerate(
            [(qkv, qkv_out), (turned.at[0], act_out), (back, back_out), (weight, weight_out),
             (turned.at[1], merged_out), (out_w, out_full)]
        )
    ]
    for store in stores[1:3]:
        store.start()
    half = rows // 2
    pairs = width // LANES

    def keep_probs(i):
        slot = lax.rem(i, 2)
        return (
            pltpu.make_async_copy(
                low_buf.at[slot], low_out.at[pl.ds(2 * i, 2)], prob_sem.at[0, slot]
            ),
            pltpu.make_async_copy(
                high_buf.at[slot], high_out.at[pl.ds(2 * i, 2)], prob_sem.at[1, slot]
            ),
        )

    def attend_pair(i):
        slot = lax.rem(i, 2)

        @pl.when(i >= 2)
        def _():
            for copy in keep_probs(i - 2):
                copy.wait()

        query, key, value = (
            qkv[:, span(part * width + i * LANES, LANES)] for part in range(3)
        )
        tops, bottoms = [], []
        for head in range(2):
            part = slice(head * HEAD_DIM, (head + 1) * HEAD_DIM)
            low, high, top, bottom = attend_head(
                query[:, part], key[:, part], value[:, part], prefix_ref[0]
            )
            low_buf[slot, head] = low
            high_buf[slot, head] = high
            tops.append(top)
            bottoms.append(bottom)
        cols = span(i * LANES, LANES)
        merged[:half, cols] = jnp.concatenate(tops, axis=1).astype(jnp.bfloat16)
        merged[half:, cols] = jnp.concatenate(bottoms, axis=1).astype(jnp.bfloat16)
        for copy in keep_probs(i):
            copy.start()

    group = pairs // pieces
    share = -(-owners // pieces)

    def front_step(n):
        @pl.when(n + 1 < pieces)
        def _():
            gathers[0].pass_on(n + 1)

        gathers[0].pass_pair(n)
        for i, partner in enumerate(dispatch.order()):
            pl.when(n == i // share)(functools.partial(dispatch.forward, partner))
        gathers[0].ready(n)
        project(n)
        pl.when(n >= 2)(lambda: gathers[1].pass_on(n - 2))

        @pl.when(n == pieces - 1)
        def _():
            gathers[1].pass_on(pieces - 2)
            gathers[1].pass_pair(0)

        for i in range(group):
            attend_pair(n * group + i)

    every(0, pieces, front_step)
    gathers[1].pass_on(pieces - 1)
    every(1, pieces, gathers[1].pass_pair)
    turned[1] = merged[...].T
    for i in (0, 3, 4):
        stores[i].start()
    order = dispatch.order()
    dispatch.relay(order[0])
    every(0, pieces, gathers[1].ready)
    stores[5].start()
    gain_two, shift_two = vector(2), vector(3)
    band_two = min(128, rows)

    def middle(i):
        part = span(i * band_two, band_two)
        value = tokens_ref[part, :].astype(jnp.float32) + dot_nn(merged[part, :], out_w[...])
        hidden_ref[part, :] = value
        scaled, _ = norm_stats(value)
        act_two[part, :] = (scaled * gain_two + shift_two).astype(jnp.bfloat16)
        for n, partner in enumerate(order[1 : 1 + bands]):
            pl.when(i == n)(functools.partial(dispatch.relay, partner))

    bands = rows // band_two
    every(0, bands, middle)
    results = [
        pltpu.make_async_copy(src, dst, first_sem.at[2 + i])
        for i, (src, dst) in enumerate(((hidden_ref, hidden_hbm), (send_ref, send_hbm)))
    ]
    results[0].start()
    to_slots(act_two, send_ref)
    results[1].start()
    for partner in order[1 + bands :]:
        dispatch.relay(partner)
    for i in (pairs - 2, pairs - 1):
        for copy in keep_probs(i):
            copy.wait()
    every(0, owners, dispatch.ready)
    for store in stores + results:
        store.wait()
    for copy in smalls:
        copy.wait_send()
    for gather in gathers:
        gather.drain()
    dispatch.drain()


def run_front(
    owners, experts, capacity, prefix, routes, priority, vectors, tokens, cotangent, router, w_qkv, w_out
):
    rows, width = tokens.shape
    shard, columns = w_qkv.shape
    half = rows // 2
    heads = width // HEAD_DIM
    pieces = 4
    any_spec = pl.BlockSpec(memory_space=pl.ANY)
    vmem_spec = pl.BlockSpec(memory_space=pltpu.VMEM)
    bf16, f32 = jnp.bfloat16, jnp.float32
    dma = pltpu.SemaphoreType.DMA

    def out(*shape):
        return jax.ShapeDtypeStruct(shape, bf16)

    def vm(*shape):
        return pltpu.VMEM(shape, bf16)

    return pl.pallas_call(
        functools.partial(front_kernel, (owners, capacity, pieces)),
        out_shape=(
            out(rows, columns),
            out(width, rows),
            out(width, rows),
            out(rows, rows),
            out(4 * shard, columns),
            out(4 * shard, width),
            out(heads, half, half),
            out(heads, half, rows),
            out(experts, owners * 4 * capacity, width),
            jax.ShapeDtypeStruct((rows, width), f32),
            out(owners, experts, capacity, width),
            out(4, 16, shard),
            out(LANES, width),
        ),
        in_specs=[pl.BlockSpec(memory_space=pltpu.SMEM)] + [vmem_spec] * 6 + [any_spec] * 5,
        out_specs=(any_spec,) * 11 + (vmem_spec,) * 2,
        scratch_shapes=[
            vm(16, shard),
            vm(rows, width),
            vm(rows, width),
            pltpu.VMEM((rows, width), f32),
            vm(owners, experts, capacity, width),
            vm(4, 16 + router.shape[0], shard),
            vm(4 * shard, columns),
            vm(4 * shard, width),
            vm(rows, columns),
            vm(rows, width),
            vm(rows, width),
            vm(rows, width),
            vm(2, width, rows),
            vm(rows, rows),
            vm(rows, rows),
            vm(owners, experts, capacity, width),
            vm(2, 2, half, half),
            vm(2, 2, half, rows),
            dma((5,)),
            dma((4, owners)),
            dma((4, owners)),
            dma((2, 3)),
            dma((2, 3)),
            dma((2, 6, pieces, 3)),
            dma((2, 6, pieces, 3)),
            dma((6,)),
            dma((2, 2)),
            dma((4,)),
        ],
        compiler_params=pltpu.CompilerParams(
            collective_id=0, has_side_effects=True, vmem_limit_bytes=VMEM_LIMIT
        ),
        name="front",
    )(prefix, routes, priority, *vectors, tokens, cotangent, router, w_qkv, w_out)


class Reduce:
    def __init__(self, place, part, got, far, pair, near, line, done, sems):
        self.p = place
        self.part, self.got, self.far = part, got, far
        self.pair, self.near, self.line, self.done = pair, near, line, done
        self.send, self.recv = sems
        self.chunks = part.shape[0]
        self.halves = done.shape[1] // 2
        self.bit = lax.rem(place.e, 2)
        self.low = lax.rem(lax.div(place.e, 2), 2)
        self.high = lax.div(place.e, 4)

    def step(self, which, n, src, dst, device):
        return remote(src, dst, self.send.at[which, n], self.recv.at[which, n], device)

    def swapped(self, n):
        return self.step(
            0, n, self.part.at[n, :, 1 - self.p.c], self.got.at[n], (self.p.e, self.p.sib)
        )

    def crossed(self, n):
        return self.step(
            1, n, self.part.at[n, 1 - self.p.x, self.p.c], self.far.at[n], (self.p.e, self.p.far)
        )

    def folded(self, n):
        other = span((1 - self.bit) * self.halves, self.halves)
        return self.step(
            2, n, self.part.at[n, self.p.x, self.p.c, other], self.pair.at[n],
            (self.p.pair, self.p.w),
        )

    def shared(self, n):
        part = self.done.at[n, span(self.bit * self.halves, self.halves)]
        return self.step(3, n, part, part, (self.p.pair, self.p.w))

    def quarter(self, low):
        size = self.halves // 2
        return span(self.bit * self.halves + low * size, size)

    def eighth(self, high):
        size = self.halves // 4
        return span(self.bit * self.halves + (self.low * 2 + high) * size, size)

    def nears(self, n):
        return self.step(
            4, n, self.part.at[n, self.p.x, self.p.c, self.quarter(1 - self.low)],
            self.near.at[n], (self.p.flip(2), self.p.w),
        )

    def lines(self, n):
        return self.step(
            5, n, self.part.at[n, self.p.x, self.p.c, self.eighth(1 - self.high)],
            self.line.at[n], (self.p.flip(4), self.p.w),
        )

    def line_back(self, n):
        part = self.done.at[n, self.eighth(self.high)]
        return self.step(6, n, part, part, (self.p.flip(4), self.p.w))

    def near_back(self, n):
        part = self.done.at[n, self.quarter(self.low)]
        return self.step(7, n, part, part, (self.p.flip(2), self.p.w))

    def add(self, n, rows, other):
        total = self.part[n, self.p.x, self.p.c, rows, :].astype(jnp.float32) + other.astype(
            jnp.float32
        )
        return total.astype(jnp.bfloat16)

    def pair_sum(self, n, side):
        return self.part[n, side, self.p.c].astype(jnp.float32) + self.got[n, side].astype(
            jnp.float32
        )

    def swap(self, n):
        self.swapped(n).start()

    def cross(self, n):
        self.swapped(n).wait_recv()
        side = 1 - self.p.x
        self.part[n, side, self.p.c] = self.pair_sum(n, side).astype(jnp.bfloat16)
        self.crossed(n).start()

    def fold(self, n):
        self.crossed(n).wait_recv()
        total = self.pair_sum(n, self.p.x) + self.far[n].astype(jnp.float32)
        self.part[n, self.p.x, self.p.c] = total.astype(jnp.bfloat16)
        self.folded(n).start()

    def spread(self, n):
        self.folded(n).wait_recv()
        own = span(self.bit * self.halves, self.halves)
        self.part[n, self.p.x, self.p.c, own, :] = self.add(n, own, self.pair[n])
        self.nears(n).start()

    def reach(self, n):
        self.nears(n).wait_recv()
        own = self.quarter(self.low)
        self.part[n, self.p.x, self.p.c, own, :] = self.add(n, own, self.near[n])
        self.lines(n).start()

    def collect(self, n):
        self.lines(n).wait_recv()
        own = self.eighth(self.high)
        self.done[n, own, :] = self.add(n, own, self.line[n])
        self.line_back(n).start()

    def widen_back(self, n):
        self.line_back(n).wait_recv()
        self.near_back(n).start()

    def share(self, n):
        self.near_back(n).wait_recv()
        self.shared(n).start()

    def finish(self, n):
        self.shared(n).wait_recv()

    def line_stages(self):
        return (self.spread, self.reach, self.collect, self.widen_back, self.share, self.finish)

    def stages(self):
        return (self.cross, self.fold) + self.line_stages()

    def drain(self):
        def one(n):
            for copy in (
                self.swapped(n), self.crossed(n), self.folded(n), self.shared(n), self.nears(n),
                self.lines(n), self.line_back(n), self.near_back(n),
            ):
                copy.wait_send()

        every(0, self.chunks, one)


class PairFirst(Reduce):
    def folded(self, n):
        other = span((1 - self.bit) * self.halves, self.halves)
        return self.step(
            2, n, self.part.at[n, :, self.p.c, other], self.pair.at[n], (self.p.pair, self.p.w)
        )

    def crossed(self, n):
        own = span(self.bit * self.halves, self.halves)
        return self.step(
            1, n, self.part.at[n, 1 - self.p.x, self.p.c, own], self.far.at[n],
            (self.p.e, self.p.far),
        )

    def fold(self, n):
        self.swapped(n).wait_recv()
        for side in range(2):
            self.part[n, side, self.p.c] = self.pair_sum(n, side).astype(jnp.bfloat16)
        self.folded(n).start()

    def cross(self, n):
        self.folded(n).wait_recv()
        own = span(self.bit * self.halves, self.halves)
        for side in range(2):
            total = self.part[n, side, self.p.c, own, :].astype(jnp.float32) + self.pair[
                n, side
            ].astype(jnp.float32)
            self.part[n, side, self.p.c, own, :] = total.astype(jnp.bfloat16)
        self.crossed(n).start()

    def spread(self, n):
        self.crossed(n).wait_recv()
        own = span(self.bit * self.halves, self.halves)
        self.part[n, self.p.x, self.p.c, own, :] = self.add(n, own, self.far[n])
        self.nears(n).start()

    def stages(self):
        return (self.fold, self.cross) + self.line_stages()


class Small:
    def __init__(self, place, value, part, got, mid, far, total, others, out, sems):
        self.p, self.value, self.part, self.got, self.mid = place, value, part, got, mid
        self.far, self.total, self.others, self.out = far, total, others, out
        self.send, self.recv, self.all_send, self.all_recv = sems

    def swapped(self):
        return remote(
            self.part.at[:, 1 - self.p.c], self.got, self.send.at[0], self.recv.at[0],
            (self.p.e, self.p.sib),
        )

    def crossed(self):
        return remote(
            self.mid, self.far, self.send.at[1], self.recv.at[1], (self.p.e, self.p.far)
        )

    def spreads(self, k):
        return remote(
            self.total, self.others.at[k], self.all_send.at[k], self.all_recv.at[k],
            (self.p.ahead(k), self.p.w),
        )

    def swap(self):
        size = self.part.shape[-1]
        for owner in range(4):
            self.part[owner // 2, owner % 2] = self.value[:, owner * size : (owner + 1) * size]
        self.swapped().start()

    def cross(self):
        self.swapped().wait_recv()
        self.mid[...] = self.part[1 - self.p.x, self.p.c] + self.got[1 - self.p.x]
        self.crossed().start()

    def spread(self):
        self.crossed().wait_recv()
        self.total[...] = self.part[self.p.x, self.p.c] + self.got[self.p.x] + self.far[...]
        for k in range(1, self.p.owners):
            self.spreads(k).start()

    def finish(self):
        total = self.total[...]
        for k in range(1, self.p.owners):
            self.spreads(k).wait_recv()
            total = total + self.others[k]
        vectors_out, gates_out = self.out
        vectors_out[...] = total[: vectors_out.shape[0]]
        gates_out[...] = total[vectors_out.shape[0] :]

    def drain(self):
        self.swapped().wait_send()
        self.crossed().wait_send()
        for k in range(1, self.p.owners):
            self.spreads(k).wait_send()


def norm_back_rows(grad, scaled, inverse, gain):
    weighted = grad * gain
    mean_one = jnp.mean(weighted, axis=1, keepdims=True)
    mean_two = jnp.mean(weighted * scaled, axis=1, keepdims=True)
    return inverse * (weighted - mean_one - scaled * mean_two)


def back_kernel(
    dims,
    home_grad_hbm, back_hbm, hidden_hbm, cot_hbm, tokens_hbm, vectors_ref, router_ref,
    far_hbm, near_hbm, home_hbm, act_hbm, merged_hbm, qkv_hbm, weight_hbm, out_hbm, low_hbm, high_hbm,
    output_hbm, grad_tokens_hbm, vectors_out, gates_out, qkv_out, out_out,
    home_grad_ref, back_ref, hidden_ref, cot_ref, tokens_ref, output_ref, tokens_out,
    near_sums, far_sums, done_rows, home_out,
    act_t, merged_t, qkv, weight, out_w, low_buf, high_buf, attn, grad_merged, grad_act,
    part_q, got_q, far_q, pair_q, near_q, line_q, done_q,
    part_o, got_o, far_o, pair_o, near_o, line_o, done_o,
    small, small_part, small_got, small_mid, small_far, small_sum, small_all,
    first_sem, load_sem, prob_sem, own_sem, early_sem, cross_send, cross_recv, home_send, home_recv, send_q, recv_q, send_o, recv_o,
    small_send, small_recv, all_send, all_recv, out_sem,
):
    owners, capacity, gates = dims
    grad_qkv = qkv
    place = Place(owners)
    loads = [
        pltpu.make_async_copy(src, dst, load_sem.at[i])
        for i, (src, dst) in enumerate(
            [(merged_hbm, merged_t), (out_hbm, out_w), (qkv_hbm, qkv), (act_hbm, act_t),
             (weight_hbm, weight), (near_hbm, near_sums)]
        )
    ]

    def load_probs(i):
        slot = lax.rem(i, 2)
        return (
            pltpu.make_async_copy(
                low_hbm.at[pl.ds(2 * i, 2)], low_buf.at[slot], prob_sem.at[0, slot]
            ),
            pltpu.make_async_copy(
                high_hbm.at[pl.ds(2 * i, 2)], high_buf.at[slot], prob_sem.at[1, slot]
            ),
        )

    firsts = [
        pltpu.make_async_copy(src, dst, first_sem.at[i])
        for i, (src, dst) in enumerate(
            [(home_grad_hbm, home_grad_ref), (back_hbm, back_ref), (hidden_hbm, hidden_ref),
             (cot_hbm, cot_ref), (tokens_hbm, tokens_ref)]
        )
    ]
    results = [
        pltpu.make_async_copy(src, dst, first_sem.at[5 + i])
        for i, (src, dst) in enumerate([(tokens_out, grad_tokens_hbm), (output_ref, output_hbm)])
    ]
    for load in firsts[:4] + loads + firsts[4:]:
        load.start()
    for load in load_probs(0):
        load.start()
    greet(
        [(place.ahead(k), place.w) for k in range(1, owners)]
        + [(place.e, place.sib), (place.e, place.far)]
    )
    experts = near_sums.shape[0]
    groups = owners // 2
    late = LateReturn(
        place, capacity, near_sums, None, far_hbm, far_sums, done_rows, home_out,
        (own_sem, cross_send, cross_recv, home_send, home_recv),
    )

    def start_late(j):
        for expert in range(experts):
            late.crossed(j, expert).start()

    every(EARLY_CHUNKS, groups, start_late)

    def early_rows(n):
        row = place.peer(n)
        return pltpu.make_async_copy(home_hbm.at[row], home_out.at[row], early_sem.at[n])

    every(0, 2 * EARLY_CHUNKS, lambda n: early_rows(n).start())
    reduce_o = PairFirst(
        place, part_o, got_o, far_o, pair_o, near_o, line_o, done_o, (send_o, recv_o)
    )
    reduce_q = Reduce(
        place, part_q, got_q, far_q, pair_q, near_q, line_q, done_q, (send_q, recv_q)
    )
    smalls = Small(
        place, small, small_part, small_got, small_mid, small_far, small_sum, small_all, (vectors_out, gates_out),
        (small_send, small_recv, all_send, all_recv),
    )
    rows, width = tokens_ref.shape
    shard = width // 4
    band = min(128, rows)
    lead = small.shape[0]

    def vector(which):
        parts = [vectors_ref[i, which : which + 1, :] for i in range(4)]
        return jnp.concatenate(parts, axis=1).astype(jnp.float32)

    gain_one, gain_two = vector(0), vector(2)
    small[: lead - gates, :] = jnp.zeros((lead - gates, width), jnp.float32)
    small[lead - gates :, :] = router_ref[:gates, :]

    def post(i):
        part = span(i * band, band)
        grad = dot_nn(back_ref[part, :], home_grad_ref.reshape(rows, width)[...])
        scaled, inverse = norm_stats(hidden_ref[part, :])
        value = cot_ref[part, :].astype(jnp.float32) + norm_back_rows(
            grad, scaled, inverse, gain_two
        )
        tokens_out[part, :] = value
        attn[part, :] = value.astype(jnp.bfloat16)
        small[2:3, :] += jnp.sum(grad * scaled, axis=0, keepdims=True)
        small[3:4, :] += jnp.sum(grad, axis=0, keepdims=True)

    for load in firsts[:4]:
        load.wait()
    every(0, rows // band, post)
    loads[0].wait()

    def weight_grad(part, n, left, right):
        value = dot_nn(left[...], right).astype(jnp.bfloat16)
        part[n] = value.reshape(part.shape[1:])

    tile_o = part_o.shape[-1]
    out_chunks = part_o.shape[0]
    for n in range(out_chunks):
        weight_grad(part_o, n, merged_t, attn[:, n * tile_o : (n + 1) * tile_o])
        reduce_o.swap(n)
    loads[1].wait()

    def merged_band(i):
        part = span(i * band, band)
        grad_merged[part, :] = dot_nt(attn[part, :], out_w[...]).astype(jnp.bfloat16)

    every(0, rows // band, merged_band)
    stages_o, stages_q = reduce_o.stages(), reduce_q.stages()
    for n in range(out_chunks):
        stages_o[0](n)
    for load in loads[2:] + firsts[4:]:
        load.wait()
    grad_act[...] = jnp.zeros_like(grad_act)
    pairs = part_q.shape[0]

    def attend_pair(i):
        slot = lax.rem(i, 2)
        for load in load_probs(i):
            load.wait()

        @pl.when(i + 1 < pairs)
        def _():
            for load in load_probs(i + 1):
                load.start()

        cols = span(i * LANES, LANES)
        query, key, value = (
            qkv[:, span(part * width + i * LANES, LANES)] for part in range(3)
        )
        grad = grad_merged[:, cols]
        results = []
        for head in range(2):
            part = slice(head * HEAD_DIM, (head + 1) * HEAD_DIM)
            results.append(
                attend_back_head(
                    query[:, part], key[:, part], value[:, part],
                    low_buf[slot, head], high_buf[slot, head], grad[:, part],
                )
            )
        for which in range(3):
            grad_qkv[:, span(which * width + i * LANES, LANES)] = jnp.concatenate(
                [results[0][which], results[1][which]], axis=1
            )
        right = jnp.concatenate(
            [grad_qkv[:, span(which * width + i * LANES, LANES)] for which in range(3)], axis=1
        )
        weight_grad(part_q, i, act_t, right)
        reduce_q.swap(i)
        columns = jnp.concatenate(
            [weight[:, span(which * width + i * LANES, LANES)] for which in range(3)], axis=1
        )
        grad_act[...] += dot_nt(right, columns)

    def input_band(i):
        part = span(i * band, band)
        grad = grad_act[part, :]
        scaled, inverse = norm_stats(tokens_ref[part, :].astype(jnp.float32))
        tokens_out[part, :] += norm_back_rows(grad, scaled, inverse, gain_one)
        small[0:1, :] += jnp.sum(grad * scaled, axis=0, keepdims=True)
        small[1:2, :] += jnp.sum(grad, axis=0, keepdims=True)

    def output_band(i):
        part = span(i * band, band)
        slots = home_out.reshape(rows, width)
        value = hidden_ref[part, :] + dot_nn(back_ref[part, :], slots[...])
        output_ref[part, :] = value.astype(jnp.bfloat16)

    def store_q(i):
        return [
            pltpu.make_async_copy(
                done_q.at[i, :, pl.ds(which * LANES, LANES)],
                qkv_out.at[:, span(which * width + i * LANES, LANES)],
                out_sem.at[which, i],
            )
            for which in range(3)
        ]

    def store_o(n):
        return pltpu.make_async_copy(
            done_o.at[n], out_out.at[:, span(n * tile_o, tile_o)], out_sem.at[3, n]
        )

    delays = (1, 3, 4, 5, 6, 7, 8, 9)
    turns_o = (-1, 3, 6, 7, 8, 9, 10, 11)
    last = len(delays) - 1
    half = rows // band // 2

    def slot_step(slot):
        @pl.when(slot + EARLY_CHUNKS < groups)
        def _():
            for expert in range(experts):
                late.finish(slot + EARLY_CHUNKS, expert)

        pl.when(slot < pairs)(lambda: attend_pair(slot))
        for s in range(last, -1, -1):
            n = slot - delays[s]

            @pl.when((n >= 0) & (n < pairs))
            def _(s=s, n=n):
                stages_q[s](n)
                if s == last:
                    for copy in store_q(n):
                        copy.start()

            @pl.when(slot == turns_o[s])
            def _(s=s):
                for n in range(out_chunks):
                    stages_o[s](n)
                    if s == last:
                        store_o(n).start()

        @pl.when(slot == pairs)
        def _():
            every(0, half, input_band)

        @pl.when(slot == pairs + 1)
        def _():
            every(half, 2 * half, input_band)
            results[0].start()

        pl.when(slot == pairs + 2)(smalls.swap)
        pl.when(slot == pairs + 3)(smalls.cross)
        pl.when(slot == pairs + 4)(smalls.spread)

        @pl.when(slot == pairs + 3)
        def _():
            late.arrived(EARLY_CHUNKS, groups, experts)
            every(0, 2 * EARLY_CHUNKS, lambda n: early_rows(n).wait())
            every(0, rows // band, output_band)
            results[1].start()

    every(0, pairs + delays[-1], slot_step)
    smalls.finish()

    def stored(i):
        for copy in store_q(i):
            copy.wait()

    every(0, pairs, stored)
    for result in results:
        result.wait()
    for n in range(out_chunks):
        store_o(n).wait()
    late.drain(EARLY_CHUNKS, groups, experts)
    reduce_o.drain()
    reduce_q.drain()
    smalls.drain()


def run_back(
    owners, capacity, gates, home_grad, far_sums, near_sums, home_out, back, hidden, cotangent, tokens,
    vectors, router_grad, act_t, merged_t, qkv, weight, w_out, low, high,
):
    rows, width = tokens.shape
    shard = width // 4
    lead = 8 + gates
    groups = owners // 2
    pairs = width // LANES
    tile_o = min(512, width)
    out_chunks = width // tile_o
    half = shard // 2
    mid = rows // 2
    any_spec = pl.BlockSpec(memory_space=pl.ANY)
    vmem_spec = pl.BlockSpec(memory_space=pltpu.VMEM)
    bf16, f32 = jnp.bfloat16, jnp.float32
    dma = pltpu.SemaphoreType.DMA

    def vm(*shape):
        return pltpu.VMEM(shape, bf16)

    def fm(*shape):
        return pltpu.VMEM(shape, f32)

    def reduce_buffers(chunks, tile, pair_first):
        far, pair = ((half,), (2, half)) if pair_first else ((shard,), (half,))
        return [
            vm(chunks, 2, 2, shard, tile),
            vm(chunks, 2, shard, tile),
            vm(chunks, *far, tile),
            vm(chunks, *pair, tile),
            vm(chunks, half // 2, tile),
            vm(chunks, half // 4, tile),
            vm(chunks, shard, tile),
        ]

    def reduce_sems(chunks):
        return [dma((8, chunks)), dma((8, chunks))]

    return pl.pallas_call(
        functools.partial(back_kernel, (owners, capacity, gates)),
        out_shape=(
            jax.ShapeDtypeStruct((rows, width), bf16),
            jax.ShapeDtypeStruct((rows, width), f32),
            jax.ShapeDtypeStruct((8, shard), f32),
            jax.ShapeDtypeStruct((gates, shard), f32),
            jax.ShapeDtypeStruct((shard, 3 * width), bf16),
            jax.ShapeDtypeStruct((shard, width), bf16),
        ),
        in_specs=[any_spec] * 5 + [vmem_spec] * 2 + [any_spec] * 10,
        out_specs=(any_spec,) * 2 + (vmem_spec,) * 2 + (any_spec,) * 2,
        scratch_shapes=[
            vm(*home_grad.shape),
            vm(rows, rows),
            fm(rows, width),
            vm(rows, width),
            vm(rows, width),
            vm(rows, width),
            fm(rows, width),
            vm(*near_sums.shape),
            vm(*near_sums.shape),
            vm(*home_grad.shape),
            vm(*home_grad.shape),
            vm(width, rows),
            vm(width, rows),
            vm(rows, 3 * width),
            vm(width, 3 * width),
            vm(width, width),
            vm(2, 2, mid, mid),
            vm(2, 2, mid, rows),
            vm(rows, width),
            vm(rows, width),
            fm(rows, width),
        ]
        + reduce_buffers(pairs, 3 * LANES, False)
        + reduce_buffers(out_chunks, tile_o, True)
        + [
            fm(lead, width),
            fm(2, 2, lead, shard),
            fm(2, lead, shard),
            fm(lead, shard),
            fm(lead, shard),
            fm(lead, shard),
            fm(owners, lead, shard),
            dma((7,)),
            dma((6,)),
            dma((2, 2)),
            dma((near_sums.shape[0],)),
            dma((owners,)),
            dma((groups, near_sums.shape[0])),
            dma((groups, near_sums.shape[0])),
            dma((owners, near_sums.shape[0])),
            dma((owners, near_sums.shape[0])),
        ]
        + reduce_sems(pairs)
        + reduce_sems(out_chunks)
        + [dma((2,)), dma((2,)), dma((owners,)), dma((owners,)), dma((4, pairs))],
        compiler_params=pltpu.CompilerParams(
            collective_id=2, has_side_effects=True, vmem_limit_bytes=VMEM_LIMIT
        ),
        name="back",
    )(
        home_grad, back, hidden, cotangent, tokens, vectors, router_grad,
        far_sums, near_sums, home_out, act_t, merged_t, qkv, weight, w_out, low, high,
    )


def widen_kernel(vectors_ref, *refs):
    count = (len(refs) - 4) // 2
    for src, dst in zip(refs[:count], refs[count:]):
        dst[...] = src[...].astype(dst.dtype)
    for i, dst in enumerate(refs[2 * count :]):
        dst[...] = vectors_ref[i, :]


def widen(steps, vectors, values, kinds):
    def spec(value):
        if value.shape[0] % (16 * steps):
            return pl.BlockSpec(value.shape, lambda i: (0, 0))
        return pl.BlockSpec((value.shape[0] // steps, value.shape[1]), lambda i: (i, 0))

    return pl.pallas_call(
        widen_kernel,
        grid=(steps,),
        in_specs=[pl.BlockSpec(vectors.shape, lambda i: (0, 0))]
        + [spec(value) for value in values],
        out_specs=[spec(value) for value in values]
        + [pl.BlockSpec((vectors.shape[1],), lambda i: (0,))] * 4,
        out_shape=[
            jax.ShapeDtypeStruct(value.shape, kind) for value, kind in zip(values, kinds)
        ]
        + [jax.ShapeDtypeStruct((vectors.shape[1],), jnp.float32)] * 4,
        name="widen",
    )(vectors, *values)


def on_device_plain(
    tokens,
    norm1_gain,
    norm1_shift,
    w_qkv,
    w_out,
    norm2_gain,
    norm2_shift,
    w_router,
    w_up,
    w_down,
    routes,
    priority,
    prefix,
    cotangent,
):
    row_count, model_width = tokens.shape
    expert_count = w_router.shape[1]
    capacity = row_count // expert_count
    owners = lax.axis_size("expert")
    local_experts = w_up.shape[0]
    slot_count = expert_count * capacity
    prefix_len = prefix[0]
    small = jnp.concatenate(
        [
            norm1_gain[None],
            norm1_shift[None],
            norm2_gain[None],
            norm2_shift[None],
            w_router.T,
        ],
        axis=0,
    )
    qkv_full = lax.all_gather(w_qkv, "wshard", axis=0, tiled=True)
    small_full = lax.all_gather(small, "wshard", axis=1, tiled=True)
    out_full = lax.all_gather(w_out, "wshard", axis=0, tiled=True)
    gain_one, shift_one, gain_two, shift_two = (small_full[i] for i in range(4))
    router_full = small_full[4:].T
    gain_one = gain_one.astype(jnp.float32)
    gain_two = gain_two.astype(jnp.float32)
    inputs = tokens.astype(jnp.float32)
    normed_one, scaled_one, inverse_one = normalize(inputs, gain_one, shift_one.astype(jnp.float32))
    act_one = normed_one.astype(jnp.bfloat16)
    qkv = jnp.dot(act_one, qkv_full, preferred_element_type=jnp.float32).astype(jnp.bfloat16)
    query_heads = qkv[:, :model_width]
    key_heads = qkv[:, model_width : 2 * model_width]
    value_heads = qkv[:, 2 * model_width :]
    merged, log_totals = attend_forward(query_heads, key_heads, value_heads, prefix_len)
    attn_out = jnp.dot(merged, out_full, preferred_element_type=jnp.float32)
    hidden = inputs + attn_out
    normed_two, scaled_two, inverse_two = normalize(hidden, gain_two, shift_two.astype(jnp.float32))
    act_two = normed_two.astype(jnp.bfloat16)
    logits = jnp.dot(act_two, router_full, preferred_element_type=jnp.float32)
    row_max = jnp.max(logits, axis=-1, keepdims=True)
    exponent = jnp.exp(logits - row_max)
    gate_prob = exponent / jnp.sum(exponent, axis=-1, keepdims=True)
    route_ids = routes[:, 0]
    chosen = route_ids[:, None] == jnp.arange(expert_count, dtype=jnp.int32)[None, :]
    gate_value = jnp.sum(jnp.where(chosen, gate_prob, 0.0), axis=1)
    slot_index, slot_source = assign_slots(route_ids, priority[0], expert_count, capacity)
    zero_row = jnp.zeros((1, model_width), jnp.bfloat16)
    padded = jnp.concatenate([act_two, zero_row], axis=0)
    send_rows = padded[slot_source].reshape(owners, local_experts * capacity, model_width)
    arrived = lax.all_to_all(send_rows, "expert", split_axis=0, concat_axis=0, tiled=True).reshape(
        owners, local_experts, capacity, model_width
    )
    group = lax.axis_size("wshard")
    local_rows = owners * capacity

    def by_expert(chunk):
        rows = jnp.transpose(chunk, (1, 0, 2, 3)).reshape(local_experts, local_rows, model_width)
        return lax.all_gather(rows, "wshard", axis=1, tiled=True)

    def home_rows(rows):
        own = lax.psum_scatter(rows.astype(jnp.bfloat16), "wshard", scatter_dimension=1, tiled=True)
        own = own.reshape(local_experts, owners, capacity, model_width)
        return jnp.transpose(own, (1, 0, 2, 3)).reshape(
            owners, local_experts * capacity, model_width
        )

    grad_output = cotangent.astype(jnp.float32)
    grad_combined = (gate_value[:, None] * grad_output).astype(jnp.bfloat16)
    grad_padded = jnp.concatenate([grad_combined, zero_row], axis=0)
    grad_send = grad_padded[slot_source].reshape(owners, local_experts * capacity, model_width)
    grad_arrived = lax.all_to_all(
        grad_send, "expert", split_axis=0, concat_axis=0, tiled=True
    ).reshape(owners, local_experts, capacity, model_width)
    rows_in = by_expert(arrived)
    grad_rows = by_expert(grad_arrived)
    pre_act = jnp.einsum("erd,edf->erf", rows_in, w_up, preferred_element_type=jnp.float32)
    activated, gelu_pull = jax.vjp(gelu_tanh, pre_act)
    act_hidden = activated.astype(jnp.bfloat16)
    produced = jnp.einsum(
        "erf,efd->erd", act_hidden, w_down, preferred_element_type=jnp.float32
    )
    expert_out = home_rows(produced)
    returned = lax.all_to_all(expert_out, "expert", split_axis=0, concat_axis=0, tiled=True)
    slots_back = jnp.concatenate([returned.reshape(slot_count, model_width), zero_row], axis=0)
    combined = slots_back[slot_index].astype(jnp.float32)
    output = (hidden + gate_value[:, None] * combined).astype(jnp.bfloat16)
    grad_gate = jnp.sum(grad_output * combined, axis=1)
    grad_down = jnp.einsum(
        "erf,erd->efd", act_hidden, grad_rows, preferred_element_type=jnp.float32
    )
    grad_hidden_units = jnp.einsum(
        "erd,efd->erf", grad_rows, w_down, preferred_element_type=jnp.float32
    )
    grad_pre = gelu_pull(grad_hidden_units)[0].astype(jnp.bfloat16)
    grad_up = jnp.einsum("erd,erf->edf", rows_in, grad_pre, preferred_element_type=jnp.float32)
    grad_expert_in = jnp.einsum(
        "erf,edf->erd", grad_pre, w_up, preferred_element_type=jnp.float32
    )
    grad_send_back = home_rows(grad_expert_in)
    grad_back = lax.all_to_all(grad_send_back, "expert", split_axis=0, concat_axis=0, tiled=True)
    grad_slots = jnp.concatenate([grad_back.reshape(slot_count, model_width), zero_row], axis=0)
    grad_act_two = grad_slots[slot_index].astype(jnp.float32)
    grad_logits = (
        gate_prob * (jnp.where(chosen, grad_gate[:, None], 0.0) - (gate_value * grad_gate)[:, None])
    ).astype(jnp.bfloat16)
    grad_router = contract_rows(act_two, grad_logits)
    grad_act_two = grad_act_two + times_transpose(grad_logits, router_full)
    grad_from_two, grad_gain_two, grad_shift_two = norm_back(
        grad_act_two, scaled_two, inverse_two, gain_two
    )
    grad_hidden = grad_output + grad_from_two
    grad_attn = grad_hidden.astype(jnp.bfloat16)
    grad_out_w = contract_rows(merged, grad_attn)
    grad_merged = times_transpose(grad_attn, out_full).astype(jnp.bfloat16)
    grad_qkv = attend_backward(
        query_heads, key_heads, value_heads, grad_merged, log_totals, prefix_len
    )
    grad_qkv_w = contract_rows(act_one, grad_qkv)
    grad_act_one = times_transpose(grad_qkv, qkv_full)
    grad_from_one, grad_gain_one, grad_shift_one = norm_back(
        grad_act_one, scaled_one, inverse_one, gain_one
    )
    grad_tokens = grad_hidden + grad_from_one
    small_grad = jnp.concatenate(
        [
            grad_gain_one[None],
            grad_shift_one[None],
            grad_gain_two[None],
            grad_shift_two[None],
            grad_router.T,
        ],
        axis=0,
    )
    out_share = lax.psum_scatter(
        grad_out_w.astype(jnp.bfloat16), "wshard", scatter_dimension=0, tiled=True
    )
    qkv_share = lax.psum_scatter(
        grad_qkv_w.astype(jnp.bfloat16), "wshard", scatter_dimension=0, tiled=True
    )
    small_share = lax.psum_scatter(small_grad, "wshard", scatter_dimension=1, tiled=True)
    out_total = lax.psum(out_share, "expert").astype(jnp.float32)
    qkv_total = lax.psum(qkv_share, "expert").astype(jnp.float32)
    small_total = lax.psum(small_share, "expert")
    totals = (
        small_total[0],
        small_total[1],
        qkv_total,
        out_total,
        small_total[2],
        small_total[3],
        small_total[4:].T,
    )
    return (
        output,
        grad_tokens,
        totals[0],
        totals[1],
        totals[2],
        totals[3],
        totals[4],
        totals[5],
        totals[6],
        grad_up,
        grad_down,
    )


def on_device(
    tokens,
    norm1_gain,
    norm1_shift,
    w_qkv,
    w_out,
    norm2_gain,
    norm2_shift,
    w_router,
    w_up,
    w_down,
    routes,
    priority,
    prefix,
    cotangent,
):
    row_count, model_width = tokens.shape
    expert_count = w_router.shape[1]
    capacity = row_count // expert_count
    owners = lax.axis_size("expert")
    experts = w_up.shape[0]
    (
        qkv, act_t, merged_t, back, weight, out_full, low, high, grad_rows, hidden, send_rows,
        vectors, router,
    ) = run_front(
        owners, experts, capacity, prefix, routes.reshape(1, row_count), priority,
        (norm1_gain, norm1_shift, norm2_gain, norm2_shift), tokens, cotangent, w_router.T, w_qkv,
        w_out,
    )
    far_sums, near_sums, home_out, home_grad, grad_up, grad_down, grad_router = run_experts(
        owners, capacity, expert_count, send_rows, grad_rows, w_up, w_down, router
    )
    output, grad_tokens, grad_vectors, grad_gates, grad_qkv, grad_out = run_back(
        owners, capacity, expert_count, home_grad, far_sums, near_sums, home_out, back, hidden, cotangent,
        tokens, vectors, grad_router, act_t, merged_t, qkv, weight, out_full, low, high,
    )
    f32 = jnp.float32
    units = w_up.shape[2]
    (
        output, grad_tokens, grad_gates, grad_qkv, grad_out, grad_up, grad_down, *grad_vectors,
    ) = widen(
        2,
        grad_vectors,
        (
            output, grad_tokens, grad_gates, grad_qkv, grad_out,
            grad_up.reshape(-1, units), grad_down.reshape(-1, model_width),
        ),
        (output.dtype,) + (f32,) * 6,
    )
    return (
        output,
        grad_tokens,
        grad_vectors[0],
        grad_vectors[1],
        grad_qkv,
        grad_out,
        grad_vectors[2],
        grad_vectors[3],
        grad_gates.T,
        grad_up.reshape(w_up.shape),
        grad_down.reshape(w_down.shape),
    )


def solution(mesh):
    placed = (
        P(("expert", "wshard"), None),
        P("wshard"),
        P("wshard"),
        P("wshard", None),
        P("wshard", None),
        P("wshard"),
        P("wshard"),
        P("wshard", None),
        P("expert", None, "wshard"),
        P("expert", "wshard", None),
        P(("expert", "wshard"), None),
        P(("expert", "wshard"), None),
        P(("expert", "wshard")),
        P(("expert", "wshard"), None),
    )
    owners, group = mesh.shape["expert"], mesh.shape["wshard"]

    def body(*args):
        capacity = args[0].shape[0] // args[7].shape[1]
        fits = group == 4 and owners == 8 and capacity % 16 == 0 and args[7].shape[1] % 16 == 0
        return (on_device if fits else on_device_plain)(*args)

    return jax.shard_map(
        body,
        mesh=mesh,
        in_specs=placed,
        out_specs=(
            P(("expert", "wshard"), None),
            P(("expert", "wshard"), None),
            P("wshard"),
            P("wshard"),
            P("wshard", None),
            P("wshard", None),
            P("wshard"),
            P("wshard"),
            P("wshard", None),
            P("expert", None, "wshard"),
            P("expert", "wshard", None),
        ),
        check_vma=False,
    )
```

```python
import functools
import math

import jax
import jax.numpy as jnp
from jax import lax
from jax.experimental import pallas as pl
from jax.experimental.pallas import tpu as pltpu
from jax.sharding import PartitionSpec as P

HEADS = 16
HEAD_DIM = 64


epsilon = 1e-05
VMEM_LIMIT = 66_000_000
TILE = 1024
EARLY_CHUNKS = 2


def normalize(values, gain_vec, shift_vec):
    row_mean = jnp.mean(values, axis=-1, keepdims=True)
    centered = values - row_mean
    inverse = lax.rsqrt(jnp.mean(centered * centered, axis=-1, keepdims=True) + epsilon)
    scaled = centered * inverse
    return (scaled * gain_vec + shift_vec, scaled, inverse)


def norm_back(grad_rows, scaled, inverse, gain_vec):
    weighted = grad_rows * gain_vec
    mean_one = jnp.mean(weighted, axis=-1, keepdims=True)
    mean_two = jnp.mean(weighted * scaled, axis=-1, keepdims=True)
    grad_inputs = inverse * (weighted - mean_one - scaled * mean_two)
    return (grad_inputs, jnp.sum(grad_rows * scaled, axis=0), jnp.sum(grad_rows, axis=0))


def contract_rows(left, right):
    return lax.dot_general(
        left, right, (((0,), (0,)), ((), ())), preferred_element_type=jnp.float32
    )


def times_transpose(left, right):
    return lax.dot_general(
        left, right, (((1,), (1,)), ((), ())), preferred_element_type=jnp.float32
    )


def gelu_tanh(values):
    return jax.nn.gelu(values, approximate=True)


def assign_slots(route_ids, order_ids, expert_count, capacity):
    token_count = route_ids.shape[0]
    same_expert = route_ids[:, None] == route_ids[None, :]
    earlier = order_ids[None, :] < order_ids[:, None]
    rank_ids = jnp.sum((same_expert & earlier).astype(jnp.int32), axis=1)
    is_kept = rank_ids < capacity
    slot_index = jnp.where(is_kept, route_ids * capacity + rank_ids, expert_count * capacity)
    slot_ids = jnp.arange(expert_count * capacity, dtype=jnp.int32)
    match_table = slot_index[None, :] == slot_ids[:, None]
    token_ids = jnp.arange(token_count, dtype=jnp.int32)
    filled = jnp.any(match_table, axis=1)
    picked = jnp.sum(jnp.where(match_table, token_ids[None, :], 0), axis=1)
    slot_source = jnp.where(filled, picked, token_count)
    return (slot_index, slot_source)


def group_heads(values, groups):
    token_count = values.shape[0]
    return jnp.transpose(values.reshape(token_count, groups, -1, HEAD_DIM), (1, 0, 2, 3))


def block_scores(query_block, key_group, block_start, prefix_len):
    block_rows = query_block.shape[0]
    key_count = key_group.shape[0]
    scores = jnp.einsum(
        "qgd,kgd->gqk", query_block, key_group, preferred_element_type=jnp.float32
    ) * (1.0 / math.sqrt(HEAD_DIM))
    query_pos = block_start + jnp.arange(block_rows, dtype=jnp.int32)
    key_pos = jnp.arange(key_count, dtype=jnp.int32)
    allowed = (key_pos[None, :] <= query_pos[:, None]) | (key_pos[None, :] < prefix_len)
    return jnp.where(allowed[None], scores, -1e30)


def attend_forward(query_heads, key_heads, value_heads, prefix_len):
    token_count = query_heads.shape[0]
    group_size = min(4, HEADS)
    groups = HEADS // group_size
    block_rows = min(512, token_count)
    blocks = token_count // block_rows
    starts = jnp.arange(blocks, dtype=jnp.int32) * block_rows

    def one_group(group_item):
        query_group, key_group, value_group = group_item
        query_blocks = query_group.reshape(blocks, block_rows, group_size, HEAD_DIM)

        def one_block(block_item):
            query_block, block_start = block_item
            scores = block_scores(query_block, key_group, block_start, prefix_len)
            row_max = jnp.max(scores, axis=-1, keepdims=True)
            exponent = jnp.exp(scores - row_max)
            row_total = jnp.sum(exponent, axis=-1, keepdims=True)
            attn_probs = (exponent / row_total).astype(jnp.bfloat16)
            result = jnp.einsum(
                "gqk,kgd->qgd", attn_probs, value_group, preferred_element_type=jnp.float32
            )
            return (result, (row_max + jnp.log(row_total))[..., 0])

        return lax.map(one_block, (query_blocks, starts))

    attended, log_totals = lax.map(
        one_group,
        (
            group_heads(query_heads, groups),
            group_heads(key_heads, groups),
            group_heads(value_heads, groups),
        ),
    )
    merged = (
        jnp.transpose(attended, (1, 2, 0, 3, 4))
        .reshape(token_count, HEADS * HEAD_DIM)
        .astype(jnp.bfloat16)
    )
    return (merged, log_totals)


def attend_backward(query_heads, key_heads, value_heads, grad_merged, log_totals, prefix_len):
    token_count = query_heads.shape[0]
    group_size = min(4, HEADS)
    groups = HEADS // group_size
    block_rows = min(512, token_count)
    blocks = token_count // block_rows
    starts = jnp.arange(blocks, dtype=jnp.int32) * block_rows
    score_scale = 1.0 / math.sqrt(HEAD_DIM)

    def one_group(group_item):
        query_group, key_group, value_group, grad_group, total_group = group_item
        query_blocks = query_group.reshape(blocks, block_rows, group_size, HEAD_DIM)
        grad_blocks = grad_group.reshape(blocks, block_rows, group_size, HEAD_DIM)

        def one_block(carry, block_item):
            grad_keys, grad_vals = carry
            query_block, grad_block, total_block, block_start = block_item
            scores = block_scores(query_block, key_group, block_start, prefix_len)
            attn_probs = jnp.exp(scores - total_block[..., None])
            grad_probs = jnp.einsum(
                "qgd,kgd->gqk", grad_block, value_group, preferred_element_type=jnp.float32
            )
            row_delta = jnp.sum(attn_probs * grad_probs, axis=-1, keepdims=True)
            grad_scores = (attn_probs * (grad_probs - row_delta)).astype(jnp.bfloat16)
            grad_vals = grad_vals + jnp.einsum(
                "gqk,qgd->kgd",
                attn_probs.astype(jnp.bfloat16),
                grad_block,
                preferred_element_type=jnp.float32,
            )
            grad_keys = (
                grad_keys
                + jnp.einsum(
                    "gqk,qgd->kgd", grad_scores, query_block, preferred_element_type=jnp.float32
                )
                * score_scale
            )
            grad_query = (
                jnp.einsum(
                    "gqk,kgd->qgd", grad_scores, key_group, preferred_element_type=jnp.float32
                )
                * score_scale
            )
            return ((grad_keys, grad_vals), grad_query)

        zero_keys = jnp.zeros(key_group.shape, jnp.float32)
        carried, grad_queries = lax.scan(
            one_block, (zero_keys, zero_keys), (query_blocks, grad_blocks, total_group, starts)
        )
        return (grad_queries, carried[0], carried[1])

    grad_queries, grad_keys, grad_vals = lax.map(
        one_group,
        (
            group_heads(query_heads, groups),
            group_heads(key_heads, groups),
            group_heads(value_heads, groups),
            group_heads(grad_merged, groups),
            log_totals,
        ),
    )
    query_part = jnp.transpose(grad_queries, (1, 2, 0, 3, 4)).reshape(token_count, HEADS * HEAD_DIM)
    key_part = jnp.transpose(grad_keys, (1, 0, 2, 3)).reshape(token_count, HEADS * HEAD_DIM)
    value_part = jnp.transpose(grad_vals, (1, 0, 2, 3)).reshape(token_count, HEADS * HEAD_DIM)
    return jnp.concatenate([query_part, key_part, value_part], axis=1).astype(jnp.bfloat16)


MESH = pl.DeviceIdType.MESH
LANES = 128


def dot_nn(left, right):
    return lax.dot_general(
        left, right, (((1,), (0,)), ((), ())), preferred_element_type=jnp.float32
    )


def dot_nt(left, right):
    return lax.dot_general(
        left, right, (((1,), (1,)), ((), ())), preferred_element_type=jnp.float32
    )


def dot_tn(left, right):
    return lax.dot_general(
        left, right, (((0,), (0,)), ((), ())), preferred_element_type=jnp.float32
    )


def span(start, size):
    return pl.ds(pl.multiple_of(start, size), size)


def every(start, stop, step):
    def body(i, carry):
        step(i)
        return carry

    lax.fori_loop(start, stop, body, 0)


class Place:
    def __init__(self, owners):
        self.owners = owners
        self.e = lax.axis_index("expert")
        self.w = lax.axis_index("wshard")
        self.c = lax.rem(self.w, 2)
        self.x = lax.div(self.w, 2)
        self.sib = self.w + 1 - 2 * self.c
        self.far = lax.rem(self.w + 2, 4)
        self.diag = 3 - self.w
        self.pair = self.e + 1 - 2 * lax.rem(self.e, 2)

    def ahead(self, k):
        return lax.rem(self.e + k, self.owners)

    def flip(self, bit):
        return self.e + bit * (1 - 2 * lax.rem(lax.div(self.e, bit), 2))

    def peer(self, n):
        other = lax.div(n, 2) + lax.rem(n, 2) * (self.owners // 2)
        result, bit = 0, 1
        while bit < self.owners:
            result = result + bit * lax.rem(lax.div(self.e, bit) + lax.div(other, bit), 2)
            bit *= 2
        return result


def remote(src, dst, send, recv, device):
    return pltpu.make_async_remote_copy(
        src_ref=src,
        dst_ref=dst,
        send_sem=send,
        recv_sem=recv,
        device_id=device,
        device_id_type=MESH,
    )


def greet(peers):
    barrier = pltpu.get_barrier_semaphore()
    for peer in peers:
        pl.semaphore_signal(barrier, inc=1, device_id=peer, device_id_type=MESH)
    pl.semaphore_wait(barrier, len(peers))


def either(test, yes, no):
    pl.when(test)(yes)
    pl.when(jnp.logical_not(test))(no)


class Dispatch:
    def __init__(self, place, capacity, send_ref, rows_ref, sems):
        self.p, self.cap, self.src, self.rows = place, capacity, send_ref, rows_ref
        self.own_sem, self.send, self.recv = sems

    def slice(self, k, core, side):
        start = (((lax.div(k, 2) * 2 + core) * 2 + side) * 2 + lax.rem(k, 2)) * self.cap
        return self.rows.at[:, span(start, self.cap)]

    def own(self):
        return pltpu.make_async_copy(
            self.src.at[self.p.e], self.slice(0, self.p.c, self.p.x), self.own_sem
        )

    def direct(self, k):
        return remote(
            self.src.at[self.p.peer(k)],
            self.slice(k, self.p.c, self.p.x),
            self.send.at[0, k],
            self.recv.at[0, k],
            (self.p.peer(k), self.p.w),
        )

    def hop(self, k, side, which, peer):
        part = self.slice(k, self.p.c, side)
        return remote(
            part, part, self.send.at[which, k], self.recv.at[which, k], (self.p.e, peer)
        )

    def to_sib(self, k):
        return self.hop(k, self.p.x, 1, self.p.sib)

    def to_far(self, k):
        return self.hop(k, self.p.x, 2, self.p.far)

    def relayed(self, k):
        return self.hop(k, 1 - self.p.x, 3, self.p.sib)

    def start(self):
        self.own().start()
        every(1, self.p.owners, lambda k: self.direct(k).start())

    def forward(self, k):
        k = jnp.int32(k)

        @pl.when(k == 0)
        def _():
            self.own().wait()

        @pl.when(k > 0)
        def _():
            self.direct(k).wait_recv()

        self.to_far(k).start()
        self.to_sib(k).start()

    def relay(self, k):
        self.to_far(k).wait_recv()
        self.relayed(k).start()

    def ready(self, k):
        self.to_sib(k).wait_recv()
        self.relayed(k).wait_recv()

    def order(self):
        return (0, 2, 4, 1, 6, 3, 5, 7)

    def drain(self):
        every(1, self.p.owners, lambda k: self.direct(k).wait_send())

        def rest(k):
            self.to_sib(k).wait_send()
            self.to_far(k).wait_send()
            self.relayed(k).wait_send()

        every(0, self.p.owners, rest)


class Return:
    def __init__(self, place, capacity, part, got, mid, far, done, home, sems):
        self.p, self.cap = place, capacity
        self.part, self.got, self.mid, self.far, self.done, self.home = (
            part, got, mid, far, done, home,
        )
        self.own_sem, self.send, self.recv, self.home_send, self.home_recv = sems

    def swapped(self, j, expert):
        size = 4 * self.cap
        return remote(
            self.part.at[expert, span((j * 2 + 1 - self.p.c) * size, size)],
            self.got.at[expert, span(j * size, size)],
            self.send.at[0, j, expert],
            self.recv.at[0, j, expert],
            (self.p.e, self.p.sib),
        )

    def crossed(self, j, expert):
        part = span(j * 2 * self.cap, 2 * self.cap)
        return remote(
            self.mid.at[expert, part],
            self.far.at[expert, part],
            self.send.at[1, j, expert],
            self.recv.at[1, j, expert],
            (self.p.e, self.p.far),
        )

    def own(self, expert):
        return pltpu.make_async_copy(
            self.done.at[0, expert], self.home.at[self.p.e, expert], self.own_sem.at[expert]
        )

    def homed(self, n, expert):
        return remote(
            self.done.at[n, expert],
            self.home.at[self.p.e, expert],
            self.home_send.at[n, expert],
            self.home_recv.at[n, expert],
            (self.p.peer(n), self.p.w),
        )

    def pair_sum(self, j, expert, side):
        size = 2 * self.cap
        mine = self.part[expert, span(((j * 2 + self.p.c) * 2 + side) * size, size), :]
        theirs = self.got[expert, span((j * 2 + side) * size, size), :]
        return mine.astype(jnp.float32) + theirs.astype(jnp.float32)

    def swap(self, j, expert):
        self.swapped(j, expert).start()

    def split(self, j, expert):
        self.swapped(j, expert).wait_recv()
        here = span(j * 2 * self.cap, 2 * self.cap)
        self.mid[expert, here, :] = self.pair_sum(j, expert, 1 - self.p.x).astype(jnp.bfloat16)
        self.keep[expert, here, :] = self.pair_sum(j, expert, self.p.x).astype(jnp.bfloat16)

    def cross(self, j, expert):
        self.swapped(j, expert).wait_recv()
        here = span(j * 2 * self.cap, 2 * self.cap)
        self.mid[expert, here, :] = self.pair_sum(j, expert, 1 - self.p.x).astype(jnp.bfloat16)
        self.crossed(j, expert).start()

    def this_side(self, j, expert):
        return self.pair_sum(j, expert, self.p.x)

    def finish(self, j, expert):
        self.crossed(j, expert).wait_recv()
        here = span(j * 2 * self.cap, 2 * self.cap)
        total = self.this_side(j, expert) + self.far[expert, here, :].astype(jnp.float32)
        total = total.astype(jnp.bfloat16)
        self.done[2 * j, expert] = total[: self.cap]
        self.done[2 * j + 1, expert] = total[self.cap :]
        j = jnp.int32(j)
        self.homed(2 * j + 1, expert).start()
        either(
            j == 0,
            lambda: self.own(expert).start(),
            lambda: self.homed(2 * j, expert).start(),
        )

    def drain_swaps(self, chunks, experts):
        for expert in range(experts):
            every(0, chunks, lambda j: self.swapped(j, expert).wait_send())

    def drain(self, first, last, experts):
        for expert in range(experts):
            every(first, last, lambda j: self.crossed(j, expert).wait_send())
            every(
                max(1, 2 * first), 2 * last, lambda n: self.homed(n, expert).wait_send()
            )

    def arrived(self, first, last, experts):
        for expert in range(experts):
            if first == 0 and last > 0:
                self.own(expert).wait()
            every(
                max(1, 2 * first), 2 * last, lambda n: self.homed(n, expert).wait_recv()
            )


class LateReturn(Return):
    def crossed(self, j, expert):
        part = span(j * 2 * self.cap, 2 * self.cap)
        return remote(
            self.mid.at[expert, part],
            self.far.at[expert, part],
            self.send.at[j, expert],
            self.recv.at[j, expert],
            (self.p.e, self.p.far),
        )

    def this_side(self, j, expert):
        here = span(j * 2 * self.cap, 2 * self.cap)
        return self.part[expert, here, :].astype(jnp.float32)


def gelu_pair(v):
    root = math.sqrt(2.0 / math.pi)
    square = v * v
    t = jnp.tanh(v * (root + (root * 0.044715) * square))
    half = 0.5 + 0.5 * t
    slope = half + (half * (1.0 - t)) * (v * (root + (3.0 * root * 0.044715) * square))
    return v * half, slope


def expert_kernel(
    dims,
    send_ref, grads_hbm, up_hbm, down_hbm, router_ref,
    far_sums, near_sums, home_out, home_grad, up_out, down_out, router_grad,
    rows, grads, scaled, hidden, pre, up, down, grad_up, grad_down,
    part_out, part_grad, got_out, got_grad, mid_out, mid_grad,
    keep_out, far_grad, far_out, done_grad, done_out,
    load_sem, own_sem, disp_send, disp_recv, red_send, red_recv, home_send, home_recv,
):
    owners, experts, capacity, width, units, expert_count = dims
    place = Place(owners)
    loads = [
        pltpu.make_async_copy(src, dst, load_sem.at[i])
        for i, (src, dst) in enumerate(
            [(up_hbm, up), (grads_hbm, grads), (down_hbm, down)]
        )
    ]
    for load in loads:
        load.start()
    greet(
        [(place.ahead(k), place.w) for k in range(1, owners)]
        + [(place.e, place.sib), (place.e, place.far)]
    )
    dispatch = Dispatch(
        place, capacity, send_ref, rows, (own_sem.at[0, 0], disp_send, disp_recv)
    )
    ret_grad = Return(
        place, capacity, part_grad, got_grad, mid_grad, far_grad, done_grad, home_grad,
        (own_sem.at[1], red_send.at[0], red_recv.at[0], home_send.at[0], home_recv.at[0]),
    )
    ret_out = Return(
        place, capacity, part_out, got_out, mid_out, far_out, done_out, home_out,
        (own_sem.at[2], red_send.at[1], red_recv.at[1], home_send.at[1], home_recv.at[1]),
    )
    dispatch.start()
    router_grad[...] = jnp.zeros_like(router_grad)
    tile = min(TILE, units)
    wide = min(TILE, width)
    chunks = owners // 2
    early = EARLY_CHUNKS
    size = 8 * capacity
    lane = lax.broadcasted_iota(jnp.int32, (size, LANES), 1)

    def compute(j, expert):
        here = span(j * size, size)
        logits = dot_nt(rows[expert, here, :], router_ref[...])
        logits = jnp.where(lane < expert_count, logits, -1e30)
        exponent = jnp.exp(logits - jnp.max(logits, axis=1, keepdims=True))
        prob = exponent * (1.0 / jnp.sum(exponent, axis=1, keepdims=True))
        mine = lane == place.e * experts + expert
        gate = jnp.sum(jnp.where(mine, prob, 0.0), axis=1, keepdims=True)
        scaled[expert, here, :] = (
            gate * grads[expert, here, :].astype(jnp.float32)
        ).astype(jnp.bfloat16)

        def one_tile(n):
            cols = span(n * tile, tile)
            value, slope = gelu_pair(dot_nn(rows[expert, here, :], up[expert, :, cols]))
            hidden[expert, here, cols] = value.astype(jnp.bfloat16)
            back = pre[expert, here, cols].astype(jnp.float32)
            pre[expert, here, cols] = (gate * back * slope).astype(jnp.bfloat16)

        every(0, units // tile, one_tile)

        def one_out(n, total):
            cols = span(n * wide, wide)
            value = dot_nn(hidden[expert, here, :], down[expert, :, cols])
            part_out[expert, here, cols] = (gate * value).astype(jnp.bfloat16)
            weighted = value * grads[expert, here, cols].astype(jnp.float32)
            for start in range(0, wide, LANES):
                total = total + weighted[:, start : start + LANES]
            return total

        total = lax.fori_loop(
            0, width // wide, one_out, jnp.zeros((size, LANES), jnp.float32)
        )
        grad_gate = jnp.sum(total, axis=1, keepdims=True)
        grad_logits = (
            prob * ((jnp.where(mine, 1.0, 0.0) - gate) * grad_gate)
        ).astype(jnp.bfloat16)

        def one_in(n):
            cols = span(n * wide, wide)
            value = dot_nt(pre[expert, here, :], up[expert, cols, :]) + dot_nn(
                grad_logits, router_ref[:, cols]
            )
            part_grad[expert, here, cols] = value.astype(jnp.bfloat16)
            router_grad[:, cols] += dot_tn(grad_logits, rows[expert, here, cols])

        every(0, width // wide, one_in)

    def unscaled(j, expert):
        here = span(j * size, size)
        pre[expert, here, :] = dot_nt(grads[expert, here, :], down[expert]).astype(jnp.bfloat16)

    block = min(256, width)

    def weight_grads(expert, first, last):
        def one(n):
            part = span(n * block, block)
            grad_down[expert, part, :] = dot_tn(
                hidden[expert, :, part], scaled[expert]
            ).astype(jnp.bfloat16)
            grad_up[expert, part, :] = dot_tn(rows[expert, :, part], pre[expert]).astype(
                jnp.bfloat16
            )

        every(first * width // block // 4, last * width // block // 4, one)

    def keep(expert):
        return [
            pltpu.make_async_copy(src.at[expert], dst.at[expert], load_sem.at[2 * expert + i])
            for i, (src, dst) in enumerate(((grad_up, up_out), (grad_down, down_out)))
        ]

    turns = [(j, expert) for j in range(chunks) for expert in range(experts)]
    ahead, through, here = dispatch.forward, dispatch.relay, dispatch.ready
    plan = [[] for _ in turns]
    for unit, acts in (
        (0, ((here, 0), (here, 1), (ahead, 5))),
        (1, ((through, 6), (ahead, 7))),
        (2, ((through, 3), (here, 2), (here, 3))),
        (3, ((through, 5),)),
        (4, ((through, 7), (here, 4), (here, 5))),
        (6, ((here, 6), (here, 7))),
    ):
        plan[unit].extend(acts)
    for u in range(2, len(turns)):
        done = turns[u - 2]
        plan[u].append((ret_grad.cross,) + done)
        plan[u].append((ret_out.cross if done[0] < early else ret_out.split,) + done)
        if u >= 4:
            done = turns[u - 4]
            plan[u].append((ret_grad.finish,) + done)
            if done[0] < early:
                plan[u].append((ret_out.finish,) + done)
    ret_out.keep = keep_out
    for load in loads:
        load.wait()

    def unscaled_pair(j):
        for expert in range(experts):
            unscaled(j, expert)

    ahead(0)
    unscaled_pair(0)
    unscaled_pair(1)
    ahead(2)
    ahead(4)
    ahead(1)
    unscaled_pair(2)
    through(0)
    unscaled_pair(3)
    through(2)
    ahead(6)
    through(4)
    through(1)
    ahead(3)

    def step(unit):
        for u, acts in enumerate(plan):

            @pl.when(unit == u)
            def _(acts=acts):
                for act, *at in acts:
                    act(*at)

        j, expert = lax.div(unit, experts), lax.rem(unit, experts)
        compute(j, expert)
        ret_grad.swap(j, expert)
        ret_out.swap(j, expert)

    every(0, len(turns), step)
    ret_grad.cross(*turns[-2])
    ret_out.split(*turns[-2])
    ret_grad.finish(*turns[-4])
    weight_grads(0, 0, 1)
    ret_grad.cross(*turns[-1])
    ret_out.split(*turns[-1])
    sums = [
        pltpu.make_async_copy(src, dst, load_sem.at[4 + i])
        for i, (src, dst) in enumerate(((mid_out, far_sums), (keep_out, near_sums)))
    ]
    for store in sums:
        store.start()
    ret_grad.finish(*turns[-3])
    weight_grads(0, 1, 2)
    ret_grad.finish(*turns[-2])
    weight_grads(0, 2, 3)
    ret_grad.finish(*turns[-1])
    weight_grads(0, 3, 4)
    for store in keep(0):
        store.start()
    for expert in range(1, experts):
        weight_grads(expert, 0, 4)
        for store in keep(expert):
            store.start()
    for expert in range(experts):
        for store in keep(expert):
            store.wait()
    for store in sums:
        store.wait()
    dispatch.drain()
    ret_grad.drain_swaps(chunks, experts)
    ret_grad.drain(0, chunks, experts)
    ret_grad.arrived(0, chunks, experts)
    ret_out.drain_swaps(chunks, experts)
    ret_out.drain(0, early, experts)
    ret_out.arrived(0, early, experts)


def run_experts(owners, capacity, expert_count, send_rows, grads, w_up, w_down, router):
    experts, width, units = w_up.shape
    slots = owners * 4 * capacity
    chunks = owners // 2
    dims = (owners, experts, capacity, width, units, expert_count)
    any_spec = pl.BlockSpec(memory_space=pl.ANY)
    vmem_spec = pl.BlockSpec(memory_space=pltpu.VMEM)
    bf16 = jnp.bfloat16
    home = jax.ShapeDtypeStruct((owners, experts, capacity, width), bf16)
    dma = pltpu.SemaphoreType.DMA

    def vm(*shape):
        return pltpu.VMEM(shape, bf16)

    return pl.pallas_call(
        functools.partial(expert_kernel, dims),
        out_shape=(
            jax.ShapeDtypeStruct((experts, slots // 4, width), bf16),
            jax.ShapeDtypeStruct((experts, slots // 4, width), bf16),
            home, home,
            jax.ShapeDtypeStruct(w_up.shape, bf16),
            jax.ShapeDtypeStruct(w_down.shape, bf16),
            jax.ShapeDtypeStruct((LANES, width), jnp.float32),
        ),
        in_specs=[any_spec] * 4 + [vmem_spec],
        out_specs=(any_spec,) * 6 + (vmem_spec,),
        scratch_shapes=[
            vm(experts, slots, width),
            vm(experts, slots, width),
            vm(experts, slots, width),
            vm(experts, slots, units),
            vm(experts, slots, units),
            vm(experts, width, units),
            vm(experts, units, width),
            vm(experts, width, units),
            vm(experts, units, width),
            vm(experts, slots, width),
            vm(experts, slots, width),
            vm(experts, slots // 2, width),
            vm(experts, slots // 2, width),
            vm(experts, slots // 4, width),
            vm(experts, slots // 4, width),
            vm(experts, slots // 4, width),
            vm(experts, slots // 4, width),
            vm(experts, slots // 4, width),
            vm(owners, experts, capacity, width),
            vm(owners, experts, capacity, width),
            dma((6,)),
            dma((3, experts)),
            dma((4, owners)),
            dma((4, owners)),
            dma((2, 2, chunks, experts)),
            dma((2, 2, chunks, experts)),
            dma((2, owners, experts)),
            dma((2, owners, experts)),
        ],
        compiler_params=pltpu.CompilerParams(
            collective_id=1, has_side_effects=True, vmem_limit_bytes=VMEM_LIMIT
        ),
        name="experts",
    )(send_rows, grads, w_up, w_down, router)


def masked_softmax(scores):
    exponent = jnp.exp(scores - jnp.max(scores, axis=1, keepdims=True))
    return exponent * (1.0 / jnp.sum(exponent, axis=1, keepdims=True))


def attend_head(query, key, value, prefix_len):
    half = query.shape[0] // 2
    query = query * (1.0 / math.sqrt(HEAD_DIM))
    row = lax.broadcasted_iota(jnp.int32, (half, half), 0)
    col = lax.broadcasted_iota(jnp.int32, (half, half), 1)
    low = dot_nt(query[:half], key[:half])
    low = jnp.where((col <= row) | (col < prefix_len), low, -1e30)
    low = masked_softmax(low).astype(jnp.bfloat16)
    high = dot_nt(query[half:], key)
    high = jnp.concatenate(
        [high[:, :half], jnp.where(col <= row, high[:, half:], -1e30)], axis=1
    )
    high = masked_softmax(high).astype(jnp.bfloat16)
    return low, high, dot_nn(low, value[:half]), dot_nn(high, value)


def score_grads(probs, grad_probs):
    probs = probs.astype(jnp.float32)
    weighted = probs * grad_probs
    total = jnp.sum(weighted, axis=1, keepdims=True)
    return (weighted - probs * total).astype(jnp.bfloat16)


def attend_back_head(query, key, value, low, high, grad):
    half = query.shape[0] // 2
    scale = 1.0 / math.sqrt(HEAD_DIM)
    query = query * scale
    grad_low = score_grads(low, dot_nt(grad[:half], value[:half]))
    grad_high = score_grads(high, dot_nt(grad[half:], value))
    grad_query = jnp.concatenate(
        [dot_nn(grad_low, key[:half]), dot_nn(grad_high, key)], axis=0
    )
    value_all = dot_tn(high, grad[half:])
    key_all = dot_tn(grad_high, query[half:])
    grad_value = jnp.concatenate(
        [value_all[:half] + dot_tn(low, grad[:half]), value_all[half:]], axis=0
    )
    grad_key = jnp.concatenate(
        [key_all[:half] + dot_tn(grad_low, query[:half]), key_all[half:]], axis=0
    )
    return (
        (grad_query * scale).astype(jnp.bfloat16),
        grad_key.astype(jnp.bfloat16),
        grad_value.astype(jnp.bfloat16),
    )


class Gather:
    def __init__(self, place, pieces, parts, src, dst, sems):
        self.p, self.src, self.dst, self.pieces, self.parts = place, src, dst, pieces, parts
        self.send, self.recv = sems
        self.shard = src.shape[0]
        self.half = self.shard // 2
        self.width = src.shape[1] // parts
        self.step = self.width // pieces
        self.first = lax.rem(place.e, 2) * self.half
        self.second = self.half - self.first

    def cols(self, n, part):
        return span(part * self.width + n * self.step, self.step)

    def block(self, owner, start, size, n, part):
        rows = pl.ds(pl.multiple_of(owner * self.shard + start, self.half), size)
        return self.dst.at[rows, self.cols(n, part)]

    def move(self, which, n, part, src, dst, device):
        return remote(
            src, dst, self.send.at[which, n, part], self.recv.at[which, n, part], device
        )

    def own(self, n, part):
        return pltpu.make_async_copy(
            self.src.at[:, self.cols(n, part)],
            self.block(self.p.w, 0, self.shard, n, part),
            self.recv.at[5, n, part],
        )

    def near(self, n, part):
        return self.move(
            4, n, part, self.src.at[:, self.cols(n, part)],
            self.block(self.p.w, 0, self.shard, n, part), (self.p.e, self.p.sib),
        )

    def hop(self, n, part):
        return self.move(
            0, n, part, self.src.at[span(self.first, self.half), self.cols(n, part)],
            self.block(self.p.w, self.first, self.half, n, part), (self.p.e, self.p.far),
        )

    def pass_from(self, which, start, n, part, device):
        block = self.block(self.p.far, start, self.half, n, part)
        return self.move(which, n, part, block, block, device)

    def pairs(self, n, part):
        return self.pass_from(1, self.first, n, part, (self.p.pair, self.p.w))

    def relay(self, n, part):
        return self.pass_from(2, self.first, n, part, (self.p.e, self.p.sib))

    def pair_relay(self, n, part):
        return self.pass_from(3, self.second, n, part, (self.p.e, self.p.sib))

    def all_parts(self, n, act):
        for part in range(self.parts):
            act(n, part)

    def start_own(self):
        every(
            0, self.pieces, lambda n: self.all_parts(n, lambda n, part: self.own(n, part).start())
        )

    def start(self):
        def hop(n, part):
            self.hop(n, part).start()

        def near(n, part):
            self.near(n, part).start()

        every(0, self.pieces, lambda n: self.all_parts(n, hop))
        every(0, self.pieces, lambda n: self.all_parts(n, near))

    def pass_on(self, n):
        def one(n, part):
            self.hop(n, part).wait_recv()
            self.pairs(n, part).start()
            self.relay(n, part).start()

        self.all_parts(n, one)

    def pass_pair(self, n):
        def one(n, part):
            self.pairs(n, part).wait_recv()
            self.pair_relay(n, part).start()

        self.all_parts(n, one)

    def ready(self, n):
        def one(n, part):
            self.own(n, part).wait()
            for copy in (self.near(n, part), self.relay(n, part), self.pair_relay(n, part)):
                copy.wait_recv()

        self.all_parts(n, one)

    def drain(self):
        def one(n, part):
            for copy in (
                self.hop(n, part), self.pairs(n, part), self.relay(n, part),
                self.pair_relay(n, part), self.near(n, part),
            ):
                copy.wait_send()

        every(0, self.pieces, lambda n: self.all_parts(n, one))


def slot_tables(routes_ref, priority_ref, capacity, pick_ref, back_ref):
    count = routes_ref.shape[1]
    row = lax.broadcasted_iota(jnp.int32, (count, count), 0).astype(jnp.float32)
    col = lax.broadcasted_iota(jnp.int32, (count, count), 1).astype(jnp.float32)
    eye = row == col
    route_row = routes_ref[...].astype(jnp.float32)
    order_row = priority_ref[...].astype(jnp.float32)
    route_col = jnp.sum(jnp.where(eye, route_row, 0.0), axis=1, keepdims=True)
    order_col = jnp.sum(jnp.where(eye, order_row, 0.0), axis=1, keepdims=True)
    same = route_col == route_row
    rank_row = jnp.sum(
        jnp.where(same & (order_col < order_row), 1.0, 0.0), axis=0, keepdims=True
    )
    rank_col = jnp.sum(
        jnp.where(same & (order_row < order_col), 1.0, 0.0), axis=1, keepdims=True
    )
    slots = float(count)
    slot_row = jnp.where(rank_row < capacity, route_row * capacity + rank_row, slots)
    slot_col = jnp.where(rank_col < capacity, route_col * capacity + rank_col, slots)
    pick_ref[...] = jnp.where(slot_row == row, 1.0, 0.0).astype(jnp.bfloat16)
    back_ref[...] = jnp.where(slot_col == col, 1.0, 0.0).astype(jnp.bfloat16)


def norm_stats(value):
    centered = value - jnp.mean(value, axis=1, keepdims=True)
    inverse = lax.rsqrt(jnp.mean(centered * centered, axis=1, keepdims=True) + epsilon)
    return centered * inverse, inverse


def front_kernel(
    dims,
    prefix_ref, routes_ref, priority_ref, gain_one_ref, shift_one_ref, gain_two_ref, shift_two_ref,
    tokens_hbm, cot_hbm, router_hbm, qkv_hbm, out_hbm,
    qkv_out, act_out, merged_out, back_out, weight_out, out_full, low_out, high_out, grads_rows,
    hidden_hbm, send_hbm, small_out, router_out,
    small_own, tokens_ref, cot_ref, hidden_ref, send_ref,
    small, weight, out_w, qkv, act, merged, act_two, turned, pick, back, grads_send, low_buf, high_buf,
    own_sem, disp_send, disp_recv, small_send, small_recv, gat_send, gat_recv, store_sem, prob_sem, first_sem,
):
    owners, capacity, pieces = dims
    place = Place(owners)
    firsts = [
        pltpu.make_async_copy(src, dst, first_sem.at[i])
        for i, (src, dst) in enumerate(((cot_hbm, cot_ref), (tokens_hbm, tokens_ref)))
    ]
    for load in firsts:
        load.start()
    small_own[...] = jnp.zeros_like(small_own)
    for i, vector_ref in enumerate((gain_one_ref, shift_one_ref, gain_two_ref, shift_two_ref)):
        small_own[i, :] = vector_ref[...]
    rows, width = tokens_ref.shape
    shard = qkv_hbm.shape[0]
    gathers = [
        Gather(place, pieces, parts, src, dst, (gat_send.at[i], gat_recv.at[i]))
        for i, (parts, src, dst) in enumerate(((3, qkv_hbm, weight), (1, out_hbm, out_w)))
    ]
    for gather in gathers:
        gather.start_own()
    vectors, gates = small_own.shape[0], router_hbm.shape[0]
    small_parts = [
        (small_own, small.at[place.w, pl.ds(0, vectors)]),
        (router_hbm, small.at[place.w, pl.ds(vectors, gates)]),
    ]
    own_smalls = [
        pltpu.make_async_copy(src, dst, own_sem.at[3 + i])
        for i, (src, dst) in enumerate(small_parts)
    ]
    for copy in own_smalls:
        copy.start()
    greet(
        [(place.ahead(k), place.w) for k in range(1, owners)]
        + [(place.e, place.sib), (place.e, place.far), (place.e, place.diag)]
    )
    smalls = [
        remote(src, dst, small_send.at[n, i], small_recv.at[n, i], (place.e, peer))
        for i, peer in enumerate((place.sib, place.far, place.diag))
        for n, (src, dst) in enumerate(small_parts)
    ]
    for copy in smalls:
        copy.start()
    for gather in gathers:
        gather.start()
    slot_tables(routes_ref, priority_ref, capacity, pick, back)
    tile = min(256, width)
    shape = grads_send.shape[:3]

    def to_slots(values_ref, slots_ref):
        def one(n):
            cols = span(n * tile, tile)
            value = dot_nn(pick[...], values_ref[:, cols]).astype(jnp.bfloat16)
            slots_ref[:, :, :, cols] = value.reshape(shape + (tile,))

        every(0, width // tile, one)

    firsts[0].wait()
    to_slots(cot_ref, grads_send)
    dispatch = Dispatch(
        place, capacity, grads_send, grads_rows, (own_sem.at[0], disp_send, disp_recv)
    )
    dispatch.start()
    for copy in own_smalls:
        copy.wait()
    for copy in smalls:
        copy.wait_recv()
    small_out[...] = small[:, :vectors, :]
    router_out[...] = jnp.zeros_like(router_out)
    router_out[:gates, :] = jnp.concatenate(
        [small[i, vectors:, :] for i in range(4)], axis=1
    )

    def vector(which):
        parts = [small[i, which : which + 1, :] for i in range(4)]
        return jnp.concatenate(parts, axis=1).astype(jnp.float32)

    band = min(64, rows)
    gain, shift = vector(0), vector(1)

    def norm_band(i):
        part = span(i * band, band)
        scaled, _ = norm_stats(tokens_ref[part, :].astype(jnp.float32))
        act[part, :] = (scaled * gain + shift).astype(jnp.bfloat16)

    def project(n):
        for part in range(3):
            cols = gathers[0].cols(n, part)
            qkv[:, cols] = dot_nn(act[...], weight[:, cols]).astype(jnp.bfloat16)

    gathers[0].pass_on(0)
    firsts[1].wait()
    every(0, rows // band, norm_band)
    turned[0] = act[...].T
    stores = [
        pltpu.make_async_copy(src, dst, store_sem.at[i])
        for i, (src, dst) in enumerate(
            [(qkv, qkv_out), (turned.at[0], act_out), (back, back_out), (weight, weight_out),
             (turned.at[1], merged_out), (out_w, out_full)]
        )
    ]
    for store in stores[1:3]:
        store.start()
    half = rows // 2
    pairs = width // LANES

    def keep_probs(i):
        slot = lax.rem(i, 2)
        return (
            pltpu.make_async_copy(
                low_buf.at[slot], low_out.at[pl.ds(2 * i, 2)], prob_sem.at[0, slot]
            ),
            pltpu.make_async_copy(
                high_buf.at[slot], high_out.at[pl.ds(2 * i, 2)], prob_sem.at[1, slot]
            ),
        )

    def attend_pair(i):
        slot = lax.rem(i, 2)

        @pl.when(i >= 2)
        def _():
            for copy in keep_probs(i - 2):
                copy.wait()

        query, key, value = (
            qkv[:, span(part * width + i * LANES, LANES)] for part in range(3)
        )
        tops, bottoms = [], []
        for head in range(2):
            part = slice(head * HEAD_DIM, (head + 1) * HEAD_DIM)
            low, high, top, bottom = attend_head(
                query[:, part], key[:, part], value[:, part], prefix_ref[0]
            )
            low_buf[slot, head] = low
            high_buf[slot, head] = high
            tops.append(top)
            bottoms.append(bottom)
        cols = span(i * LANES, LANES)
        merged[:half, cols] = jnp.concatenate(tops, axis=1).astype(jnp.bfloat16)
        merged[half:, cols] = jnp.concatenate(bottoms, axis=1).astype(jnp.bfloat16)
        for copy in keep_probs(i):
            copy.start()

    group = pairs // pieces
    share = -(-owners // pieces)

    def front_step(n):
        @pl.when(n + 1 < pieces)
        def _():
            gathers[0].pass_on(n + 1)

        gathers[0].pass_pair(n)
        for i, partner in enumerate(dispatch.order()):
            pl.when(n == i // share)(functools.partial(dispatch.forward, partner))
        gathers[0].ready(n)
        project(n)
        pl.when(n >= 2)(lambda: gathers[1].pass_on(n - 2))

        @pl.when(n == pieces - 1)
        def _():
            gathers[1].pass_on(pieces - 2)
            gathers[1].pass_pair(0)

        for i in range(group):
            attend_pair(n * group + i)

    every(0, pieces, front_step)
    gathers[1].pass_on(pieces - 1)
    every(1, pieces, gathers[1].pass_pair)
    turned[1] = merged[...].T
    for i in (0, 3, 4):
        stores[i].start()
    order = dispatch.order()
    dispatch.relay(order[0])
    every(0, pieces, gathers[1].ready)
    stores[5].start()
    gain_two, shift_two = vector(2), vector(3)
    band_two = min(128, rows)

    def middle(i):
        part = span(i * band_two, band_two)
        value = tokens_ref[part, :].astype(jnp.float32) + dot_nn(merged[part, :], out_w[...])
        hidden_ref[part, :] = value
        scaled, _ = norm_stats(value)
        act_two[part, :] = (scaled * gain_two + shift_two).astype(jnp.bfloat16)
        for n, partner in enumerate(order[1 : 1 + bands]):
            pl.when(i == n)(functools.partial(dispatch.relay, partner))

    bands = rows // band_two
    every(0, bands, middle)
    results = [
        pltpu.make_async_copy(src, dst, first_sem.at[2 + i])
        for i, (src, dst) in enumerate(((hidden_ref, hidden_hbm), (send_ref, send_hbm)))
    ]
    results[0].start()
    to_slots(act_two, send_ref)
    results[1].start()
    for partner in order[1 + bands :]:
        dispatch.relay(partner)
    for i in (pairs - 2, pairs - 1):
        for copy in keep_probs(i):
            copy.wait()
    every(0, owners, dispatch.ready)
    for store in stores + results:
        store.wait()
    for copy in smalls:
        copy.wait_send()
    for gather in gathers:
        gather.drain()
    dispatch.drain()


def run_front(
    owners, experts, capacity, prefix, routes, priority, vectors, tokens, cotangent, router, w_qkv, w_out
):
    rows, width = tokens.shape
    shard, columns = w_qkv.shape
    half = rows // 2
    heads = width // HEAD_DIM
    pieces = 4
    any_spec = pl.BlockSpec(memory_space=pl.ANY)
    vmem_spec = pl.BlockSpec(memory_space=pltpu.VMEM)
    bf16, f32 = jnp.bfloat16, jnp.float32
    dma = pltpu.SemaphoreType.DMA

    def out(*shape):
        return jax.ShapeDtypeStruct(shape, bf16)

    def vm(*shape):
        return pltpu.VMEM(shape, bf16)

    return pl.pallas_call(
        functools.partial(front_kernel, (owners, capacity, pieces)),
        out_shape=(
            out(rows, columns),
            out(width, rows),
            out(width, rows),
            out(rows, rows),
            out(4 * shard, columns),
            out(4 * shard, width),
            out(heads, half, half),
            out(heads, half, rows),
            out(experts, owners * 4 * capacity, width),
            jax.ShapeDtypeStruct((rows, width), f32),
            out(owners, experts, capacity, width),
            out(4, 16, shard),
            out(LANES, width),
        ),
        in_specs=[pl.BlockSpec(memory_space=pltpu.SMEM)] + [vmem_spec] * 6 + [any_spec] * 5,
        out_specs=(any_spec,) * 11 + (vmem_spec,) * 2,
        scratch_shapes=[
            vm(16, shard),
            vm(rows, width),
            vm(rows, width),
            pltpu.VMEM((rows, width), f32),
            vm(owners, experts, capacity, width),
            vm(4, 16 + router.shape[0], shard),
            vm(4 * shard, columns),
            vm(4 * shard, width),
            vm(rows, columns),
            vm(rows, width),
            vm(rows, width),
            vm(rows, width),
            vm(2, width, rows),
            vm(rows, rows),
            vm(rows, rows),
            vm(owners, experts, capacity, width),
            vm(2, 2, half, half),
            vm(2, 2, half, rows),
            dma((5,)),
            dma((4, owners)),
            dma((4, owners)),
            dma((2, 3)),
            dma((2, 3)),
            dma((2, 6, pieces, 3)),
            dma((2, 6, pieces, 3)),
            dma((6,)),
            dma((2, 2)),
            dma((4,)),
        ],
        compiler_params=pltpu.CompilerParams(
            collective_id=0, has_side_effects=True, vmem_limit_bytes=VMEM_LIMIT
        ),
        name="front",
    )(prefix, routes, priority, *vectors, tokens, cotangent, router, w_qkv, w_out)


class Reduce:
    def __init__(self, place, part, got, far, pair, near, line, done, sems):
        self.p = place
        self.part, self.got, self.far = part, got, far
        self.pair, self.near, self.line, self.done = pair, near, line, done
        self.send, self.recv = sems
        self.chunks = part.shape[0]
        self.halves = done.shape[1] // 2
        self.bit = lax.rem(place.e, 2)
        self.low = lax.rem(lax.div(place.e, 2), 2)
        self.high = lax.div(place.e, 4)

    def step(self, which, n, src, dst, device):
        return remote(src, dst, self.send.at[which, n], self.recv.at[which, n], device)

    def swapped(self, n):
        return self.step(
            0, n, self.part.at[n, :, 1 - self.p.c], self.got.at[n], (self.p.e, self.p.sib)
        )

    def crossed(self, n):
        return self.step(
            1, n, self.part.at[n, 1 - self.p.x, self.p.c], self.far.at[n], (self.p.e, self.p.far)
        )

    def folded(self, n):
        other = span((1 - self.bit) * self.halves, self.halves)
        return self.step(
            2, n, self.part.at[n, self.p.x, self.p.c, other], self.pair.at[n],
            (self.p.pair, self.p.w),
        )

    def shared(self, n):
        part = self.done.at[n, span(self.bit * self.halves, self.halves)]
        return self.step(3, n, part, part, (self.p.pair, self.p.w))

    def quarter(self, low):
        size = self.halves // 2
        return span(self.bit * self.halves + low * size, size)

    def eighth(self, high):
        size = self.halves // 4
        return span(self.bit * self.halves + (self.low * 2 + high) * size, size)

    def nears(self, n):
        return self.step(
            4, n, self.part.at[n, self.p.x, self.p.c, self.quarter(1 - self.low)],
            self.near.at[n], (self.p.flip(2), self.p.w),
        )

    def lines(self, n):
        return self.step(
            5, n, self.part.at[n, self.p.x, self.p.c, self.eighth(1 - self.high)],
            self.line.at[n], (self.p.flip(4), self.p.w),
        )

    def line_back(self, n):
        part = self.done.at[n, self.eighth(self.high)]
        return self.step(6, n, part, part, (self.p.flip(4), self.p.w))

    def near_back(self, n):
        part = self.done.at[n, self.quarter(self.low)]
        return self.step(7, n, part, part, (self.p.flip(2), self.p.w))

    def add(self, n, rows, other):
        total = self.part[n, self.p.x, self.p.c, rows, :].astype(jnp.float32) + other.astype(
            jnp.float32
        )
        return total.astype(jnp.bfloat16)

    def pair_sum(self, n, side):
        return self.part[n, side, self.p.c].astype(jnp.float32) + self.got[n, side].astype(
            jnp.float32
        )

    def swap(self, n):
        self.swapped(n).start()

    def cross(self, n):
        self.swapped(n).wait_recv()
        side = 1 - self.p.x
        self.part[n, side, self.p.c] = self.pair_sum(n, side).astype(jnp.bfloat16)
        self.crossed(n).start()

    def fold(self, n):
        self.crossed(n).wait_recv()
        total = self.pair_sum(n, self.p.x) + self.far[n].astype(jnp.float32)
        self.part[n, self.p.x, self.p.c] = total.astype(jnp.bfloat16)
        self.folded(n).start()

    def spread(self, n):
        self.folded(n).wait_recv()
        own = span(self.bit * self.halves, self.halves)
        self.part[n, self.p.x, self.p.c, own, :] = self.add(n, own, self.pair[n])
        self.nears(n).start()

    def reach(self, n):
        self.nears(n).wait_recv()
        own = self.quarter(self.low)
        self.part[n, self.p.x, self.p.c, own, :] = self.add(n, own, self.near[n])
        self.lines(n).start()

    def collect(self, n):
        self.lines(n).wait_recv()
        own = self.eighth(self.high)
        self.done[n, own, :] = self.add(n, own, self.line[n])
        self.line_back(n).start()

    def widen_back(self, n):
        self.line_back(n).wait_recv()
        self.near_back(n).start()

    def share(self, n):
        self.near_back(n).wait_recv()
        self.shared(n).start()

    def finish(self, n):
        self.shared(n).wait_recv()

    def line_stages(self):
        return (self.spread, self.reach, self.collect, self.widen_back, self.share, self.finish)

    def stages(self):
        return (self.cross, self.fold) + self.line_stages()

    def drain(self):
        def one(n):
            for copy in (
                self.swapped(n), self.crossed(n), self.folded(n), self.shared(n), self.nears(n),
                self.lines(n), self.line_back(n), self.near_back(n),
            ):
                copy.wait_send()

        every(0, self.chunks, one)


class PairFirst(Reduce):
    def folded(self, n):
        other = span((1 - self.bit) * self.halves, self.halves)
        return self.step(
            2, n, self.part.at[n, :, self.p.c, other], self.pair.at[n], (self.p.pair, self.p.w)
        )

    def crossed(self, n):
        own = span(self.bit * self.halves, self.halves)
        return self.step(
            1, n, self.part.at[n, 1 - self.p.x, self.p.c, own], self.far.at[n],
            (self.p.e, self.p.far),
        )

    def fold(self, n):
        self.swapped(n).wait_recv()
        for side in range(2):
            self.part[n, side, self.p.c] = self.pair_sum(n, side).astype(jnp.bfloat16)
        self.folded(n).start()

    def cross(self, n):
        self.folded(n).wait_recv()
        own = span(self.bit * self.halves, self.halves)
        for side in range(2):
            total = self.part[n, side, self.p.c, own, :].astype(jnp.float32) + self.pair[
                n, side
            ].astype(jnp.float32)
            self.part[n, side, self.p.c, own, :] = total.astype(jnp.bfloat16)
        self.crossed(n).start()

    def spread(self, n):
        self.crossed(n).wait_recv()
        own = span(self.bit * self.halves, self.halves)
        self.part[n, self.p.x, self.p.c, own, :] = self.add(n, own, self.far[n])
        self.nears(n).start()

    def stages(self):
        return (self.fold, self.cross) + self.line_stages()


class Small:
    def __init__(self, place, value, part, got, mid, far, total, others, out, sems):
        self.p, self.value, self.part, self.got, self.mid = place, value, part, got, mid
        self.far, self.total, self.others, self.out = far, total, others, out
        self.send, self.recv, self.all_send, self.all_recv = sems

    def swapped(self):
        return remote(
            self.part.at[:, 1 - self.p.c], self.got, self.send.at[0], self.recv.at[0],
            (self.p.e, self.p.sib),
        )

    def crossed(self):
        return remote(
            self.mid, self.far, self.send.at[1], self.recv.at[1], (self.p.e, self.p.far)
        )

    def spreads(self, k):
        return remote(
            self.total, self.others.at[k], self.all_send.at[k], self.all_recv.at[k],
            (self.p.ahead(k), self.p.w),
        )

    def swap(self):
        size = self.part.shape[-1]
        for owner in range(4):
            self.part[owner // 2, owner % 2] = self.value[:, owner * size : (owner + 1) * size]
        self.swapped().start()

    def cross(self):
        self.swapped().wait_recv()
        self.mid[...] = self.part[1 - self.p.x, self.p.c] + self.got[1 - self.p.x]
        self.crossed().start()

    def spread(self):
        self.crossed().wait_recv()
        self.total[...] = self.part[self.p.x, self.p.c] + self.got[self.p.x] + self.far[...]
        for k in range(1, self.p.owners):
            self.spreads(k).start()

    def finish(self):
        total = self.total[...]
        for k in range(1, self.p.owners):
            self.spreads(k).wait_recv()
            total = total + self.others[k]
        vectors_out, gates_out = self.out
        vectors_out[...] = total[: vectors_out.shape[0]]
        gates_out[...] = total[vectors_out.shape[0] :]

    def drain(self):
        self.swapped().wait_send()
        self.crossed().wait_send()
        for k in range(1, self.p.owners):
            self.spreads(k).wait_send()


def norm_back_rows(grad, scaled, inverse, gain):
    weighted = grad * gain
    mean_one = jnp.mean(weighted, axis=1, keepdims=True)
    mean_two = jnp.mean(weighted * scaled, axis=1, keepdims=True)
    return inverse * (weighted - mean_one - scaled * mean_two)


def back_kernel(
    dims,
    home_grad_hbm, back_hbm, hidden_hbm, cot_hbm, tokens_hbm, vectors_ref, router_ref,
    far_hbm, near_hbm, home_hbm, act_hbm, merged_hbm, qkv_hbm, weight_hbm, out_hbm, low_hbm, high_hbm,
    output_hbm, grad_tokens_hbm, vectors_out, gates_out, qkv_out, out_out,
    home_grad_ref, back_ref, hidden_ref, cot_ref, tokens_ref, output_ref, tokens_out,
    near_sums, far_sums, done_rows, home_out,
    act_t, merged_t, qkv, weight, out_w, low_buf, high_buf, attn, grad_merged, grad_act,
    part_q, got_q, far_q, pair_q, near_q, line_q, done_q,
    part_o, got_o, far_o, pair_o, near_o, line_o, done_o,
    small, small_part, small_got, small_mid, small_far, small_sum, small_all,
    first_sem, load_sem, prob_sem, own_sem, early_sem, cross_send, cross_recv, home_send, home_recv, send_q, recv_q, send_o, recv_o,
    small_send, small_recv, all_send, all_recv, out_sem,
):
    owners, capacity, gates = dims
    grad_qkv = qkv
    place = Place(owners)
    loads = [
        pltpu.make_async_copy(src, dst, load_sem.at[i])
        for i, (src, dst) in enumerate(
            [(merged_hbm, merged_t), (out_hbm, out_w), (qkv_hbm, qkv), (act_hbm, act_t),
             (weight_hbm, weight), (near_hbm, near_sums)]
        )
    ]

    def load_probs(i):
        slot = lax.rem(i, 2)
        return (
            pltpu.make_async_copy(
                low_hbm.at[pl.ds(2 * i, 2)], low_buf.at[slot], prob_sem.at[0, slot]
            ),
            pltpu.make_async_copy(
                high_hbm.at[pl.ds(2 * i, 2)], high_buf.at[slot], prob_sem.at[1, slot]
            ),
        )

    firsts = [
        pltpu.make_async_copy(src, dst, first_sem.at[i])
        for i, (src, dst) in enumerate(
            [(home_grad_hbm, home_grad_ref), (back_hbm, back_ref), (hidden_hbm, hidden_ref),
             (cot_hbm, cot_ref), (tokens_hbm, tokens_ref)]
        )
    ]
    results = [
        pltpu.make_async_copy(src, dst, first_sem.at[5 + i])
        for i, (src, dst) in enumerate([(tokens_out, grad_tokens_hbm), (output_ref, output_hbm)])
    ]
    for load in firsts[:4] + loads + firsts[4:]:
        load.start()
    for load in load_probs(0):
        load.start()
    greet(
        [(place.ahead(k), place.w) for k in range(1, owners)]
        + [(place.e, place.sib), (place.e, place.far)]
    )
    experts = near_sums.shape[0]
    groups = owners // 2
    late = LateReturn(
        place, capacity, near_sums, None, far_hbm, far_sums, done_rows, home_out,
        (own_sem, cross_send, cross_recv, home_send, home_recv),
    )

    def start_late(j):
        for expert in range(experts):
            late.crossed(j, expert).start()

    every(EARLY_CHUNKS, groups, start_late)

    def early_rows(n):
        row = place.peer(n)
        return pltpu.make_async_copy(home_hbm.at[row], home_out.at[row], early_sem.at[n])

    every(0, 2 * EARLY_CHUNKS, lambda n: early_rows(n).start())
    reduce_o = PairFirst(
        place, part_o, got_o, far_o, pair_o, near_o, line_o, done_o, (send_o, recv_o)
    )
    reduce_q = Reduce(
        place, part_q, got_q, far_q, pair_q, near_q, line_q, done_q, (send_q, recv_q)
    )
    smalls = Small(
        place, small, small_part, small_got, small_mid, small_far, small_sum, small_all, (vectors_out, gates_out),
        (small_send, small_recv, all_send, all_recv),
    )
    rows, width = tokens_ref.shape
    shard = width // 4
    band = min(128, rows)
    lead = small.shape[0]

    def vector(which):
        parts = [vectors_ref[i, which : which + 1, :] for i in range(4)]
        return jnp.concatenate(parts, axis=1).astype(jnp.float32)

    gain_one, gain_two = vector(0), vector(2)
    small[: lead - gates, :] = jnp.zeros((lead - gates, width), jnp.float32)
    small[lead - gates :, :] = router_ref[:gates, :]

    def post(i):
        part = span(i * band, band)
        grad = dot_nn(back_ref[part, :], home_grad_ref.reshape(rows, width)[...])
        scaled, inverse = norm_stats(hidden_ref[part, :])
        value = cot_ref[part, :].astype(jnp.float32) + norm_back_rows(
            grad, scaled, inverse, gain_two
        )
        tokens_out[part, :] = value
        attn[part, :] = value.astype(jnp.bfloat16)
        small[2:3, :] += jnp.sum(grad * scaled, axis=0, keepdims=True)
        small[3:4, :] += jnp.sum(grad, axis=0, keepdims=True)

    for load in firsts[:4]:
        load.wait()
    every(0, rows // band, post)
    loads[0].wait()

    def weight_grad(part, n, left, right):
        value = dot_nn(left[...], right).astype(jnp.bfloat16)
        part[n] = value.reshape(part.shape[1:])

    tile_o = part_o.shape[-1]
    out_chunks = part_o.shape[0]
    for n in range(out_chunks):
        weight_grad(part_o, n, merged_t, attn[:, n * tile_o : (n + 1) * tile_o])
        reduce_o.swap(n)
    loads[1].wait()

    def merged_band(i):
        part = span(i * band, band)
        grad_merged[part, :] = dot_nt(attn[part, :], out_w[...]).astype(jnp.bfloat16)

    every(0, rows // band, merged_band)
    stages_o, stages_q = reduce_o.stages(), reduce_q.stages()
    for n in range(out_chunks):
        stages_o[0](n)
    for load in loads[2:] + firsts[4:]:
        load.wait()
    grad_act[...] = jnp.zeros_like(grad_act)
    pairs = part_q.shape[0]

    def attend_pair(i):
        slot = lax.rem(i, 2)
        for load in load_probs(i):
            load.wait()

        @pl.when(i + 1 < pairs)
        def _():
            for load in load_probs(i + 1):
                load.start()

        cols = span(i * LANES, LANES)
        query, key, value = (
            qkv[:, span(part * width + i * LANES, LANES)] for part in range(3)
        )
        grad = grad_merged[:, cols]
        results = []
        for head in range(2):
            part = slice(head * HEAD_DIM, (head + 1) * HEAD_DIM)
            results.append(
                attend_back_head(
                    query[:, part], key[:, part], value[:, part],
                    low_buf[slot, head], high_buf[slot, head], grad[:, part],
                )
            )
        for which in range(3):
            grad_qkv[:, span(which * width + i * LANES, LANES)] = jnp.concatenate(
                [results[0][which], results[1][which]], axis=1
            )
        right = jnp.concatenate(
            [grad_qkv[:, span(which * width + i * LANES, LANES)] for which in range(3)], axis=1
        )
        weight_grad(part_q, i, act_t, right)
        reduce_q.swap(i)
        columns = jnp.concatenate(
            [weight[:, span(which * width + i * LANES, LANES)] for which in range(3)], axis=1
        )
        grad_act[...] += dot_nt(right, columns)

    def input_band(i):
        part = span(i * band, band)
        grad = grad_act[part, :]
        scaled, inverse = norm_stats(tokens_ref[part, :].astype(jnp.float32))
        tokens_out[part, :] += norm_back_rows(grad, scaled, inverse, gain_one)
        small[0:1, :] += jnp.sum(grad * scaled, axis=0, keepdims=True)
        small[1:2, :] += jnp.sum(grad, axis=0, keepdims=True)

    def output_band(i):
        part = span(i * band, band)
        slots = home_out.reshape(rows, width)
        value = hidden_ref[part, :] + dot_nn(back_ref[part, :], slots[...])
        output_ref[part, :] = value.astype(jnp.bfloat16)

    def store_q(i):
        return [
            pltpu.make_async_copy(
                done_q.at[i, :, pl.ds(which * LANES, LANES)],
                qkv_out.at[:, span(which * width + i * LANES, LANES)],
                out_sem.at[which, i],
            )
            for which in range(3)
        ]

    def store_o(n):
        return pltpu.make_async_copy(
            done_o.at[n], out_out.at[:, span(n * tile_o, tile_o)], out_sem.at[3, n]
        )

    delays = (1, 3, 4, 5, 6, 7, 8, 9)
    turns_o = (-1, 3, 6, 7, 8, 9, 10, 11)
    last = len(delays) - 1
    half = rows // band // 2

    def slot_step(slot):
        @pl.when(slot + EARLY_CHUNKS < groups)
        def _():
            for expert in range(experts):
                late.finish(slot + EARLY_CHUNKS, expert)

        pl.when(slot < pairs)(lambda: attend_pair(slot))
        for s in range(last, -1, -1):
            n = slot - delays[s]

            @pl.when((n >= 0) & (n < pairs))
            def _(s=s, n=n):
                stages_q[s](n)
                if s == last:
                    for copy in store_q(n):
                        copy.start()

            @pl.when(slot == turns_o[s])
            def _(s=s):
                for n in range(out_chunks):
                    stages_o[s](n)
                    if s == last:
                        store_o(n).start()

        @pl.when(slot == pairs)
        def _():
            every(0, half, input_band)

        @pl.when(slot == pairs + 1)
        def _():
            every(half, 2 * half, input_band)
            results[0].start()

        pl.when(slot == pairs + 2)(smalls.swap)
        pl.when(slot == pairs + 3)(smalls.cross)
        pl.when(slot == pairs + 4)(smalls.spread)

        @pl.when(slot == pairs + 3)
        def _():
            late.arrived(EARLY_CHUNKS, groups, experts)
            every(0, 2 * EARLY_CHUNKS, lambda n: early_rows(n).wait())
            every(0, rows // band, output_band)
            results[1].start()

    every(0, pairs + delays[-1], slot_step)
    smalls.finish()

    def stored(i):
        for copy in store_q(i):
            copy.wait()

    every(0, pairs, stored)
    for result in results:
        result.wait()
    for n in range(out_chunks):
        store_o(n).wait()
    late.drain(EARLY_CHUNKS, groups, experts)
    reduce_o.drain()
    reduce_q.drain()
    smalls.drain()


def run_back(
    owners, capacity, gates, home_grad, far_sums, near_sums, home_out, back, hidden, cotangent, tokens,
    vectors, router_grad, act_t, merged_t, qkv, weight, w_out, low, high,
):
    rows, width = tokens.shape
    shard = width // 4
    lead = 8 + gates
    groups = owners // 2
    pairs = width // LANES
    tile_o = min(512, width)
    out_chunks = width // tile_o
    half = shard // 2
    mid = rows // 2
    any_spec = pl.BlockSpec(memory_space=pl.ANY)
    vmem_spec = pl.BlockSpec(memory_space=pltpu.VMEM)
    bf16, f32 = jnp.bfloat16, jnp.float32
    dma = pltpu.SemaphoreType.DMA

    def vm(*shape):
        return pltpu.VMEM(shape, bf16)

    def fm(*shape):
        return pltpu.VMEM(shape, f32)

    def reduce_buffers(chunks, tile, pair_first):
        far, pair = ((half,), (2, half)) if pair_first else ((shard,), (half,))
        return [
            vm(chunks, 2, 2, shard, tile),
            vm(chunks, 2, shard, tile),
            vm(chunks, *far, tile),
            vm(chunks, *pair, tile),
            vm(chunks, half // 2, tile),
            vm(chunks, half // 4, tile),
            vm(chunks, shard, tile),
        ]

    def reduce_sems(chunks):
        return [dma((8, chunks)), dma((8, chunks))]

    return pl.pallas_call(
        functools.partial(back_kernel, (owners, capacity, gates)),
        out_shape=(
            jax.ShapeDtypeStruct((rows, width), bf16),
            jax.ShapeDtypeStruct((rows, width), f32),
            jax.ShapeDtypeStruct((8, shard), f32),
            jax.ShapeDtypeStruct((gates, shard), f32),
            jax.ShapeDtypeStruct((shard, 3 * width), bf16),
            jax.ShapeDtypeStruct((shard, width), bf16),
        ),
        in_specs=[any_spec] * 5 + [vmem_spec] * 2 + [any_spec] * 10,
        out_specs=(any_spec,) * 2 + (vmem_spec,) * 2 + (any_spec,) * 2,
        scratch_shapes=[
            vm(*home_grad.shape),
            vm(rows, rows),
            fm(rows, width),
            vm(rows, width),
            vm(rows, width),
            vm(rows, width),
            fm(rows, width),
            vm(*near_sums.shape),
            vm(*near_sums.shape),
            vm(*home_grad.shape),
            vm(*home_grad.shape),
            vm(width, rows),
            vm(width, rows),
            vm(rows, 3 * width),
            vm(width, 3 * width),
            vm(width, width),
            vm(2, 2, mid, mid),
            vm(2, 2, mid, rows),
            vm(rows, width),
            vm(rows, width),
            fm(rows, width),
        ]
        + reduce_buffers(pairs, 3 * LANES, False)
        + reduce_buffers(out_chunks, tile_o, True)
        + [
            fm(lead, width),
            fm(2, 2, lead, shard),
            fm(2, lead, shard),
            fm(lead, shard),
            fm(lead, shard),
            fm(lead, shard),
            fm(owners, lead, shard),
            dma((7,)),
            dma((6,)),
            dma((2, 2)),
            dma((near_sums.shape[0],)),
            dma((owners,)),
            dma((groups, near_sums.shape[0])),
            dma((groups, near_sums.shape[0])),
            dma((owners, near_sums.shape[0])),
            dma((owners, near_sums.shape[0])),
        ]
        + reduce_sems(pairs)
        + reduce_sems(out_chunks)
        + [dma((2,)), dma((2,)), dma((owners,)), dma((owners,)), dma((4, pairs))],
        compiler_params=pltpu.CompilerParams(
            collective_id=2, has_side_effects=True, vmem_limit_bytes=VMEM_LIMIT
        ),
        name="back",
    )(
        home_grad, back, hidden, cotangent, tokens, vectors, router_grad,
        far_sums, near_sums, home_out, act_t, merged_t, qkv, weight, w_out, low, high,
    )


def widen_kernel(vectors_ref, *refs):
    count = (len(refs) - 4) // 2
    for src, dst in zip(refs[:count], refs[count:]):
        dst[...] = src[...].astype(dst.dtype)
    for i, dst in enumerate(refs[2 * count :]):
        dst[...] = vectors_ref[i, :]


def widen(steps, vectors, values, kinds):
    def spec(value):
        if value.shape[0] % (16 * steps):
            return pl.BlockSpec(value.shape, lambda i: (0, 0))
        return pl.BlockSpec((value.shape[0] // steps, value.shape[1]), lambda i: (i, 0))

    return pl.pallas_call(
        widen_kernel,
        grid=(steps,),
        in_specs=[pl.BlockSpec(vectors.shape, lambda i: (0, 0))]
        + [spec(value) for value in values],
        out_specs=[spec(value) for value in values]
        + [pl.BlockSpec((vectors.shape[1],), lambda i: (0,))] * 4,
        out_shape=[
            jax.ShapeDtypeStruct(value.shape, kind) for value, kind in zip(values, kinds)
        ]
        + [jax.ShapeDtypeStruct((vectors.shape[1],), jnp.float32)] * 4,
        name="widen",
    )(vectors, *values)


def on_device_plain(
    tokens,
    norm1_gain,
    norm1_shift,
    w_qkv,
    w_out,
    norm2_gain,
    norm2_shift,
    w_router,
    w_up,
    w_down,
    routes,
    priority,
    prefix,
    cotangent,
):
    row_count, model_width = tokens.shape
    expert_count = w_router.shape[1]
    capacity = row_count // expert_count
    owners = lax.axis_size("expert")
    local_experts = w_up.shape[0]
    slot_count = expert_count * capacity
    prefix_len = prefix[0]
    small = jnp.concatenate(
        [
            norm1_gain[None],
            norm1_shift[None],
            norm2_gain[None],
            norm2_shift[None],
            w_router.T,
        ],
        axis=0,
    )
    qkv_full = lax.all_gather(w_qkv, "wshard", axis=0, tiled=True)
    small_full = lax.all_gather(small, "wshard", axis=1, tiled=True)
    out_full = lax.all_gather(w_out, "wshard", axis=0, tiled=True)
    gain_one, shift_one, gain_two, shift_two = (small_full[i] for i in range(4))
    router_full = small_full[4:].T
    gain_one = gain_one.astype(jnp.float32)
    gain_two = gain_two.astype(jnp.float32)
    inputs = tokens.astype(jnp.float32)
    normed_one, scaled_one, inverse_one = normalize(inputs, gain_one, shift_one.astype(jnp.float32))
    act_one = normed_one.astype(jnp.bfloat16)
    qkv = jnp.dot(act_one, qkv_full, preferred_element_type=jnp.float32).astype(jnp.bfloat16)
    query_heads = qkv[:, :model_width]
    key_heads = qkv[:, model_width : 2 * model_width]
    value_heads = qkv[:, 2 * model_width :]
    merged, log_totals = attend_forward(query_heads, key_heads, value_heads, prefix_len)
    attn_out = jnp.dot(merged, out_full, preferred_element_type=jnp.float32)
    hidden = inputs + attn_out
    normed_two, scaled_two, inverse_two = normalize(hidden, gain_two, shift_two.astype(jnp.float32))
    act_two = normed_two.astype(jnp.bfloat16)
    logits = jnp.dot(act_two, router_full, preferred_element_type=jnp.float32)
    row_max = jnp.max(logits, axis=-1, keepdims=True)
    exponent = jnp.exp(logits - row_max)
    gate_prob = exponent / jnp.sum(exponent, axis=-1, keepdims=True)
    route_ids = routes[:, 0]
    chosen = route_ids[:, None] == jnp.arange(expert_count, dtype=jnp.int32)[None, :]
    gate_value = jnp.sum(jnp.where(chosen, gate_prob, 0.0), axis=1)
    slot_index, slot_source = assign_slots(route_ids, priority[0], expert_count, capacity)
    zero_row = jnp.zeros((1, model_width), jnp.bfloat16)
    padded = jnp.concatenate([act_two, zero_row], axis=0)
    send_rows = padded[slot_source].reshape(owners, local_experts * capacity, model_width)
    arrived = lax.all_to_all(send_rows, "expert", split_axis=0, concat_axis=0, tiled=True).reshape(
        owners, local_experts, capacity, model_width
    )
    group = lax.axis_size("wshard")
    local_rows = owners * capacity

    def by_expert(chunk):
        rows = jnp.transpose(chunk, (1, 0, 2, 3)).reshape(local_experts, local_rows, model_width)
        return lax.all_gather(rows, "wshard", axis=1, tiled=True)

    def home_rows(rows):
        own = lax.psum_scatter(rows.astype(jnp.bfloat16), "wshard", scatter_dimension=1, tiled=True)
        own = own.reshape(local_experts, owners, capacity, model_width)
        return jnp.transpose(own, (1, 0, 2, 3)).reshape(
            owners, local_experts * capacity, model_width
        )

    grad_output = cotangent.astype(jnp.float32)
    grad_combined = (gate_value[:, None] * grad_output).astype(jnp.bfloat16)
    grad_padded = jnp.concatenate([grad_combined, zero_row], axis=0)
    grad_send = grad_padded[slot_source].reshape(owners, local_experts * capacity, model_width)
    grad_arrived = lax.all_to_all(
        grad_send, "expert", split_axis=0, concat_axis=0, tiled=True
    ).reshape(owners, local_experts, capacity, model_width)
    rows_in = by_expert(arrived)
    grad_rows = by_expert(grad_arrived)
    pre_act = jnp.einsum("erd,edf->erf", rows_in, w_up, preferred_element_type=jnp.float32)
    activated, gelu_pull = jax.vjp(gelu_tanh, pre_act)
    act_hidden = activated.astype(jnp.bfloat16)
    produced = jnp.einsum(
        "erf,efd->erd", act_hidden, w_down, preferred_element_type=jnp.float32
    )
    expert_out = home_rows(produced)
    returned = lax.all_to_all(expert_out, "expert", split_axis=0, concat_axis=0, tiled=True)
    slots_back = jnp.concatenate([returned.reshape(slot_count, model_width), zero_row], axis=0)
    combined = slots_back[slot_index].astype(jnp.float32)
    output = (hidden + gate_value[:, None] * combined).astype(jnp.bfloat16)
    grad_gate = jnp.sum(grad_output * combined, axis=1)
    grad_down = jnp.einsum(
        "erf,erd->efd", act_hidden, grad_rows, preferred_element_type=jnp.float32
    )
    grad_hidden_units = jnp.einsum(
        "erd,efd->erf", grad_rows, w_down, preferred_element_type=jnp.float32
    )
    grad_pre = gelu_pull(grad_hidden_units)[0].astype(jnp.bfloat16)
    grad_up = jnp.einsum("erd,erf->edf", rows_in, grad_pre, preferred_element_type=jnp.float32)
    grad_expert_in = jnp.einsum(
        "erf,edf->erd", grad_pre, w_up, preferred_element_type=jnp.float32
    )
    grad_send_back = home_rows(grad_expert_in)
    grad_back = lax.all_to_all(grad_send_back, "expert", split_axis=0, concat_axis=0, tiled=True)
    grad_slots = jnp.concatenate([grad_back.reshape(slot_count, model_width), zero_row], axis=0)
    grad_act_two = grad_slots[slot_index].astype(jnp.float32)
    grad_logits = (
        gate_prob * (jnp.where(chosen, grad_gate[:, None], 0.0) - (gate_value * grad_gate)[:, None])
    ).astype(jnp.bfloat16)
    grad_router = contract_rows(act_two, grad_logits)
    grad_act_two = grad_act_two + times_transpose(grad_logits, router_full)
    grad_from_two, grad_gain_two, grad_shift_two = norm_back(
        grad_act_two, scaled_two, inverse_two, gain_two
    )
    grad_hidden = grad_output + grad_from_two
    grad_attn = grad_hidden.astype(jnp.bfloat16)
    grad_out_w = contract_rows(merged, grad_attn)
    grad_merged = times_transpose(grad_attn, out_full).astype(jnp.bfloat16)
    grad_qkv = attend_backward(
        query_heads, key_heads, value_heads, grad_merged, log_totals, prefix_len
    )
    grad_qkv_w = contract_rows(act_one, grad_qkv)
    grad_act_one = times_transpose(grad_qkv, qkv_full)
    grad_from_one, grad_gain_one, grad_shift_one = norm_back(
        grad_act_one, scaled_one, inverse_one, gain_one
    )
    grad_tokens = grad_hidden + grad_from_one
    small_grad = jnp.concatenate(
        [
            grad_gain_one[None],
            grad_shift_one[None],
            grad_gain_two[None],
            grad_shift_two[None],
            grad_router.T,
        ],
        axis=0,
    )
    out_share = lax.psum_scatter(
        grad_out_w.astype(jnp.bfloat16), "wshard", scatter_dimension=0, tiled=True
    )
    qkv_share = lax.psum_scatter(
        grad_qkv_w.astype(jnp.bfloat16), "wshard", scatter_dimension=0, tiled=True
    )
    small_share = lax.psum_scatter(small_grad, "wshard", scatter_dimension=1, tiled=True)
    out_total = lax.psum(out_share, "expert").astype(jnp.float32)
    qkv_total = lax.psum(qkv_share, "expert").astype(jnp.float32)
    small_total = lax.psum(small_share, "expert")
    totals = (
        small_total[0],
        small_total[1],
        qkv_total,
        out_total,
        small_total[2],
        small_total[3],
        small_total[4:].T,
    )
    return (
        output,
        grad_tokens,
        totals[0],
        totals[1],
        totals[2],
        totals[3],
        totals[4],
        totals[5],
        totals[6],
        grad_up,
        grad_down,
    )


def on_device(
    tokens,
    norm1_gain,
    norm1_shift,
    w_qkv,
    w_out,
    norm2_gain,
    norm2_shift,
    w_router,
    w_up,
    w_down,
    routes,
    priority,
    prefix,
    cotangent,
):
    row_count, model_width = tokens.shape
    expert_count = w_router.shape[1]
    capacity = row_count // expert_count
    owners = lax.axis_size("expert")
    experts = w_up.shape[0]
    (
        qkv, act_t, merged_t, back, weight, out_full, low, high, grad_rows, hidden, send_rows,
        vectors, router,
    ) = run_front(
        owners, experts, capacity, prefix, routes.reshape(1, row_count), priority,
        (norm1_gain, norm1_shift, norm2_gain, norm2_shift), tokens, cotangent, w_router.T, w_qkv,
        w_out,
    )
    far_sums, near_sums, home_out, home_grad, grad_up, grad_down, grad_router = run_experts(
        owners, capacity, expert_count, send_rows, grad_rows, w_up, w_down, router
    )
    output, grad_tokens, grad_vectors, grad_gates, grad_qkv, grad_out = run_back(
        owners, capacity, expert_count, home_grad, far_sums, near_sums, home_out, back, hidden, cotangent,
        tokens, vectors, grad_router, act_t, merged_t, qkv, weight, out_full, low, high,
    )
    f32 = jnp.float32
    units = w_up.shape[2]
    (
        output, grad_tokens, grad_gates, grad_qkv, grad_out, grad_up, grad_down, *grad_vectors,
    ) = widen(
        2,
        grad_vectors,
        (
            output, grad_tokens, grad_gates, grad_qkv, grad_out,
            grad_up.reshape(-1, units), grad_down.reshape(-1, model_width),
        ),
        (output.dtype,) + (f32,) * 6,
    )
    return (
        output,
        grad_tokens,
        grad_vectors[0],
        grad_vectors[1],
        grad_qkv,
        grad_out,
        grad_vectors[2],
        grad_vectors[3],
        grad_gates.T,
        grad_up.reshape(w_up.shape),
        grad_down.reshape(w_down.shape),
    )


def solution(mesh):
    placed = (
        P(("expert", "wshard"), None),
        P("wshard"),
        P("wshard"),
        P("wshard", None),
        P("wshard", None),
        P("wshard"),
        P("wshard"),
        P("wshard", None),
        P("expert", None, "wshard"),
        P("expert", "wshard", None),
        P(("expert", "wshard"), None),
        P(("expert", "wshard"), None),
        P(("expert", "wshard")),
        P(("expert", "wshard"), None),
    )
    owners, group = mesh.shape["expert"], mesh.shape["wshard"]

    def body(*args):
        capacity = args[0].shape[0] // args[7].shape[1]
        fits = group == 4 and owners == 8 and capacity % 16 == 0 and args[7].shape[1] % 16 == 0
        return (on_device if fits else on_device_plain)(*args)

    return jax.shard_map(
        body,
        mesh=mesh,
        in_specs=placed,
        out_specs=(
            P(("expert", "wshard"), None),
            P(("expert", "wshard"), None),
            P("wshard"),
            P("wshard"),
            P("wshard", None),
            P("wshard", None),
            P("wshard"),
            P("wshard"),
            P("wshard", None),
            P("expert", None, "wshard"),
            P("expert", "wshard", None),
        ),
        check_vma=False,
    )
```
